32 devices in a mesh: slot: 2 (over y), ctx: 4 (over z), fsdp: 4 (over x, core).
Axes of the slice: x: 2, y: 2, z: 4, core: 2. Of those that a mesh axis runs over, the one named last changes fastest.
Arguments:
- tokens: bfloat16 [4, 2048, 1024], P('slot', ('ctx', 'fsdp')), may hold values from -6 to 6
- lengths: int32 [4], P('slot'), may hold values from 1024 to 2048, as said below
- w_qkv: bfloat16 [1024, 3072], P(('ctx', 'fsdp')), may hold values from -0.25 to 0.25
- b_qkv: bfloat16 [3072], P(('ctx', 'fsdp')), may hold values from -1.796875 to 1.796875
- w_out: bfloat16 [1024, 1024], P(('ctx', 'fsdp')), may hold values from -1.5 to 1.5
- b_out: bfloat16 [1024], P(('ctx', 'fsdp')), may hold values from -1.796875 to 1.796875
- ln1_gain: bfloat16 [1024], P(('ctx', 'fsdp')), may hold values from 0.5 to 1.5
- ln1_bias: bfloat16 [1024], P(('ctx', 'fsdp')), may hold values from -1.796875 to 1.796875
- w_up: bfloat16 [1024, 4096], P(('ctx', 'fsdp')), may hold values from -0.1875 to 0.1875
- b_up: bfloat16 [4096], P(('ctx', 'fsdp')), may hold values from -1.796875 to 1.796875
- w_down: bfloat16 [4096, 1024], P(('ctx', 'fsdp')), may hold values from -0.09375 to 0.09375
- b_down: bfloat16 [1024], P(('ctx', 'fsdp')), may hold values from -1.796875 to 1.796875
- ln2_gain: bfloat16 [1024], P(('ctx', 'fsdp')), may hold values from 0.5 to 1.5
- ln2_bias: bfloat16 [1024], P(('ctx', 'fsdp')), may hold values from -1.796875 to 1.796875
- w_proj: bfloat16 [1024, 128], P(('ctx', 'fsdp')), may hold values from -0.1875 to 0.1875
- cot_out: bfloat16 [4, 2048, 1024], P('slot', ('ctx', 'fsdp')), may hold values from -6 to 6
- cot_emb: bfloat16 [4, 2048, 128], P('slot', ('ctx', 'fsdp')), may hold values from -6 to 6
Outputs:
- layer_out: bfloat16 [4, 2048, 1024], P('slot', ('ctx', 'fsdp'))
- embeds: bfloat16 [4, 2048, 128], P('slot', ('ctx', 'fsdp'))
- input_grad: bfloat16 [4, 2048, 1024], P('slot', ('ctx', 'fsdp'))
- grad_w_qkv: float32 [1024, 3072], P(('ctx', 'fsdp'))
- grad_b_qkv: float32 [3072], P(('ctx', 'fsdp'))
- grad_w_out: float32 [1024, 1024], P(('ctx', 'fsdp'))
- grad_b_out: float32 [1024], P(('ctx', 'fsdp'))
- grad_ln1_gain: float32 [1024], P(('ctx', 'fsdp'))
- grad_ln1_bias: float32 [1024], P(('ctx', 'fsdp'))
- grad_w_up: float32 [1024, 4096], P(('ctx', 'fsdp'))
- grad_b_up: float32 [4096], P(('ctx', 'fsdp'))
- grad_w_down: float32 [4096, 1024], P(('ctx', 'fsdp'))
- grad_b_down: float32 [1024], P(('ctx', 'fsdp'))
- grad_ln2_gain: float32 [1024], P(('ctx', 'fsdp'))
- grad_ln2_bias: float32 [1024], P(('ctx', 'fsdp'))
- grad_w_proj: float32 [1024, 128], P(('ctx', 'fsdp'))
The draws below stay inside these ranges and needn't reach their ends.
Inputs may be any that keep to these rules, and one draw needn't show every extreme that they name: Each slot holds lengths valid positions at its start; in every draw some slot is full (2048) and some slot holds exactly 1024.
All inputs are finite; a program needn't handle non-finite values.
Results may differ from the reference program's by a relative error of at most 0.018.
Values may be sent and summed in bfloat16 or wider, within the bound.
A program may use at most 192 MiB of HBM per device.

```python
import jax
import jax.numpy as jnp
from jax import lax

D = 1024
H = 16
HD = 64
FF = 4096
PROJ = 128
SLOT_LEN = 2048
SLOTS = 4


def draw_lengths(key, part):
    first_key = jax.random.fold_in(key, 11)
    second_key = jax.random.fold_in(key, 12)
    drawn_lengths = jax.random.randint(first_key, (SLOTS,), SLOT_LEN // 2, SLOT_LEN + 1, dtype=jnp.int32)
    slot_order = jax.random.permutation(second_key, SLOTS)
    drawn_lengths = drawn_lengths.at[slot_order[0]].set(SLOT_LEN)
    return drawn_lengths.at[slot_order[1]].set(SLOT_LEN // 2)


def level_of(own_key, shape, split, smallest, top_value):
    factor_of = 1.0
    for axis_at, parts in split:
        heights = jax.random.uniform(jax.random.fold_in(jax.random.fold_in(own_key, 6), axis_at), (parts,), jnp.float32, smallest / len(split), top_value / len(split))
        factor_of = factor_of * jnp.repeat(jnp.exp(heights), shape[axis_at] // parts).reshape((-1,) + (1,) * (len(shape) - 1 - axis_at))
    return factor_of


def gaussian(own_key, shape, scale, most, cuts=(), held_as=jnp.bfloat16):
    result = jax.random.normal(own_key, shape, jnp.float32) * scale
    if len(cuts) > 0:
        result = level_of(own_key, shape, cuts, -0.22, 0.18) * result
    return jnp.clip(result, min=-most, max=most).astype(held_as)


def setup_inputs(seed: int = 0) -> dict:
    arg_keys = jax.random.split(jax.random.key(seed), 18)
    tokens = gaussian(arg_keys[0], (SLOTS, SLOT_LEN, D), 1.0, 6.0, ((0, 2), (1, 16)))
    lengths = draw_lengths(jax.random.fold_in(arg_keys[17], 71), 0)
    w_qkv = gaussian(arg_keys[2], (D, 3 * D), (D // 2) ** -0.5, 0.25, ((0, 16),))
    b_qkv = gaussian(arg_keys[3], (3 * D,), 0.3, 1.796875, ((0, 16),))
    w_out = gaussian(arg_keys[4], (D, D), 16 ** -0.5, 1.5, ((0, 16),))
    b_out = gaussian(arg_keys[5], (D,), 0.3, 1.796875, ((0, 16),))
    ln1_gain = jnp.clip(1.0 + 0.1 * jax.random.normal(arg_keys[6], (D,), jnp.float32), 0.5, 1.5).astype(jnp.bfloat16)
    ln1_bias = gaussian(arg_keys[7], (D,), 0.3, 1.796875, ((0, 16),))
    w_up = gaussian(arg_keys[8], (D, FF), D ** -0.5, 0.1875, ((0, 16),))
    b_up = gaussian(arg_keys[9], (FF,), 0.3, 1.796875, ((0, 16),))
    w_down = gaussian(arg_keys[10], (FF, D), FF ** -0.5, 0.09375, ((0, 16),))
    b_down = gaussian(arg_keys[11], (D,), 0.3, 1.796875, ((0, 16),))
    ln2_gain = jnp.clip(1.0 + 0.1 * jax.random.normal(arg_keys[12], (D,), jnp.float32), 0.5, 1.5).astype(jnp.bfloat16)
    ln2_bias = gaussian(arg_keys[13], (D,), 0.3, 1.796875, ((0, 16),))
    w_proj = gaussian(arg_keys[14], (D, PROJ), D ** -0.5, 0.1875, ((0, 16),))
    cot_out = gaussian(arg_keys[15], (SLOTS, SLOT_LEN, D), 1.0, 6.0, ((0, 2), (1, 16)))
    cot_emb = gaussian(arg_keys[16], (SLOTS, SLOT_LEN, PROJ), 1.0, 6.0, ((0, 2), (1, 16)))
    return {"tokens": tokens, "lengths": lengths, "w_qkv": w_qkv, "b_qkv": b_qkv, "w_out": w_out, "b_out": b_out, "ln1_gain": ln1_gain, "ln1_bias": ln1_bias, "w_up": w_up, "b_up": b_up, "w_down": w_down, "b_down": b_down, "ln2_gain": ln2_gain, "ln2_bias": ln2_bias, "w_proj": w_proj, "cot_out": cot_out, "cot_emb": cot_emb}


@jax.custom_vjp
def low(v):
    return lax.optimization_barrier(v.astype(jnp.bfloat16)).astype(jnp.float32)

@jax.custom_vjp
def low_back(v):
    return v

def low_keep(v):
    return (low(v), None)

def low_pass(kept, grad):
    return (grad,)

def back_keep(v):
    return (v, None)

def back_low(kept, grad):
    return (low(grad),)
low.defvjp(low_keep, low_pass)
low_back.defvjp(back_keep, back_low)
HIGHEST_PREC = lax.Precision.HIGHEST
NEG_FILL = -1e+30
LN_EPS = 1e-05

def layer_norm(hidden, gain, shift):
    center = hidden - lax.optimization_barrier(jnp.mean(hidden, axis=-1, keepdims=True))
    spread = lax.optimization_barrier(jnp.mean(center * center, axis=-1, keepdims=True))
    return center * lax.rsqrt(spread + LN_EPS) * gain + shift

def rope_tables(positions, head_width):
    halfway = head_width // 2
    ladder = jnp.arange(halfway, dtype=jnp.float32) * (2.0 / head_width)
    frequency = jnp.power(jnp.float32(10000.0), -ladder)
    angles = positions[:, None] * frequency[None, :]
    return (jnp.cos(angles)[:, None, :], jnp.sin(angles)[:, None, :])

def rotate(values, cosine, sine_part):
    halfway = values.shape[-1] // 2
    first_half = values[..., :halfway]
    second_half = values[..., halfway:]
    return jnp.concatenate([first_half * cosine - second_half * sine_part, second_half * cosine + first_half * sine_part], axis=-1)

def dense(left_side, right_side):
    return jnp.dot(left_side, right_side, precision=HIGHEST_PREC, preferred_element_type=jnp.float32)

def slot_forward(tokens_slot, length, params):
    w_qkv, b_qkv, w_out, b_out, gain_one, shift_one, w_up, b_up, w_down, b_down, gain_two, shift_two, w_proj = params
    seq_len = tokens_slot.shape[0]
    width = tokens_slot.shape[1]
    joined = low_back(dense(tokens_slot, w_qkv) + b_qkv)
    positions = jnp.arange(seq_len).astype(jnp.float32)
    cosine, sine_part = rope_tables(positions, HD)
    queries = low(rotate(joined[:, :width].reshape(seq_len, H, HD), cosine, sine_part))
    keyset = low(rotate(joined[:, width:2 * width].reshape(seq_len, H, HD), cosine, sine_part))
    valset = low(joined[:, 2 * width:].reshape(seq_len, H, HD))
    live_keys = jnp.arange(seq_len) < length
    scale = HD ** (-0.5)
    block_rows = min(512, seq_len)

    def attend_block(query_block):
        scores = jnp.einsum('qhd,khd->hqk', query_block, keyset, precision=HIGHEST_PREC) * scale
        scores = low_back(jnp.where(live_keys[None, None, :], scores, NEG_FILL))
        weights = low(jax.nn.softmax(scores, axis=-1))
        return jnp.einsum('hqk,khd->qhd', weights, valset, precision=HIGHEST_PREC)
    mixture = lax.map(jax.checkpoint(attend_block), queries.reshape(seq_len // block_rows, block_rows, H, HD)).reshape(seq_len, width)
    merged = low_back(low(mixture))
    attended = low_back(dense(merged, w_out) + b_out)
    hidden_one = layer_norm(tokens_slot + attended, gain_one, shift_one)
    upward = low_back(dense(low(hidden_one), w_up) + b_up)
    active = low(jax.nn.gelu(upward, approximate=False))
    downward = low_back(dense(active, w_down) + b_down)
    output = layer_norm(hidden_one + downward, gain_two, shift_two)
    projected = dense(low(output), w_proj)
    return (output, projected)

def reference(tokens, lengths, w_qkv, b_qkv, w_out, b_out, ln1_gain, ln1_bias, w_up, b_up, w_down, b_down, ln2_gain, ln2_bias, w_proj, cot_out, cot_emb):
    params = tuple((array_in.astype(jnp.float32) for array_in in (w_qkv, b_qkv, w_out, b_out, ln1_gain, ln1_bias, w_up, b_up, w_down, b_down, ln2_gain, ln2_bias, w_proj)))
    inputs = tokens.astype(jnp.float32)
    live_mask = (jnp.arange(SLOT_LEN)[None, :] < lengths[:, None]).astype(jnp.float32)[:, :, None]

    def forward(values, weight_set):

        def per_slot(slot_item):
            return slot_forward(slot_item[0], slot_item[1], weight_set)
        return lax.map(per_slot, (values, lengths))
    (outputs, projected), pullback = jax.vjp(forward, inputs, params)
    grad_inputs, gradients = pullback((cot_out.astype(jnp.float32) * live_mask, cot_emb.astype(jnp.float32) * live_mask))
    return (outputs.astype(jnp.bfloat16), projected.astype(jnp.bfloat16), grad_inputs.astype(jnp.bfloat16), gradients[0], gradients[1], gradients[2], gradients[3], gradients[4], gradients[5], gradients[6], gradients[7], gradients[8], gradients[9], gradients[10], gradients[11], gradients[12])
```

```python
from functools import partial

import jax
import jax.numpy as jnp
from jax import lax
from jax.experimental import pallas as pl
from jax.experimental.pallas import tpu as pltpu
from jax.sharding import Mesh
from jax.sharding import PartitionSpec as P

H = 16
HD = 64
LN_EPS = 1e-05
NEG_FILL = -1e30
F32 = jnp.float32
BF16 = jnp.bfloat16
GROUP = ("ctx", "x", "core")
LANE = ("ctx", "x")
SWAP = [(0, 1), (1, 0)]
VMEM_LIMIT = 60 * 1024 * 1024


def mm(left, right):
    return jnp.dot(left, right, preferred_element_type=F32)


def contract(left, right, left_dim, right_dim):
    return lax.dot_general(
        left, right, (((left_dim,), (right_dim,)), ((), ())), preferred_element_type=F32
    )


def swap_core(value):
    return lax.ppermute(value, "core", SWAP)


def swap_slot(value):
    return lax.ppermute(value, "slot", SWAP)


def pick(stacked, index, axis):
    return lax.dynamic_index_in_dim(stacked, index, axis, keepdims=False)


def project_kernel(tok_ref, w_ref, b_ref, cos_ref, sin_ref, q_ref, k_ref, v_ref):
    joined = mm(tok_ref[...], w_ref[...]) + b_ref[...]
    wide = 2 * HD
    turned = joined[:, :wide] * cos_ref[...] + joined[:, wide : 2 * wide] * sin_ref[...]
    q_ref[...] = (turned[:, :HD].astype(BF16) * HD ** (-0.5)).astype(BF16)
    k_ref[...] = turned[:, HD:].astype(BF16)
    v_ref[...] = joined[:, 2 * wide :].astype(BF16)


def project(tokens, weight, bias, cosine, sine):
    rows, width = tokens.shape
    seq = cosine.shape[0]
    block = min(512, seq)
    per_slot = seq // block
    cols = weight.shape[1]
    head_out = jax.ShapeDtypeStruct((rows, HD), BF16)
    head_spec = pl.BlockSpec((block, HD), lambda i: (i, 0))
    return pl.pallas_call(
        project_kernel,
        grid=(rows // block,),
        in_specs=[
            pl.BlockSpec((block, width), lambda i: (i, 0)),
            pl.BlockSpec((width, cols), lambda i: (0, 0)),
            pl.BlockSpec((1, cols), lambda i: (0, 0)),
            pl.BlockSpec((block, 2 * HD), lambda i: (i % per_slot, 0)),
            pl.BlockSpec((block, 2 * HD), lambda i: (i % per_slot, 0)),
        ],
        out_specs=[head_spec] * 3,
        out_shape=[head_out] * 3,
        compiler_params=pltpu.CompilerParams(vmem_limit_bytes=VMEM_LIMIT),
        cost_estimate=pl.CostEstimate(
            flops=2 * rows * width * cols, bytes_accessed=2 * rows * width, transcendentals=0
        ),
        name="project",
    )(tokens, weight, bias, cosine, sine)


QB = 512
KB = 512


def forward_kernel(
    len_ref, core_ref, q_ref, k_ref, v_ref, out_ref, send_ref, norm_ref, *, part
):
    length = len_ref[pl.program_id(0)]
    core = core_ref[0]
    queries = q_ref[0]
    rows = queries.shape[0]

    def step(j, state):
        highest, total, mix = state
        start = pl.multiple_of(j * KB, KB)
        scores = contract(queries, k_ref[0, pl.ds(start, KB), :], 1, 1)
        ids = start + lax.broadcasted_iota(jnp.int32, (1, KB), 1)
        scores = jnp.where(ids < length, scores, NEG_FILL)
        higher = jnp.maximum(highest, jnp.max(scores, axis=1, keepdims=True))
        fade = jnp.exp(highest - higher)
        weights = jnp.exp(scores - higher)
        total = total * fade + jnp.sum(weights, axis=1, keepdims=True)
        mix = mix * fade + mm(weights.astype(BF16), v_ref[0, pl.ds(start, KB), :])
        return higher, total, mix

    blocks = (length + KB - 1) // KB
    highest, total, mix = lax.fori_loop(
        0,
        blocks,
        step,
        (
            jnp.full((rows, 1), NEG_FILL, F32),
            jnp.zeros((rows, 1), F32),
            jnp.zeros((rows, HD), F32),
        ),
    )
    mix = mix / total
    out_ref[0] = mix
    log_norm = jnp.broadcast_to(highest + jnp.log(total), (rows, 128))
    norm_ref[0] = jnp.transpose(log_norm)[0:1, :]
    low = mix.astype(BF16)
    for chip in range(rows // (2 * part)):
        for half in range(2):
            at = (2 * chip + half) * part
            send_ref[chip, half ^ core, 0] = low[at : at + part]


def attend(lengths, core, queries, keys, values, part):
    slots, seq, _ = queries.shape
    chips = seq // (2 * part)
    spec_q = pl.BlockSpec((1, QB, HD), lambda s, i, *_: (s, i, 0))
    spec_k = pl.BlockSpec((1, seq, HD), lambda s, i, *_: (s, 0, 0))
    return pl.pallas_call(
        partial(forward_kernel, part=part),
        grid_spec=pltpu.PrefetchScalarGridSpec(
            num_scalar_prefetch=2,
            grid=(slots, seq // QB),
            in_specs=[spec_q, spec_k, spec_k],
            out_specs=[
                spec_q,
                pl.BlockSpec(
                    (QB // (2 * part), 2, 1, part, HD), lambda s, i, *_: (i, 0, s, 0, 0)
                ),
                pl.BlockSpec((1, 1, QB), lambda s, i, *_: (s, 0, i)),
            ],
        ),
        out_shape=[
            jax.ShapeDtypeStruct((slots, seq, HD), F32),
            jax.ShapeDtypeStruct((chips, 2, slots, part, HD), BF16),
            jax.ShapeDtypeStruct((slots, 1, seq), F32),
        ],
        compiler_params=pltpu.CompilerParams(vmem_limit_bytes=VMEM_LIMIT),
        cost_estimate=pl.CostEstimate(
            flops=16 * slots * seq * seq * HD,
            bytes_accessed=8 * slots * seq * HD,
            transcendentals=slots * seq * seq,
        ),
        name="attend",
    )(lengths, core, queries, keys, values)


def backward_kernel(
    len_ref, q_ref, k_ref, v_ref, g_ref, norm_ref, dot_ref, dq_ref, dk_ref, dv_ref, dqt
):
    length = len_ref[pl.program_id(0)]
    j = pl.program_id(1)
    start = j * KB
    key_block = k_ref[0]
    value_block = v_ref[0]

    @pl.when(j == 0)
    def _():
        dqt[...] = jnp.zeros_like(dqt)

    turned = jnp.transpose(key_block.astype(F32)).astype(BF16)
    ids = start + lax.broadcasted_iota(jnp.int32, (KB, 1), 0)
    shift = jnp.where(ids < length, 0.0, NEG_FILL)

    def step(i, state):
        key_grad, value_grad = state
        at = pl.multiple_of(i * QB, QB)
        queries = q_ref[0, pl.ds(at, QB), :]
        grads = g_ref[0, pl.ds(at, QB), :]
        scores = contract(key_block, queries, 1, 1) + shift
        probs = jnp.exp(scores - norm_ref[0, :, pl.ds(at, QB)])
        grad_probs = contract(value_block, grads, 1, 1)
        grad_scores = (probs * (grad_probs - dot_ref[0, :, pl.ds(at, QB)])).astype(BF16)
        value_grad = value_grad + mm(probs.astype(BF16), grads)
        key_grad = key_grad + mm(grad_scores, queries)
        dqt[:, pl.ds(at, QB)] += mm(turned, grad_scores)
        return key_grad, value_grad

    blocks = jnp.where(start < length, (length + QB - 1) // QB, 0)
    zero = jnp.zeros((KB, HD), F32)
    key_grad, value_grad = lax.fori_loop(0, blocks, step, (zero, zero))
    dk_ref[0] = key_grad
    dv_ref[0] = value_grad

    @pl.when(j == pl.num_programs(1) - 1)
    def _():
        dq_ref[0] = jnp.transpose(dqt[...])


def attend_back(lengths, queries, keys, values, grads, norms, dots):
    slots, seq, _ = queries.shape
    whole = pl.BlockSpec((1, seq, HD), lambda s, j, *_: (s, 0, 0))
    block = pl.BlockSpec((1, KB, HD), lambda s, j, *_: (s, j, 0))
    row = pl.BlockSpec((1, 1, seq), lambda s, j, *_: (s, 0, 0))
    out = jax.ShapeDtypeStruct((slots, seq, HD), F32)
    return pl.pallas_call(
        backward_kernel,
        grid_spec=pltpu.PrefetchScalarGridSpec(
            num_scalar_prefetch=1,
            grid=(slots, seq // KB),
            in_specs=[whole, block, block, whole, row, row],
            out_specs=[whole, block, block],
            scratch_shapes=[pltpu.VMEM((HD, seq), F32)],
        ),
        out_shape=[out] * 3,
        compiler_params=pltpu.CompilerParams(vmem_limit_bytes=VMEM_LIMIT),
        cost_estimate=pl.CostEstimate(
            flops=40 * slots * seq * seq * HD,
            bytes_accessed=20 * slots * seq * HD,
            transcendentals=slots * seq * seq,
        ),
        name="attend_back",
    )(lengths, queries, keys, values, grads, norms, dots)


def norm_forward(values, gain, shift):
    center = values - jnp.mean(values, axis=-1, keepdims=True)
    spread = jnp.mean(center * center, axis=-1, keepdims=True)
    root = lax.rsqrt(spread + LN_EPS)
    unit = center * root
    return unit * gain + shift, unit, root


def norm_backward(grad, unit, root, gain):
    scaled = grad * gain
    inner = scaled - jnp.mean(scaled, axis=-1, keepdims=True)
    inner = inner - unit * jnp.mean(scaled * unit, axis=-1, keepdims=True)
    return root * inner, jnp.sum(grad * unit, axis=0), jnp.sum(grad, axis=0)


def gelu_pair(values):
    half = 0.5 + 0.5 * lax.erf(values * 0.7071067811865476)
    bell = jnp.exp(-0.5 * values * values) * 0.3989422804014327
    return values * half, half + values * bell


def rope_rows(positions):
    halfway = HD // 2
    ladder = jnp.arange(halfway, dtype=F32) * (2.0 / HD)
    frequency = jnp.power(jnp.float32(10000.0), -ladder)
    angles = positions[:, None] * frequency[None, :]
    return jnp.cos(angles), jnp.sin(angles)


def head_device(
    tokens,
    lengths,
    w_qkv,
    b_qkv,
    w_out,
    b_out,
    ln1_gain,
    ln1_bias,
    w_up,
    b_up,
    w_down,
    b_down,
    ln2_gain,
    ln2_bias,
    w_proj,
    cot_out,
    cot_emb,
):
    n_lane = lax.axis_size("ctx") * lax.axis_size("x")
    n_group = 2 * n_lane
    core = lax.axis_index("core")
    slot = lax.axis_index("slot")
    chip = lax.axis_index("ctx") * lax.axis_size("x") + lax.axis_index("x")
    me = 2 * chip + core
    slots, part, width = tokens.shape
    seq = part * n_group
    rows = slots * part
    shard = width // n_group
    ff_shard = w_down.shape[0]
    ff_half = ff_shard // 2
    proj = w_proj.shape[1]
    head_cols = 3 * HD

    small = jnp.concatenate(
        [b_qkv, b_out, ln1_gain, ln1_bias, b_up, b_down, ln2_gain, ln2_bias]
    )
    small_at = [0]
    for piece in (b_qkv, b_out, ln1_gain, ln1_bias, b_up, b_down, ln2_gain, ln2_bias):
        small_at.append(small_at[-1] + piece.shape[0])
    small_rows = -(-small.shape[0] // proj)
    small_rows = -(-small_rows // 16) * 16
    small = jnp.pad(small, (0, small_rows * proj - small.shape[0])).reshape(small_rows, proj)
    packed = lax.all_gather(jnp.concatenate([w_proj, small], axis=0), GROUP, axis=0, tiled=False)
    proj_full = packed[:, :shard].reshape(width, proj)
    smalls = packed[:, shard:].reshape(n_group, small_rows * proj).astype(F32)
    qkv_bias, out_bias, gain_one, shift_one, up_bias, down_bias, gain_two, shift_two = (
        smalls[:, a:b].reshape(-1) for a, b in zip(small_at[:-1], small_at[1:])
    )

    by_head = w_qkv.reshape(shard, 3, n_group, HD).transpose(2, 0, 1, 3)
    my_head = lax.all_to_all(by_head.reshape(n_group, shard, head_cols), GROUP, 0, 0, tiled=True)
    my_head = my_head.reshape(width, 3, HD)
    all_tokens = lax.all_gather(tokens, GROUP, axis=1, tiled=True).reshape(slots * seq, width)

    def with_swapped(joined):
        first = joined[:, 0:2]
        halves = first.reshape(-1, 2, 2, HD // 2)
        swapped = jnp.stack([-halves[:, :, 1], halves[:, :, 0]], axis=2)
        return jnp.concatenate(
            [
                first.reshape(-1, 2 * HD),
                swapped.reshape(-1, 2 * HD),
                joined[:, 2],
            ],
            axis=1,
        )

    head_weight = with_swapped(my_head)
    head_bias = with_swapped(pick(qkv_bias.reshape(1, 3, n_group, HD), me, 2))
    cosine, sine = rope_rows(jnp.arange(seq, dtype=jnp.int32).astype(F32))
    cos_wide = jnp.tile(cosine, (1, 4))
    sin_wide = jnp.tile(sine, (1, 4))
    queries, keys, values = project(all_tokens, head_weight, head_bias, cos_wide, sin_wide)
    queries, keys, values = (t.reshape(slots, seq, HD) for t in (queries, keys, values))

    def two_lanes(mine, theirs):
        low_first = jnp.stack([mine, theirs], axis=0)
        high_first = jnp.stack([theirs, mine], axis=0)
        return jnp.where(core == 0, low_first, high_first)

    out_lane = lax.all_gather(w_out, LANE, axis=0, tiled=True)
    up_split = w_up.reshape(shard, n_lane, 2, 2, ff_half)
    up_mine = pick(up_split, core, 2)
    up_theirs = swap_core(pick(up_split, 1 - core, 2))
    up_chip = two_lanes(up_mine, up_theirs).reshape(2 * shard, n_lane, 2, ff_half)
    down_split = w_down.reshape(2, ff_half, width)
    ups, downs = [], []
    for half in (slot, 1 - slot):
        up_part = pick(up_chip, half, 2).reshape(2 * shard, n_lane * ff_half)
        ups.append(lax.all_gather(up_part, LANE, axis=0, tiled=True))
        downs.append(lax.all_gather(pick(down_split, half, 0), LANE, axis=0, tiled=True))
    bias_lane = pick(up_bias.reshape(n_lane, 2, 2, ff_half), core, 1)
    up_biases = [pick(bias_lane, half, 1).reshape(-1) for half in (slot, 1 - slot)]

    qkv_split = w_qkv.reshape(shard, 3, n_lane, 2, HD)
    qkv_mine = pick(qkv_split, core, 3)
    qkv_theirs = swap_core(pick(qkv_split, 1 - core, 3))
    qkv_chip = two_lanes(qkv_mine, qkv_theirs).transpose(0, 1, 3, 2, 4)
    qkv_lane = lax.all_gather(
        qkv_chip.reshape(2 * shard, n_lane * head_cols), LANE, axis=0, tiled=True
    )

    mixture, send, norms = attend(
        lengths, core.reshape(1).astype(jnp.int32), queries, keys, values, part
    )
    merged = lax.all_to_all(send, LANE, 0, 0, tiled=True)
    merged = merged.transpose(1, 2, 3, 0, 4).reshape(2 * rows, n_lane * HD)

    def own_sum(partial_rows):
        return partial_rows[:rows] + swap_core(partial_rows[rows:])

    def both(value):
        return jnp.concatenate([value, swap_core(value)], axis=0)

    flat_tokens = tokens.reshape(rows, width).astype(F32)
    attended = own_sum(mm(merged, out_lane)) + out_bias
    hidden_one, unit_one, root_one = norm_forward(flat_tokens + attended, gain_one, shift_one)
    hidden_low = both(hidden_one.astype(BF16))

    actives, slopes = [], []
    downward = None
    for up, bias, down in zip(ups, up_biases, downs):
        active, slope = gelu_pair(mm(hidden_low, up) + bias)
        active = active.astype(BF16)
        actives.append(active)
        slopes.append(slope)
        term = mm(active, down)
        downward = term if downward is None else downward + term
    downward = own_sum(downward) + down_bias
    out_rows, unit_two, root_two = norm_forward(hidden_one + downward, gain_two, shift_two)
    out_low = out_rows.astype(BF16)
    embeds = mm(out_low, proj_full).astype(BF16)

    place = me * part + jnp.arange(part, dtype=jnp.int32)
    live = (place[None, :] < lengths[:, None]).reshape(rows, 1)
    grad_out = jnp.where(live, cot_out.reshape(rows, width).astype(F32), 0.0)
    grad_emb = jnp.where(live, cot_emb.reshape(rows, proj), 0)
    d_proj = contract(out_low, grad_emb, 0, 0)
    grad_full = grad_out + contract(grad_emb, proj_full, 1, 1)
    grad_two, d_gain_two, d_shift_two = norm_backward(grad_full, unit_two, root_two, gain_two)
    grad_down_own = grad_two.astype(BF16)
    d_down_bias = jnp.sum(grad_down_own.astype(F32), axis=0)
    grad_down = both(grad_down_own)

    d_ups, d_downs, d_up_biases = [], [], []
    grad_hidden = None
    for up, down, active, slope in zip(ups, downs, actives, slopes):
        grad_up = (contract(grad_down, down, 1, 1) * slope).astype(BF16)
        d_downs.append(contract(active, grad_down, 0, 0).astype(BF16))
        d_ups.append(contract(hidden_low, grad_up, 0, 0).astype(BF16))
        d_up_biases.append(jnp.sum(grad_up.astype(F32), axis=0))
        term = contract(grad_up, up, 1, 1)
        grad_hidden = term if grad_hidden is None else grad_hidden + term
    grad_hidden = grad_two + own_sum(grad_hidden)
    grad_one, d_gain_one, d_shift_one = norm_backward(grad_hidden, unit_one, root_one, gain_one)
    grad_att_own = grad_one.astype(BF16)
    d_out_bias = jnp.sum(grad_att_own.astype(F32), axis=0)
    grad_att = both(grad_att_own)
    grad_merged = contract(grad_att, out_lane, 1, 1).astype(BF16)
    grad_merged = grad_merged.reshape(2, slots, part, n_lane, HD).transpose(3, 0, 1, 2, 4)
    grad_heads = lax.all_to_all(grad_merged, LANE, 0, 0, tiled=True)

    def core_order(value):
        return jnp.where(core == 0, value, jnp.flip(value, axis=1))

    grad_heads = core_order(grad_heads).transpose(2, 0, 1, 3, 4).reshape(slots, seq, HD)

    half_width = width // 2
    att_split = grad_att.reshape(2 * rows, 2, half_width)
    d_outs = [
        contract(merged, pick(att_split, half, 1), 0, 0).astype(BF16)
        for half in (slot, 1 - slot)
    ]

    def reduced(pair):
        both_slots = pair[0].astype(F32) + swap_slot(pair[1]).astype(F32)
        return lax.psum_scatter(both_slots.astype(BF16), LANE, scatter_dimension=0, tiled=True)

    red_down = reduced(d_downs)
    red_up = reduced(d_ups)
    red_out = reduced(d_outs)

    def halves(mine, axis):
        theirs = swap_slot(mine)
        return jnp.where(
            slot == 0, jnp.stack([mine, theirs], axis), jnp.stack([theirs, mine], axis)
        )

    grad_w_down = halves(red_down, 0).reshape(ff_shard, width).astype(F32)
    grad_w_out = halves(red_out, 1).reshape(shard, width).astype(F32)
    up_rows = red_up.reshape(2, shard, n_lane, ff_half)
    up_keep = pick(up_rows, core, 0)
    up_got = swap_core(pick(up_rows, 1 - core, 0))
    up_lanes = jnp.where(
        core == 0, jnp.stack([up_keep, up_got], 2), jnp.stack([up_got, up_keep], 2)
    )
    grad_w_up = halves(up_lanes, 3).reshape(shard, w_up.shape[1]).astype(F32)

    up_bias_grad = jnp.stack(d_up_biases, axis=0)
    up_bias_grad = jnp.where(slot == 0, up_bias_grad, jnp.flip(up_bias_grad, axis=0))
    up_bias_grad = up_bias_grad.reshape(2, n_lane, ff_half).transpose(1, 0, 2)
    zero_lane = jnp.zeros_like(up_bias_grad)
    up_bias_grad = jnp.where(
        core == 0,
        jnp.stack([up_bias_grad, zero_lane], 1),
        jnp.stack([zero_lane, up_bias_grad], 1),
    )
    vectors = (
        d_out_bias,
        d_gain_one,
        d_shift_one,
        up_bias_grad.reshape(-1),
        d_down_bias,
        d_gain_two,
        d_shift_two,
    )
    small_grad = jnp.concatenate([v.reshape(n_group, -1) for v in vectors], axis=1)
    small_cols = small_grad.shape[1]
    vec_rows = -(-small_cols // proj)
    vec_rows = -(-vec_rows // 8) * 8
    small_grad = jnp.pad(small_grad, ((0, 0), (0, vec_rows * proj - small_cols)))
    small_grad = jnp.concatenate(
        [d_proj.reshape(n_group, shard, proj), small_grad.reshape(n_group, vec_rows, proj)], axis=1
    )
    small_red = lax.psum_scatter(
        small_grad.reshape(n_group * (shard + vec_rows), proj), GROUP, scatter_dimension=0, tiled=True
    )
    small_low = small_red.astype(BF16)
    small_sum = small_low.astype(F32) + swap_slot(small_low).astype(F32)
    grad_w_proj = small_sum[:shard]
    vec_sum = small_sum[shard:].reshape(-1)
    vec_outs = []
    at = 0
    for v in vectors:
        size = v.size // n_group
        vec_outs.append(vec_sum[at : at + size])
        at += size
    (
        grad_b_out,
        grad_gain_one,
        grad_shift_one,
        grad_b_up,
        grad_b_down,
        grad_gain_two,
        grad_shift_two,
    ) = vec_outs

    row_dots = jnp.sum(grad_heads.astype(F32) * mixture, axis=-1).reshape(slots, 1, seq)
    grad_q, grad_k, grad_v = attend_back(
        lengths, queries, keys, values, grad_heads, norms, row_dots
    )

    def turn_back(value):
        first, second = value[..., : HD // 2], value[..., HD // 2 :]
        return jnp.concatenate(
            [first * cosine + second * sine, second * cosine - first * sine], axis=-1
        )

    grad_joined = jnp.concatenate(
        [turn_back(grad_q * HD ** (-0.5)), turn_back(grad_k), grad_v], axis=-1
    ).astype(BF16)
    d_qkv = contract(all_tokens, grad_joined.reshape(slots * seq, head_cols), 0, 0)
    d_qkv_bias = jnp.sum(grad_joined.astype(F32), axis=(0, 1))
    d_qkv = jnp.concatenate(
        [
            d_qkv.reshape(n_group, shard, head_cols),
            jnp.broadcast_to(d_qkv_bias, (n_group, 16, head_cols)),
        ],
        axis=1,
    ).astype(BF16)
    d_qkv = (d_qkv.astype(F32) + swap_slot(d_qkv).astype(F32)).astype(BF16)
    d_qkv = lax.all_to_all(d_qkv, GROUP, 0, 0, tiled=True).astype(F32)
    grad_w_qkv = (
        d_qkv[:, :shard].reshape(n_group, shard, 3, HD).transpose(1, 2, 0, 3).reshape(shard, 3 * width)
    )
    qkv_bias_grad = d_qkv[:, shard].reshape(n_group, 3, HD).transpose(1, 0, 2).reshape(-1)
    grad_b_qkv = lax.dynamic_slice(qkv_bias_grad, (me * b_qkv.shape[0],), (b_qkv.shape[0],))

    to_chips = grad_joined.reshape(slots, n_lane, 2, part, head_cols).transpose(1, 2, 0, 3, 4)
    joined_rows = lax.all_to_all(core_order(to_chips), LANE, 0, 0, tiled=True)
    joined_rows = joined_rows.transpose(1, 2, 3, 0, 4).reshape(2 * rows, n_lane * head_cols)
    input_grad = own_sum(contract(joined_rows, qkv_lane, 1, 1)) + grad_one

    return (
        out_low.reshape(slots, part, width),
        embeds.reshape(slots, part, proj),
        input_grad.astype(BF16).reshape(slots, part, width),
        grad_w_qkv,
        grad_b_qkv,
        grad_w_out,
        grad_b_out,
        grad_gain_one,
        grad_shift_one,
        grad_w_up,
        grad_b_up,
        grad_w_down,
        grad_b_down,
        grad_gain_two,
        grad_shift_two,
        grad_w_proj,
    )


def layer_norm(hidden, gain, shift):
    center = hidden - jnp.mean(hidden, axis=-1, keepdims=True)
    spread = jnp.mean(center * center, axis=-1, keepdims=True)
    return center * lax.rsqrt(spread + LN_EPS) * gain + shift


def rope_tables(positions, head_width):
    halfway = head_width // 2
    ladder = jnp.arange(halfway, dtype=jnp.float32) * (2.0 / head_width)
    frequency = jnp.power(jnp.float32(10000.0), -ladder)
    angles = positions[:, None] * frequency[None, :]
    return (jnp.cos(angles)[:, None, :], jnp.sin(angles)[:, None, :])


def rotate(values, cosine, sine_part):
    halfway = values.shape[-1] // 2
    first_half = values[..., :halfway]
    second_half = values[..., halfway:]
    return jnp.concatenate(
        [
            first_half * cosine - second_half * sine_part,
            second_half * cosine + first_half * sine_part,
        ],
        axis=-1,
    )


def block_scores(query_block, key_block, key_start, length, scale):
    scores = (
        jnp.einsum("qhd,khd->hqk", query_block, key_block, preferred_element_type=jnp.float32)
        * scale
    )
    key_ids = key_start + jnp.arange(key_block.shape[0], dtype=jnp.int32)
    return jnp.where((key_ids < length)[None, None, :], scores, NEG_FILL)


def per_device(
    tokens,
    lengths,
    w_qkv,
    b_qkv,
    w_out,
    b_out,
    ln1_gain,
    ln1_bias,
    w_up,
    b_up,
    w_down,
    b_down,
    ln2_gain,
    ln2_bias,
    w_proj,
    cot_out,
    cot_emb,
):
    n_fsdp = lax.axis_size("fsdp")
    n_ctx = lax.axis_size("ctx")
    ctx_at = lax.axis_index("ctx")
    fsdp_at = lax.axis_index("fsdp")
    groups, tok_slot, width = tokens.shape
    heads_here = H // n_fsdp
    lane_width = heads_here * HD
    span_rows = tok_slot * n_fsdp
    key_count = span_rows * n_ctx
    row_count = groups * tok_slot
    scale = HD ** (-0.5)
    query_rows = min(512, span_rows)
    key_rows = min(2048, key_count // 4)
    query_blocks = span_rows // query_rows
    key_blocks = key_count // key_rows
    key_starts = jnp.arange(key_blocks, dtype=jnp.int32) * key_rows
    qkv_full, qkv_bias, out_full, out_bias, gain_one, shift_one = (
        lax.all_gather(w_qkv, ("ctx", "fsdp"), axis=0, tiled=True),
        lax.all_gather(b_qkv, ("ctx", "fsdp"), axis=0, tiled=True),
        lax.all_gather(w_out, ("ctx", "fsdp"), axis=0, tiled=True),
        lax.all_gather(b_out, ("ctx", "fsdp"), axis=0, tiled=True),
        lax.all_gather(ln1_gain, ("ctx", "fsdp"), axis=0, tiled=True),
        lax.all_gather(ln1_bias, ("ctx", "fsdp"), axis=0, tiled=True),
    )
    token_pos = (ctx_at * n_fsdp + fsdp_at) * tok_slot + jnp.arange(tok_slot, dtype=jnp.int32)
    live_rows = (token_pos[None, :] < lengths[:, None]).reshape(row_count, 1)
    flat_tokens = tokens.reshape(row_count, width)
    joined = jnp.dot(flat_tokens, qkv_full, preferred_element_type=jnp.float32) + qkv_bias.astype(
        jnp.float32
    )
    cosine, sine_part = rope_tables(token_pos.astype(jnp.float32), HD)
    split_heads = joined.reshape(groups, tok_slot, 3, H, HD)
    rotated_query = rotate(split_heads[:, :, 0], cosine, sine_part)
    rotated_key = rotate(split_heads[:, :, 1], cosine, sine_part)
    packed = (
        jnp.stack([rotated_query, rotated_key, split_heads[:, :, 2]], axis=2)
        .astype(jnp.bfloat16)
        .reshape(groups, tok_slot, 3, n_fsdp, lane_width)
    )
    by_heads = lax.all_to_all(packed, "fsdp", split_axis=3, concat_axis=1, tiled=True)
    queries = by_heads[:, :, 0, 0]
    local_keys = by_heads[:, :, 1, 0]
    local_values = by_heads[:, :, 2, 0]
    all_keys, all_values = (
        lax.all_gather(local_keys, "ctx", axis=1, tiled=True),
        lax.all_gather(local_values, "ctx", axis=1, tiled=True),
    )

    def attend_slot(slot_item):
        slot_queries, slot_keys, slot_values, length = slot_item
        query_split = slot_queries.reshape(query_blocks, query_rows, heads_here, HD)
        key_split = slot_keys.reshape(key_blocks, key_rows, heads_here, HD)
        value_split = slot_values.reshape(key_blocks, key_rows, heads_here, HD)

        def per_query(query_block):

            def row_stats(state_pair, key_item):
                highest, running_sum = state_pair
                scores = block_scores(query_block, key_item[0], key_item[1], length, scale)
                new_high = jnp.maximum(highest, jnp.max(scores, axis=-1))
                running_sum = running_sum * jnp.exp(highest - new_high) + jnp.sum(
                    jnp.exp(scores - new_high[..., None]), axis=-1
                )
                return ((new_high, running_sum), None)

            start_state = (
                jnp.full((heads_here, query_rows), NEG_FILL, jnp.float32),
                jnp.zeros((heads_here, query_rows), jnp.float32),
            )
            highest, running_sum = lax.scan(row_stats, start_state, (key_split, key_starts))[0]
            log_norm = highest + jnp.log(running_sum)

            def weigh_values(accumulated, key_item):
                scores = block_scores(query_block, key_item[0], key_item[2], length, scale)
                weights = jnp.exp(scores - log_norm[..., None]).astype(jnp.bfloat16)
                return (
                    accumulated
                    + jnp.einsum(
                        "hqk,khd->qhd", weights, key_item[1], preferred_element_type=jnp.float32
                    ),
                    None,
                )

            mixture = lax.scan(
                weigh_values,
                jnp.zeros((query_rows, heads_here, HD), jnp.float32),
                (key_split, value_split, key_starts),
            )[0]
            return (mixture, log_norm)

        mixture, log_norm = lax.map(per_query, query_split)
        return (mixture.reshape(span_rows, lane_width), log_norm)

    mixture, log_norms = lax.map(attend_slot, (queries, all_keys, all_values, lengths))
    merged = lax.all_to_all(
        mixture.astype(jnp.bfloat16).reshape(groups, span_rows, 1, lane_width),
        "fsdp",
        split_axis=1,
        concat_axis=2,
        tiled=True,
    ).reshape(row_count, width)
    attended = jnp.dot(merged, out_full, preferred_element_type=jnp.float32) + out_bias.astype(
        jnp.float32
    )
    hidden_one, pull_one = jax.vjp(
        layer_norm,
        flat_tokens.astype(jnp.float32) + attended,
        gain_one.astype(jnp.float32),
        shift_one.astype(jnp.float32),
    )
    hidden_low = hidden_one.astype(jnp.bfloat16)
    up_full, up_bias, down_full, down_bias, gain_two, shift_two, proj_full = (
        lax.all_gather(w_up, ("ctx", "fsdp"), axis=0, tiled=True),
        lax.all_gather(b_up, ("ctx", "fsdp"), axis=0, tiled=True),
        lax.all_gather(w_down, ("ctx", "fsdp"), axis=0, tiled=True),
        lax.all_gather(b_down, ("ctx", "fsdp"), axis=0, tiled=True),
        lax.all_gather(ln2_gain, ("ctx", "fsdp"), axis=0, tiled=True),
        lax.all_gather(ln2_bias, ("ctx", "fsdp"), axis=0, tiled=True),
        lax.all_gather(w_proj, ("ctx", "fsdp"), axis=0, tiled=True),
    )
    upward = jnp.dot(hidden_low, up_full, preferred_element_type=jnp.float32) + up_bias.astype(
        jnp.float32
    )
    active_full, pull_gelu = jax.vjp(partial(jax.nn.gelu, approximate=False), upward)
    active = active_full.astype(jnp.bfloat16)
    downward = jnp.dot(active, down_full, preferred_element_type=jnp.float32) + down_bias.astype(
        jnp.float32
    )
    out_full_rows, pull_two = jax.vjp(
        layer_norm,
        hidden_one + downward,
        gain_two.astype(jnp.float32),
        shift_two.astype(jnp.float32),
    )
    out_low = out_full_rows.astype(jnp.bfloat16)
    projected = jnp.dot(out_low, proj_full, preferred_element_type=jnp.float32)
    back_qkv, back_qkv_bias, back_out, back_out_bias, back_gain_one, back_shift_one = (
        lax.all_gather(w_qkv, ("ctx", "fsdp"), axis=0, tiled=True),
        lax.all_gather(b_qkv, ("ctx", "fsdp"), axis=0, tiled=True),
        lax.all_gather(w_out, ("ctx", "fsdp"), axis=0, tiled=True),
        lax.all_gather(b_out, ("ctx", "fsdp"), axis=0, tiled=True),
        lax.all_gather(ln1_gain, ("ctx", "fsdp"), axis=0, tiled=True),
        lax.all_gather(ln1_bias, ("ctx", "fsdp"), axis=0, tiled=True),
    )
    back_up, back_up_bias, back_down, back_down_bias, back_gain_two, back_shift_two, back_proj = (
        lax.all_gather(w_up, ("ctx", "fsdp"), axis=0, tiled=True),
        lax.all_gather(b_up, ("ctx", "fsdp"), axis=0, tiled=True),
        lax.all_gather(w_down, ("ctx", "fsdp"), axis=0, tiled=True),
        lax.all_gather(b_down, ("ctx", "fsdp"), axis=0, tiled=True),
        lax.all_gather(ln2_gain, ("ctx", "fsdp"), axis=0, tiled=True),
        lax.all_gather(ln2_bias, ("ctx", "fsdp"), axis=0, tiled=True),
        lax.all_gather(w_proj, ("ctx", "fsdp"), axis=0, tiled=True),
    )
    grad_out = jnp.where(live_rows, cot_out.reshape(row_count, width).astype(jnp.float32), 0.0)
    grad_emb = jnp.where(live_rows, cot_emb.reshape(row_count, -1), 0)
    d_proj = jnp.einsum("rd,rp->dp", out_low, grad_emb, preferred_element_type=jnp.float32)
    grad_full = grad_out + jnp.einsum(
        "rp,dp->rd", grad_emb, back_proj, preferred_element_type=jnp.float32
    )
    grad_two, d_gain_two, d_shift_two = pull_two(grad_full)
    grad_down = grad_two.astype(jnp.bfloat16)
    d_down = jnp.einsum("rf,rd->fd", active, grad_down, preferred_element_type=jnp.float32)
    d_down_bias = jnp.sum(grad_down.astype(jnp.float32), axis=0)
    grad_act = jnp.einsum("rd,fd->rf", grad_down, back_down, preferred_element_type=jnp.float32)
    grad_up = pull_gelu(grad_act)[0].astype(jnp.bfloat16)
    d_up = jnp.einsum("rd,rf->df", hidden_low, grad_up, preferred_element_type=jnp.float32)
    d_up_bias = jnp.sum(grad_up.astype(jnp.float32), axis=0)
    grad_hidden = grad_two + jnp.einsum(
        "rf,df->rd", grad_up, back_up, preferred_element_type=jnp.float32
    )
    grad_one, d_gain_one, d_shift_one = pull_one(grad_hidden)
    grad_att = grad_one.astype(jnp.bfloat16)
    d_out = jnp.einsum("rd,re->de", merged, grad_att, preferred_element_type=jnp.float32)
    d_out_bias = jnp.sum(grad_att.astype(jnp.float32), axis=0)
    grad_merged = jnp.einsum(
        "re,de->rd", grad_att, back_out, preferred_element_type=jnp.float32
    ).astype(jnp.bfloat16)
    grad_heads = lax.all_to_all(
        grad_merged.reshape(groups, tok_slot, n_fsdp, lane_width),
        "fsdp",
        split_axis=2,
        concat_axis=1,
        tiled=True,
    ).reshape(groups, span_rows, lane_width)

    def attend_back(slot_item):
        slot_queries, slot_keys, slot_values, grad_mix, log_norm, length = slot_item
        query_split = slot_queries.reshape(query_blocks, query_rows, heads_here, HD)
        key_split = slot_keys.reshape(key_blocks, key_rows, heads_here, HD)
        value_split = slot_values.reshape(key_blocks, key_rows, heads_here, HD)
        grad_split = grad_mix.reshape(query_blocks, query_rows, heads_here, HD)

        def value_pass(value_total, query_item):
            query_block, grad_block, norm_block = query_item

            def value_per_key(row_dot, key_item):
                key_block, value_block, key_start = key_item
                scores = block_scores(query_block, key_block, key_start, length, scale)
                probability = jnp.exp(scores - norm_block[..., None])
                grad_probs = jnp.einsum(
                    "qhd,khd->hqk", grad_block, value_block, preferred_element_type=jnp.float32
                )
                value_part = jnp.einsum(
                    "hqk,qhd->khd",
                    probability.astype(jnp.bfloat16),
                    grad_block,
                    preferred_element_type=jnp.float32,
                )
                return (row_dot + jnp.sum(probability * grad_probs, axis=-1), value_part)

            row_dot, value_parts = lax.scan(
                value_per_key,
                jnp.zeros((heads_here, query_rows), jnp.float32),
                (key_split, value_split, key_starts),
            )
            return (value_total + value_parts.reshape(key_count, heads_here, HD), row_dot)

        value_grad, row_dots = lax.scan(
            value_pass,
            jnp.zeros((key_count, heads_here, HD), jnp.float32),
            (query_split, grad_split, log_norm),
        )

        def key_pass(key_total, query_item):
            query_block, grad_block, norm_block, dot_block = query_item

            def key_per_key(query_accum, key_item):
                key_block, value_block, key_start = key_item
                scores = block_scores(query_block, key_block, key_start, length, scale)
                probability = jnp.exp(scores - norm_block[..., None])
                grad_probs = jnp.einsum(
                    "qhd,khd->hqk", grad_block, value_block, preferred_element_type=jnp.float32
                )
                grad_scores = (probability * (grad_probs - dot_block[..., None])).astype(
                    jnp.bfloat16
                )
                query_accum = query_accum + jnp.einsum(
                    "hqk,khd->qhd", grad_scores, key_block, preferred_element_type=jnp.float32
                )
                key_part = jnp.einsum(
                    "hqk,qhd->khd", grad_scores, query_block, preferred_element_type=jnp.float32
                )
                return (query_accum, key_part)

            query_grad, key_parts = lax.scan(
                key_per_key,
                jnp.zeros((query_rows, heads_here, HD), jnp.float32),
                (key_split, value_split, key_starts),
            )
            return (key_total + key_parts.reshape(key_count, heads_here, HD), query_grad)

        key_grad, query_grads = lax.scan(
            key_pass,
            jnp.zeros((key_count, heads_here, HD), jnp.float32),
            (query_split, grad_split, log_norm, row_dots),
        )
        return (
            query_grads.reshape(span_rows, lane_width) * scale,
            key_grad.reshape(key_count, lane_width) * scale,
            value_grad.reshape(key_count, lane_width),
        )

    grad_queries, key_terms, value_terms = lax.map(
        attend_back, (queries, all_keys, all_values, grad_heads, log_norms, lengths)
    )
    grad_keys, grad_values = (
        lax.psum_scatter(
            key_terms.astype(jnp.bfloat16), "ctx", scatter_dimension=1, tiled=True
        ).astype(jnp.float32),
        lax.psum_scatter(
            value_terms.astype(jnp.bfloat16), "ctx", scatter_dimension=1, tiled=True
        ).astype(jnp.float32),
    )
    head_pos = (ctx_at * span_rows + jnp.arange(span_rows, dtype=jnp.int32)).astype(jnp.float32)
    head_cosine, head_sine = rope_tables(head_pos, HD)
    query_back = rotate(
        grad_queries.reshape(groups, span_rows, heads_here, HD), head_cosine, -head_sine
    )
    key_back = rotate(grad_keys.reshape(groups, span_rows, heads_here, HD), head_cosine, -head_sine)
    value_back = grad_values.reshape(groups, span_rows, heads_here, HD)
    grad_pack = (
        jnp.stack([query_back, key_back, value_back], axis=2)
        .astype(jnp.bfloat16)
        .reshape(groups, span_rows, 3, 1, lane_width)
    )
    grad_joined = lax.all_to_all(
        grad_pack, "fsdp", split_axis=1, concat_axis=3, tiled=True
    ).reshape(row_count, 3 * width)
    d_qkv = jnp.einsum("rd,re->de", flat_tokens, grad_joined, preferred_element_type=jnp.float32)
    d_qkv_bias = jnp.sum(grad_joined.astype(jnp.float32), axis=0)
    input_grad = (
        jnp.einsum("re,de->rd", grad_joined, back_qkv, preferred_element_type=jnp.float32)
        + grad_one
    ).astype(jnp.bfloat16)
    shards = (
        lax.psum_scatter(d_qkv, ("ctx", "fsdp"), scatter_dimension=0, tiled=True),
        lax.psum_scatter(d_qkv_bias, ("ctx", "fsdp"), scatter_dimension=0, tiled=True),
        lax.psum_scatter(d_out, ("ctx", "fsdp"), scatter_dimension=0, tiled=True),
        lax.psum_scatter(d_out_bias, ("ctx", "fsdp"), scatter_dimension=0, tiled=True),
        lax.psum_scatter(d_gain_one, ("ctx", "fsdp"), scatter_dimension=0, tiled=True),
        lax.psum_scatter(d_shift_one, ("ctx", "fsdp"), scatter_dimension=0, tiled=True),
        lax.psum_scatter(d_up, ("ctx", "fsdp"), scatter_dimension=0, tiled=True),
        lax.psum_scatter(d_up_bias, ("ctx", "fsdp"), scatter_dimension=0, tiled=True),
        lax.psum_scatter(d_down, ("ctx", "fsdp"), scatter_dimension=0, tiled=True),
        lax.psum_scatter(d_down_bias, ("ctx", "fsdp"), scatter_dimension=0, tiled=True),
        lax.psum_scatter(d_gain_two, ("ctx", "fsdp"), scatter_dimension=0, tiled=True),
        lax.psum_scatter(d_shift_two, ("ctx", "fsdp"), scatter_dimension=0, tiled=True),
        lax.psum_scatter(d_proj, ("ctx", "fsdp"), scatter_dimension=0, tiled=True),
    )
    totals = (
        lax.psum(shards[0].astype(jnp.bfloat16), "slot").astype(jnp.float32),
        lax.psum(shards[1].astype(jnp.bfloat16), "slot").astype(jnp.float32),
        lax.psum(shards[2].astype(jnp.bfloat16), "slot").astype(jnp.float32),
        lax.psum(shards[3].astype(jnp.bfloat16), "slot").astype(jnp.float32),
        lax.psum(shards[4].astype(jnp.bfloat16), "slot").astype(jnp.float32),
        lax.psum(shards[5].astype(jnp.bfloat16), "slot").astype(jnp.float32),
        lax.psum(shards[6].astype(jnp.bfloat16), "slot").astype(jnp.float32),
        lax.psum(shards[7].astype(jnp.bfloat16), "slot").astype(jnp.float32),
        lax.psum(shards[8].astype(jnp.bfloat16), "slot").astype(jnp.float32),
        lax.psum(shards[9].astype(jnp.bfloat16), "slot").astype(jnp.float32),
        lax.psum(shards[10].astype(jnp.bfloat16), "slot").astype(jnp.float32),
        lax.psum(shards[11].astype(jnp.bfloat16), "slot").astype(jnp.float32),
        lax.psum(shards[12].astype(jnp.bfloat16), "slot").astype(jnp.float32),
    )
    return (
        out_low.reshape(groups, tok_slot, width),
        projected.astype(jnp.bfloat16).reshape(groups, tok_slot, -1),
        input_grad.reshape(groups, tok_slot, width),
        totals[0],
        totals[1],
        totals[2],
        totals[3],
        totals[4],
        totals[5],
        totals[6],
        totals[7],
        totals[8],
        totals[9],
        totals[10],
        totals[11],
        totals[12],
    )


def solution(mesh):
    n_slot, n_ctx, n_fsdp = (mesh.shape[a] for a in ("slot", "ctx", "fsdp"))
    rows_axes = ("ctx", "fsdp")
    step = per_device
    if n_slot == 2 and n_fsdp % 2 == 0 and n_ctx * n_fsdp == H:
        mesh = Mesh(
            mesh.devices.reshape(n_slot, n_ctx, n_fsdp // 2, 2), ("slot", "ctx", "x", "core")
        )
        rows_axes = GROUP
        step = head_device
    in_specs = (
        P("slot", rows_axes, None),
        P("slot"),
        P(rows_axes, None),
        P(rows_axes),
        P(rows_axes, None),
        P(rows_axes),
        P(rows_axes),
        P(rows_axes),
        P(rows_axes, None),
        P(rows_axes),
        P(rows_axes, None),
        P(rows_axes),
        P(rows_axes),
        P(rows_axes),
        P(rows_axes, None),
        P("slot", rows_axes, None),
        P("slot", rows_axes, None),
    )
    out_specs = (
        P("slot", rows_axes, None),
        P("slot", rows_axes, None),
        P("slot", rows_axes, None),
        P(rows_axes, None),
        P(rows_axes),
        P(rows_axes, None),
        P(rows_axes),
        P(rows_axes),
        P(rows_axes),
        P(rows_axes, None),
        P(rows_axes),
        P(rows_axes, None),
        P(rows_axes),
        P(rows_axes),
        P(rows_axes),
        P(rows_axes, None),
    )
    return jax.shard_map(
        step, mesh=mesh, in_specs=in_specs, out_specs=out_specs, check_vma=False
    )
```

```python
from functools import partial

import jax
import jax.numpy as jnp
from jax import lax
from jax.experimental import pallas as pl
from jax.experimental.pallas import tpu as pltpu
from jax.sharding import Mesh
from jax.sharding import PartitionSpec as P

H = 16
HD = 64
LN_EPS = 1e-05
NEG_FILL = -1e30
F32 = jnp.float32
BF16 = jnp.bfloat16
GROUP = ("ctx", "x", "core")
LANE = ("ctx", "x")
SWAP = [(0, 1), (1, 0)]
VMEM_LIMIT = 60 * 1024 * 1024


def mm(left, right):
    return jnp.dot(left, right, preferred_element_type=F32)


def contract(left, right, left_dim, right_dim):
    return lax.dot_general(
        left, right, (((left_dim,), (right_dim,)), ((), ())), preferred_element_type=F32
    )


def swap_core(value):
    return lax.ppermute(value, "core", SWAP)


def swap_slot(value):
    return lax.ppermute(value, "slot", SWAP)


def pick(stacked, index, axis):
    return lax.dynamic_index_in_dim(stacked, index, axis, keepdims=False)


def project_kernel(tok_ref, w_ref, b_ref, cos_ref, sin_ref, q_ref, k_ref, v_ref):
    joined = mm(tok_ref[...], w_ref[...]) + b_ref[...]
    wide = 2 * HD
    turned = joined[:, :wide] * cos_ref[...] + joined[:, wide : 2 * wide] * sin_ref[...]
    q_ref[...] = (turned[:, :HD].astype(BF16) * HD ** (-0.5)).astype(BF16)
    k_ref[...] = turned[:, HD:].astype(BF16)
    v_ref[...] = joined[:, 2 * wide :].astype(BF16)


def project(tokens, weight, bias, cosine, sine):
    rows, width = tokens.shape
    seq = cosine.shape[0]
    block = min(512, seq)
    per_slot = seq // block
    cols = weight.shape[1]
    head_out = jax.ShapeDtypeStruct((rows, HD), BF16)
    head_spec = pl.BlockSpec((block, HD), lambda i: (i, 0))
    return pl.pallas_call(
        project_kernel,
        grid=(rows // block,),
        in_specs=[
            pl.BlockSpec((block, width), lambda i: (i, 0)),
            pl.BlockSpec((width, cols), lambda i: (0, 0)),
            pl.BlockSpec((1, cols), lambda i: (0, 0)),
            pl.BlockSpec((block, 2 * HD), lambda i: (i % per_slot, 0)),
            pl.BlockSpec((block, 2 * HD), lambda i: (i % per_slot, 0)),
        ],
        out_specs=[head_spec] * 3,
        out_shape=[head_out] * 3,
        compiler_params=pltpu.CompilerParams(vmem_limit_bytes=VMEM_LIMIT),
        cost_estimate=pl.CostEstimate(
            flops=2 * rows * width * cols, bytes_accessed=2 * rows * width, transcendentals=0
        ),
        name="project",
    )(tokens, weight, bias, cosine, sine)


QB = 512
KB = 512


def forward_kernel(
    len_ref, core_ref, q_ref, k_ref, v_ref, out_ref, send_ref, norm_ref, *, part
):
    length = len_ref[pl.program_id(0)]
    core = core_ref[0]
    queries = q_ref[0]
    rows = queries.shape[0]

    def step(j, state):
        highest, total, mix = state
        start = pl.multiple_of(j * KB, KB)
        scores = contract(queries, k_ref[0, pl.ds(start, KB), :], 1, 1)
        ids = start + lax.broadcasted_iota(jnp.int32, (1, KB), 1)
        scores = jnp.where(ids < length, scores, NEG_FILL)
        higher = jnp.maximum(highest, jnp.max(scores, axis=1, keepdims=True))
        fade = jnp.exp(highest - higher)
        weights = jnp.exp(scores - higher)
        total = total * fade + jnp.sum(weights, axis=1, keepdims=True)
        mix = mix * fade + mm(weights.astype(BF16), v_ref[0, pl.ds(start, KB), :])
        return higher, total, mix

    blocks = (length + KB - 1) // KB
    highest, total, mix = lax.fori_loop(
        0,
        blocks,
        step,
        (
            jnp.full((rows, 1), NEG_FILL, F32),
            jnp.zeros((rows, 1), F32),
            jnp.zeros((rows, HD), F32),
        ),
    )
    mix = mix / total
    out_ref[0] = mix
    log_norm = jnp.broadcast_to(highest + jnp.log(total), (rows, 128))
    norm_ref[0] = jnp.transpose(log_norm)[0:1, :]
    low = mix.astype(BF16)
    for chip in range(rows // (2 * part)):
        for half in range(2):
            at = (2 * chip + half) * part
            send_ref[chip, half ^ core, 0] = low[at : at + part]


def attend(lengths, core, queries, keys, values, part):
    slots, seq, _ = queries.shape
    chips = seq // (2 * part)
    spec_q = pl.BlockSpec((1, QB, HD), lambda s, i, *_: (s, i, 0))
    spec_k = pl.BlockSpec((1, seq, HD), lambda s, i, *_: (s, 0, 0))
    return pl.pallas_call(
        partial(forward_kernel, part=part),
        grid_spec=pltpu.PrefetchScalarGridSpec(
            num_scalar_prefetch=2,
            grid=(slots, seq // QB),
            in_specs=[spec_q, spec_k, spec_k],
            out_specs=[
                spec_q,
                pl.BlockSpec(
                    (QB // (2 * part), 2, 1, part, HD), lambda s, i, *_: (i, 0, s, 0, 0)
                ),
                pl.BlockSpec((1, 1, QB), lambda s, i, *_: (s, 0, i)),
            ],
        ),
        out_shape=[
            jax.ShapeDtypeStruct((slots, seq, HD), F32),
            jax.ShapeDtypeStruct((chips, 2, slots, part, HD), BF16),
            jax.ShapeDtypeStruct((slots, 1, seq), F32),
        ],
        compiler_params=pltpu.CompilerParams(vmem_limit_bytes=VMEM_LIMIT),
        cost_estimate=pl.CostEstimate(
            flops=16 * slots * seq * seq * HD,
            bytes_accessed=8 * slots * seq * HD,
            transcendentals=slots * seq * seq,
        ),
        name="attend",
    )(lengths, core, queries, keys, values)


def backward_kernel(
    len_ref, q_ref, k_ref, v_ref, g_ref, norm_ref, dot_ref, dq_ref, dk_ref, dv_ref, dqt
):
    length = len_ref[pl.program_id(0)]
    j = pl.program_id(1)
    start = j * KB
    key_block = k_ref[0]
    value_block = v_ref[0]

    @pl.when(j == 0)
    def _():
        dqt[...] = jnp.zeros_like(dqt)

    turned = jnp.transpose(key_block.astype(F32)).astype(BF16)
    ids = start + lax.broadcasted_iota(jnp.int32, (KB, 1), 0)
    shift = jnp.where(ids < length, 0.0, NEG_FILL)

    def step(i, state):
        key_grad, value_grad = state
        at = pl.multiple_of(i * QB, QB)
        queries = q_ref[0, pl.ds(at, QB), :]
        grads = g_ref[0, pl.ds(at, QB), :]
        scores = contract(key_block, queries, 1, 1) + shift
        probs = jnp.exp(scores - norm_ref[0, :, pl.ds(at, QB)])
        grad_probs = contract(value_block, grads, 1, 1)
        grad_scores = (probs * (grad_probs - dot_ref[0, :, pl.ds(at, QB)])).astype(BF16)
        value_grad = value_grad + mm(probs.astype(BF16), grads)
        key_grad = key_grad + mm(grad_scores, queries)
        dqt[:, pl.ds(at, QB)] += mm(turned, grad_scores)
        return key_grad, value_grad

    blocks = jnp.where(start < length, (length + QB - 1) // QB, 0)
    zero = jnp.zeros((KB, HD), F32)
    key_grad, value_grad = lax.fori_loop(0, blocks, step, (zero, zero))
    dk_ref[0] = key_grad
    dv_ref[0] = value_grad

    @pl.when(j == pl.num_programs(1) - 1)
    def _():
        dq_ref[0] = jnp.transpose(dqt[...])


def attend_back(lengths, queries, keys, values, grads, norms, dots):
    slots, seq, _ = queries.shape
    whole = pl.BlockSpec((1, seq, HD), lambda s, j, *_: (s, 0, 0))
    block = pl.BlockSpec((1, KB, HD), lambda s, j, *_: (s, j, 0))
    row = pl.BlockSpec((1, 1, seq), lambda s, j, *_: (s, 0, 0))
    out = jax.ShapeDtypeStruct((slots, seq, HD), F32)
    return pl.pallas_call(
        backward_kernel,
        grid_spec=pltpu.PrefetchScalarGridSpec(
            num_scalar_prefetch=1,
            grid=(slots, seq // KB),
            in_specs=[whole, block, block, whole, row, row],
            out_specs=[whole, block, block],
            scratch_shapes=[pltpu.VMEM((HD, seq), F32)],
        ),
        out_shape=[out] * 3,
        compiler_params=pltpu.CompilerParams(vmem_limit_bytes=VMEM_LIMIT),
        cost_estimate=pl.CostEstimate(
            flops=40 * slots * seq * seq * HD,
            bytes_accessed=20 * slots * seq * HD,
            transcendentals=slots * seq * seq,
        ),
        name="attend_back",
    )(lengths, queries, keys, values, grads, norms, dots)


def norm_forward(values, gain, shift):
    center = values - jnp.mean(values, axis=-1, keepdims=True)
    spread = jnp.mean(center * center, axis=-1, keepdims=True)
    root = lax.rsqrt(spread + LN_EPS)
    unit = center * root
    return unit * gain + shift, unit, root


def norm_backward(grad, unit, root, gain):
    scaled = grad * gain
    inner = scaled - jnp.mean(scaled, axis=-1, keepdims=True)
    inner = inner - unit * jnp.mean(scaled * unit, axis=-1, keepdims=True)
    return root * inner, jnp.sum(grad * unit, axis=0), jnp.sum(grad, axis=0)


def gelu_pair(values):
    half = 0.5 + 0.5 * lax.erf(values * 0.7071067811865476)
    bell = jnp.exp(-0.5 * values * values) * 0.3989422804014327
    return values * half, half + values * bell


def rope_rows(positions):
    halfway = HD // 2
    ladder = jnp.arange(halfway, dtype=F32) * (2.0 / HD)
    frequency = jnp.power(jnp.float32(10000.0), -ladder)
    angles = positions[:, None] * frequency[None, :]
    return jnp.cos(angles), jnp.sin(angles)


def head_device(
    tokens,
    lengths,
    w_qkv,
    b_qkv,
    w_out,
    b_out,
    ln1_gain,
    ln1_bias,
    w_up,
    b_up,
    w_down,
    b_down,
    ln2_gain,
    ln2_bias,
    w_proj,
    cot_out,
    cot_emb,
):
    n_lane = lax.axis_size("ctx") * lax.axis_size("x")
    n_group = 2 * n_lane
    core = lax.axis_index("core")
    slot = lax.axis_index("slot")
    chip = lax.axis_index("ctx") * lax.axis_size("x") + lax.axis_index("x")
    me = 2 * chip + core
    slots, part, width = tokens.shape
    seq = part * n_group
    rows = slots * part
    shard = width // n_group
    ff_shard = w_down.shape[0]
    ff_half = ff_shard // 2
    proj = w_proj.shape[1]
    head_cols = 3 * HD

    small = jnp.concatenate(
        [b_qkv, b_out, ln1_gain, ln1_bias, b_up, b_down, ln2_gain, ln2_bias]
    )
    small_at = [0]
    for piece in (b_qkv, b_out, ln1_gain, ln1_bias, b_up, b_down, ln2_gain, ln2_bias):
        small_at.append(small_at[-1] + piece.shape[0])
    small_rows = -(-small.shape[0] // proj)
    small_rows = -(-small_rows // 16) * 16
    small = jnp.pad(small, (0, small_rows * proj - small.shape[0])).reshape(small_rows, proj)
    packed = lax.all_gather(jnp.concatenate([w_proj, small], axis=0), GROUP, axis=0, tiled=False)
    proj_full = packed[:, :shard].reshape(width, proj)
    smalls = packed[:, shard:].reshape(n_group, small_rows * proj).astype(F32)
    qkv_bias, out_bias, gain_one, shift_one, up_bias, down_bias, gain_two, shift_two = (
        smalls[:, a:b].reshape(-1) for a, b in zip(small_at[:-1], small_at[1:])
    )

    by_head = w_qkv.reshape(shard, 3, n_group, HD).transpose(2, 0, 1, 3)
    my_head = lax.all_to_all(by_head.reshape(n_group, shard, head_cols), GROUP, 0, 0, tiled=True)
    my_head = my_head.reshape(width, 3, HD)
    all_tokens = lax.all_gather(tokens, GROUP, axis=1, tiled=True).reshape(slots * seq, width)

    def with_swapped(joined):
        first = joined[:, 0:2]
        halves = first.reshape(-1, 2, 2, HD // 2)
        swapped = jnp.stack([-halves[:, :, 1], halves[:, :, 0]], axis=2)
        return jnp.concatenate(
            [
                first.reshape(-1, 2 * HD),
                swapped.reshape(-1, 2 * HD),
                joined[:, 2],
            ],
            axis=1,
        )

    head_weight = with_swapped(my_head)
    head_bias = with_swapped(pick(qkv_bias.reshape(1, 3, n_group, HD), me, 2))
    cosine, sine = rope_rows(jnp.arange(seq, dtype=jnp.int32).astype(F32))
    cos_wide = jnp.tile(cosine, (1, 4))
    sin_wide = jnp.tile(sine, (1, 4))
    queries, keys, values = project(all_tokens, head_weight, head_bias, cos_wide, sin_wide)
    queries, keys, values = (t.reshape(slots, seq, HD) for t in (queries, keys, values))

    def two_lanes(mine, theirs):
        low_first = jnp.stack([mine, theirs], axis=0)
        high_first = jnp.stack([theirs, mine], axis=0)
        return jnp.where(core == 0, low_first, high_first)

    out_lane = lax.all_gather(w_out, LANE, axis=0, tiled=True)
    up_split = w_up.reshape(shard, n_lane, 2, 2, ff_half)
    up_mine = pick(up_split, core, 2)
    up_theirs = swap_core(pick(up_split, 1 - core, 2))
    up_chip = two_lanes(up_mine, up_theirs).reshape(2 * shard, n_lane, 2, ff_half)
    down_split = w_down.reshape(2, ff_half, width)
    up_part = pick(up_chip, slot, 2).reshape(2 * shard, n_lane * ff_half)
    up = lax.all_gather(up_part, LANE, axis=0, tiled=True)
    down = lax.all_gather(pick(down_split, slot, 0), LANE, axis=0, tiled=True)
    bias_lane = pick(up_bias.reshape(n_lane, 2, 2, ff_half), core, 1)
    up_bias_own = pick(bias_lane, slot, 1).reshape(-1)

    qkv_split = w_qkv.reshape(shard, 3, n_lane, 2, HD)
    qkv_mine = pick(qkv_split, core, 3)
    qkv_theirs = swap_core(pick(qkv_split, 1 - core, 3))
    qkv_chip = two_lanes(qkv_mine, qkv_theirs).transpose(0, 1, 3, 2, 4)
    qkv_lane = lax.all_gather(
        qkv_chip.reshape(2 * shard, n_lane * head_cols), LANE, axis=0, tiled=True
    )

    mixture, send, norms = attend(
        lengths, core.reshape(1).astype(jnp.int32), queries, keys, values, part
    )
    merged = lax.all_to_all(send, LANE, 0, 0, tiled=True)
    merged = merged.transpose(1, 2, 3, 0, 4).reshape(2 * rows, n_lane * HD)

    def own_sum(partial_rows):
        return partial_rows[:rows] + swap_core(partial_rows[rows:])

    def both(value):
        return jnp.concatenate([value, swap_core(value)], axis=0)

    def quad(value):
        pair = jnp.concatenate([value, swap_slot(value)], axis=0)
        return jnp.concatenate([pair, swap_core(pair)], axis=0)

    def quad_sum(partial_rows):
        pair = partial_rows[: 2 * rows] + swap_core(partial_rows[2 * rows :])
        return pair[:rows] + swap_slot(pair[rows:].astype(BF16)).astype(F32)

    flat_tokens = tokens.reshape(rows, width).astype(F32)
    attended = own_sum(mm(merged, out_lane)) + out_bias
    hidden_one, unit_one, root_one = norm_forward(flat_tokens + attended, gain_one, shift_one)
    hidden_low = quad(hidden_one.astype(BF16))

    active, slope = gelu_pair(mm(hidden_low, up) + up_bias_own)
    active = active.astype(BF16)
    downward = quad_sum(mm(active, down)) + down_bias
    out_rows, unit_two, root_two = norm_forward(hidden_one + downward, gain_two, shift_two)
    out_low = out_rows.astype(BF16)
    embeds = mm(out_low, proj_full).astype(BF16)

    place = me * part + jnp.arange(part, dtype=jnp.int32)
    live = (place[None, :] < lengths[:, None]).reshape(rows, 1)
    grad_out = jnp.where(live, cot_out.reshape(rows, width).astype(F32), 0.0)
    grad_emb = jnp.where(live, cot_emb.reshape(rows, proj), 0)
    d_proj = contract(out_low, grad_emb, 0, 0)
    grad_full = grad_out + contract(grad_emb, proj_full, 1, 1)
    grad_two, d_gain_two, d_shift_two = norm_backward(grad_full, unit_two, root_two, gain_two)
    grad_down_own = grad_two.astype(BF16)
    d_down_bias = jnp.sum(grad_down_own.astype(F32), axis=0)
    grad_down = quad(grad_down_own)
    grad_up = (contract(grad_down, down, 1, 1) * slope).astype(BF16)
    d_down = contract(active, grad_down, 0, 0).astype(BF16)
    d_up = contract(hidden_low, grad_up, 0, 0).astype(BF16)
    up_bias_own_grad = jnp.sum(grad_up.astype(F32), axis=0)
    grad_hidden = grad_two + quad_sum(contract(grad_up, up, 1, 1))
    grad_one, d_gain_one, d_shift_one = norm_backward(grad_hidden, unit_one, root_one, gain_one)
    grad_att_own = grad_one.astype(BF16)
    d_out_bias = jnp.sum(grad_att_own.astype(F32), axis=0)
    grad_att = both(grad_att_own)
    grad_merged = contract(grad_att, out_lane, 1, 1).astype(BF16)
    grad_merged = grad_merged.reshape(2, slots, part, n_lane, HD).transpose(3, 0, 1, 2, 4)
    grad_heads = lax.all_to_all(grad_merged, LANE, 0, 0, tiled=True)

    def core_order(value):
        return jnp.where(core == 0, value, jnp.flip(value, axis=1))

    grad_heads = core_order(grad_heads).transpose(2, 0, 1, 3, 4).reshape(slots, seq, HD)

    half_width = width // 2
    att_split = grad_att.reshape(2 * rows, 2, half_width)
    d_outs = [
        contract(merged, pick(att_split, half, 1), 0, 0).astype(BF16)
        for half in (slot, 1 - slot)
    ]

    def reduced(pair):
        both_slots = pair[0].astype(F32) + swap_slot(pair[1]).astype(F32)
        return lax.psum_scatter(both_slots.astype(BF16), LANE, scatter_dimension=0, tiled=True)

    red_down = lax.psum_scatter(d_down, LANE, scatter_dimension=0, tiled=True)
    red_up = lax.psum_scatter(d_up, LANE, scatter_dimension=0, tiled=True)
    red_out = reduced(d_outs)

    def halves(mine, axis):
        theirs = swap_slot(mine)
        return jnp.where(
            slot == 0, jnp.stack([mine, theirs], axis), jnp.stack([theirs, mine], axis)
        )

    grad_w_down = halves(red_down, 0).reshape(ff_shard, width).astype(F32)
    grad_w_out = halves(red_out, 1).reshape(shard, width).astype(F32)
    up_rows = red_up.reshape(2, shard, n_lane, ff_half)
    up_keep = pick(up_rows, core, 0)
    up_got = swap_core(pick(up_rows, 1 - core, 0))
    up_lanes = jnp.where(
        core == 0, jnp.stack([up_keep, up_got], 2), jnp.stack([up_got, up_keep], 2)
    )
    grad_w_up = halves(up_lanes, 3).reshape(shard, w_up.shape[1]).astype(F32)

    spread = (
        (jnp.arange(2) == core)[:, None, None] & (jnp.arange(2) == slot)[None, :, None]
    ).astype(F32)
    up_bias_grad = up_bias_own_grad.reshape(n_lane, 1, 1, ff_half) * spread[None]
    vectors = (
        d_out_bias,
        d_gain_one,
        d_shift_one,
        up_bias_grad.reshape(-1),
        d_down_bias,
        d_gain_two,
        d_shift_two,
    )
    small_grad = jnp.concatenate([v.reshape(n_group, -1) for v in vectors], axis=1)
    small_cols = small_grad.shape[1]
    vec_rows = -(-small_cols // proj)
    vec_rows = -(-vec_rows // 8) * 8
    small_grad = jnp.pad(small_grad, ((0, 0), (0, vec_rows * proj - small_cols)))
    small_grad = jnp.concatenate(
        [d_proj.reshape(n_group, shard, proj), small_grad.reshape(n_group, vec_rows, proj)], axis=1
    )
    small_red = lax.psum_scatter(
        small_grad.reshape(n_group * (shard + vec_rows), proj), GROUP, scatter_dimension=0, tiled=True
    )
    small_low = small_red.astype(BF16)
    small_sum = small_low.astype(F32) + swap_slot(small_low).astype(F32)
    grad_w_proj = small_sum[:shard]
    vec_sum = small_sum[shard:].reshape(-1)
    vec_outs = []
    at = 0
    for v in vectors:
        size = v.size // n_group
        vec_outs.append(vec_sum[at : at + size])
        at += size
    (
        grad_b_out,
        grad_gain_one,
        grad_shift_one,
        grad_b_up,
        grad_b_down,
        grad_gain_two,
        grad_shift_two,
    ) = vec_outs

    row_dots = jnp.sum(grad_heads.astype(F32) * mixture, axis=-1).reshape(slots, 1, seq)
    grad_q, grad_k, grad_v = attend_back(
        lengths, queries, keys, values, grad_heads, norms, row_dots
    )

    def turn_back(value):
        first, second = value[..., : HD // 2], value[..., HD // 2 :]
        return jnp.concatenate(
            [first * cosine + second * sine, second * cosine - first * sine], axis=-1
        )

    grad_joined = jnp.concatenate(
        [turn_back(grad_q * HD ** (-0.5)), turn_back(grad_k), grad_v], axis=-1
    ).astype(BF16)
    d_qkv = contract(all_tokens, grad_joined.reshape(slots * seq, head_cols), 0, 0)
    d_qkv_bias = jnp.sum(grad_joined.astype(F32), axis=(0, 1))
    d_qkv = jnp.concatenate(
        [
            d_qkv.reshape(n_group, shard, head_cols),
            jnp.broadcast_to(d_qkv_bias, (n_group, 16, head_cols)),
        ],
        axis=1,
    ).astype(BF16)
    d_qkv = (d_qkv.astype(F32) + swap_slot(d_qkv).astype(F32)).astype(BF16)
    d_qkv = lax.all_to_all(d_qkv, GROUP, 0, 0, tiled=True).astype(F32)
    grad_w_qkv = (
        d_qkv[:, :shard].reshape(n_group, shard, 3, HD).transpose(1, 2, 0, 3).reshape(shard, 3 * width)
    )
    qkv_bias_grad = d_qkv[:, shard].reshape(n_group, 3, HD).transpose(1, 0, 2).reshape(-1)
    grad_b_qkv = lax.dynamic_slice(qkv_bias_grad, (me * b_qkv.shape[0],), (b_qkv.shape[0],))

    to_chips = grad_joined.reshape(slots, n_lane, 2, part, head_cols).transpose(1, 2, 0, 3, 4)
    joined_rows = lax.all_to_all(core_order(to_chips), LANE, 0, 0, tiled=True)
    joined_rows = joined_rows.transpose(1, 2, 3, 0, 4).reshape(2 * rows, n_lane * head_cols)
    input_grad = own_sum(contract(joined_rows, qkv_lane, 1, 1)) + grad_one

    return (
        out_low.reshape(slots, part, width),
        embeds.reshape(slots, part, proj),
        input_grad.astype(BF16).reshape(slots, part, width),
        grad_w_qkv,
        grad_b_qkv,
        grad_w_out,
        grad_b_out,
        grad_gain_one,
        grad_shift_one,
        grad_w_up,
        grad_b_up,
        grad_w_down,
        grad_b_down,
        grad_gain_two,
        grad_shift_two,
        grad_w_proj,
    )


def layer_norm(hidden, gain, shift):
    center = hidden - jnp.mean(hidden, axis=-1, keepdims=True)
    spread = jnp.mean(center * center, axis=-1, keepdims=True)
    return center * lax.rsqrt(spread + LN_EPS) * gain + shift


def rope_tables(positions, head_width):
    halfway = head_width // 2
    ladder = jnp.arange(halfway, dtype=jnp.float32) * (2.0 / head_width)
    frequency = jnp.power(jnp.float32(10000.0), -ladder)
    angles = positions[:, None] * frequency[None, :]
    return (jnp.cos(angles)[:, None, :], jnp.sin(angles)[:, None, :])


def rotate(values, cosine, sine_part):
    halfway = values.shape[-1] // 2
    first_half = values[..., :halfway]
    second_half = values[..., halfway:]
    return jnp.concatenate(
        [
            first_half * cosine - second_half * sine_part,
            second_half * cosine + first_half * sine_part,
        ],
        axis=-1,
    )


def block_scores(query_block, key_block, key_start, length, scale):
    scores = (
        jnp.einsum("qhd,khd->hqk", query_block, key_block, preferred_element_type=jnp.float32)
        * scale
    )
    key_ids = key_start + jnp.arange(key_block.shape[0], dtype=jnp.int32)
    return jnp.where((key_ids < length)[None, None, :], scores, NEG_FILL)


def per_device(
    tokens,
    lengths,
    w_qkv,
    b_qkv,
    w_out,
    b_out,
    ln1_gain,
    ln1_bias,
    w_up,
    b_up,
    w_down,
    b_down,
    ln2_gain,
    ln2_bias,
    w_proj,
    cot_out,
    cot_emb,
):
    n_fsdp = lax.axis_size("fsdp")
    n_ctx = lax.axis_size("ctx")
    ctx_at = lax.axis_index("ctx")
    fsdp_at = lax.axis_index("fsdp")
    groups, tok_slot, width = tokens.shape
    heads_here = H // n_fsdp
    lane_width = heads_here * HD
    span_rows = tok_slot * n_fsdp
    key_count = span_rows * n_ctx
    row_count = groups * tok_slot
    scale = HD ** (-0.5)
    query_rows = min(512, span_rows)
    key_rows = min(2048, key_count // 4)
    query_blocks = span_rows // query_rows
    key_blocks = key_count // key_rows
    key_starts = jnp.arange(key_blocks, dtype=jnp.int32) * key_rows
    qkv_full, qkv_bias, out_full, out_bias, gain_one, shift_one = (
        lax.all_gather(w_qkv, ("ctx", "fsdp"), axis=0, tiled=True),
        lax.all_gather(b_qkv, ("ctx", "fsdp"), axis=0, tiled=True),
        lax.all_gather(w_out, ("ctx", "fsdp"), axis=0, tiled=True),
        lax.all_gather(b_out, ("ctx", "fsdp"), axis=0, tiled=True),
        lax.all_gather(ln1_gain, ("ctx", "fsdp"), axis=0, tiled=True),
        lax.all_gather(ln1_bias, ("ctx", "fsdp"), axis=0, tiled=True),
    )
    token_pos = (ctx_at * n_fsdp + fsdp_at) * tok_slot + jnp.arange(tok_slot, dtype=jnp.int32)
    live_rows = (token_pos[None, :] < lengths[:, None]).reshape(row_count, 1)
    flat_tokens = tokens.reshape(row_count, width)
    joined = jnp.dot(flat_tokens, qkv_full, preferred_element_type=jnp.float32) + qkv_bias.astype(
        jnp.float32
    )
    cosine, sine_part = rope_tables(token_pos.astype(jnp.float32), HD)
    split_heads = joined.reshape(groups, tok_slot, 3, H, HD)
    rotated_query = rotate(split_heads[:, :, 0], cosine, sine_part)
    rotated_key = rotate(split_heads[:, :, 1], cosine, sine_part)
    packed = (
        jnp.stack([rotated_query, rotated_key, split_heads[:, :, 2]], axis=2)
        .astype(jnp.bfloat16)
        .reshape(groups, tok_slot, 3, n_fsdp, lane_width)
    )
    by_heads = lax.all_to_all(packed, "fsdp", split_axis=3, concat_axis=1, tiled=True)
    queries = by_heads[:, :, 0, 0]
    local_keys = by_heads[:, :, 1, 0]
    local_values = by_heads[:, :, 2, 0]
    all_keys, all_values = (
        lax.all_gather(local_keys, "ctx", axis=1, tiled=True),
        lax.all_gather(local_values, "ctx", axis=1, tiled=True),
    )

    def attend_slot(slot_item):
        slot_queries, slot_keys, slot_values, length = slot_item
        query_split = slot_queries.reshape(query_blocks, query_rows, heads_here, HD)
        key_split = slot_keys.reshape(key_blocks, key_rows, heads_here, HD)
        value_split = slot_values.reshape(key_blocks, key_rows, heads_here, HD)

        def per_query(query_block):

            def row_stats(state_pair, key_item):
                highest, running_sum = state_pair
                scores = block_scores(query_block, key_item[0], key_item[1], length, scale)
                new_high = jnp.maximum(highest, jnp.max(scores, axis=-1))
                running_sum = running_sum * jnp.exp(highest - new_high) + jnp.sum(
                    jnp.exp(scores - new_high[..., None]), axis=-1
                )
                return ((new_high, running_sum), None)

            start_state = (
                jnp.full((heads_here, query_rows), NEG_FILL, jnp.float32),
                jnp.zeros((heads_here, query_rows), jnp.float32),
            )
            highest, running_sum = lax.scan(row_stats, start_state, (key_split, key_starts))[0]
            log_norm = highest + jnp.log(running_sum)

            def weigh_values(accumulated, key_item):
                scores = block_scores(query_block, key_item[0], key_item[2], length, scale)
                weights = jnp.exp(scores - log_norm[..., None]).astype(jnp.bfloat16)
                return (
                    accumulated
                    + jnp.einsum(
                        "hqk,khd->qhd", weights, key_item[1], preferred_element_type=jnp.float32
                    ),
                    None,
                )

            mixture = lax.scan(
                weigh_values,
                jnp.zeros((query_rows, heads_here, HD), jnp.float32),
                (key_split, value_split, key_starts),
            )[0]
            return (mixture, log_norm)

        mixture, log_norm = lax.map(per_query, query_split)
        return (mixture.reshape(span_rows, lane_width), log_norm)

    mixture, log_norms = lax.map(attend_slot, (queries, all_keys, all_values, lengths))
    merged = lax.all_to_all(
        mixture.astype(jnp.bfloat16).reshape(groups, span_rows, 1, lane_width),
        "fsdp",
        split_axis=1,
        concat_axis=2,
        tiled=True,
    ).reshape(row_count, width)
    attended = jnp.dot(merged, out_full, preferred_element_type=jnp.float32) + out_bias.astype(
        jnp.float32
    )
    hidden_one, pull_one = jax.vjp(
        layer_norm,
        flat_tokens.astype(jnp.float32) + attended,
        gain_one.astype(jnp.float32),
        shift_one.astype(jnp.float32),
    )
    hidden_low = hidden_one.astype(jnp.bfloat16)
    up_full, up_bias, down_full, down_bias, gain_two, shift_two, proj_full = (
        lax.all_gather(w_up, ("ctx", "fsdp"), axis=0, tiled=True),
        lax.all_gather(b_up, ("ctx", "fsdp"), axis=0, tiled=True),
        lax.all_gather(w_down, ("ctx", "fsdp"), axis=0, tiled=True),
        lax.all_gather(b_down, ("ctx", "fsdp"), axis=0, tiled=True),
        lax.all_gather(ln2_gain, ("ctx", "fsdp"), axis=0, tiled=True),
        lax.all_gather(ln2_bias, ("ctx", "fsdp"), axis=0, tiled=True),
        lax.all_gather(w_proj, ("ctx", "fsdp"), axis=0, tiled=True),
    )
    upward = jnp.dot(hidden_low, up_full, preferred_element_type=jnp.float32) + up_bias.astype(
        jnp.float32
    )
    active_full, pull_gelu = jax.vjp(partial(jax.nn.gelu, approximate=False), upward)
    active = active_full.astype(jnp.bfloat16)
    downward = jnp.dot(active, down_full, preferred_element_type=jnp.float32) + down_bias.astype(
        jnp.float32
    )
    out_full_rows, pull_two = jax.vjp(
        layer_norm,
        hidden_one + downward,
        gain_two.astype(jnp.float32),
        shift_two.astype(jnp.float32),
    )
    out_low = out_full_rows.astype(jnp.bfloat16)
    projected = jnp.dot(out_low, proj_full, preferred_element_type=jnp.float32)
    back_qkv, back_qkv_bias, back_out, back_out_bias, back_gain_one, back_shift_one = (
        lax.all_gather(w_qkv, ("ctx", "fsdp"), axis=0, tiled=True),
        lax.all_gather(b_qkv, ("ctx", "fsdp"), axis=0, tiled=True),
        lax.all_gather(w_out, ("ctx", "fsdp"), axis=0, tiled=True),
        lax.all_gather(b_out, ("ctx", "fsdp"), axis=0, tiled=True),
        lax.all_gather(ln1_gain, ("ctx", "fsdp"), axis=0, tiled=True),
        lax.all_gather(ln1_bias, ("ctx", "fsdp"), axis=0, tiled=True),
    )
    back_up, back_up_bias, back_down, back_down_bias, back_gain_two, back_shift_two, back_proj = (
        lax.all_gather(w_up, ("ctx", "fsdp"), axis=0, tiled=True),
        lax.all_gather(b_up, ("ctx", "fsdp"), axis=0, tiled=True),
        lax.all_gather(w_down, ("ctx", "fsdp"), axis=0, tiled=True),
        lax.all_gather(b_down, ("ctx", "fsdp"), axis=0, tiled=True),
        lax.all_gather(ln2_gain, ("ctx", "fsdp"), axis=0, tiled=True),
        lax.all_gather(ln2_bias, ("ctx", "fsdp"), axis=0, tiled=True),
        lax.all_gather(w_proj, ("ctx", "fsdp"), axis=0, tiled=True),
    )
    grad_out = jnp.where(live_rows, cot_out.reshape(row_count, width).astype(jnp.float32), 0.0)
    grad_emb = jnp.where(live_rows, cot_emb.reshape(row_count, -1), 0)
    d_proj = jnp.einsum("rd,rp->dp", out_low, grad_emb, preferred_element_type=jnp.float32)
    grad_full = grad_out + jnp.einsum(
        "rp,dp->rd", grad_emb, back_proj, preferred_element_type=jnp.float32
    )
    grad_two, d_gain_two, d_shift_two = pull_two(grad_full)
    grad_down = grad_two.astype(jnp.bfloat16)
    d_down = jnp.einsum("rf,rd->fd", active, grad_down, preferred_element_type=jnp.float32)
    d_down_bias = jnp.sum(grad_down.astype(jnp.float32), axis=0)
    grad_act = jnp.einsum("rd,fd->rf", grad_down, back_down, preferred_element_type=jnp.float32)
    grad_up = pull_gelu(grad_act)[0].astype(jnp.bfloat16)
    d_up = jnp.einsum("rd,rf->df", hidden_low, grad_up, preferred_element_type=jnp.float32)
    d_up_bias = jnp.sum(grad_up.astype(jnp.float32), axis=0)
    grad_hidden = grad_two + jnp.einsum(
        "rf,df->rd", grad_up, back_up, preferred_element_type=jnp.float32
    )
    grad_one, d_gain_one, d_shift_one = pull_one(grad_hidden)
    grad_att = grad_one.astype(jnp.bfloat16)
    d_out = jnp.einsum("rd,re->de", merged, grad_att, preferred_element_type=jnp.float32)
    d_out_bias = jnp.sum(grad_att.astype(jnp.float32), axis=0)
    grad_merged = jnp.einsum(
        "re,de->rd", grad_att, back_out, preferred_element_type=jnp.float32
    ).astype(jnp.bfloat16)
    grad_heads = lax.all_to_all(
        grad_merged.reshape(groups, tok_slot, n_fsdp, lane_width),
        "fsdp",
        split_axis=2,
        concat_axis=1,
        tiled=True,
    ).reshape(groups, span_rows, lane_width)

    def attend_back(slot_item):
        slot_queries, slot_keys, slot_values, grad_mix, log_norm, length = slot_item
        query_split = slot_queries.reshape(query_blocks, query_rows, heads_here, HD)
        key_split = slot_keys.reshape(key_blocks, key_rows, heads_here, HD)
        value_split = slot_values.reshape(key_blocks, key_rows, heads_here, HD)
        grad_split = grad_mix.reshape(query_blocks, query_rows, heads_here, HD)

        def value_pass(value_total, query_item):
            query_block, grad_block, norm_block = query_item

            def value_per_key(row_dot, key_item):
                key_block, value_block, key_start = key_item
                scores = block_scores(query_block, key_block, key_start, length, scale)
                probability = jnp.exp(scores - norm_block[..., None])
                grad_probs = jnp.einsum(
                    "qhd,khd->hqk", grad_block, value_block, preferred_element_type=jnp.float32
                )
                value_part = jnp.einsum(
                    "hqk,qhd->khd",
                    probability.astype(jnp.bfloat16),
                    grad_block,
                    preferred_element_type=jnp.float32,
                )
                return (row_dot + jnp.sum(probability * grad_probs, axis=-1), value_part)

            row_dot, value_parts = lax.scan(
                value_per_key,
                jnp.zeros((heads_here, query_rows), jnp.float32),
                (key_split, value_split, key_starts),
            )
            return (value_total + value_parts.reshape(key_count, heads_here, HD), row_dot)

        value_grad, row_dots = lax.scan(
            value_pass,
            jnp.zeros((key_count, heads_here, HD), jnp.float32),
            (query_split, grad_split, log_norm),
        )

        def key_pass(key_total, query_item):
            query_block, grad_block, norm_block, dot_block = query_item

            def key_per_key(query_accum, key_item):
                key_block, value_block, key_start = key_item
                scores = block_scores(query_block, key_block, key_start, length, scale)
                probability = jnp.exp(scores - norm_block[..., None])
                grad_probs = jnp.einsum(
                    "qhd,khd->hqk", grad_block, value_block, preferred_element_type=jnp.float32
                )
                grad_scores = (probability * (grad_probs - dot_block[..., None])).astype(
                    jnp.bfloat16
                )
                query_accum = query_accum + jnp.einsum(
                    "hqk,khd->qhd", grad_scores, key_block, preferred_element_type=jnp.float32
                )
                key_part = jnp.einsum(
                    "hqk,qhd->khd", grad_scores, query_block, preferred_element_type=jnp.float32
                )
                return (query_accum, key_part)

            query_grad, key_parts = lax.scan(
                key_per_key,
                jnp.zeros((query_rows, heads_here, HD), jnp.float32),
                (key_split, value_split, key_starts),
            )
            return (key_total + key_parts.reshape(key_count, heads_here, HD), query_grad)

        key_grad, query_grads = lax.scan(
            key_pass,
            jnp.zeros((key_count, heads_here, HD), jnp.float32),
            (query_split, grad_split, log_norm, row_dots),
        )
        return (
            query_grads.reshape(span_rows, lane_width) * scale,
            key_grad.reshape(key_count, lane_width) * scale,
            value_grad.reshape(key_count, lane_width),
        )

    grad_queries, key_terms, value_terms = lax.map(
        attend_back, (queries, all_keys, all_values, grad_heads, log_norms, lengths)
    )
    grad_keys, grad_values = (
        lax.psum_scatter(
            key_terms.astype(jnp.bfloat16), "ctx", scatter_dimension=1, tiled=True
        ).astype(jnp.float32),
        lax.psum_scatter(
            value_terms.astype(jnp.bfloat16), "ctx", scatter_dimension=1, tiled=True
        ).astype(jnp.float32),
    )
    head_pos = (ctx_at * span_rows + jnp.arange(span_rows, dtype=jnp.int32)).astype(jnp.float32)
    head_cosine, head_sine = rope_tables(head_pos, HD)
    query_back = rotate(
        grad_queries.reshape(groups, span_rows, heads_here, HD), head_cosine, -head_sine
    )
    key_back = rotate(grad_keys.reshape(groups, span_rows, heads_here, HD), head_cosine, -head_sine)
    value_back = grad_values.reshape(groups, span_rows, heads_here, HD)
    grad_pack = (
        jnp.stack([query_back, key_back, value_back], axis=2)
        .astype(jnp.bfloat16)
        .reshape(groups, span_rows, 3, 1, lane_width)
    )
    grad_joined = lax.all_to_all(
        grad_pack, "fsdp", split_axis=1, concat_axis=3, tiled=True
    ).reshape(row_count, 3 * width)
    d_qkv = jnp.einsum("rd,re->de", flat_tokens, grad_joined, preferred_element_type=jnp.float32)
    d_qkv_bias = jnp.sum(grad_joined.astype(jnp.float32), axis=0)
    input_grad = (
        jnp.einsum("re,de->rd", grad_joined, back_qkv, preferred_element_type=jnp.float32)
        + grad_one
    ).astype(jnp.bfloat16)
    shards = (
        lax.psum_scatter(d_qkv, ("ctx", "fsdp"), scatter_dimension=0, tiled=True),
        lax.psum_scatter(d_qkv_bias, ("ctx", "fsdp"), scatter_dimension=0, tiled=True),
        lax.psum_scatter(d_out, ("ctx", "fsdp"), scatter_dimension=0, tiled=True),
        lax.psum_scatter(d_out_bias, ("ctx", "fsdp"), scatter_dimension=0, tiled=True),
        lax.psum_scatter(d_gain_one, ("ctx", "fsdp"), scatter_dimension=0, tiled=True),
        lax.psum_scatter(d_shift_one, ("ctx", "fsdp"), scatter_dimension=0, tiled=True),
        lax.psum_scatter(d_up, ("ctx", "fsdp"), scatter_dimension=0, tiled=True),
        lax.psum_scatter(d_up_bias, ("ctx", "fsdp"), scatter_dimension=0, tiled=True),
        lax.psum_scatter(d_down, ("ctx", "fsdp"), scatter_dimension=0, tiled=True),
        lax.psum_scatter(d_down_bias, ("ctx", "fsdp"), scatter_dimension=0, tiled=True),
        lax.psum_scatter(d_gain_two, ("ctx", "fsdp"), scatter_dimension=0, tiled=True),
        lax.psum_scatter(d_shift_two, ("ctx", "fsdp"), scatter_dimension=0, tiled=True),
        lax.psum_scatter(d_proj, ("ctx", "fsdp"), scatter_dimension=0, tiled=True),
    )
    totals = (
        lax.psum(shards[0].astype(jnp.bfloat16), "slot").astype(jnp.float32),
        lax.psum(shards[1].astype(jnp.bfloat16), "slot").astype(jnp.float32),
        lax.psum(shards[2].astype(jnp.bfloat16), "slot").astype(jnp.float32),
        lax.psum(shards[3].astype(jnp.bfloat16), "slot").astype(jnp.float32),
        lax.psum(shards[4].astype(jnp.bfloat16), "slot").astype(jnp.float32),
        lax.psum(shards[5].astype(jnp.bfloat16), "slot").astype(jnp.float32),
        lax.psum(shards[6].astype(jnp.bfloat16), "slot").astype(jnp.float32),
        lax.psum(shards[7].astype(jnp.bfloat16), "slot").astype(jnp.float32),
        lax.psum(shards[8].astype(jnp.bfloat16), "slot").astype(jnp.float32),
        lax.psum(shards[9].astype(jnp.bfloat16), "slot").astype(jnp.float32),
        lax.psum(shards[10].astype(jnp.bfloat16), "slot").astype(jnp.float32),
        lax.psum(shards[11].astype(jnp.bfloat16), "slot").astype(jnp.float32),
        lax.psum(shards[12].astype(jnp.bfloat16), "slot").astype(jnp.float32),
    )
    return (
        out_low.reshape(groups, tok_slot, width),
        projected.astype(jnp.bfloat16).reshape(groups, tok_slot, -1),
        input_grad.reshape(groups, tok_slot, width),
        totals[0],
        totals[1],
        totals[2],
        totals[3],
        totals[4],
        totals[5],
        totals[6],
        totals[7],
        totals[8],
        totals[9],
        totals[10],
        totals[11],
        totals[12],
    )


def solution(mesh):
    n_slot, n_ctx, n_fsdp = (mesh.shape[a] for a in ("slot", "ctx", "fsdp"))
    rows_axes = ("ctx", "fsdp")
    step = per_device
    if n_slot == 2 and n_fsdp % 2 == 0 and n_ctx * n_fsdp == H:
        mesh = Mesh(
            mesh.devices.reshape(n_slot, n_ctx, n_fsdp // 2, 2), ("slot", "ctx", "x", "core")
        )
        rows_axes = GROUP
        step = head_device
    in_specs = (
        P("slot", rows_axes, None),
        P("slot"),
        P(rows_axes, None),
        P(rows_axes),
        P(rows_axes, None),
        P(rows_axes),
        P(rows_axes),
        P(rows_axes),
        P(rows_axes, None),
        P(rows_axes),
        P(rows_axes, None),
        P(rows_axes),
        P(rows_axes),
        P(rows_axes),
        P(rows_axes, None),
        P("slot", rows_axes, None),
        P("slot", rows_axes, None),
    )
    out_specs = (
        P("slot", rows_axes, None),
        P("slot", rows_axes, None),
        P("slot", rows_axes, None),
        P(rows_axes, None),
        P(rows_axes),
        P(rows_axes, None),
        P(rows_axes),
        P(rows_axes),
        P(rows_axes),
        P(rows_axes, None),
        P(rows_axes),
        P(rows_axes, None),
        P(rows_axes),
        P(rows_axes),
        P(rows_axes),
        P(rows_axes, None),
    )
    return jax.shard_map(
        step, mesh=mesh, in_specs=in_specs, out_specs=out_specs, check_vma=False
    )
```

```python
from functools import partial

import jax
import jax.numpy as jnp
from jax import lax
from jax.experimental import pallas as pl
from jax.experimental.pallas import tpu as pltpu
from jax.sharding import Mesh
from jax.sharding import PartitionSpec as P

H = 16
HD = 64
LN_EPS = 1e-05
NEG_FILL = -1e30
F32 = jnp.float32
BF16 = jnp.bfloat16
GROUP = ("ctx", "x", "core")
LANE = ("ctx", "x")
SWAP = [(0, 1), (1, 0)]
VMEM_LIMIT = 60 * 1024 * 1024


def mm(left, right):
    return jnp.dot(left, right, preferred_element_type=F32)


def contract(left, right, left_dim, right_dim):
    return lax.dot_general(
        left, right, (((left_dim,), (right_dim,)), ((), ())), preferred_element_type=F32
    )


def swap_core(value):
    return lax.ppermute(value, "core", SWAP)


def swap_slot(value):
    return lax.ppermute(value, "slot", SWAP)


def pick(stacked, index, axis):
    return lax.dynamic_index_in_dim(stacked, index, axis, keepdims=False)


MESH = pl.DeviceIdType.MESH


def at_device(**where):
    names = ("slot", "ctx", "x", "core")
    return tuple(where[n] if n in where else lax.axis_index(n) for n in names)


def greet(peers):
    barrier = pltpu.get_barrier_semaphore()
    for peer in peers:
        pl.semaphore_signal(barrier, inc=1, device_id=peer, device_id_type=MESH)
    pl.semaphore_wait(barrier, len(peers))


def group_peers(n_ctx, n_x):
    ctx, x, core = (lax.axis_index(n) for n in GROUP)
    peers = []
    for dz in range(n_ctx):
        for dx in range(n_x):
            for dc in range(2):
                if dz or dx or dc:
                    where = (lax.rem(ctx + dz, n_ctx), lax.rem(x + dx, n_x), lax.rem(core + dc, 2))
                    peers.append(where)
    return peers


def start_kernel(
    tok_ref, head_ref, small_ref, all_ref, heads_ref, smalls_ref,
    far_send, block_send, local_sem, head_recv, small_recv, block_recv, *, n_ctx, n_x
):
    part = tok_ref.shape[1]
    ctx, x, core = (lax.axis_index(n) for n in GROUP)
    me = (ctx * n_x + x) * 2 + core
    peers = group_peers(n_ctx, n_x)
    greet([at_device(ctx=z, x=a, core=c) for z, a, c in peers])

    def block_at(b):
        return all_ref.at[:, pl.ds(pl.multiple_of(b * part, part), part), :]

    pushes = []
    for k, (z, a, c) in enumerate(peers):
        them = (z * n_x + a) * 2 + c
        target = at_device(ctx=z, x=a, core=c)
        pushes.append(pltpu.make_async_remote_copy(
            head_ref.at[them], heads_ref.at[me], far_send.at[2 * k], head_recv.at[me],
            device_id=target, device_id_type=MESH))
        pushes.append(pltpu.make_async_remote_copy(
            small_ref, smalls_ref.at[me], far_send.at[2 * k + 1], small_recv.at[me],
            device_id=target, device_id_type=MESH))
    locals_ = [
        pltpu.make_async_copy(tok_ref, block_at(me), local_sem.at[0]),
        pltpu.make_async_copy(head_ref.at[me], heads_ref.at[me], local_sem.at[1]),
        pltpu.make_async_copy(small_ref, smalls_ref.at[me], local_sem.at[2]),
    ]

    def send(b, source, lane, target):
        return pltpu.make_async_remote_copy(
            source, block_at(b), block_send.at[lane, b], block_recv.at[b],
            device_id=target, device_id_type=MESH)

    up = at_device(ctx=lax.rem(ctx + 1, n_ctx))
    down = at_device(ctx=lax.rem(ctx + n_ctx - 1, n_ctx))
    side = at_device(x=1 - x)
    twin = at_device(core=1 - core)

    def here(b):
        return send(b, block_at(b), 0, twin)

    @pl.when(ctx + 1 < n_ctx)
    def _():
        send(me, tok_ref, 0, up).start()

    @pl.when(ctx > 0)
    def _():
        send(me, tok_ref, 1, down).start()

    send(me, tok_ref, 2, side).start()
    for push in pushes:
        push.start()
    send(me, tok_ref, 3, twin).start()
    for copy in locals_:
        copy.start()

    for r in range(1, n_ctx):
        low = ctx - r
        high = ctx + r

        @pl.when(low >= 0)
        def _():
            b = (low * n_x + x) * 2 + core
            here(b).wait_recv()

            @pl.when(ctx + 1 < n_ctx)
            def _():
                send(b, block_at(b), 0, up).start()

            send(b, block_at(b), 2, side).start()
            send(b, block_at(b), 3, twin).start()

        @pl.when(high < n_ctx)
        def _():
            b = (high * n_x + x) * 2 + core
            here(b).wait_recv()

            @pl.when(ctx > 0)
            def _():
                send(b, block_at(b), 1, down).start()

            send(b, block_at(b), 2, side).start()
            send(b, block_at(b), 3, twin).start()

    def from_side(z):
        b = (z * n_x + (1 - x)) * 2 + core
        here(b).wait_recv()
        send(b, block_at(b), 3, twin).start()

    from_side(ctx)
    for r in range(1, n_ctx):
        @pl.when(ctx - r >= 0)
        def _():
            from_side(ctx - r)

        @pl.when(ctx + r < n_ctx)
        def _():
            from_side(ctx + r)

    for z in range(n_ctx):
        for a in range(n_x):
            here((z * n_x + a) * 2 + 1 - core).wait_recv()
    for k, (z, a, c) in enumerate(peers):
        them = (z * n_x + a) * 2 + c
        pltpu.make_async_remote_copy(
            head_ref.at[them], heads_ref.at[them], far_send.at[2 * k], head_recv.at[them],
            device_id=twin, device_id_type=MESH).wait_recv()
        pltpu.make_async_remote_copy(
            small_ref, smalls_ref.at[them], far_send.at[2 * k + 1], small_recv.at[them],
            device_id=twin, device_id_type=MESH).wait_recv()
    for push in pushes:
        push.wait_send()
    for copy in locals_:
        copy.wait()

    for z in range(n_ctx):
        b = (z * n_x + x) * 2 + core

        @pl.when((z <= ctx) & (ctx + 1 < n_ctx))
        def _():
            send(b, block_at(b), 0, up).wait_send()

        @pl.when((z >= ctx) & (ctx > 0))
        def _():
            send(b, block_at(b), 1, down).wait_send()

        send(b, block_at(b), 2, side).wait_send()
        send(b, block_at(b), 3, twin).wait_send()
        other = (z * n_x + (1 - x)) * 2 + core
        send(other, block_at(other), 3, twin).wait_send()


def gather_start(tokens, heads, small):
    n_ctx, n_x = lax.axis_size("ctx"), lax.axis_size("x")
    n = 2 * n_ctx * n_x
    slots, part, width = tokens.shape
    vmem = pl.BlockSpec(memory_space=pltpu.VMEM)
    anywhere = pl.BlockSpec(memory_space=pl.ANY)
    dma = pltpu.SemaphoreType.DMA
    return pl.pallas_call(
        partial(start_kernel, n_ctx=n_ctx, n_x=n_x),
        in_specs=[vmem, vmem, vmem],
        out_specs=[anywhere, vmem, vmem],
        out_shape=[
            jax.ShapeDtypeStruct((slots, n * part, width), tokens.dtype),
            jax.ShapeDtypeStruct(heads.shape, heads.dtype),
            jax.ShapeDtypeStruct((n,) + small.shape, small.dtype),
        ],
        scratch_shapes=[
            dma((2 * (n - 1),)), dma((4, n)), dma((3,)), dma((n,)), dma((n,)), dma((n,))
        ],
        compiler_params=pltpu.CompilerParams(
            collective_id=1, has_side_effects=True, vmem_limit_bytes=VMEM_LIMIT
        ),
        cost_estimate=pl.CostEstimate(
            flops=0, bytes_accessed=2 * n * tokens.size, transcendentals=0
        ),
        name="gather_start",
    )(tokens, heads, small)


def project_kernel(tok_ref, w_ref, b_ref, cos_ref, sin_ref, q_ref, k_ref, v_ref):
    joined = mm(tok_ref[...], w_ref[...]) + b_ref[...]
    wide = 2 * HD
    turned = joined[:, :wide] * cos_ref[...] + joined[:, wide : 2 * wide] * sin_ref[...]
    q_ref[...] = (turned[:, :HD].astype(BF16) * HD ** (-0.5)).astype(BF16)
    k_ref[...] = turned[:, HD:].astype(BF16)
    v_ref[...] = joined[:, 2 * wide :].astype(BF16)


def project(tokens, weight, bias, cosine, sine):
    rows, width = tokens.shape
    seq = cosine.shape[0]
    block = min(512, seq)
    per_slot = seq // block
    cols = weight.shape[1]
    head_out = jax.ShapeDtypeStruct((rows, HD), BF16)
    head_spec = pl.BlockSpec((block, HD), lambda i: (i, 0))
    return pl.pallas_call(
        project_kernel,
        grid=(rows // block,),
        in_specs=[
            pl.BlockSpec((block, width), lambda i: (i, 0)),
            pl.BlockSpec((width, cols), lambda i: (0, 0)),
            pl.BlockSpec((1, cols), lambda i: (0, 0)),
            pl.BlockSpec((block, 2 * HD), lambda i: (i % per_slot, 0)),
            pl.BlockSpec((block, 2 * HD), lambda i: (i % per_slot, 0)),
        ],
        out_specs=[head_spec] * 3,
        out_shape=[head_out] * 3,
        compiler_params=pltpu.CompilerParams(vmem_limit_bytes=VMEM_LIMIT),
        cost_estimate=pl.CostEstimate(
            flops=2 * rows * width * cols, bytes_accessed=2 * rows * width, transcendentals=0
        ),
        name="project",
    )(tokens, weight, bias, cosine, sine)


QB = 512
KB = 512


def forward_kernel(
    len_ref, core_ref, q_ref, k_ref, v_ref, out_ref, send_ref, norm_ref, *, part
):
    length = len_ref[pl.program_id(0)]
    core = core_ref[0]
    queries = q_ref[0]
    rows = queries.shape[0]

    def step(j, state):
        highest, total, mix = state
        start = pl.multiple_of(j * KB, KB)
        scores = contract(queries, k_ref[0, pl.ds(start, KB), :], 1, 1)
        ids = start + lax.broadcasted_iota(jnp.int32, (1, KB), 1)
        scores = jnp.where(ids < length, scores, NEG_FILL)
        higher = jnp.maximum(highest, jnp.max(scores, axis=1, keepdims=True))
        fade = jnp.exp(highest - higher)
        weights = jnp.exp(scores - higher)
        total = total * fade + jnp.sum(weights, axis=1, keepdims=True)
        mix = mix * fade + mm(weights.astype(BF16), v_ref[0, pl.ds(start, KB), :])
        return higher, total, mix

    blocks = (length + KB - 1) // KB
    highest, total, mix = lax.fori_loop(
        0,
        blocks,
        step,
        (
            jnp.full((rows, 1), NEG_FILL, F32),
            jnp.zeros((rows, 1), F32),
            jnp.zeros((rows, HD), F32),
        ),
    )
    mix = mix / total
    out_ref[0] = mix
    log_norm = jnp.broadcast_to(highest + jnp.log(total), (rows, 128))
    norm_ref[0] = jnp.transpose(log_norm)[0:1, :]
    low = mix.astype(BF16)
    for chip in range(rows // (2 * part)):
        for half in range(2):
            at = (2 * chip + half) * part
            send_ref[chip, half ^ core, 0] = low[at : at + part]


def attend(lengths, core, queries, keys, values, part):
    slots, seq, _ = queries.shape
    chips = seq // (2 * part)
    spec_q = pl.BlockSpec((1, QB, HD), lambda s, i, *_: (s, i, 0))
    spec_k = pl.BlockSpec((1, seq, HD), lambda s, i, *_: (s, 0, 0))
    return pl.pallas_call(
        partial(forward_kernel, part=part),
        grid_spec=pltpu.PrefetchScalarGridSpec(
            num_scalar_prefetch=2,
            grid=(slots, seq // QB),
            in_specs=[spec_q, spec_k, spec_k],
            out_specs=[
                spec_q,
                pl.BlockSpec(
                    (QB // (2 * part), 2, 1, part, HD), lambda s, i, *_: (i, 0, s, 0, 0)
                ),
                pl.BlockSpec((1, 1, QB), lambda s, i, *_: (s, 0, i)),
            ],
        ),
        out_shape=[
            jax.ShapeDtypeStruct((slots, seq, HD), F32),
            jax.ShapeDtypeStruct((chips, 2, slots, part, HD), BF16),
            jax.ShapeDtypeStruct((slots, 1, seq), F32),
        ],
        compiler_params=pltpu.CompilerParams(vmem_limit_bytes=VMEM_LIMIT),
        cost_estimate=pl.CostEstimate(
            flops=16 * slots * seq * seq * HD,
            bytes_accessed=8 * slots * seq * HD,
            transcendentals=slots * seq * seq,
        ),
        name="attend",
    )(lengths, core, queries, keys, values)


def backward_kernel(
    len_ref, q_ref, k_ref, v_ref, g_ref, norm_ref, dot_ref, dq_ref, dk_ref, dv_ref, dqt
):
    length = len_ref[pl.program_id(0)]
    j = pl.program_id(1)
    start = j * KB
    key_block = k_ref[0]
    value_block = v_ref[0]

    @pl.when(j == 0)
    def _():
        dqt[...] = jnp.zeros_like(dqt)

    turned = jnp.transpose(key_block.astype(F32)).astype(BF16)
    ids = start + lax.broadcasted_iota(jnp.int32, (KB, 1), 0)
    shift = jnp.where(ids < length, 0.0, NEG_FILL)

    def step(i, state):
        key_grad, value_grad = state
        at = pl.multiple_of(i * QB, QB)
        queries = q_ref[0, pl.ds(at, QB), :]
        grads = g_ref[0, pl.ds(at, QB), :]
        scores = contract(key_block, queries, 1, 1) + shift
        probs = jnp.exp(scores - norm_ref[0, :, pl.ds(at, QB)])
        grad_probs = contract(value_block, grads, 1, 1)
        grad_scores = (probs * (grad_probs - dot_ref[0, :, pl.ds(at, QB)])).astype(BF16)
        value_grad = value_grad + mm(probs.astype(BF16), grads)
        key_grad = key_grad + mm(grad_scores, queries)
        dqt[:, pl.ds(at, QB)] += mm(turned, grad_scores)
        return key_grad, value_grad

    blocks = jnp.where(start < length, (length + QB - 1) // QB, 0)
    zero = jnp.zeros((KB, HD), F32)
    key_grad, value_grad = lax.fori_loop(0, blocks, step, (zero, zero))
    dk_ref[0] = key_grad
    dv_ref[0] = value_grad

    @pl.when(j == pl.num_programs(1) - 1)
    def _():
        dq_ref[0] = jnp.transpose(dqt[...])


def attend_back(lengths, queries, keys, values, grads, norms, dots):
    slots, seq, _ = queries.shape
    whole = pl.BlockSpec((1, seq, HD), lambda s, j, *_: (s, 0, 0))
    block = pl.BlockSpec((1, KB, HD), lambda s, j, *_: (s, j, 0))
    row = pl.BlockSpec((1, 1, seq), lambda s, j, *_: (s, 0, 0))
    out = jax.ShapeDtypeStruct((slots, seq, HD), F32)
    return pl.pallas_call(
        backward_kernel,
        grid_spec=pltpu.PrefetchScalarGridSpec(
            num_scalar_prefetch=1,
            grid=(slots, seq // KB),
            in_specs=[whole, block, block, whole, row, row],
            out_specs=[whole, block, block],
            scratch_shapes=[pltpu.VMEM((HD, seq), F32)],
        ),
        out_shape=[out] * 3,
        compiler_params=pltpu.CompilerParams(vmem_limit_bytes=VMEM_LIMIT),
        cost_estimate=pl.CostEstimate(
            flops=40 * slots * seq * seq * HD,
            bytes_accessed=20 * slots * seq * HD,
            transcendentals=slots * seq * seq,
        ),
        name="attend_back",
    )(lengths, queries, keys, values, grads, norms, dots)


def norm_forward(values, gain, shift):
    center = values - jnp.mean(values, axis=-1, keepdims=True)
    spread = jnp.mean(center * center, axis=-1, keepdims=True)
    root = lax.rsqrt(spread + LN_EPS)
    unit = center * root
    return unit * gain + shift, unit, root


def norm_backward(grad, unit, root, gain):
    scaled = grad * gain
    inner = scaled - jnp.mean(scaled, axis=-1, keepdims=True)
    inner = inner - unit * jnp.mean(scaled * unit, axis=-1, keepdims=True)
    return root * inner, jnp.sum(grad * unit, axis=0), jnp.sum(grad, axis=0)


def gelu_pair(values):
    half = 0.5 + 0.5 * lax.erf(values * 0.7071067811865476)
    bell = jnp.exp(-0.5 * values * values) * 0.3989422804014327
    return values * half, half + values * bell


def rope_rows(positions):
    halfway = HD // 2
    ladder = jnp.arange(halfway, dtype=F32) * (2.0 / HD)
    frequency = jnp.power(jnp.float32(10000.0), -ladder)
    angles = positions[:, None] * frequency[None, :]
    return jnp.cos(angles), jnp.sin(angles)


def head_device(
    tokens,
    lengths,
    w_qkv,
    b_qkv,
    w_out,
    b_out,
    ln1_gain,
    ln1_bias,
    w_up,
    b_up,
    w_down,
    b_down,
    ln2_gain,
    ln2_bias,
    w_proj,
    cot_out,
    cot_emb,
):
    n_lane = lax.axis_size("ctx") * lax.axis_size("x")
    n_group = 2 * n_lane
    core = lax.axis_index("core")
    slot = lax.axis_index("slot")
    chip = lax.axis_index("ctx") * lax.axis_size("x") + lax.axis_index("x")
    me = 2 * chip + core
    slots, part, width = tokens.shape
    seq = part * n_group
    rows = slots * part
    shard = width // n_group
    ff_shard = w_down.shape[0]
    ff_half = ff_shard // 2
    proj = w_proj.shape[1]
    head_cols = 3 * HD

    small = jnp.concatenate(
        [b_qkv, b_out, ln1_gain, ln1_bias, b_up, b_down, ln2_gain, ln2_bias]
    )
    small_at = [0]
    for piece in (b_qkv, b_out, ln1_gain, ln1_bias, b_up, b_down, ln2_gain, ln2_bias):
        small_at.append(small_at[-1] + piece.shape[0])
    small_rows = -(-small.shape[0] // proj)
    small_rows = -(-small_rows // 16) * 16
    small = jnp.pad(small, (0, small_rows * proj - small.shape[0])).reshape(small_rows, proj)
    by_head = w_qkv.reshape(shard, 3, n_group, HD).transpose(2, 0, 1, 3)
    all_tokens, my_head, packed = gather_start(
        tokens,
        by_head.reshape(n_group, shard, head_cols),
        jnp.concatenate([w_proj, small], axis=0),
    )
    proj_full = packed[:, :shard].reshape(width, proj)
    smalls = packed[:, shard:].reshape(n_group, small_rows * proj).astype(F32)
    qkv_bias, out_bias, gain_one, shift_one, up_bias, down_bias, gain_two, shift_two = (
        smalls[:, a:b].reshape(-1) for a, b in zip(small_at[:-1], small_at[1:])
    )

    my_head = my_head.reshape(width, 3, HD)
    all_tokens = all_tokens.reshape(slots * seq, width)

    def with_swapped(joined):
        first = joined[:, 0:2]
        halves = first.reshape(-1, 2, 2, HD // 2)
        swapped = jnp.stack([-halves[:, :, 1], halves[:, :, 0]], axis=2)
        return jnp.concatenate(
            [
                first.reshape(-1, 2 * HD),
                swapped.reshape(-1, 2 * HD),
                joined[:, 2],
            ],
            axis=1,
        )

    head_weight = with_swapped(my_head)
    head_bias = with_swapped(pick(qkv_bias.reshape(1, 3, n_group, HD), me, 2))
    cosine, sine = rope_rows(jnp.arange(seq, dtype=jnp.int32).astype(F32))
    cos_wide = jnp.tile(cosine, (1, 4))
    sin_wide = jnp.tile(sine, (1, 4))
    queries, keys, values = project(all_tokens, head_weight, head_bias, cos_wide, sin_wide)
    queries, keys, values = (t.reshape(slots, seq, HD) for t in (queries, keys, values))

    def two_lanes(mine, theirs):
        low_first = jnp.stack([mine, theirs], axis=0)
        high_first = jnp.stack([theirs, mine], axis=0)
        return jnp.where(core == 0, low_first, high_first)

    out_lane = lax.all_gather(w_out, LANE, axis=0, tiled=True)
    up_split = w_up.reshape(shard, n_lane, 2, 2, ff_half)
    up_mine = pick(up_split, core, 2)
    up_theirs = swap_core(pick(up_split, 1 - core, 2))
    up_chip = two_lanes(up_mine, up_theirs).reshape(2 * shard, n_lane, 2, ff_half)
    down_split = w_down.reshape(2, ff_half, width)
    up_part = pick(up_chip, slot, 2).reshape(2 * shard, n_lane * ff_half)
    up = lax.all_gather(up_part, LANE, axis=0, tiled=True)
    down = lax.all_gather(pick(down_split, slot, 0), LANE, axis=0, tiled=True)
    bias_lane = pick(up_bias.reshape(n_lane, 2, 2, ff_half), core, 1)
    up_bias_own = pick(bias_lane, slot, 1).reshape(-1)

    qkv_split = w_qkv.reshape(shard, 3, n_lane, 2, HD)
    qkv_mine = pick(qkv_split, core, 3)
    qkv_theirs = swap_core(pick(qkv_split, 1 - core, 3))
    qkv_chip = two_lanes(qkv_mine, qkv_theirs).transpose(0, 1, 3, 2, 4)
    qkv_lane = lax.all_gather(
        qkv_chip.reshape(2 * shard, n_lane * head_cols), LANE, axis=0, tiled=True
    )

    mixture, send, norms = attend(
        lengths, core.reshape(1).astype(jnp.int32), queries, keys, values, part
    )
    merged = lax.all_to_all(send, LANE, 0, 0, tiled=True)
    merged = merged.transpose(1, 2, 3, 0, 4).reshape(2 * rows, n_lane * HD)

    def own_sum(partial_rows):
        return partial_rows[:rows] + swap_core(partial_rows[rows:])

    def both(value):
        return jnp.concatenate([value, swap_core(value)], axis=0)

    def quad(value):
        pair = jnp.concatenate([value, swap_slot(value)], axis=0)
        return jnp.concatenate([pair, swap_core(pair)], axis=0)

    def quad_sum(partial_rows):
        pair = partial_rows[: 2 * rows] + swap_core(partial_rows[2 * rows :])
        return pair[:rows] + swap_slot(pair[rows:].astype(BF16)).astype(F32)

    flat_tokens = tokens.reshape(rows, width).astype(F32)
    attended = own_sum(mm(merged, out_lane)) + out_bias
    hidden_one, unit_one, root_one = norm_forward(flat_tokens + attended, gain_one, shift_one)
    hidden_low = quad(hidden_one.astype(BF16))

    active, slope = gelu_pair(mm(hidden_low, up) + up_bias_own)
    active = active.astype(BF16)
    downward = quad_sum(mm(active, down)) + down_bias
    out_rows, unit_two, root_two = norm_forward(hidden_one + downward, gain_two, shift_two)
    out_low = out_rows.astype(BF16)
    embeds = mm(out_low, proj_full).astype(BF16)

    place = me * part + jnp.arange(part, dtype=jnp.int32)
    live = (place[None, :] < lengths[:, None]).reshape(rows, 1)
    grad_out = jnp.where(live, cot_out.reshape(rows, width).astype(F32), 0.0)
    grad_emb = jnp.where(live, cot_emb.reshape(rows, proj), 0)
    d_proj = contract(out_low, grad_emb, 0, 0)
    grad_full = grad_out + contract(grad_emb, proj_full, 1, 1)
    grad_two, d_gain_two, d_shift_two = norm_backward(grad_full, unit_two, root_two, gain_two)
    grad_down_own = grad_two.astype(BF16)
    d_down_bias = jnp.sum(grad_down_own.astype(F32), axis=0)
    grad_down = quad(grad_down_own)
    grad_up = (contract(grad_down, down, 1, 1) * slope).astype(BF16)
    d_down = contract(active, grad_down, 0, 0).astype(BF16)
    d_up = contract(hidden_low, grad_up, 0, 0).astype(BF16)
    up_bias_own_grad = jnp.sum(grad_up.astype(F32), axis=0)
    grad_hidden = grad_two + quad_sum(contract(grad_up, up, 1, 1))
    grad_one, d_gain_one, d_shift_one = norm_backward(grad_hidden, unit_one, root_one, gain_one)
    grad_att_own = grad_one.astype(BF16)
    d_out_bias = jnp.sum(grad_att_own.astype(F32), axis=0)
    grad_att = both(grad_att_own)
    grad_merged = contract(grad_att, out_lane, 1, 1).astype(BF16)
    grad_merged = grad_merged.reshape(2, slots, part, n_lane, HD).transpose(3, 0, 1, 2, 4)
    grad_heads = lax.all_to_all(grad_merged, LANE, 0, 0, tiled=True)

    def core_order(value):
        return jnp.where(core == 0, value, jnp.flip(value, axis=1))

    grad_heads = core_order(grad_heads).transpose(2, 0, 1, 3, 4).reshape(slots, seq, HD)

    half_width = width // 2
    att_split = grad_att.reshape(2 * rows, 2, half_width)
    d_outs = [
        contract(merged, pick(att_split, half, 1), 0, 0).astype(BF16)
        for half in (slot, 1 - slot)
    ]

    def reduced(pair):
        both_slots = pair[0].astype(F32) + swap_slot(pair[1]).astype(F32)
        return lax.psum_scatter(both_slots.astype(BF16), LANE, scatter_dimension=0, tiled=True)

    red_down = lax.psum_scatter(d_down, LANE, scatter_dimension=0, tiled=True)
    red_up = lax.psum_scatter(d_up, LANE, scatter_dimension=0, tiled=True)
    red_out = reduced(d_outs)

    def halves(mine, axis):
        theirs = swap_slot(mine)
        return jnp.where(
            slot == 0, jnp.stack([mine, theirs], axis), jnp.stack([theirs, mine], axis)
        )

    grad_w_down = halves(red_down, 0).reshape(ff_shard, width).astype(F32)
    grad_w_out = halves(red_out, 1).reshape(shard, width).astype(F32)
    up_rows = red_up.reshape(2, shard, n_lane, ff_half)
    up_keep = pick(up_rows, core, 0)
    up_got = swap_core(pick(up_rows, 1 - core, 0))
    up_lanes = jnp.where(
        core == 0, jnp.stack([up_keep, up_got], 2), jnp.stack([up_got, up_keep], 2)
    )
    grad_w_up = halves(up_lanes, 3).reshape(shard, w_up.shape[1]).astype(F32)

    spread = (
        (jnp.arange(2) == core)[:, None, None] & (jnp.arange(2) == slot)[None, :, None]
    ).astype(F32)
    up_bias_grad = up_bias_own_grad.reshape(n_lane, 1, 1, ff_half) * spread[None]
    vectors = (
        d_out_bias,
        d_gain_one,
        d_shift_one,
        up_bias_grad.reshape(-1),
        d_down_bias,
        d_gain_two,
        d_shift_two,
    )
    small_grad = jnp.concatenate([v.reshape(n_group, -1) for v in vectors], axis=1)
    small_cols = small_grad.shape[1]
    vec_rows = -(-small_cols // proj)
    vec_rows = -(-vec_rows // 8) * 8
    small_grad = jnp.pad(small_grad, ((0, 0), (0, vec_rows * proj - small_cols)))
    small_grad = jnp.concatenate(
        [d_proj.reshape(n_group, shard, proj), small_grad.reshape(n_group, vec_rows, proj)], axis=1
    )
    small_red = lax.psum_scatter(
        small_grad.reshape(n_group * (shard + vec_rows), proj), GROUP, scatter_dimension=0, tiled=True
    )
    small_low = small_red.astype(BF16)
    small_sum = small_low.astype(F32) + swap_slot(small_low).astype(F32)
    grad_w_proj = small_sum[:shard]
    vec_sum = small_sum[shard:].reshape(-1)
    vec_outs = []
    at = 0
    for v in vectors:
        size = v.size // n_group
        vec_outs.append(vec_sum[at : at + size])
        at += size
    (
        grad_b_out,
        grad_gain_one,
        grad_shift_one,
        grad_b_up,
        grad_b_down,
        grad_gain_two,
        grad_shift_two,
    ) = vec_outs

    row_dots = jnp.sum(grad_heads.astype(F32) * mixture, axis=-1).reshape(slots, 1, seq)
    grad_q, grad_k, grad_v = attend_back(
        lengths, queries, keys, values, grad_heads, norms, row_dots
    )

    def turn_back(value):
        first, second = value[..., : HD // 2], value[..., HD // 2 :]
        return jnp.concatenate(
            [first * cosine + second * sine, second * cosine - first * sine], axis=-1
        )

    grad_joined = jnp.concatenate(
        [turn_back(grad_q * HD ** (-0.5)), turn_back(grad_k), grad_v], axis=-1
    ).astype(BF16)
    d_qkv = contract(all_tokens, grad_joined.reshape(slots * seq, head_cols), 0, 0)
    d_qkv_bias = jnp.sum(grad_joined.astype(F32), axis=(0, 1))
    d_qkv = jnp.concatenate(
        [
            d_qkv.reshape(n_group, shard, head_cols),
            jnp.broadcast_to(d_qkv_bias, (n_group, 16, head_cols)),
        ],
        axis=1,
    ).astype(BF16)
    d_qkv = (d_qkv.astype(F32) + swap_slot(d_qkv).astype(F32)).astype(BF16)
    d_qkv = lax.all_to_all(d_qkv, GROUP, 0, 0, tiled=True).astype(F32)
    grad_w_qkv = (
        d_qkv[:, :shard].reshape(n_group, shard, 3, HD).transpose(1, 2, 0, 3).reshape(shard, 3 * width)
    )
    qkv_bias_grad = d_qkv[:, shard].reshape(n_group, 3, HD).transpose(1, 0, 2).reshape(-1)
    grad_b_qkv = lax.dynamic_slice(qkv_bias_grad, (me * b_qkv.shape[0],), (b_qkv.shape[0],))

    to_chips = grad_joined.reshape(slots, n_lane, 2, part, head_cols).transpose(1, 2, 0, 3, 4)
    joined_rows = lax.all_to_all(core_order(to_chips), LANE, 0, 0, tiled=True)
    joined_rows = joined_rows.transpose(1, 2, 3, 0, 4).reshape(2 * rows, n_lane * head_cols)
    input_grad = own_sum(contract(joined_rows, qkv_lane, 1, 1)) + grad_one

    return (
        out_low.reshape(slots, part, width),
        embeds.reshape(slots, part, proj),
        input_grad.astype(BF16).reshape(slots, part, width),
        grad_w_qkv,
        grad_b_qkv,
        grad_w_out,
        grad_b_out,
        grad_gain_one,
        grad_shift_one,
        grad_w_up,
        grad_b_up,
        grad_w_down,
        grad_b_down,
        grad_gain_two,
        grad_shift_two,
        grad_w_proj,
    )


def layer_norm(hidden, gain, shift):
    center = hidden - jnp.mean(hidden, axis=-1, keepdims=True)
    spread = jnp.mean(center * center, axis=-1, keepdims=True)
    return center * lax.rsqrt(spread + LN_EPS) * gain + shift


def rope_tables(positions, head_width):
    halfway = head_width // 2
    ladder = jnp.arange(halfway, dtype=jnp.float32) * (2.0 / head_width)
    frequency = jnp.power(jnp.float32(10000.0), -ladder)
    angles = positions[:, None] * frequency[None, :]
    return (jnp.cos(angles)[:, None, :], jnp.sin(angles)[:, None, :])


def rotate(values, cosine, sine_part):
    halfway = values.shape[-1] // 2
    first_half = values[..., :halfway]
    second_half = values[..., halfway:]
    return jnp.concatenate(
        [
            first_half * cosine - second_half * sine_part,
            second_half * cosine + first_half * sine_part,
        ],
        axis=-1,
    )


def block_scores(query_block, key_block, key_start, length, scale):
    scores = (
        jnp.einsum("qhd,khd->hqk", query_block, key_block, preferred_element_type=jnp.float32)
        * scale
    )
    key_ids = key_start + jnp.arange(key_block.shape[0], dtype=jnp.int32)
    return jnp.where((key_ids < length)[None, None, :], scores, NEG_FILL)


def per_device(
    tokens,
    lengths,
    w_qkv,
    b_qkv,
    w_out,
    b_out,
    ln1_gain,
    ln1_bias,
    w_up,
    b_up,
    w_down,
    b_down,
    ln2_gain,
    ln2_bias,
    w_proj,
    cot_out,
    cot_emb,
):
    n_fsdp = lax.axis_size("fsdp")
    n_ctx = lax.axis_size("ctx")
    ctx_at = lax.axis_index("ctx")
    fsdp_at = lax.axis_index("fsdp")
    groups, tok_slot, width = tokens.shape
    heads_here = H // n_fsdp
    lane_width = heads_here * HD
    span_rows = tok_slot * n_fsdp
    key_count = span_rows * n_ctx
    row_count = groups * tok_slot
    scale = HD ** (-0.5)
    query_rows = min(512, span_rows)
    key_rows = min(2048, key_count // 4)
    query_blocks = span_rows // query_rows
    key_blocks = key_count // key_rows
    key_starts = jnp.arange(key_blocks, dtype=jnp.int32) * key_rows
    qkv_full, qkv_bias, out_full, out_bias, gain_one, shift_one = (
        lax.all_gather(w_qkv, ("ctx", "fsdp"), axis=0, tiled=True),
        lax.all_gather(b_qkv, ("ctx", "fsdp"), axis=0, tiled=True),
        lax.all_gather(w_out, ("ctx", "fsdp"), axis=0, tiled=True),
        lax.all_gather(b_out, ("ctx", "fsdp"), axis=0, tiled=True),
        lax.all_gather(ln1_gain, ("ctx", "fsdp"), axis=0, tiled=True),
        lax.all_gather(ln1_bias, ("ctx", "fsdp"), axis=0, tiled=True),
    )
    token_pos = (ctx_at * n_fsdp + fsdp_at) * tok_slot + jnp.arange(tok_slot, dtype=jnp.int32)
    live_rows = (token_pos[None, :] < lengths[:, None]).reshape(row_count, 1)
    flat_tokens = tokens.reshape(row_count, width)
    joined = jnp.dot(flat_tokens, qkv_full, preferred_element_type=jnp.float32) + qkv_bias.astype(
        jnp.float32
    )
    cosine, sine_part = rope_tables(token_pos.astype(jnp.float32), HD)
    split_heads = joined.reshape(groups, tok_slot, 3, H, HD)
    rotated_query = rotate(split_heads[:, :, 0], cosine, sine_part)
    rotated_key = rotate(split_heads[:, :, 1], cosine, sine_part)
    packed = (
        jnp.stack([rotated_query, rotated_key, split_heads[:, :, 2]], axis=2)
        .astype(jnp.bfloat16)
        .reshape(groups, tok_slot, 3, n_fsdp, lane_width)
    )
    by_heads = lax.all_to_all(packed, "fsdp", split_axis=3, concat_axis=1, tiled=True)
    queries = by_heads[:, :, 0, 0]
    local_keys = by_heads[:, :, 1, 0]
    local_values = by_heads[:, :, 2, 0]
    all_keys, all_values = (
        lax.all_gather(local_keys, "ctx", axis=1, tiled=True),
        lax.all_gather(local_values, "ctx", axis=1, tiled=True),
    )

    def attend_slot(slot_item):
        slot_queries, slot_keys, slot_values, length = slot_item
        query_split = slot_queries.reshape(query_blocks, query_rows, heads_here, HD)
        key_split = slot_keys.reshape(key_blocks, key_rows, heads_here, HD)
        value_split = slot_values.reshape(key_blocks, key_rows, heads_here, HD)

        def per_query(query_block):

            def row_stats(state_pair, key_item):
                highest, running_sum = state_pair
                scores = block_scores(query_block, key_item[0], key_item[1], length, scale)
                new_high = jnp.maximum(highest, jnp.max(scores, axis=-1))
                running_sum = running_sum * jnp.exp(highest - new_high) + jnp.sum(
                    jnp.exp(scores - new_high[..., None]), axis=-1
                )
                return ((new_high, running_sum), None)

            start_state = (
                jnp.full((heads_here, query_rows), NEG_FILL, jnp.float32),
                jnp.zeros((heads_here, query_rows), jnp.float32),
            )
            highest, running_sum = lax.scan(row_stats, start_state, (key_split, key_starts))[0]
            log_norm = highest + jnp.log(running_sum)

            def weigh_values(accumulated, key_item):
                scores = block_scores(query_block, key_item[0], key_item[2], length, scale)
                weights = jnp.exp(scores - log_norm[..., None]).astype(jnp.bfloat16)
                return (
                    accumulated
                    + jnp.einsum(
                        "hqk,khd->qhd", weights, key_item[1], preferred_element_type=jnp.float32
                    ),
                    None,
                )

            mixture = lax.scan(
                weigh_values,
                jnp.zeros((query_rows, heads_here, HD), jnp.float32),
                (key_split, value_split, key_starts),
            )[0]
            return (mixture, log_norm)

        mixture, log_norm = lax.map(per_query, query_split)
        return (mixture.reshape(span_rows, lane_width), log_norm)

    mixture, log_norms = lax.map(attend_slot, (queries, all_keys, all_values, lengths))
    merged = lax.all_to_all(
        mixture.astype(jnp.bfloat16).reshape(groups, span_rows, 1, lane_width),
        "fsdp",
        split_axis=1,
        concat_axis=2,
        tiled=True,
    ).reshape(row_count, width)
    attended = jnp.dot(merged, out_full, preferred_element_type=jnp.float32) + out_bias.astype(
        jnp.float32
    )
    hidden_one, pull_one = jax.vjp(
        layer_norm,
        flat_tokens.astype(jnp.float32) + attended,
        gain_one.astype(jnp.float32),
        shift_one.astype(jnp.float32),
    )
    hidden_low = hidden_one.astype(jnp.bfloat16)
    up_full, up_bias, down_full, down_bias, gain_two, shift_two, proj_full = (
        lax.all_gather(w_up, ("ctx", "fsdp"), axis=0, tiled=True),
        lax.all_gather(b_up, ("ctx", "fsdp"), axis=0, tiled=True),
        lax.all_gather(w_down, ("ctx", "fsdp"), axis=0, tiled=True),
        lax.all_gather(b_down, ("ctx", "fsdp"), axis=0, tiled=True),
        lax.all_gather(ln2_gain, ("ctx", "fsdp"), axis=0, tiled=True),
        lax.all_gather(ln2_bias, ("ctx", "fsdp"), axis=0, tiled=True),
        lax.all_gather(w_proj, ("ctx", "fsdp"), axis=0, tiled=True),
    )
    upward = jnp.dot(hidden_low, up_full, preferred_element_type=jnp.float32) + up_bias.astype(
        jnp.float32
    )
    active_full, pull_gelu = jax.vjp(partial(jax.nn.gelu, approximate=False), upward)
    active = active_full.astype(jnp.bfloat16)
    downward = jnp.dot(active, down_full, preferred_element_type=jnp.float32) + down_bias.astype(
        jnp.float32
    )
    out_full_rows, pull_two = jax.vjp(
        layer_norm,
        hidden_one + downward,
        gain_two.astype(jnp.float32),
        shift_two.astype(jnp.float32),
    )
    out_low = out_full_rows.astype(jnp.bfloat16)
    projected = jnp.dot(out_low, proj_full, preferred_element_type=jnp.float32)
    back_qkv, back_qkv_bias, back_out, back_out_bias, back_gain_one, back_shift_one = (
        lax.all_gather(w_qkv, ("ctx", "fsdp"), axis=0, tiled=True),
        lax.all_gather(b_qkv, ("ctx", "fsdp"), axis=0, tiled=True),
        lax.all_gather(w_out, ("ctx", "fsdp"), axis=0, tiled=True),
        lax.all_gather(b_out, ("ctx", "fsdp"), axis=0, tiled=True),
        lax.all_gather(ln1_gain, ("ctx", "fsdp"), axis=0, tiled=True),
        lax.all_gather(ln1_bias, ("ctx", "fsdp"), axis=0, tiled=True),
    )
    back_up, back_up_bias, back_down, back_down_bias, back_gain_two, back_shift_two, back_proj = (
        lax.all_gather(w_up, ("ctx", "fsdp"), axis=0, tiled=True),
        lax.all_gather(b_up, ("ctx", "fsdp"), axis=0, tiled=True),
        lax.all_gather(w_down, ("ctx", "fsdp"), axis=0, tiled=True),
        lax.all_gather(b_down, ("ctx", "fsdp"), axis=0, tiled=True),
        lax.all_gather(ln2_gain, ("ctx", "fsdp"), axis=0, tiled=True),
        lax.all_gather(ln2_bias, ("ctx", "fsdp"), axis=0, tiled=True),
        lax.all_gather(w_proj, ("ctx", "fsdp"), axis=0, tiled=True),
    )
    grad_out = jnp.where(live_rows, cot_out.reshape(row_count, width).astype(jnp.float32), 0.0)
    grad_emb = jnp.where(live_rows, cot_emb.reshape(row_count, -1), 0)
    d_proj = jnp.einsum("rd,rp->dp", out_low, grad_emb, preferred_element_type=jnp.float32)
    grad_full = grad_out + jnp.einsum(
        "rp,dp->rd", grad_emb, back_proj, preferred_element_type=jnp.float32
    )
    grad_two, d_gain_two, d_shift_two = pull_two(grad_full)
    grad_down = grad_two.astype(jnp.bfloat16)
    d_down = jnp.einsum("rf,rd->fd", active, grad_down, preferred_element_type=jnp.float32)
    d_down_bias = jnp.sum(grad_down.astype(jnp.float32), axis=0)
    grad_act = jnp.einsum("rd,fd->rf", grad_down, back_down, preferred_element_type=jnp.float32)
    grad_up = pull_gelu(grad_act)[0].astype(jnp.bfloat16)
    d_up = jnp.einsum("rd,rf->df", hidden_low, grad_up, preferred_element_type=jnp.float32)
    d_up_bias = jnp.sum(grad_up.astype(jnp.float32), axis=0)
    grad_hidden = grad_two + jnp.einsum(
        "rf,df->rd", grad_up, back_up, preferred_element_type=jnp.float32
    )
    grad_one, d_gain_one, d_shift_one = pull_one(grad_hidden)
    grad_att = grad_one.astype(jnp.bfloat16)
    d_out = jnp.einsum("rd,re->de", merged, grad_att, preferred_element_type=jnp.float32)
    d_out_bias = jnp.sum(grad_att.astype(jnp.float32), axis=0)
    grad_merged = jnp.einsum(
        "re,de->rd", grad_att, back_out, preferred_element_type=jnp.float32
    ).astype(jnp.bfloat16)
    grad_heads = lax.all_to_all(
        grad_merged.reshape(groups, tok_slot, n_fsdp, lane_width),
        "fsdp",
        split_axis=2,
        concat_axis=1,
        tiled=True,
    ).reshape(groups, span_rows, lane_width)

    def attend_back(slot_item):
        slot_queries, slot_keys, slot_values, grad_mix, log_norm, length = slot_item
        query_split = slot_queries.reshape(query_blocks, query_rows, heads_here, HD)
        key_split = slot_keys.reshape(key_blocks, key_rows, heads_here, HD)
        value_split = slot_values.reshape(key_blocks, key_rows, heads_here, HD)
        grad_split = grad_mix.reshape(query_blocks, query_rows, heads_here, HD)

        def value_pass(value_total, query_item):
            query_block, grad_block, norm_block = query_item

            def value_per_key(row_dot, key_item):
                key_block, value_block, key_start = key_item
                scores = block_scores(query_block, key_block, key_start, length, scale)
                probability = jnp.exp(scores - norm_block[..., None])
                grad_probs = jnp.einsum(
                    "qhd,khd->hqk", grad_block, value_block, preferred_element_type=jnp.float32
                )
                value_part = jnp.einsum(
                    "hqk,qhd->khd",
                    probability.astype(jnp.bfloat16),
                    grad_block,
                    preferred_element_type=jnp.float32,
                )
                return (row_dot + jnp.sum(probability * grad_probs, axis=-1), value_part)

            row_dot, value_parts = lax.scan(
                value_per_key,
                jnp.zeros((heads_here, query_rows), jnp.float32),
                (key_split, value_split, key_starts),
            )
            return (value_total + value_parts.reshape(key_count, heads_here, HD), row_dot)

        value_grad, row_dots = lax.scan(
            value_pass,
            jnp.zeros((key_count, heads_here, HD), jnp.float32),
            (query_split, grad_split, log_norm),
        )

        def key_pass(key_total, query_item):
            query_block, grad_block, norm_block, dot_block = query_item

            def key_per_key(query_accum, key_item):
                key_block, value_block, key_start = key_item
                scores = block_scores(query_block, key_block, key_start, length, scale)
                probability = jnp.exp(scores - norm_block[..., None])
                grad_probs = jnp.einsum(
                    "qhd,khd->hqk", grad_block, value_block, preferred_element_type=jnp.float32
                )
                grad_scores = (probability * (grad_probs - dot_block[..., None])).astype(
                    jnp.bfloat16
                )
                query_accum = query_accum + jnp.einsum(
                    "hqk,khd->qhd", grad_scores, key_block, preferred_element_type=jnp.float32
                )
                key_part = jnp.einsum(
                    "hqk,qhd->khd", grad_scores, query_block, preferred_element_type=jnp.float32
                )
                return (query_accum, key_part)

            query_grad, key_parts = lax.scan(
                key_per_key,
                jnp.zeros((query_rows, heads_here, HD), jnp.float32),
                (key_split, value_split, key_starts),
            )
            return (key_total + key_parts.reshape(key_count, heads_here, HD), query_grad)

        key_grad, query_grads = lax.scan(
            key_pass,
            jnp.zeros((key_count, heads_here, HD), jnp.float32),
            (query_split, grad_split, log_norm, row_dots),
        )
        return (
            query_grads.reshape(span_rows, lane_width) * scale,
            key_grad.reshape(key_count, lane_width) * scale,
            value_grad.reshape(key_count, lane_width),
        )

    grad_queries, key_terms, value_terms = lax.map(
        attend_back, (queries, all_keys, all_values, grad_heads, log_norms, lengths)
    )
    grad_keys, grad_values = (
        lax.psum_scatter(
            key_terms.astype(jnp.bfloat16), "ctx", scatter_dimension=1, tiled=True
        ).astype(jnp.float32),
        lax.psum_scatter(
            value_terms.astype(jnp.bfloat16), "ctx", scatter_dimension=1, tiled=True
        ).astype(jnp.float32),
    )
    head_pos = (ctx_at * span_rows + jnp.arange(span_rows, dtype=jnp.int32)).astype(jnp.float32)
    head_cosine, head_sine = rope_tables(head_pos, HD)
    query_back = rotate(
        grad_queries.reshape(groups, span_rows, heads_here, HD), head_cosine, -head_sine
    )
    key_back = rotate(grad_keys.reshape(groups, span_rows, heads_here, HD), head_cosine, -head_sine)
    value_back = grad_values.reshape(groups, span_rows, heads_here, HD)
    grad_pack = (
        jnp.stack([query_back, key_back, value_back], axis=2)
        .astype(jnp.bfloat16)
        .reshape(groups, span_rows, 3, 1, lane_width)
    )
    grad_joined = lax.all_to_all(
        grad_pack, "fsdp", split_axis=1, concat_axis=3, tiled=True
    ).reshape(row_count, 3 * width)
    d_qkv = jnp.einsum("rd,re->de", flat_tokens, grad_joined, preferred_element_type=jnp.float32)
    d_qkv_bias = jnp.sum(grad_joined.astype(jnp.float32), axis=0)
    input_grad = (
        jnp.einsum("re,de->rd", grad_joined, back_qkv, preferred_element_type=jnp.float32)
        + grad_one
    ).astype(jnp.bfloat16)
    shards = (
        lax.psum_scatter(d_qkv, ("ctx", "fsdp"), scatter_dimension=0, tiled=True),
        lax.psum_scatter(d_qkv_bias, ("ctx", "fsdp"), scatter_dimension=0, tiled=True),
        lax.psum_scatter(d_out, ("ctx", "fsdp"), scatter_dimension=0, tiled=True),
        lax.psum_scatter(d_out_bias, ("ctx", "fsdp"), scatter_dimension=0, tiled=True),
        lax.psum_scatter(d_gain_one, ("ctx", "fsdp"), scatter_dimension=0, tiled=True),
        lax.psum_scatter(d_shift_one, ("ctx", "fsdp"), scatter_dimension=0, tiled=True),
        lax.psum_scatter(d_up, ("ctx", "fsdp"), scatter_dimension=0, tiled=True),
        lax.psum_scatter(d_up_bias, ("ctx", "fsdp"), scatter_dimension=0, tiled=True),
        lax.psum_scatter(d_down, ("ctx", "fsdp"), scatter_dimension=0, tiled=True),
        lax.psum_scatter(d_down_bias, ("ctx", "fsdp"), scatter_dimension=0, tiled=True),
        lax.psum_scatter(d_gain_two, ("ctx", "fsdp"), scatter_dimension=0, tiled=True),
        lax.psum_scatter(d_shift_two, ("ctx", "fsdp"), scatter_dimension=0, tiled=True),
        lax.psum_scatter(d_proj, ("ctx", "fsdp"), scatter_dimension=0, tiled=True),
    )
    totals = (
        lax.psum(shards[0].astype(jnp.bfloat16), "slot").astype(jnp.float32),
        lax.psum(shards[1].astype(jnp.bfloat16), "slot").astype(jnp.float32),
        lax.psum(shards[2].astype(jnp.bfloat16), "slot").astype(jnp.float32),
        lax.psum(shards[3].astype(jnp.bfloat16), "slot").astype(jnp.float32),
        lax.psum(shards[4].astype(jnp.bfloat16), "slot").astype(jnp.float32),
        lax.psum(shards[5].astype(jnp.bfloat16), "slot").astype(jnp.float32),
        lax.psum(shards[6].astype(jnp.bfloat16), "slot").astype(jnp.float32),
        lax.psum(shards[7].astype(jnp.bfloat16), "slot").astype(jnp.float32),
        lax.psum(shards[8].astype(jnp.bfloat16), "slot").astype(jnp.float32),
        lax.psum(shards[9].astype(jnp.bfloat16), "slot").astype(jnp.float32),
        lax.psum(shards[10].astype(jnp.bfloat16), "slot").astype(jnp.float32),
        lax.psum(shards[11].astype(jnp.bfloat16), "slot").astype(jnp.float32),
        lax.psum(shards[12].astype(jnp.bfloat16), "slot").astype(jnp.float32),
    )
    return (
        out_low.reshape(groups, tok_slot, width),
        projected.astype(jnp.bfloat16).reshape(groups, tok_slot, -1),
        input_grad.reshape(groups, tok_slot, width),
        totals[0],
        totals[1],
        totals[2],
        totals[3],
        totals[4],
        totals[5],
        totals[6],
        totals[7],
        totals[8],
        totals[9],
        totals[10],
        totals[11],
        totals[12],
    )


def solution(mesh):
    n_slot, n_ctx, n_fsdp = (mesh.shape[a] for a in ("slot", "ctx", "fsdp"))
    rows_axes = ("ctx", "fsdp")
    step = per_device
    if n_slot == 2 and n_fsdp % 2 == 0 and n_ctx * n_fsdp == H:
        mesh = Mesh(
            mesh.devices.reshape(n_slot, n_ctx, n_fsdp // 2, 2), ("slot", "ctx", "x", "core")
        )
        rows_axes = GROUP
        step = head_device
    in_specs = (
        P("slot", rows_axes, None),
        P("slot"),
        P(rows_axes, None),
        P(rows_axes),
        P(rows_axes, None),
        P(rows_axes),
        P(rows_axes),
        P(rows_axes),
        P(rows_axes, None),
        P(rows_axes),
        P(rows_axes, None),
        P(rows_axes),
        P(rows_axes),
        P(rows_axes),
        P(rows_axes, None),
        P("slot", rows_axes, None),
        P("slot", rows_axes, None),
    )
    out_specs = (
        P("slot", rows_axes, None),
        P("slot", rows_axes, None),
        P("slot", rows_axes, None),
        P(rows_axes, None),
        P(rows_axes),
        P(rows_axes, None),
        P(rows_axes),
        P(rows_axes),
        P(rows_axes),
        P(rows_axes, None),
        P(rows_axes),
        P(rows_axes, None),
        P(rows_axes),
        P(rows_axes),
        P(rows_axes),
        P(rows_axes, None),
    )
    return jax.shard_map(
        step, mesh=mesh, in_specs=in_specs, out_specs=out_specs, check_vma=False
    )
```

```python
from functools import partial

import jax
import jax.numpy as jnp
from jax import lax
from jax.experimental import pallas as pl
from jax.experimental.pallas import tpu as pltpu
from jax.sharding import Mesh
from jax.sharding import PartitionSpec as P

H = 16
HD = 64
LN_EPS = 1e-05
NEG_FILL = -1e30
F32 = jnp.float32
BF16 = jnp.bfloat16
GROUP = ("ctx", "x", "core")
LANE = ("ctx", "x")
SWAP = [(0, 1), (1, 0)]
VMEM_LIMIT = 60 * 1024 * 1024


def mm(left, right):
    return jnp.dot(left, right, preferred_element_type=F32)


def contract(left, right, left_dim, right_dim):
    return lax.dot_general(
        left, right, (((left_dim,), (right_dim,)), ((), ())), preferred_element_type=F32
    )


def swap_core(value):
    return lax.ppermute(value, "core", SWAP)


def swap_slot(value):
    return lax.ppermute(value, "slot", SWAP)


def pick(stacked, index, axis):
    return lax.dynamic_index_in_dim(stacked, index, axis, keepdims=False)


MESH = pl.DeviceIdType.MESH


def at_device(**where):
    names = ("slot", "ctx", "x", "core")
    return tuple(where[n] if n in where else lax.axis_index(n) for n in names)


def greet(peers):
    barrier = pltpu.get_barrier_semaphore()
    for peer in peers:
        pl.semaphore_signal(barrier, inc=1, device_id=peer, device_id_type=MESH)
    pl.semaphore_wait(barrier, len(peers))


def group_peers(n_ctx, n_x):
    ctx, x, core = (lax.axis_index(n) for n in GROUP)
    peers = []
    for dz in range(n_ctx):
        for dx in range(n_x):
            for dc in range(2):
                if dz or dx or dc:
                    where = (lax.rem(ctx + dz, n_ctx), lax.rem(x + dx, n_x), lax.rem(core + dc, 2))
                    peers.append(where)
    return peers


def start_kernel(
    tok_ref, head_ref, small_ref, all_ref, heads_ref, smalls_ref,
    far_send, block_send, local_sem, head_recv, small_recv, block_recv, *, n_ctx, n_x
):
    part = tok_ref.shape[1]
    ctx, x, core = (lax.axis_index(n) for n in GROUP)
    me = (ctx * n_x + x) * 2 + core
    peers = group_peers(n_ctx, n_x)
    greet([at_device(ctx=z, x=a, core=c) for z, a, c in peers])

    def block_at(b):
        return all_ref.at[:, pl.ds(pl.multiple_of(b * part, part), part), :]

    pushes = []
    for k, (z, a, c) in enumerate(peers):
        them = (z * n_x + a) * 2 + c
        target = at_device(ctx=z, x=a, core=c)
        pushes.append(pltpu.make_async_remote_copy(
            head_ref.at[them], heads_ref.at[me], far_send.at[2 * k], head_recv.at[me],
            device_id=target, device_id_type=MESH))
        pushes.append(pltpu.make_async_remote_copy(
            small_ref, smalls_ref.at[me], far_send.at[2 * k + 1], small_recv.at[me],
            device_id=target, device_id_type=MESH))
    locals_ = [
        pltpu.make_async_copy(tok_ref, block_at(me), local_sem.at[0]),
        pltpu.make_async_copy(head_ref.at[me], heads_ref.at[me], local_sem.at[1]),
        pltpu.make_async_copy(small_ref, smalls_ref.at[me], local_sem.at[2]),
    ]

    def send(b, source, lane, target):
        return pltpu.make_async_remote_copy(
            source, block_at(b), block_send.at[lane, b], block_recv.at[b],
            device_id=target, device_id_type=MESH)

    up = at_device(ctx=lax.rem(ctx + 1, n_ctx))
    down = at_device(ctx=lax.rem(ctx + n_ctx - 1, n_ctx))
    side = at_device(x=1 - x)
    twin = at_device(core=1 - core)

    def here(b):
        return send(b, block_at(b), 0, twin)

    @pl.when(ctx + 1 < n_ctx)
    def _():
        send(me, tok_ref, 0, up).start()

    @pl.when(ctx > 0)
    def _():
        send(me, tok_ref, 1, down).start()

    send(me, tok_ref, 2, side).start()
    for push in pushes:
        push.start()
    send(me, tok_ref, 3, twin).start()
    for copy in locals_:
        copy.start()

    for r in range(1, n_ctx):
        low = ctx - r
        high = ctx + r

        @pl.when(low >= 0)
        def _():
            b = (low * n_x + x) * 2 + core
            here(b).wait_recv()

            @pl.when(ctx + 1 < n_ctx)
            def _():
                send(b, block_at(b), 0, up).start()

            send(b, block_at(b), 2, side).start()
            send(b, block_at(b), 3, twin).start()

        @pl.when(high < n_ctx)
        def _():
            b = (high * n_x + x) * 2 + core
            here(b).wait_recv()

            @pl.when(ctx > 0)
            def _():
                send(b, block_at(b), 1, down).start()

            send(b, block_at(b), 2, side).start()
            send(b, block_at(b), 3, twin).start()

    def from_side(z):
        b = (z * n_x + (1 - x)) * 2 + core
        here(b).wait_recv()
        send(b, block_at(b), 3, twin).start()

    from_side(ctx)
    for r in range(1, n_ctx):
        @pl.when(ctx - r >= 0)
        def _():
            from_side(ctx - r)

        @pl.when(ctx + r < n_ctx)
        def _():
            from_side(ctx + r)

    for z in range(n_ctx):
        for a in range(n_x):
            here((z * n_x + a) * 2 + 1 - core).wait_recv()
    for k, (z, a, c) in enumerate(peers):
        them = (z * n_x + a) * 2 + c
        pltpu.make_async_remote_copy(
            head_ref.at[them], heads_ref.at[them], far_send.at[2 * k], head_recv.at[them],
            device_id=twin, device_id_type=MESH).wait_recv()
        pltpu.make_async_remote_copy(
            small_ref, smalls_ref.at[them], far_send.at[2 * k + 1], small_recv.at[them],
            device_id=twin, device_id_type=MESH).wait_recv()
    for push in pushes:
        push.wait_send()
    for copy in locals_:
        copy.wait()

    for z in range(n_ctx):
        b = (z * n_x + x) * 2 + core

        @pl.when((z <= ctx) & (ctx + 1 < n_ctx))
        def _():
            send(b, block_at(b), 0, up).wait_send()

        @pl.when((z >= ctx) & (ctx > 0))
        def _():
            send(b, block_at(b), 1, down).wait_send()

        send(b, block_at(b), 2, side).wait_send()
        send(b, block_at(b), 3, twin).wait_send()
        other = (z * n_x + (1 - x)) * 2 + core
        send(other, block_at(other), 3, twin).wait_send()


def gather_start(tokens, heads, small):
    n_ctx, n_x = lax.axis_size("ctx"), lax.axis_size("x")
    n = 2 * n_ctx * n_x
    slots, part, width = tokens.shape
    vmem = pl.BlockSpec(memory_space=pltpu.VMEM)
    anywhere = pl.BlockSpec(memory_space=pl.ANY)
    dma = pltpu.SemaphoreType.DMA
    return pl.pallas_call(
        partial(start_kernel, n_ctx=n_ctx, n_x=n_x),
        in_specs=[vmem, vmem, vmem],
        out_specs=[anywhere, vmem, vmem],
        out_shape=[
            jax.ShapeDtypeStruct((slots, n * part, width), tokens.dtype),
            jax.ShapeDtypeStruct(heads.shape, heads.dtype),
            jax.ShapeDtypeStruct((n,) + small.shape, small.dtype),
        ],
        scratch_shapes=[
            dma((2 * (n - 1),)), dma((4, n)), dma((3,)), dma((n,)), dma((n,)), dma((n,))
        ],
        compiler_params=pltpu.CompilerParams(
            collective_id=1, has_side_effects=True, vmem_limit_bytes=VMEM_LIMIT
        ),
        cost_estimate=pl.CostEstimate(
            flops=0, bytes_accessed=2 * n * tokens.size, transcendentals=0
        ),
        name="gather_start",
    )(tokens, heads, small)


def finish_kernel(
    up_ref, out_ref, small_ref, qkv_ref, red_ref,
    g_down, g_up, g_out, g_small, g_qkv,
    x_up, x_out, s_up, s_out, z_up, z_out, own_up, own_out,
    smalls, own_small, pair_small, qkvs, pair_qkv, pair_down, pair_out, last_up, low_up,
    far_send, small_recv, qkv_recv, x_send, x_recv, z_send, z_recv, y_send, y_recv, *, n_ctx, n_x
):
    ctx, x, core = (lax.axis_index(n) for n in GROUP)
    slot = lax.axis_index("slot")
    me = (ctx * n_x + x) * 2 + core
    shard = g_up.shape[0]
    part = g_down.shape[0] // 2
    peers = group_peers(n_ctx, n_x)
    across = at_device(slot=1 - slot)
    corner = at_device(slot=1 - slot, core=1 - core)
    twin = at_device(core=1 - core)
    side = at_device(x=1 - x)
    greet([at_device(ctx=z, x=a, core=c) for z, a, c in peers] + [across, corner])

    def remote(source, target_ref, send_sem, recv_sem, target):
        return pltpu.make_async_remote_copy(
            source, target_ref, send_sem, recv_sem, device_id=target, device_id_type=MESH)

    started = []

    def launch(copy):
        copy.start()
        started.append(copy)
        return copy

    first_up, first_out, places = [], [], []
    for j in range(n_ctx):
        place = lax.rem(ctx + 1 + j, n_ctx)
        places.append(place)
        there = place * n_x + 1 - x
        first_up.append(launch(remote(
            up_ref.at[there], x_up.at[j], x_send.at[0, j], x_recv.at[0, j], side)))
        first_out.append(launch(remote(
            out_ref.at[there], x_out.at[j], x_send.at[1, j], x_recv.at[1, j], side)))
    down_copy = launch(remote(red_ref, pair_down, y_send.at[0], y_recv.at[0], across))
    for k, (z, a, c) in enumerate(peers):
        them = (z * n_x + a) * 2 + c
        target = at_device(ctx=z, x=a, core=c)
        launch(remote(
            qkv_ref.at[them], qkvs.at[me], far_send.at[2 * k], qkv_recv.at[me], target))
        launch(remote(
            small_ref.at[them], smalls.at[me], far_send.at[2 * k + 1], small_recv.at[me], target))
    qkvs[me] = qkv_ref[me]
    smalls[me] = small_ref[me]

    second_up, second_out = [], []
    for j in range(n_ctx):
        mine = places[j] * n_x + x
        first_up[j].wait_recv()
        first_out[j].wait_recv()
        sum_up = up_ref[mine].astype(F32) + x_up[j].astype(F32)
        sum_out = out_ref[mine].astype(F32) + x_out[j].astype(F32)
        if j < n_ctx - 1:
            s_up[j] = sum_up.astype(BF16)
            s_out[j] = sum_out.astype(BF16)
            target = at_device(ctx=places[j])
            second_up.append(launch(remote(
                s_up.at[j], z_up.at[j], z_send.at[0, j], z_recv.at[0, j], target)))
            second_out.append(launch(remote(
                s_out.at[j], z_out.at[j], z_send.at[1, j], z_recv.at[1, j], target)))
        else:
            own_up[...] = sum_up
            own_out[...] = sum_out

    for z, a, c in peers:
        them = (z * n_x + a) * 2 + c
        remote(
            qkv_ref.at[them], qkvs.at[them], far_send.at[0], qkv_recv.at[them], twin
        ).wait_recv()
        remote(
            small_ref.at[them], smalls.at[them], far_send.at[1], small_recv.at[them], twin
        ).wait_recv()
    qkv_copy = launch(remote(qkvs, pair_qkv, y_send.at[1], y_recv.at[1], across))
    own_small[...] = jnp.sum(smalls[...].astype(F32), axis=0).astype(BF16)
    small_copy = launch(remote(own_small, pair_small, y_send.at[2], y_recv.at[2], across))

    for j in range(n_ctx - 1):
        second_out[j].wait_recv()
        own_out[...] += z_out[j].astype(F32)
    s_out[n_ctx - 1] = own_out[...].astype(BF16)
    out_copy = launch(remote(
        s_out.at[n_ctx - 1], pair_out, y_send.at[3], y_recv.at[3], across))
    for j in range(n_ctx - 1):
        second_up[j].wait_recv()
        own_up[...] += z_up[j].astype(F32)
    low_up[...] = own_up[...].astype(BF16).reshape(low_up.shape)
    quarter_copies = [
        launch(remote(low_up.at[1 - core], last_up.at[0], y_send.at[4], y_recv.at[4], twin)),
        launch(remote(low_up.at[core], last_up.at[1], y_send.at[5], y_recv.at[5], across)),
        launch(remote(low_up.at[1 - core], last_up.at[2], y_send.at[6], y_recv.at[6], corner)),
    ]

    half = pl.multiple_of(slot * part, part)
    other_half = pl.multiple_of((1 - slot) * part, part)
    g_down[pl.ds(half, part), :] = red_ref[...].astype(F32)
    down_copy.wait_recv()
    g_down[pl.ds(other_half, part), :] = pair_down[...].astype(F32)
    qkv_copy.wait_recv()
    g_qkv[...] = qkvs[...].astype(F32) + pair_qkv[...].astype(F32)
    small_copy.wait_recv()
    g_small[...] = own_small[...].astype(F32) + pair_small[...].astype(F32)
    out_copy.wait_recv()
    g_out[...] = s_out[n_ctx - 1].astype(F32) + pair_out[...].astype(F32)

    def place_quarter(rows, quarter_core, quarter_slot):
        for k in range(n_ctx * n_x):
            at = pl.multiple_of(((2 * k + quarter_core) * 2 + quarter_slot) * part, part)
            g_up[:, pl.ds(at, part)] = rows[:, k * part : (k + 1) * part].astype(F32)

    place_quarter(low_up[core], core, slot)
    quarter_copies[0].wait_recv()
    place_quarter(last_up[0], 1 - core, slot)
    quarter_copies[1].wait_recv()
    place_quarter(last_up[1], core, 1 - slot)
    quarter_copies[2].wait_recv()
    place_quarter(last_up[2], 1 - core, 1 - slot)
    for copy in started:
        copy.wait_send()


def finish_grads(up, out, small, qkv, red_down):
    n_ctx, n_x = lax.axis_size("ctx"), lax.axis_size("x")
    n = 2 * n_ctx * n_x
    part, width = red_down.shape
    shard = out.shape[1]
    vmem = pl.BlockSpec(memory_space=pltpu.VMEM)
    dma = pltpu.SemaphoreType.DMA

    def low(*shape):
        return pltpu.VMEM(shape, BF16)

    def wide(*shape):
        return jax.ShapeDtypeStruct(shape, F32)

    return pl.pallas_call(
        partial(finish_kernel, n_ctx=n_ctx, n_x=n_x),
        in_specs=[vmem] * 5,
        out_specs=[vmem] * 5,
        out_shape=[
            wide(2 * part, width),
            wide(shard, 4 * up.shape[2]),
            wide(shard, width),
            wide(*small.shape[1:]),
            wide(*qkv.shape),
        ],
        scratch_shapes=[
            low(n_ctx, *up.shape[1:]),
            low(n_ctx, *out.shape[1:]),
            low(n_ctx - 1, *up.shape[1:]),
            low(n_ctx, *out.shape[1:]),
            low(n_ctx - 1, *up.shape[1:]),
            low(n_ctx - 1, *out.shape[1:]),
            pltpu.VMEM(up.shape[1:], F32),
            pltpu.VMEM(out.shape[1:], F32),
            low(*small.shape),
            low(*small.shape[1:]),
            low(*small.shape[1:]),
            low(*qkv.shape),
            low(*qkv.shape),
            low(part, width),
            low(*out.shape[1:]),
            low(3, shard, up.shape[2]),
            low(2, shard, up.shape[2]),
            dma((2 * (n - 1),)),
            dma((n,)),
            dma((n,)),
            dma((2, n_ctx)),
            dma((2, n_ctx)),
            dma((2, n_ctx - 1)),
            dma((2, n_ctx - 1)),
            dma((7,)),
            dma((7,)),
        ],
        compiler_params=pltpu.CompilerParams(
            collective_id=2, has_side_effects=True, vmem_limit_bytes=VMEM_LIMIT
        ),
        cost_estimate=pl.CostEstimate(flops=0, bytes_accessed=16 * up.size, transcendentals=0),
        name="finish_grads",
    )(up, out, small, qkv, red_down)


def project_kernel(tok_ref, w_ref, b_ref, cos_ref, sin_ref, q_ref, k_ref, v_ref):
    joined = mm(tok_ref[...], w_ref[...]) + b_ref[...]
    wide = 2 * HD
    turned = joined[:, :wide] * cos_ref[...] + joined[:, wide : 2 * wide] * sin_ref[...]
    q_ref[...] = (turned[:, :HD].astype(BF16) * HD ** (-0.5)).astype(BF16)
    k_ref[...] = turned[:, HD:].astype(BF16)
    v_ref[...] = joined[:, 2 * wide :].astype(BF16)


def project(tokens, weight, bias, cosine, sine):
    rows, width = tokens.shape
    seq = cosine.shape[0]
    block = min(512, seq)
    per_slot = seq // block
    cols = weight.shape[1]
    head_out = jax.ShapeDtypeStruct((rows, HD), BF16)
    head_spec = pl.BlockSpec((block, HD), lambda i: (i, 0))
    return pl.pallas_call(
        project_kernel,
        grid=(rows // block,),
        in_specs=[
            pl.BlockSpec((block, width), lambda i: (i, 0)),
            pl.BlockSpec((width, cols), lambda i: (0, 0)),
            pl.BlockSpec((1, cols), lambda i: (0, 0)),
            pl.BlockSpec((block, 2 * HD), lambda i: (i % per_slot, 0)),
            pl.BlockSpec((block, 2 * HD), lambda i: (i % per_slot, 0)),
        ],
        out_specs=[head_spec] * 3,
        out_shape=[head_out] * 3,
        compiler_params=pltpu.CompilerParams(vmem_limit_bytes=VMEM_LIMIT),
        cost_estimate=pl.CostEstimate(
            flops=2 * rows * width * cols, bytes_accessed=2 * rows * width, transcendentals=0
        ),
        name="project",
    )(tokens, weight, bias, cosine, sine)


QB = 512
KB = 512


def forward_kernel(
    len_ref, core_ref, q_ref, k_ref, v_ref, out_ref, send_ref, norm_ref, *, part
):
    length = len_ref[pl.program_id(0)]
    core = core_ref[0]
    queries = q_ref[0]
    rows = queries.shape[0]

    def step(j, state):
        highest, total, mix = state
        start = pl.multiple_of(j * KB, KB)
        scores = contract(queries, k_ref[0, pl.ds(start, KB), :], 1, 1)
        ids = start + lax.broadcasted_iota(jnp.int32, (1, KB), 1)
        scores = jnp.where(ids < length, scores, NEG_FILL)
        higher = jnp.maximum(highest, jnp.max(scores, axis=1, keepdims=True))
        fade = jnp.exp(highest - higher)
        weights = jnp.exp(scores - higher)
        total = total * fade + jnp.sum(weights, axis=1, keepdims=True)
        mix = mix * fade + mm(weights.astype(BF16), v_ref[0, pl.ds(start, KB), :])
        return higher, total, mix

    blocks = (length + KB - 1) // KB
    highest, total, mix = lax.fori_loop(
        0,
        blocks,
        step,
        (
            jnp.full((rows, 1), NEG_FILL, F32),
            jnp.zeros((rows, 1), F32),
            jnp.zeros((rows, HD), F32),
        ),
    )
    mix = mix / total
    out_ref[0] = mix
    log_norm = jnp.broadcast_to(highest + jnp.log(total), (rows, 128))
    norm_ref[0] = jnp.transpose(log_norm)[0:1, :]
    low = mix.astype(BF16)
    for chip in range(rows // (2 * part)):
        for half in range(2):
            at = (2 * chip + half) * part
            send_ref[chip, half ^ core, 0] = low[at : at + part]


def attend(lengths, core, queries, keys, values, part):
    slots, seq, _ = queries.shape
    chips = seq // (2 * part)
    spec_q = pl.BlockSpec((1, QB, HD), lambda s, i, *_: (s, i, 0))
    spec_k = pl.BlockSpec((1, seq, HD), lambda s, i, *_: (s, 0, 0))
    return pl.pallas_call(
        partial(forward_kernel, part=part),
        grid_spec=pltpu.PrefetchScalarGridSpec(
            num_scalar_prefetch=2,
            grid=(slots, seq // QB),
            in_specs=[spec_q, spec_k, spec_k],
            out_specs=[
                spec_q,
                pl.BlockSpec(
                    (QB // (2 * part), 2, 1, part, HD), lambda s, i, *_: (i, 0, s, 0, 0)
                ),
                pl.BlockSpec((1, 1, QB), lambda s, i, *_: (s, 0, i)),
            ],
        ),
        out_shape=[
            jax.ShapeDtypeStruct((slots, seq, HD), F32),
            jax.ShapeDtypeStruct((chips, 2, slots, part, HD), BF16),
            jax.ShapeDtypeStruct((slots, 1, seq), F32),
        ],
        compiler_params=pltpu.CompilerParams(vmem_limit_bytes=VMEM_LIMIT),
        cost_estimate=pl.CostEstimate(
            flops=16 * slots * seq * seq * HD,
            bytes_accessed=8 * slots * seq * HD,
            transcendentals=slots * seq * seq,
        ),
        name="attend",
    )(lengths, core, queries, keys, values)


def backward_kernel(
    len_ref, q_ref, k_ref, v_ref, g_ref, norm_ref, dot_ref, dq_ref, dk_ref, dv_ref, dqt
):
    length = len_ref[pl.program_id(0)]
    j = pl.program_id(1)
    start = j * KB
    key_block = k_ref[0]
    value_block = v_ref[0]

    @pl.when(j == 0)
    def _():
        dqt[...] = jnp.zeros_like(dqt)

    turned = jnp.transpose(key_block.astype(F32)).astype(BF16)
    ids = start + lax.broadcasted_iota(jnp.int32, (KB, 1), 0)
    shift = jnp.where(ids < length, 0.0, NEG_FILL)

    def step(i, state):
        key_grad, value_grad = state
        at = pl.multiple_of(i * QB, QB)
        queries = q_ref[0, pl.ds(at, QB), :]
        grads = g_ref[0, pl.ds(at, QB), :]
        scores = contract(key_block, queries, 1, 1) + shift
        probs = jnp.exp(scores - norm_ref[0, :, pl.ds(at, QB)])
        grad_probs = contract(value_block, grads, 1, 1)
        grad_scores = (probs * (grad_probs - dot_ref[0, :, pl.ds(at, QB)])).astype(BF16)
        value_grad = value_grad + mm(probs.astype(BF16), grads)
        key_grad = key_grad + mm(grad_scores, queries)
        dqt[:, pl.ds(at, QB)] += mm(turned, grad_scores)
        return key_grad, value_grad

    blocks = jnp.where(start < length, (length + QB - 1) // QB, 0)
    zero = jnp.zeros((KB, HD), F32)
    key_grad, value_grad = lax.fori_loop(0, blocks, step, (zero, zero))
    dk_ref[0] = key_grad
    dv_ref[0] = value_grad

    @pl.when(j == pl.num_programs(1) - 1)
    def _():
        dq_ref[0] = jnp.transpose(dqt[...])


def attend_back(lengths, queries, keys, values, grads, norms, dots):
    slots, seq, _ = queries.shape
    whole = pl.BlockSpec((1, seq, HD), lambda s, j, *_: (s, 0, 0))
    block = pl.BlockSpec((1, KB, HD), lambda s, j, *_: (s, j, 0))
    row = pl.BlockSpec((1, 1, seq), lambda s, j, *_: (s, 0, 0))
    out = jax.ShapeDtypeStruct((slots, seq, HD), F32)
    return pl.pallas_call(
        backward_kernel,
        grid_spec=pltpu.PrefetchScalarGridSpec(
            num_scalar_prefetch=1,
            grid=(slots, seq // KB),
            in_specs=[whole, block, block, whole, row, row],
            out_specs=[whole, block, block],
            scratch_shapes=[pltpu.VMEM((HD, seq), F32)],
        ),
        out_shape=[out] * 3,
        compiler_params=pltpu.CompilerParams(vmem_limit_bytes=VMEM_LIMIT),
        cost_estimate=pl.CostEstimate(
            flops=40 * slots * seq * seq * HD,
            bytes_accessed=20 * slots * seq * HD,
            transcendentals=slots * seq * seq,
        ),
        name="attend_back",
    )(lengths, queries, keys, values, grads, norms, dots)


def norm_forward(values, gain, shift):
    center = values - jnp.mean(values, axis=-1, keepdims=True)
    spread = jnp.mean(center * center, axis=-1, keepdims=True)
    root = lax.rsqrt(spread + LN_EPS)
    unit = center * root
    return unit * gain + shift, unit, root


def norm_backward(grad, unit, root, gain):
    scaled = grad * gain
    inner = scaled - jnp.mean(scaled, axis=-1, keepdims=True)
    inner = inner - unit * jnp.mean(scaled * unit, axis=-1, keepdims=True)
    return root * inner, jnp.sum(grad * unit, axis=0), jnp.sum(grad, axis=0)


def gelu_pair(values):
    half = 0.5 + 0.5 * lax.erf(values * 0.7071067811865476)
    bell = jnp.exp(-0.5 * values * values) * 0.3989422804014327
    return values * half, half + values * bell


def rope_rows(positions):
    halfway = HD // 2
    ladder = jnp.arange(halfway, dtype=F32) * (2.0 / HD)
    frequency = jnp.power(jnp.float32(10000.0), -ladder)
    angles = positions[:, None] * frequency[None, :]
    return jnp.cos(angles), jnp.sin(angles)


def head_device(
    tokens,
    lengths,
    w_qkv,
    b_qkv,
    w_out,
    b_out,
    ln1_gain,
    ln1_bias,
    w_up,
    b_up,
    w_down,
    b_down,
    ln2_gain,
    ln2_bias,
    w_proj,
    cot_out,
    cot_emb,
):
    n_lane = lax.axis_size("ctx") * lax.axis_size("x")
    n_group = 2 * n_lane
    core = lax.axis_index("core")
    slot = lax.axis_index("slot")
    chip = lax.axis_index("ctx") * lax.axis_size("x") + lax.axis_index("x")
    me = 2 * chip + core
    slots, part, width = tokens.shape
    seq = part * n_group
    rows = slots * part
    shard = width // n_group
    ff_shard = w_down.shape[0]
    ff_half = ff_shard // 2
    proj = w_proj.shape[1]
    head_cols = 3 * HD

    small = jnp.concatenate(
        [b_qkv, b_out, ln1_gain, ln1_bias, b_up, b_down, ln2_gain, ln2_bias]
    )
    small_at = [0]
    for piece in (b_qkv, b_out, ln1_gain, ln1_bias, b_up, b_down, ln2_gain, ln2_bias):
        small_at.append(small_at[-1] + piece.shape[0])
    small_rows = -(-small.shape[0] // proj)
    small_rows = -(-small_rows // 16) * 16
    small = jnp.pad(small, (0, small_rows * proj - small.shape[0])).reshape(small_rows, proj)
    by_head = w_qkv.reshape(shard, 3, n_group, HD).transpose(2, 0, 1, 3)
    all_tokens, my_head, packed = gather_start(
        tokens,
        by_head.reshape(n_group, shard, head_cols),
        jnp.concatenate([w_proj, small], axis=0),
    )
    proj_full = packed[:, :shard].reshape(width, proj)
    smalls = packed[:, shard:].reshape(n_group, small_rows * proj).astype(F32)
    qkv_bias, out_bias, gain_one, shift_one, up_bias, down_bias, gain_two, shift_two = (
        smalls[:, a:b].reshape(-1) for a, b in zip(small_at[:-1], small_at[1:])
    )

    my_head = my_head.reshape(width, 3, HD)
    all_tokens = all_tokens.reshape(slots * seq, width)

    def with_swapped(joined):
        first = joined[:, 0:2]
        halves = first.reshape(-1, 2, 2, HD // 2)
        swapped = jnp.stack([-halves[:, :, 1], halves[:, :, 0]], axis=2)
        return jnp.concatenate(
            [
                first.reshape(-1, 2 * HD),
                swapped.reshape(-1, 2 * HD),
                joined[:, 2],
            ],
            axis=1,
        )

    head_weight = with_swapped(my_head)
    head_bias = with_swapped(pick(qkv_bias.reshape(1, 3, n_group, HD), me, 2))
    cosine, sine = rope_rows(jnp.arange(seq, dtype=jnp.int32).astype(F32))
    cos_wide = jnp.tile(cosine, (1, 4))
    sin_wide = jnp.tile(sine, (1, 4))
    queries, keys, values = project(all_tokens, head_weight, head_bias, cos_wide, sin_wide)
    queries, keys, values = (t.reshape(slots, seq, HD) for t in (queries, keys, values))

    def two_lanes(mine, theirs):
        low_first = jnp.stack([mine, theirs], axis=0)
        high_first = jnp.stack([theirs, mine], axis=0)
        return jnp.where(core == 0, low_first, high_first)

    out_lane = lax.all_gather(w_out, LANE, axis=0, tiled=True)
    up_split = w_up.reshape(shard, n_lane, 2, 2, ff_half)
    up_mine = pick(up_split, core, 2)
    up_theirs = swap_core(pick(up_split, 1 - core, 2))
    up_chip = two_lanes(up_mine, up_theirs).reshape(2 * shard, n_lane, 2, ff_half)
    down_split = w_down.reshape(2, ff_half, width)
    up_part = pick(up_chip, slot, 2).reshape(2 * shard, n_lane * ff_half)
    up = lax.all_gather(up_part, LANE, axis=0, tiled=True)
    down = lax.all_gather(pick(down_split, slot, 0), LANE, axis=0, tiled=True)
    bias_lane = pick(up_bias.reshape(n_lane, 2, 2, ff_half), core, 1)
    up_bias_own = pick(bias_lane, slot, 1).reshape(-1)

    qkv_split = w_qkv.reshape(shard, 3, n_lane, 2, HD)
    qkv_mine = pick(qkv_split, core, 3)
    qkv_theirs = swap_core(pick(qkv_split, 1 - core, 3))
    qkv_chip = two_lanes(qkv_mine, qkv_theirs).transpose(0, 1, 3, 2, 4)
    qkv_lane = lax.all_gather(
        qkv_chip.reshape(2 * shard, n_lane * head_cols), LANE, axis=0, tiled=True
    )

    mixture, send, norms = attend(
        lengths, core.reshape(1).astype(jnp.int32), queries, keys, values, part
    )
    merged = lax.all_to_all(send, LANE, 0, 0, tiled=True)
    merged = merged.transpose(1, 2, 3, 0, 4).reshape(2 * rows, n_lane * HD)

    def own_sum(partial_rows):
        return partial_rows[:rows] + swap_core(partial_rows[rows:])

    def both(value):
        return jnp.concatenate([value, swap_core(value)], axis=0)

    def quad(value):
        pair = jnp.concatenate([value, swap_slot(value)], axis=0)
        return jnp.concatenate([pair, swap_core(pair)], axis=0)

    def quad_sum(partial_rows):
        pair = partial_rows[: 2 * rows] + swap_core(partial_rows[2 * rows :])
        return pair[:rows] + swap_slot(pair[rows:].astype(BF16)).astype(F32)

    flat_tokens = tokens.reshape(rows, width).astype(F32)
    attended = own_sum(mm(merged, out_lane)) + out_bias
    hidden_one, unit_one, root_one = norm_forward(flat_tokens + attended, gain_one, shift_one)
    hidden_low = quad(hidden_one.astype(BF16))

    active, slope = gelu_pair(mm(hidden_low, up) + up_bias_own)
    active = active.astype(BF16)
    downward = quad_sum(mm(active, down)) + down_bias
    out_rows, unit_two, root_two = norm_forward(hidden_one + downward, gain_two, shift_two)
    out_low = out_rows.astype(BF16)
    embeds = mm(out_low, proj_full).astype(BF16)

    place = me * part + jnp.arange(part, dtype=jnp.int32)
    live = (place[None, :] < lengths[:, None]).reshape(rows, 1)
    grad_out = jnp.where(live, cot_out.reshape(rows, width).astype(F32), 0.0)
    grad_emb = jnp.where(live, cot_emb.reshape(rows, proj), 0)
    d_proj = contract(out_low, grad_emb, 0, 0)
    grad_full = grad_out + contract(grad_emb, proj_full, 1, 1)
    grad_two, d_gain_two, d_shift_two = norm_backward(grad_full, unit_two, root_two, gain_two)
    grad_down_own = grad_two.astype(BF16)
    d_down_bias = jnp.sum(grad_down_own.astype(F32), axis=0)
    grad_down = quad(grad_down_own)
    grad_up = (contract(grad_down, down, 1, 1) * slope).astype(BF16)
    d_down = contract(active, grad_down, 0, 0).astype(BF16)
    d_up = contract(hidden_low, grad_up, 0, 0).astype(BF16)
    up_bias_own_grad = jnp.sum(grad_up.astype(F32), axis=0)
    grad_hidden = grad_two + quad_sum(contract(grad_up, up, 1, 1))
    grad_one, d_gain_one, d_shift_one = norm_backward(grad_hidden, unit_one, root_one, gain_one)
    grad_att_own = grad_one.astype(BF16)
    d_out_bias = jnp.sum(grad_att_own.astype(F32), axis=0)
    grad_att_own, qkv_lane = lax.optimization_barrier((grad_att_own, qkv_lane))
    grad_att = both(grad_att_own)
    grad_merged = contract(grad_att, out_lane, 1, 1).astype(BF16)
    grad_merged = grad_merged.reshape(2, slots, part, n_lane, HD).transpose(3, 0, 1, 2, 4)
    grad_heads = lax.all_to_all(grad_merged, LANE, 0, 0, tiled=True)

    def core_order(value):
        return jnp.where(core == 0, value, jnp.flip(value, axis=1))

    grad_heads = core_order(grad_heads).transpose(2, 0, 1, 3, 4).reshape(slots, seq, HD)

    d_out = contract(merged, grad_att, 0, 0).astype(BF16)

    red_down = lax.psum_scatter(d_down, LANE, scatter_dimension=0, tiled=True)

    spread = (
        (jnp.arange(2) == core)[:, None, None] & (jnp.arange(2) == slot)[None, :, None]
    ).astype(F32)
    up_bias_grad = up_bias_own_grad.reshape(n_lane, 1, 1, ff_half) * spread[None]
    vectors = (
        d_out_bias,
        d_gain_one,
        d_shift_one,
        up_bias_grad.reshape(-1),
        d_down_bias,
        d_gain_two,
        d_shift_two,
    )
    small_grad = jnp.concatenate([v.reshape(n_group, -1) for v in vectors], axis=1)
    small_cols = small_grad.shape[1]
    vec_rows = -(-small_cols // proj)
    vec_rows = -(-(shard + vec_rows) // 16) * 16 - shard
    small_grad = jnp.pad(small_grad, ((0, 0), (0, vec_rows * proj - small_cols)))
    small_grad = jnp.concatenate(
        [d_proj.reshape(n_group, shard, proj), small_grad.reshape(n_group, vec_rows, proj)], axis=1
    )
    row_dots = jnp.sum(grad_heads.astype(F32) * mixture, axis=-1).reshape(slots, 1, seq)
    grad_q, grad_k, grad_v = attend_back(
        lengths, queries, keys, values, grad_heads, norms, row_dots
    )

    def turn_back(value):
        first, second = value[..., : HD // 2], value[..., HD // 2 :]
        return jnp.concatenate(
            [first * cosine + second * sine, second * cosine - first * sine], axis=-1
        )

    grad_joined = jnp.concatenate(
        [turn_back(grad_q * HD ** (-0.5)), turn_back(grad_k), grad_v], axis=-1
    ).astype(BF16)
    d_qkv = contract(all_tokens, grad_joined.reshape(slots * seq, head_cols), 0, 0)
    d_qkv_bias = jnp.sum(grad_joined.astype(F32), axis=(0, 1))
    d_qkv = jnp.concatenate(
        [
            d_qkv.reshape(n_group, shard, head_cols),
            jnp.broadcast_to(d_qkv_bias, (n_group, 16, head_cols)),
        ],
        axis=1,
    ).astype(BF16)
    grad_w_down, grad_w_up, grad_w_out, small_sum, d_qkv = finish_grads(
        d_up.reshape(n_lane, 2 * shard, width),
        d_out.reshape(n_lane, shard, width),
        small_grad.astype(BF16),
        d_qkv,
        red_down,
    )
    grad_w_proj = small_sum[:shard]
    vec_sum = small_sum[shard:].reshape(-1)
    vec_outs = []
    at = 0
    for v in vectors:
        size = v.size // n_group
        vec_outs.append(vec_sum[at : at + size])
        at += size
    (
        grad_b_out,
        grad_gain_one,
        grad_shift_one,
        grad_b_up,
        grad_b_down,
        grad_gain_two,
        grad_shift_two,
    ) = vec_outs

    grad_w_qkv = (
        d_qkv[:, :shard].reshape(n_group, shard, 3, HD).transpose(1, 2, 0, 3).reshape(shard, 3 * width)
    )
    qkv_bias_grad = d_qkv[:, shard].reshape(n_group, 3, HD).transpose(1, 0, 2).reshape(-1)
    grad_b_qkv = lax.dynamic_slice(qkv_bias_grad, (me * b_qkv.shape[0],), (b_qkv.shape[0],))

    to_chips = grad_joined.reshape(slots, n_lane, 2, part, head_cols).transpose(1, 2, 0, 3, 4)
    joined_rows = lax.all_to_all(core_order(to_chips), LANE, 0, 0, tiled=True)
    joined_rows = joined_rows.transpose(1, 2, 3, 0, 4).reshape(2 * rows, n_lane * head_cols)
    input_grad = own_sum(contract(joined_rows, qkv_lane, 1, 1)) + grad_one

    return (
        out_low.reshape(slots, part, width),
        embeds.reshape(slots, part, proj),
        input_grad.astype(BF16).reshape(slots, part, width),
        grad_w_qkv,
        grad_b_qkv,
        grad_w_out,
        grad_b_out,
        grad_gain_one,
        grad_shift_one,
        grad_w_up,
        grad_b_up,
        grad_w_down,
        grad_b_down,
        grad_gain_two,
        grad_shift_two,
        grad_w_proj,
    )


def layer_norm(hidden, gain, shift):
    center = hidden - jnp.mean(hidden, axis=-1, keepdims=True)
    spread = jnp.mean(center * center, axis=-1, keepdims=True)
    return center * lax.rsqrt(spread + LN_EPS) * gain + shift


def rope_tables(positions, head_width):
    halfway = head_width // 2
    ladder = jnp.arange(halfway, dtype=jnp.float32) * (2.0 / head_width)
    frequency = jnp.power(jnp.float32(10000.0), -ladder)
    angles = positions[:, None] * frequency[None, :]
    return (jnp.cos(angles)[:, None, :], jnp.sin(angles)[:, None, :])


def rotate(values, cosine, sine_part):
    halfway = values.shape[-1] // 2
    first_half = values[..., :halfway]
    second_half = values[..., halfway:]
    return jnp.concatenate(
        [
            first_half * cosine - second_half * sine_part,
            second_half * cosine + first_half * sine_part,
        ],
        axis=-1,
    )


def block_scores(query_block, key_block, key_start, length, scale):
    scores = (
        jnp.einsum("qhd,khd->hqk", query_block, key_block, preferred_element_type=jnp.float32)
        * scale
    )
    key_ids = key_start + jnp.arange(key_block.shape[0], dtype=jnp.int32)
    return jnp.where((key_ids < length)[None, None, :], scores, NEG_FILL)


def per_device(
    tokens,
    lengths,
    w_qkv,
    b_qkv,
    w_out,
    b_out,
    ln1_gain,
    ln1_bias,
    w_up,
    b_up,
    w_down,
    b_down,
    ln2_gain,
    ln2_bias,
    w_proj,
    cot_out,
    cot_emb,
):
    n_fsdp = lax.axis_size("fsdp")
    n_ctx = lax.axis_size("ctx")
    ctx_at = lax.axis_index("ctx")
    fsdp_at = lax.axis_index("fsdp")
    groups, tok_slot, width = tokens.shape
    heads_here = H // n_fsdp
    lane_width = heads_here * HD
    span_rows = tok_slot * n_fsdp
    key_count = span_rows * n_ctx
    row_count = groups * tok_slot
    scale = HD ** (-0.5)
    query_rows = min(512, span_rows)
    key_rows = min(2048, key_count // 4)
    query_blocks = span_rows // query_rows
    key_blocks = key_count // key_rows
    key_starts = jnp.arange(key_blocks, dtype=jnp.int32) * key_rows
    qkv_full, qkv_bias, out_full, out_bias, gain_one, shift_one = (
        lax.all_gather(w_qkv, ("ctx", "fsdp"), axis=0, tiled=True),
        lax.all_gather(b_qkv, ("ctx", "fsdp"), axis=0, tiled=True),
        lax.all_gather(w_out, ("ctx", "fsdp"), axis=0, tiled=True),
        lax.all_gather(b_out, ("ctx", "fsdp"), axis=0, tiled=True),
        lax.all_gather(ln1_gain, ("ctx", "fsdp"), axis=0, tiled=True),
        lax.all_gather(ln1_bias, ("ctx", "fsdp"), axis=0, tiled=True),
    )
    token_pos = (ctx_at * n_fsdp + fsdp_at) * tok_slot + jnp.arange(tok_slot, dtype=jnp.int32)
    live_rows = (token_pos[None, :] < lengths[:, None]).reshape(row_count, 1)
    flat_tokens = tokens.reshape(row_count, width)
    joined = jnp.dot(flat_tokens, qkv_full, preferred_element_type=jnp.float32) + qkv_bias.astype(
        jnp.float32
    )
    cosine, sine_part = rope_tables(token_pos.astype(jnp.float32), HD)
    split_heads = joined.reshape(groups, tok_slot, 3, H, HD)
    rotated_query = rotate(split_heads[:, :, 0], cosine, sine_part)
    rotated_key = rotate(split_heads[:, :, 1], cosine, sine_part)
    packed = (
        jnp.stack([rotated_query, rotated_key, split_heads[:, :, 2]], axis=2)
        .astype(jnp.bfloat16)
        .reshape(groups, tok_slot, 3, n_fsdp, lane_width)
    )
    by_heads = lax.all_to_all(packed, "fsdp", split_axis=3, concat_axis=1, tiled=True)
    queries = by_heads[:, :, 0, 0]
    local_keys = by_heads[:, :, 1, 0]
    local_values = by_heads[:, :, 2, 0]
    all_keys, all_values = (
        lax.all_gather(local_keys, "ctx", axis=1, tiled=True),
        lax.all_gather(local_values, "ctx", axis=1, tiled=True),
    )

    def attend_slot(slot_item):
        slot_queries, slot_keys, slot_values, length = slot_item
        query_split = slot_queries.reshape(query_blocks, query_rows, heads_here, HD)
        key_split = slot_keys.reshape(key_blocks, key_rows, heads_here, HD)
        value_split = slot_values.reshape(key_blocks, key_rows, heads_here, HD)

        def per_query(query_block):

            def row_stats(state_pair, key_item):
                highest, running_sum = state_pair
                scores = block_scores(query_block, key_item[0], key_item[1], length, scale)
                new_high = jnp.maximum(highest, jnp.max(scores, axis=-1))
                running_sum = running_sum * jnp.exp(highest - new_high) + jnp.sum(
                    jnp.exp(scores - new_high[..., None]), axis=-1
                )
                return ((new_high, running_sum), None)

            start_state = (
                jnp.full((heads_here, query_rows), NEG_FILL, jnp.float32),
                jnp.zeros((heads_here, query_rows), jnp.float32),
            )
            highest, running_sum = lax.scan(row_stats, start_state, (key_split, key_starts))[0]
            log_norm = highest + jnp.log(running_sum)

            def weigh_values(accumulated, key_item):
                scores = block_scores(query_block, key_item[0], key_item[2], length, scale)
                weights = jnp.exp(scores - log_norm[..., None]).astype(jnp.bfloat16)
                return (
                    accumulated
                    + jnp.einsum(
                        "hqk,khd->qhd", weights, key_item[1], preferred_element_type=jnp.float32
                    ),
                    None,
                )

            mixture = lax.scan(
                weigh_values,
                jnp.zeros((query_rows, heads_here, HD), jnp.float32),
                (key_split, value_split, key_starts),
            )[0]
            return (mixture, log_norm)

        mixture, log_norm = lax.map(per_query, query_split)
        return (mixture.reshape(span_rows, lane_width), log_norm)

    mixture, log_norms = lax.map(attend_slot, (queries, all_keys, all_values, lengths))
    merged = lax.all_to_all(
        mixture.astype(jnp.bfloat16).reshape(groups, span_rows, 1, lane_width),
        "fsdp",
        split_axis=1,
        concat_axis=2,
        tiled=True,
    ).reshape(row_count, width)
    attended = jnp.dot(merged, out_full, preferred_element_type=jnp.float32) + out_bias.astype(
        jnp.float32
    )
    hidden_one, pull_one = jax.vjp(
        layer_norm,
        flat_tokens.astype(jnp.float32) + attended,
        gain_one.astype(jnp.float32),
        shift_one.astype(jnp.float32),
    )
    hidden_low = hidden_one.astype(jnp.bfloat16)
    up_full, up_bias, down_full, down_bias, gain_two, shift_two, proj_full = (
        lax.all_gather(w_up, ("ctx", "fsdp"), axis=0, tiled=True),
        lax.all_gather(b_up, ("ctx", "fsdp"), axis=0, tiled=True),
        lax.all_gather(w_down, ("ctx", "fsdp"), axis=0, tiled=True),
        lax.all_gather(b_down, ("ctx", "fsdp"), axis=0, tiled=True),
        lax.all_gather(ln2_gain, ("ctx", "fsdp"), axis=0, tiled=True),
        lax.all_gather(ln2_bias, ("ctx", "fsdp"), axis=0, tiled=True),
        lax.all_gather(w_proj, ("ctx", "fsdp"), axis=0, tiled=True),
    )
    upward = jnp.dot(hidden_low, up_full, preferred_element_type=jnp.float32) + up_bias.astype(
        jnp.float32
    )
    active_full, pull_gelu = jax.vjp(partial(jax.nn.gelu, approximate=False), upward)
    active = active_full.astype(jnp.bfloat16)
    downward = jnp.dot(active, down_full, preferred_element_type=jnp.float32) + down_bias.astype(
        jnp.float32
    )
    out_full_rows, pull_two = jax.vjp(
        layer_norm,
        hidden_one + downward,
        gain_two.astype(jnp.float32),
        shift_two.astype(jnp.float32),
    )
    out_low = out_full_rows.astype(jnp.bfloat16)
    projected = jnp.dot(out_low, proj_full, preferred_element_type=jnp.float32)
    back_qkv, back_qkv_bias, back_out, back_out_bias, back_gain_one, back_shift_one = (
        lax.all_gather(w_qkv, ("ctx", "fsdp"), axis=0, tiled=True),
        lax.all_gather(b_qkv, ("ctx", "fsdp"), axis=0, tiled=True),
        lax.all_gather(w_out, ("ctx", "fsdp"), axis=0, tiled=True),
        lax.all_gather(b_out, ("ctx", "fsdp"), axis=0, tiled=True),
        lax.all_gather(ln1_gain, ("ctx", "fsdp"), axis=0, tiled=True),
        lax.all_gather(ln1_bias, ("ctx", "fsdp"), axis=0, tiled=True),
    )
    back_up, back_up_bias, back_down, back_down_bias, back_gain_two, back_shift_two, back_proj = (
        lax.all_gather(w_up, ("ctx", "fsdp"), axis=0, tiled=True),
        lax.all_gather(b_up, ("ctx", "fsdp"), axis=0, tiled=True),
        lax.all_gather(w_down, ("ctx", "fsdp"), axis=0, tiled=True),
        lax.all_gather(b_down, ("ctx", "fsdp"), axis=0, tiled=True),
        lax.all_gather(ln2_gain, ("ctx", "fsdp"), axis=0, tiled=True),
        lax.all_gather(ln2_bias, ("ctx", "fsdp"), axis=0, tiled=True),
        lax.all_gather(w_proj, ("ctx", "fsdp"), axis=0, tiled=True),
    )
    grad_out = jnp.where(live_rows, cot_out.reshape(row_count, width).astype(jnp.float32), 0.0)
    grad_emb = jnp.where(live_rows, cot_emb.reshape(row_count, -1), 0)
    d_proj = jnp.einsum("rd,rp->dp", out_low, grad_emb, preferred_element_type=jnp.float32)
    grad_full = grad_out + jnp.einsum(
        "rp,dp->rd", grad_emb, back_proj, preferred_element_type=jnp.float32
    )
    grad_two, d_gain_two, d_shift_two = pull_two(grad_full)
    grad_down = grad_two.astype(jnp.bfloat16)
    d_down = jnp.einsum("rf,rd->fd", active, grad_down, preferred_element_type=jnp.float32)
    d_down_bias = jnp.sum(grad_down.astype(jnp.float32), axis=0)
    grad_act = jnp.einsum("rd,fd->rf", grad_down, back_down, preferred_element_type=jnp.float32)
    grad_up = pull_gelu(grad_act)[0].astype(jnp.bfloat16)
    d_up = jnp.einsum("rd,rf->df", hidden_low, grad_up, preferred_element_type=jnp.float32)
    d_up_bias = jnp.sum(grad_up.astype(jnp.float32), axis=0)
    grad_hidden = grad_two + jnp.einsum(
        "rf,df->rd", grad_up, back_up, preferred_element_type=jnp.float32
    )
    grad_one, d_gain_one, d_shift_one = pull_one(grad_hidden)
    grad_att = grad_one.astype(jnp.bfloat16)
    d_out = jnp.einsum("rd,re->de", merged, grad_att, preferred_element_type=jnp.float32)
    d_out_bias = jnp.sum(grad_att.astype(jnp.float32), axis=0)
    grad_merged = jnp.einsum(
        "re,de->rd", grad_att, back_out, preferred_element_type=jnp.float32
    ).astype(jnp.bfloat16)
    grad_heads = lax.all_to_all(
        grad_merged.reshape(groups, tok_slot, n_fsdp, lane_width),
        "fsdp",
        split_axis=2,
        concat_axis=1,
        tiled=True,
    ).reshape(groups, span_rows, lane_width)

    def attend_back(slot_item):
        slot_queries, slot_keys, slot_values, grad_mix, log_norm, length = slot_item
        query_split = slot_queries.reshape(query_blocks, query_rows, heads_here, HD)
        key_split = slot_keys.reshape(key_blocks, key_rows, heads_here, HD)
        value_split = slot_values.reshape(key_blocks, key_rows, heads_here, HD)
        grad_split = grad_mix.reshape(query_blocks, query_rows, heads_here, HD)

        def value_pass(value_total, query_item):
            query_block, grad_block, norm_block = query_item

            def value_per_key(row_dot, key_item):
                key_block, value_block, key_start = key_item
                scores = block_scores(query_block, key_block, key_start, length, scale)
                probability = jnp.exp(scores - norm_block[..., None])
                grad_probs = jnp.einsum(
                    "qhd,khd->hqk", grad_block, value_block, preferred_element_type=jnp.float32
                )
                value_part = jnp.einsum(
                    "hqk,qhd->khd",
                    probability.astype(jnp.bfloat16),
                    grad_block,
                    preferred_element_type=jnp.float32,
                )
                return (row_dot + jnp.sum(probability * grad_probs, axis=-1), value_part)

            row_dot, value_parts = lax.scan(
                value_per_key,
                jnp.zeros((heads_here, query_rows), jnp.float32),
                (key_split, value_split, key_starts),
            )
            return (value_total + value_parts.reshape(key_count, heads_here, HD), row_dot)

        value_grad, row_dots = lax.scan(
            value_pass,
            jnp.zeros((key_count, heads_here, HD), jnp.float32),
            (query_split, grad_split, log_norm),
        )

        def key_pass(key_total, query_item):
            query_block, grad_block, norm_block, dot_block = query_item

            def key_per_key(query_accum, key_item):
                key_block, value_block, key_start = key_item
                scores = block_scores(query_block, key_block, key_start, length, scale)
                probability = jnp.exp(scores - norm_block[..., None])
                grad_probs = jnp.einsum(
                    "qhd,khd->hqk", grad_block, value_block, preferred_element_type=jnp.float32
                )
                grad_scores = (probability * (grad_probs - dot_block[..., None])).astype(
                    jnp.bfloat16
                )
                query_accum = query_accum + jnp.einsum(
                    "hqk,khd->qhd", grad_scores, key_block, preferred_element_type=jnp.float32
                )
                key_part = jnp.einsum(
                    "hqk,qhd->khd", grad_scores, query_block, preferred_element_type=jnp.float32
                )
                return (query_accum, key_part)

            query_grad, key_parts = lax.scan(
                key_per_key,
                jnp.zeros((query_rows, heads_here, HD), jnp.float32),
                (key_split, value_split, key_starts),
            )
            return (key_total + key_parts.reshape(key_count, heads_here, HD), query_grad)

        key_grad, query_grads = lax.scan(
            key_pass,
            jnp.zeros((key_count, heads_here, HD), jnp.float32),
            (query_split, grad_split, log_norm, row_dots),
        )
        return (
            query_grads.reshape(span_rows, lane_width) * scale,
            key_grad.reshape(key_count, lane_width) * scale,
            value_grad.reshape(key_count, lane_width),
        )

    grad_queries, key_terms, value_terms = lax.map(
        attend_back, (queries, all_keys, all_values, grad_heads, log_norms, lengths)
    )
    grad_keys, grad_values = (
        lax.psum_scatter(
            key_terms.astype(jnp.bfloat16), "ctx", scatter_dimension=1, tiled=True
        ).astype(jnp.float32),
        lax.psum_scatter(
            value_terms.astype(jnp.bfloat16), "ctx", scatter_dimension=1, tiled=True
        ).astype(jnp.float32),
    )
    head_pos = (ctx_at * span_rows + jnp.arange(span_rows, dtype=jnp.int32)).astype(jnp.float32)
    head_cosine, head_sine = rope_tables(head_pos, HD)
    query_back = rotate(
        grad_queries.reshape(groups, span_rows, heads_here, HD), head_cosine, -head_sine
    )
    key_back = rotate(grad_keys.reshape(groups, span_rows, heads_here, HD), head_cosine, -head_sine)
    value_back = grad_values.reshape(groups, span_rows, heads_here, HD)
    grad_pack = (
        jnp.stack([query_back, key_back, value_back], axis=2)
        .astype(jnp.bfloat16)
        .reshape(groups, span_rows, 3, 1, lane_width)
    )
    grad_joined = lax.all_to_all(
        grad_pack, "fsdp", split_axis=1, concat_axis=3, tiled=True
    ).reshape(row_count, 3 * width)
    d_qkv = jnp.einsum("rd,re->de", flat_tokens, grad_joined, preferred_element_type=jnp.float32)
    d_qkv_bias = jnp.sum(grad_joined.astype(jnp.float32), axis=0)
    input_grad = (
        jnp.einsum("re,de->rd", grad_joined, back_qkv, preferred_element_type=jnp.float32)
        + grad_one
    ).astype(jnp.bfloat16)
    shards = (
        lax.psum_scatter(d_qkv, ("ctx", "fsdp"), scatter_dimension=0, tiled=True),
        lax.psum_scatter(d_qkv_bias, ("ctx", "fsdp"), scatter_dimension=0, tiled=True),
        lax.psum_scatter(d_out, ("ctx", "fsdp"), scatter_dimension=0, tiled=True),
        lax.psum_scatter(d_out_bias, ("ctx", "fsdp"), scatter_dimension=0, tiled=True),
        lax.psum_scatter(d_gain_one, ("ctx", "fsdp"), scatter_dimension=0, tiled=True),
        lax.psum_scatter(d_shift_one, ("ctx", "fsdp"), scatter_dimension=0, tiled=True),
        lax.psum_scatter(d_up, ("ctx", "fsdp"), scatter_dimension=0, tiled=True),
        lax.psum_scatter(d_up_bias, ("ctx", "fsdp"), scatter_dimension=0, tiled=True),
        lax.psum_scatter(d_down, ("ctx", "fsdp"), scatter_dimension=0, tiled=True),
        lax.psum_scatter(d_down_bias, ("ctx", "fsdp"), scatter_dimension=0, tiled=True),
        lax.psum_scatter(d_gain_two, ("ctx", "fsdp"), scatter_dimension=0, tiled=True),
        lax.psum_scatter(d_shift_two, ("ctx", "fsdp"), scatter_dimension=0, tiled=True),
        lax.psum_scatter(d_proj, ("ctx", "fsdp"), scatter_dimension=0, tiled=True),
    )
    totals = (
        lax.psum(shards[0].astype(jnp.bfloat16), "slot").astype(jnp.float32),
        lax.psum(shards[1].astype(jnp.bfloat16), "slot").astype(jnp.float32),
        lax.psum(shards[2].astype(jnp.bfloat16), "slot").astype(jnp.float32),
        lax.psum(shards[3].astype(jnp.bfloat16), "slot").astype(jnp.float32),
        lax.psum(shards[4].astype(jnp.bfloat16), "slot").astype(jnp.float32),
        lax.psum(shards[5].astype(jnp.bfloat16), "slot").astype(jnp.float32),
        lax.psum(shards[6].astype(jnp.bfloat16), "slot").astype(jnp.float32),
        lax.psum(shards[7].astype(jnp.bfloat16), "slot").astype(jnp.float32),
        lax.psum(shards[8].astype(jnp.bfloat16), "slot").astype(jnp.float32),
        lax.psum(shards[9].astype(jnp.bfloat16), "slot").astype(jnp.float32),
        lax.psum(shards[10].astype(jnp.bfloat16), "slot").astype(jnp.float32),
        lax.psum(shards[11].astype(jnp.bfloat16), "slot").astype(jnp.float32),
        lax.psum(shards[12].astype(jnp.bfloat16), "slot").astype(jnp.float32),
    )
    return (
        out_low.reshape(groups, tok_slot, width),
        projected.astype(jnp.bfloat16).reshape(groups, tok_slot, -1),
        input_grad.reshape(groups, tok_slot, width),
        totals[0],
        totals[1],
        totals[2],
        totals[3],
        totals[4],
        totals[5],
        totals[6],
        totals[7],
        totals[8],
        totals[9],
        totals[10],
        totals[11],
        totals[12],
    )


def solution(mesh):
    n_slot, n_ctx, n_fsdp = (mesh.shape[a] for a in ("slot", "ctx", "fsdp"))
    rows_axes = ("ctx", "fsdp")
    step = per_device
    if n_slot == 2 and n_fsdp % 2 == 0 and n_ctx * n_fsdp == H:
        mesh = Mesh(
            mesh.devices.reshape(n_slot, n_ctx, n_fsdp // 2, 2), ("slot", "ctx", "x", "core")
        )
        rows_axes = GROUP
        step = head_device
    in_specs = (
        P("slot", rows_axes, None),
        P("slot"),
        P(rows_axes, None),
        P(rows_axes),
        P(rows_axes, None),
        P(rows_axes),
        P(rows_axes),
        P(rows_axes),
        P(rows_axes, None),
        P(rows_axes),
        P(rows_axes, None),
        P(rows_axes),
        P(rows_axes),
        P(rows_axes),
        P(rows_axes, None),
        P("slot", rows_axes, None),
        P("slot", rows_axes, None),
    )
    out_specs = (
        P("slot", rows_axes, None),
        P("slot", rows_axes, None),
        P("slot", rows_axes, None),
        P(rows_axes, None),
        P(rows_axes),
        P(rows_axes, None),
        P(rows_axes),
        P(rows_axes),
        P(rows_axes),
        P(rows_axes, None),
        P(rows_axes),
        P(rows_axes, None),
        P(rows_axes),
        P(rows_axes),
        P(rows_axes),
        P(rows_axes, None),
    )
    return jax.shard_map(
        step, mesh=mesh, in_specs=in_specs, out_specs=out_specs, check_vma=False
    )
```

```python
from functools import partial

import jax
import jax.numpy as jnp
from jax import lax
from jax.experimental import pallas as pl
from jax.experimental.pallas import tpu as pltpu
from jax.sharding import Mesh
from jax.sharding import PartitionSpec as P

H = 16
HD = 64
LN_EPS = 1e-05
NEG_FILL = -1e30
F32 = jnp.float32
BF16 = jnp.bfloat16
GROUP = ("ctx", "x", "core")
LANE = ("ctx", "x")
SWAP = [(0, 1), (1, 0)]
VMEM_LIMIT = 60 * 1024 * 1024


def mm(left, right):
    return jnp.dot(left, right, preferred_element_type=F32)


def contract(left, right, left_dim, right_dim):
    return lax.dot_general(
        left, right, (((left_dim,), (right_dim,)), ((), ())), preferred_element_type=F32
    )


def swap_core(value):
    return lax.ppermute(value, "core", SWAP)


def swap_slot(value):
    return lax.ppermute(value, "slot", SWAP)


def pick(stacked, index, axis):
    return lax.dynamic_index_in_dim(stacked, index, axis, keepdims=False)


MESH = pl.DeviceIdType.MESH


def at_device(**where):
    names = ("slot", "ctx", "x", "core")
    return tuple(where[n] if n in where else lax.axis_index(n) for n in names)


def greet(peers):
    barrier = pltpu.get_barrier_semaphore()
    for peer in peers:
        pl.semaphore_signal(barrier, inc=1, device_id=peer, device_id_type=MESH)
    pl.semaphore_wait(barrier, len(peers))


def group_peers(n_ctx, n_x):
    ctx, x, core = (lax.axis_index(n) for n in GROUP)
    peers = []
    for dz in range(n_ctx):
        for dx in range(n_x):
            for dc in range(2):
                if dz or dx or dc:
                    where = (lax.rem(ctx + dz, n_ctx), lax.rem(x + dx, n_x), lax.rem(core + dc, 2))
                    peers.append(where)
    return peers


def start_kernel(
    tok_ref, head_ref, small_ref, all_ref, heads_ref, smalls_ref,
    far_send, block_send, local_sem, head_recv, small_recv, block_recv, *, n_ctx, n_x
):
    part = tok_ref.shape[1]
    ctx, x, core = (lax.axis_index(n) for n in GROUP)
    me = (ctx * n_x + x) * 2 + core
    peers = group_peers(n_ctx, n_x)
    greet([at_device(ctx=z, x=a, core=c) for z, a, c in peers])

    def block_at(b):
        return all_ref.at[:, pl.ds(pl.multiple_of(b * part, part), part), :]

    pushes = []
    for k, (z, a, c) in enumerate(peers):
        them = (z * n_x + a) * 2 + c
        target = at_device(ctx=z, x=a, core=c)
        pushes.append(pltpu.make_async_remote_copy(
            head_ref.at[them], heads_ref.at[me], far_send.at[2 * k], head_recv.at[me],
            device_id=target, device_id_type=MESH))
        pushes.append(pltpu.make_async_remote_copy(
            small_ref, smalls_ref.at[me], far_send.at[2 * k + 1], small_recv.at[me],
            device_id=target, device_id_type=MESH))
    locals_ = [
        pltpu.make_async_copy(tok_ref, block_at(me), local_sem.at[0]),
        pltpu.make_async_copy(head_ref.at[me], heads_ref.at[me], local_sem.at[1]),
        pltpu.make_async_copy(small_ref, smalls_ref.at[me], local_sem.at[2]),
    ]

    def send(b, source, lane, target):
        return pltpu.make_async_remote_copy(
            source, block_at(b), block_send.at[lane, b], block_recv.at[b],
            device_id=target, device_id_type=MESH)

    up = at_device(ctx=lax.rem(ctx + 1, n_ctx))
    down = at_device(ctx=lax.rem(ctx + n_ctx - 1, n_ctx))
    side = at_device(x=1 - x)
    twin = at_device(core=1 - core)

    def here(b):
        return send(b, block_at(b), 0, twin)

    @pl.when(ctx + 1 < n_ctx)
    def _():
        send(me, tok_ref, 0, up).start()

    @pl.when(ctx > 0)
    def _():
        send(me, tok_ref, 1, down).start()

    send(me, tok_ref, 2, side).start()
    for push in pushes:
        push.start()
    send(me, tok_ref, 3, twin).start()
    for copy in locals_:
        copy.start()

    for r in range(1, n_ctx):
        low = ctx - r
        high = ctx + r

        @pl.when(low >= 0)
        def _():
            b = (low * n_x + x) * 2 + core
            here(b).wait_recv()

            @pl.when(ctx + 1 < n_ctx)
            def _():
                send(b, block_at(b), 0, up).start()

            send(b, block_at(b), 2, side).start()
            send(b, block_at(b), 3, twin).start()

        @pl.when(high < n_ctx)
        def _():
            b = (high * n_x + x) * 2 + core
            here(b).wait_recv()

            @pl.when(ctx > 0)
            def _():
                send(b, block_at(b), 1, down).start()

            send(b, block_at(b), 2, side).start()
            send(b, block_at(b), 3, twin).start()

    def from_side(z):
        b = (z * n_x + (1 - x)) * 2 + core
        here(b).wait_recv()
        send(b, block_at(b), 3, twin).start()

    from_side(ctx)
    for r in range(1, n_ctx):
        @pl.when(ctx - r >= 0)
        def _():
            from_side(ctx - r)

        @pl.when(ctx + r < n_ctx)
        def _():
            from_side(ctx + r)

    for z in range(n_ctx):
        for a in range(n_x):
            here((z * n_x + a) * 2 + 1 - core).wait_recv()
    for k, (z, a, c) in enumerate(peers):
        them = (z * n_x + a) * 2 + c
        pltpu.make_async_remote_copy(
            head_ref.at[them], heads_ref.at[them], far_send.at[2 * k], head_recv.at[them],
            device_id=twin, device_id_type=MESH).wait_recv()
        pltpu.make_async_remote_copy(
            small_ref, smalls_ref.at[them], far_send.at[2 * k + 1], small_recv.at[them],
            device_id=twin, device_id_type=MESH).wait_recv()
    for push in pushes:
        push.wait_send()
    for copy in locals_:
        copy.wait()

    for z in range(n_ctx):
        b = (z * n_x + x) * 2 + core

        @pl.when((z <= ctx) & (ctx + 1 < n_ctx))
        def _():
            send(b, block_at(b), 0, up).wait_send()

        @pl.when((z >= ctx) & (ctx > 0))
        def _():
            send(b, block_at(b), 1, down).wait_send()

        send(b, block_at(b), 2, side).wait_send()
        send(b, block_at(b), 3, twin).wait_send()
        other = (z * n_x + (1 - x)) * 2 + core
        send(other, block_at(other), 3, twin).wait_send()


def gather_start(tokens, heads, small):
    n_ctx, n_x = lax.axis_size("ctx"), lax.axis_size("x")
    n = 2 * n_ctx * n_x
    slots, part, width = tokens.shape
    vmem = pl.BlockSpec(memory_space=pltpu.VMEM)
    anywhere = pl.BlockSpec(memory_space=pl.ANY)
    dma = pltpu.SemaphoreType.DMA
    return pl.pallas_call(
        partial(start_kernel, n_ctx=n_ctx, n_x=n_x),
        in_specs=[vmem, vmem, vmem],
        out_specs=[anywhere, vmem, vmem],
        out_shape=[
            jax.ShapeDtypeStruct((slots, n * part, width), tokens.dtype),
            jax.ShapeDtypeStruct(heads.shape, heads.dtype),
            jax.ShapeDtypeStruct((n,) + small.shape, small.dtype),
        ],
        scratch_shapes=[
            dma((2 * (n - 1),)), dma((4, n)), dma((3,)), dma((n,)), dma((n,)), dma((n,))
        ],
        compiler_params=pltpu.CompilerParams(
            collective_id=1, has_side_effects=True, vmem_limit_bytes=VMEM_LIMIT
        ),
        cost_estimate=pl.CostEstimate(
            flops=0, bytes_accessed=2 * n * tokens.size, transcendentals=0
        ),
        name="gather_start",
    )(tokens, heads, small)


def finish_kernel(
    up_ref, out_ref, small_ref, qkv_ref, red_ref, join_ref, weight_ref, one_ref,
    g_down, g_up, g_out, g_small, g_qkv, g_in,
    x_up, x_out, s_up, s_out, z_up, z_out, own_up, own_out,
    smalls, own_small, pair_small, qkvs, pair_qkv, pair_down, pair_out, last_up, low_up,
    joins, partial_in, pair_in,
    join_send, join_recv, in_send, in_recv,
    far_send, small_recv, qkv_recv, x_send, x_recv, z_send, z_recv, y_send, y_recv, *, n_ctx, n_x
):
    ctx, x, core = (lax.axis_index(n) for n in GROUP)
    slot = lax.axis_index("slot")
    me = (ctx * n_x + x) * 2 + core
    shard = g_up.shape[0]
    part = g_down.shape[0] // 2
    peers = group_peers(n_ctx, n_x)
    across = at_device(slot=1 - slot)
    corner = at_device(slot=1 - slot, core=1 - core)
    twin = at_device(core=1 - core)
    side = at_device(x=1 - x)
    greet([at_device(ctx=z, x=a, core=c) for z, a, c in peers] + [across, corner])

    def remote(source, target_ref, send_sem, recv_sem, target):
        return pltpu.make_async_remote_copy(
            source, target_ref, send_sem, recv_sem, device_id=target, device_id_type=MESH)

    started = []

    def launch(copy):
        copy.start()
        started.append(copy)
        return copy

    first_up, first_out, places = [], [], []
    for j in range(n_ctx):
        place = lax.rem(ctx + 1 + j, n_ctx)
        places.append(place)
        there = place * n_x + 1 - x
        first_up.append(launch(remote(
            up_ref.at[there], x_up.at[j], x_send.at[0, j], x_recv.at[0, j], side)))
        first_out.append(launch(remote(
            out_ref.at[there], x_out.at[j], x_send.at[1, j], x_recv.at[1, j], side)))
    chip = ctx * n_x + x
    lane_peers = [(z, a) for z, a, c in peers[1::2]]
    for k, (z, a) in enumerate(lane_peers):
        launch(remote(
            join_ref.at[z * n_x + a], joins.at[chip], join_send.at[k], join_recv.at[chip],
            at_device(ctx=z, x=a)))
    down_copy = launch(remote(red_ref, pair_down, y_send.at[0], y_recv.at[0], across))
    for k, (z, a, c) in enumerate(peers):
        them = (z * n_x + a) * 2 + c
        target = at_device(ctx=z, x=a, core=c)
        launch(remote(
            qkv_ref.at[them], qkvs.at[me], far_send.at[2 * k], qkv_recv.at[me], target))
        launch(remote(
            small_ref.at[them], smalls.at[me], far_send.at[2 * k + 1], small_recv.at[me], target))
    qkvs[me] = qkv_ref[me]
    smalls[me] = small_ref[me]

    second_up, second_out = [], []
    for j in range(n_ctx):
        mine = places[j] * n_x + x
        first_up[j].wait_recv()
        first_out[j].wait_recv()
        sum_up = up_ref[mine].astype(F32) + x_up[j].astype(F32)
        sum_out = out_ref[mine].astype(F32) + x_out[j].astype(F32)
        if j < n_ctx - 1:
            s_up[j] = sum_up.astype(BF16)
            s_out[j] = sum_out.astype(BF16)
            target = at_device(ctx=places[j])
            second_up.append(launch(remote(
                s_up.at[j], z_up.at[j], z_send.at[0, j], z_recv.at[0, j], target)))
            second_out.append(launch(remote(
                s_out.at[j], z_out.at[j], z_send.at[1, j], z_recv.at[1, j], target)))
        else:
            own_up[...] = sum_up
            own_out[...] = sum_out

    def add_head(source, rows_of, first):
        weight = jnp.concatenate(
            [weight_ref[b, source] for b in range(weight_ref.shape[0])], axis=0)
        for h in range(2):
            owner = core if h == 0 else 1 - core
            rows = rows_of(owner)
            rows = rows.reshape(rows.shape[0] * rows.shape[1], rows.shape[2])
            term = contract(rows, weight, 1, 1)
            partial_in[h] = term if first else partial_in[h] + term

    add_head(chip, lambda owner: join_ref[chip, owner], True)
    for k, (z, a) in enumerate(lane_peers):
        source = z * n_x + a
        remote(
            join_ref.at[source], joins.at[source], join_send.at[k], join_recv.at[source], twin
        ).wait_recv()
        add_head(source, lambda owner: joins[source, owner], False)
    in_copy = launch(remote(partial_in.at[1], pair_in, in_send, in_recv, twin))

    for z, a, c in peers:
        them = (z * n_x + a) * 2 + c
        remote(
            qkv_ref.at[them], qkvs.at[them], far_send.at[0], qkv_recv.at[them], twin
        ).wait_recv()
        remote(
            small_ref.at[them], smalls.at[them], far_send.at[1], small_recv.at[them], twin
        ).wait_recv()
    qkv_copy = launch(remote(qkvs, pair_qkv, y_send.at[1], y_recv.at[1], across))
    own_small[...] = jnp.sum(smalls[...].astype(F32), axis=0).astype(BF16)
    small_copy = launch(remote(own_small, pair_small, y_send.at[2], y_recv.at[2], across))

    for j in range(n_ctx - 1):
        second_out[j].wait_recv()
        own_out[...] += z_out[j].astype(F32)
    s_out[n_ctx - 1] = own_out[...].astype(BF16)
    out_copy = launch(remote(
        s_out.at[n_ctx - 1], pair_out, y_send.at[3], y_recv.at[3], across))
    for j in range(n_ctx - 1):
        second_up[j].wait_recv()
        own_up[...] += z_up[j].astype(F32)
    low_up[...] = own_up[...].astype(BF16).reshape(low_up.shape)
    quarter_copies = [
        launch(remote(low_up.at[1 - core], last_up.at[0], y_send.at[4], y_recv.at[4], twin)),
        launch(remote(low_up.at[core], last_up.at[1], y_send.at[5], y_recv.at[5], across)),
        launch(remote(low_up.at[1 - core], last_up.at[2], y_send.at[6], y_recv.at[6], corner)),
    ]

    in_copy.wait_recv()
    g_in[...] = (partial_in[0] + pair_in[...] + one_ref[...]).astype(BF16)
    half = pl.multiple_of(slot * part, part)
    other_half = pl.multiple_of((1 - slot) * part, part)
    g_down[pl.ds(half, part), :] = red_ref[...].astype(F32)
    down_copy.wait_recv()
    g_down[pl.ds(other_half, part), :] = pair_down[...].astype(F32)
    qkv_copy.wait_recv()
    g_qkv[...] = qkvs[...].astype(F32) + pair_qkv[...].astype(F32)
    small_copy.wait_recv()
    g_small[...] = own_small[...].astype(F32) + pair_small[...].astype(F32)
    out_copy.wait_recv()
    g_out[...] = s_out[n_ctx - 1].astype(F32) + pair_out[...].astype(F32)

    def place_quarter(rows, quarter_core, quarter_slot):
        for k in range(n_ctx * n_x):
            at = pl.multiple_of(((2 * k + quarter_core) * 2 + quarter_slot) * part, part)
            g_up[:, pl.ds(at, part)] = rows[:, k * part : (k + 1) * part].astype(F32)

    place_quarter(low_up[core], core, slot)
    quarter_copies[0].wait_recv()
    place_quarter(last_up[0], 1 - core, slot)
    quarter_copies[1].wait_recv()
    place_quarter(last_up[1], core, 1 - slot)
    quarter_copies[2].wait_recv()
    place_quarter(last_up[2], 1 - core, 1 - slot)
    for copy in started:
        copy.wait_send()


def finish_grads(up, out, small, qkv, red_down, joined, weight, grad_one):
    n_ctx, n_x = lax.axis_size("ctx"), lax.axis_size("x")
    n = 2 * n_ctx * n_x
    part, width = red_down.shape
    shard = out.shape[1]
    vmem = pl.BlockSpec(memory_space=pltpu.VMEM)
    dma = pltpu.SemaphoreType.DMA

    def low(*shape):
        return pltpu.VMEM(shape, BF16)

    def wide(*shape):
        return jax.ShapeDtypeStruct(shape, F32)

    return pl.pallas_call(
        partial(finish_kernel, n_ctx=n_ctx, n_x=n_x),
        in_specs=[vmem] * 8,
        out_specs=[vmem] * 6,
        out_shape=[
            wide(2 * part, width),
            wide(shard, 4 * up.shape[2]),
            wide(shard, width),
            wide(*small.shape[1:]),
            wide(*qkv.shape),
            jax.ShapeDtypeStruct(grad_one.shape, BF16),
        ],
        scratch_shapes=[
            low(n_ctx, *up.shape[1:]),
            low(n_ctx, *out.shape[1:]),
            low(n_ctx - 1, *up.shape[1:]),
            low(n_ctx, *out.shape[1:]),
            low(n_ctx - 1, *up.shape[1:]),
            low(n_ctx - 1, *out.shape[1:]),
            pltpu.VMEM(up.shape[1:], F32),
            pltpu.VMEM(out.shape[1:], F32),
            low(*small.shape),
            low(*small.shape[1:]),
            low(*small.shape[1:]),
            low(*qkv.shape),
            low(*qkv.shape),
            low(part, width),
            low(*out.shape[1:]),
            low(3, shard, up.shape[2]),
            low(2, shard, up.shape[2]),
            low(*joined.shape),
            pltpu.VMEM((2,) + grad_one.shape, F32),
            pltpu.VMEM(grad_one.shape, F32),
            dma((n_ctx * n_x - 1,)),
            dma((n_ctx * n_x,)),
            dma,
            dma,
            dma((2 * (n - 1),)),
            dma((n,)),
            dma((n,)),
            dma((2, n_ctx)),
            dma((2, n_ctx)),
            dma((2, n_ctx - 1)),
            dma((2, n_ctx - 1)),
            dma((7,)),
            dma((7,)),
        ],
        compiler_params=pltpu.CompilerParams(
            collective_id=2, has_side_effects=True, vmem_limit_bytes=VMEM_LIMIT
        ),
        cost_estimate=pl.CostEstimate(flops=0, bytes_accessed=16 * up.size, transcendentals=0),
        name="finish_grads",
    )(up, out, small, qkv, red_down, joined, weight, grad_one)


def project_kernel(tok_ref, w_ref, b_ref, cos_ref, sin_ref, q_ref, k_ref, v_ref):
    joined = mm(tok_ref[...], w_ref[...]) + b_ref[...]
    wide = 2 * HD
    turned = joined[:, :wide] * cos_ref[...] + joined[:, wide : 2 * wide] * sin_ref[...]
    q_ref[...] = (turned[:, :HD].astype(BF16) * HD ** (-0.5)).astype(BF16)
    k_ref[...] = turned[:, HD:].astype(BF16)
    v_ref[...] = joined[:, 2 * wide :].astype(BF16)


def project(tokens, weight, bias, cosine, sine):
    rows, width = tokens.shape
    seq = cosine.shape[0]
    block = min(512, seq)
    per_slot = seq // block
    cols = weight.shape[1]
    head_out = jax.ShapeDtypeStruct((rows, HD), BF16)
    head_spec = pl.BlockSpec((block, HD), lambda i: (i, 0))
    return pl.pallas_call(
        project_kernel,
        grid=(rows // block,),
        in_specs=[
            pl.BlockSpec((block, width), lambda i: (i, 0)),
            pl.BlockSpec((width, cols), lambda i: (0, 0)),
            pl.BlockSpec((1, cols), lambda i: (0, 0)),
            pl.BlockSpec((block, 2 * HD), lambda i: (i % per_slot, 0)),
            pl.BlockSpec((block, 2 * HD), lambda i: (i % per_slot, 0)),
        ],
        out_specs=[head_spec] * 3,
        out_shape=[head_out] * 3,
        compiler_params=pltpu.CompilerParams(vmem_limit_bytes=VMEM_LIMIT),
        cost_estimate=pl.CostEstimate(
            flops=2 * rows * width * cols, bytes_accessed=2 * rows * width, transcendentals=0
        ),
        name="project",
    )(tokens, weight, bias, cosine, sine)


QB = 512
KB = 512


def forward_kernel(
    len_ref, core_ref, q_ref, k_ref, v_ref, out_ref, send_ref, norm_ref, *, part
):
    length = len_ref[pl.program_id(0)]
    core = core_ref[0]
    queries = q_ref[0]
    rows = queries.shape[0]

    def step(j, state):
        highest, total, mix = state
        start = pl.multiple_of(j * KB, KB)
        scores = contract(queries, k_ref[0, pl.ds(start, KB), :], 1, 1)
        ids = start + lax.broadcasted_iota(jnp.int32, (1, KB), 1)
        scores = jnp.where(ids < length, scores, NEG_FILL)
        higher = jnp.maximum(highest, jnp.max(scores, axis=1, keepdims=True))
        fade = jnp.exp(highest - higher)
        weights = jnp.exp(scores - higher)
        total = total * fade + jnp.sum(weights, axis=1, keepdims=True)
        mix = mix * fade + mm(weights.astype(BF16), v_ref[0, pl.ds(start, KB), :])
        return higher, total, mix

    blocks = (length + KB - 1) // KB
    highest, total, mix = lax.fori_loop(
        0,
        blocks,
        step,
        (
            jnp.full((rows, 1), NEG_FILL, F32),
            jnp.zeros((rows, 1), F32),
            jnp.zeros((rows, HD), F32),
        ),
    )
    mix = mix / total
    out_ref[0] = mix
    log_norm = jnp.broadcast_to(highest + jnp.log(total), (rows, 128))
    norm_ref[0] = jnp.transpose(log_norm)[0:1, :]
    low = mix.astype(BF16)
    for chip in range(rows // (2 * part)):
        for half in range(2):
            at = (2 * chip + half) * part
            send_ref[chip, half ^ core, 0] = low[at : at + part]


def attend(lengths, core, queries, keys, values, part):
    slots, seq, _ = queries.shape
    chips = seq // (2 * part)
    spec_q = pl.BlockSpec((1, QB, HD), lambda s, i, *_: (s, i, 0))
    spec_k = pl.BlockSpec((1, seq, HD), lambda s, i, *_: (s, 0, 0))
    return pl.pallas_call(
        partial(forward_kernel, part=part),
        grid_spec=pltpu.PrefetchScalarGridSpec(
            num_scalar_prefetch=2,
            grid=(slots, seq // QB),
            in_specs=[spec_q, spec_k, spec_k],
            out_specs=[
                spec_q,
                pl.BlockSpec(
                    (QB // (2 * part), 2, 1, part, HD), lambda s, i, *_: (i, 0, s, 0, 0)
                ),
                pl.BlockSpec((1, 1, QB), lambda s, i, *_: (s, 0, i)),
            ],
        ),
        out_shape=[
            jax.ShapeDtypeStruct((slots, seq, HD), F32),
            jax.ShapeDtypeStruct((chips, 2, slots, part, HD), BF16),
            jax.ShapeDtypeStruct((slots, 1, seq), F32),
        ],
        compiler_params=pltpu.CompilerParams(vmem_limit_bytes=VMEM_LIMIT),
        cost_estimate=pl.CostEstimate(
            flops=16 * slots * seq * seq * HD,
            bytes_accessed=8 * slots * seq * HD,
            transcendentals=slots * seq * seq,
        ),
        name="attend",
    )(lengths, core, queries, keys, values)


def backward_kernel(
    len_ref, q_ref, k_ref, v_ref, g_ref, norm_ref, dot_ref, dq_ref, dk_ref, dv_ref, dqt
):
    length = len_ref[pl.program_id(0)]
    j = pl.program_id(1)
    start = j * KB
    key_block = k_ref[0]
    value_block = v_ref[0]

    @pl.when(j == 0)
    def _():
        dqt[...] = jnp.zeros_like(dqt)

    turned = jnp.transpose(key_block.astype(F32)).astype(BF16)
    ids = start + lax.broadcasted_iota(jnp.int32, (KB, 1), 0)
    shift = jnp.where(ids < length, 0.0, NEG_FILL)

    def step(i, state):
        key_grad, value_grad = state
        at = pl.multiple_of(i * QB, QB)
        queries = q_ref[0, pl.ds(at, QB), :]
        grads = g_ref[0, pl.ds(at, QB), :]
        scores = contract(key_block, queries, 1, 1) + shift
        probs = jnp.exp(scores - norm_ref[0, :, pl.ds(at, QB)])
        grad_probs = contract(value_block, grads, 1, 1)
        grad_scores = (probs * (grad_probs - dot_ref[0, :, pl.ds(at, QB)])).astype(BF16)
        value_grad = value_grad + mm(probs.astype(BF16), grads)
        key_grad = key_grad + mm(grad_scores, queries)
        dqt[:, pl.ds(at, QB)] += mm(turned, grad_scores)
        return key_grad, value_grad

    blocks = jnp.where(start < length, (length + QB - 1) // QB, 0)
    zero = jnp.zeros((KB, HD), F32)
    key_grad, value_grad = lax.fori_loop(0, blocks, step, (zero, zero))
    dk_ref[0] = key_grad
    dv_ref[0] = value_grad

    @pl.when(j == pl.num_programs(1) - 1)
    def _():
        dq_ref[0] = jnp.transpose(dqt[...])


def attend_back(lengths, queries, keys, values, grads, norms, dots):
    slots, seq, _ = queries.shape
    whole = pl.BlockSpec((1, seq, HD), lambda s, j, *_: (s, 0, 0))
    block = pl.BlockSpec((1, KB, HD), lambda s, j, *_: (s, j, 0))
    row = pl.BlockSpec((1, 1, seq), lambda s, j, *_: (s, 0, 0))
    out = jax.ShapeDtypeStruct((slots, seq, HD), F32)
    return pl.pallas_call(
        backward_kernel,
        grid_spec=pltpu.PrefetchScalarGridSpec(
            num_scalar_prefetch=1,
            grid=(slots, seq // KB),
            in_specs=[whole, block, block, whole, row, row],
            out_specs=[whole, block, block],
            scratch_shapes=[pltpu.VMEM((HD, seq), F32)],
        ),
        out_shape=[out] * 3,
        compiler_params=pltpu.CompilerParams(vmem_limit_bytes=VMEM_LIMIT),
        cost_estimate=pl.CostEstimate(
            flops=40 * slots * seq * seq * HD,
            bytes_accessed=20 * slots * seq * HD,
            transcendentals=slots * seq * seq,
        ),
        name="attend_back",
    )(lengths, queries, keys, values, grads, norms, dots)


def join_kernel(
    q_ref, k_ref, v_ref, tok_ref, cos_ref, sin_ref, join_ref, grad_ref, total, bias, *, part
):
    i = pl.program_id(0)

    @pl.when(i == 0)
    def _():
        total[...] = jnp.zeros_like(total)
        bias[...] = jnp.zeros_like(bias)

    pair = jnp.concatenate([q_ref[...] * HD ** (-0.5), k_ref[...]], axis=1)
    half = HD // 2
    lanes = lax.broadcasted_iota(jnp.int32, (1, 2 * HD), 1)
    low = lax.rem(lanes, HD) < half
    swapped = jnp.where(low, pltpu.roll(pair, 2 * HD - half, 1), pltpu.roll(pair, half, 1))
    sine = jnp.where(low, sin_ref[...], -sin_ref[...])
    turned = pair * cos_ref[...] + swapped * sine
    joined = jnp.concatenate([turned, v_ref[...]], axis=1).astype(BF16)
    for chip in range(joined.shape[0] // (2 * part)):
        for core in range(2):
            at = (2 * chip + core) * part
            join_ref[chip, core, 0] = joined[at : at + part]
    total[...] += contract(joined, tok_ref[...], 0, 0)
    bias[...] += jnp.sum(joined.astype(F32), axis=0, keepdims=True)

    @pl.when(i == pl.num_programs(0) - 1)
    def _():
        turned_total = jnp.transpose(total[...])
        shard = turned_total.shape[0] // grad_ref.shape[0]
        extra = jnp.broadcast_to(bias[...], (grad_ref.shape[1] - shard, bias.shape[1]))
        for d in range(grad_ref.shape[0]):
            grad_ref[d, :shard] = turned_total[d * shard : (d + 1) * shard].astype(BF16)
            grad_ref[d, shard:] = extra.astype(BF16)


def join_grads(grad_q, grad_k, grad_v, tokens, cosine, sine, part, n_group):
    slots, seq, _ = grad_q.shape
    rows, width = tokens.shape
    block = min(512, seq)
    per_slot = seq // block
    cols = 3 * HD
    head = pl.BlockSpec((block, HD), lambda i: (i, 0))
    table = pl.BlockSpec((block, 2 * HD), lambda i: (i % per_slot, 0))
    chips = block // (2 * part)
    shard = width // n_group
    flat = [t.reshape(rows, HD) for t in (grad_q, grad_k, grad_v)]
    return pl.pallas_call(
        partial(join_kernel, part=part),
        grid=(rows // block,),
        in_specs=[
            head, head, head, pl.BlockSpec((block, width), lambda i: (i, 0)), table, table,
        ],
        out_specs=[
            pl.BlockSpec(
                (chips, 2, 1, part, cols), lambda i: (i % per_slot, 0, i // per_slot, 0, 0)
            ),
            pl.BlockSpec((n_group, shard + 16, cols), lambda i: (0, 0, 0)),
        ],
        out_shape=[
            jax.ShapeDtypeStruct((seq // (2 * part), 2, slots, part, cols), BF16),
            jax.ShapeDtypeStruct((n_group, shard + 16, cols), BF16),
        ],
        scratch_shapes=[pltpu.VMEM((cols, width), F32), pltpu.VMEM((1, cols), F32)],
        compiler_params=pltpu.CompilerParams(vmem_limit_bytes=VMEM_LIMIT),
        cost_estimate=pl.CostEstimate(
            flops=2 * rows * width * cols, bytes_accessed=2 * rows * width, transcendentals=0
        ),
        name="join_grads",
    )(*flat, tokens, cosine, sine)


def norm_forward(values, gain, shift):
    center = values - jnp.mean(values, axis=-1, keepdims=True)
    spread = jnp.mean(center * center, axis=-1, keepdims=True)
    root = lax.rsqrt(spread + LN_EPS)
    unit = center * root
    return unit * gain + shift, unit, root


def norm_backward(grad, unit, root, gain):
    scaled = grad * gain
    inner = scaled - jnp.mean(scaled, axis=-1, keepdims=True)
    inner = inner - unit * jnp.mean(scaled * unit, axis=-1, keepdims=True)
    return root * inner, jnp.sum(grad * unit, axis=0), jnp.sum(grad, axis=0)


def gelu_pair(values):
    half = 0.5 + 0.5 * lax.erf(values * 0.7071067811865476)
    bell = jnp.exp(-0.5 * values * values) * 0.3989422804014327
    return values * half, half + values * bell


def rope_rows(positions):
    halfway = HD // 2
    ladder = jnp.arange(halfway, dtype=F32) * (2.0 / HD)
    frequency = jnp.power(jnp.float32(10000.0), -ladder)
    angles = positions[:, None] * frequency[None, :]
    return jnp.cos(angles), jnp.sin(angles)


def head_device(
    tokens,
    lengths,
    w_qkv,
    b_qkv,
    w_out,
    b_out,
    ln1_gain,
    ln1_bias,
    w_up,
    b_up,
    w_down,
    b_down,
    ln2_gain,
    ln2_bias,
    w_proj,
    cot_out,
    cot_emb,
):
    n_lane = lax.axis_size("ctx") * lax.axis_size("x")
    n_group = 2 * n_lane
    core = lax.axis_index("core")
    slot = lax.axis_index("slot")
    chip = lax.axis_index("ctx") * lax.axis_size("x") + lax.axis_index("x")
    me = 2 * chip + core
    slots, part, width = tokens.shape
    seq = part * n_group
    rows = slots * part
    shard = width // n_group
    ff_shard = w_down.shape[0]
    ff_half = ff_shard // 2
    proj = w_proj.shape[1]
    head_cols = 3 * HD

    small = jnp.concatenate(
        [b_qkv, b_out, ln1_gain, ln1_bias, b_up, b_down, ln2_gain, ln2_bias]
    )
    small_at = [0]
    for piece in (b_qkv, b_out, ln1_gain, ln1_bias, b_up, b_down, ln2_gain, ln2_bias):
        small_at.append(small_at[-1] + piece.shape[0])
    small_rows = -(-small.shape[0] // proj)
    small_rows = -(-small_rows // 16) * 16
    small = jnp.pad(small, (0, small_rows * proj - small.shape[0])).reshape(small_rows, proj)
    by_head = w_qkv.reshape(shard, 3, n_group, HD).transpose(2, 0, 1, 3)
    all_tokens, my_head, packed = gather_start(
        tokens,
        by_head.reshape(n_group, shard, head_cols),
        jnp.concatenate([w_proj, small], axis=0),
    )
    proj_full = packed[:, :shard].reshape(width, proj)
    smalls = packed[:, shard:].reshape(n_group, small_rows * proj).astype(F32)
    qkv_bias, out_bias, gain_one, shift_one, up_bias, down_bias, gain_two, shift_two = (
        smalls[:, a:b].reshape(-1) for a, b in zip(small_at[:-1], small_at[1:])
    )

    my_head = my_head.reshape(width, 3, HD)
    all_tokens = all_tokens.reshape(slots * seq, width)

    def with_swapped(joined):
        first = joined[:, 0:2]
        halves = first.reshape(-1, 2, 2, HD // 2)
        swapped = jnp.stack([-halves[:, :, 1], halves[:, :, 0]], axis=2)
        return jnp.concatenate(
            [
                first.reshape(-1, 2 * HD),
                swapped.reshape(-1, 2 * HD),
                joined[:, 2],
            ],
            axis=1,
        )

    head_weight = with_swapped(my_head)
    head_bias = with_swapped(pick(qkv_bias.reshape(1, 3, n_group, HD), me, 2))
    cosine, sine = rope_rows(jnp.arange(seq, dtype=jnp.int32).astype(F32))
    cos_wide = jnp.tile(cosine, (1, 4))
    sin_wide = jnp.tile(sine, (1, 4))
    queries, keys, values = project(all_tokens, head_weight, head_bias, cos_wide, sin_wide)
    queries, keys, values = (t.reshape(slots, seq, HD) for t in (queries, keys, values))

    def two_lanes(mine, theirs):
        low_first = jnp.stack([mine, theirs], axis=0)
        high_first = jnp.stack([theirs, mine], axis=0)
        return jnp.where(core == 0, low_first, high_first)

    up_split = w_up.reshape(shard, n_lane, 2, 2, ff_half)
    up_mine = pick(up_split, core, 2)
    up_theirs = swap_core(pick(up_split, 1 - core, 2))
    up_chip = two_lanes(up_mine, up_theirs).reshape(2 * shard, n_lane, 2, ff_half)
    down_split = w_down.reshape(2, ff_half, width)
    up_part = pick(up_chip, slot, 2).reshape(2 * shard, n_lane * ff_half)
    out_up = jnp.concatenate([w_out, up_part], axis=0)
    out_up, down_part, packed = lax.optimization_barrier(
        (out_up, pick(down_split, slot, 0), packed)
    )
    gathered = lax.all_gather(out_up, LANE, axis=0, tiled=False)
    out_lane = gathered[:, :shard].reshape(n_lane * shard, width)
    up = gathered[:, shard:].reshape(width, n_lane * ff_half)
    down = lax.all_gather(down_part, LANE, axis=0, tiled=True)
    bias_lane = pick(up_bias.reshape(n_lane, 2, 2, ff_half), core, 1)
    up_bias_own = pick(bias_lane, slot, 1).reshape(-1)

    qkv_split = w_qkv.reshape(shard, 3, n_lane, 2, HD)
    qkv_mine = pick(qkv_split, core, 3)
    qkv_theirs = swap_core(pick(qkv_split, 1 - core, 3))
    qkv_chip = two_lanes(qkv_mine, qkv_theirs).transpose(3, 0, 1, 2, 4)
    qkv_chip = qkv_chip.reshape(n_lane, 2 * shard, head_cols)

    mixture, send, norms = attend(
        lengths, core.reshape(1).astype(jnp.int32), queries, keys, values, part
    )
    merged = lax.all_to_all(send, LANE, 0, 0, tiled=True)
    merged = merged.transpose(1, 2, 3, 0, 4).reshape(2 * rows, n_lane * HD)

    def own_sum(partial_rows):
        return partial_rows[:rows] + swap_core(partial_rows[rows:])

    def both(value):
        return jnp.concatenate([value, swap_core(value)], axis=0)

    def quad(value):
        pair = jnp.concatenate([value, swap_slot(value)], axis=0)
        return jnp.concatenate([pair, swap_core(pair)], axis=0)

    def quad_sum(partial_rows):
        pair = partial_rows[: 2 * rows] + swap_core(partial_rows[2 * rows :])
        return pair[:rows] + swap_slot(pair[rows:].astype(BF16)).astype(F32)

    flat_tokens = tokens.reshape(rows, width).astype(F32)
    attended = own_sum(mm(merged, out_lane)) + out_bias
    hidden_one, unit_one, root_one = norm_forward(flat_tokens + attended, gain_one, shift_one)
    hidden_low, qkv_chip = lax.optimization_barrier((hidden_one.astype(BF16), qkv_chip))
    qkv_lane = lax.all_gather(qkv_chip, LANE, axis=0, tiled=True)
    hidden_low = quad(hidden_low)

    active, slope = gelu_pair(mm(hidden_low, up) + up_bias_own)
    active = active.astype(BF16)
    downward = quad_sum(mm(active, down)) + down_bias
    out_rows, unit_two, root_two = norm_forward(hidden_one + downward, gain_two, shift_two)
    out_low = out_rows.astype(BF16)
    embeds = mm(out_low, proj_full).astype(BF16)

    place = me * part + jnp.arange(part, dtype=jnp.int32)
    live = (place[None, :] < lengths[:, None]).reshape(rows, 1)
    grad_out = jnp.where(live, cot_out.reshape(rows, width).astype(F32), 0.0)
    grad_emb = jnp.where(live, cot_emb.reshape(rows, proj), 0)
    d_proj = contract(out_low, grad_emb, 0, 0)
    grad_full = grad_out + contract(grad_emb, proj_full, 1, 1)
    grad_two, d_gain_two, d_shift_two = norm_backward(grad_full, unit_two, root_two, gain_two)
    grad_down_own = grad_two.astype(BF16)
    d_down_bias = jnp.sum(grad_down_own.astype(F32), axis=0)
    grad_down = quad(grad_down_own)
    grad_up = (contract(grad_down, down, 1, 1) * slope).astype(BF16)
    d_down = contract(active, grad_down, 0, 0).astype(BF16)
    d_up = contract(hidden_low, grad_up, 0, 0).astype(BF16)
    up_bias_own_grad = jnp.sum(grad_up.astype(F32), axis=0)
    grad_hidden = grad_two + quad_sum(contract(grad_up, up, 1, 1))
    grad_one, d_gain_one, d_shift_one = norm_backward(grad_hidden, unit_one, root_one, gain_one)
    grad_att_own = grad_one.astype(BF16)
    d_out_bias = jnp.sum(grad_att_own.astype(F32), axis=0)
    grad_att_own, qkv_lane = lax.optimization_barrier((grad_att_own, qkv_lane))
    grad_att = both(grad_att_own)
    grad_merged = contract(grad_att, out_lane, 1, 1).astype(BF16)
    grad_merged = grad_merged.reshape(2, slots, part, n_lane, HD).transpose(3, 0, 1, 2, 4)
    grad_heads = lax.all_to_all(grad_merged, LANE, 0, 0, tiled=True)

    def core_order(value):
        return jnp.where(core == 0, value, jnp.flip(value, axis=1))

    grad_heads = core_order(grad_heads).transpose(2, 0, 1, 3, 4).reshape(slots, seq, HD)

    d_out = contract(merged, grad_att, 0, 0).astype(BF16)

    red_down = lax.psum_scatter(d_down, LANE, scatter_dimension=0, tiled=True)

    spread = (
        (jnp.arange(2) == core)[:, None, None] & (jnp.arange(2) == slot)[None, :, None]
    ).astype(F32)
    up_bias_grad = up_bias_own_grad.reshape(n_lane, 1, 1, ff_half) * spread[None]
    vectors = (
        d_out_bias,
        d_gain_one,
        d_shift_one,
        up_bias_grad.reshape(-1),
        d_down_bias,
        d_gain_two,
        d_shift_two,
    )
    small_grad = jnp.concatenate([v.reshape(n_group, -1) for v in vectors], axis=1)
    small_cols = small_grad.shape[1]
    vec_rows = -(-small_cols // proj)
    vec_rows = -(-(shard + vec_rows) // 16) * 16 - shard
    small_grad = jnp.pad(small_grad, ((0, 0), (0, vec_rows * proj - small_cols)))
    small_grad = jnp.concatenate(
        [d_proj.reshape(n_group, shard, proj), small_grad.reshape(n_group, vec_rows, proj)], axis=1
    )
    row_dots = jnp.sum(grad_heads.astype(F32) * mixture, axis=-1).reshape(slots, 1, seq)
    grad_q, grad_k, grad_v = attend_back(
        lengths, queries, keys, values, grad_heads, norms, row_dots
    )

    joined, d_qkv = join_grads(
        grad_q, grad_k, grad_v, all_tokens, cos_wide, sin_wide, part, n_group
    )
    grad_w_down, grad_w_up, grad_w_out, small_sum, d_qkv, input_grad = finish_grads(
        d_up.reshape(n_lane, 2 * shard, width),
        d_out.reshape(n_lane, shard, width),
        small_grad.astype(BF16),
        d_qkv,
        red_down,
        joined,
        qkv_lane.reshape(n_lane, n_lane, 2 * shard, head_cols),
        grad_one,
    )
    grad_w_proj = small_sum[:shard]
    vec_sum = small_sum[shard:].reshape(-1)
    vec_outs = []
    at = 0
    for v in vectors:
        size = v.size // n_group
        vec_outs.append(vec_sum[at : at + size])
        at += size
    (
        grad_b_out,
        grad_gain_one,
        grad_shift_one,
        grad_b_up,
        grad_b_down,
        grad_gain_two,
        grad_shift_two,
    ) = vec_outs

    grad_w_qkv = (
        d_qkv[:, :shard].reshape(n_group, shard, 3, HD).transpose(1, 2, 0, 3).reshape(shard, 3 * width)
    )
    qkv_bias_grad = d_qkv[:, shard].reshape(n_group, 3, HD).transpose(1, 0, 2).reshape(-1)
    grad_b_qkv = lax.dynamic_slice(qkv_bias_grad, (me * b_qkv.shape[0],), (b_qkv.shape[0],))

    return (
        out_low.reshape(slots, part, width),
        embeds.reshape(slots, part, proj),
        input_grad.reshape(slots, part, width),
        grad_w_qkv,
        grad_b_qkv,
        grad_w_out,
        grad_b_out,
        grad_gain_one,
        grad_shift_one,
        grad_w_up,
        grad_b_up,
        grad_w_down,
        grad_b_down,
        grad_gain_two,
        grad_shift_two,
        grad_w_proj,
    )


def layer_norm(hidden, gain, shift):
    center = hidden - jnp.mean(hidden, axis=-1, keepdims=True)
    spread = jnp.mean(center * center, axis=-1, keepdims=True)
    return center * lax.rsqrt(spread + LN_EPS) * gain + shift


def rope_tables(positions, head_width):
    halfway = head_width // 2
    ladder = jnp.arange(halfway, dtype=jnp.float32) * (2.0 / head_width)
    frequency = jnp.power(jnp.float32(10000.0), -ladder)
    angles = positions[:, None] * frequency[None, :]
    return (jnp.cos(angles)[:, None, :], jnp.sin(angles)[:, None, :])


def rotate(values, cosine, sine_part):
    halfway = values.shape[-1] // 2
    first_half = values[..., :halfway]
    second_half = values[..., halfway:]
    return jnp.concatenate(
        [
            first_half * cosine - second_half * sine_part,
            second_half * cosine + first_half * sine_part,
        ],
        axis=-1,
    )


def block_scores(query_block, key_block, key_start, length, scale):
    scores = (
        jnp.einsum("qhd,khd->hqk", query_block, key_block, preferred_element_type=jnp.float32)
        * scale
    )
    key_ids = key_start + jnp.arange(key_block.shape[0], dtype=jnp.int32)
    return jnp.where((key_ids < length)[None, None, :], scores, NEG_FILL)


def per_device(
    tokens,
    lengths,
    w_qkv,
    b_qkv,
    w_out,
    b_out,
    ln1_gain,
    ln1_bias,
    w_up,
    b_up,
    w_down,
    b_down,
    ln2_gain,
    ln2_bias,
    w_proj,
    cot_out,
    cot_emb,
):
    n_fsdp = lax.axis_size("fsdp")
    n_ctx = lax.axis_size("ctx")
    ctx_at = lax.axis_index("ctx")
    fsdp_at = lax.axis_index("fsdp")
    groups, tok_slot, width = tokens.shape
    heads_here = H // n_fsdp
    lane_width = heads_here * HD
    span_rows = tok_slot * n_fsdp
    key_count = span_rows * n_ctx
    row_count = groups * tok_slot
    scale = HD ** (-0.5)
    query_rows = min(512, span_rows)
    key_rows = min(2048, key_count // 4)
    query_blocks = span_rows // query_rows
    key_blocks = key_count // key_rows
    key_starts = jnp.arange(key_blocks, dtype=jnp.int32) * key_rows
    qkv_full, qkv_bias, out_full, out_bias, gain_one, shift_one = (
        lax.all_gather(w_qkv, ("ctx", "fsdp"), axis=0, tiled=True),
        lax.all_gather(b_qkv, ("ctx", "fsdp"), axis=0, tiled=True),
        lax.all_gather(w_out, ("ctx", "fsdp"), axis=0, tiled=True),
        lax.all_gather(b_out, ("ctx", "fsdp"), axis=0, tiled=True),
        lax.all_gather(ln1_gain, ("ctx", "fsdp"), axis=0, tiled=True),
        lax.all_gather(ln1_bias, ("ctx", "fsdp"), axis=0, tiled=True),
    )
    token_pos = (ctx_at * n_fsdp + fsdp_at) * tok_slot + jnp.arange(tok_slot, dtype=jnp.int32)
    live_rows = (token_pos[None, :] < lengths[:, None]).reshape(row_count, 1)
    flat_tokens = tokens.reshape(row_count, width)
    joined = jnp.dot(flat_tokens, qkv_full, preferred_element_type=jnp.float32) + qkv_bias.astype(
        jnp.float32
    )
    cosine, sine_part = rope_tables(token_pos.astype(jnp.float32), HD)
    split_heads = joined.reshape(groups, tok_slot, 3, H, HD)
    rotated_query = rotate(split_heads[:, :, 0], cosine, sine_part)
    rotated_key = rotate(split_heads[:, :, 1], cosine, sine_part)
    packed = (
        jnp.stack([rotated_query, rotated_key, split_heads[:, :, 2]], axis=2)
        .astype(jnp.bfloat16)
        .reshape(groups, tok_slot, 3, n_fsdp, lane_width)
    )
    by_heads = lax.all_to_all(packed, "fsdp", split_axis=3, concat_axis=1, tiled=True)
    queries = by_heads[:, :, 0, 0]
    local_keys = by_heads[:, :, 1, 0]
    local_values = by_heads[:, :, 2, 0]
    all_keys, all_values = (
        lax.all_gather(local_keys, "ctx", axis=1, tiled=True),
        lax.all_gather(local_values, "ctx", axis=1, tiled=True),
    )

    def attend_slot(slot_item):
        slot_queries, slot_keys, slot_values, length = slot_item
        query_split = slot_queries.reshape(query_blocks, query_rows, heads_here, HD)
        key_split = slot_keys.reshape(key_blocks, key_rows, heads_here, HD)
        value_split = slot_values.reshape(key_blocks, key_rows, heads_here, HD)

        def per_query(query_block):

            def row_stats(state_pair, key_item):
                highest, running_sum = state_pair
                scores = block_scores(query_block, key_item[0], key_item[1], length, scale)
                new_high = jnp.maximum(highest, jnp.max(scores, axis=-1))
                running_sum = running_sum * jnp.exp(highest - new_high) + jnp.sum(
                    jnp.exp(scores - new_high[..., None]), axis=-1
                )
                return ((new_high, running_sum), None)

            start_state = (
                jnp.full((heads_here, query_rows), NEG_FILL, jnp.float32),
                jnp.zeros((heads_here, query_rows), jnp.float32),
            )
            highest, running_sum = lax.scan(row_stats, start_state, (key_split, key_starts))[0]
            log_norm = highest + jnp.log(running_sum)

            def weigh_values(accumulated, key_item):
                scores = block_scores(query_block, key_item[0], key_item[2], length, scale)
                weights = jnp.exp(scores - log_norm[..., None]).astype(jnp.bfloat16)
                return (
                    accumulated
                    + jnp.einsum(
                        "hqk,khd->qhd", weights, key_item[1], preferred_element_type=jnp.float32
                    ),
                    None,
                )

            mixture = lax.scan(
                weigh_values,
                jnp.zeros((query_rows, heads_here, HD), jnp.float32),
                (key_split, value_split, key_starts),
            )[0]
            return (mixture, log_norm)

        mixture, log_norm = lax.map(per_query, query_split)
        return (mixture.reshape(span_rows, lane_width), log_norm)

    mixture, log_norms = lax.map(attend_slot, (queries, all_keys, all_values, lengths))
    merged = lax.all_to_all(
        mixture.astype(jnp.bfloat16).reshape(groups, span_rows, 1, lane_width),
        "fsdp",
        split_axis=1,
        concat_axis=2,
        tiled=True,
    ).reshape(row_count, width)
    attended = jnp.dot(merged, out_full, preferred_element_type=jnp.float32) + out_bias.astype(
        jnp.float32
    )
    hidden_one, pull_one = jax.vjp(
        layer_norm,
        flat_tokens.astype(jnp.float32) + attended,
        gain_one.astype(jnp.float32),
        shift_one.astype(jnp.float32),
    )
    hidden_low = hidden_one.astype(jnp.bfloat16)
    up_full, up_bias, down_full, down_bias, gain_two, shift_two, proj_full = (
        lax.all_gather(w_up, ("ctx", "fsdp"), axis=0, tiled=True),
        lax.all_gather(b_up, ("ctx", "fsdp"), axis=0, tiled=True),
        lax.all_gather(w_down, ("ctx", "fsdp"), axis=0, tiled=True),
        lax.all_gather(b_down, ("ctx", "fsdp"), axis=0, tiled=True),
        lax.all_gather(ln2_gain, ("ctx", "fsdp"), axis=0, tiled=True),
        lax.all_gather(ln2_bias, ("ctx", "fsdp"), axis=0, tiled=True),
        lax.all_gather(w_proj, ("ctx", "fsdp"), axis=0, tiled=True),
    )
    upward = jnp.dot(hidden_low, up_full, preferred_element_type=jnp.float32) + up_bias.astype(
        jnp.float32
    )
    active_full, pull_gelu = jax.vjp(partial(jax.nn.gelu, approximate=False), upward)
    active = active_full.astype(jnp.bfloat16)
    downward = jnp.dot(active, down_full, preferred_element_type=jnp.float32) + down_bias.astype(
        jnp.float32
    )
    out_full_rows, pull_two = jax.vjp(
        layer_norm,
        hidden_one + downward,
        gain_two.astype(jnp.float32),
        shift_two.astype(jnp.float32),
    )
    out_low = out_full_rows.astype(jnp.bfloat16)
    projected = jnp.dot(out_low, proj_full, preferred_element_type=jnp.float32)
    back_qkv, back_qkv_bias, back_out, back_out_bias, back_gain_one, back_shift_one = (
        lax.all_gather(w_qkv, ("ctx", "fsdp"), axis=0, tiled=True),
        lax.all_gather(b_qkv, ("ctx", "fsdp"), axis=0, tiled=True),
        lax.all_gather(w_out, ("ctx", "fsdp"), axis=0, tiled=True),
        lax.all_gather(b_out, ("ctx", "fsdp"), axis=0, tiled=True),
        lax.all_gather(ln1_gain, ("ctx", "fsdp"), axis=0, tiled=True),
        lax.all_gather(ln1_bias, ("ctx", "fsdp"), axis=0, tiled=True),
    )
    back_up, back_up_bias, back_down, back_down_bias, back_gain_two, back_shift_two, back_proj = (
        lax.all_gather(w_up, ("ctx", "fsdp"), axis=0, tiled=True),
        lax.all_gather(b_up, ("ctx", "fsdp"), axis=0, tiled=True),
        lax.all_gather(w_down, ("ctx", "fsdp"), axis=0, tiled=True),
        lax.all_gather(b_down, ("ctx", "fsdp"), axis=0, tiled=True),
        lax.all_gather(ln2_gain, ("ctx", "fsdp"), axis=0, tiled=True),
        lax.all_gather(ln2_bias, ("ctx", "fsdp"), axis=0, tiled=True),
        lax.all_gather(w_proj, ("ctx", "fsdp"), axis=0, tiled=True),
    )
    grad_out = jnp.where(live_rows, cot_out.reshape(row_count, width).astype(jnp.float32), 0.0)
    grad_emb = jnp.where(live_rows, cot_emb.reshape(row_count, -1), 0)
    d_proj = jnp.einsum("rd,rp->dp", out_low, grad_emb, preferred_element_type=jnp.float32)
    grad_full = grad_out + jnp.einsum(
        "rp,dp->rd", grad_emb, back_proj, preferred_element_type=jnp.float32
    )
    grad_two, d_gain_two, d_shift_two = pull_two(grad_full)
    grad_down = grad_two.astype(jnp.bfloat16)
    d_down = jnp.einsum("rf,rd->fd", active, grad_down, preferred_element_type=jnp.float32)
    d_down_bias = jnp.sum(grad_down.astype(jnp.float32), axis=0)
    grad_act = jnp.einsum("rd,fd->rf", grad_down, back_down, preferred_element_type=jnp.float32)
    grad_up = pull_gelu(grad_act)[0].astype(jnp.bfloat16)
    d_up = jnp.einsum("rd,rf->df", hidden_low, grad_up, preferred_element_type=jnp.float32)
    d_up_bias = jnp.sum(grad_up.astype(jnp.float32), axis=0)
    grad_hidden = grad_two + jnp.einsum(
        "rf,df->rd", grad_up, back_up, preferred_element_type=jnp.float32
    )
    grad_one, d_gain_one, d_shift_one = pull_one(grad_hidden)
    grad_att = grad_one.astype(jnp.bfloat16)
    d_out = jnp.einsum("rd,re->de", merged, grad_att, preferred_element_type=jnp.float32)
    d_out_bias = jnp.sum(grad_att.astype(jnp.float32), axis=0)
    grad_merged = jnp.einsum(
        "re,de->rd", grad_att, back_out, preferred_element_type=jnp.float32
    ).astype(jnp.bfloat16)
    grad_heads = lax.all_to_all(
        grad_merged.reshape(groups, tok_slot, n_fsdp, lane_width),
        "fsdp",
        split_axis=2,
        concat_axis=1,
        tiled=True,
    ).reshape(groups, span_rows, lane_width)

    def attend_back(slot_item):
        slot_queries, slot_keys, slot_values, grad_mix, log_norm, length = slot_item
        query_split = slot_queries.reshape(query_blocks, query_rows, heads_here, HD)
        key_split = slot_keys.reshape(key_blocks, key_rows, heads_here, HD)
        value_split = slot_values.reshape(key_blocks, key_rows, heads_here, HD)
        grad_split = grad_mix.reshape(query_blocks, query_rows, heads_here, HD)

        def value_pass(value_total, query_item):
            query_block, grad_block, norm_block = query_item

            def value_per_key(row_dot, key_item):
                key_block, value_block, key_start = key_item
                scores = block_scores(query_block, key_block, key_start, length, scale)
                probability = jnp.exp(scores - norm_block[..., None])
                grad_probs = jnp.einsum(
                    "qhd,khd->hqk", grad_block, value_block, preferred_element_type=jnp.float32
                )
                value_part = jnp.einsum(
                    "hqk,qhd->khd",
                    probability.astype(jnp.bfloat16),
                    grad_block,
                    preferred_element_type=jnp.float32,
                )
                return (row_dot + jnp.sum(probability * grad_probs, axis=-1), value_part)

            row_dot, value_parts = lax.scan(
                value_per_key,
                jnp.zeros((heads_here, query_rows), jnp.float32),
                (key_split, value_split, key_starts),
            )
            return (value_total + value_parts.reshape(key_count, heads_here, HD), row_dot)

        value_grad, row_dots = lax.scan(
            value_pass,
            jnp.zeros((key_count, heads_here, HD), jnp.float32),
            (query_split, grad_split, log_norm),
        )

        def key_pass(key_total, query_item):
            query_block, grad_block, norm_block, dot_block = query_item

            def key_per_key(query_accum, key_item):
                key_block, value_block, key_start = key_item
                scores = block_scores(query_block, key_block, key_start, length, scale)
                probability = jnp.exp(scores - norm_block[..., None])
                grad_probs = jnp.einsum(
                    "qhd,khd->hqk", grad_block, value_block, preferred_element_type=jnp.float32
                )
                grad_scores = (probability * (grad_probs - dot_block[..., None])).astype(
                    jnp.bfloat16
                )
                query_accum = query_accum + jnp.einsum(
                    "hqk,khd->qhd", grad_scores, key_block, preferred_element_type=jnp.float32
                )
                key_part = jnp.einsum(
                    "hqk,qhd->khd", grad_scores, query_block, preferred_element_type=jnp.float32
                )
                return (query_accum, key_part)

            query_grad, key_parts = lax.scan(
                key_per_key,
                jnp.zeros((query_rows, heads_here, HD), jnp.float32),
                (key_split, value_split, key_starts),
            )
            return (key_total + key_parts.reshape(key_count, heads_here, HD), query_grad)

        key_grad, query_grads = lax.scan(
            key_pass,
            jnp.zeros((key_count, heads_here, HD), jnp.float32),
            (query_split, grad_split, log_norm, row_dots),
        )
        return (
            query_grads.reshape(span_rows, lane_width) * scale,
            key_grad.reshape(key_count, lane_width) * scale,
            value_grad.reshape(key_count, lane_width),
        )

    grad_queries, key_terms, value_terms = lax.map(
        attend_back, (queries, all_keys, all_values, grad_heads, log_norms, lengths)
    )
    grad_keys, grad_values = (
        lax.psum_scatter(
            key_terms.astype(jnp.bfloat16), "ctx", scatter_dimension=1, tiled=True
        ).astype(jnp.float32),
        lax.psum_scatter(
            value_terms.astype(jnp.bfloat16), "ctx", scatter_dimension=1, tiled=True
        ).astype(jnp.float32),
    )
    head_pos = (ctx_at * span_rows + jnp.arange(span_rows, dtype=jnp.int32)).astype(jnp.float32)
    head_cosine, head_sine = rope_tables(head_pos, HD)
    query_back = rotate(
        grad_queries.reshape(groups, span_rows, heads_here, HD), head_cosine, -head_sine
    )
    key_back = rotate(grad_keys.reshape(groups, span_rows, heads_here, HD), head_cosine, -head_sine)
    value_back = grad_values.reshape(groups, span_rows, heads_here, HD)
    grad_pack = (
        jnp.stack([query_back, key_back, value_back], axis=2)
        .astype(jnp.bfloat16)
        .reshape(groups, span_rows, 3, 1, lane_width)
    )
    grad_joined = lax.all_to_all(
        grad_pack, "fsdp", split_axis=1, concat_axis=3, tiled=True
    ).reshape(row_count, 3 * width)
    d_qkv = jnp.einsum("rd,re->de", flat_tokens, grad_joined, preferred_element_type=jnp.float32)
    d_qkv_bias = jnp.sum(grad_joined.astype(jnp.float32), axis=0)
    input_grad = (
        jnp.einsum("re,de->rd", grad_joined, back_qkv, preferred_element_type=jnp.float32)
        + grad_one
    ).astype(jnp.bfloat16)
    shards = (
        lax.psum_scatter(d_qkv, ("ctx", "fsdp"), scatter_dimension=0, tiled=True),
        lax.psum_scatter(d_qkv_bias, ("ctx", "fsdp"), scatter_dimension=0, tiled=True),
        lax.psum_scatter(d_out, ("ctx", "fsdp"), scatter_dimension=0, tiled=True),
        lax.psum_scatter(d_out_bias, ("ctx", "fsdp"), scatter_dimension=0, tiled=True),
        lax.psum_scatter(d_gain_one, ("ctx", "fsdp"), scatter_dimension=0, tiled=True),
        lax.psum_scatter(d_shift_one, ("ctx", "fsdp"), scatter_dimension=0, tiled=True),
        lax.psum_scatter(d_up, ("ctx", "fsdp"), scatter_dimension=0, tiled=True),
        lax.psum_scatter(d_up_bias, ("ctx", "fsdp"), scatter_dimension=0, tiled=True),
        lax.psum_scatter(d_down, ("ctx", "fsdp"), scatter_dimension=0, tiled=True),
        lax.psum_scatter(d_down_bias, ("ctx", "fsdp"), scatter_dimension=0, tiled=True),
        lax.psum_scatter(d_gain_two, ("ctx", "fsdp"), scatter_dimension=0, tiled=True),
        lax.psum_scatter(d_shift_two, ("ctx", "fsdp"), scatter_dimension=0, tiled=True),
        lax.psum_scatter(d_proj, ("ctx", "fsdp"), scatter_dimension=0, tiled=True),
    )
    totals = (
        lax.psum(shards[0].astype(jnp.bfloat16), "slot").astype(jnp.float32),
        lax.psum(shards[1].astype(jnp.bfloat16), "slot").astype(jnp.float32),
        lax.psum(shards[2].astype(jnp.bfloat16), "slot").astype(jnp.float32),
        lax.psum(shards[3].astype(jnp.bfloat16), "slot").astype(jnp.float32),
        lax.psum(shards[4].astype(jnp.bfloat16), "slot").astype(jnp.float32),
        lax.psum(shards[5].astype(jnp.bfloat16), "slot").astype(jnp.float32),
        lax.psum(shards[6].astype(jnp.bfloat16), "slot").astype(jnp.float32),
        lax.psum(shards[7].astype(jnp.bfloat16), "slot").astype(jnp.float32),
        lax.psum(shards[8].astype(jnp.bfloat16), "slot").astype(jnp.float32),
        lax.psum(shards[9].astype(jnp.bfloat16), "slot").astype(jnp.float32),
        lax.psum(shards[10].astype(jnp.bfloat16), "slot").astype(jnp.float32),
        lax.psum(shards[11].astype(jnp.bfloat16), "slot").astype(jnp.float32),
        lax.psum(shards[12].astype(jnp.bfloat16), "slot").astype(jnp.float32),
    )
    return (
        out_low.reshape(groups, tok_slot, width),
        projected.astype(jnp.bfloat16).reshape(groups, tok_slot, -1),
        input_grad.reshape(groups, tok_slot, width),
        totals[0],
        totals[1],
        totals[2],
        totals[3],
        totals[4],
        totals[5],
        totals[6],
        totals[7],
        totals[8],
        totals[9],
        totals[10],
        totals[11],
        totals[12],
    )


def solution(mesh):
    n_slot, n_ctx, n_fsdp = (mesh.shape[a] for a in ("slot", "ctx", "fsdp"))
    rows_axes = ("ctx", "fsdp")
    step = per_device
    if n_slot == 2 and n_fsdp % 2 == 0 and n_ctx * n_fsdp == H:
        mesh = Mesh(
            mesh.devices.reshape(n_slot, n_ctx, n_fsdp // 2, 2), ("slot", "ctx", "x", "core")
        )
        rows_axes = GROUP
        step = head_device
    in_specs = (
        P("slot", rows_axes, None),
        P("slot"),
        P(rows_axes, None),
        P(rows_axes),
        P(rows_axes, None),
        P(rows_axes),
        P(rows_axes),
        P(rows_axes),
        P(rows_axes, None),
        P(rows_axes),
        P(rows_axes, None),
        P(rows_axes),
        P(rows_axes),
        P(rows_axes),
        P(rows_axes, None),
        P("slot", rows_axes, None),
        P("slot", rows_axes, None),
    )
    out_specs = (
        P("slot", rows_axes, None),
        P("slot", rows_axes, None),
        P("slot", rows_axes, None),
        P(rows_axes, None),
        P(rows_axes),
        P(rows_axes, None),
        P(rows_axes),
        P(rows_axes),
        P(rows_axes),
        P(rows_axes, None),
        P(rows_axes),
        P(rows_axes, None),
        P(rows_axes),
        P(rows_axes),
        P(rows_axes),
        P(rows_axes, None),
    )
    return jax.shard_map(
        step, mesh=mesh, in_specs=in_specs, out_specs=out_specs, check_vma=False
    )
```

```python
from functools import partial

import jax
import jax.numpy as jnp
from jax import lax
from jax.experimental import pallas as pl
from jax.experimental.pallas import tpu as pltpu
from jax.sharding import Mesh
from jax.sharding import PartitionSpec as P

H = 16
HD = 64
LN_EPS = 1e-05
NEG_FILL = -1e30
F32 = jnp.float32
BF16 = jnp.bfloat16
GROUP = ("ctx", "x", "core")
LANE = ("ctx", "x")
SWAP = [(0, 1), (1, 0)]
VMEM_LIMIT = 60 * 1024 * 1024


def mm(left, right):
    return jnp.dot(left, right, preferred_element_type=F32)


def contract(left, right, left_dim, right_dim):
    return lax.dot_general(
        left, right, (((left_dim,), (right_dim,)), ((), ())), preferred_element_type=F32
    )


def swap_core(value):
    return lax.ppermute(value, "core", SWAP)


def swap_slot(value):
    return lax.ppermute(value, "slot", SWAP)


def pick(stacked, index, axis):
    return lax.dynamic_index_in_dim(stacked, index, axis, keepdims=False)


MESH = pl.DeviceIdType.MESH


def at_device(**where):
    names = ("slot", "ctx", "x", "core")
    return tuple(where[n] if n in where else lax.axis_index(n) for n in names)


def greet(peers):
    barrier = pltpu.get_barrier_semaphore()
    for peer in peers:
        pl.semaphore_signal(barrier, inc=1, device_id=peer, device_id_type=MESH)
    pl.semaphore_wait(barrier, len(peers))


def group_peers(n_ctx, n_x):
    ctx, x, core = (lax.axis_index(n) for n in GROUP)
    peers = []
    for dz in range(n_ctx):
        for dx in range(n_x):
            for dc in range(2):
                if dz or dx or dc:
                    where = (lax.rem(ctx + dz, n_ctx), lax.rem(x + dx, n_x), lax.rem(core + dc, 2))
                    peers.append(where)
    return peers


def start_kernel(
    tok_ref, head_ref, small_ref, wa_ref, wb_ref, wc_ref,
    all_ref, heads_ref, smalls_ref, fa_ref, fb_ref, fc_ref,
    far_send, local_sem, head_recv, small_recv, block_send, block_recv, lane_send, lane_recv,
    *, n_ctx, n_x
):
    part = tok_ref.shape[1]
    ctx, x, core = (lax.axis_index(n) for n in GROUP)
    me = (ctx * n_x + x) * 2 + core
    chip = ctx * n_x + x
    peers = group_peers(n_ctx, n_x)
    greet([at_device(ctx=z, x=a, core=c) for z, a, c in peers])
    up = at_device(ctx=lax.rem(ctx + 1, n_ctx))
    down = at_device(ctx=lax.rem(ctx + n_ctx - 1, n_ctx))
    side = at_device(x=1 - x)
    twin = at_device(core=1 - core)
    routes = (up, down, side, twin)

    def block_at(k, parity):
        b = 2 * k + parity
        return all_ref.at[:, pl.ds(pl.multiple_of(b * part, part), part), :]

    class Tokens:
        lanes = 4

        @staticmethod
        def copies(k, lane, own=False, parity=None):
            parity = core if parity is None else parity
            b = 2 * k + parity
            source = tok_ref if own else block_at(k, parity)
            return [pltpu.make_async_remote_copy(
                source, block_at(k, parity), block_send.at[lane, b], block_recv.at[b],
                device_id=routes[lane], device_id_type=MESH)]

    class Weights:
        lanes = 3

        @staticmethod
        def copies(k, lane, own=False):
            out = []
            for i, (mine, full) in enumerate(((wa_ref, fa_ref), (wb_ref, fb_ref), (wc_ref, fc_ref))):
                rows = mine.shape[0]
                place = full.at[pl.ds(pl.multiple_of(k * rows, rows), rows), :]
                out.append(pltpu.make_async_remote_copy(
                    mine if own else place, place, lane_send.at[i, lane, k], lane_recv.at[i, k],
                    device_id=routes[lane], device_id_type=MESH))
            return out

    def start(copies):
        for copy in copies:
            copy.start()

    def arrived(copies):
        for copy in copies:
            copy.wait_recv()

    def begin(kind):
        @pl.when(ctx + 1 < n_ctx)
        def _():
            start(kind.copies(chip, 0, own=True))

        @pl.when(ctx > 0)
        def _():
            start(kind.copies(chip, 1, own=True))

        for lane in range(2, kind.lanes):
            start(kind.copies(chip, lane, own=True))

    def relay(kind):
        for r in range(1, n_ctx):
            for sign, lane, more in ((-1, 0, ctx + 1 < n_ctx), (1, 1, ctx > 0)):
                z = ctx + sign * r

                @pl.when((z >= 0) & (z < n_ctx))
                def _():
                    k = z * n_x + x
                    arrived(kind.copies(k, 0))

                    @pl.when(more)
                    def _():
                        start(kind.copies(k, lane))

                    for other in range(2, kind.lanes):
                        start(kind.copies(k, other))

    def from_side(kind):
        def one(z):
            k = z * n_x + 1 - x
            arrived(kind.copies(k, 0))
            if kind.lanes == 4:
                start(kind.copies(k, 3))

        one(ctx)
        for r in range(1, n_ctx):
            for sign in (-1, 1):
                z = ctx + sign * r

                @pl.when((z >= 0) & (z < n_ctx))
                def _():
                    one(z)

    def drained(kind):
        def left(copies):
            for copy in copies:
                copy.wait_send()

        for z in range(n_ctx):
            k = z * n_x + x

            @pl.when((z <= ctx) & (ctx + 1 < n_ctx))
            def _():
                left(kind.copies(k, 0))

            @pl.when((z >= ctx) & (ctx > 0))
            def _():
                left(kind.copies(k, 1))

            for lane in range(2, kind.lanes):
                left(kind.copies(k, lane))
            if kind.lanes == 4:
                left(kind.copies(z * n_x + 1 - x, 3))

    pushes = []
    for k, (z, a, c) in enumerate(peers):
        them = (z * n_x + a) * 2 + c
        target = at_device(ctx=z, x=a, core=c)
        pushes.append(pltpu.make_async_remote_copy(
            head_ref.at[them], heads_ref.at[me], far_send.at[2 * k], head_recv.at[me],
            device_id=target, device_id_type=MESH))
        pushes.append(pltpu.make_async_remote_copy(
            small_ref, smalls_ref.at[me], far_send.at[2 * k + 1], small_recv.at[me],
            device_id=target, device_id_type=MESH))
    locals_ = [
        pltpu.make_async_copy(tok_ref, block_at(chip, core), local_sem.at[0]),
        pltpu.make_async_copy(head_ref.at[me], heads_ref.at[me], local_sem.at[1]),
        pltpu.make_async_copy(small_ref, smalls_ref.at[me], local_sem.at[2]),
    ]
    for i, (mine, full) in enumerate(((wa_ref, fa_ref), (wb_ref, fb_ref), (wc_ref, fc_ref))):
        rows = mine.shape[0]
        place = full.at[pl.ds(pl.multiple_of(chip * rows, rows), rows), :]
        locals_.append(pltpu.make_async_copy(mine, place, local_sem.at[3 + i]))

    begin(Tokens)
    for push in pushes:
        push.start()
    for copy in locals_:
        copy.start()
    relay(Tokens)
    begin(Weights)
    from_side(Tokens)
    relay(Weights)
    from_side(Weights)
    for z in range(n_ctx):
        for a in range(n_x):
            arrived(Tokens.copies(z * n_x + a, 0, parity=1 - core))
    for k, (z, a, c) in enumerate(peers):
        them = (z * n_x + a) * 2 + c
        pltpu.make_async_remote_copy(
            head_ref.at[them], heads_ref.at[them], far_send.at[2 * k], head_recv.at[them],
            device_id=twin, device_id_type=MESH).wait_recv()
        pltpu.make_async_remote_copy(
            small_ref, smalls_ref.at[them], far_send.at[2 * k + 1], small_recv.at[them],
            device_id=twin, device_id_type=MESH).wait_recv()
    for push in pushes:
        push.wait_send()
    for copy in locals_:
        copy.wait()
    drained(Tokens)
    drained(Weights)


def gather_start(tokens, heads, small, *weights):
    n_ctx, n_x = lax.axis_size("ctx"), lax.axis_size("x")
    chips = n_ctx * n_x
    n = 2 * chips
    slots, part, width = tokens.shape
    vmem = pl.BlockSpec(memory_space=pltpu.VMEM)
    anywhere = pl.BlockSpec(memory_space=pl.ANY)
    dma = pltpu.SemaphoreType.DMA
    return pl.pallas_call(
        partial(start_kernel, n_ctx=n_ctx, n_x=n_x),
        in_specs=[vmem] * 6,
        out_specs=[anywhere, vmem, vmem, anywhere, anywhere, anywhere],
        out_shape=[
            jax.ShapeDtypeStruct((slots, n * part, width), tokens.dtype),
            jax.ShapeDtypeStruct(heads.shape, heads.dtype),
            jax.ShapeDtypeStruct((n,) + small.shape, small.dtype),
        ]
        + [jax.ShapeDtypeStruct((chips * w.shape[0], w.shape[1]), w.dtype) for w in weights],
        scratch_shapes=[
            dma((2 * (n - 1),)),
            dma((6,)),
            dma((n,)),
            dma((n,)),
            dma((4, n)),
            dma((n,)),
            dma((3, 3, chips)),
            dma((3, chips)),
        ],
        compiler_params=pltpu.CompilerParams(
            collective_id=1, has_side_effects=True, vmem_limit_bytes=VMEM_LIMIT
        ),
        cost_estimate=pl.CostEstimate(
            flops=0, bytes_accessed=2 * n * tokens.size, transcendentals=0
        ),
        name="gather_start",
    )(tokens, heads, small, *weights)


def finish_kernel(
    up_ref, out_ref, x_up, x_out, small_ref, qkv_ref, red_ref, join_ref, weight_ref, one_ref,
    g_down, g_up, g_out, g_small, g_qkv, g_in,
    s_up, s_out, z_up, z_out, own_up, own_out,
    smalls, own_small, pair_small, qkvs, pair_qkv, pair_down, pair_out, last_up, low_up,
    joins, partial_in, pair_in,
    join_send, join_recv, in_send, in_recv,
    far_send, small_recv, qkv_recv, z_send, z_recv, y_send, y_recv, *, n_ctx, n_x
):
    ctx, x, core = (lax.axis_index(n) for n in GROUP)
    slot = lax.axis_index("slot")
    me = (ctx * n_x + x) * 2 + core
    shard = g_up.shape[0]
    part = g_down.shape[0] // 2
    peers = group_peers(n_ctx, n_x)
    across = at_device(slot=1 - slot)
    corner = at_device(slot=1 - slot, core=1 - core)
    twin = at_device(core=1 - core)
    greet([at_device(ctx=z, x=a, core=c) for z, a, c in peers] + [across, corner])

    def remote(source, target_ref, send_sem, recv_sem, target):
        return pltpu.make_async_remote_copy(
            source, target_ref, send_sem, recv_sem, device_id=target, device_id_type=MESH)

    started = []

    def launch(copy):
        copy.start()
        started.append(copy)
        return copy

    chip = ctx * n_x + x
    lane_peers = [(z, a) for z, a, c in peers[1::2]]
    for k, (z, a) in enumerate(lane_peers):
        launch(remote(
            join_ref.at[z * n_x + a], joins.at[chip], join_send.at[k], join_recv.at[chip],
            at_device(ctx=z, x=a)))
    second_up, second_out = [], []
    for j in range(n_ctx):
        place = lax.rem(ctx + 1 + j, n_ctx)
        sum_up = up_ref[place].astype(F32) + x_up[place].astype(F32)
        sum_out = out_ref[place].astype(F32) + x_out[place].astype(F32)
        if j < n_ctx - 1:
            s_up[j] = sum_up.astype(BF16)
            s_out[j] = sum_out.astype(BF16)
            target = at_device(ctx=place)
            second_up.append(launch(remote(
                s_up.at[j], z_up.at[j], z_send.at[0, j], z_recv.at[0, j], target)))
            second_out.append(launch(remote(
                s_out.at[j], z_out.at[j], z_send.at[1, j], z_recv.at[1, j], target)))
        else:
            own_up[...] = sum_up
            own_out[...] = sum_out

    down_copy = launch(remote(red_ref, pair_down, y_send.at[0], y_recv.at[0], across))
    for k, (z, a, c) in enumerate(peers):
        them = (z * n_x + a) * 2 + c
        target = at_device(ctx=z, x=a, core=c)
        launch(remote(
            qkv_ref.at[them], qkvs.at[me], far_send.at[2 * k], qkv_recv.at[me], target))
        launch(remote(
            small_ref.at[them], smalls.at[me], far_send.at[2 * k + 1], small_recv.at[me], target))
    qkvs[me] = qkv_ref[me]
    smalls[me] = small_ref[me]

    def add_head(source, rows_of, first):
        weight = jnp.concatenate(
            [weight_ref[b, source] for b in range(weight_ref.shape[0])], axis=0)
        for h in range(2):
            owner = core if h == 0 else 1 - core
            rows = rows_of(owner)
            cols = rows.shape[2] // 2
            rows = jnp.concatenate(
                [r for t in range(rows.shape[0]) for r in (rows[t, :, :cols], rows[t, :, cols:])],
                axis=0)
            term = contract(rows, weight, 1, 1)
            partial_in[h] = term if first else partial_in[h] + term

    add_head(chip, lambda owner: join_ref[chip, owner], True)
    for k, (z, a) in enumerate(lane_peers):
        source = z * n_x + a
        remote(
            join_ref.at[source], joins.at[source], join_send.at[k], join_recv.at[source], twin
        ).wait_recv()
        add_head(source, lambda owner: joins[source, owner], False)
    in_copy = launch(remote(partial_in.at[1], pair_in, in_send, in_recv, twin))

    for z, a, c in peers:
        them = (z * n_x + a) * 2 + c
        remote(
            qkv_ref.at[them], qkvs.at[them], far_send.at[0], qkv_recv.at[them], twin
        ).wait_recv()
        remote(
            small_ref.at[them], smalls.at[them], far_send.at[1], small_recv.at[them], twin
        ).wait_recv()
    qkv_copy = launch(remote(qkvs, pair_qkv, y_send.at[1], y_recv.at[1], across))
    own_small[...] = jnp.sum(smalls[...].astype(F32), axis=0).astype(BF16)
    small_copy = launch(remote(own_small, pair_small, y_send.at[2], y_recv.at[2], across))

    for j in range(n_ctx - 1):
        second_out[j].wait_recv()
        own_out[...] += z_out[j].astype(F32)
    s_out[n_ctx - 1] = own_out[...].astype(BF16)
    out_copy = launch(remote(
        s_out.at[n_ctx - 1], pair_out, y_send.at[3], y_recv.at[3], across))
    for j in range(n_ctx - 1):
        second_up[j].wait_recv()
        own_up[...] += z_up[j].astype(F32)
    low_up[...] = own_up[...].astype(BF16).reshape(low_up.shape)
    quarter_copies = [
        launch(remote(low_up.at[1 - core], last_up.at[0], y_send.at[4], y_recv.at[4], twin)),
        launch(remote(low_up.at[core], last_up.at[1], y_send.at[5], y_recv.at[5], across)),
        launch(remote(low_up.at[1 - core], last_up.at[2], y_send.at[6], y_recv.at[6], corner)),
    ]

    in_copy.wait_recv()
    g_in[...] = (partial_in[0] + pair_in[...] + one_ref[...]).astype(BF16)
    half = pl.multiple_of(slot * part, part)
    other_half = pl.multiple_of((1 - slot) * part, part)
    g_down[pl.ds(half, part), :] = red_ref[...].astype(F32)
    down_copy.wait_recv()
    g_down[pl.ds(other_half, part), :] = pair_down[...].astype(F32)
    qkv_copy.wait_recv()
    g_qkv[...] = qkvs[...].astype(F32) + pair_qkv[...].astype(F32)
    small_copy.wait_recv()
    g_small[...] = own_small[...].astype(F32) + pair_small[...].astype(F32)
    out_copy.wait_recv()
    g_out[...] = s_out[n_ctx - 1].astype(F32) + pair_out[...].astype(F32)

    def place_quarter(rows, quarter_core, quarter_slot):
        for k in range(n_ctx * n_x):
            at = pl.multiple_of(((2 * k + quarter_core) * 2 + quarter_slot) * part, part)
            g_up[:, pl.ds(at, part)] = rows[:, k * part : (k + 1) * part].astype(F32)

    place_quarter(low_up[core], core, slot)
    quarter_copies[0].wait_recv()
    place_quarter(last_up[0], 1 - core, slot)
    quarter_copies[1].wait_recv()
    place_quarter(last_up[1], core, 1 - slot)
    quarter_copies[2].wait_recv()
    place_quarter(last_up[2], 1 - core, 1 - slot)
    for copy in started:
        copy.wait_send()


def finish_grads(up, out, x_up, x_out, small, qkv, red_down, joined, weight, grad_one):
    n_ctx, n_x = lax.axis_size("ctx"), lax.axis_size("x")
    n = 2 * n_ctx * n_x
    part, width = red_down.shape
    shard = out.shape[1]
    vmem = pl.BlockSpec(memory_space=pltpu.VMEM)
    dma = pltpu.SemaphoreType.DMA

    def low(*shape):
        return pltpu.VMEM(shape, BF16)

    def wide(*shape):
        return jax.ShapeDtypeStruct(shape, F32)

    return pl.pallas_call(
        partial(finish_kernel, n_ctx=n_ctx, n_x=n_x),
        in_specs=[vmem] * 10,
        out_specs=[vmem] * 6,
        out_shape=[
            wide(2 * part, width),
            wide(shard, 4 * up.shape[2]),
            wide(shard, width),
            wide(*small.shape[1:]),
            wide(*qkv.shape),
            jax.ShapeDtypeStruct(grad_one.shape, BF16),
        ],
        scratch_shapes=[
            low(n_ctx - 1, *up.shape[1:]),
            low(n_ctx, *out.shape[1:]),
            low(n_ctx - 1, *up.shape[1:]),
            low(n_ctx - 1, *out.shape[1:]),
            pltpu.VMEM(up.shape[1:], F32),
            pltpu.VMEM(out.shape[1:], F32),
            low(*small.shape),
            low(*small.shape[1:]),
            low(*small.shape[1:]),
            low(*qkv.shape),
            low(*qkv.shape),
            low(part, width),
            low(*out.shape[1:]),
            low(3, shard, up.shape[2]),
            low(2, shard, up.shape[2]),
            low(*joined.shape),
            pltpu.VMEM((2,) + grad_one.shape, F32),
            pltpu.VMEM(grad_one.shape, F32),
            dma((n_ctx * n_x - 1,)),
            dma((n_ctx * n_x,)),
            dma,
            dma,
            dma((2 * (n - 1),)),
            dma((n,)),
            dma((n,)),
            dma((2, n_ctx - 1)),
            dma((2, n_ctx - 1)),
            dma((7,)),
            dma((7,)),
        ],
        compiler_params=pltpu.CompilerParams(
            collective_id=2, has_side_effects=True, vmem_limit_bytes=VMEM_LIMIT
        ),
        cost_estimate=pl.CostEstimate(flops=0, bytes_accessed=16 * up.size, transcendentals=0),
        name="finish_grads",
    )(up, out, x_up, x_out, small, qkv, red_down, joined, weight, grad_one)


def project_kernel(tok_ref, w_ref, b_ref, cos_ref, sin_ref, q_ref, k_ref, v_ref):
    joined = mm(tok_ref[...], w_ref[...]) + b_ref[...]
    wide = 2 * HD
    turned = joined[:, :wide] * cos_ref[...] + joined[:, wide : 2 * wide] * sin_ref[...]
    q_ref[...] = (turned[:, :HD].astype(BF16) * HD ** (-0.5)).astype(BF16)
    k_ref[...] = turned[:, HD:].astype(BF16)
    v_ref[...] = joined[:, 2 * wide :].astype(BF16)


def project(tokens, weight, bias, cosine, sine):
    rows, width = tokens.shape
    seq = cosine.shape[0]
    block = min(512, seq)
    per_slot = seq // block
    cols = weight.shape[1]
    head_out = jax.ShapeDtypeStruct((rows, HD), BF16)
    head_spec = pl.BlockSpec((block, HD), lambda i: (i, 0))
    return pl.pallas_call(
        project_kernel,
        grid=(rows // block,),
        in_specs=[
            pl.BlockSpec((block, width), lambda i: (i, 0)),
            pl.BlockSpec((width, cols), lambda i: (0, 0)),
            pl.BlockSpec((1, cols), lambda i: (0, 0)),
            pl.BlockSpec((block, 2 * HD), lambda i: (i % per_slot, 0)),
            pl.BlockSpec((block, 2 * HD), lambda i: (i % per_slot, 0)),
        ],
        out_specs=[head_spec] * 3,
        out_shape=[head_out] * 3,
        compiler_params=pltpu.CompilerParams(vmem_limit_bytes=VMEM_LIMIT),
        cost_estimate=pl.CostEstimate(
            flops=2 * rows * width * cols, bytes_accessed=2 * rows * width, transcendentals=0
        ),
        name="project",
    )(tokens, weight, bias, cosine, sine)


QB = 512
KB = 512


def forward_kernel(
    len_ref, core_ref, q_ref, k_ref, v_ref, out_ref, send_ref, norm_ref, *, part
):
    length = len_ref[pl.program_id(0)]
    core = core_ref[0]
    queries = q_ref[0]
    rows = queries.shape[0]

    def step(j, state):
        highest, total, mix = state
        start = pl.multiple_of(j * KB, KB)
        scores = contract(queries, k_ref[0, pl.ds(start, KB), :], 1, 1)
        ids = start + lax.broadcasted_iota(jnp.int32, (1, KB), 1)
        scores = jnp.where(ids < length, scores, NEG_FILL)
        higher = jnp.maximum(highest, jnp.max(scores, axis=1, keepdims=True))
        fade = jnp.exp(highest - higher)
        weights = jnp.exp(scores - higher)
        total = total * fade + jnp.sum(weights, axis=1, keepdims=True)
        mix = mix * fade + mm(weights.astype(BF16), v_ref[0, pl.ds(start, KB), :])
        return higher, total, mix

    blocks = (length + KB - 1) // KB
    highest, total, mix = lax.fori_loop(
        0,
        blocks,
        step,
        (
            jnp.full((rows, 1), NEG_FILL, F32),
            jnp.zeros((rows, 1), F32),
            jnp.zeros((rows, HD), F32),
        ),
    )
    mix = mix / total
    out_ref[0] = mix
    log_norm = jnp.broadcast_to(highest + jnp.log(total), (rows, 128))
    norm_ref[0] = jnp.transpose(log_norm)[0:1, :]
    low = mix.astype(BF16)
    for chip in range(rows // (2 * part)):
        for half in range(2):
            at = (2 * chip + half) * part
            send_ref[chip, half ^ core, 0] = low[at : at + part]


def attend(lengths, core, queries, keys, values, part):
    slots, seq, _ = queries.shape
    chips = seq // (2 * part)
    spec_q = pl.BlockSpec((1, QB, HD), lambda s, i, *_: (s, i, 0))
    spec_k = pl.BlockSpec((1, seq, HD), lambda s, i, *_: (s, 0, 0))
    return pl.pallas_call(
        partial(forward_kernel, part=part),
        grid_spec=pltpu.PrefetchScalarGridSpec(
            num_scalar_prefetch=2,
            grid=(slots, seq // QB),
            in_specs=[spec_q, spec_k, spec_k],
            out_specs=[
                spec_q,
                pl.BlockSpec(
                    (QB // (2 * part), 2, 1, part, HD), lambda s, i, *_: (i, 0, s, 0, 0)
                ),
                pl.BlockSpec((1, 1, QB), lambda s, i, *_: (s, 0, i)),
            ],
        ),
        out_shape=[
            jax.ShapeDtypeStruct((slots, seq, HD), F32),
            jax.ShapeDtypeStruct((chips, 2, slots, part, HD), BF16),
            jax.ShapeDtypeStruct((slots, 1, seq), F32),
        ],
        compiler_params=pltpu.CompilerParams(vmem_limit_bytes=VMEM_LIMIT),
        cost_estimate=pl.CostEstimate(
            flops=16 * slots * seq * seq * HD,
            bytes_accessed=8 * slots * seq * HD,
            transcendentals=slots * seq * seq,
        ),
        name="attend",
    )(lengths, core, queries, keys, values)


def backward_kernel(
    len_ref, q_ref, k_ref, v_ref, g_ref, norm_ref, dot_ref, dq_ref, dk_ref, dv_ref, dqt
):
    length = len_ref[pl.program_id(0)]
    j = pl.program_id(1)
    start = j * KB
    key_block = k_ref[0]
    value_block = v_ref[0]

    @pl.when(j == 0)
    def _():
        dqt[...] = jnp.zeros_like(dqt)

    turned = jnp.transpose(key_block.astype(F32)).astype(BF16)
    ids = start + lax.broadcasted_iota(jnp.int32, (KB, 1), 0)
    shift = jnp.where(ids < length, 0.0, NEG_FILL)

    def step(i, state):
        key_grad, value_grad = state
        at = pl.multiple_of(i * QB, QB)
        queries = q_ref[0, pl.ds(at, QB), :]
        grads = g_ref[0, pl.ds(at, QB), :]
        scores = contract(key_block, queries, 1, 1) + shift
        probs = jnp.exp(scores - norm_ref[0, :, pl.ds(at, QB)])
        grad_probs = contract(value_block, grads, 1, 1)
        grad_scores = (probs * (grad_probs - dot_ref[0, :, pl.ds(at, QB)])).astype(BF16)
        value_grad = value_grad + mm(probs.astype(BF16), grads)
        key_grad = key_grad + mm(grad_scores, queries)
        dqt[:, pl.ds(at, QB)] += mm(turned, grad_scores)
        return key_grad, value_grad

    blocks = jnp.where(start < length, (length + QB - 1) // QB, 0)
    zero = jnp.zeros((KB, HD), F32)
    key_grad, value_grad = lax.fori_loop(0, blocks, step, (zero, zero))
    dk_ref[0] = key_grad
    dv_ref[0] = value_grad

    @pl.when(j == pl.num_programs(1) - 1)
    def _():
        dq_ref[0] = jnp.transpose(dqt[...])


def attend_back(lengths, queries, keys, values, grads, norms, dots):
    slots, seq, _ = queries.shape
    whole = pl.BlockSpec((1, seq, HD), lambda s, j, *_: (s, 0, 0))
    block = pl.BlockSpec((1, KB, HD), lambda s, j, *_: (s, j, 0))
    row = pl.BlockSpec((1, 1, seq), lambda s, j, *_: (s, 0, 0))
    out = jax.ShapeDtypeStruct((slots, seq, HD), F32)
    return pl.pallas_call(
        backward_kernel,
        grid_spec=pltpu.PrefetchScalarGridSpec(
            num_scalar_prefetch=1,
            grid=(slots, seq // KB),
            in_specs=[whole, block, block, whole, row, row],
            out_specs=[whole, block, block],
            scratch_shapes=[pltpu.VMEM((HD, seq), F32)],
        ),
        out_shape=[out] * 3,
        compiler_params=pltpu.CompilerParams(vmem_limit_bytes=VMEM_LIMIT),
        cost_estimate=pl.CostEstimate(
            flops=40 * slots * seq * seq * HD,
            bytes_accessed=20 * slots * seq * HD,
            transcendentals=slots * seq * seq,
        ),
        name="attend_back",
    )(lengths, queries, keys, values, grads, norms, dots)


def join_kernel(
    q_ref, k_ref, v_ref, tok_ref, cos_ref, sin_ref, join_ref, grad_ref, total, bias, *, part
):
    i = pl.program_id(0)

    @pl.when(i == 0)
    def _():
        total[...] = jnp.zeros_like(total)
        bias[...] = jnp.zeros_like(bias)

    pair = jnp.concatenate([q_ref[...] * HD ** (-0.5), k_ref[...]], axis=1)
    half = HD // 2
    lanes = lax.broadcasted_iota(jnp.int32, (1, 2 * HD), 1)
    low = lax.rem(lanes, HD) < half
    swapped = jnp.where(low, pltpu.roll(pair, 2 * HD - half, 1), pltpu.roll(pair, half, 1))
    sine = jnp.where(low, sin_ref[...], -sin_ref[...])
    turned = pair * cos_ref[...] + swapped * sine
    joined = jnp.concatenate([turned, v_ref[...]], axis=1).astype(BF16)
    for chip in range(joined.shape[0] // (2 * part)):
        for core in range(2):
            at = (2 * chip + core) * part
            upper, lower = joined[at : at + part // 2], joined[at + part // 2 : at + part]
            join_ref[chip, core, 0] = jnp.concatenate([upper, lower], axis=1)
    total[...] += contract(joined, tok_ref[...], 0, 0)
    bias[...] += jnp.sum(joined.astype(F32), axis=0, keepdims=True)

    @pl.when(i == pl.num_programs(0) - 1)
    def _():
        turned_total = jnp.transpose(total[...])
        shard = turned_total.shape[0] // grad_ref.shape[0]
        extra = jnp.broadcast_to(bias[...], (grad_ref.shape[1] - shard, bias.shape[1]))
        for d in range(grad_ref.shape[0]):
            grad_ref[d, :shard] = turned_total[d * shard : (d + 1) * shard].astype(BF16)
            grad_ref[d, shard:] = extra.astype(BF16)


def join_grads(grad_q, grad_k, grad_v, tokens, cosine, sine, part, n_group):
    slots, seq, _ = grad_q.shape
    rows, width = tokens.shape
    block = min(512, seq)
    per_slot = seq // block
    cols = 3 * HD
    head = pl.BlockSpec((block, HD), lambda i: (i, 0))
    table = pl.BlockSpec((block, 2 * HD), lambda i: (i % per_slot, 0))
    chips = block // (2 * part)
    shard = width // n_group
    flat = [t.reshape(rows, HD) for t in (grad_q, grad_k, grad_v)]
    return pl.pallas_call(
        partial(join_kernel, part=part),
        grid=(rows // block,),
        in_specs=[
            head, head, head, pl.BlockSpec((block, width), lambda i: (i, 0)), table, table,
        ],
        out_specs=[
            pl.BlockSpec(
                (chips, 2, 1, part // 2, 2 * cols), lambda i: (i % per_slot, 0, i // per_slot, 0, 0)
            ),
            pl.BlockSpec((n_group, shard + 16, cols), lambda i: (0, 0, 0)),
        ],
        out_shape=[
            jax.ShapeDtypeStruct((seq // (2 * part), 2, slots, part // 2, 2 * cols), BF16),
            jax.ShapeDtypeStruct((n_group, shard + 16, cols), BF16),
        ],
        scratch_shapes=[pltpu.VMEM((cols, width), F32), pltpu.VMEM((1, cols), F32)],
        compiler_params=pltpu.CompilerParams(vmem_limit_bytes=VMEM_LIMIT),
        cost_estimate=pl.CostEstimate(
            flops=2 * rows * width * cols, bytes_accessed=2 * rows * width, transcendentals=0
        ),
        name="join_grads",
    )(*flat, tokens, cosine, sine)


def norm_forward(values, gain, shift):
    center = values - jnp.mean(values, axis=-1, keepdims=True)
    spread = jnp.mean(center * center, axis=-1, keepdims=True)
    root = lax.rsqrt(spread + LN_EPS)
    unit = center * root
    return unit * gain + shift, unit, root


def norm_backward(grad, unit, root, gain):
    scaled = grad * gain
    inner = scaled - jnp.mean(scaled, axis=-1, keepdims=True)
    inner = inner - unit * jnp.mean(scaled * unit, axis=-1, keepdims=True)
    return root * inner, jnp.sum(grad * unit, axis=0), jnp.sum(grad, axis=0)


def gelu_pair(values):
    half = 0.5 + 0.5 * lax.erf(values * 0.7071067811865476)
    bell = jnp.exp(-0.5 * values * values) * 0.3989422804014327
    return values * half, half + values * bell


def rope_rows(positions):
    halfway = HD // 2
    ladder = jnp.arange(halfway, dtype=F32) * (2.0 / HD)
    frequency = jnp.power(jnp.float32(10000.0), -ladder)
    angles = positions[:, None] * frequency[None, :]
    return jnp.cos(angles), jnp.sin(angles)


def head_device(
    tokens,
    lengths,
    w_qkv,
    b_qkv,
    w_out,
    b_out,
    ln1_gain,
    ln1_bias,
    w_up,
    b_up,
    w_down,
    b_down,
    ln2_gain,
    ln2_bias,
    w_proj,
    cot_out,
    cot_emb,
):
    n_lane = lax.axis_size("ctx") * lax.axis_size("x")
    n_group = 2 * n_lane
    core = lax.axis_index("core")
    slot = lax.axis_index("slot")
    chip = lax.axis_index("ctx") * lax.axis_size("x") + lax.axis_index("x")
    me = 2 * chip + core
    slots, part, width = tokens.shape
    seq = part * n_group
    rows = slots * part
    shard = width // n_group
    ff_shard = w_down.shape[0]
    ff_half = ff_shard // 2
    proj = w_proj.shape[1]
    head_cols = 3 * HD

    small = jnp.concatenate(
        [b_qkv, b_out, ln1_gain, ln1_bias, b_up, b_down, ln2_gain, ln2_bias]
    )
    small_at = [0]
    for piece in (b_qkv, b_out, ln1_gain, ln1_bias, b_up, b_down, ln2_gain, ln2_bias):
        small_at.append(small_at[-1] + piece.shape[0])
    small_rows = -(-small.shape[0] // proj)
    small_rows = -(-small_rows // 16) * 16
    small = jnp.pad(small, (0, small_rows * proj - small.shape[0])).reshape(small_rows, proj)
    def two_lanes(mine, theirs):
        low_first = jnp.stack([mine, theirs], axis=0)
        high_first = jnp.stack([theirs, mine], axis=0)
        return jnp.where(core == 0, low_first, high_first)

    up_split = w_up.reshape(shard, n_lane, 2, 2, ff_half)
    up_mine = pick(up_split, core, 2)
    up_theirs = swap_core(pick(up_split, 1 - core, 2))
    up_chip = two_lanes(pick(up_mine, slot, 2), pick(up_theirs, slot, 2))
    down_split = w_down.reshape(2, ff_half, width)

    by_head = w_qkv.reshape(shard, 3, n_group, HD).transpose(2, 0, 1, 3)
    all_tokens, my_head, packed, out_lane, up, down = gather_start(
        tokens,
        by_head.reshape(n_group, shard, head_cols),
        jnp.concatenate([w_proj, small], axis=0),
        w_out,
        up_chip.reshape(2 * shard, n_lane * ff_half),
        pick(down_split, slot, 0),
    )
    proj_full = packed[:, :shard].reshape(width, proj)
    smalls = packed[:, shard:].reshape(n_group, small_rows * proj).astype(F32)
    qkv_bias, out_bias, gain_one, shift_one, up_bias, down_bias, gain_two, shift_two = (
        smalls[:, a:b].reshape(-1) for a, b in zip(small_at[:-1], small_at[1:])
    )

    my_head = my_head.reshape(width, 3, HD)
    all_tokens = all_tokens.reshape(slots * seq, width)

    def with_swapped(joined):
        first = joined[:, 0:2]
        halves = first.reshape(-1, 2, 2, HD // 2)
        swapped = jnp.stack([-halves[:, :, 1], halves[:, :, 0]], axis=2)
        return jnp.concatenate(
            [
                first.reshape(-1, 2 * HD),
                swapped.reshape(-1, 2 * HD),
                joined[:, 2],
            ],
            axis=1,
        )

    head_weight = with_swapped(my_head)
    head_bias = with_swapped(pick(qkv_bias.reshape(1, 3, n_group, HD), me, 2))
    cosine, sine = rope_rows(jnp.arange(seq, dtype=jnp.int32).astype(F32))
    cos_wide = jnp.tile(cosine, (1, 4))
    sin_wide = jnp.tile(sine, (1, 4))
    queries, keys, values = project(all_tokens, head_weight, head_bias, cos_wide, sin_wide)
    queries, keys, values = (t.reshape(slots, seq, HD) for t in (queries, keys, values))

    bias_lane = pick(up_bias.reshape(n_lane, 2, 2, ff_half), core, 1)
    up_bias_own = pick(bias_lane, slot, 1).reshape(-1)

    qkv_split = w_qkv.reshape(shard, 3, n_lane, 2, HD)
    qkv_mine = pick(qkv_split, core, 3)
    qkv_theirs = swap_core(pick(qkv_split, 1 - core, 3))
    qkv_chip = two_lanes(qkv_mine, qkv_theirs).transpose(3, 0, 1, 2, 4)
    qkv_chip = qkv_chip.reshape(n_lane, 2 * shard, head_cols)

    mixture, send, norms = attend(
        lengths, core.reshape(1).astype(jnp.int32), queries, keys, values, part
    )
    merged = lax.all_to_all(send, LANE, 0, 0, tiled=True)
    merged = merged.transpose(1, 2, 3, 0, 4).reshape(2 * rows, n_lane * HD)

    def own_sum(partial_rows):
        return partial_rows[:rows] + swap_core(partial_rows[rows:])

    def both(value):
        return jnp.concatenate([value, swap_core(value)], axis=0)

    def quad(value):
        pair = jnp.concatenate([value, swap_slot(value)], axis=0)
        return jnp.concatenate([pair, swap_core(pair)], axis=0)

    def quad_sum(partial_rows):
        pair = partial_rows[: 2 * rows] + swap_core(partial_rows[2 * rows :])
        return pair[:rows] + swap_slot(pair[rows:].astype(BF16)).astype(F32)

    flat_tokens = tokens.reshape(rows, width).astype(F32)
    attended = own_sum(mm(merged, out_lane)) + out_bias
    hidden_one, unit_one, root_one = norm_forward(flat_tokens + attended, gain_one, shift_one)
    hidden_low, qkv_chip = lax.optimization_barrier((hidden_one.astype(BF16), qkv_chip))
    qkv_lane = lax.all_gather(qkv_chip, LANE, axis=0, tiled=True)
    hidden_low = quad(hidden_low)

    active, slope = gelu_pair(mm(hidden_low, up) + up_bias_own)
    active = active.astype(BF16)
    downward = quad_sum(mm(active, down)) + down_bias
    out_rows, unit_two, root_two = norm_forward(hidden_one + downward, gain_two, shift_two)
    out_low = out_rows.astype(BF16)
    embeds = mm(out_low, proj_full).astype(BF16)

    place = me * part + jnp.arange(part, dtype=jnp.int32)
    live = (place[None, :] < lengths[:, None]).reshape(rows, 1)
    grad_out = jnp.where(live, cot_out.reshape(rows, width).astype(F32), 0.0)
    grad_emb = jnp.where(live, cot_emb.reshape(rows, proj), 0)
    d_proj = contract(out_low, grad_emb, 0, 0)
    grad_full = grad_out + contract(grad_emb, proj_full, 1, 1)
    grad_two, d_gain_two, d_shift_two = norm_backward(grad_full, unit_two, root_two, gain_two)
    grad_down_own = grad_two.astype(BF16)
    d_down_bias = jnp.sum(grad_down_own.astype(F32), axis=0)
    grad_down = quad(grad_down_own)
    grad_up = (contract(grad_down, down, 1, 1) * slope).astype(BF16)
    d_down = contract(active, grad_down, 0, 0).astype(BF16)
    d_up = contract(hidden_low, grad_up, 0, 0).astype(BF16)
    up_bias_own_grad = jnp.sum(grad_up.astype(F32), axis=0)
    grad_hidden = grad_two + quad_sum(contract(grad_up, up, 1, 1))
    grad_one, d_gain_one, d_shift_one = norm_backward(grad_hidden, unit_one, root_one, gain_one)
    grad_att_own = grad_one.astype(BF16)
    d_out_bias = jnp.sum(grad_att_own.astype(F32), axis=0)
    grad_att_own, qkv_lane = lax.optimization_barrier((grad_att_own, qkv_lane))
    grad_att = both(grad_att_own)
    grad_merged = contract(grad_att, out_lane, 1, 1).astype(BF16)
    grad_merged = grad_merged.reshape(2, slots, part, n_lane, HD).transpose(3, 0, 1, 2, 4)
    grad_heads = lax.all_to_all(grad_merged, LANE, 0, 0, tiled=True)

    def core_order(value):
        return jnp.where(core == 0, value, jnp.flip(value, axis=1))

    grad_heads = core_order(grad_heads).transpose(2, 0, 1, 3, 4).reshape(slots, seq, HD)

    d_out = contract(merged, grad_att, 0, 0).astype(BF16)

    red_down = lax.psum_scatter(d_down, LANE, scatter_dimension=0, tiled=True)
    x_at = lax.axis_index("x")
    up_rows = d_up.reshape(-1, 2, 2 * shard, width)
    out_rows_ = d_out.reshape(-1, 2, shard, width)
    keep_up, keep_out = pick(up_rows, x_at, 1), pick(out_rows_, x_at, 1)
    got_up, got_out = (
        lax.ppermute(pick(t, 1 - x_at, 1), "x", SWAP) for t in (up_rows, out_rows_)
    )

    spread = (
        (jnp.arange(2) == core)[:, None, None] & (jnp.arange(2) == slot)[None, :, None]
    ).astype(F32)
    up_bias_grad = up_bias_own_grad.reshape(n_lane, 1, 1, ff_half) * spread[None]
    vectors = (
        d_out_bias,
        d_gain_one,
        d_shift_one,
        up_bias_grad.reshape(-1),
        d_down_bias,
        d_gain_two,
        d_shift_two,
    )
    small_grad = jnp.concatenate([v.reshape(n_group, -1) for v in vectors], axis=1)
    small_cols = small_grad.shape[1]
    vec_rows = -(-small_cols // proj)
    vec_rows = -(-(shard + vec_rows) // 16) * 16 - shard
    small_grad = jnp.pad(small_grad, ((0, 0), (0, vec_rows * proj - small_cols)))
    small_grad = jnp.concatenate(
        [d_proj.reshape(n_group, shard, proj), small_grad.reshape(n_group, vec_rows, proj)], axis=1
    )
    row_dots = jnp.sum(grad_heads.astype(F32) * mixture, axis=-1).reshape(slots, 1, seq)
    grad_q, grad_k, grad_v = attend_back(
        lengths, queries, keys, values, grad_heads, norms, row_dots
    )

    joined, d_qkv = join_grads(
        grad_q, grad_k, grad_v, all_tokens, cos_wide, sin_wide, part, n_group
    )
    grad_w_down, grad_w_up, grad_w_out, small_sum, d_qkv, input_grad = finish_grads(
        keep_up,
        keep_out,
        got_up,
        got_out,
        small_grad.astype(BF16),
        d_qkv,
        red_down,
        joined,
        qkv_lane.reshape(n_lane, n_lane, 2 * shard, head_cols),
        grad_one,
    )
    grad_w_proj = small_sum[:shard]
    vec_sum = small_sum[shard:].reshape(-1)
    vec_outs = []
    at = 0
    for v in vectors:
        size = v.size // n_group
        vec_outs.append(vec_sum[at : at + size])
        at += size
    (
        grad_b_out,
        grad_gain_one,
        grad_shift_one,
        grad_b_up,
        grad_b_down,
        grad_gain_two,
        grad_shift_two,
    ) = vec_outs

    grad_w_qkv = (
        d_qkv[:, :shard].reshape(n_group, shard, 3, HD).transpose(1, 2, 0, 3).reshape(shard, 3 * width)
    )
    qkv_bias_grad = d_qkv[:, shard].reshape(n_group, 3, HD).transpose(1, 0, 2).reshape(-1)
    grad_b_qkv = lax.dynamic_slice(qkv_bias_grad, (me * b_qkv.shape[0],), (b_qkv.shape[0],))

    return (
        out_low.reshape(slots, part, width),
        embeds.reshape(slots, part, proj),
        input_grad.reshape(slots, part, width),
        grad_w_qkv,
        grad_b_qkv,
        grad_w_out,
        grad_b_out,
        grad_gain_one,
        grad_shift_one,
        grad_w_up,
        grad_b_up,
        grad_w_down,
        grad_b_down,
        grad_gain_two,
        grad_shift_two,
        grad_w_proj,
    )


def layer_norm(hidden, gain, shift):
    center = hidden - jnp.mean(hidden, axis=-1, keepdims=True)
    spread = jnp.mean(center * center, axis=-1, keepdims=True)
    return center * lax.rsqrt(spread + LN_EPS) * gain + shift


def rope_tables(positions, head_width):
    halfway = head_width // 2
    ladder = jnp.arange(halfway, dtype=jnp.float32) * (2.0 / head_width)
    frequency = jnp.power(jnp.float32(10000.0), -ladder)
    angles = positions[:, None] * frequency[None, :]
    return (jnp.cos(angles)[:, None, :], jnp.sin(angles)[:, None, :])


def rotate(values, cosine, sine_part):
    halfway = values.shape[-1] // 2
    first_half = values[..., :halfway]
    second_half = values[..., halfway:]
    return jnp.concatenate(
        [
            first_half * cosine - second_half * sine_part,
            second_half * cosine + first_half * sine_part,
        ],
        axis=-1,
    )


def block_scores(query_block, key_block, key_start, length, scale):
    scores = (
        jnp.einsum("qhd,khd->hqk", query_block, key_block, preferred_element_type=jnp.float32)
        * scale
    )
    key_ids = key_start + jnp.arange(key_block.shape[0], dtype=jnp.int32)
    return jnp.where((key_ids < length)[None, None, :], scores, NEG_FILL)


def per_device(
    tokens,
    lengths,
    w_qkv,
    b_qkv,
    w_out,
    b_out,
    ln1_gain,
    ln1_bias,
    w_up,
    b_up,
    w_down,
    b_down,
    ln2_gain,
    ln2_bias,
    w_proj,
    cot_out,
    cot_emb,
):
    n_fsdp = lax.axis_size("fsdp")
    n_ctx = lax.axis_size("ctx")
    ctx_at = lax.axis_index("ctx")
    fsdp_at = lax.axis_index("fsdp")
    groups, tok_slot, width = tokens.shape
    heads_here = H // n_fsdp
    lane_width = heads_here * HD
    span_rows = tok_slot * n_fsdp
    key_count = span_rows * n_ctx
    row_count = groups * tok_slot
    scale = HD ** (-0.5)
    query_rows = min(512, span_rows)
    key_rows = min(2048, key_count // 4)
    query_blocks = span_rows // query_rows
    key_blocks = key_count // key_rows
    key_starts = jnp.arange(key_blocks, dtype=jnp.int32) * key_rows
    qkv_full, qkv_bias, out_full, out_bias, gain_one, shift_one = (
        lax.all_gather(w_qkv, ("ctx", "fsdp"), axis=0, tiled=True),
        lax.all_gather(b_qkv, ("ctx", "fsdp"), axis=0, tiled=True),
        lax.all_gather(w_out, ("ctx", "fsdp"), axis=0, tiled=True),
        lax.all_gather(b_out, ("ctx", "fsdp"), axis=0, tiled=True),
        lax.all_gather(ln1_gain, ("ctx", "fsdp"), axis=0, tiled=True),
        lax.all_gather(ln1_bias, ("ctx", "fsdp"), axis=0, tiled=True),
    )
    token_pos = (ctx_at * n_fsdp + fsdp_at) * tok_slot + jnp.arange(tok_slot, dtype=jnp.int32)
    live_rows = (token_pos[None, :] < lengths[:, None]).reshape(row_count, 1)
    flat_tokens = tokens.reshape(row_count, width)
    joined = jnp.dot(flat_tokens, qkv_full, preferred_element_type=jnp.float32) + qkv_bias.astype(
        jnp.float32
    )
    cosine, sine_part = rope_tables(token_pos.astype(jnp.float32), HD)
    split_heads = joined.reshape(groups, tok_slot, 3, H, HD)
    rotated_query = rotate(split_heads[:, :, 0], cosine, sine_part)
    rotated_key = rotate(split_heads[:, :, 1], cosine, sine_part)
    packed = (
        jnp.stack([rotated_query, rotated_key, split_heads[:, :, 2]], axis=2)
        .astype(jnp.bfloat16)
        .reshape(groups, tok_slot, 3, n_fsdp, lane_width)
    )
    by_heads = lax.all_to_all(packed, "fsdp", split_axis=3, concat_axis=1, tiled=True)
    queries = by_heads[:, :, 0, 0]
    local_keys = by_heads[:, :, 1, 0]
    local_values = by_heads[:, :, 2, 0]
    all_keys, all_values = (
        lax.all_gather(local_keys, "ctx", axis=1, tiled=True),
        lax.all_gather(local_values, "ctx", axis=1, tiled=True),
    )

    def attend_slot(slot_item):
        slot_queries, slot_keys, slot_values, length = slot_item
        query_split = slot_queries.reshape(query_blocks, query_rows, heads_here, HD)
        key_split = slot_keys.reshape(key_blocks, key_rows, heads_here, HD)
        value_split = slot_values.reshape(key_blocks, key_rows, heads_here, HD)

        def per_query(query_block):

            def row_stats(state_pair, key_item):
                highest, running_sum = state_pair
                scores = block_scores(query_block, key_item[0], key_item[1], length, scale)
                new_high = jnp.maximum(highest, jnp.max(scores, axis=-1))
                running_sum = running_sum * jnp.exp(highest - new_high) + jnp.sum(
                    jnp.exp(scores - new_high[..., None]), axis=-1
                )
                return ((new_high, running_sum), None)

            start_state = (
                jnp.full((heads_here, query_rows), NEG_FILL, jnp.float32),
                jnp.zeros((heads_here, query_rows), jnp.float32),
            )
            highest, running_sum = lax.scan(row_stats, start_state, (key_split, key_starts))[0]
            log_norm = highest + jnp.log(running_sum)

            def weigh_values(accumulated, key_item):
                scores = block_scores(query_block, key_item[0], key_item[2], length, scale)
                weights = jnp.exp(scores - log_norm[..., None]).astype(jnp.bfloat16)
                return (
                    accumulated
                    + jnp.einsum(
                        "hqk,khd->qhd", weights, key_item[1], preferred_element_type=jnp.float32
                    ),
                    None,
                )

            mixture = lax.scan(
                weigh_values,
                jnp.zeros((query_rows, heads_here, HD), jnp.float32),
                (key_split, value_split, key_starts),
            )[0]
            return (mixture, log_norm)

        mixture, log_norm = lax.map(per_query, query_split)
        return (mixture.reshape(span_rows, lane_width), log_norm)

    mixture, log_norms = lax.map(attend_slot, (queries, all_keys, all_values, lengths))
    merged = lax.all_to_all(
        mixture.astype(jnp.bfloat16).reshape(groups, span_rows, 1, lane_width),
        "fsdp",
        split_axis=1,
        concat_axis=2,
        tiled=True,
    ).reshape(row_count, width)
    attended = jnp.dot(merged, out_full, preferred_element_type=jnp.float32) + out_bias.astype(
        jnp.float32
    )
    hidden_one, pull_one = jax.vjp(
        layer_norm,
        flat_tokens.astype(jnp.float32) + attended,
        gain_one.astype(jnp.float32),
        shift_one.astype(jnp.float32),
    )
    hidden_low = hidden_one.astype(jnp.bfloat16)
    up_full, up_bias, down_full, down_bias, gain_two, shift_two, proj_full = (
        lax.all_gather(w_up, ("ctx", "fsdp"), axis=0, tiled=True),
        lax.all_gather(b_up, ("ctx", "fsdp"), axis=0, tiled=True),
        lax.all_gather(w_down, ("ctx", "fsdp"), axis=0, tiled=True),
        lax.all_gather(b_down, ("ctx", "fsdp"), axis=0, tiled=True),
        lax.all_gather(ln2_gain, ("ctx", "fsdp"), axis=0, tiled=True),
        lax.all_gather(ln2_bias, ("ctx", "fsdp"), axis=0, tiled=True),
        lax.all_gather(w_proj, ("ctx", "fsdp"), axis=0, tiled=True),
    )
    upward = jnp.dot(hidden_low, up_full, preferred_element_type=jnp.float32) + up_bias.astype(
        jnp.float32
    )
    active_full, pull_gelu = jax.vjp(partial(jax.nn.gelu, approximate=False), upward)
    active = active_full.astype(jnp.bfloat16)
    downward = jnp.dot(active, down_full, preferred_element_type=jnp.float32) + down_bias.astype(
        jnp.float32
    )
    out_full_rows, pull_two = jax.vjp(
        layer_norm,
        hidden_one + downward,
        gain_two.astype(jnp.float32),
        shift_two.astype(jnp.float32),
    )
    out_low = out_full_rows.astype(jnp.bfloat16)
    projected = jnp.dot(out_low, proj_full, preferred_element_type=jnp.float32)
    back_qkv, back_qkv_bias, back_out, back_out_bias, back_gain_one, back_shift_one = (
        lax.all_gather(w_qkv, ("ctx", "fsdp"), axis=0, tiled=True),
        lax.all_gather(b_qkv, ("ctx", "fsdp"), axis=0, tiled=True),
        lax.all_gather(w_out, ("ctx", "fsdp"), axis=0, tiled=True),
        lax.all_gather(b_out, ("ctx", "fsdp"), axis=0, tiled=True),
        lax.all_gather(ln1_gain, ("ctx", "fsdp"), axis=0, tiled=True),
        lax.all_gather(ln1_bias, ("ctx", "fsdp"), axis=0, tiled=True),
    )
    back_up, back_up_bias, back_down, back_down_bias, back_gain_two, back_shift_two, back_proj = (
        lax.all_gather(w_up, ("ctx", "fsdp"), axis=0, tiled=True),
        lax.all_gather(b_up, ("ctx", "fsdp"), axis=0, tiled=True),
        lax.all_gather(w_down, ("ctx", "fsdp"), axis=0, tiled=True),
        lax.all_gather(b_down, ("ctx", "fsdp"), axis=0, tiled=True),
        lax.all_gather(ln2_gain, ("ctx", "fsdp"), axis=0, tiled=True),
        lax.all_gather(ln2_bias, ("ctx", "fsdp"), axis=0, tiled=True),
        lax.all_gather(w_proj, ("ctx", "fsdp"), axis=0, tiled=True),
    )
    grad_out = jnp.where(live_rows, cot_out.reshape(row_count, width).astype(jnp.float32), 0.0)
    grad_emb = jnp.where(live_rows, cot_emb.reshape(row_count, -1), 0)
    d_proj = jnp.einsum("rd,rp->dp", out_low, grad_emb, preferred_element_type=jnp.float32)
    grad_full = grad_out + jnp.einsum(
        "rp,dp->rd", grad_emb, back_proj, preferred_element_type=jnp.float32
    )
    grad_two, d_gain_two, d_shift_two = pull_two(grad_full)
    grad_down = grad_two.astype(jnp.bfloat16)
    d_down = jnp.einsum("rf,rd->fd", active, grad_down, preferred_element_type=jnp.float32)
    d_down_bias = jnp.sum(grad_down.astype(jnp.float32), axis=0)
    grad_act = jnp.einsum("rd,fd->rf", grad_down, back_down, preferred_element_type=jnp.float32)
    grad_up = pull_gelu(grad_act)[0].astype(jnp.bfloat16)
    d_up = jnp.einsum("rd,rf->df", hidden_low, grad_up, preferred_element_type=jnp.float32)
    d_up_bias = jnp.sum(grad_up.astype(jnp.float32), axis=0)
    grad_hidden = grad_two + jnp.einsum(
        "rf,df->rd", grad_up, back_up, preferred_element_type=jnp.float32
    )
    grad_one, d_gain_one, d_shift_one = pull_one(grad_hidden)
    grad_att = grad_one.astype(jnp.bfloat16)
    d_out = jnp.einsum("rd,re->de", merged, grad_att, preferred_element_type=jnp.float32)
    d_out_bias = jnp.sum(grad_att.astype(jnp.float32), axis=0)
    grad_merged = jnp.einsum(
        "re,de->rd", grad_att, back_out, preferred_element_type=jnp.float32
    ).astype(jnp.bfloat16)
    grad_heads = lax.all_to_all(
        grad_merged.reshape(groups, tok_slot, n_fsdp, lane_width),
        "fsdp",
        split_axis=2,
        concat_axis=1,
        tiled=True,
    ).reshape(groups, span_rows, lane_width)

    def attend_back(slot_item):
        slot_queries, slot_keys, slot_values, grad_mix, log_norm, length = slot_item
        query_split = slot_queries.reshape(query_blocks, query_rows, heads_here, HD)
        key_split = slot_keys.reshape(key_blocks, key_rows, heads_here, HD)
        value_split = slot_values.reshape(key_blocks, key_rows, heads_here, HD)
        grad_split = grad_mix.reshape(query_blocks, query_rows, heads_here, HD)

        def value_pass(value_total, query_item):
            query_block, grad_block, norm_block = query_item

            def value_per_key(row_dot, key_item):
                key_block, value_block, key_start = key_item
                scores = block_scores(query_block, key_block, key_start, length, scale)
                probability = jnp.exp(scores - norm_block[..., None])
                grad_probs = jnp.einsum(
                    "qhd,khd->hqk", grad_block, value_block, preferred_element_type=jnp.float32
                )
                value_part = jnp.einsum(
                    "hqk,qhd->khd",
                    probability.astype(jnp.bfloat16),
                    grad_block,
                    preferred_element_type=jnp.float32,
                )
                return (row_dot + jnp.sum(probability * grad_probs, axis=-1), value_part)

            row_dot, value_parts = lax.scan(
                value_per_key,
                jnp.zeros((heads_here, query_rows), jnp.float32),
                (key_split, value_split, key_starts),
            )
            return (value_total + value_parts.reshape(key_count, heads_here, HD), row_dot)

        value_grad, row_dots = lax.scan(
            value_pass,
            jnp.zeros((key_count, heads_here, HD), jnp.float32),
            (query_split, grad_split, log_norm),
        )

        def key_pass(key_total, query_item):
            query_block, grad_block, norm_block, dot_block = query_item

            def key_per_key(query_accum, key_item):
                key_block, value_block, key_start = key_item
                scores = block_scores(query_block, key_block, key_start, length, scale)
                probability = jnp.exp(scores - norm_block[..., None])
                grad_probs = jnp.einsum(
                    "qhd,khd->hqk", grad_block, value_block, preferred_element_type=jnp.float32
                )
                grad_scores = (probability * (grad_probs - dot_block[..., None])).astype(
                    jnp.bfloat16
                )
                query_accum = query_accum + jnp.einsum(
                    "hqk,khd->qhd", grad_scores, key_block, preferred_element_type=jnp.float32
                )
                key_part = jnp.einsum(
                    "hqk,qhd->khd", grad_scores, query_block, preferred_element_type=jnp.float32
                )
                return (query_accum, key_part)

            query_grad, key_parts = lax.scan(
                key_per_key,
                jnp.zeros((query_rows, heads_here, HD), jnp.float32),
                (key_split, value_split, key_starts),
            )
            return (key_total + key_parts.reshape(key_count, heads_here, HD), query_grad)

        key_grad, query_grads = lax.scan(
            key_pass,
            jnp.zeros((key_count, heads_here, HD), jnp.float32),
            (query_split, grad_split, log_norm, row_dots),
        )
        return (
            query_grads.reshape(span_rows, lane_width) * scale,
            key_grad.reshape(key_count, lane_width) * scale,
            value_grad.reshape(key_count, lane_width),
        )

    grad_queries, key_terms, value_terms = lax.map(
        attend_back, (queries, all_keys, all_values, grad_heads, log_norms, lengths)
    )
    grad_keys, grad_values = (
        lax.psum_scatter(
            key_terms.astype(jnp.bfloat16), "ctx", scatter_dimension=1, tiled=True
        ).astype(jnp.float32),
        lax.psum_scatter(
            value_terms.astype(jnp.bfloat16), "ctx", scatter_dimension=1, tiled=True
        ).astype(jnp.float32),
    )
    head_pos = (ctx_at * span_rows + jnp.arange(span_rows, dtype=jnp.int32)).astype(jnp.float32)
    head_cosine, head_sine = rope_tables(head_pos, HD)
    query_back = rotate(
        grad_queries.reshape(groups, span_rows, heads_here, HD), head_cosine, -head_sine
    )
    key_back = rotate(grad_keys.reshape(groups, span_rows, heads_here, HD), head_cosine, -head_sine)
    value_back = grad_values.reshape(groups, span_rows, heads_here, HD)
    grad_pack = (
        jnp.stack([query_back, key_back, value_back], axis=2)
        .astype(jnp.bfloat16)
        .reshape(groups, span_rows, 3, 1, lane_width)
    )
    grad_joined = lax.all_to_all(
        grad_pack, "fsdp", split_axis=1, concat_axis=3, tiled=True
    ).reshape(row_count, 3 * width)
    d_qkv = jnp.einsum("rd,re->de", flat_tokens, grad_joined, preferred_element_type=jnp.float32)
    d_qkv_bias = jnp.sum(grad_joined.astype(jnp.float32), axis=0)
    input_grad = (
        jnp.einsum("re,de->rd", grad_joined, back_qkv, preferred_element_type=jnp.float32)
        + grad_one
    ).astype(jnp.bfloat16)
    shards = (
        lax.psum_scatter(d_qkv, ("ctx", "fsdp"), scatter_dimension=0, tiled=True),
        lax.psum_scatter(d_qkv_bias, ("ctx", "fsdp"), scatter_dimension=0, tiled=True),
        lax.psum_scatter(d_out, ("ctx", "fsdp"), scatter_dimension=0, tiled=True),
        lax.psum_scatter(d_out_bias, ("ctx", "fsdp"), scatter_dimension=0, tiled=True),
        lax.psum_scatter(d_gain_one, ("ctx", "fsdp"), scatter_dimension=0, tiled=True),
        lax.psum_scatter(d_shift_one, ("ctx", "fsdp"), scatter_dimension=0, tiled=True),
        lax.psum_scatter(d_up, ("ctx", "fsdp"), scatter_dimension=0, tiled=True),
        lax.psum_scatter(d_up_bias, ("ctx", "fsdp"), scatter_dimension=0, tiled=True),
        lax.psum_scatter(d_down, ("ctx", "fsdp"), scatter_dimension=0, tiled=True),
        lax.psum_scatter(d_down_bias, ("ctx", "fsdp"), scatter_dimension=0, tiled=True),
        lax.psum_scatter(d_gain_two, ("ctx", "fsdp"), scatter_dimension=0, tiled=True),
        lax.psum_scatter(d_shift_two, ("ctx", "fsdp"), scatter_dimension=0, tiled=True),
        lax.psum_scatter(d_proj, ("ctx", "fsdp"), scatter_dimension=0, tiled=True),
    )
    totals = (
        lax.psum(shards[0].astype(jnp.bfloat16), "slot").astype(jnp.float32),
        lax.psum(shards[1].astype(jnp.bfloat16), "slot").astype(jnp.float32),
        lax.psum(shards[2].astype(jnp.bfloat16), "slot").astype(jnp.float32),
        lax.psum(shards[3].astype(jnp.bfloat16), "slot").astype(jnp.float32),
        lax.psum(shards[4].astype(jnp.bfloat16), "slot").astype(jnp.float32),
        lax.psum(shards[5].astype(jnp.bfloat16), "slot").astype(jnp.float32),
        lax.psum(shards[6].astype(jnp.bfloat16), "slot").astype(jnp.float32),
        lax.psum(shards[7].astype(jnp.bfloat16), "slot").astype(jnp.float32),
        lax.psum(shards[8].astype(jnp.bfloat16), "slot").astype(jnp.float32),
        lax.psum(shards[9].astype(jnp.bfloat16), "slot").astype(jnp.float32),
        lax.psum(shards[10].astype(jnp.bfloat16), "slot").astype(jnp.float32),
        lax.psum(shards[11].astype(jnp.bfloat16), "slot").astype(jnp.float32),
        lax.psum(shards[12].astype(jnp.bfloat16), "slot").astype(jnp.float32),
    )
    return (
        out_low.reshape(groups, tok_slot, width),
        projected.astype(jnp.bfloat16).reshape(groups, tok_slot, -1),
        input_grad.reshape(groups, tok_slot, width),
        totals[0],
        totals[1],
        totals[2],
        totals[3],
        totals[4],
        totals[5],
        totals[6],
        totals[7],
        totals[8],
        totals[9],
        totals[10],
        totals[11],
        totals[12],
    )


def solution(mesh):
    n_slot, n_ctx, n_fsdp = (mesh.shape[a] for a in ("slot", "ctx", "fsdp"))
    rows_axes = ("ctx", "fsdp")
    step = per_device
    if n_slot == 2 and n_fsdp % 2 == 0 and n_ctx * n_fsdp == H:
        mesh = Mesh(
            mesh.devices.reshape(n_slot, n_ctx, n_fsdp // 2, 2), ("slot", "ctx", "x", "core")
        )
        rows_axes = GROUP
        step = head_device
    in_specs = (
        P("slot", rows_axes, None),
        P("slot"),
        P(rows_axes, None),
        P(rows_axes),
        P(rows_axes, None),
        P(rows_axes),
        P(rows_axes),
        P(rows_axes),
        P(rows_axes, None),
        P(rows_axes),
        P(rows_axes, None),
        P(rows_axes),
        P(rows_axes),
        P(rows_axes),
        P(rows_axes, None),
        P("slot", rows_axes, None),
        P("slot", rows_axes, None),
    )
    out_specs = (
        P("slot", rows_axes, None),
        P("slot", rows_axes, None),
        P("slot", rows_axes, None),
        P(rows_axes, None),
        P(rows_axes),
        P(rows_axes, None),
        P(rows_axes),
        P(rows_axes),
        P(rows_axes),
        P(rows_axes, None),
        P(rows_axes),
        P(rows_axes, None),
        P(rows_axes),
        P(rows_axes),
        P(rows_axes),
        P(rows_axes, None),
    )
    return jax.shard_map(
        step, mesh=mesh, in_specs=in_specs, out_specs=out_specs, check_vma=False
    )
```

```python
from functools import partial

import jax
import jax.numpy as jnp
from jax import lax
from jax.experimental import pallas as pl
from jax.experimental.pallas import tpu as pltpu
from jax.sharding import Mesh
from jax.sharding import PartitionSpec as P

H = 16
HD = 64
LN_EPS = 1e-05
NEG_FILL = -1e30
F32 = jnp.float32
BF16 = jnp.bfloat16
GROUP = ("ctx", "x", "core")
LANE = ("ctx", "x")
SWAP = [(0, 1), (1, 0)]
VMEM_LIMIT = 60 * 1024 * 1024


def mm(left, right):
    return jnp.dot(left, right, preferred_element_type=F32)


def contract(left, right, left_dim, right_dim):
    return lax.dot_general(
        left, right, (((left_dim,), (right_dim,)), ((), ())), preferred_element_type=F32
    )


def swap_core(value):
    return lax.ppermute(value, "core", SWAP)


def swap_slot(value):
    return lax.ppermute(value, "slot", SWAP)


def pick(stacked, index, axis):
    return lax.dynamic_index_in_dim(stacked, index, axis, keepdims=False)


MESH = pl.DeviceIdType.MESH


def at_device(**where):
    names = ("slot", "ctx", "x", "core")
    return tuple(where[n] if n in where else lax.axis_index(n) for n in names)


def greet(peers):
    barrier = pltpu.get_barrier_semaphore()
    for peer in peers:
        pl.semaphore_signal(barrier, inc=1, device_id=peer, device_id_type=MESH)
    pl.semaphore_wait(barrier, len(peers))


def group_peers(n_ctx, n_x):
    ctx, x, core = (lax.axis_index(n) for n in GROUP)
    peers = []
    for dz in range(n_ctx):
        for dx in range(n_x):
            for dc in range(2):
                if dz or dx or dc:
                    where = (lax.rem(ctx + dz, n_ctx), lax.rem(x + dx, n_x), lax.rem(core + dc, 2))
                    peers.append(where)
    return peers


def start_kernel(
    tok_ref, head_ref, small_ref, all_ref, heads_ref, smalls_ref,
    far_send, block_send, local_sem, head_recv, small_recv, block_recv, *, n_ctx, n_x
):
    part = tok_ref.shape[1]
    ctx, x, core = (lax.axis_index(n) for n in GROUP)
    me = (ctx * n_x + x) * 2 + core
    peers = group_peers(n_ctx, n_x)
    greet([at_device(ctx=z, x=a, core=c) for z, a, c in peers])

    def block_at(b):
        return all_ref.at[:, pl.ds(pl.multiple_of(b * part, part), part), :]

    pushes = []
    for k, (z, a, c) in enumerate(peers):
        them = (z * n_x + a) * 2 + c
        target = at_device(ctx=z, x=a, core=c)
        pushes.append(pltpu.make_async_remote_copy(
            head_ref.at[them], heads_ref.at[me], far_send.at[2 * k], head_recv.at[me],
            device_id=target, device_id_type=MESH))
        pushes.append(pltpu.make_async_remote_copy(
            small_ref, smalls_ref.at[me], far_send.at[2 * k + 1], small_recv.at[me],
            device_id=target, device_id_type=MESH))
    locals_ = [
        pltpu.make_async_copy(tok_ref, block_at(me), local_sem.at[0]),
        pltpu.make_async_copy(head_ref.at[me], heads_ref.at[me], local_sem.at[1]),
        pltpu.make_async_copy(small_ref, smalls_ref.at[me], local_sem.at[2]),
    ]

    def send(b, source, lane, target):
        return pltpu.make_async_remote_copy(
            source, block_at(b), block_send.at[lane, b], block_recv.at[b],
            device_id=target, device_id_type=MESH)

    up = at_device(ctx=lax.rem(ctx + 1, n_ctx))
    down = at_device(ctx=lax.rem(ctx + n_ctx - 1, n_ctx))
    side = at_device(x=1 - x)
    twin = at_device(core=1 - core)

    def here(b):
        return send(b, block_at(b), 0, twin)

    @pl.when(ctx + 1 < n_ctx)
    def _():
        send(me, tok_ref, 0, up).start()

    @pl.when(ctx > 0)
    def _():
        send(me, tok_ref, 1, down).start()

    send(me, tok_ref, 2, side).start()
    for push in pushes:
        push.start()
    send(me, tok_ref, 3, twin).start()
    for copy in locals_:
        copy.start()

    for r in range(1, n_ctx):
        low = ctx - r
        high = ctx + r

        @pl.when(low >= 0)
        def _():
            b = (low * n_x + x) * 2 + core
            here(b).wait_recv()

            @pl.when(ctx + 1 < n_ctx)
            def _():
                send(b, block_at(b), 0, up).start()

            send(b, block_at(b), 2, side).start()
            send(b, block_at(b), 3, twin).start()

        @pl.when(high < n_ctx)
        def _():
            b = (high * n_x + x) * 2 + core
            here(b).wait_recv()

            @pl.when(ctx > 0)
            def _():
                send(b, block_at(b), 1, down).start()

            send(b, block_at(b), 2, side).start()
            send(b, block_at(b), 3, twin).start()

    def from_side(z):
        b = (z * n_x + (1 - x)) * 2 + core
        here(b).wait_recv()
        send(b, block_at(b), 3, twin).start()

    from_side(ctx)
    for r in range(1, n_ctx):
        @pl.when(ctx - r >= 0)
        def _():
            from_side(ctx - r)

        @pl.when(ctx + r < n_ctx)
        def _():
            from_side(ctx + r)

    for z in range(n_ctx):
        for a in range(n_x):
            here((z * n_x + a) * 2 + 1 - core).wait_recv()
    for k, (z, a, c) in enumerate(peers):
        them = (z * n_x + a) * 2 + c
        pltpu.make_async_remote_copy(
            head_ref.at[them], heads_ref.at[them], far_send.at[2 * k], head_recv.at[them],
            device_id=twin, device_id_type=MESH).wait_recv()
        pltpu.make_async_remote_copy(
            small_ref, smalls_ref.at[them], far_send.at[2 * k + 1], small_recv.at[them],
            device_id=twin, device_id_type=MESH).wait_recv()
    for push in pushes:
        push.wait_send()
    for copy in locals_:
        copy.wait()

    for z in range(n_ctx):
        b = (z * n_x + x) * 2 + core

        @pl.when((z <= ctx) & (ctx + 1 < n_ctx))
        def _():
            send(b, block_at(b), 0, up).wait_send()

        @pl.when((z >= ctx) & (ctx > 0))
        def _():
            send(b, block_at(b), 1, down).wait_send()

        send(b, block_at(b), 2, side).wait_send()
        send(b, block_at(b), 3, twin).wait_send()
        other = (z * n_x + (1 - x)) * 2 + core
        send(other, block_at(other), 3, twin).wait_send()


def gather_start(tokens, heads, small):
    n_ctx, n_x = lax.axis_size("ctx"), lax.axis_size("x")
    n = 2 * n_ctx * n_x
    slots, part, width = tokens.shape
    vmem = pl.BlockSpec(memory_space=pltpu.VMEM)
    anywhere = pl.BlockSpec(memory_space=pl.ANY)
    dma = pltpu.SemaphoreType.DMA
    return pl.pallas_call(
        partial(start_kernel, n_ctx=n_ctx, n_x=n_x),
        in_specs=[vmem, vmem, vmem],
        out_specs=[anywhere, vmem, vmem],
        out_shape=[
            jax.ShapeDtypeStruct((slots, n * part, width), tokens.dtype),
            jax.ShapeDtypeStruct(heads.shape, heads.dtype),
            jax.ShapeDtypeStruct((n,) + small.shape, small.dtype),
        ],
        scratch_shapes=[
            dma((2 * (n - 1),)), dma((4, n)), dma((3,)), dma((n,)), dma((n,)), dma((n,))
        ],
        compiler_params=pltpu.CompilerParams(
            collective_id=1, has_side_effects=True, vmem_limit_bytes=VMEM_LIMIT
        ),
        cost_estimate=pl.CostEstimate(
            flops=0, bytes_accessed=2 * n * tokens.size, transcendentals=0
        ),
        name="gather_start",
    )(tokens, heads, small)


def finish_kernel(
    out_ref, x_out, small_ref, qkv_ref, red_ref, join_ref, weight_ref, one_ref,
    g_down, g_up, g_out, g_small, g_qkv, g_in,
    s_out, z_out, own_out, smalls, own_small, pair_small, pair_qkv, sum_qkv, qkvs,
    pair_down, pair_out, last_up, joins, partial_in, pair_in,
    join_send, join_recv, far_send, small_recv, qkv_recv, z_send, z_recv, y_send, y_recv,
    *, n_ctx, n_x
):
    ctx, x, core = (lax.axis_index(n) for n in GROUP)
    slot = lax.axis_index("slot")
    chip = ctx * n_x + x
    me = 2 * chip + core
    shard = g_up.shape[0]
    part = g_down.shape[0] // 2
    peers = group_peers(n_ctx, n_x)
    lane_peers = [(z, a) for z, a, c in peers[1::2]]
    across = at_device(slot=1 - slot)
    corner = at_device(slot=1 - slot, core=1 - core)
    twin = at_device(core=1 - core)
    greet([at_device(ctx=z, x=a, core=c) for z, a, c in peers] + [across, corner])

    def remote(source, target_ref, send_sem, recv_sem, target):
        return pltpu.make_async_remote_copy(
            source, target_ref, send_sem, recv_sem, device_id=target, device_id_type=MESH)

    started = []

    def launch(copy):
        copy.start()
        started.append(copy)
        return copy

    def pair_copy(i, source, target_ref, target):
        return launch(remote(source, target_ref, y_send.at[i], y_recv.at[i], target))

    qkv_copy = pair_copy(0, qkv_ref, pair_qkv, across)
    mine = pl.multiple_of(part + core * shard, shard)
    theirs = pl.multiple_of(part + (1 - core) * shard, shard)
    for k, (z, a, c) in enumerate(peers):
        them = (z * n_x + a) * 2 + c
        launch(remote(
            small_ref.at[them], smalls.at[me], far_send.at[2 * k + 1], small_recv.at[me],
            at_device(ctx=z, x=a, core=c)))
    smalls[me] = small_ref[me]
    for k, (z, a) in enumerate(lane_peers):
        launch(remote(
            join_ref.at[z * n_x + a], joins.at[chip], join_send.at[k], join_recv.at[chip],
            at_device(ctx=z, x=a)))
    down_copy = pair_copy(1, red_ref.at[pl.ds(0, part)], pair_down, across)
    quarter_copies = [
        pair_copy(2, red_ref.at[pl.ds(theirs, shard)], last_up.at[0], twin),
        pair_copy(3, red_ref.at[pl.ds(mine, shard)], last_up.at[1], across),
        pair_copy(4, red_ref.at[pl.ds(theirs, shard)], last_up.at[2], corner),
    ]

    second_out = []
    for j in range(n_ctx):
        place = lax.rem(ctx + 1 + j, n_ctx)
        sum_out = out_ref[place].astype(F32) + x_out[place].astype(F32)
        if j < n_ctx - 1:
            s_out[j] = sum_out.astype(BF16)
            second_out.append(launch(remote(
                s_out.at[j], z_out.at[j], z_send.at[j], z_recv.at[j], at_device(ctx=place))))
        else:
            own_out[...] = sum_out

    qkv_copy.wait_recv()
    sum_qkv[...] = (qkv_ref[...].astype(F32) + pair_qkv[...].astype(F32)).astype(BF16)
    for k, (z, a, c) in enumerate(peers):
        them = (z * n_x + a) * 2 + c
        launch(remote(
            sum_qkv.at[them], qkvs.at[me], far_send.at[2 * k], qkv_recv.at[me],
            at_device(ctx=z, x=a, core=c)))
    g_qkv[me] = sum_qkv[me].astype(F32)

    def add_head(source, rows_of, first):
        weight = jnp.concatenate(
            [weight_ref[b, source] for b in range(weight_ref.shape[0])], axis=0)
        for h in range(2):
            owner = core if h == 0 else 1 - core
            rows = rows_of(owner)
            cols = rows.shape[2] // 2
            rows = jnp.concatenate(
                [r for t in range(rows.shape[0]) for r in (rows[t, :, :cols], rows[t, :, cols:])],
                axis=0)
            term = contract(rows, weight, 1, 1)
            partial_in[h] = term if first else partial_in[h] + term

    add_head(chip, lambda owner: join_ref[chip, owner], True)

    half = pl.multiple_of(slot * part, part)
    other_half = pl.multiple_of((1 - slot) * part, part)
    g_down[pl.ds(half, part), :] = red_ref[pl.ds(0, part), :].astype(F32)
    down_copy.wait_recv()
    g_down[pl.ds(other_half, part), :] = pair_down[...].astype(F32)

    def place_quarter(rows, quarter_core, quarter_slot):
        for k in range(n_ctx * n_x):
            at = pl.multiple_of(((2 * k + quarter_core) * 2 + quarter_slot) * part, part)
            g_up[:, pl.ds(at, part)] = rows[:, k * part : (k + 1) * part].astype(F32)

    place_quarter(red_ref[pl.ds(mine, shard), :], core, slot)
    quarter_copies[0].wait_recv()
    place_quarter(last_up[0], 1 - core, slot)
    quarter_copies[1].wait_recv()
    place_quarter(last_up[1], core, 1 - slot)
    quarter_copies[2].wait_recv()
    place_quarter(last_up[2], 1 - core, 1 - slot)

    for z, a, c in peers:
        them = (z * n_x + a) * 2 + c
        remote(
            small_ref.at[them], smalls.at[them], far_send.at[1], small_recv.at[them], twin
        ).wait_recv()
    own_small[...] = jnp.sum(smalls[...].astype(F32), axis=0).astype(BF16)
    small_copy = pair_copy(5, own_small, pair_small, across)

    for k, (z, a) in enumerate(lane_peers):
        source = z * n_x + a
        remote(
            join_ref.at[source], joins.at[source], join_send.at[k], join_recv.at[source], twin
        ).wait_recv()
        add_head(source, lambda owner: joins[source, owner], False)
    in_copy = pair_copy(6, partial_in.at[1], pair_in, twin)

    for j in range(n_ctx - 1):
        second_out[j].wait_recv()
        own_out[...] += z_out[j].astype(F32)
    s_out[n_ctx - 1] = own_out[...].astype(BF16)
    out_copy = pair_copy(7, s_out.at[n_ctx - 1], pair_out, across)
    small_copy.wait_recv()
    g_small[...] = own_small[...].astype(F32) + pair_small[...].astype(F32)
    in_copy.wait_recv()
    g_in[...] = (partial_in[0] + pair_in[...] + one_ref[...]).astype(BF16)
    for z, a, c in peers:
        them = (z * n_x + a) * 2 + c
        remote(
            sum_qkv.at[them], qkvs.at[them], far_send.at[0], qkv_recv.at[them], twin
        ).wait_recv()
        g_qkv[them] = qkvs[them].astype(F32)
    out_copy.wait_recv()
    g_out[...] = s_out[n_ctx - 1].astype(F32) + pair_out[...].astype(F32)
    for copy in started:
        copy.wait_send()


def finish_grads(out, x_out, small, qkv, reduced, joined, weight, grad_one):
    n_ctx, n_x = lax.axis_size("ctx"), lax.axis_size("x")
    n = 2 * n_ctx * n_x
    width = reduced.shape[1]
    part = reduced.shape[0] // 2
    shard = out.shape[1]
    vmem = pl.BlockSpec(memory_space=pltpu.VMEM)
    dma = pltpu.SemaphoreType.DMA

    def low(*shape):
        return pltpu.VMEM(shape, BF16)

    def wide(*shape):
        return jax.ShapeDtypeStruct(shape, F32)

    return pl.pallas_call(
        partial(finish_kernel, n_ctx=n_ctx, n_x=n_x),
        in_specs=[vmem] * 8,
        out_specs=[vmem] * 6,
        out_shape=[
            wide(2 * part, width),
            wide(shard, 4 * width),
            wide(shard, width),
            wide(*small.shape[1:]),
            wide(*qkv.shape),
            jax.ShapeDtypeStruct(grad_one.shape, BF16),
        ],
        scratch_shapes=[
            low(n_ctx, *out.shape[1:]),
            low(n_ctx - 1, *out.shape[1:]),
            pltpu.VMEM(out.shape[1:], F32),
            low(*small.shape),
            low(*small.shape[1:]),
            low(*small.shape[1:]),
            low(*qkv.shape),
            low(*qkv.shape),
            low(*qkv.shape),
            low(part, width),
            low(*out.shape[1:]),
            low(3, shard, width),
            low(*joined.shape),
            pltpu.VMEM((2,) + grad_one.shape, F32),
            pltpu.VMEM(grad_one.shape, F32),
            dma((n_ctx * n_x - 1,)),
            dma((n_ctx * n_x,)),
            dma((2 * (n - 1),)),
            dma((n,)),
            dma((n,)),
            dma((n_ctx - 1,)),
            dma((n_ctx - 1,)),
            dma((8,)),
            dma((8,)),
        ],
        compiler_params=pltpu.CompilerParams(
            collective_id=2, has_side_effects=True, vmem_limit_bytes=VMEM_LIMIT
        ),
        cost_estimate=pl.CostEstimate(flops=0, bytes_accessed=16 * joined.size, transcendentals=0),
        name="finish_grads",
    )(out, x_out, small, qkv, reduced, joined, weight, grad_one)


def project_kernel(tok_ref, w_ref, b_ref, cos_ref, sin_ref, q_ref, k_ref, v_ref):
    joined = mm(tok_ref[...], w_ref[...]) + b_ref[...]
    wide = 2 * HD
    turned = joined[:, :wide] * cos_ref[...] + joined[:, wide : 2 * wide] * sin_ref[...]
    q_ref[...] = (turned[:, :HD].astype(BF16) * HD ** (-0.5)).astype(BF16)
    k_ref[...] = turned[:, HD:].astype(BF16)
    v_ref[...] = joined[:, 2 * wide :].astype(BF16)


def project(tokens, weight, bias, cosine, sine):
    rows, width = tokens.shape
    seq = cosine.shape[0]
    block = min(512, seq)
    per_slot = seq // block
    cols = weight.shape[1]
    head_out = jax.ShapeDtypeStruct((rows, HD), BF16)
    head_spec = pl.BlockSpec((block, HD), lambda i: (i, 0))
    return pl.pallas_call(
        project_kernel,
        grid=(rows // block,),
        in_specs=[
            pl.BlockSpec((block, width), lambda i: (i, 0)),
            pl.BlockSpec((width, cols), lambda i: (0, 0)),
            pl.BlockSpec((1, cols), lambda i: (0, 0)),
            pl.BlockSpec((block, 2 * HD), lambda i: (i % per_slot, 0)),
            pl.BlockSpec((block, 2 * HD), lambda i: (i % per_slot, 0)),
        ],
        out_specs=[head_spec] * 3,
        out_shape=[head_out] * 3,
        compiler_params=pltpu.CompilerParams(vmem_limit_bytes=VMEM_LIMIT),
        cost_estimate=pl.CostEstimate(
            flops=2 * rows * width * cols, bytes_accessed=2 * rows * width, transcendentals=0
        ),
        name="project",
    )(tokens, weight, bias, cosine, sine)


QB = 512
KB = 512


def forward_kernel(
    len_ref, core_ref, q_ref, k_ref, v_ref, out_ref, send_ref, norm_ref, *, part
):
    length = len_ref[pl.program_id(0)]
    core = core_ref[0]
    queries = q_ref[0]
    rows = queries.shape[0]

    def step(j, state):
        highest, total, mix = state
        start = pl.multiple_of(j * KB, KB)
        scores = contract(queries, k_ref[0, pl.ds(start, KB), :], 1, 1)
        ids = start + lax.broadcasted_iota(jnp.int32, (1, KB), 1)
        scores = jnp.where(ids < length, scores, NEG_FILL)
        higher = jnp.maximum(highest, jnp.max(scores, axis=1, keepdims=True))
        fade = jnp.exp(highest - higher)
        weights = jnp.exp(scores - higher)
        total = total * fade + jnp.sum(weights, axis=1, keepdims=True)
        mix = mix * fade + mm(weights.astype(BF16), v_ref[0, pl.ds(start, KB), :])
        return higher, total, mix

    blocks = (length + KB - 1) // KB
    highest, total, mix = lax.fori_loop(
        0,
        blocks,
        step,
        (
            jnp.full((rows, 1), NEG_FILL, F32),
            jnp.zeros((rows, 1), F32),
            jnp.zeros((rows, HD), F32),
        ),
    )
    mix = mix / total
    out_ref[0] = mix
    log_norm = jnp.broadcast_to(highest + jnp.log(total), (rows, 128))
    norm_ref[0] = jnp.transpose(log_norm)[0:1, :]
    low = mix.astype(BF16)
    for chip in range(rows // (2 * part)):
        for half in range(2):
            at = (2 * chip + half) * part
            send_ref[chip, half ^ core, 0] = low[at : at + part]


def attend(lengths, core, queries, keys, values, part):
    slots, seq, _ = queries.shape
    chips = seq // (2 * part)
    spec_q = pl.BlockSpec((1, QB, HD), lambda s, i, *_: (s, i, 0))
    spec_k = pl.BlockSpec((1, seq, HD), lambda s, i, *_: (s, 0, 0))
    return pl.pallas_call(
        partial(forward_kernel, part=part),
        grid_spec=pltpu.PrefetchScalarGridSpec(
            num_scalar_prefetch=2,
            grid=(slots, seq // QB),
            in_specs=[spec_q, spec_k, spec_k],
            out_specs=[
                spec_q,
                pl.BlockSpec(
                    (QB // (2 * part), 2, 1, part, HD), lambda s, i, *_: (i, 0, s, 0, 0)
                ),
                pl.BlockSpec((1, 1, QB), lambda s, i, *_: (s, 0, i)),
            ],
        ),
        out_shape=[
            jax.ShapeDtypeStruct((slots, seq, HD), F32),
            jax.ShapeDtypeStruct((chips, 2, slots, part, HD), BF16),
            jax.ShapeDtypeStruct((slots, 1, seq), F32),
        ],
        compiler_params=pltpu.CompilerParams(vmem_limit_bytes=VMEM_LIMIT),
        cost_estimate=pl.CostEstimate(
            flops=16 * slots * seq * seq * HD,
            bytes_accessed=8 * slots * seq * HD,
            transcendentals=slots * seq * seq,
        ),
        name="attend",
    )(lengths, core, queries, keys, values)


def backward_kernel(
    len_ref, q_ref, k_ref, v_ref, g_ref, norm_ref, dot_ref, dq_ref, dk_ref, dv_ref, dqt
):
    length = len_ref[pl.program_id(0)]
    j = pl.program_id(1)
    start = j * KB
    key_block = k_ref[0]
    value_block = v_ref[0]

    @pl.when(j == 0)
    def _():
        dqt[...] = jnp.zeros_like(dqt)

    turned = jnp.transpose(key_block.astype(F32)).astype(BF16)
    ids = start + lax.broadcasted_iota(jnp.int32, (KB, 1), 0)
    shift = jnp.where(ids < length, 0.0, NEG_FILL)

    def step(i, state):
        key_grad, value_grad = state
        at = pl.multiple_of(i * QB, QB)
        queries = q_ref[0, pl.ds(at, QB), :]
        grads = g_ref[0, pl.ds(at, QB), :]
        scores = contract(key_block, queries, 1, 1) + shift
        probs = jnp.exp(scores - norm_ref[0, :, pl.ds(at, QB)])
        grad_probs = contract(value_block, grads, 1, 1)
        grad_scores = (probs * (grad_probs - dot_ref[0, :, pl.ds(at, QB)])).astype(BF16)
        value_grad = value_grad + mm(probs.astype(BF16), grads)
        key_grad = key_grad + mm(grad_scores, queries)
        dqt[:, pl.ds(at, QB)] += mm(turned, grad_scores)
        return key_grad, value_grad

    blocks = jnp.where(start < length, (length + QB - 1) // QB, 0)
    zero = jnp.zeros((KB, HD), F32)
    key_grad, value_grad = lax.fori_loop(0, blocks, step, (zero, zero))
    dk_ref[0] = key_grad
    dv_ref[0] = value_grad

    @pl.when(j == pl.num_programs(1) - 1)
    def _():
        dq_ref[0] = jnp.transpose(dqt[...])


def attend_back(lengths, queries, keys, values, grads, norms, dots):
    slots, seq, _ = queries.shape
    whole = pl.BlockSpec((1, seq, HD), lambda s, j, *_: (s, 0, 0))
    block = pl.BlockSpec((1, KB, HD), lambda s, j, *_: (s, j, 0))
    row = pl.BlockSpec((1, 1, seq), lambda s, j, *_: (s, 0, 0))
    out = jax.ShapeDtypeStruct((slots, seq, HD), F32)
    return pl.pallas_call(
        backward_kernel,
        grid_spec=pltpu.PrefetchScalarGridSpec(
            num_scalar_prefetch=1,
            grid=(slots, seq // KB),
            in_specs=[whole, block, block, whole, row, row],
            out_specs=[whole, block, block],
            scratch_shapes=[pltpu.VMEM((HD, seq), F32)],
        ),
        out_shape=[out] * 3,
        compiler_params=pltpu.CompilerParams(vmem_limit_bytes=VMEM_LIMIT),
        cost_estimate=pl.CostEstimate(
            flops=40 * slots * seq * seq * HD,
            bytes_accessed=20 * slots * seq * HD,
            transcendentals=slots * seq * seq,
        ),
        name="attend_back",
    )(lengths, queries, keys, values, grads, norms, dots)


def join_kernel(
    q_ref, k_ref, v_ref, tok_ref, cos_ref, sin_ref, join_ref, grad_ref, total, bias, *, part
):
    i = pl.program_id(0)

    @pl.when(i == 0)
    def _():
        total[...] = jnp.zeros_like(total)
        bias[...] = jnp.zeros_like(bias)

    pair = jnp.concatenate([q_ref[...] * HD ** (-0.5), k_ref[...]], axis=1)
    half = HD // 2
    lanes = lax.broadcasted_iota(jnp.int32, (1, 2 * HD), 1)
    low = lax.rem(lanes, HD) < half
    swapped = jnp.where(low, pltpu.roll(pair, 2 * HD - half, 1), pltpu.roll(pair, half, 1))
    sine = jnp.where(low, sin_ref[...], -sin_ref[...])
    turned = pair * cos_ref[...] + swapped * sine
    joined = jnp.concatenate([turned, v_ref[...]], axis=1).astype(BF16)
    for chip in range(joined.shape[0] // (2 * part)):
        for core in range(2):
            at = (2 * chip + core) * part
            upper, lower = joined[at : at + part // 2], joined[at + part // 2 : at + part]
            join_ref[chip, core, 0] = jnp.concatenate([upper, lower], axis=1)
    total[...] += contract(joined, tok_ref[...], 0, 0)
    bias[...] += jnp.sum(joined.astype(F32), axis=0, keepdims=True)

    @pl.when(i == pl.num_programs(0) - 1)
    def _():
        turned_total = jnp.transpose(total[...])
        shard = turned_total.shape[0] // grad_ref.shape[0]
        extra = jnp.broadcast_to(bias[...], (grad_ref.shape[1] - shard, bias.shape[1]))
        for d in range(grad_ref.shape[0]):
            grad_ref[d, :shard] = turned_total[d * shard : (d + 1) * shard].astype(BF16)
            grad_ref[d, shard:] = extra.astype(BF16)


def join_grads(grad_q, grad_k, grad_v, tokens, cosine, sine, part, n_group):
    slots, seq, _ = grad_q.shape
    rows, width = tokens.shape
    block = min(512, seq)
    per_slot = seq // block
    cols = 3 * HD
    head = pl.BlockSpec((block, HD), lambda i: (i, 0))
    table = pl.BlockSpec((block, 2 * HD), lambda i: (i % per_slot, 0))
    chips = block // (2 * part)
    shard = width // n_group
    flat = [t.reshape(rows, HD) for t in (grad_q, grad_k, grad_v)]
    return pl.pallas_call(
        partial(join_kernel, part=part),
        grid=(rows // block,),
        in_specs=[
            head, head, head, pl.BlockSpec((block, width), lambda i: (i, 0)), table, table,
        ],
        out_specs=[
            pl.BlockSpec(
                (chips, 2, 1, part // 2, 2 * cols), lambda i: (i % per_slot, 0, i // per_slot, 0, 0)
            ),
            pl.BlockSpec((n_group, shard + 16, cols), lambda i: (0, 0, 0)),
        ],
        out_shape=[
            jax.ShapeDtypeStruct((seq // (2 * part), 2, slots, part // 2, 2 * cols), BF16),
            jax.ShapeDtypeStruct((n_group, shard + 16, cols), BF16),
        ],
        scratch_shapes=[pltpu.VMEM((cols, width), F32), pltpu.VMEM((1, cols), F32)],
        compiler_params=pltpu.CompilerParams(vmem_limit_bytes=VMEM_LIMIT),
        cost_estimate=pl.CostEstimate(
            flops=2 * rows * width * cols, bytes_accessed=2 * rows * width, transcendentals=0
        ),
        name="join_grads",
    )(*flat, tokens, cosine, sine)


def norm_forward(values, gain, shift):
    center = values - jnp.mean(values, axis=-1, keepdims=True)
    spread = jnp.mean(center * center, axis=-1, keepdims=True)
    root = lax.rsqrt(spread + LN_EPS)
    unit = center * root
    return unit * gain + shift, unit, root


def norm_backward(grad, unit, root, gain):
    scaled = grad * gain
    inner = scaled - jnp.mean(scaled, axis=-1, keepdims=True)
    inner = inner - unit * jnp.mean(scaled * unit, axis=-1, keepdims=True)
    return root * inner, jnp.sum(grad * unit, axis=0), jnp.sum(grad, axis=0)


def gelu_pair(values):
    half = 0.5 + 0.5 * lax.erf(values * 0.7071067811865476)
    bell = jnp.exp(-0.5 * values * values) * 0.3989422804014327
    return values * half, half + values * bell


def rope_rows(positions):
    halfway = HD // 2
    ladder = jnp.arange(halfway, dtype=F32) * (2.0 / HD)
    frequency = jnp.power(jnp.float32(10000.0), -ladder)
    angles = positions[:, None] * frequency[None, :]
    return jnp.cos(angles), jnp.sin(angles)


def head_device(
    tokens,
    lengths,
    w_qkv,
    b_qkv,
    w_out,
    b_out,
    ln1_gain,
    ln1_bias,
    w_up,
    b_up,
    w_down,
    b_down,
    ln2_gain,
    ln2_bias,
    w_proj,
    cot_out,
    cot_emb,
):
    n_lane = lax.axis_size("ctx") * lax.axis_size("x")
    n_group = 2 * n_lane
    core = lax.axis_index("core")
    slot = lax.axis_index("slot")
    chip = lax.axis_index("ctx") * lax.axis_size("x") + lax.axis_index("x")
    me = 2 * chip + core
    slots, part, width = tokens.shape
    seq = part * n_group
    rows = slots * part
    shard = width // n_group
    ff_shard = w_down.shape[0]
    ff_half = ff_shard // 2
    proj = w_proj.shape[1]
    head_cols = 3 * HD

    small = jnp.concatenate(
        [b_qkv, b_out, ln1_gain, ln1_bias, b_up, b_down, ln2_gain, ln2_bias]
    )
    small_at = [0]
    for piece in (b_qkv, b_out, ln1_gain, ln1_bias, b_up, b_down, ln2_gain, ln2_bias):
        small_at.append(small_at[-1] + piece.shape[0])
    small_rows = -(-small.shape[0] // proj)
    small_rows = -(-small_rows // 16) * 16
    small = jnp.pad(small, (0, small_rows * proj - small.shape[0])).reshape(small_rows, proj)
    def two_lanes(mine, theirs):
        low_first = jnp.stack([mine, theirs], axis=0)
        high_first = jnp.stack([theirs, mine], axis=0)
        return jnp.where(core == 0, low_first, high_first)

    up_split = w_up.reshape(shard, n_lane, 2, 2, ff_half)
    up_mine = pick(up_split, core, 2)
    up_theirs = swap_core(pick(up_split, 1 - core, 2))
    up_chip = two_lanes(pick(up_mine, slot, 2), pick(up_theirs, slot, 2))
    down_split = w_down.reshape(2, ff_half, width)

    by_head = w_qkv.reshape(shard, 3, n_group, HD).transpose(2, 0, 1, 3)
    all_tokens, my_head, packed = gather_start(
        tokens,
        by_head.reshape(n_group, shard, head_cols),
        jnp.concatenate([w_proj, small], axis=0),
    )
    lane_shard = jnp.concatenate(
        [w_out, up_chip.reshape(2 * shard, n_lane * ff_half), pick(down_split, slot, 0)], axis=0
    )
    lane_shard, packed = lax.optimization_barrier((lane_shard, packed))
    gathered = lax.all_gather(lane_shard, LANE, axis=0, tiled=False)
    out_lane = gathered[:, :shard].reshape(n_lane * shard, width)
    up = gathered[:, shard : 3 * shard].reshape(width, n_lane * ff_half)
    down = gathered[:, 3 * shard :].reshape(n_lane * ff_half, width)
    proj_full = packed[:, :shard].reshape(width, proj)
    smalls = packed[:, shard:].reshape(n_group, small_rows * proj).astype(F32)
    qkv_bias, out_bias, gain_one, shift_one, up_bias, down_bias, gain_two, shift_two = (
        smalls[:, a:b].reshape(-1) for a, b in zip(small_at[:-1], small_at[1:])
    )

    my_head = my_head.reshape(width, 3, HD)
    all_tokens = all_tokens.reshape(slots * seq, width)

    def with_swapped(joined):
        first = joined[:, 0:2]
        halves = first.reshape(-1, 2, 2, HD // 2)
        swapped = jnp.stack([-halves[:, :, 1], halves[:, :, 0]], axis=2)
        return jnp.concatenate(
            [
                first.reshape(-1, 2 * HD),
                swapped.reshape(-1, 2 * HD),
                joined[:, 2],
            ],
            axis=1,
        )

    head_weight = with_swapped(my_head)
    head_bias = with_swapped(pick(qkv_bias.reshape(1, 3, n_group, HD), me, 2))
    cosine, sine = rope_rows(jnp.arange(seq, dtype=jnp.int32).astype(F32))
    cos_wide = jnp.tile(cosine, (1, 4))
    sin_wide = jnp.tile(sine, (1, 4))
    queries, keys, values = project(all_tokens, head_weight, head_bias, cos_wide, sin_wide)
    queries, keys, values = (t.reshape(slots, seq, HD) for t in (queries, keys, values))

    bias_lane = pick(up_bias.reshape(n_lane, 2, 2, ff_half), core, 1)
    up_bias_own = pick(bias_lane, slot, 1).reshape(-1)

    qkv_split = w_qkv.reshape(shard, 3, n_lane, 2, HD)
    qkv_mine = pick(qkv_split, core, 3)
    qkv_theirs = swap_core(pick(qkv_split, 1 - core, 3))
    qkv_chip = two_lanes(qkv_mine, qkv_theirs).transpose(3, 0, 1, 2, 4)
    qkv_chip = qkv_chip.reshape(n_lane, 2 * shard, head_cols)

    mixture, send, norms = attend(
        lengths, core.reshape(1).astype(jnp.int32), queries, keys, values, part
    )
    merged = lax.all_to_all(send, LANE, 0, 0, tiled=True)
    merged = merged.transpose(1, 2, 3, 0, 4).reshape(2 * rows, n_lane * HD)

    def own_sum(partial_rows):
        return partial_rows[:rows] + swap_core(partial_rows[rows:])

    def both(value):
        return jnp.concatenate([value, swap_core(value)], axis=0)

    def quad(value):
        pair = jnp.concatenate([value, swap_slot(value)], axis=0)
        return jnp.concatenate([pair, swap_core(pair)], axis=0)

    def quad_sum(partial_rows):
        pair = partial_rows[: 2 * rows] + swap_core(partial_rows[2 * rows :])
        return pair[:rows] + swap_slot(pair[rows:].astype(BF16)).astype(F32)

    flat_tokens = tokens.reshape(rows, width).astype(F32)
    attended = own_sum(mm(merged, out_lane)) + out_bias
    hidden_one, unit_one, root_one = norm_forward(flat_tokens + attended, gain_one, shift_one)
    hidden_low, qkv_chip = lax.optimization_barrier((hidden_one.astype(BF16), qkv_chip))
    qkv_lane = lax.all_gather(qkv_chip, LANE, axis=0, tiled=True)
    hidden_low = quad(hidden_low)

    active, slope = gelu_pair(mm(hidden_low, up) + up_bias_own)
    active = active.astype(BF16)
    downward = quad_sum(mm(active, down)) + down_bias
    out_rows, unit_two, root_two = norm_forward(hidden_one + downward, gain_two, shift_two)
    out_low = out_rows.astype(BF16)
    embeds = mm(out_low, proj_full).astype(BF16)

    place = me * part + jnp.arange(part, dtype=jnp.int32)
    live = (place[None, :] < lengths[:, None]).reshape(rows, 1)
    grad_out = jnp.where(live, cot_out.reshape(rows, width).astype(F32), 0.0)
    grad_emb = jnp.where(live, cot_emb.reshape(rows, proj), 0)
    d_proj = contract(out_low, grad_emb, 0, 0)
    grad_full = grad_out + contract(grad_emb, proj_full, 1, 1)
    grad_two, d_gain_two, d_shift_two = norm_backward(grad_full, unit_two, root_two, gain_two)
    grad_down_own = grad_two.astype(BF16)
    d_down_bias = jnp.sum(grad_down_own.astype(F32), axis=0)
    grad_down = quad(grad_down_own)
    grad_up = (contract(grad_down, down, 1, 1) * slope).astype(BF16)
    d_down = contract(active, grad_down, 0, 0).astype(BF16)
    d_up = contract(hidden_low, grad_up, 0, 0).astype(BF16)
    up_bias_own_grad = jnp.sum(grad_up.astype(F32), axis=0)
    grad_hidden = grad_two + quad_sum(contract(grad_up, up, 1, 1))
    grad_one, d_gain_one, d_shift_one = norm_backward(grad_hidden, unit_one, root_one, gain_one)
    grad_att_own = grad_one.astype(BF16)
    d_out_bias = jnp.sum(grad_att_own.astype(F32), axis=0)
    grad_att_own, qkv_lane = lax.optimization_barrier((grad_att_own, qkv_lane))
    grad_att = both(grad_att_own)
    grad_merged = contract(grad_att, out_lane, 1, 1).astype(BF16)
    grad_merged = grad_merged.reshape(2, slots, part, n_lane, HD).transpose(3, 0, 1, 2, 4)
    grad_heads = lax.all_to_all(grad_merged, LANE, 0, 0, tiled=True)

    def core_order(value):
        return jnp.where(core == 0, value, jnp.flip(value, axis=1))

    grad_heads = core_order(grad_heads).transpose(2, 0, 1, 3, 4).reshape(slots, seq, HD)

    d_out = contract(merged, grad_att, 0, 0).astype(BF16)

    both_ff = jnp.concatenate(
        [d_down.reshape(n_lane, 2 * shard, width), d_up.reshape(n_lane, 2 * shard, width)], axis=1
    )
    reduced = lax.psum_scatter(both_ff, LANE, scatter_dimension=0, tiled=False)
    x_at = lax.axis_index("x")
    out_rows_ = d_out.reshape(-1, 2, shard, width)
    keep_out = pick(out_rows_, x_at, 1)
    got_out = lax.ppermute(pick(out_rows_, 1 - x_at, 1), "x", SWAP)

    spread = (
        (jnp.arange(2) == core)[:, None, None] & (jnp.arange(2) == slot)[None, :, None]
    ).astype(F32)
    up_bias_grad = up_bias_own_grad.reshape(n_lane, 1, 1, ff_half) * spread[None]
    vectors = (
        d_out_bias,
        d_gain_one,
        d_shift_one,
        up_bias_grad.reshape(-1),
        d_down_bias,
        d_gain_two,
        d_shift_two,
    )
    small_grad = jnp.concatenate([v.reshape(n_group, -1) for v in vectors], axis=1)
    small_cols = small_grad.shape[1]
    vec_rows = -(-small_cols // proj)
    vec_rows = -(-(shard + vec_rows) // 16) * 16 - shard
    small_grad = jnp.pad(small_grad, ((0, 0), (0, vec_rows * proj - small_cols)))
    small_grad = jnp.concatenate(
        [d_proj.reshape(n_group, shard, proj), small_grad.reshape(n_group, vec_rows, proj)], axis=1
    )
    row_dots = jnp.sum(grad_heads.astype(F32) * mixture, axis=-1).reshape(slots, 1, seq)
    grad_q, grad_k, grad_v = attend_back(
        lengths, queries, keys, values, grad_heads, norms, row_dots
    )

    joined, d_qkv = join_grads(
        grad_q, grad_k, grad_v, all_tokens, cos_wide, sin_wide, part, n_group
    )
    grad_w_down, grad_w_up, grad_w_out, small_sum, d_qkv, input_grad = finish_grads(
        keep_out,
        got_out,
        small_grad.astype(BF16),
        d_qkv,
        reduced,
        joined,
        qkv_lane.reshape(n_lane, n_lane, 2 * shard, head_cols),
        grad_one,
    )
    grad_w_proj = small_sum[:shard]
    vec_sum = small_sum[shard:].reshape(-1)
    vec_outs = []
    at = 0
    for v in vectors:
        size = v.size // n_group
        vec_outs.append(vec_sum[at : at + size])
        at += size
    (
        grad_b_out,
        grad_gain_one,
        grad_shift_one,
        grad_b_up,
        grad_b_down,
        grad_gain_two,
        grad_shift_two,
    ) = vec_outs

    grad_w_qkv = (
        d_qkv[:, :shard].reshape(n_group, shard, 3, HD).transpose(1, 2, 0, 3).reshape(shard, 3 * width)
    )
    qkv_bias_grad = d_qkv[:, shard].reshape(n_group, 3, HD).transpose(1, 0, 2).reshape(-1)
    grad_b_qkv = lax.dynamic_slice(qkv_bias_grad, (me * b_qkv.shape[0],), (b_qkv.shape[0],))

    return (
        out_low.reshape(slots, part, width),
        embeds.reshape(slots, part, proj),
        input_grad.reshape(slots, part, width),
        grad_w_qkv,
        grad_b_qkv,
        grad_w_out,
        grad_b_out,
        grad_gain_one,
        grad_shift_one,
        grad_w_up,
        grad_b_up,
        grad_w_down,
        grad_b_down,
        grad_gain_two,
        grad_shift_two,
        grad_w_proj,
    )


def layer_norm(hidden, gain, shift):
    center = hidden - jnp.mean(hidden, axis=-1, keepdims=True)
    spread = jnp.mean(center * center, axis=-1, keepdims=True)
    return center * lax.rsqrt(spread + LN_EPS) * gain + shift


def rope_tables(positions, head_width):
    halfway = head_width // 2
    ladder = jnp.arange(halfway, dtype=jnp.float32) * (2.0 / head_width)
    frequency = jnp.power(jnp.float32(10000.0), -ladder)
    angles = positions[:, None] * frequency[None, :]
    return (jnp.cos(angles)[:, None, :], jnp.sin(angles)[:, None, :])


def rotate(values, cosine, sine_part):
    halfway = values.shape[-1] // 2
    first_half = values[..., :halfway]
    second_half = values[..., halfway:]
    return jnp.concatenate(
        [
            first_half * cosine - second_half * sine_part,
            second_half * cosine + first_half * sine_part,
        ],
        axis=-1,
    )


def block_scores(query_block, key_block, key_start, length, scale):
    scores = (
        jnp.einsum("qhd,khd->hqk", query_block, key_block, preferred_element_type=jnp.float32)
        * scale
    )
    key_ids = key_start + jnp.arange(key_block.shape[0], dtype=jnp.int32)
    return jnp.where((key_ids < length)[None, None, :], scores, NEG_FILL)


def per_device(
    tokens,
    lengths,
    w_qkv,
    b_qkv,
    w_out,
    b_out,
    ln1_gain,
    ln1_bias,
    w_up,
    b_up,
    w_down,
    b_down,
    ln2_gain,
    ln2_bias,
    w_proj,
    cot_out,
    cot_emb,
):
    n_fsdp = lax.axis_size("fsdp")
    n_ctx = lax.axis_size("ctx")
    ctx_at = lax.axis_index("ctx")
    fsdp_at = lax.axis_index("fsdp")
    groups, tok_slot, width = tokens.shape
    heads_here = H // n_fsdp
    lane_width = heads_here * HD
    span_rows = tok_slot * n_fsdp
    key_count = span_rows * n_ctx
    row_count = groups * tok_slot
    scale = HD ** (-0.5)
    query_rows = min(512, span_rows)
    key_rows = min(2048, key_count // 4)
    query_blocks = span_rows // query_rows
    key_blocks = key_count // key_rows
    key_starts = jnp.arange(key_blocks, dtype=jnp.int32) * key_rows
    qkv_full, qkv_bias, out_full, out_bias, gain_one, shift_one = (
        lax.all_gather(w_qkv, ("ctx", "fsdp"), axis=0, tiled=True),
        lax.all_gather(b_qkv, ("ctx", "fsdp"), axis=0, tiled=True),
        lax.all_gather(w_out, ("ctx", "fsdp"), axis=0, tiled=True),
        lax.all_gather(b_out, ("ctx", "fsdp"), axis=0, tiled=True),
        lax.all_gather(ln1_gain, ("ctx", "fsdp"), axis=0, tiled=True),
        lax.all_gather(ln1_bias, ("ctx", "fsdp"), axis=0, tiled=True),
    )
    token_pos = (ctx_at * n_fsdp + fsdp_at) * tok_slot + jnp.arange(tok_slot, dtype=jnp.int32)
    live_rows = (token_pos[None, :] < lengths[:, None]).reshape(row_count, 1)
    flat_tokens = tokens.reshape(row_count, width)
    joined = jnp.dot(flat_tokens, qkv_full, preferred_element_type=jnp.float32) + qkv_bias.astype(
        jnp.float32
    )
    cosine, sine_part = rope_tables(token_pos.astype(jnp.float32), HD)
    split_heads = joined.reshape(groups, tok_slot, 3, H, HD)
    rotated_query = rotate(split_heads[:, :, 0], cosine, sine_part)
    rotated_key = rotate(split_heads[:, :, 1], cosine, sine_part)
    packed = (
        jnp.stack([rotated_query, rotated_key, split_heads[:, :, 2]], axis=2)
        .astype(jnp.bfloat16)
        .reshape(groups, tok_slot, 3, n_fsdp, lane_width)
    )
    by_heads = lax.all_to_all(packed, "fsdp", split_axis=3, concat_axis=1, tiled=True)
    queries = by_heads[:, :, 0, 0]
    local_keys = by_heads[:, :, 1, 0]
    local_values = by_heads[:, :, 2, 0]
    all_keys, all_values = (
        lax.all_gather(local_keys, "ctx", axis=1, tiled=True),
        lax.all_gather(local_values, "ctx", axis=1, tiled=True),
    )

    def attend_slot(slot_item):
        slot_queries, slot_keys, slot_values, length = slot_item
        query_split = slot_queries.reshape(query_blocks, query_rows, heads_here, HD)
        key_split = slot_keys.reshape(key_blocks, key_rows, heads_here, HD)
        value_split = slot_values.reshape(key_blocks, key_rows, heads_here, HD)

        def per_query(query_block):

            def row_stats(state_pair, key_item):
                highest, running_sum = state_pair
                scores = block_scores(query_block, key_item[0], key_item[1], length, scale)
                new_high = jnp.maximum(highest, jnp.max(scores, axis=-1))
                running_sum = running_sum * jnp.exp(highest - new_high) + jnp.sum(
                    jnp.exp(scores - new_high[..., None]), axis=-1
                )
                return ((new_high, running_sum), None)

            start_state = (
                jnp.full((heads_here, query_rows), NEG_FILL, jnp.float32),
                jnp.zeros((heads_here, query_rows), jnp.float32),
            )
            highest, running_sum = lax.scan(row_stats, start_state, (key_split, key_starts))[0]
            log_norm = highest + jnp.log(running_sum)

            def weigh_values(accumulated, key_item):
                scores = block_scores(query_block, key_item[0], key_item[2], length, scale)
                weights = jnp.exp(scores - log_norm[..., None]).astype(jnp.bfloat16)
                return (
                    accumulated
                    + jnp.einsum(
                        "hqk,khd->qhd", weights, key_item[1], preferred_element_type=jnp.float32
                    ),
                    None,
                )

            mixture = lax.scan(
                weigh_values,
                jnp.zeros((query_rows, heads_here, HD), jnp.float32),
                (key_split, value_split, key_starts),
            )[0]
            return (mixture, log_norm)

        mixture, log_norm = lax.map(per_query, query_split)
        return (mixture.reshape(span_rows, lane_width), log_norm)

    mixture, log_norms = lax.map(attend_slot, (queries, all_keys, all_values, lengths))
    merged = lax.all_to_all(
        mixture.astype(jnp.bfloat16).reshape(groups, span_rows, 1, lane_width),
        "fsdp",
        split_axis=1,
        concat_axis=2,
        tiled=True,
    ).reshape(row_count, width)
    attended = jnp.dot(merged, out_full, preferred_element_type=jnp.float32) + out_bias.astype(
        jnp.float32
    )
    hidden_one, pull_one = jax.vjp(
        layer_norm,
        flat_tokens.astype(jnp.float32) + attended,
        gain_one.astype(jnp.float32),
        shift_one.astype(jnp.float32),
    )
    hidden_low = hidden_one.astype(jnp.bfloat16)
    up_full, up_bias, down_full, down_bias, gain_two, shift_two, proj_full = (
        lax.all_gather(w_up, ("ctx", "fsdp"), axis=0, tiled=True),
        lax.all_gather(b_up, ("ctx", "fsdp"), axis=0, tiled=True),
        lax.all_gather(w_down, ("ctx", "fsdp"), axis=0, tiled=True),
        lax.all_gather(b_down, ("ctx", "fsdp"), axis=0, tiled=True),
        lax.all_gather(ln2_gain, ("ctx", "fsdp"), axis=0, tiled=True),
        lax.all_gather(ln2_bias, ("ctx", "fsdp"), axis=0, tiled=True),
        lax.all_gather(w_proj, ("ctx", "fsdp"), axis=0, tiled=True),
    )
    upward = jnp.dot(hidden_low, up_full, preferred_element_type=jnp.float32) + up_bias.astype(
        jnp.float32
    )
    active_full, pull_gelu = jax.vjp(partial(jax.nn.gelu, approximate=False), upward)
    active = active_full.astype(jnp.bfloat16)
    downward = jnp.dot(active, down_full, preferred_element_type=jnp.float32) + down_bias.astype(
        jnp.float32
    )
    out_full_rows, pull_two = jax.vjp(
        layer_norm,
        hidden_one + downward,
        gain_two.astype(jnp.float32),
        shift_two.astype(jnp.float32),
    )
    out_low = out_full_rows.astype(jnp.bfloat16)
    projected = jnp.dot(out_low, proj_full, preferred_element_type=jnp.float32)
    back_qkv, back_qkv_bias, back_out, back_out_bias, back_gain_one, back_shift_one = (
        lax.all_gather(w_qkv, ("ctx", "fsdp"), axis=0, tiled=True),
        lax.all_gather(b_qkv, ("ctx", "fsdp"), axis=0, tiled=True),
        lax.all_gather(w_out, ("ctx", "fsdp"), axis=0, tiled=True),
        lax.all_gather(b_out, ("ctx", "fsdp"), axis=0, tiled=True),
        lax.all_gather(ln1_gain, ("ctx", "fsdp"), axis=0, tiled=True),
        lax.all_gather(ln1_bias, ("ctx", "fsdp"), axis=0, tiled=True),
    )
    back_up, back_up_bias, back_down, back_down_bias, back_gain_two, back_shift_two, back_proj = (
        lax.all_gather(w_up, ("ctx", "fsdp"), axis=0, tiled=True),
        lax.all_gather(b_up, ("ctx", "fsdp"), axis=0, tiled=True),
        lax.all_gather(w_down, ("ctx", "fsdp"), axis=0, tiled=True),
        lax.all_gather(b_down, ("ctx", "fsdp"), axis=0, tiled=True),
        lax.all_gather(ln2_gain, ("ctx", "fsdp"), axis=0, tiled=True),
        lax.all_gather(ln2_bias, ("ctx", "fsdp"), axis=0, tiled=True),
        lax.all_gather(w_proj, ("ctx", "fsdp"), axis=0, tiled=True),
    )
    grad_out = jnp.where(live_rows, cot_out.reshape(row_count, width).astype(jnp.float32), 0.0)
    grad_emb = jnp.where(live_rows, cot_emb.reshape(row_count, -1), 0)
    d_proj = jnp.einsum("rd,rp->dp", out_low, grad_emb, preferred_element_type=jnp.float32)
    grad_full = grad_out + jnp.einsum(
        "rp,dp->rd", grad_emb, back_proj, preferred_element_type=jnp.float32
    )
    grad_two, d_gain_two, d_shift_two = pull_two(grad_full)
    grad_down = grad_two.astype(jnp.bfloat16)
    d_down = jnp.einsum("rf,rd->fd", active, grad_down, preferred_element_type=jnp.float32)
    d_down_bias = jnp.sum(grad_down.astype(jnp.float32), axis=0)
    grad_act = jnp.einsum("rd,fd->rf", grad_down, back_down, preferred_element_type=jnp.float32)
    grad_up = pull_gelu(grad_act)[0].astype(jnp.bfloat16)
    d_up = jnp.einsum("rd,rf->df", hidden_low, grad_up, preferred_element_type=jnp.float32)
    d_up_bias = jnp.sum(grad_up.astype(jnp.float32), axis=0)
    grad_hidden = grad_two + jnp.einsum(
        "rf,df->rd", grad_up, back_up, preferred_element_type=jnp.float32
    )
    grad_one, d_gain_one, d_shift_one = pull_one(grad_hidden)
    grad_att = grad_one.astype(jnp.bfloat16)
    d_out = jnp.einsum("rd,re->de", merged, grad_att, preferred_element_type=jnp.float32)
    d_out_bias = jnp.sum(grad_att.astype(jnp.float32), axis=0)
    grad_merged = jnp.einsum(
        "re,de->rd", grad_att, back_out, preferred_element_type=jnp.float32
    ).astype(jnp.bfloat16)
    grad_heads = lax.all_to_all(
        grad_merged.reshape(groups, tok_slot, n_fsdp, lane_width),
        "fsdp",
        split_axis=2,
        concat_axis=1,
        tiled=True,
    ).reshape(groups, span_rows, lane_width)

    def attend_back(slot_item):
        slot_queries, slot_keys, slot_values, grad_mix, log_norm, length = slot_item
        query_split = slot_queries.reshape(query_blocks, query_rows, heads_here, HD)
        key_split = slot_keys.reshape(key_blocks, key_rows, heads_here, HD)
        value_split = slot_values.reshape(key_blocks, key_rows, heads_here, HD)
        grad_split = grad_mix.reshape(query_blocks, query_rows, heads_here, HD)

        def value_pass(value_total, query_item):
            query_block, grad_block, norm_block = query_item

            def value_per_key(row_dot, key_item):
                key_block, value_block, key_start = key_item
                scores = block_scores(query_block, key_block, key_start, length, scale)
                probability = jnp.exp(scores - norm_block[..., None])
                grad_probs = jnp.einsum(
                    "qhd,khd->hqk", grad_block, value_block, preferred_element_type=jnp.float32
                )
                value_part = jnp.einsum(
                    "hqk,qhd->khd",
                    probability.astype(jnp.bfloat16),
                    grad_block,
                    preferred_element_type=jnp.float32,
                )
                return (row_dot + jnp.sum(probability * grad_probs, axis=-1), value_part)

            row_dot, value_parts = lax.scan(
                value_per_key,
                jnp.zeros((heads_here, query_rows), jnp.float32),
                (key_split, value_split, key_starts),
            )
            return (value_total + value_parts.reshape(key_count, heads_here, HD), row_dot)

        value_grad, row_dots = lax.scan(
            value_pass,
            jnp.zeros((key_count, heads_here, HD), jnp.float32),
            (query_split, grad_split, log_norm),
        )

        def key_pass(key_total, query_item):
            query_block, grad_block, norm_block, dot_block = query_item

            def key_per_key(query_accum, key_item):
                key_block, value_block, key_start = key_item
                scores = block_scores(query_block, key_block, key_start, length, scale)
                probability = jnp.exp(scores - norm_block[..., None])
                grad_probs = jnp.einsum(
                    "qhd,khd->hqk", grad_block, value_block, preferred_element_type=jnp.float32
                )
                grad_scores = (probability * (grad_probs - dot_block[..., None])).astype(
                    jnp.bfloat16
                )
                query_accum = query_accum + jnp.einsum(
                    "hqk,khd->qhd", grad_scores, key_block, preferred_element_type=jnp.float32
                )
                key_part = jnp.einsum(
                    "hqk,qhd->khd", grad_scores, query_block, preferred_element_type=jnp.float32
                )
                return (query_accum, key_part)

            query_grad, key_parts = lax.scan(
                key_per_key,
                jnp.zeros((query_rows, heads_here, HD), jnp.float32),
                (key_split, value_split, key_starts),
            )
            return (key_total + key_parts.reshape(key_count, heads_here, HD), query_grad)

        key_grad, query_grads = lax.scan(
            key_pass,
            jnp.zeros((key_count, heads_here, HD), jnp.float32),
            (query_split, grad_split, log_norm, row_dots),
        )
        return (
            query_grads.reshape(span_rows, lane_width) * scale,
            key_grad.reshape(key_count, lane_width) * scale,
            value_grad.reshape(key_count, lane_width),
        )

    grad_queries, key_terms, value_terms = lax.map(
        attend_back, (queries, all_keys, all_values, grad_heads, log_norms, lengths)
    )
    grad_keys, grad_values = (
        lax.psum_scatter(
            key_terms.astype(jnp.bfloat16), "ctx", scatter_dimension=1, tiled=True
        ).astype(jnp.float32),
        lax.psum_scatter(
            value_terms.astype(jnp.bfloat16), "ctx", scatter_dimension=1, tiled=True
        ).astype(jnp.float32),
    )
    head_pos = (ctx_at * span_rows + jnp.arange(span_rows, dtype=jnp.int32)).astype(jnp.float32)
    head_cosine, head_sine = rope_tables(head_pos, HD)
    query_back = rotate(
        grad_queries.reshape(groups, span_rows, heads_here, HD), head_cosine, -head_sine
    )
    key_back = rotate(grad_keys.reshape(groups, span_rows, heads_here, HD), head_cosine, -head_sine)
    value_back = grad_values.reshape(groups, span_rows, heads_here, HD)
    grad_pack = (
        jnp.stack([query_back, key_back, value_back], axis=2)
        .astype(jnp.bfloat16)
        .reshape(groups, span_rows, 3, 1, lane_width)
    )
    grad_joined = lax.all_to_all(
        grad_pack, "fsdp", split_axis=1, concat_axis=3, tiled=True
    ).reshape(row_count, 3 * width)
    d_qkv = jnp.einsum("rd,re->de", flat_tokens, grad_joined, preferred_element_type=jnp.float32)
    d_qkv_bias = jnp.sum(grad_joined.astype(jnp.float32), axis=0)
    input_grad = (
        jnp.einsum("re,de->rd", grad_joined, back_qkv, preferred_element_type=jnp.float32)
        + grad_one
    ).astype(jnp.bfloat16)
    shards = (
        lax.psum_scatter(d_qkv, ("ctx", "fsdp"), scatter_dimension=0, tiled=True),
        lax.psum_scatter(d_qkv_bias, ("ctx", "fsdp"), scatter_dimension=0, tiled=True),
        lax.psum_scatter(d_out, ("ctx", "fsdp"), scatter_dimension=0, tiled=True),
        lax.psum_scatter(d_out_bias, ("ctx", "fsdp"), scatter_dimension=0, tiled=True),
        lax.psum_scatter(d_gain_one, ("ctx", "fsdp"), scatter_dimension=0, tiled=True),
        lax.psum_scatter(d_shift_one, ("ctx", "fsdp"), scatter_dimension=0, tiled=True),
        lax.psum_scatter(d_up, ("ctx", "fsdp"), scatter_dimension=0, tiled=True),
        lax.psum_scatter(d_up_bias, ("ctx", "fsdp"), scatter_dimension=0, tiled=True),
        lax.psum_scatter(d_down, ("ctx", "fsdp"), scatter_dimension=0, tiled=True),
        lax.psum_scatter(d_down_bias, ("ctx", "fsdp"), scatter_dimension=0, tiled=True),
        lax.psum_scatter(d_gain_two, ("ctx", "fsdp"), scatter_dimension=0, tiled=True),
        lax.psum_scatter(d_shift_two, ("ctx", "fsdp"), scatter_dimension=0, tiled=True),
        lax.psum_scatter(d_proj, ("ctx", "fsdp"), scatter_dimension=0, tiled=True),
    )
    totals = (
        lax.psum(shards[0].astype(jnp.bfloat16), "slot").astype(jnp.float32),
        lax.psum(shards[1].astype(jnp.bfloat16), "slot").astype(jnp.float32),
        lax.psum(shards[2].astype(jnp.bfloat16), "slot").astype(jnp.float32),
        lax.psum(shards[3].astype(jnp.bfloat16), "slot").astype(jnp.float32),
        lax.psum(shards[4].astype(jnp.bfloat16), "slot").astype(jnp.float32),
        lax.psum(shards[5].astype(jnp.bfloat16), "slot").astype(jnp.float32),
        lax.psum(shards[6].astype(jnp.bfloat16), "slot").astype(jnp.float32),
        lax.psum(shards[7].astype(jnp.bfloat16), "slot").astype(jnp.float32),
        lax.psum(shards[8].astype(jnp.bfloat16), "slot").astype(jnp.float32),
        lax.psum(shards[9].astype(jnp.bfloat16), "slot").astype(jnp.float32),
        lax.psum(shards[10].astype(jnp.bfloat16), "slot").astype(jnp.float32),
        lax.psum(shards[11].astype(jnp.bfloat16), "slot").astype(jnp.float32),
        lax.psum(shards[12].astype(jnp.bfloat16), "slot").astype(jnp.float32),
    )
    return (
        out_low.reshape(groups, tok_slot, width),
        projected.astype(jnp.bfloat16).reshape(groups, tok_slot, -1),
        input_grad.reshape(groups, tok_slot, width),
        totals[0],
        totals[1],
        totals[2],
        totals[3],
        totals[4],
        totals[5],
        totals[6],
        totals[7],
        totals[8],
        totals[9],
        totals[10],
        totals[11],
        totals[12],
    )


def solution(mesh):
    n_slot, n_ctx, n_fsdp = (mesh.shape[a] for a in ("slot", "ctx", "fsdp"))
    rows_axes = ("ctx", "fsdp")
    step = per_device
    if n_slot == 2 and n_fsdp % 2 == 0 and n_ctx * n_fsdp == H:
        mesh = Mesh(
            mesh.devices.reshape(n_slot, n_ctx, n_fsdp // 2, 2), ("slot", "ctx", "x", "core")
        )
        rows_axes = GROUP
        step = head_device
    in_specs = (
        P("slot", rows_axes, None),
        P("slot"),
        P(rows_axes, None),
        P(rows_axes),
        P(rows_axes, None),
        P(rows_axes),
        P(rows_axes),
        P(rows_axes),
        P(rows_axes, None),
        P(rows_axes),
        P(rows_axes, None),
        P(rows_axes),
        P(rows_axes),
        P(rows_axes),
        P(rows_axes, None),
        P("slot", rows_axes, None),
        P("slot", rows_axes, None),
    )
    out_specs = (
        P("slot", rows_axes, None),
        P("slot", rows_axes, None),
        P("slot", rows_axes, None),
        P(rows_axes, None),
        P(rows_axes),
        P(rows_axes, None),
        P(rows_axes),
        P(rows_axes),
        P(rows_axes),
        P(rows_axes, None),
        P(rows_axes),
        P(rows_axes, None),
        P(rows_axes),
        P(rows_axes),
        P(rows_axes),
        P(rows_axes, None),
    )
    return jax.shard_map(
        step, mesh=mesh, in_specs=in_specs, out_specs=out_specs, check_vma=False
    )
```

```python
from functools import partial

import jax
import jax.numpy as jnp
from jax import lax
from jax.experimental import pallas as pl
from jax.experimental.pallas import tpu as pltpu
from jax.sharding import Mesh
from jax.sharding import PartitionSpec as P

H = 16
HD = 64
LN_EPS = 1e-05
NEG_FILL = -1e30
F32 = jnp.float32
BF16 = jnp.bfloat16
GROUP = ("ctx", "x", "core")
LANE = ("ctx", "x")
SWAP = [(0, 1), (1, 0)]
VMEM_LIMIT = 60 * 1024 * 1024


def mm(left, right):
    return jnp.dot(left, right, preferred_element_type=F32)


def contract(left, right, left_dim, right_dim):
    return lax.dot_general(
        left, right, (((left_dim,), (right_dim,)), ((), ())), preferred_element_type=F32
    )


def swap_core(value):
    return lax.ppermute(value, "core", SWAP)


def swap_slot(value):
    return lax.ppermute(value, "slot", SWAP)


def pick(stacked, index, axis):
    return lax.dynamic_index_in_dim(stacked, index, axis, keepdims=False)


MESH = pl.DeviceIdType.MESH


def at_device(**where):
    names = ("slot", "ctx", "x", "core")
    return tuple(where[n] if n in where else lax.axis_index(n) for n in names)


def greet(peers):
    barrier = pltpu.get_barrier_semaphore()
    for peer in peers:
        pl.semaphore_signal(barrier, inc=1, device_id=peer, device_id_type=MESH)
    pl.semaphore_wait(barrier, len(peers))


def group_peers(n_ctx, n_x):
    ctx, x, core = (lax.axis_index(n) for n in GROUP)
    peers = []
    for dz in range(n_ctx):
        for dx in range(n_x):
            for dc in range(2):
                if dz or dx or dc:
                    where = (lax.rem(ctx + dz, n_ctx), lax.rem(x + dx, n_x), lax.rem(core + dc, 2))
                    peers.append(where)
    return peers


def start_kernel(
    tok_ref, head_ref, small_ref, all_ref, heads_ref, smalls_ref,
    far_send, block_send, local_sem, head_recv, small_recv, block_recv, *, n_ctx, n_x
):
    part = tok_ref.shape[1]
    ctx, x, core = (lax.axis_index(n) for n in GROUP)
    me = (ctx * n_x + x) * 2 + core
    peers = group_peers(n_ctx, n_x)
    greet([at_device(ctx=z, x=a, core=c) for z, a, c in peers])

    def block_at(b):
        return all_ref.at[:, pl.ds(pl.multiple_of(b * part, part), part), :]

    pushes = []
    for k, (z, a, c) in enumerate(peers):
        them = (z * n_x + a) * 2 + c
        target = at_device(ctx=z, x=a, core=c)
        pushes.append(pltpu.make_async_remote_copy(
            head_ref.at[them], heads_ref.at[me], far_send.at[2 * k], head_recv.at[me],
            device_id=target, device_id_type=MESH))
        pushes.append(pltpu.make_async_remote_copy(
            small_ref, smalls_ref.at[me], far_send.at[2 * k + 1], small_recv.at[me],
            device_id=target, device_id_type=MESH))
    locals_ = [
        pltpu.make_async_copy(tok_ref, block_at(me), local_sem.at[0]),
        pltpu.make_async_copy(head_ref.at[me], heads_ref.at[me], local_sem.at[1]),
        pltpu.make_async_copy(small_ref, smalls_ref.at[me], local_sem.at[2]),
    ]

    def send(b, source, lane, target):
        return pltpu.make_async_remote_copy(
            source, block_at(b), block_send.at[lane, b], block_recv.at[b],
            device_id=target, device_id_type=MESH)

    up = at_device(ctx=lax.rem(ctx + 1, n_ctx))
    down = at_device(ctx=lax.rem(ctx + n_ctx - 1, n_ctx))
    side = at_device(x=1 - x)
    twin = at_device(core=1 - core)

    def here(b):
        return send(b, block_at(b), 0, twin)

    @pl.when(ctx + 1 < n_ctx)
    def _():
        send(me, tok_ref, 0, up).start()

    @pl.when(ctx > 0)
    def _():
        send(me, tok_ref, 1, down).start()

    send(me, tok_ref, 2, side).start()
    for push in pushes:
        push.start()
    send(me, tok_ref, 3, twin).start()
    for copy in locals_:
        copy.start()

    for r in range(1, n_ctx):
        low = ctx - r
        high = ctx + r

        @pl.when(low >= 0)
        def _():
            b = (low * n_x + x) * 2 + core
            here(b).wait_recv()

            @pl.when(ctx + 1 < n_ctx)
            def _():
                send(b, block_at(b), 0, up).start()

            send(b, block_at(b), 2, side).start()
            send(b, block_at(b), 3, twin).start()

        @pl.when(high < n_ctx)
        def _():
            b = (high * n_x + x) * 2 + core
            here(b).wait_recv()

            @pl.when(ctx > 0)
            def _():
                send(b, block_at(b), 1, down).start()

            send(b, block_at(b), 2, side).start()
            send(b, block_at(b), 3, twin).start()

    def from_side(z):
        b = (z * n_x + (1 - x)) * 2 + core
        here(b).wait_recv()
        send(b, block_at(b), 3, twin).start()

    from_side(ctx)
    for r in range(1, n_ctx):
        @pl.when(ctx - r >= 0)
        def _():
            from_side(ctx - r)

        @pl.when(ctx + r < n_ctx)
        def _():
            from_side(ctx + r)

    for z in range(n_ctx):
        for a in range(n_x):
            here((z * n_x + a) * 2 + 1 - core).wait_recv()
    for k, (z, a, c) in enumerate(peers):
        them = (z * n_x + a) * 2 + c
        pltpu.make_async_remote_copy(
            head_ref.at[them], heads_ref.at[them], far_send.at[2 * k], head_recv.at[them],
            device_id=twin, device_id_type=MESH).wait_recv()
        pltpu.make_async_remote_copy(
            small_ref, smalls_ref.at[them], far_send.at[2 * k + 1], small_recv.at[them],
            device_id=twin, device_id_type=MESH).wait_recv()
    for push in pushes:
        push.wait_send()
    for copy in locals_:
        copy.wait()

    for z in range(n_ctx):
        b = (z * n_x + x) * 2 + core

        @pl.when((z <= ctx) & (ctx + 1 < n_ctx))
        def _():
            send(b, block_at(b), 0, up).wait_send()

        @pl.when((z >= ctx) & (ctx > 0))
        def _():
            send(b, block_at(b), 1, down).wait_send()

        send(b, block_at(b), 2, side).wait_send()
        send(b, block_at(b), 3, twin).wait_send()
        other = (z * n_x + (1 - x)) * 2 + core
        send(other, block_at(other), 3, twin).wait_send()


def gather_start(tokens, heads, small):
    n_ctx, n_x = lax.axis_size("ctx"), lax.axis_size("x")
    n = 2 * n_ctx * n_x
    slots, part, width = tokens.shape
    vmem = pl.BlockSpec(memory_space=pltpu.VMEM)
    anywhere = pl.BlockSpec(memory_space=pl.ANY)
    dma = pltpu.SemaphoreType.DMA
    return pl.pallas_call(
        partial(start_kernel, n_ctx=n_ctx, n_x=n_x),
        in_specs=[vmem, vmem, vmem],
        out_specs=[anywhere, vmem, vmem],
        out_shape=[
            jax.ShapeDtypeStruct((slots, n * part, width), tokens.dtype),
            jax.ShapeDtypeStruct(heads.shape, heads.dtype),
            jax.ShapeDtypeStruct((n,) + small.shape, small.dtype),
        ],
        scratch_shapes=[
            dma((2 * (n - 1),)), dma((4, n)), dma((3,)), dma((n,)), dma((n,)), dma((n,))
        ],
        compiler_params=pltpu.CompilerParams(
            collective_id=1, has_side_effects=True, vmem_limit_bytes=VMEM_LIMIT
        ),
        cost_estimate=pl.CostEstimate(
            flops=0, bytes_accessed=2 * n * tokens.size, transcendentals=0
        ),
        name="gather_start",
    )(tokens, heads, small)


def finish_kernel(
    out_ref, x_out, small_ref, qkv_ref, red_ref, join_ref, weight_ref, one_ref,
    g_down, g_up, g_out, g_small, g_qkv, g_in,
    s_out, z_out, own_out, smalls, own_small, pair_small, pair_qkv, sum_qkv, qkvs,
    pair_down, pair_out, last_up, joins, partial_in, pair_in,
    join_send, join_recv, far_send, small_recv, qkv_recv, z_send, z_recv, y_send, y_recv,
    *, n_ctx, n_x
):
    ctx, x, core = (lax.axis_index(n) for n in GROUP)
    slot = lax.axis_index("slot")
    chip = ctx * n_x + x
    me = 2 * chip + core
    shard = g_up.shape[0]
    part = g_down.shape[0] // 2
    peers = group_peers(n_ctx, n_x)
    lane_peers = [(z, a) for z, a, c in peers[1::2]]
    across = at_device(slot=1 - slot)
    corner = at_device(slot=1 - slot, core=1 - core)
    twin = at_device(core=1 - core)
    greet([at_device(ctx=z, x=a, core=c) for z, a, c in peers] + [across, corner])

    def remote(source, target_ref, send_sem, recv_sem, target):
        return pltpu.make_async_remote_copy(
            source, target_ref, send_sem, recv_sem, device_id=target, device_id_type=MESH)

    started = []

    def launch(copy):
        copy.start()
        started.append(copy)
        return copy

    def pair_copy(i, source, target_ref, target):
        return launch(remote(source, target_ref, y_send.at[i], y_recv.at[i], target))

    qkv_copy = pair_copy(0, qkv_ref, pair_qkv, across)
    mine = pl.multiple_of(part + core * shard, shard)
    theirs = pl.multiple_of(part + (1 - core) * shard, shard)
    for k, (z, a, c) in enumerate(peers):
        them = (z * n_x + a) * 2 + c
        launch(remote(
            small_ref.at[them], smalls.at[me], far_send.at[2 * k + 1], small_recv.at[me],
            at_device(ctx=z, x=a, core=c)))
    smalls[me] = small_ref[me]
    for k, (z, a) in enumerate(lane_peers):
        launch(remote(
            join_ref.at[z * n_x + a], joins.at[chip], join_send.at[k], join_recv.at[chip],
            at_device(ctx=z, x=a)))
    down_copy = pair_copy(1, red_ref.at[pl.ds(0, part)], pair_down, across)
    quarter_copies = [
        pair_copy(2, red_ref.at[pl.ds(theirs, shard)], last_up.at[0], twin),
        pair_copy(3, red_ref.at[pl.ds(mine, shard)], last_up.at[1], across),
        pair_copy(4, red_ref.at[pl.ds(theirs, shard)], last_up.at[2], corner),
    ]

    second_out = []
    for j in range(n_ctx):
        place = lax.rem(ctx + 1 + j, n_ctx)
        sum_out = out_ref[place].astype(F32) + x_out[place].astype(F32)
        if j < n_ctx - 1:
            s_out[j] = sum_out.astype(BF16)
            second_out.append(launch(remote(
                s_out.at[j], z_out.at[j], z_send.at[j], z_recv.at[j], at_device(ctx=place))))
        else:
            own_out[...] = sum_out

    qkv_copy.wait_recv()
    sum_qkv[...] = (qkv_ref[...].astype(F32) + pair_qkv[...].astype(F32)).astype(BF16)
    for k, (z, a, c) in enumerate(peers):
        them = (z * n_x + a) * 2 + c
        launch(remote(
            sum_qkv.at[them], qkvs.at[me], far_send.at[2 * k], qkv_recv.at[me],
            at_device(ctx=z, x=a, core=c)))
    g_qkv[me] = sum_qkv[me].astype(F32)

    def add_head(source, rows_of, first):
        weight = jnp.concatenate(
            [weight_ref[b, source] for b in range(weight_ref.shape[0])], axis=0)
        for h in range(2):
            owner = core if h == 0 else 1 - core
            rows = rows_of(owner)
            cols = rows.shape[2] // 2
            rows = jnp.concatenate(
                [r for t in range(rows.shape[0]) for r in (rows[t, :, :cols], rows[t, :, cols:])],
                axis=0)
            term = contract(rows, weight, 1, 1)
            partial_in[h] = term if first else partial_in[h] + term

    add_head(chip, lambda owner: join_ref[chip, owner], True)

    half = pl.multiple_of(slot * part, part)
    other_half = pl.multiple_of((1 - slot) * part, part)
    g_down[pl.ds(half, part), :] = red_ref[pl.ds(0, part), :].astype(F32)
    down_copy.wait_recv()
    g_down[pl.ds(other_half, part), :] = pair_down[...].astype(F32)

    def place_quarter(rows, quarter_core, quarter_slot):
        for k in range(n_ctx * n_x):
            at = pl.multiple_of(((2 * k + quarter_core) * 2 + quarter_slot) * part, part)
            g_up[:, pl.ds(at, part)] = rows[:, k * part : (k + 1) * part].astype(F32)

    place_quarter(red_ref[pl.ds(mine, shard), :], core, slot)
    quarter_copies[0].wait_recv()
    place_quarter(last_up[0], 1 - core, slot)
    quarter_copies[1].wait_recv()
    place_quarter(last_up[1], core, 1 - slot)
    quarter_copies[2].wait_recv()
    place_quarter(last_up[2], 1 - core, 1 - slot)

    for z, a, c in peers:
        them = (z * n_x + a) * 2 + c
        remote(
            small_ref.at[them], smalls.at[them], far_send.at[1], small_recv.at[them], twin
        ).wait_recv()
    own_small[...] = jnp.sum(smalls[...].astype(F32), axis=0).astype(BF16)
    small_copy = pair_copy(5, own_small, pair_small, across)

    for k, (z, a) in enumerate(lane_peers):
        source = z * n_x + a
        remote(
            join_ref.at[source], joins.at[source], join_send.at[k], join_recv.at[source], twin
        ).wait_recv()
        add_head(source, lambda owner: joins[source, owner], False)
    in_copy = pair_copy(6, partial_in.at[1], pair_in, twin)

    for j in range(n_ctx - 1):
        second_out[j].wait_recv()
        own_out[...] += z_out[j].astype(F32)
    s_out[n_ctx - 1] = own_out[...].astype(BF16)
    out_copy = pair_copy(7, s_out.at[n_ctx - 1], pair_out, across)
    small_copy.wait_recv()
    g_small[...] = own_small[...].astype(F32) + pair_small[...].astype(F32)
    in_copy.wait_recv()
    g_in[...] = (partial_in[0] + pair_in[...] + one_ref[...]).astype(BF16)
    for z, a, c in peers:
        them = (z * n_x + a) * 2 + c
        remote(
            sum_qkv.at[them], qkvs.at[them], far_send.at[0], qkv_recv.at[them], twin
        ).wait_recv()
        g_qkv[them] = qkvs[them].astype(F32)
    out_copy.wait_recv()
    g_out[...] = s_out[n_ctx - 1].astype(F32) + pair_out[...].astype(F32)
    for copy in started:
        copy.wait_send()


def finish_grads(out, x_out, small, qkv, reduced, joined, weight, grad_one):
    n_ctx, n_x = lax.axis_size("ctx"), lax.axis_size("x")
    n = 2 * n_ctx * n_x
    width = reduced.shape[1]
    part = reduced.shape[0] // 2
    shard = out.shape[1]
    vmem = pl.BlockSpec(memory_space=pltpu.VMEM)
    dma = pltpu.SemaphoreType.DMA

    def low(*shape):
        return pltpu.VMEM(shape, BF16)

    def wide(*shape):
        return jax.ShapeDtypeStruct(shape, F32)

    return pl.pallas_call(
        partial(finish_kernel, n_ctx=n_ctx, n_x=n_x),
        in_specs=[vmem] * 8,
        out_specs=[vmem] * 6,
        out_shape=[
            wide(2 * part, width),
            wide(shard, 4 * width),
            wide(shard, width),
            wide(*small.shape[1:]),
            wide(*qkv.shape),
            jax.ShapeDtypeStruct(grad_one.shape, BF16),
        ],
        scratch_shapes=[
            low(n_ctx, *out.shape[1:]),
            low(n_ctx - 1, *out.shape[1:]),
            pltpu.VMEM(out.shape[1:], F32),
            low(*small.shape),
            low(*small.shape[1:]),
            low(*small.shape[1:]),
            low(*qkv.shape),
            low(*qkv.shape),
            low(*qkv.shape),
            low(part, width),
            low(*out.shape[1:]),
            low(3, shard, width),
            low(*joined.shape),
            pltpu.VMEM((2,) + grad_one.shape, F32),
            pltpu.VMEM(grad_one.shape, F32),
            dma((n_ctx * n_x - 1,)),
            dma((n_ctx * n_x,)),
            dma((2 * (n - 1),)),
            dma((n,)),
            dma((n,)),
            dma((n_ctx - 1,)),
            dma((n_ctx - 1,)),
            dma((8,)),
            dma((8,)),
        ],
        compiler_params=pltpu.CompilerParams(
            collective_id=2, has_side_effects=True, vmem_limit_bytes=VMEM_LIMIT
        ),
        cost_estimate=pl.CostEstimate(flops=0, bytes_accessed=16 * joined.size, transcendentals=0),
        name="finish_grads",
    )(out, x_out, small, qkv, reduced, joined, weight, grad_one)


def project_kernel(tok_ref, w_ref, b_ref, cos_ref, sin_ref, q_ref, k_ref, v_ref):
    joined = mm(tok_ref[...], w_ref[...]) + b_ref[...]
    wide = 2 * HD
    turned = joined[:, :wide] * cos_ref[...] + joined[:, wide : 2 * wide] * sin_ref[...]
    q_ref[...] = (turned[:, :HD].astype(BF16) * HD ** (-0.5)).astype(BF16)
    k_ref[...] = turned[:, HD:].astype(BF16)
    v_ref[...] = joined[:, 2 * wide :].astype(BF16)


def project(tokens, weight, bias, cosine, sine):
    rows, width = tokens.shape
    seq = cosine.shape[0]
    block = min(512, seq)
    per_slot = seq // block
    cols = weight.shape[1]
    head_out = jax.ShapeDtypeStruct((rows, HD), BF16)
    head_spec = pl.BlockSpec((block, HD), lambda i: (i, 0))
    return pl.pallas_call(
        project_kernel,
        grid=(rows // block,),
        in_specs=[
            pl.BlockSpec((block, width), lambda i: (i, 0)),
            pl.BlockSpec((width, cols), lambda i: (0, 0)),
            pl.BlockSpec((1, cols), lambda i: (0, 0)),
            pl.BlockSpec((block, 2 * HD), lambda i: (i % per_slot, 0)),
            pl.BlockSpec((block, 2 * HD), lambda i: (i % per_slot, 0)),
        ],
        out_specs=[head_spec] * 3,
        out_shape=[head_out] * 3,
        compiler_params=pltpu.CompilerParams(vmem_limit_bytes=VMEM_LIMIT),
        cost_estimate=pl.CostEstimate(
            flops=2 * rows * width * cols, bytes_accessed=2 * rows * width, transcendentals=0
        ),
        name="project",
    )(tokens, weight, bias, cosine, sine)


QB = 512
KB = 512


def forward_kernel(
    len_ref, core_ref, q_ref, k_ref, v_ref, out_ref, send_ref, norm_ref, *, part
):
    length = len_ref[pl.program_id(0)]
    core = core_ref[0]
    queries = q_ref[0]
    rows = queries.shape[0]

    def step(j, state):
        highest, total, mix = state
        start = pl.multiple_of(j * KB, KB)
        scores = contract(queries, k_ref[0, pl.ds(start, KB), :], 1, 1)
        ids = start + lax.broadcasted_iota(jnp.int32, (1, KB), 1)
        scores = jnp.where(ids < length, scores, NEG_FILL)
        higher = jnp.maximum(highest, jnp.max(scores, axis=1, keepdims=True))
        fade = jnp.exp(highest - higher)
        weights = jnp.exp(scores - higher)
        total = total * fade + jnp.sum(weights, axis=1, keepdims=True)
        mix = mix * fade + mm(weights.astype(BF16), v_ref[0, pl.ds(start, KB), :])
        return higher, total, mix

    blocks = (length + KB - 1) // KB
    highest, total, mix = lax.fori_loop(
        0,
        blocks,
        step,
        (
            jnp.full((rows, 1), NEG_FILL, F32),
            jnp.zeros((rows, 1), F32),
            jnp.zeros((rows, HD), F32),
        ),
    )
    mix = mix / total
    out_ref[0] = mix
    log_norm = jnp.broadcast_to(highest + jnp.log(total), (rows, 128))
    norm_ref[0] = jnp.transpose(log_norm)[0:1, :]
    low = mix.astype(BF16)
    for chip in range(rows // (2 * part)):
        for half in range(2):
            at = (2 * chip + half) * part
            send_ref[chip, half ^ core, 0] = low[at : at + part]


def attend(lengths, core, queries, keys, values, part):
    slots, seq, _ = queries.shape
    chips = seq // (2 * part)
    spec_q = pl.BlockSpec((1, QB, HD), lambda s, i, *_: (s, i, 0))
    spec_k = pl.BlockSpec((1, seq, HD), lambda s, i, *_: (s, 0, 0))
    return pl.pallas_call(
        partial(forward_kernel, part=part),
        grid_spec=pltpu.PrefetchScalarGridSpec(
            num_scalar_prefetch=2,
            grid=(slots, seq // QB),
            in_specs=[spec_q, spec_k, spec_k],
            out_specs=[
                spec_q,
                pl.BlockSpec(
                    (QB // (2 * part), 2, 1, part, HD), lambda s, i, *_: (i, 0, s, 0, 0)
                ),
                pl.BlockSpec((1, 1, QB), lambda s, i, *_: (s, 0, i)),
            ],
        ),
        out_shape=[
            jax.ShapeDtypeStruct((slots, seq, HD), F32),
            jax.ShapeDtypeStruct((chips, 2, slots, part, HD), BF16),
            jax.ShapeDtypeStruct((slots, 1, seq), F32),
        ],
        compiler_params=pltpu.CompilerParams(vmem_limit_bytes=VMEM_LIMIT),
        cost_estimate=pl.CostEstimate(
            flops=16 * slots * seq * seq * HD,
            bytes_accessed=8 * slots * seq * HD,
            transcendentals=slots * seq * seq,
        ),
        name="attend",
    )(lengths, core, queries, keys, values)


def backward_kernel(
    len_ref, q_ref, k_ref, v_ref, g_ref, norm_ref, dot_ref, dq_ref, dk_ref, dv_ref, dqt
):
    length = len_ref[pl.program_id(0)]
    j = pl.program_id(1)
    start = j * KB
    key_block = k_ref[0]
    value_block = v_ref[0]

    @pl.when(j == 0)
    def _():
        dqt[...] = jnp.zeros_like(dqt)

    turned = jnp.transpose(key_block.astype(F32)).astype(BF16)
    ids = start + lax.broadcasted_iota(jnp.int32, (KB, 1), 0)
    shift = jnp.where(ids < length, 0.0, NEG_FILL)

    def step(i, state):
        key_grad, value_grad = state
        at = pl.multiple_of(i * QB, QB)
        queries = q_ref[0, pl.ds(at, QB), :]
        grads = g_ref[0, pl.ds(at, QB), :]
        scores = contract(key_block, queries, 1, 1) + shift
        probs = jnp.exp(scores - norm_ref[0, :, pl.ds(at, QB)])
        grad_probs = contract(value_block, grads, 1, 1)
        grad_scores = (probs * (grad_probs - dot_ref[0, :, pl.ds(at, QB)])).astype(BF16)
        value_grad = value_grad + mm(probs.astype(BF16), grads)
        key_grad = key_grad + mm(grad_scores, queries)
        dqt[:, pl.ds(at, QB)] += mm(turned, grad_scores)
        return key_grad, value_grad

    blocks = jnp.where(start < length, (length + QB - 1) // QB, 0)
    zero = jnp.zeros((KB, HD), F32)
    key_grad, value_grad = lax.fori_loop(0, blocks, step, (zero, zero))
    dk_ref[0] = key_grad
    dv_ref[0] = value_grad

    @pl.when(j == pl.num_programs(1) - 1)
    def _():
        dq_ref[0] = jnp.transpose(dqt[...])


def attend_back(lengths, queries, keys, values, grads, norms, dots):
    slots, seq, _ = queries.shape
    whole = pl.BlockSpec((1, seq, HD), lambda s, j, *_: (s, 0, 0))
    block = pl.BlockSpec((1, KB, HD), lambda s, j, *_: (s, j, 0))
    row = pl.BlockSpec((1, 1, seq), lambda s, j, *_: (s, 0, 0))
    out = jax.ShapeDtypeStruct((slots, seq, HD), F32)
    return pl.pallas_call(
        backward_kernel,
        grid_spec=pltpu.PrefetchScalarGridSpec(
            num_scalar_prefetch=1,
            grid=(slots, seq // KB),
            in_specs=[whole, block, block, whole, row, row],
            out_specs=[whole, block, block],
            scratch_shapes=[pltpu.VMEM((HD, seq), F32)],
        ),
        out_shape=[out] * 3,
        compiler_params=pltpu.CompilerParams(vmem_limit_bytes=VMEM_LIMIT),
        cost_estimate=pl.CostEstimate(
            flops=40 * slots * seq * seq * HD,
            bytes_accessed=20 * slots * seq * HD,
            transcendentals=slots * seq * seq,
        ),
        name="attend_back",
    )(lengths, queries, keys, values, grads, norms, dots)


def join_kernel(
    q_ref, k_ref, v_ref, tok_ref, cos_ref, sin_ref, join_ref, grad_ref, total, bias, *, part
):
    i = pl.program_id(0)

    @pl.when(i == 0)
    def _():
        total[...] = jnp.zeros_like(total)
        bias[...] = jnp.zeros_like(bias)

    pair = jnp.concatenate([q_ref[...] * HD ** (-0.5), k_ref[...]], axis=1)
    half = HD // 2
    lanes = lax.broadcasted_iota(jnp.int32, (1, 2 * HD), 1)
    low = lax.rem(lanes, HD) < half
    swapped = jnp.where(low, pltpu.roll(pair, 2 * HD - half, 1), pltpu.roll(pair, half, 1))
    sine = jnp.where(low, sin_ref[...], -sin_ref[...])
    turned = pair * cos_ref[...] + swapped * sine
    joined = jnp.concatenate([turned, v_ref[...]], axis=1).astype(BF16)
    for chip in range(joined.shape[0] // (2 * part)):
        for core in range(2):
            at = (2 * chip + core) * part
            upper, lower = joined[at : at + part // 2], joined[at + part // 2 : at + part]
            join_ref[chip, core, 0] = jnp.concatenate([upper, lower], axis=1)
    total[...] += contract(joined, tok_ref[...], 0, 0)
    bias[...] += jnp.sum(joined.astype(F32), axis=0, keepdims=True)

    @pl.when(i == pl.num_programs(0) - 1)
    def _():
        turned_total = jnp.transpose(total[...])
        shard = turned_total.shape[0] // grad_ref.shape[0]
        extra = jnp.broadcast_to(bias[...], (grad_ref.shape[1] - shard, bias.shape[1]))
        for d in range(grad_ref.shape[0]):
            grad_ref[d, :shard] = turned_total[d * shard : (d + 1) * shard].astype(BF16)
            grad_ref[d, shard:] = extra.astype(BF16)


def join_grads(grad_q, grad_k, grad_v, tokens, cosine, sine, part, n_group):
    slots, seq, _ = grad_q.shape
    rows, width = tokens.shape
    block = min(512, seq)
    per_slot = seq // block
    cols = 3 * HD
    head = pl.BlockSpec((block, HD), lambda i: (i, 0))
    table = pl.BlockSpec((block, 2 * HD), lambda i: (i % per_slot, 0))
    chips = block // (2 * part)
    shard = width // n_group
    flat = [t.reshape(rows, HD) for t in (grad_q, grad_k, grad_v)]
    return pl.pallas_call(
        partial(join_kernel, part=part),
        grid=(rows // block,),
        in_specs=[
            head, head, head, pl.BlockSpec((block, width), lambda i: (i, 0)), table, table,
        ],
        out_specs=[
            pl.BlockSpec(
                (chips, 2, 1, part // 2, 2 * cols), lambda i: (i % per_slot, 0, i // per_slot, 0, 0)
            ),
            pl.BlockSpec((n_group, shard + 16, cols), lambda i: (0, 0, 0)),
        ],
        out_shape=[
            jax.ShapeDtypeStruct((seq // (2 * part), 2, slots, part // 2, 2 * cols), BF16),
            jax.ShapeDtypeStruct((n_group, shard + 16, cols), BF16),
        ],
        scratch_shapes=[pltpu.VMEM((cols, width), F32), pltpu.VMEM((1, cols), F32)],
        compiler_params=pltpu.CompilerParams(vmem_limit_bytes=VMEM_LIMIT),
        cost_estimate=pl.CostEstimate(
            flops=2 * rows * width * cols, bytes_accessed=2 * rows * width, transcendentals=0
        ),
        name="join_grads",
    )(*flat, tokens, cosine, sine)


def norm_forward(values, gain, shift):
    center = values - jnp.mean(values, axis=-1, keepdims=True)
    spread = jnp.mean(center * center, axis=-1, keepdims=True)
    root = lax.rsqrt(spread + LN_EPS)
    unit = center * root
    return unit * gain + shift, unit, root


def norm_backward(grad, unit, root, gain):
    scaled = grad * gain
    inner = scaled - jnp.mean(scaled, axis=-1, keepdims=True)
    inner = inner - unit * jnp.mean(scaled * unit, axis=-1, keepdims=True)
    return root * inner, jnp.sum(grad * unit, axis=0), jnp.sum(grad, axis=0)


def gelu_pair(values):
    half = 0.5 + 0.5 * lax.erf(values * 0.7071067811865476)
    bell = jnp.exp(-0.5 * values * values) * 0.3989422804014327
    return values * half, half + values * bell


def rope_rows(positions):
    halfway = HD // 2
    ladder = jnp.arange(halfway, dtype=F32) * (2.0 / HD)
    frequency = jnp.power(jnp.float32(10000.0), -ladder)
    angles = positions[:, None] * frequency[None, :]
    return jnp.cos(angles), jnp.sin(angles)


def lane_gather(mine_ref, all_ref, send_sem, recv_sem, local_sem, n_ctx, n_x):
    ctx, x = lax.axis_index("ctx"), lax.axis_index("x")
    chip = ctx * n_x + x
    routes = (
        at_device(ctx=lax.rem(ctx + 1, n_ctx)),
        at_device(ctx=lax.rem(ctx + n_ctx - 1, n_ctx)),
        at_device(x=1 - x),
    )

    def send(k, lane, own=False):
        return pltpu.make_async_remote_copy(
            mine_ref if own else all_ref.at[k], all_ref.at[k], send_sem.at[lane, k], recv_sem.at[k],
            device_id=routes[lane], device_id_type=MESH)

    local = pltpu.make_async_copy(mine_ref, all_ref.at[chip], local_sem)

    def begin():
        @pl.when(ctx + 1 < n_ctx)
        def _():
            send(chip, 0, own=True).start()

        @pl.when(ctx > 0)
        def _():
            send(chip, 1, own=True).start()

        send(chip, 2, own=True).start()
        local.start()

    def relay(r):
        for sign, lane, more in ((-1, 0, ctx + 1 < n_ctx), (1, 1, ctx > 0)):
            z = ctx + sign * r

            @pl.when((z >= 0) & (z < n_ctx))
            def _():
                k = z * n_x + x
                send(k, 0).wait_recv()

                @pl.when(more)
                def _():
                    send(k, lane).start()

                send(k, 2).start()

    def end():
        for z in range(n_ctx):
            k = z * n_x + x
            send(z * n_x + 1 - x, 0).wait_recv()

            @pl.when((z <= ctx) & (ctx + 1 < n_ctx))
            def _():
                send(k, 0).wait_send()

            @pl.when((z >= ctx) & (ctx > 0))
            def _():
                send(k, 1).wait_send()

            send(k, 2).wait_send()
        local.wait()

    return begin, relay, end


def layer_kernel(
    merged_ref, tok_ref, wo_ref, up_ref, down_ref, vec_ref, full_ref, lane_ref,
    out_ref, one_ref, gm_ref, att_ref, vecs_ref, act_out, hid_out, gdn_out, gup_out, lanes_out,
    first, first_in, hid, act, slope, gdn, gup, hidden, unit_one, two,
    roots, near, near_in, far, far_in, low_out, low_in, send_sem, recv_sem, out_sem,
    lane_send, lane_recv, *, n_ctx, n_x
):
    core, slot = lax.axis_index("core"), lax.axis_index("slot")
    twin, across = at_device(core=1 - core), at_device(slot=1 - slot)
    ctx, x = lax.axis_index("ctx"), lax.axis_index("x")
    greet([
        twin,
        across,
        at_device(x=1 - x),
        at_device(ctx=lax.rem(ctx + 1, n_ctx)),
        at_device(ctx=lax.rem(ctx + n_ctx - 1, n_ctx)),
    ])
    begin_lane, relay_lane, end_lane = lane_gather(
        lane_ref, lanes_out, lane_send, lane_recv, out_sem.at[4], n_ctx, n_x)
    begin_lane()
    rows, width = tok_ref.shape
    half = rows // 2
    tile = 256
    count = [0]
    started = []

    def launch(source, target_ref, target):
        i = count[0]
        count[0] += 1
        copy = pltpu.make_async_remote_copy(
            source, target_ref, send_sem.at[i], recv_sem.at[i],
            device_id=target, device_id_type=MESH)
        copy.start()
        started.append(copy)
        return copy

    def columns(body, n=width // tile):
        @pl.loop(0, n)
        def _(t):
            body(pl.ds(pl.multiple_of(t * tile, tile), tile))

    def chunks(body, size=64):
        @pl.loop(0, rows // size)
        def _(t):
            body(pl.ds(pl.multiple_of(t * size, size), size))

    def exchange(buf, turn, stage, product):
        halves = [
            launch(buf.at[pl.ds(h * half, half)], buf.at[pl.ds((2 + h) * rows, half)], across)
            for h in range(2)
        ]
        to_twin = launch(buf.at[pl.ds(0, rows)], buf.at[pl.ds(rows, rows)], twin)
        near_buf, far_buf = near.at[turn], far.at[turn]
        to_twin.wait_recv()
        stage(0, 2 * rows)
        product(0, 2 * rows, near_buf, 0)
        near_copy = launch(
            near_buf.at[pl.ds(rows, rows)], near_in.at[turn], twin)
        back = []
        for h in range(2):
            at = (2 + h) * rows
            halves[h].wait_recv()
            launch(
                buf.at[pl.ds(at, half)], buf.at[pl.ds(at + half, half)], twin).wait_recv()
            stage(at, rows)
            product(at, rows, far_buf, h * rows)
            i = 2 * turn + h
            launch(
                far_buf.at[pl.ds(h * rows + half, half)], far_in.at[i], twin).wait_recv()
            low_out[i] = (far_buf[pl.ds(h * rows, half), :] + far_in[i]).astype(BF16)
            back.append(launch(low_out.at[i], low_in.at[i], across))
        return near_copy, back

    def out_product(cols):
        first[:, cols] = mm(merged_ref[...], wo_ref[:, cols])

    columns(out_product)
    launch(first.at[pl.ds(rows, rows)], first_in, twin).wait_recv()

    def norm_one(at):
        values = tok_ref[at, :].astype(F32) + first[at, :] + first_in[at, :] + vec_ref[0:1, :]
        normed, unit, root = norm_forward(values, vec_ref[1:2, :], vec_ref[2:3, :])
        hidden[at, :] = normed
        unit_one[at, :] = unit
        roots[0, at, :] = jnp.broadcast_to(root, (root.shape[0], 128))
        hid[at, :] = normed.astype(BF16)

    chunks(norm_one)

    def up_stage(start, size):
        def body(cols):
            values = mm(hid[start : start + size, :], up_ref[:, cols]) + vec_ref[3:4, cols]
            active, bend = gelu_pair(values)
            act[start : start + size, cols] = active.astype(BF16)
            slope[start : start + size, cols] = bend

        columns(body)

    def down_product(start, size, target, at):
        def body(cols):
            target[at : at + size, cols] = mm(act[start : start + size, :], down_ref[:, cols])

        columns(body)

    near_copy, back = exchange(hid, 0, up_stage, down_product)
    relay_lane(1)
    out_copies = [
        pltpu.make_async_copy(hid, hid_out, out_sem.at[0]),
        pltpu.make_async_copy(act, act_out, out_sem.at[1]),
    ]
    for copy in out_copies:
        copy.start()
    vecs_ref[...] = jnp.zeros_like(vecs_ref)
    near_copy.wait_recv()

    def norm_two(at, h, local):
        downward = near[0, at, :] + near_in[0, at, :] + low_in[h, local, :].astype(F32)
        values = hidden[at, :] + downward + vec_ref[4:5, :]
        normed, unit, root = norm_forward(values, vec_ref[5:6, :], vec_ref[6:7, :])
        out_ref[at, :] = normed.astype(BF16)
        grad, gain, shift = norm_backward(full_ref[at, :], unit, root, vec_ref[5:6, :])
        two[at, :] = grad
        low = grad.astype(BF16)
        gdn[at, :] = low
        vecs_ref[5:6, :] += gain[None]
        vecs_ref[6:7, :] += shift[None]
        vecs_ref[4:5, :] += jnp.sum(low.astype(F32), axis=0, keepdims=True)

    def by_half(body, h, size=64):
        @pl.loop(0, half // size)
        def _(t):
            local = pl.multiple_of(t * size, size)
            body(pl.ds(h * half + local, size), h, pl.ds(local, size))

    for h in range(2):
        back[h].wait_recv()
        by_half(norm_two, h)

    def back_stage(start, size):
        def body(cols):
            grads = contract(gdn[start : start + size, :], down_ref[cols, :], 1, 1)
            low = (grads * slope[start : start + size, cols]).astype(BF16)
            gup[start : start + size, cols] = low
            vecs_ref[3:4, cols] += jnp.sum(low.astype(F32), axis=0, keepdims=True)

        columns(body)

    def back_product(start, size, target, at):
        def body(cols):
            target[at : at + size, cols] = contract(
                gup[start : start + size, :], up_ref[cols, :], 1, 1)

        columns(body)

    relay_lane(2)
    near_copy, back = exchange(gdn, 1, back_stage, back_product)
    for r in range(3, n_ctx):
        relay_lane(r)
    late_copies = [
        pltpu.make_async_copy(gdn, gdn_out, out_sem.at[2]),
        pltpu.make_async_copy(gup, gup_out, out_sem.at[3]),
    ]
    for copy in late_copies:
        copy.start()
    near_copy.wait_recv()

    def norm_back(at, h, local):
        grad = near[1, at, :] + near_in[1, at, :] + low_in[2 + h, local, :].astype(F32)
        grad = grad + two[at, :]
        root = roots[0, at, 0:1]
        one, gain, shift = norm_backward(grad, unit_one[at, :], root, vec_ref[1:2, :])
        one_ref[at, :] = one
        low = one.astype(BF16)
        att_ref[at, :] = low
        vecs_ref[1:2, :] += gain[None]
        vecs_ref[2:3, :] += shift[None]
        vecs_ref[0:1, :] += jnp.sum(low.astype(F32), axis=0, keepdims=True)

    for h in range(2):
        back[h].wait_recv()
        by_half(norm_back, h)
    launch(att_ref.at[pl.ds(0, rows)], att_ref.at[pl.ds(rows, rows)], twin).wait_recv()

    def merged_product(cols):
        gm_ref[:, cols] = contract(att_ref[...], wo_ref[cols, :], 1, 1).astype(BF16)

    columns(merged_product, wo_ref.shape[0] // tile)
    end_lane()
    for copy in started:
        copy.wait_send()
    for copy in out_copies + late_copies:
        copy.wait()


def layer(merged, tokens, w_out, up, down, vectors, grad_full, lane_shard):
    n_ctx, n_x = lax.axis_size("ctx"), lax.axis_size("x")
    chips = n_ctx * n_x
    rows, width = tokens.shape
    hidden = up.shape[1]
    lane = w_out.shape[0]
    vmem = pl.BlockSpec(memory_space=pltpu.VMEM)
    anywhere = pl.BlockSpec(memory_space=pl.ANY)
    dma = pltpu.SemaphoreType.DMA

    def shape(*dims, dtype=BF16):
        return jax.ShapeDtypeStruct(dims, dtype)

    def wide(*dims):
        return pltpu.VMEM(dims, F32)

    def low(*dims):
        return pltpu.VMEM(dims, BF16)

    return pl.pallas_call(
        partial(layer_kernel, n_ctx=n_ctx, n_x=n_x),
        in_specs=[vmem] * 8,
        out_specs=[vmem] * 5 + [anywhere] * 5,
        out_shape=[
            shape(rows, width),
            shape(rows, width, dtype=F32),
            shape(2 * rows, lane),
            shape(2 * rows, width),
            shape(8, width, dtype=F32),
            shape(4 * rows, hidden),
            shape(4 * rows, width),
            shape(4 * rows, width),
            shape(4 * rows, hidden),
            shape(chips, *lane_shard.shape),
        ],
        scratch_shapes=[
            wide(2 * rows, width),
            wide(rows, width),
            low(4 * rows, width),
            low(4 * rows, hidden),
            wide(4 * rows, hidden),
            low(4 * rows, width),
            low(4 * rows, hidden),
            wide(rows, width),
            wide(rows, width),
            wide(rows, width),
            wide(1, rows, 128),
            wide(2, 2 * rows, width),
            wide(2, rows, width),
            wide(2, 2 * rows, width),
            wide(4, rows // 2, width),
            low(4, rows // 2, width),
            low(4, rows // 2, width),
            dma((24,)),
            dma((24,)),
            dma((5,)),
            dma((3, chips)),
            dma((chips,)),
        ],
        compiler_params=pltpu.CompilerParams(
            collective_id=3, has_side_effects=True, vmem_limit_bytes=VMEM_LIMIT
        ),
        cost_estimate=pl.CostEstimate(
            flops=16 * rows * width * hidden, bytes_accessed=16 * rows * width, transcendentals=0
        ),
        name="layer",
    )(merged, tokens, w_out, up, down, vectors, grad_full, lane_shard)


def head_device(
    tokens,
    lengths,
    w_qkv,
    b_qkv,
    w_out,
    b_out,
    ln1_gain,
    ln1_bias,
    w_up,
    b_up,
    w_down,
    b_down,
    ln2_gain,
    ln2_bias,
    w_proj,
    cot_out,
    cot_emb,
):
    n_lane = lax.axis_size("ctx") * lax.axis_size("x")
    n_group = 2 * n_lane
    core = lax.axis_index("core")
    slot = lax.axis_index("slot")
    chip = lax.axis_index("ctx") * lax.axis_size("x") + lax.axis_index("x")
    me = 2 * chip + core
    slots, part, width = tokens.shape
    seq = part * n_group
    rows = slots * part
    shard = width // n_group
    ff_shard = w_down.shape[0]
    ff_half = ff_shard // 2
    proj = w_proj.shape[1]
    head_cols = 3 * HD

    small = jnp.concatenate(
        [b_qkv, b_out, ln1_gain, ln1_bias, b_up, b_down, ln2_gain, ln2_bias]
    )
    small_at = [0]
    for piece in (b_qkv, b_out, ln1_gain, ln1_bias, b_up, b_down, ln2_gain, ln2_bias):
        small_at.append(small_at[-1] + piece.shape[0])
    small_rows = -(-small.shape[0] // proj)
    small_rows = -(-small_rows // 16) * 16
    small = jnp.pad(small, (0, small_rows * proj - small.shape[0])).reshape(small_rows, proj)
    def two_lanes(mine, theirs):
        low_first = jnp.stack([mine, theirs], axis=0)
        high_first = jnp.stack([theirs, mine], axis=0)
        return jnp.where(core == 0, low_first, high_first)

    up_split = w_up.reshape(shard, n_lane, 2, 2, ff_half)
    up_mine = pick(up_split, core, 2)
    up_theirs = swap_core(pick(up_split, 1 - core, 2))
    up_chip = two_lanes(pick(up_mine, slot, 2), pick(up_theirs, slot, 2))
    down_split = w_down.reshape(2, ff_half, width)

    by_head = w_qkv.reshape(shard, 3, n_group, HD).transpose(2, 0, 1, 3)
    all_tokens, my_head, packed = gather_start(
        tokens,
        by_head.reshape(n_group, shard, head_cols),
        jnp.concatenate([w_proj, small], axis=0),
    )
    lane_shard = jnp.concatenate(
        [w_out, up_chip.reshape(2 * shard, n_lane * ff_half), pick(down_split, slot, 0)], axis=0
    )
    lane_shard, packed = lax.optimization_barrier((lane_shard, packed))
    gathered = lax.all_gather(lane_shard, LANE, axis=0, tiled=False)
    out_lane = gathered[:, :shard].reshape(n_lane * shard, width)
    up = gathered[:, shard : 3 * shard].reshape(width, n_lane * ff_half)
    down = gathered[:, 3 * shard :].reshape(n_lane * ff_half, width)
    proj_full = packed[:, :shard].reshape(width, proj)
    smalls = packed[:, shard:].reshape(n_group, small_rows * proj).astype(F32)
    qkv_bias, out_bias, gain_one, shift_one, up_bias, down_bias, gain_two, shift_two = (
        smalls[:, a:b].reshape(-1) for a, b in zip(small_at[:-1], small_at[1:])
    )

    my_head = my_head.reshape(width, 3, HD)
    all_tokens = all_tokens.reshape(slots * seq, width)

    def with_swapped(joined):
        first = joined[:, 0:2]
        halves = first.reshape(-1, 2, 2, HD // 2)
        swapped = jnp.stack([-halves[:, :, 1], halves[:, :, 0]], axis=2)
        return jnp.concatenate(
            [
                first.reshape(-1, 2 * HD),
                swapped.reshape(-1, 2 * HD),
                joined[:, 2],
            ],
            axis=1,
        )

    head_weight = with_swapped(my_head)
    head_bias = with_swapped(pick(qkv_bias.reshape(1, 3, n_group, HD), me, 2))
    cosine, sine = rope_rows(jnp.arange(seq, dtype=jnp.int32).astype(F32))
    cos_wide = jnp.tile(cosine, (1, 4))
    sin_wide = jnp.tile(sine, (1, 4))
    queries, keys, values = project(all_tokens, head_weight, head_bias, cos_wide, sin_wide)
    queries, keys, values = (t.reshape(slots, seq, HD) for t in (queries, keys, values))

    bias_lane = pick(up_bias.reshape(n_lane, 2, 2, ff_half), core, 1)
    up_bias_own = pick(bias_lane, slot, 1).reshape(-1)

    qkv_split = w_qkv.reshape(shard, 3, n_lane, 2, HD)
    qkv_mine = pick(qkv_split, core, 3)
    qkv_theirs = swap_core(pick(qkv_split, 1 - core, 3))
    qkv_chip = two_lanes(qkv_mine, qkv_theirs).transpose(3, 0, 1, 2, 4)
    qkv_chip = qkv_chip.reshape(n_lane, 2 * shard, head_cols)

    mixture, send, norms = attend(
        lengths, core.reshape(1).astype(jnp.int32), queries, keys, values, part
    )
    merged = lax.all_to_all(send, LANE, 0, 0, tiled=True)
    merged = merged.transpose(1, 2, 3, 0, 4).reshape(2 * rows, n_lane * HD)

    place = me * part + jnp.arange(part, dtype=jnp.int32)
    live = (place[None, :] < lengths[:, None]).reshape(rows, 1)
    grad_out = jnp.where(live, cot_out.reshape(rows, width).astype(F32), 0.0)
    grad_emb = jnp.where(live, cot_emb.reshape(rows, proj), 0)
    grad_full = grad_out + contract(grad_emb, proj_full, 1, 1)
    vectors = jnp.stack(
        [out_bias, gain_one, shift_one, up_bias_own, down_bias, gain_two, shift_two, shift_two]
    )
    (
        out_low,
        grad_one,
        grad_merged,
        grad_att,
        vector_grads,
        active,
        hidden_low,
        grad_down,
        grad_up,
        qkv_lane,
    ) = layer(
        merged, tokens.reshape(rows, width), out_lane, up, down, vectors, grad_full, qkv_chip
    )
    d_down = contract(active, grad_down, 0, 0).astype(BF16)
    d_up = contract(hidden_low, grad_up, 0, 0).astype(BF16)
    embeds = mm(out_low, proj_full).astype(BF16)
    d_proj = contract(out_low, grad_emb, 0, 0)
    (
        d_out_bias,
        d_gain_one,
        d_shift_one,
        up_bias_own_grad,
        d_down_bias,
        d_gain_two,
        d_shift_two,
    ) = (vector_grads[i] for i in range(7))
    grad_merged = grad_merged.reshape(2, slots, part, n_lane, HD).transpose(3, 0, 1, 2, 4)
    grad_heads = lax.all_to_all(grad_merged, LANE, 0, 0, tiled=True)

    def core_order(value):
        return jnp.where(core == 0, value, jnp.flip(value, axis=1))

    grad_heads = core_order(grad_heads).transpose(2, 0, 1, 3, 4).reshape(slots, seq, HD)

    d_out = contract(merged, grad_att, 0, 0).astype(BF16)

    both_ff = jnp.concatenate(
        [d_down.reshape(n_lane, 2 * shard, width), d_up.reshape(n_lane, 2 * shard, width)], axis=1
    )
    reduced = lax.psum_scatter(both_ff, LANE, scatter_dimension=0, tiled=False)
    x_at = lax.axis_index("x")
    out_rows_ = d_out.reshape(-1, 2, shard, width)
    keep_out = pick(out_rows_, x_at, 1)
    got_out = lax.ppermute(pick(out_rows_, 1 - x_at, 1), "x", SWAP)

    spread = (
        (jnp.arange(2) == core)[:, None, None] & (jnp.arange(2) == slot)[None, :, None]
    ).astype(F32)
    up_bias_grad = up_bias_own_grad.reshape(n_lane, 1, 1, ff_half) * spread[None]
    vectors = (
        d_out_bias,
        d_gain_one,
        d_shift_one,
        up_bias_grad.reshape(-1),
        d_down_bias,
        d_gain_two,
        d_shift_two,
    )
    small_grad = jnp.concatenate([v.reshape(n_group, -1) for v in vectors], axis=1)
    small_cols = small_grad.shape[1]
    vec_rows = -(-small_cols // proj)
    vec_rows = -(-(shard + vec_rows) // 16) * 16 - shard
    small_grad = jnp.pad(small_grad, ((0, 0), (0, vec_rows * proj - small_cols)))
    small_grad = jnp.concatenate(
        [d_proj.reshape(n_group, shard, proj), small_grad.reshape(n_group, vec_rows, proj)], axis=1
    )
    row_dots = jnp.sum(grad_heads.astype(F32) * mixture, axis=-1).reshape(slots, 1, seq)
    grad_q, grad_k, grad_v = attend_back(
        lengths, queries, keys, values, grad_heads, norms, row_dots
    )

    joined, d_qkv = join_grads(
        grad_q, grad_k, grad_v, all_tokens, cos_wide, sin_wide, part, n_group
    )
    grad_w_down, grad_w_up, grad_w_out, small_sum, d_qkv, input_grad = finish_grads(
        keep_out,
        got_out,
        small_grad.astype(BF16),
        d_qkv,
        reduced,
        joined,
        qkv_lane,
        grad_one,
    )
    grad_w_proj = small_sum[:shard]
    vec_sum = small_sum[shard:].reshape(-1)
    vec_outs = []
    at = 0
    for v in vectors:
        size = v.size // n_group
        vec_outs.append(vec_sum[at : at + size])
        at += size
    (
        grad_b_out,
        grad_gain_one,
        grad_shift_one,
        grad_b_up,
        grad_b_down,
        grad_gain_two,
        grad_shift_two,
    ) = vec_outs

    grad_w_qkv = (
        d_qkv[:, :shard].reshape(n_group, shard, 3, HD).transpose(1, 2, 0, 3).reshape(shard, 3 * width)
    )
    qkv_bias_grad = d_qkv[:, shard].reshape(n_group, 3, HD).transpose(1, 0, 2).reshape(-1)
    grad_b_qkv = lax.dynamic_slice(qkv_bias_grad, (me * b_qkv.shape[0],), (b_qkv.shape[0],))

    return (
        out_low.reshape(slots, part, width),
        embeds.reshape(slots, part, proj),
        input_grad.reshape(slots, part, width),
        grad_w_qkv,
        grad_b_qkv,
        grad_w_out,
        grad_b_out,
        grad_gain_one,
        grad_shift_one,
        grad_w_up,
        grad_b_up,
        grad_w_down,
        grad_b_down,
        grad_gain_two,
        grad_shift_two,
        grad_w_proj,
    )


def layer_norm(hidden, gain, shift):
    center = hidden - jnp.mean(hidden, axis=-1, keepdims=True)
    spread = jnp.mean(center * center, axis=-1, keepdims=True)
    return center * lax.rsqrt(spread + LN_EPS) * gain + shift


def rope_tables(positions, head_width):
    halfway = head_width // 2
    ladder = jnp.arange(halfway, dtype=jnp.float32) * (2.0 / head_width)
    frequency = jnp.power(jnp.float32(10000.0), -ladder)
    angles = positions[:, None] * frequency[None, :]
    return (jnp.cos(angles)[:, None, :], jnp.sin(angles)[:, None, :])


def rotate(values, cosine, sine_part):
    halfway = values.shape[-1] // 2
    first_half = values[..., :halfway]
    second_half = values[..., halfway:]
    return jnp.concatenate(
        [
            first_half * cosine - second_half * sine_part,
            second_half * cosine + first_half * sine_part,
        ],
        axis=-1,
    )


def block_scores(query_block, key_block, key_start, length, scale):
    scores = (
        jnp.einsum("qhd,khd->hqk", query_block, key_block, preferred_element_type=jnp.float32)
        * scale
    )
    key_ids = key_start + jnp.arange(key_block.shape[0], dtype=jnp.int32)
    return jnp.where((key_ids < length)[None, None, :], scores, NEG_FILL)


def per_device(
    tokens,
    lengths,
    w_qkv,
    b_qkv,
    w_out,
    b_out,
    ln1_gain,
    ln1_bias,
    w_up,
    b_up,
    w_down,
    b_down,
    ln2_gain,
    ln2_bias,
    w_proj,
    cot_out,
    cot_emb,
):
    n_fsdp = lax.axis_size("fsdp")
    n_ctx = lax.axis_size("ctx")
    ctx_at = lax.axis_index("ctx")
    fsdp_at = lax.axis_index("fsdp")
    groups, tok_slot, width = tokens.shape
    heads_here = H // n_fsdp
    lane_width = heads_here * HD
    span_rows = tok_slot * n_fsdp
    key_count = span_rows * n_ctx
    row_count = groups * tok_slot
    scale = HD ** (-0.5)
    query_rows = min(512, span_rows)
    key_rows = min(2048, key_count // 4)
    query_blocks = span_rows // query_rows
    key_blocks = key_count // key_rows
    key_starts = jnp.arange(key_blocks, dtype=jnp.int32) * key_rows
    qkv_full, qkv_bias, out_full, out_bias, gain_one, shift_one = (
        lax.all_gather(w_qkv, ("ctx", "fsdp"), axis=0, tiled=True),
        lax.all_gather(b_qkv, ("ctx", "fsdp"), axis=0, tiled=True),
        lax.all_gather(w_out, ("ctx", "fsdp"), axis=0, tiled=True),
        lax.all_gather(b_out, ("ctx", "fsdp"), axis=0, tiled=True),
        lax.all_gather(ln1_gain, ("ctx", "fsdp"), axis=0, tiled=True),
        lax.all_gather(ln1_bias, ("ctx", "fsdp"), axis=0, tiled=True),
    )
    token_pos = (ctx_at * n_fsdp + fsdp_at) * tok_slot + jnp.arange(tok_slot, dtype=jnp.int32)
    live_rows = (token_pos[None, :] < lengths[:, None]).reshape(row_count, 1)
    flat_tokens = tokens.reshape(row_count, width)
    joined = jnp.dot(flat_tokens, qkv_full, preferred_element_type=jnp.float32) + qkv_bias.astype(
        jnp.float32
    )
    cosine, sine_part = rope_tables(token_pos.astype(jnp.float32), HD)
    split_heads = joined.reshape(groups, tok_slot, 3, H, HD)
    rotated_query = rotate(split_heads[:, :, 0], cosine, sine_part)
    rotated_key = rotate(split_heads[:, :, 1], cosine, sine_part)
    packed = (
        jnp.stack([rotated_query, rotated_key, split_heads[:, :, 2]], axis=2)
        .astype(jnp.bfloat16)
        .reshape(groups, tok_slot, 3, n_fsdp, lane_width)
    )
    by_heads = lax.all_to_all(packed, "fsdp", split_axis=3, concat_axis=1, tiled=True)
    queries = by_heads[:, :, 0, 0]
    local_keys = by_heads[:, :, 1, 0]
    local_values = by_heads[:, :, 2, 0]
    all_keys, all_values = (
        lax.all_gather(local_keys, "ctx", axis=1, tiled=True),
        lax.all_gather(local_values, "ctx", axis=1, tiled=True),
    )

    def attend_slot(slot_item):
        slot_queries, slot_keys, slot_values, length = slot_item
        query_split = slot_queries.reshape(query_blocks, query_rows, heads_here, HD)
        key_split = slot_keys.reshape(key_blocks, key_rows, heads_here, HD)
        value_split = slot_values.reshape(key_blocks, key_rows, heads_here, HD)

        def per_query(query_block):

            def row_stats(state_pair, key_item):
                highest, running_sum = state_pair
                scores = block_scores(query_block, key_item[0], key_item[1], length, scale)
                new_high = jnp.maximum(highest, jnp.max(scores, axis=-1))
                running_sum = running_sum * jnp.exp(highest - new_high) + jnp.sum(
                    jnp.exp(scores - new_high[..., None]), axis=-1
                )
                return ((new_high, running_sum), None)

            start_state = (
                jnp.full((heads_here, query_rows), NEG_FILL, jnp.float32),
                jnp.zeros((heads_here, query_rows), jnp.float32),
            )
            highest, running_sum = lax.scan(row_stats, start_state, (key_split, key_starts))[0]
            log_norm = highest + jnp.log(running_sum)

            def weigh_values(accumulated, key_item):
                scores = block_scores(query_block, key_item[0], key_item[2], length, scale)
                weights = jnp.exp(scores - log_norm[..., None]).astype(jnp.bfloat16)
                return (
                    accumulated
                    + jnp.einsum(
                        "hqk,khd->qhd", weights, key_item[1], preferred_element_type=jnp.float32
                    ),
                    None,
                )

            mixture = lax.scan(
                weigh_values,
                jnp.zeros((query_rows, heads_here, HD), jnp.float32),
                (key_split, value_split, key_starts),
            )[0]
            return (mixture, log_norm)

        mixture, log_norm = lax.map(per_query, query_split)
        return (mixture.reshape(span_rows, lane_width), log_norm)

    mixture, log_norms = lax.map(attend_slot, (queries, all_keys, all_values, lengths))
    merged = lax.all_to_all(
        mixture.astype(jnp.bfloat16).reshape(groups, span_rows, 1, lane_width),
        "fsdp",
        split_axis=1,
        concat_axis=2,
        tiled=True,
    ).reshape(row_count, width)
    attended = jnp.dot(merged, out_full, preferred_element_type=jnp.float32) + out_bias.astype(
        jnp.float32
    )
    hidden_one, pull_one = jax.vjp(
        layer_norm,
        flat_tokens.astype(jnp.float32) + attended,
        gain_one.astype(jnp.float32),
        shift_one.astype(jnp.float32),
    )
    hidden_low = hidden_one.astype(jnp.bfloat16)
    up_full, up_bias, down_full, down_bias, gain_two, shift_two, proj_full = (
        lax.all_gather(w_up, ("ctx", "fsdp"), axis=0, tiled=True),
        lax.all_gather(b_up, ("ctx", "fsdp"), axis=0, tiled=True),
        lax.all_gather(w_down, ("ctx", "fsdp"), axis=0, tiled=True),
        lax.all_gather(b_down, ("ctx", "fsdp"), axis=0, tiled=True),
        lax.all_gather(ln2_gain, ("ctx", "fsdp"), axis=0, tiled=True),
        lax.all_gather(ln2_bias, ("ctx", "fsdp"), axis=0, tiled=True),
        lax.all_gather(w_proj, ("ctx", "fsdp"), axis=0, tiled=True),
    )
    upward = jnp.dot(hidden_low, up_full, preferred_element_type=jnp.float32) + up_bias.astype(
        jnp.float32
    )
    active_full, pull_gelu = jax.vjp(partial(jax.nn.gelu, approximate=False), upward)
    active = active_full.astype(jnp.bfloat16)
    downward = jnp.dot(active, down_full, preferred_element_type=jnp.float32) + down_bias.astype(
        jnp.float32
    )
    out_full_rows, pull_two = jax.vjp(
        layer_norm,
        hidden_one + downward,
        gain_two.astype(jnp.float32),
        shift_two.astype(jnp.float32),
    )
    out_low = out_full_rows.astype(jnp.bfloat16)
    projected = jnp.dot(out_low, proj_full, preferred_element_type=jnp.float32)
    back_qkv, back_qkv_bias, back_out, back_out_bias, back_gain_one, back_shift_one = (
        lax.all_gather(w_qkv, ("ctx", "fsdp"), axis=0, tiled=True),
        lax.all_gather(b_qkv, ("ctx", "fsdp"), axis=0, tiled=True),
        lax.all_gather(w_out, ("ctx", "fsdp"), axis=0, tiled=True),
        lax.all_gather(b_out, ("ctx", "fsdp"), axis=0, tiled=True),
        lax.all_gather(ln1_gain, ("ctx", "fsdp"), axis=0, tiled=True),
        lax.all_gather(ln1_bias, ("ctx", "fsdp"), axis=0, tiled=True),
    )
    back_up, back_up_bias, back_down, back_down_bias, back_gain_two, back_shift_two, back_proj = (
        lax.all_gather(w_up, ("ctx", "fsdp"), axis=0, tiled=True),
        lax.all_gather(b_up, ("ctx", "fsdp"), axis=0, tiled=True),
        lax.all_gather(w_down, ("ctx", "fsdp"), axis=0, tiled=True),
        lax.all_gather(b_down, ("ctx", "fsdp"), axis=0, tiled=True),
        lax.all_gather(ln2_gain, ("ctx", "fsdp"), axis=0, tiled=True),
        lax.all_gather(ln2_bias, ("ctx", "fsdp"), axis=0, tiled=True),
        lax.all_gather(w_proj, ("ctx", "fsdp"), axis=0, tiled=True),
    )
    grad_out = jnp.where(live_rows, cot_out.reshape(row_count, width).astype(jnp.float32), 0.0)
    grad_emb = jnp.where(live_rows, cot_emb.reshape(row_count, -1), 0)
    d_proj = jnp.einsum("rd,rp->dp", out_low, grad_emb, preferred_element_type=jnp.float32)
    grad_full = grad_out + jnp.einsum(
        "rp,dp->rd", grad_emb, back_proj, preferred_element_type=jnp.float32
    )
    grad_two, d_gain_two, d_shift_two = pull_two(grad_full)
    grad_down = grad_two.astype(jnp.bfloat16)
    d_down = jnp.einsum("rf,rd->fd", active, grad_down, preferred_element_type=jnp.float32)
    d_down_bias = jnp.sum(grad_down.astype(jnp.float32), axis=0)
    grad_act = jnp.einsum("rd,fd->rf", grad_down, back_down, preferred_element_type=jnp.float32)
    grad_up = pull_gelu(grad_act)[0].astype(jnp.bfloat16)
    d_up = jnp.einsum("rd,rf->df", hidden_low, grad_up, preferred_element_type=jnp.float32)
    d_up_bias = jnp.sum(grad_up.astype(jnp.float32), axis=0)
    grad_hidden = grad_two + jnp.einsum(
        "rf,df->rd", grad_up, back_up, preferred_element_type=jnp.float32
    )
    grad_one, d_gain_one, d_shift_one = pull_one(grad_hidden)
    grad_att = grad_one.astype(jnp.bfloat16)
    d_out = jnp.einsum("rd,re->de", merged, grad_att, preferred_element_type=jnp.float32)
    d_out_bias = jnp.sum(grad_att.astype(jnp.float32), axis=0)
    grad_merged = jnp.einsum(
        "re,de->rd", grad_att, back_out, preferred_element_type=jnp.float32
    ).astype(jnp.bfloat16)
    grad_heads = lax.all_to_all(
        grad_merged.reshape(groups, tok_slot, n_fsdp, lane_width),
        "fsdp",
        split_axis=2,
        concat_axis=1,
        tiled=True,
    ).reshape(groups, span_rows, lane_width)

    def attend_back(slot_item):
        slot_queries, slot_keys, slot_values, grad_mix, log_norm, length = slot_item
        query_split = slot_queries.reshape(query_blocks, query_rows, heads_here, HD)
        key_split = slot_keys.reshape(key_blocks, key_rows, heads_here, HD)
        value_split = slot_values.reshape(key_blocks, key_rows, heads_here, HD)
        grad_split = grad_mix.reshape(query_blocks, query_rows, heads_here, HD)

        def value_pass(value_total, query_item):
            query_block, grad_block, norm_block = query_item

            def value_per_key(row_dot, key_item):
                key_block, value_block, key_start = key_item
                scores = block_scores(query_block, key_block, key_start, length, scale)
                probability = jnp.exp(scores - norm_block[..., None])
                grad_probs = jnp.einsum(
                    "qhd,khd->hqk", grad_block, value_block, preferred_element_type=jnp.float32
                )
                value_part = jnp.einsum(
                    "hqk,qhd->khd",
                    probability.astype(jnp.bfloat16),
                    grad_block,
                    preferred_element_type=jnp.float32,
                )
                return (row_dot + jnp.sum(probability * grad_probs, axis=-1), value_part)

            row_dot, value_parts = lax.scan(
                value_per_key,
                jnp.zeros((heads_here, query_rows), jnp.float32),
                (key_split, value_split, key_starts),
            )
            return (value_total + value_parts.reshape(key_count, heads_here, HD), row_dot)

        value_grad, row_dots = lax.scan(
            value_pass,
            jnp.zeros((key_count, heads_here, HD), jnp.float32),
            (query_split, grad_split, log_norm),
        )

        def key_pass(key_total, query_item):
            query_block, grad_block, norm_block, dot_block = query_item

            def key_per_key(query_accum, key_item):
                key_block, value_block, key_start = key_item
                scores = block_scores(query_block, key_block, key_start, length, scale)
                probability = jnp.exp(scores - norm_block[..., None])
                grad_probs = jnp.einsum(
                    "qhd,khd->hqk", grad_block, value_block, preferred_element_type=jnp.float32
                )
                grad_scores = (probability * (grad_probs - dot_block[..., None])).astype(
                    jnp.bfloat16
                )
                query_accum = query_accum + jnp.einsum(
                    "hqk,khd->qhd", grad_scores, key_block, preferred_element_type=jnp.float32
                )
                key_part = jnp.einsum(
                    "hqk,qhd->khd", grad_scores, query_block, preferred_element_type=jnp.float32
                )
                return (query_accum, key_part)

            query_grad, key_parts = lax.scan(
                key_per_key,
                jnp.zeros((query_rows, heads_here, HD), jnp.float32),
                (key_split, value_split, key_starts),
            )
            return (key_total + key_parts.reshape(key_count, heads_here, HD), query_grad)

        key_grad, query_grads = lax.scan(
            key_pass,
            jnp.zeros((key_count, heads_here, HD), jnp.float32),
            (query_split, grad_split, log_norm, row_dots),
        )
        return (
            query_grads.reshape(span_rows, lane_width) * scale,
            key_grad.reshape(key_count, lane_width) * scale,
            value_grad.reshape(key_count, lane_width),
        )

    grad_queries, key_terms, value_terms = lax.map(
        attend_back, (queries, all_keys, all_values, grad_heads, log_norms, lengths)
    )
    grad_keys, grad_values = (
        lax.psum_scatter(
            key_terms.astype(jnp.bfloat16), "ctx", scatter_dimension=1, tiled=True
        ).astype(jnp.float32),
        lax.psum_scatter(
            value_terms.astype(jnp.bfloat16), "ctx", scatter_dimension=1, tiled=True
        ).astype(jnp.float32),
    )
    head_pos = (ctx_at * span_rows + jnp.arange(span_rows, dtype=jnp.int32)).astype(jnp.float32)
    head_cosine, head_sine = rope_tables(head_pos, HD)
    query_back = rotate(
        grad_queries.reshape(groups, span_rows, heads_here, HD), head_cosine, -head_sine
    )
    key_back = rotate(grad_keys.reshape(groups, span_rows, heads_here, HD), head_cosine, -head_sine)
    value_back = grad_values.reshape(groups, span_rows, heads_here, HD)
    grad_pack = (
        jnp.stack([query_back, key_back, value_back], axis=2)
        .astype(jnp.bfloat16)
        .reshape(groups, span_rows, 3, 1, lane_width)
    )
    grad_joined = lax.all_to_all(
        grad_pack, "fsdp", split_axis=1, concat_axis=3, tiled=True
    ).reshape(row_count, 3 * width)
    d_qkv = jnp.einsum("rd,re->de", flat_tokens, grad_joined, preferred_element_type=jnp.float32)
    d_qkv_bias = jnp.sum(grad_joined.astype(jnp.float32), axis=0)
    input_grad = (
        jnp.einsum("re,de->rd", grad_joined, back_qkv, preferred_element_type=jnp.float32)
        + grad_one
    ).astype(jnp.bfloat16)
    shards = (
        lax.psum_scatter(d_qkv, ("ctx", "fsdp"), scatter_dimension=0, tiled=True),
        lax.psum_scatter(d_qkv_bias, ("ctx", "fsdp"), scatter_dimension=0, tiled=True),
        lax.psum_scatter(d_out, ("ctx", "fsdp"), scatter_dimension=0, tiled=True),
        lax.psum_scatter(d_out_bias, ("ctx", "fsdp"), scatter_dimension=0, tiled=True),
        lax.psum_scatter(d_gain_one, ("ctx", "fsdp"), scatter_dimension=0, tiled=True),
        lax.psum_scatter(d_shift_one, ("ctx", "fsdp"), scatter_dimension=0, tiled=True),
        lax.psum_scatter(d_up, ("ctx", "fsdp"), scatter_dimension=0, tiled=True),
        lax.psum_scatter(d_up_bias, ("ctx", "fsdp"), scatter_dimension=0, tiled=True),
        lax.psum_scatter(d_down, ("ctx", "fsdp"), scatter_dimension=0, tiled=True),
        lax.psum_scatter(d_down_bias, ("ctx", "fsdp"), scatter_dimension=0, tiled=True),
        lax.psum_scatter(d_gain_two, ("ctx", "fsdp"), scatter_dimension=0, tiled=True),
        lax.psum_scatter(d_shift_two, ("ctx", "fsdp"), scatter_dimension=0, tiled=True),
        lax.psum_scatter(d_proj, ("ctx", "fsdp"), scatter_dimension=0, tiled=True),
    )
    totals = (
        lax.psum(shards[0].astype(jnp.bfloat16), "slot").astype(jnp.float32),
        lax.psum(shards[1].astype(jnp.bfloat16), "slot").astype(jnp.float32),
        lax.psum(shards[2].astype(jnp.bfloat16), "slot").astype(jnp.float32),
        lax.psum(shards[3].astype(jnp.bfloat16), "slot").astype(jnp.float32),
        lax.psum(shards[4].astype(jnp.bfloat16), "slot").astype(jnp.float32),
        lax.psum(shards[5].astype(jnp.bfloat16), "slot").astype(jnp.float32),
        lax.psum(shards[6].astype(jnp.bfloat16), "slot").astype(jnp.float32),
        lax.psum(shards[7].astype(jnp.bfloat16), "slot").astype(jnp.float32),
        lax.psum(shards[8].astype(jnp.bfloat16), "slot").astype(jnp.float32),
        lax.psum(shards[9].astype(jnp.bfloat16), "slot").astype(jnp.float32),
        lax.psum(shards[10].astype(jnp.bfloat16), "slot").astype(jnp.float32),
        lax.psum(shards[11].astype(jnp.bfloat16), "slot").astype(jnp.float32),
        lax.psum(shards[12].astype(jnp.bfloat16), "slot").astype(jnp.float32),
    )
    return (
        out_low.reshape(groups, tok_slot, width),
        projected.astype(jnp.bfloat16).reshape(groups, tok_slot, -1),
        input_grad.reshape(groups, tok_slot, width),
        totals[0],
        totals[1],
        totals[2],
        totals[3],
        totals[4],
        totals[5],
        totals[6],
        totals[7],
        totals[8],
        totals[9],
        totals[10],
        totals[11],
        totals[12],
    )


def solution(mesh):
    n_slot, n_ctx, n_fsdp = (mesh.shape[a] for a in ("slot", "ctx", "fsdp"))
    rows_axes = ("ctx", "fsdp")
    step = per_device
    if n_slot == 2 and n_fsdp % 2 == 0 and n_ctx * n_fsdp == H:
        mesh = Mesh(
            mesh.devices.reshape(n_slot, n_ctx, n_fsdp // 2, 2), ("slot", "ctx", "x", "core")
        )
        rows_axes = GROUP
        step = head_device
    in_specs = (
        P("slot", rows_axes, None),
        P("slot"),
        P(rows_axes, None),
        P(rows_axes),
        P(rows_axes, None),
        P(rows_axes),
        P(rows_axes),
        P(rows_axes),
        P(rows_axes, None),
        P(rows_axes),
        P(rows_axes, None),
        P(rows_axes),
        P(rows_axes),
        P(rows_axes),
        P(rows_axes, None),
        P("slot", rows_axes, None),
        P("slot", rows_axes, None),
    )
    out_specs = (
        P("slot", rows_axes, None),
        P("slot", rows_axes, None),
        P("slot", rows_axes, None),
        P(rows_axes, None),
        P(rows_axes),
        P(rows_axes, None),
        P(rows_axes),
        P(rows_axes),
        P(rows_axes),
        P(rows_axes, None),
        P(rows_axes),
        P(rows_axes, None),
        P(rows_axes),
        P(rows_axes),
        P(rows_axes),
        P(rows_axes, None),
    )
    return jax.shard_map(
        step, mesh=mesh, in_specs=in_specs, out_specs=out_specs, check_vma=False
    )
```

```python
from functools import partial

import jax
import jax.numpy as jnp
from jax import lax
from jax.experimental import pallas as pl
from jax.experimental.pallas import tpu as pltpu
from jax.sharding import Mesh
from jax.sharding import PartitionSpec as P

H = 16
HD = 64
LN_EPS = 1e-05
NEG_FILL = -1e30
F32 = jnp.float32
BF16 = jnp.bfloat16
GROUP = ("ctx", "x", "core")
LANE = ("ctx", "x")
SWAP = [(0, 1), (1, 0)]
VMEM_LIMIT = 60 * 1024 * 1024


def mm(left, right):
    return jnp.dot(left, right, preferred_element_type=F32)


def contract(left, right, left_dim, right_dim):
    return lax.dot_general(
        left, right, (((left_dim,), (right_dim,)), ((), ())), preferred_element_type=F32
    )


def swap_core(value):
    return lax.ppermute(value, "core", SWAP)


def swap_slot(value):
    return lax.ppermute(value, "slot", SWAP)


def pick(stacked, index, axis):
    return lax.dynamic_index_in_dim(stacked, index, axis, keepdims=False)


MESH = pl.DeviceIdType.MESH


def at_device(**where):
    names = ("slot", "ctx", "x", "core")
    return tuple(where[n] if n in where else lax.axis_index(n) for n in names)


def greet(peers):
    barrier = pltpu.get_barrier_semaphore()
    for peer in peers:
        pl.semaphore_signal(barrier, inc=1, device_id=peer, device_id_type=MESH)
    pl.semaphore_wait(barrier, len(peers))


def group_peers(n_ctx, n_x):
    ctx, x, core = (lax.axis_index(n) for n in GROUP)
    peers = []
    for dz in range(n_ctx):
        for dx in range(n_x):
            for dc in range(2):
                if dz or dx or dc:
                    where = (lax.rem(ctx + dz, n_ctx), lax.rem(x + dx, n_x), lax.rem(core + dc, 2))
                    peers.append(where)
    return peers


def start_kernel(
    tok_ref, head_ref, small_ref, all_ref, heads_ref, smalls_ref,
    far_send, block_send, local_sem, head_recv, small_recv, block_recv, *, n_ctx, n_x
):
    part = tok_ref.shape[1]
    ctx, x, core = (lax.axis_index(n) for n in GROUP)
    me = (ctx * n_x + x) * 2 + core
    peers = group_peers(n_ctx, n_x)
    greet([at_device(ctx=z, x=a, core=c) for z, a, c in peers])

    def block_at(b):
        return all_ref.at[:, pl.ds(pl.multiple_of(b * part, part), part), :]

    pushes = []
    for k, (z, a, c) in enumerate(peers):
        them = (z * n_x + a) * 2 + c
        target = at_device(ctx=z, x=a, core=c)
        pushes.append(pltpu.make_async_remote_copy(
            head_ref.at[them], heads_ref.at[me], far_send.at[2 * k], head_recv.at[me],
            device_id=target, device_id_type=MESH))
        pushes.append(pltpu.make_async_remote_copy(
            small_ref, smalls_ref.at[me], far_send.at[2 * k + 1], small_recv.at[me],
            device_id=target, device_id_type=MESH))
    locals_ = [
        pltpu.make_async_copy(tok_ref, block_at(me), local_sem.at[0]),
        pltpu.make_async_copy(head_ref.at[me], heads_ref.at[me], local_sem.at[1]),
        pltpu.make_async_copy(small_ref, smalls_ref.at[me], local_sem.at[2]),
    ]

    def send(b, source, lane, target):
        return pltpu.make_async_remote_copy(
            source, block_at(b), block_send.at[lane, b], block_recv.at[b],
            device_id=target, device_id_type=MESH)

    up = at_device(ctx=lax.rem(ctx + 1, n_ctx))
    down = at_device(ctx=lax.rem(ctx + n_ctx - 1, n_ctx))
    side = at_device(x=1 - x)
    twin = at_device(core=1 - core)

    def here(b):
        return send(b, block_at(b), 0, twin)

    @pl.when(ctx + 1 < n_ctx)
    def _():
        send(me, tok_ref, 0, up).start()

    @pl.when(ctx > 0)
    def _():
        send(me, tok_ref, 1, down).start()

    send(me, tok_ref, 2, side).start()
    for push in pushes:
        push.start()
    send(me, tok_ref, 3, twin).start()
    for copy in locals_:
        copy.start()

    for r in range(1, n_ctx):
        low = ctx - r
        high = ctx + r

        @pl.when(low >= 0)
        def _():
            b = (low * n_x + x) * 2 + core
            here(b).wait_recv()

            @pl.when(ctx + 1 < n_ctx)
            def _():
                send(b, block_at(b), 0, up).start()

            send(b, block_at(b), 2, side).start()
            send(b, block_at(b), 3, twin).start()

        @pl.when(high < n_ctx)
        def _():
            b = (high * n_x + x) * 2 + core
            here(b).wait_recv()

            @pl.when(ctx > 0)
            def _():
                send(b, block_at(b), 1, down).start()

            send(b, block_at(b), 2, side).start()
            send(b, block_at(b), 3, twin).start()

    def from_side(z):
        b = (z * n_x + (1 - x)) * 2 + core
        here(b).wait_recv()
        send(b, block_at(b), 3, twin).start()

    from_side(ctx)
    for r in range(1, n_ctx):
        @pl.when(ctx - r >= 0)
        def _():
            from_side(ctx - r)

        @pl.when(ctx + r < n_ctx)
        def _():
            from_side(ctx + r)

    for z in range(n_ctx):
        for a in range(n_x):
            here((z * n_x + a) * 2 + 1 - core).wait_recv()
    for k, (z, a, c) in enumerate(peers):
        them = (z * n_x + a) * 2 + c
        pltpu.make_async_remote_copy(
            head_ref.at[them], heads_ref.at[them], far_send.at[2 * k], head_recv.at[them],
            device_id=twin, device_id_type=MESH).wait_recv()
        pltpu.make_async_remote_copy(
            small_ref, smalls_ref.at[them], far_send.at[2 * k + 1], small_recv.at[them],
            device_id=twin, device_id_type=MESH).wait_recv()
    for push in pushes:
        push.wait_send()
    for copy in locals_:
        copy.wait()

    for z in range(n_ctx):
        b = (z * n_x + x) * 2 + core

        @pl.when((z <= ctx) & (ctx + 1 < n_ctx))
        def _():
            send(b, block_at(b), 0, up).wait_send()

        @pl.when((z >= ctx) & (ctx > 0))
        def _():
            send(b, block_at(b), 1, down).wait_send()

        send(b, block_at(b), 2, side).wait_send()
        send(b, block_at(b), 3, twin).wait_send()
        other = (z * n_x + (1 - x)) * 2 + core
        send(other, block_at(other), 3, twin).wait_send()


def gather_start(tokens, heads, small):
    n_ctx, n_x = lax.axis_size("ctx"), lax.axis_size("x")
    n = 2 * n_ctx * n_x
    slots, part, width = tokens.shape
    vmem = pl.BlockSpec(memory_space=pltpu.VMEM)
    anywhere = pl.BlockSpec(memory_space=pl.ANY)
    dma = pltpu.SemaphoreType.DMA
    return pl.pallas_call(
        partial(start_kernel, n_ctx=n_ctx, n_x=n_x),
        in_specs=[vmem, vmem, vmem],
        out_specs=[anywhere, vmem, vmem],
        out_shape=[
            jax.ShapeDtypeStruct((slots, n * part, width), tokens.dtype),
            jax.ShapeDtypeStruct(heads.shape, heads.dtype),
            jax.ShapeDtypeStruct((n,) + small.shape, small.dtype),
        ],
        scratch_shapes=[
            dma((2 * (n - 1),)), dma((4, n)), dma((3,)), dma((n,)), dma((n,)), dma((n,))
        ],
        compiler_params=pltpu.CompilerParams(
            collective_id=1, has_side_effects=True, vmem_limit_bytes=VMEM_LIMIT
        ),
        cost_estimate=pl.CostEstimate(
            flops=0, bytes_accessed=2 * n * tokens.size, transcendentals=0
        ),
        name="gather_start",
    )(tokens, heads, small)


def finish_kernel(
    out_ref, x_out, small_ref, qkv_ref, join_ref, weight_ref, one_ref,
    g_out, g_small, g_qkv, g_bias, g_in,
    s_out, z_out, own_out, smalls, own_small, pair_small, pair_qkv, sum_qkv, qkvs,
    pair_out, joins, partial_in, pair_in,
    join_send, join_recv, far_send, small_recv, qkv_recv, z_send, z_recv, y_send, y_recv,
    *, n_ctx, n_x
):
    ctx, x, core = (lax.axis_index(n) for n in GROUP)
    slot = lax.axis_index("slot")
    chip = ctx * n_x + x
    me = 2 * chip + core
    shard, width = g_out.shape
    peers = group_peers(n_ctx, n_x)
    lane_peers = [(z, a) for z, a, c in peers[1::2]]
    across = at_device(slot=1 - slot)
    twin = at_device(core=1 - core)
    greet([at_device(ctx=z, x=a, core=c) for z, a, c in peers] + [across])

    def remote(source, target_ref, send_sem, recv_sem, target):
        return pltpu.make_async_remote_copy(
            source, target_ref, send_sem, recv_sem, device_id=target, device_id_type=MESH)

    started = []

    def launch(copy):
        copy.start()
        started.append(copy)
        return copy

    def pair_copy(i, source, target_ref, target):
        return launch(remote(source, target_ref, y_send.at[i], y_recv.at[i], target))

    qkv_copy = pair_copy(0, qkv_ref, pair_qkv, across)
    for k, (z, a, c) in enumerate(peers):
        them = (z * n_x + a) * 2 + c
        launch(remote(
            small_ref.at[them], smalls.at[me], far_send.at[2 * k + 1], small_recv.at[me],
            at_device(ctx=z, x=a, core=c)))
    smalls[me] = small_ref[me]
    for k, (z, a) in enumerate(lane_peers):
        launch(remote(
            join_ref.at[z * n_x + a], joins.at[chip], join_send.at[k], join_recv.at[chip],
            at_device(ctx=z, x=a)))
    second_out = []
    for j in range(n_ctx):
        place = lax.rem(ctx + 1 + j, n_ctx)
        sum_out = out_ref[place].astype(F32) + x_out[place].astype(F32)
        if j < n_ctx - 1:
            s_out[j] = sum_out.astype(BF16)
            second_out.append(launch(remote(
                s_out.at[j], z_out.at[j], z_send.at[j], z_recv.at[j], at_device(ctx=place))))
        else:
            own_out[...] = sum_out

    qkv_copy.wait_recv()
    sum_qkv[...] = (qkv_ref[...].astype(F32) + pair_qkv[...].astype(F32)).astype(BF16)
    for k, (z, a, c) in enumerate(peers):
        them = (z * n_x + a) * 2 + c
        launch(remote(
            sum_qkv.at[them], qkvs.at[me], far_send.at[2 * k], qkv_recv.at[me],
            at_device(ctx=z, x=a, core=c)))
    qkvs[me] = sum_qkv[me]

    def add_head(source, rows_of, first):
        weight = jnp.concatenate(
            [weight_ref[b, source] for b in range(weight_ref.shape[0])], axis=0)
        for h in range(2):
            owner = core if h == 0 else 1 - core
            rows = rows_of(owner)
            cols = rows.shape[2] // 2
            rows = jnp.concatenate(
                [r for t in range(rows.shape[0]) for r in (rows[t, :, :cols], rows[t, :, cols:])],
                axis=0)
            term = contract(rows, weight, 1, 1)
            partial_in[h] = term if first else partial_in[h] + term

    add_head(chip, lambda owner: join_ref[chip, owner], True)

    for z, a, c in peers:
        them = (z * n_x + a) * 2 + c
        remote(
            small_ref.at[them], smalls.at[them], far_send.at[1], small_recv.at[them], twin
        ).wait_recv()
    own_small[...] = jnp.sum(smalls[...].astype(F32), axis=0).astype(BF16)
    small_copy = pair_copy(1, own_small, pair_small, across)

    for k, (z, a) in enumerate(lane_peers):
        source = z * n_x + a
        remote(
            join_ref.at[source], joins.at[source], join_send.at[k], join_recv.at[source], twin
        ).wait_recv()
        add_head(source, lambda owner: joins[source, owner], False)
    in_copy = pair_copy(2, partial_in.at[1], pair_in, twin)

    for j in range(n_ctx - 1):
        second_out[j].wait_recv()
        own_out[...] += z_out[j].astype(F32)
    s_out[n_ctx - 1] = own_out[...].astype(BF16)
    out_copy = pair_copy(3, s_out.at[n_ctx - 1], pair_out, across)
    small_copy.wait_recv()
    g_small[...] = own_small[...].astype(F32) + pair_small[...].astype(F32)
    in_copy.wait_recv()
    g_in[...] = (partial_in[0] + pair_in[...] + one_ref[...]).astype(BF16)
    for z, a, c in peers:
        them = (z * n_x + a) * 2 + c
        remote(
            sum_qkv.at[them], qkvs.at[them], far_send.at[0], qkv_recv.at[them], twin
        ).wait_recv()
    for k in range(n_ctx * n_x):
        heads = [qkvs[2 * k + c, :shard, :].astype(F32) for c in range(2)]
        for t in range(3):
            at = t * width + 2 * HD * k
            g_qkv[:, at : at + 2 * HD] = jnp.concatenate(
                [h[:, t * HD : (t + 1) * HD] for h in heads], axis=1)
        for c in range(2):
            g_bias[2 * k + c : 2 * k + c + 1, :] = qkvs[2 * k + c, shard : shard + 1, :].astype(F32)
    out_copy.wait_recv()
    g_out[...] = s_out[n_ctx - 1].astype(F32) + pair_out[...].astype(F32)
    for copy in started:
        copy.wait_send()


def finish_grads(out, x_out, small, qkv, joined, weight, grad_one):
    n_ctx, n_x = lax.axis_size("ctx"), lax.axis_size("x")
    n = 2 * n_ctx * n_x
    shard, width = out.shape[1:]
    vmem = pl.BlockSpec(memory_space=pltpu.VMEM)
    dma = pltpu.SemaphoreType.DMA

    def low(*shape):
        return pltpu.VMEM(shape, BF16)

    def wide(*shape):
        return jax.ShapeDtypeStruct(shape, F32)

    return pl.pallas_call(
        partial(finish_kernel, n_ctx=n_ctx, n_x=n_x),
        in_specs=[vmem] * 7,
        out_specs=[vmem] * 5,
        out_shape=[
            wide(shard, width),
            wide(*small.shape[1:]),
            wide(shard, 3 * width),
            wide(n, qkv.shape[2]),
            jax.ShapeDtypeStruct(grad_one.shape, BF16),
        ],
        scratch_shapes=[
            low(n_ctx, *out.shape[1:]),
            low(n_ctx - 1, *out.shape[1:]),
            pltpu.VMEM(out.shape[1:], F32),
            low(*small.shape),
            low(*small.shape[1:]),
            low(*small.shape[1:]),
            low(*qkv.shape),
            low(*qkv.shape),
            low(*qkv.shape),
            low(*out.shape[1:]),
            low(*joined.shape),
            pltpu.VMEM((2,) + grad_one.shape, F32),
            pltpu.VMEM(grad_one.shape, F32),
            dma((n_ctx * n_x - 1,)),
            dma((n_ctx * n_x,)),
            dma((2 * (n - 1),)),
            dma((n,)),
            dma((n,)),
            dma((n_ctx - 1,)),
            dma((n_ctx - 1,)),
            dma((4,)),
            dma((4,)),
        ],
        compiler_params=pltpu.CompilerParams(
            collective_id=2, has_side_effects=True, vmem_limit_bytes=VMEM_LIMIT
        ),
        cost_estimate=pl.CostEstimate(flops=0, bytes_accessed=16 * joined.size, transcendentals=0),
        name="finish_grads",
    )(out, x_out, small, qkv, joined, weight, grad_one)


def share_kernel(
    red_ref, g_down, g_up, pair_down, last_up, send_sem, recv_sem
):
    core, slot = lax.axis_index("core"), lax.axis_index("slot")
    across = at_device(slot=1 - slot)
    corner = at_device(slot=1 - slot, core=1 - core)
    twin = at_device(core=1 - core)
    greet([twin, across, corner])
    shard = g_up.shape[0]
    part = g_down.shape[0] // 2
    mine = pl.multiple_of(part + core * shard, shard)
    theirs = pl.multiple_of(part + (1 - core) * shard, shard)
    copies = [
        pltpu.make_async_remote_copy(
            red_ref.at[rows], target_ref, send_sem.at[i], recv_sem.at[i],
            device_id=target, device_id_type=MESH)
        for i, (rows, target_ref, target) in enumerate((
            (pl.ds(mine, shard), last_up.at[0], across),
            (pl.ds(theirs, shard), last_up.at[1], corner),
            (pl.ds(0, part), pair_down, across),
            (pl.ds(theirs, shard), last_up.at[2], twin),
        ))
    ]
    for copy in copies:
        copy.start()

    def place_quarter(rows, quarter_core, quarter_slot):
        for k in range(rows.shape[1] // part):
            at = pl.multiple_of(((2 * k + quarter_core) * 2 + quarter_slot) * part, part)
            g_up[:, pl.ds(at, part)] = rows[:, k * part : (k + 1) * part].astype(F32)

    half = pl.multiple_of(slot * part, part)
    other_half = pl.multiple_of((1 - slot) * part, part)
    g_down[pl.ds(half, part), :] = red_ref[pl.ds(0, part), :].astype(F32)
    place_quarter(red_ref[pl.ds(mine, shard), :], core, slot)
    copies[3].wait_recv()
    place_quarter(last_up[2], 1 - core, slot)
    copies[0].wait_recv()
    place_quarter(last_up[0], core, 1 - slot)
    copies[1].wait_recv()
    place_quarter(last_up[1], 1 - core, 1 - slot)
    copies[2].wait_recv()
    g_down[pl.ds(other_half, part), :] = pair_down[...].astype(F32)
    for copy in copies:
        copy.wait_send()


def share_shards(reduced, shard):
    width = reduced.shape[1]
    part = reduced.shape[0] // 2
    vmem = pl.BlockSpec(memory_space=pltpu.VMEM)
    dma = pltpu.SemaphoreType.DMA
    return pl.pallas_call(
        share_kernel,
        in_specs=[vmem],
        out_specs=[vmem] * 2,
        out_shape=[
            jax.ShapeDtypeStruct((2 * part, width), F32),
            jax.ShapeDtypeStruct((shard, 4 * width), F32),
        ],
        scratch_shapes=[
            pltpu.VMEM((part, width), BF16),
            pltpu.VMEM((3, shard, width), BF16),
            dma((4,)),
            dma((4,)),
        ],
        compiler_params=pltpu.CompilerParams(
            collective_id=4, has_side_effects=True, vmem_limit_bytes=VMEM_LIMIT
        ),
        cost_estimate=pl.CostEstimate(flops=0, bytes_accessed=8 * reduced.size, transcendentals=0),
        name="share_shards",
    )(reduced)


def turn(pair, cosine, sine):
    half = HD // 2
    lanes = lax.broadcasted_iota(jnp.int32, (1, 2 * HD), 1)
    low = lax.rem(lanes, HD) < half
    swapped = jnp.where(low, pltpu.roll(pair, 2 * HD - half, 1), pltpu.roll(pair, half, 1))
    return pair * cosine + swapped * jnp.where(low, -sine, sine)


def project_kernel(tok_ref, w_ref, b_ref, cos_ref, sin_ref, q_ref, k_ref, v_ref):
    joined = mm(tok_ref[...], w_ref[...]) + b_ref[...]
    turned = turn(joined[:, : 2 * HD], cos_ref[...], sin_ref[...])
    q_ref[...] = (turned[:, :HD].astype(BF16) * HD ** (-0.5)).astype(BF16)
    k_ref[...] = turned[:, HD:].astype(BF16)
    v_ref[...] = joined[:, 2 * HD :].astype(BF16)


def project(tokens, weight, bias, cosine, sine):
    rows, width = tokens.shape
    seq = cosine.shape[0]
    block = min(512, seq)
    per_slot = seq // block
    cols = weight.shape[1]
    head_out = jax.ShapeDtypeStruct((rows, HD), BF16)
    head_spec = pl.BlockSpec((block, HD), lambda i: (i, 0))
    return pl.pallas_call(
        project_kernel,
        grid=(rows // block,),
        in_specs=[
            pl.BlockSpec((block, width), lambda i: (i, 0)),
            pl.BlockSpec((width, cols), lambda i: (0, 0)),
            pl.BlockSpec((1, cols), lambda i: (0, 0)),
            pl.BlockSpec((block, 2 * HD), lambda i: (i % per_slot, 0)),
            pl.BlockSpec((block, 2 * HD), lambda i: (i % per_slot, 0)),
        ],
        out_specs=[head_spec] * 3,
        out_shape=[head_out] * 3,
        compiler_params=pltpu.CompilerParams(vmem_limit_bytes=VMEM_LIMIT),
        cost_estimate=pl.CostEstimate(
            flops=2 * rows * width * cols, bytes_accessed=2 * rows * width, transcendentals=0
        ),
        name="project",
    )(tokens, weight, bias, cosine, sine)


QB = 512
KB = 512


def forward_kernel(
    len_ref, core_ref, q_ref, k_ref, v_ref, out_ref, send_ref, norm_ref, *, part
):
    length = len_ref[pl.program_id(0)]
    core = core_ref[0]
    queries = q_ref[0]
    rows = queries.shape[0]

    def step(j, state):
        highest, total, mix = state
        start = pl.multiple_of(j * KB, KB)
        scores = contract(queries, k_ref[0, pl.ds(start, KB), :], 1, 1)
        ids = start + lax.broadcasted_iota(jnp.int32, (1, KB), 1)
        scores = jnp.where(ids < length, scores, NEG_FILL)
        higher = jnp.maximum(highest, jnp.max(scores, axis=1, keepdims=True))
        fade = jnp.exp(highest - higher)
        weights = jnp.exp(scores - higher)
        total = total * fade + jnp.sum(weights, axis=1, keepdims=True)
        mix = mix * fade + mm(weights.astype(BF16), v_ref[0, pl.ds(start, KB), :])
        return higher, total, mix

    blocks = (length + KB - 1) // KB
    highest, total, mix = lax.fori_loop(
        0,
        blocks,
        step,
        (
            jnp.full((rows, 1), NEG_FILL, F32),
            jnp.zeros((rows, 1), F32),
            jnp.zeros((rows, HD), F32),
        ),
    )
    mix = mix / total
    out_ref[0] = mix
    log_norm = jnp.broadcast_to(highest + jnp.log(total), (rows, 128))
    norm_ref[0] = jnp.transpose(log_norm)[0:1, :]
    low = mix.astype(BF16)
    for chip in range(rows // (2 * part)):
        for half in range(2):
            at = (2 * chip + half) * part
            send_ref[chip, half ^ core, 0] = low[at : at + part]


def attend(lengths, core, queries, keys, values, part):
    slots, seq, _ = queries.shape
    chips = seq // (2 * part)
    spec_q = pl.BlockSpec((1, QB, HD), lambda s, i, *_: (s, i, 0))
    spec_k = pl.BlockSpec((1, seq, HD), lambda s, i, *_: (s, 0, 0))
    return pl.pallas_call(
        partial(forward_kernel, part=part),
        grid_spec=pltpu.PrefetchScalarGridSpec(
            num_scalar_prefetch=2,
            grid=(slots, seq // QB),
            in_specs=[spec_q, spec_k, spec_k],
            out_specs=[
                spec_q,
                pl.BlockSpec(
                    (QB // (2 * part), 2, 1, part, HD), lambda s, i, *_: (i, 0, s, 0, 0)
                ),
                pl.BlockSpec((1, 1, QB), lambda s, i, *_: (s, 0, i)),
            ],
        ),
        out_shape=[
            jax.ShapeDtypeStruct((slots, seq, HD), F32),
            jax.ShapeDtypeStruct((chips, 2, slots, part, HD), BF16),
            jax.ShapeDtypeStruct((slots, 1, seq), F32),
        ],
        compiler_params=pltpu.CompilerParams(vmem_limit_bytes=VMEM_LIMIT),
        cost_estimate=pl.CostEstimate(
            flops=16 * slots * seq * seq * HD,
            bytes_accessed=8 * slots * seq * HD,
            transcendentals=slots * seq * seq,
        ),
        name="attend",
    )(lengths, core, queries, keys, values)


def backward_kernel(
    len_ref, q_ref, k_ref, v_ref, g_ref, norm_ref, dot_ref, dq_ref, dk_ref, dv_ref, dqt
):
    length = len_ref[pl.program_id(0)]
    j = pl.program_id(1)
    start = j * KB
    key_block = k_ref[0]
    value_block = v_ref[0]

    @pl.when(j == 0)
    def _():
        dqt[...] = jnp.zeros_like(dqt)

    turned = jnp.transpose(key_block.astype(F32)).astype(BF16)
    ids = start + lax.broadcasted_iota(jnp.int32, (KB, 1), 0)
    shift = jnp.where(ids < length, 0.0, NEG_FILL)

    def step(i, state):
        key_grad, value_grad = state
        at = pl.multiple_of(i * QB, QB)
        queries = q_ref[0, pl.ds(at, QB), :]
        grads = g_ref[0, pl.ds(at, QB), :]
        scores = contract(key_block, queries, 1, 1) + shift
        probs = jnp.exp(scores - norm_ref[0, :, pl.ds(at, QB)])
        grad_probs = contract(value_block, grads, 1, 1)
        grad_scores = (probs * (grad_probs - dot_ref[0, :, pl.ds(at, QB)])).astype(BF16)
        value_grad = value_grad + mm(probs.astype(BF16), grads)
        key_grad = key_grad + mm(grad_scores, queries)
        dqt[:, pl.ds(at, QB)] += mm(turned, grad_scores)
        return key_grad, value_grad

    blocks = jnp.where(start < length, (length + QB - 1) // QB, 0)
    zero = jnp.zeros((KB, HD), F32)
    key_grad, value_grad = lax.fori_loop(0, blocks, step, (zero, zero))
    dk_ref[0] = key_grad
    dv_ref[0] = value_grad

    @pl.when(j == pl.num_programs(1) - 1)
    def _():
        dq_ref[0] = jnp.transpose(dqt[...])


def attend_back(lengths, queries, keys, values, grads, norms, dots):
    slots, seq, _ = queries.shape
    whole = pl.BlockSpec((1, seq, HD), lambda s, j, *_: (s, 0, 0))
    block = pl.BlockSpec((1, KB, HD), lambda s, j, *_: (s, j, 0))
    row = pl.BlockSpec((1, 1, seq), lambda s, j, *_: (s, 0, 0))
    out = jax.ShapeDtypeStruct((slots, seq, HD), F32)
    return pl.pallas_call(
        backward_kernel,
        grid_spec=pltpu.PrefetchScalarGridSpec(
            num_scalar_prefetch=1,
            grid=(slots, seq // KB),
            in_specs=[whole, block, block, whole, row, row],
            out_specs=[whole, block, block],
            scratch_shapes=[pltpu.VMEM((HD, seq), F32)],
        ),
        out_shape=[out] * 3,
        compiler_params=pltpu.CompilerParams(vmem_limit_bytes=VMEM_LIMIT),
        cost_estimate=pl.CostEstimate(
            flops=40 * slots * seq * seq * HD,
            bytes_accessed=20 * slots * seq * HD,
            transcendentals=slots * seq * seq,
        ),
        name="attend_back",
    )(lengths, queries, keys, values, grads, norms, dots)


def join_kernel(
    q_ref, k_ref, v_ref, tok_ref, cos_ref, sin_ref, join_ref, grad_ref, total, bias, *, part
):
    i = pl.program_id(0)

    @pl.when(i == 0)
    def _():
        total[...] = jnp.zeros_like(total)
        bias[...] = jnp.zeros_like(bias)

    pair = jnp.concatenate([q_ref[...] * HD ** (-0.5), k_ref[...]], axis=1)
    turned = turn(pair, cos_ref[...], -sin_ref[...])
    joined = jnp.concatenate([turned, v_ref[...]], axis=1).astype(BF16)
    for chip in range(joined.shape[0] // (2 * part)):
        for core in range(2):
            at = (2 * chip + core) * part
            upper, lower = joined[at : at + part // 2], joined[at + part // 2 : at + part]
            join_ref[chip, core, 0] = jnp.concatenate([upper, lower], axis=1)
    total[...] += contract(joined, tok_ref[...], 0, 0)
    bias[...] += jnp.sum(joined.astype(F32), axis=0, keepdims=True)

    @pl.when(i == pl.num_programs(0) - 1)
    def _():
        turned_total = jnp.transpose(total[...])
        shard = turned_total.shape[0] // grad_ref.shape[0]
        extra = jnp.broadcast_to(bias[...], (grad_ref.shape[1] - shard, bias.shape[1]))
        for d in range(grad_ref.shape[0]):
            grad_ref[d, :shard] = turned_total[d * shard : (d + 1) * shard].astype(BF16)
            grad_ref[d, shard:] = extra.astype(BF16)


def join_grads(grad_q, grad_k, grad_v, tokens, cosine, sine, part, n_group):
    slots, seq, _ = grad_q.shape
    rows, width = tokens.shape
    block = min(512, seq)
    per_slot = seq // block
    cols = 3 * HD
    head = pl.BlockSpec((block, HD), lambda i: (i, 0))
    table = pl.BlockSpec((block, 2 * HD), lambda i: (i % per_slot, 0))
    chips = block // (2 * part)
    shard = width // n_group
    flat = [t.reshape(rows, HD) for t in (grad_q, grad_k, grad_v)]
    return pl.pallas_call(
        partial(join_kernel, part=part),
        grid=(rows // block,),
        in_specs=[
            head, head, head, pl.BlockSpec((block, width), lambda i: (i, 0)), table, table,
        ],
        out_specs=[
            pl.BlockSpec(
                (chips, 2, 1, part // 2, 2 * cols), lambda i: (i % per_slot, 0, i // per_slot, 0, 0)
            ),
            pl.BlockSpec((n_group, shard + 16, cols), lambda i: (0, 0, 0)),
        ],
        out_shape=[
            jax.ShapeDtypeStruct((seq // (2 * part), 2, slots, part // 2, 2 * cols), BF16),
            jax.ShapeDtypeStruct((n_group, shard + 16, cols), BF16),
        ],
        scratch_shapes=[pltpu.VMEM((cols, width), F32), pltpu.VMEM((1, cols), F32)],
        compiler_params=pltpu.CompilerParams(vmem_limit_bytes=VMEM_LIMIT),
        cost_estimate=pl.CostEstimate(
            flops=2 * rows * width * cols, bytes_accessed=2 * rows * width, transcendentals=0
        ),
        name="join_grads",
    )(*flat, tokens, cosine, sine)


def norm_forward(values, gain, shift):
    center = values - jnp.mean(values, axis=-1, keepdims=True)
    spread = jnp.mean(center * center, axis=-1, keepdims=True)
    root = lax.rsqrt(spread + LN_EPS)
    unit = center * root
    return unit * gain + shift, unit, root


def norm_backward(grad, unit, root, gain):
    scaled = grad * gain
    inner = scaled - jnp.mean(scaled, axis=-1, keepdims=True)
    inner = inner - unit * jnp.mean(scaled * unit, axis=-1, keepdims=True)
    return root * inner, jnp.sum(grad * unit, axis=0), jnp.sum(grad, axis=0)


def gelu_pair(values):
    half = 0.5 + 0.5 * lax.erf(values * 0.7071067811865476)
    bell = jnp.exp(-0.5 * values * values) * 0.3989422804014327
    return values * half, half + values * bell


def rope_rows(positions):
    halfway = HD // 2
    ladder = jnp.arange(halfway, dtype=F32) * (2.0 / HD)
    frequency = jnp.power(jnp.float32(10000.0), -ladder)
    angles = positions[:, None] * frequency[None, :]
    return jnp.cos(angles), jnp.sin(angles)


def lane_gather(mine_ref, all_ref, send_sem, recv_sem, local_sem, n_ctx, n_x):
    ctx, x = lax.axis_index("ctx"), lax.axis_index("x")
    chip = ctx * n_x + x
    routes = (
        at_device(ctx=lax.rem(ctx + 1, n_ctx)),
        at_device(ctx=lax.rem(ctx + n_ctx - 1, n_ctx)),
        at_device(x=1 - x),
    )

    def send(k, lane, own=False):
        return pltpu.make_async_remote_copy(
            mine_ref if own else all_ref.at[k], all_ref.at[k], send_sem.at[lane, k], recv_sem.at[k],
            device_id=routes[lane], device_id_type=MESH)

    local = pltpu.make_async_copy(mine_ref, all_ref.at[chip], local_sem)

    def begin():
        @pl.when(ctx + 1 < n_ctx)
        def _():
            send(chip, 0, own=True).start()

        @pl.when(ctx > 0)
        def _():
            send(chip, 1, own=True).start()

        send(chip, 2, own=True).start()
        local.start()

    def relay(r):
        for sign, lane, more in ((-1, 0, ctx + 1 < n_ctx), (1, 1, ctx > 0)):
            z = ctx + sign * r

            @pl.when((z >= 0) & (z < n_ctx))
            def _():
                k = z * n_x + x
                send(k, 0).wait_recv()

                @pl.when(more)
                def _():
                    send(k, lane).start()

                send(k, 2).start()

    def end():
        for z in range(n_ctx):
            k = z * n_x + x
            send(z * n_x + 1 - x, 0).wait_recv()

            @pl.when((z <= ctx) & (ctx + 1 < n_ctx))
            def _():
                send(k, 0).wait_send()

            @pl.when((z >= ctx) & (ctx > 0))
            def _():
                send(k, 1).wait_send()

            send(k, 2).wait_send()
        local.wait()

    return begin, relay, end


def layer_kernel(
    merged_ref, tok_ref, wo_ref, up_ref, down_ref, vec_ref, full_ref, lane_ref,
    out_ref, one_ref, gm_ref, att_ref, vecs_ref, act_out, hid_out, gdn_out, gup_out, lanes_out,
    first, first_in, hid, act, slope, gdn, gup, hidden, unit_one, two,
    roots, near, near_in, far, far_in, low_out, low_in, send_sem, recv_sem, out_sem,
    lane_send, lane_recv, *, n_ctx, n_x
):
    core, slot = lax.axis_index("core"), lax.axis_index("slot")
    twin, across = at_device(core=1 - core), at_device(slot=1 - slot)
    ctx, x = lax.axis_index("ctx"), lax.axis_index("x")
    greet([
        twin,
        across,
        at_device(x=1 - x),
        at_device(ctx=lax.rem(ctx + 1, n_ctx)),
        at_device(ctx=lax.rem(ctx + n_ctx - 1, n_ctx)),
    ])
    begin_lane, relay_lane, end_lane = lane_gather(
        lane_ref, lanes_out, lane_send, lane_recv, out_sem.at[4], n_ctx, n_x)
    begin_lane()
    rows, width = tok_ref.shape
    half = rows // 2
    tile = 256
    count = [0]
    started = []

    def launch(source, target_ref, target):
        i = count[0]
        count[0] += 1
        copy = pltpu.make_async_remote_copy(
            source, target_ref, send_sem.at[i], recv_sem.at[i],
            device_id=target, device_id_type=MESH)
        copy.start()
        started.append(copy)
        return copy

    def columns(body, n=width // tile):
        @pl.loop(0, n)
        def _(t):
            body(pl.ds(pl.multiple_of(t * tile, tile), tile))

    def chunks(body, size=64):
        @pl.loop(0, rows // size)
        def _(t):
            body(pl.ds(pl.multiple_of(t * size, size), size))

    def exchange(buf, turn, stage, product):
        halves = [
            launch(buf.at[pl.ds(h * half, half)], buf.at[pl.ds((2 + h) * rows, half)], across)
            for h in range(2)
        ]
        to_twin = launch(buf.at[pl.ds(0, rows)], buf.at[pl.ds(rows, rows)], twin)
        near_buf, far_buf = near.at[turn], far.at[turn]
        to_twin.wait_recv()
        stage(0, 2 * rows)
        product(0, 2 * rows, near_buf, 0)
        near_copy = launch(
            near_buf.at[pl.ds(rows, rows)], near_in.at[turn], twin)
        back = []
        for h in range(2):
            at = (2 + h) * rows
            halves[h].wait_recv()
            launch(
                buf.at[pl.ds(at, half)], buf.at[pl.ds(at + half, half)], twin).wait_recv()
            stage(at, rows)
            product(at, rows, far_buf, h * rows)
            i = 2 * turn + h
            launch(
                far_buf.at[pl.ds(h * rows + half, half)], far_in.at[i], twin).wait_recv()
            low_out[i] = (far_buf[pl.ds(h * rows, half), :] + far_in[i]).astype(BF16)
            back.append(launch(low_out.at[i], low_in.at[i], across))
        return near_copy, back

    def out_product(cols):
        first[:, cols] = mm(merged_ref[...], wo_ref[:, cols])

    columns(out_product)
    launch(first.at[pl.ds(rows, rows)], first_in, twin).wait_recv()

    def norm_one(at):
        values = tok_ref[at, :].astype(F32) + first[at, :] + first_in[at, :] + vec_ref[0:1, :]
        normed, unit, root = norm_forward(values, vec_ref[1:2, :], vec_ref[2:3, :])
        hidden[at, :] = normed
        unit_one[at, :] = unit
        roots[0, at, :] = jnp.broadcast_to(root, (root.shape[0], 128))
        hid[at, :] = normed.astype(BF16)

    chunks(norm_one)

    def up_stage(start, size):
        def body(cols):
            values = mm(hid[start : start + size, :], up_ref[:, cols]) + vec_ref[3:4, cols]
            active, bend = gelu_pair(values)
            act[start : start + size, cols] = active.astype(BF16)
            slope[start : start + size, cols] = bend

        columns(body)

    def down_product(start, size, target, at):
        def body(cols):
            target[at : at + size, cols] = mm(act[start : start + size, :], down_ref[:, cols])

        columns(body)

    near_copy, back = exchange(hid, 0, up_stage, down_product)
    relay_lane(1)
    out_copies = [
        pltpu.make_async_copy(hid, hid_out, out_sem.at[0]),
        pltpu.make_async_copy(act, act_out, out_sem.at[1]),
    ]
    for copy in out_copies:
        copy.start()
    vecs_ref[...] = jnp.zeros_like(vecs_ref)
    near_copy.wait_recv()

    def norm_two(at, h, local):
        downward = near[0, at, :] + near_in[0, at, :] + low_in[h, local, :].astype(F32)
        values = hidden[at, :] + downward + vec_ref[4:5, :]
        normed, unit, root = norm_forward(values, vec_ref[5:6, :], vec_ref[6:7, :])
        out_ref[at, :] = normed.astype(BF16)
        grad, gain, shift = norm_backward(full_ref[at, :], unit, root, vec_ref[5:6, :])
        two[at, :] = grad
        low = grad.astype(BF16)
        gdn[at, :] = low
        vecs_ref[5:6, :] += gain[None]
        vecs_ref[6:7, :] += shift[None]
        vecs_ref[4:5, :] += jnp.sum(low.astype(F32), axis=0, keepdims=True)

    def by_half(body, h, size=64):
        @pl.loop(0, half // size)
        def _(t):
            local = pl.multiple_of(t * size, size)
            body(pl.ds(h * half + local, size), h, pl.ds(local, size))

    for h in range(2):
        back[h].wait_recv()
        by_half(norm_two, h)

    def back_stage(start, size):
        def body(cols):
            grads = contract(gdn[start : start + size, :], down_ref[cols, :], 1, 1)
            low = (grads * slope[start : start + size, cols]).astype(BF16)
            gup[start : start + size, cols] = low
            vecs_ref[3:4, cols] += jnp.sum(low.astype(F32), axis=0, keepdims=True)

        columns(body)

    def back_product(start, size, target, at):
        def body(cols):
            target[at : at + size, cols] = contract(
                gup[start : start + size, :], up_ref[cols, :], 1, 1)

        columns(body)

    relay_lane(2)
    near_copy, back = exchange(gdn, 1, back_stage, back_product)
    for r in range(3, n_ctx):
        relay_lane(r)
    late_copies = [
        pltpu.make_async_copy(gdn, gdn_out, out_sem.at[2]),
        pltpu.make_async_copy(gup, gup_out, out_sem.at[3]),
    ]
    for copy in late_copies:
        copy.start()
    near_copy.wait_recv()

    def norm_back(at, h, local):
        grad = near[1, at, :] + near_in[1, at, :] + low_in[2 + h, local, :].astype(F32)
        grad = grad + two[at, :]
        root = roots[0, at, 0:1]
        one, gain, shift = norm_backward(grad, unit_one[at, :], root, vec_ref[1:2, :])
        one_ref[at, :] = one
        low = one.astype(BF16)
        att_ref[at, :] = low
        vecs_ref[1:2, :] += gain[None]
        vecs_ref[2:3, :] += shift[None]
        vecs_ref[0:1, :] += jnp.sum(low.astype(F32), axis=0, keepdims=True)

    for h in range(2):
        back[h].wait_recv()
        by_half(norm_back, h)
    launch(att_ref.at[pl.ds(0, rows)], att_ref.at[pl.ds(rows, rows)], twin).wait_recv()

    def merged_product(cols):
        gm_ref[:, cols] = contract(att_ref[...], wo_ref[cols, :], 1, 1).astype(BF16)

    columns(merged_product, wo_ref.shape[0] // tile)
    end_lane()
    for copy in started:
        copy.wait_send()
    for copy in out_copies + late_copies:
        copy.wait()


def layer(merged, tokens, w_out, up, down, vectors, grad_full, lane_shard):
    n_ctx, n_x = lax.axis_size("ctx"), lax.axis_size("x")
    chips = n_ctx * n_x
    rows, width = tokens.shape
    hidden = up.shape[1]
    lane = w_out.shape[0]
    vmem = pl.BlockSpec(memory_space=pltpu.VMEM)
    anywhere = pl.BlockSpec(memory_space=pl.ANY)
    dma = pltpu.SemaphoreType.DMA

    def shape(*dims, dtype=BF16):
        return jax.ShapeDtypeStruct(dims, dtype)

    def wide(*dims):
        return pltpu.VMEM(dims, F32)

    def low(*dims):
        return pltpu.VMEM(dims, BF16)

    return pl.pallas_call(
        partial(layer_kernel, n_ctx=n_ctx, n_x=n_x),
        in_specs=[vmem] * 8,
        out_specs=[vmem] * 5 + [anywhere] * 5,
        out_shape=[
            shape(rows, width),
            shape(rows, width, dtype=F32),
            shape(2 * rows, lane),
            shape(2 * rows, width),
            shape(8, width, dtype=F32),
            shape(4 * rows, hidden),
            shape(4 * rows, width),
            shape(4 * rows, width),
            shape(4 * rows, hidden),
            shape(chips, *lane_shard.shape),
        ],
        scratch_shapes=[
            wide(2 * rows, width),
            wide(rows, width),
            low(4 * rows, width),
            low(4 * rows, hidden),
            wide(4 * rows, hidden),
            low(4 * rows, width),
            low(4 * rows, hidden),
            wide(rows, width),
            wide(rows, width),
            wide(rows, width),
            wide(1, rows, 128),
            wide(2, 2 * rows, width),
            wide(2, rows, width),
            wide(2, 2 * rows, width),
            wide(4, rows // 2, width),
            low(4, rows // 2, width),
            low(4, rows // 2, width),
            dma((24,)),
            dma((24,)),
            dma((5,)),
            dma((3, chips)),
            dma((chips,)),
        ],
        compiler_params=pltpu.CompilerParams(
            collective_id=3, has_side_effects=True, vmem_limit_bytes=VMEM_LIMIT
        ),
        cost_estimate=pl.CostEstimate(
            flops=16 * rows * width * hidden, bytes_accessed=16 * rows * width, transcendentals=0
        ),
        name="layer",
    )(merged, tokens, w_out, up, down, vectors, grad_full, lane_shard)


def head_device(
    tokens,
    lengths,
    w_qkv,
    b_qkv,
    w_out,
    b_out,
    ln1_gain,
    ln1_bias,
    w_up,
    b_up,
    w_down,
    b_down,
    ln2_gain,
    ln2_bias,
    w_proj,
    cot_out,
    cot_emb,
):
    n_lane = lax.axis_size("ctx") * lax.axis_size("x")
    n_group = 2 * n_lane
    core = lax.axis_index("core")
    slot = lax.axis_index("slot")
    chip = lax.axis_index("ctx") * lax.axis_size("x") + lax.axis_index("x")
    me = 2 * chip + core
    slots, part, width = tokens.shape
    seq = part * n_group
    rows = slots * part
    shard = width // n_group
    ff_shard = w_down.shape[0]
    ff_half = ff_shard // 2
    proj = w_proj.shape[1]
    head_cols = 3 * HD

    small = jnp.concatenate(
        [b_qkv, b_out, ln1_gain, ln1_bias, b_up, b_down, ln2_gain, ln2_bias]
    )
    small_at = [0]
    for piece in (b_qkv, b_out, ln1_gain, ln1_bias, b_up, b_down, ln2_gain, ln2_bias):
        small_at.append(small_at[-1] + piece.shape[0])
    small_rows = -(-small.shape[0] // proj)
    small_rows = -(-small_rows // 16) * 16
    small = jnp.pad(small, (0, small_rows * proj - small.shape[0])).reshape(small_rows, proj)
    def two_lanes(mine, theirs):
        low_first = jnp.stack([mine, theirs], axis=0)
        high_first = jnp.stack([theirs, mine], axis=0)
        return jnp.where(core == 0, low_first, high_first)

    up_split = w_up.reshape(shard, n_lane, 2, 2, ff_half)
    up_mine = pick(up_split, core, 2)
    up_theirs = swap_core(pick(up_split, 1 - core, 2))
    up_chip = two_lanes(pick(up_mine, slot, 2), pick(up_theirs, slot, 2))
    down_split = w_down.reshape(2, ff_half, width)

    by_head = w_qkv.reshape(shard, 3, n_group, HD).transpose(2, 0, 1, 3)
    all_tokens, my_head, packed = gather_start(
        tokens,
        by_head.reshape(n_group, shard, head_cols),
        jnp.concatenate([w_proj, small], axis=0),
    )
    lane_shard = jnp.concatenate(
        [w_out, up_chip.reshape(2 * shard, n_lane * ff_half), pick(down_split, slot, 0)], axis=0
    )
    gathered = lax.all_gather(lane_shard, LANE, axis=0, tiled=False)
    out_lane = gathered[:, :shard].reshape(n_lane * shard, width)
    up = gathered[:, shard : 3 * shard].reshape(width, n_lane * ff_half)
    down = gathered[:, 3 * shard :].reshape(n_lane * ff_half, width)
    proj_full = packed[:, :shard].reshape(width, proj)
    smalls = packed[:, shard:].reshape(n_group, small_rows * proj).astype(F32)
    qkv_bias, out_bias, gain_one, shift_one, up_bias, down_bias, gain_two, shift_two = (
        smalls[:, a:b].reshape(-1) for a, b in zip(small_at[:-1], small_at[1:])
    )

    head_weight = my_head.reshape(width, head_cols)
    all_tokens = all_tokens.reshape(slots * seq, width)
    head_bias = pick(qkv_bias.reshape(1, 3, n_group, HD), me, 2).reshape(1, head_cols)
    cosine, sine = rope_rows(jnp.arange(seq, dtype=jnp.int32).astype(F32))
    cos_wide = jnp.tile(cosine, (1, 4))
    sin_wide = jnp.tile(sine, (1, 4))
    queries, keys, values = project(all_tokens, head_weight, head_bias, cos_wide, sin_wide)
    queries, keys, values = (t.reshape(slots, seq, HD) for t in (queries, keys, values))

    bias_lane = pick(up_bias.reshape(n_lane, 2, 2, ff_half), core, 1)
    up_bias_own = pick(bias_lane, slot, 1).reshape(-1)

    qkv_split = w_qkv.reshape(shard, 3, n_lane, 2, HD)
    qkv_mine = pick(qkv_split, core, 3)
    qkv_theirs = swap_core(pick(qkv_split, 1 - core, 3))
    qkv_chip = two_lanes(qkv_mine, qkv_theirs).transpose(3, 0, 1, 2, 4)
    qkv_chip = qkv_chip.reshape(n_lane, 2 * shard, head_cols)

    mixture, send, norms = attend(
        lengths, core.reshape(1).astype(jnp.int32), queries, keys, values, part
    )
    merged = lax.all_to_all(send, LANE, 0, 0, tiled=True)
    merged = merged.transpose(1, 2, 3, 0, 4).reshape(2 * rows, n_lane * HD)

    place = me * part + jnp.arange(part, dtype=jnp.int32)
    live = (place[None, :] < lengths[:, None]).reshape(rows, 1)
    grad_out = jnp.where(live, cot_out.reshape(rows, width).astype(F32), 0.0)
    grad_emb = jnp.where(live, cot_emb.reshape(rows, proj), 0)
    grad_full = grad_out + contract(grad_emb, proj_full, 1, 1)
    vectors = jnp.stack(
        [out_bias, gain_one, shift_one, up_bias_own, down_bias, gain_two, shift_two, shift_two]
    )
    (
        out_low,
        grad_one,
        grad_merged,
        grad_att,
        vector_grads,
        active,
        hidden_low,
        grad_down,
        grad_up,
        qkv_lane,
    ) = layer(
        merged, tokens.reshape(rows, width), out_lane, up, down, vectors, grad_full, qkv_chip
    )
    d_down = contract(active, grad_down, 0, 0).astype(BF16)
    d_up = contract(hidden_low, grad_up, 0, 0).astype(BF16)
    embeds = mm(out_low, proj_full).astype(BF16)
    d_proj = contract(out_low, grad_emb, 0, 0)
    (
        d_out_bias,
        d_gain_one,
        d_shift_one,
        up_bias_own_grad,
        d_down_bias,
        d_gain_two,
        d_shift_two,
    ) = (vector_grads[i] for i in range(7))
    grad_merged = grad_merged.reshape(2, slots, part, n_lane, HD).transpose(3, 0, 1, 2, 4)
    grad_heads = lax.all_to_all(grad_merged, LANE, 0, 0, tiled=True)

    def core_order(value):
        return jnp.where(core == 0, value, jnp.flip(value, axis=1))

    grad_heads = core_order(grad_heads).transpose(2, 0, 1, 3, 4).reshape(slots, seq, HD)

    d_out = contract(merged, grad_att, 0, 0).astype(BF16)

    both_ff = jnp.concatenate(
        [d_down.reshape(n_lane, 2 * shard, width), d_up.reshape(n_lane, 2 * shard, width)], axis=1
    )
    reduced = lax.psum_scatter(both_ff, LANE, scatter_dimension=0, tiled=False)
    x_at = lax.axis_index("x")
    out_rows_ = d_out.reshape(-1, 2, shard, width)
    keep_out = pick(out_rows_, x_at, 1)
    got_out = lax.ppermute(pick(out_rows_, 1 - x_at, 1), "x", SWAP)

    spread = (
        (jnp.arange(2) == core)[:, None, None] & (jnp.arange(2) == slot)[None, :, None]
    ).astype(F32)
    up_bias_grad = up_bias_own_grad.reshape(n_lane, 1, 1, ff_half) * spread[None]
    vectors = (
        d_out_bias,
        d_gain_one,
        d_shift_one,
        up_bias_grad.reshape(-1),
        d_down_bias,
        d_gain_two,
        d_shift_two,
    )
    small_grad = jnp.concatenate([v.reshape(n_group, -1) for v in vectors], axis=1)
    small_cols = small_grad.shape[1]
    vec_rows = -(-small_cols // proj)
    vec_rows = -(-(shard + vec_rows) // 16) * 16 - shard
    small_grad = jnp.pad(small_grad, ((0, 0), (0, vec_rows * proj - small_cols)))
    small_grad = jnp.concatenate(
        [d_proj.reshape(n_group, shard, proj), small_grad.reshape(n_group, vec_rows, proj)], axis=1
    )
    row_dots = jnp.sum(grad_heads.astype(F32) * mixture, axis=-1).reshape(slots, 1, seq)
    grad_q, grad_k, grad_v = attend_back(
        lengths, queries, keys, values, grad_heads, norms, row_dots
    )

    joined, d_qkv = join_grads(
        grad_q, grad_k, grad_v, all_tokens, cos_wide, sin_wide, part, n_group
    )
    grad_w_out, small_sum, grad_w_qkv, bias_rows, input_grad = finish_grads(
        keep_out,
        got_out,
        small_grad.astype(BF16),
        d_qkv,
        joined,
        qkv_lane,
        grad_one,
    )
    grad_w_proj = small_sum[:shard]
    vec_sum = small_sum[shard:].reshape(-1)
    vec_outs = []
    at = 0
    for v in vectors:
        size = v.size // n_group
        vec_outs.append(vec_sum[at : at + size])
        at += size
    (
        grad_b_out,
        grad_gain_one,
        grad_shift_one,
        grad_b_up,
        grad_b_down,
        grad_gain_two,
        grad_shift_two,
    ) = vec_outs

    reduced, input_grad = lax.optimization_barrier((reduced, input_grad))
    grad_w_down, grad_w_up = share_shards(reduced, shard)
    qkv_bias_grad = bias_rows.reshape(n_group, 3, HD).transpose(1, 0, 2).reshape(-1)
    grad_b_qkv = lax.dynamic_slice(qkv_bias_grad, (me * b_qkv.shape[0],), (b_qkv.shape[0],))

    return (
        out_low.reshape(slots, part, width),
        embeds.reshape(slots, part, proj),
        input_grad.reshape(slots, part, width),
        grad_w_qkv,
        grad_b_qkv,
        grad_w_out,
        grad_b_out,
        grad_gain_one,
        grad_shift_one,
        grad_w_up,
        grad_b_up,
        grad_w_down,
        grad_b_down,
        grad_gain_two,
        grad_shift_two,
        grad_w_proj,
    )


def layer_norm(hidden, gain, shift):
    center = hidden - jnp.mean(hidden, axis=-1, keepdims=True)
    spread = jnp.mean(center * center, axis=-1, keepdims=True)
    return center * lax.rsqrt(spread + LN_EPS) * gain + shift


def rope_tables(positions, head_width):
    halfway = head_width // 2
    ladder = jnp.arange(halfway, dtype=jnp.float32) * (2.0 / head_width)
    frequency = jnp.power(jnp.float32(10000.0), -ladder)
    angles = positions[:, None] * frequency[None, :]
    return (jnp.cos(angles)[:, None, :], jnp.sin(angles)[:, None, :])


def rotate(values, cosine, sine_part):
    halfway = values.shape[-1] // 2
    first_half = values[..., :halfway]
    second_half = values[..., halfway:]
    return jnp.concatenate(
        [
            first_half * cosine - second_half * sine_part,
            second_half * cosine + first_half * sine_part,
        ],
        axis=-1,
    )


def block_scores(query_block, key_block, key_start, length, scale):
    scores = (
        jnp.einsum("qhd,khd->hqk", query_block, key_block, preferred_element_type=jnp.float32)
        * scale
    )
    key_ids = key_start + jnp.arange(key_block.shape[0], dtype=jnp.int32)
    return jnp.where((key_ids < length)[None, None, :], scores, NEG_FILL)


def per_device(
    tokens,
    lengths,
    w_qkv,
    b_qkv,
    w_out,
    b_out,
    ln1_gain,
    ln1_bias,
    w_up,
    b_up,
    w_down,
    b_down,
    ln2_gain,
    ln2_bias,
    w_proj,
    cot_out,
    cot_emb,
):
    n_fsdp = lax.axis_size("fsdp")
    n_ctx = lax.axis_size("ctx")
    ctx_at = lax.axis_index("ctx")
    fsdp_at = lax.axis_index("fsdp")
    groups, tok_slot, width = tokens.shape
    heads_here = H // n_fsdp
    lane_width = heads_here * HD
    span_rows = tok_slot * n_fsdp
    key_count = span_rows * n_ctx
    row_count = groups * tok_slot
    scale = HD ** (-0.5)
    query_rows = min(512, span_rows)
    key_rows = min(2048, key_count // 4)
    query_blocks = span_rows // query_rows
    key_blocks = key_count // key_rows
    key_starts = jnp.arange(key_blocks, dtype=jnp.int32) * key_rows
    qkv_full, qkv_bias, out_full, out_bias, gain_one, shift_one = (
        lax.all_gather(w_qkv, ("ctx", "fsdp"), axis=0, tiled=True),
        lax.all_gather(b_qkv, ("ctx", "fsdp"), axis=0, tiled=True),
        lax.all_gather(w_out, ("ctx", "fsdp"), axis=0, tiled=True),
        lax.all_gather(b_out, ("ctx", "fsdp"), axis=0, tiled=True),
        lax.all_gather(ln1_gain, ("ctx", "fsdp"), axis=0, tiled=True),
        lax.all_gather(ln1_bias, ("ctx", "fsdp"), axis=0, tiled=True),
    )
    token_pos = (ctx_at * n_fsdp + fsdp_at) * tok_slot + jnp.arange(tok_slot, dtype=jnp.int32)
    live_rows = (token_pos[None, :] < lengths[:, None]).reshape(row_count, 1)
    flat_tokens = tokens.reshape(row_count, width)
    joined = jnp.dot(flat_tokens, qkv_full, preferred_element_type=jnp.float32) + qkv_bias.astype(
        jnp.float32
    )
    cosine, sine_part = rope_tables(token_pos.astype(jnp.float32), HD)
    split_heads = joined.reshape(groups, tok_slot, 3, H, HD)
    rotated_query = rotate(split_heads[:, :, 0], cosine, sine_part)
    rotated_key = rotate(split_heads[:, :, 1], cosine, sine_part)
    packed = (
        jnp.stack([rotated_query, rotated_key, split_heads[:, :, 2]], axis=2)
        .astype(jnp.bfloat16)
        .reshape(groups, tok_slot, 3, n_fsdp, lane_width)
    )
    by_heads = lax.all_to_all(packed, "fsdp", split_axis=3, concat_axis=1, tiled=True)
    queries = by_heads[:, :, 0, 0]
    local_keys = by_heads[:, :, 1, 0]
    local_values = by_heads[:, :, 2, 0]
    all_keys, all_values = (
        lax.all_gather(local_keys, "ctx", axis=1, tiled=True),
        lax.all_gather(local_values, "ctx", axis=1, tiled=True),
    )

    def attend_slot(slot_item):
        slot_queries, slot_keys, slot_values, length = slot_item
        query_split = slot_queries.reshape(query_blocks, query_rows, heads_here, HD)
        key_split = slot_keys.reshape(key_blocks, key_rows, heads_here, HD)
        value_split = slot_values.reshape(key_blocks, key_rows, heads_here, HD)

        def per_query(query_block):

            def row_stats(state_pair, key_item):
                highest, running_sum = state_pair
                scores = block_scores(query_block, key_item[0], key_item[1], length, scale)
                new_high = jnp.maximum(highest, jnp.max(scores, axis=-1))
                running_sum = running_sum * jnp.exp(highest - new_high) + jnp.sum(
                    jnp.exp(scores - new_high[..., None]), axis=-1
                )
                return ((new_high, running_sum), None)

            start_state = (
                jnp.full((heads_here, query_rows), NEG_FILL, jnp.float32),
                jnp.zeros((heads_here, query_rows), jnp.float32),
            )
            highest, running_sum = lax.scan(row_stats, start_state, (key_split, key_starts))[0]
            log_norm = highest + jnp.log(running_sum)

            def weigh_values(accumulated, key_item):
                scores = block_scores(query_block, key_item[0], key_item[2], length, scale)
                weights = jnp.exp(scores - log_norm[..., None]).astype(jnp.bfloat16)
                return (
                    accumulated
                    + jnp.einsum(
                        "hqk,khd->qhd", weights, key_item[1], preferred_element_type=jnp.float32
                    ),
                    None,
                )

            mixture = lax.scan(
                weigh_values,
                jnp.zeros((query_rows, heads_here, HD), jnp.float32),
                (key_split, value_split, key_starts),
            )[0]
            return (mixture, log_norm)

        mixture, log_norm = lax.map(per_query, query_split)
        return (mixture.reshape(span_rows, lane_width), log_norm)

    mixture, log_norms = lax.map(attend_slot, (queries, all_keys, all_values, lengths))
    merged = lax.all_to_all(
        mixture.astype(jnp.bfloat16).reshape(groups, span_rows, 1, lane_width),
        "fsdp",
        split_axis=1,
        concat_axis=2,
        tiled=True,
    ).reshape(row_count, width)
    attended = jnp.dot(merged, out_full, preferred_element_type=jnp.float32) + out_bias.astype(
        jnp.float32
    )
    hidden_one, pull_one = jax.vjp(
        layer_norm,
        flat_tokens.astype(jnp.float32) + attended,
        gain_one.astype(jnp.float32),
        shift_one.astype(jnp.float32),
    )
    hidden_low = hidden_one.astype(jnp.bfloat16)
    up_full, up_bias, down_full, down_bias, gain_two, shift_two, proj_full = (
        lax.all_gather(w_up, ("ctx", "fsdp"), axis=0, tiled=True),
        lax.all_gather(b_up, ("ctx", "fsdp"), axis=0, tiled=True),
        lax.all_gather(w_down, ("ctx", "fsdp"), axis=0, tiled=True),
        lax.all_gather(b_down, ("ctx", "fsdp"), axis=0, tiled=True),
        lax.all_gather(ln2_gain, ("ctx", "fsdp"), axis=0, tiled=True),
        lax.all_gather(ln2_bias, ("ctx", "fsdp"), axis=0, tiled=True),
        lax.all_gather(w_proj, ("ctx", "fsdp"), axis=0, tiled=True),
    )
    upward = jnp.dot(hidden_low, up_full, preferred_element_type=jnp.float32) + up_bias.astype(
        jnp.float32
    )
    active_full, pull_gelu = jax.vjp(partial(jax.nn.gelu, approximate=False), upward)
    active = active_full.astype(jnp.bfloat16)
    downward = jnp.dot(active, down_full, preferred_element_type=jnp.float32) + down_bias.astype(
        jnp.float32
    )
    out_full_rows, pull_two = jax.vjp(
        layer_norm,
        hidden_one + downward,
        gain_two.astype(jnp.float32),
        shift_two.astype(jnp.float32),
    )
    out_low = out_full_rows.astype(jnp.bfloat16)
    projected = jnp.dot(out_low, proj_full, preferred_element_type=jnp.float32)
    back_qkv, back_qkv_bias, back_out, back_out_bias, back_gain_one, back_shift_one = (
        lax.all_gather(w_qkv, ("ctx", "fsdp"), axis=0, tiled=True),
        lax.all_gather(b_qkv, ("ctx", "fsdp"), axis=0, tiled=True),
        lax.all_gather(w_out, ("ctx", "fsdp"), axis=0, tiled=True),
        lax.all_gather(b_out, ("ctx", "fsdp"), axis=0, tiled=True),
        lax.all_gather(ln1_gain, ("ctx", "fsdp"), axis=0, tiled=True),
        lax.all_gather(ln1_bias, ("ctx", "fsdp"), axis=0, tiled=True),
    )
    back_up, back_up_bias, back_down, back_down_bias, back_gain_two, back_shift_two, back_proj = (
        lax.all_gather(w_up, ("ctx", "fsdp"), axis=0, tiled=True),
        lax.all_gather(b_up, ("ctx", "fsdp"), axis=0, tiled=True),
        lax.all_gather(w_down, ("ctx", "fsdp"), axis=0, tiled=True),
        lax.all_gather(b_down, ("ctx", "fsdp"), axis=0, tiled=True),
        lax.all_gather(ln2_gain, ("ctx", "fsdp"), axis=0, tiled=True),
        lax.all_gather(ln2_bias, ("ctx", "fsdp"), axis=0, tiled=True),
        lax.all_gather(w_proj, ("ctx", "fsdp"), axis=0, tiled=True),
    )
    grad_out = jnp.where(live_rows, cot_out.reshape(row_count, width).astype(jnp.float32), 0.0)
    grad_emb = jnp.where(live_rows, cot_emb.reshape(row_count, -1), 0)
    d_proj = jnp.einsum("rd,rp->dp", out_low, grad_emb, preferred_element_type=jnp.float32)
    grad_full = grad_out + jnp.einsum(
        "rp,dp->rd", grad_emb, back_proj, preferred_element_type=jnp.float32
    )
    grad_two, d_gain_two, d_shift_two = pull_two(grad_full)
    grad_down = grad_two.astype(jnp.bfloat16)
    d_down = jnp.einsum("rf,rd->fd", active, grad_down, preferred_element_type=jnp.float32)
    d_down_bias = jnp.sum(grad_down.astype(jnp.float32), axis=0)
    grad_act = jnp.einsum("rd,fd->rf", grad_down, back_down, preferred_element_type=jnp.float32)
    grad_up = pull_gelu(grad_act)[0].astype(jnp.bfloat16)
    d_up = jnp.einsum("rd,rf->df", hidden_low, grad_up, preferred_element_type=jnp.float32)
    d_up_bias = jnp.sum(grad_up.astype(jnp.float32), axis=0)
    grad_hidden = grad_two + jnp.einsum(
        "rf,df->rd", grad_up, back_up, preferred_element_type=jnp.float32
    )
    grad_one, d_gain_one, d_shift_one = pull_one(grad_hidden)
    grad_att = grad_one.astype(jnp.bfloat16)
    d_out = jnp.einsum("rd,re->de", merged, grad_att, preferred_element_type=jnp.float32)
    d_out_bias = jnp.sum(grad_att.astype(jnp.float32), axis=0)
    grad_merged = jnp.einsum(
        "re,de->rd", grad_att, back_out, preferred_element_type=jnp.float32
    ).astype(jnp.bfloat16)
    grad_heads = lax.all_to_all(
        grad_merged.reshape(groups, tok_slot, n_fsdp, lane_width),
        "fsdp",
        split_axis=2,
        concat_axis=1,
        tiled=True,
    ).reshape(groups, span_rows, lane_width)

    def attend_back(slot_item):
        slot_queries, slot_keys, slot_values, grad_mix, log_norm, length = slot_item
        query_split = slot_queries.reshape(query_blocks, query_rows, heads_here, HD)
        key_split = slot_keys.reshape(key_blocks, key_rows, heads_here, HD)
        value_split = slot_values.reshape(key_blocks, key_rows, heads_here, HD)
        grad_split = grad_mix.reshape(query_blocks, query_rows, heads_here, HD)

        def value_pass(value_total, query_item):
            query_block, grad_block, norm_block = query_item

            def value_per_key(row_dot, key_item):
                key_block, value_block, key_start = key_item
                scores = block_scores(query_block, key_block, key_start, length, scale)
                probability = jnp.exp(scores - norm_block[..., None])
                grad_probs = jnp.einsum(
                    "qhd,khd->hqk", grad_block, value_block, preferred_element_type=jnp.float32
                )
                value_part = jnp.einsum(
                    "hqk,qhd->khd",
                    probability.astype(jnp.bfloat16),
                    grad_block,
                    preferred_element_type=jnp.float32,
                )
                return (row_dot + jnp.sum(probability * grad_probs, axis=-1), value_part)

            row_dot, value_parts = lax.scan(
                value_per_key,
                jnp.zeros((heads_here, query_rows), jnp.float32),
                (key_split, value_split, key_starts),
            )
            return (value_total + value_parts.reshape(key_count, heads_here, HD), row_dot)

        value_grad, row_dots = lax.scan(
            value_pass,
            jnp.zeros((key_count, heads_here, HD), jnp.float32),
            (query_split, grad_split, log_norm),
        )

        def key_pass(key_total, query_item):
            query_block, grad_block, norm_block, dot_block = query_item

            def key_per_key(query_accum, key_item):
                key_block, value_block, key_start = key_item
                scores = block_scores(query_block, key_block, key_start, length, scale)
                probability = jnp.exp(scores - norm_block[..., None])
                grad_probs = jnp.einsum(
                    "qhd,khd->hqk", grad_block, value_block, preferred_element_type=jnp.float32
                )
                grad_scores = (probability * (grad_probs - dot_block[..., None])).astype(
                    jnp.bfloat16
                )
                query_accum = query_accum + jnp.einsum(
                    "hqk,khd->qhd", grad_scores, key_block, preferred_element_type=jnp.float32
                )
                key_part = jnp.einsum(
                    "hqk,qhd->khd", grad_scores, query_block, preferred_element_type=jnp.float32
                )
                return (query_accum, key_part)

            query_grad, key_parts = lax.scan(
                key_per_key,
                jnp.zeros((query_rows, heads_here, HD), jnp.float32),
                (key_split, value_split, key_starts),
            )
            return (key_total + key_parts.reshape(key_count, heads_here, HD), query_grad)

        key_grad, query_grads = lax.scan(
            key_pass,
            jnp.zeros((key_count, heads_here, HD), jnp.float32),
            (query_split, grad_split, log_norm, row_dots),
        )
        return (
            query_grads.reshape(span_rows, lane_width) * scale,
            key_grad.reshape(key_count, lane_width) * scale,
            value_grad.reshape(key_count, lane_width),
        )

    grad_queries, key_terms, value_terms = lax.map(
        attend_back, (queries, all_keys, all_values, grad_heads, log_norms, lengths)
    )
    grad_keys, grad_values = (
        lax.psum_scatter(
            key_terms.astype(jnp.bfloat16), "ctx", scatter_dimension=1, tiled=True
        ).astype(jnp.float32),
        lax.psum_scatter(
            value_terms.astype(jnp.bfloat16), "ctx", scatter_dimension=1, tiled=True
        ).astype(jnp.float32),
    )
    head_pos = (ctx_at * span_rows + jnp.arange(span_rows, dtype=jnp.int32)).astype(jnp.float32)
    head_cosine, head_sine = rope_tables(head_pos, HD)
    query_back = rotate(
        grad_queries.reshape(groups, span_rows, heads_here, HD), head_cosine, -head_sine
    )
    key_back = rotate(grad_keys.reshape(groups, span_rows, heads_here, HD), head_cosine, -head_sine)
    value_back = grad_values.reshape(groups, span_rows, heads_here, HD)
    grad_pack = (
        jnp.stack([query_back, key_back, value_back], axis=2)
        .astype(jnp.bfloat16)
        .reshape(groups, span_rows, 3, 1, lane_width)
    )
    grad_joined = lax.all_to_all(
        grad_pack, "fsdp", split_axis=1, concat_axis=3, tiled=True
    ).reshape(row_count, 3 * width)
    d_qkv = jnp.einsum("rd,re->de", flat_tokens, grad_joined, preferred_element_type=jnp.float32)
    d_qkv_bias = jnp.sum(grad_joined.astype(jnp.float32), axis=0)
    input_grad = (
        jnp.einsum("re,de->rd", grad_joined, back_qkv, preferred_element_type=jnp.float32)
        + grad_one
    ).astype(jnp.bfloat16)
    shards = (
        lax.psum_scatter(d_qkv, ("ctx", "fsdp"), scatter_dimension=0, tiled=True),
        lax.psum_scatter(d_qkv_bias, ("ctx", "fsdp"), scatter_dimension=0, tiled=True),
        lax.psum_scatter(d_out, ("ctx", "fsdp"), scatter_dimension=0, tiled=True),
        lax.psum_scatter(d_out_bias, ("ctx", "fsdp"), scatter_dimension=0, tiled=True),
        lax.psum_scatter(d_gain_one, ("ctx", "fsdp"), scatter_dimension=0, tiled=True),
        lax.psum_scatter(d_shift_one, ("ctx", "fsdp"), scatter_dimension=0, tiled=True),
        lax.psum_scatter(d_up, ("ctx", "fsdp"), scatter_dimension=0, tiled=True),
        lax.psum_scatter(d_up_bias, ("ctx", "fsdp"), scatter_dimension=0, tiled=True),
        lax.psum_scatter(d_down, ("ctx", "fsdp"), scatter_dimension=0, tiled=True),
        lax.psum_scatter(d_down_bias, ("ctx", "fsdp"), scatter_dimension=0, tiled=True),
        lax.psum_scatter(d_gain_two, ("ctx", "fsdp"), scatter_dimension=0, tiled=True),
        lax.psum_scatter(d_shift_two, ("ctx", "fsdp"), scatter_dimension=0, tiled=True),
        lax.psum_scatter(d_proj, ("ctx", "fsdp"), scatter_dimension=0, tiled=True),
    )
    totals = (
        lax.psum(shards[0].astype(jnp.bfloat16), "slot").astype(jnp.float32),
        lax.psum(shards[1].astype(jnp.bfloat16), "slot").astype(jnp.float32),
        lax.psum(shards[2].astype(jnp.bfloat16), "slot").astype(jnp.float32),
        lax.psum(shards[3].astype(jnp.bfloat16), "slot").astype(jnp.float32),
        lax.psum(shards[4].astype(jnp.bfloat16), "slot").astype(jnp.float32),
        lax.psum(shards[5].astype(jnp.bfloat16), "slot").astype(jnp.float32),
        lax.psum(shards[6].astype(jnp.bfloat16), "slot").astype(jnp.float32),
        lax.psum(shards[7].astype(jnp.bfloat16), "slot").astype(jnp.float32),
        lax.psum(shards[8].astype(jnp.bfloat16), "slot").astype(jnp.float32),
        lax.psum(shards[9].astype(jnp.bfloat16), "slot").astype(jnp.float32),
        lax.psum(shards[10].astype(jnp.bfloat16), "slot").astype(jnp.float32),
        lax.psum(shards[11].astype(jnp.bfloat16), "slot").astype(jnp.float32),
        lax.psum(shards[12].astype(jnp.bfloat16), "slot").astype(jnp.float32),
    )
    return (
        out_low.reshape(groups, tok_slot, width),
        projected.astype(jnp.bfloat16).reshape(groups, tok_slot, -1),
        input_grad.reshape(groups, tok_slot, width),
        totals[0],
        totals[1],
        totals[2],
        totals[3],
        totals[4],
        totals[5],
        totals[6],
        totals[7],
        totals[8],
        totals[9],
        totals[10],
        totals[11],
        totals[12],
    )


def solution(mesh):
    n_slot, n_ctx, n_fsdp = (mesh.shape[a] for a in ("slot", "ctx", "fsdp"))
    rows_axes = ("ctx", "fsdp")
    step = per_device
    if n_slot == 2 and n_fsdp % 2 == 0 and n_ctx * n_fsdp == H:
        mesh = Mesh(
            mesh.devices.reshape(n_slot, n_ctx, n_fsdp // 2, 2), ("slot", "ctx", "x", "core")
        )
        rows_axes = GROUP
        step = head_device
    in_specs = (
        P("slot", rows_axes, None),
        P("slot"),
        P(rows_axes, None),
        P(rows_axes),
        P(rows_axes, None),
        P(rows_axes),
        P(rows_axes),
        P(rows_axes),
        P(rows_axes, None),
        P(rows_axes),
        P(rows_axes, None),
        P(rows_axes),
        P(rows_axes),
        P(rows_axes),
        P(rows_axes, None),
        P("slot", rows_axes, None),
        P("slot", rows_axes, None),
    )
    out_specs = (
        P("slot", rows_axes, None),
        P("slot", rows_axes, None),
        P("slot", rows_axes, None),
        P(rows_axes, None),
        P(rows_axes),
        P(rows_axes, None),
        P(rows_axes),
        P(rows_axes),
        P(rows_axes),
        P(rows_axes, None),
        P(rows_axes),
        P(rows_axes, None),
        P(rows_axes),
        P(rows_axes),
        P(rows_axes),
        P(rows_axes, None),
    )
    return jax.shard_map(
        step, mesh=mesh, in_specs=in_specs, out_specs=out_specs, check_vma=False
    )
```

```python
from functools import partial

import jax
import jax.numpy as jnp
from jax import lax
from jax.experimental import pallas as pl
from jax.experimental.pallas import tpu as pltpu
from jax.sharding import Mesh
from jax.sharding import PartitionSpec as P

H = 16
HD = 64
LN_EPS = 1e-05
NEG_FILL = -1e30
F32 = jnp.float32
BF16 = jnp.bfloat16
GROUP = ("ctx", "x", "core")
LANE = ("ctx", "x")
SWAP = [(0, 1), (1, 0)]
VMEM_LIMIT = 60 * 1024 * 1024


def mm(left, right):
    return jnp.dot(left, right, preferred_element_type=F32)


def contract(left, right, left_dim, right_dim):
    return lax.dot_general(
        left, right, (((left_dim,), (right_dim,)), ((), ())), preferred_element_type=F32
    )


def swap_core(value):
    return lax.ppermute(value, "core", SWAP)


def swap_slot(value):
    return lax.ppermute(value, "slot", SWAP)


def pick(stacked, index, axis):
    return lax.dynamic_index_in_dim(stacked, index, axis, keepdims=False)


MESH = pl.DeviceIdType.MESH


def at_device(**where):
    names = ("slot", "ctx", "x", "core")
    return tuple(where[n] if n in where else lax.axis_index(n) for n in names)


def greet(peers):
    barrier = pltpu.get_barrier_semaphore()
    for peer in peers:
        pl.semaphore_signal(barrier, inc=1, device_id=peer, device_id_type=MESH)
    pl.semaphore_wait(barrier, len(peers))


def group_peers(n_ctx, n_x):
    ctx, x, core = (lax.axis_index(n) for n in GROUP)
    peers = []
    for dz in range(n_ctx):
        for dx in range(n_x):
            for dc in range(2):
                if dz or dx or dc:
                    where = (lax.rem(ctx + dz, n_ctx), lax.rem(x + dx, n_x), lax.rem(core + dc, 2))
                    peers.append(where)
    return peers


def start_kernel(
    tok_ref, head_ref, small_ref, all_ref, heads_ref, smalls_ref,
    far_send, block_send, local_sem, head_recv, small_recv, block_recv, *, n_ctx, n_x
):
    part = tok_ref.shape[1]
    ctx, x, core = (lax.axis_index(n) for n in GROUP)
    me = (ctx * n_x + x) * 2 + core
    peers = group_peers(n_ctx, n_x)
    greet([at_device(ctx=z, x=a, core=c) for z, a, c in peers])

    def block_at(b):
        return all_ref.at[:, pl.ds(pl.multiple_of(b * part, part), part), :]

    pushes = []
    for k, (z, a, c) in enumerate(peers):
        them = (z * n_x + a) * 2 + c
        target = at_device(ctx=z, x=a, core=c)
        pushes.append(pltpu.make_async_remote_copy(
            head_ref.at[them], heads_ref.at[me], far_send.at[2 * k], head_recv.at[me],
            device_id=target, device_id_type=MESH))
        pushes.append(pltpu.make_async_remote_copy(
            small_ref, smalls_ref.at[me], far_send.at[2 * k + 1], small_recv.at[me],
            device_id=target, device_id_type=MESH))
    locals_ = [
        pltpu.make_async_copy(tok_ref, block_at(me), local_sem.at[0]),
        pltpu.make_async_copy(head_ref.at[me], heads_ref.at[me], local_sem.at[1]),
        pltpu.make_async_copy(small_ref, smalls_ref.at[me], local_sem.at[2]),
    ]

    def send(b, source, lane, target):
        return pltpu.make_async_remote_copy(
            source, block_at(b), block_send.at[lane, b], block_recv.at[b],
            device_id=target, device_id_type=MESH)

    up = at_device(ctx=lax.rem(ctx + 1, n_ctx))
    down = at_device(ctx=lax.rem(ctx + n_ctx - 1, n_ctx))
    side = at_device(x=1 - x)
    twin = at_device(core=1 - core)

    def here(b):
        return send(b, block_at(b), 0, twin)

    @pl.when(ctx + 1 < n_ctx)
    def _():
        send(me, tok_ref, 0, up).start()

    @pl.when(ctx > 0)
    def _():
        send(me, tok_ref, 1, down).start()

    send(me, tok_ref, 2, side).start()
    send(me, tok_ref, 3, twin).start()
    for copy in locals_:
        copy.start()

    for r in range(1, n_ctx):
        if r == n_ctx - 1:
            for push in pushes:
                push.start()
        low = ctx - r
        high = ctx + r

        @pl.when(low >= 0)
        def _():
            b = (low * n_x + x) * 2 + core
            here(b).wait_recv()

            @pl.when(ctx + 1 < n_ctx)
            def _():
                send(b, block_at(b), 0, up).start()

            send(b, block_at(b), 2, side).start()
            send(b, block_at(b), 3, twin).start()

        @pl.when(high < n_ctx)
        def _():
            b = (high * n_x + x) * 2 + core
            here(b).wait_recv()

            @pl.when(ctx > 0)
            def _():
                send(b, block_at(b), 1, down).start()

            send(b, block_at(b), 2, side).start()
            send(b, block_at(b), 3, twin).start()

    def from_side(z):
        b = (z * n_x + (1 - x)) * 2 + core
        here(b).wait_recv()
        send(b, block_at(b), 3, twin).start()

    from_side(ctx)
    for r in range(1, n_ctx):
        @pl.when(ctx - r >= 0)
        def _():
            from_side(ctx - r)

        @pl.when(ctx + r < n_ctx)
        def _():
            from_side(ctx + r)

    for z in range(n_ctx):
        for a in range(n_x):
            here((z * n_x + a) * 2 + 1 - core).wait_recv()
    for k, (z, a, c) in enumerate(peers):
        them = (z * n_x + a) * 2 + c
        pltpu.make_async_remote_copy(
            head_ref.at[them], heads_ref.at[them], far_send.at[2 * k], head_recv.at[them],
            device_id=twin, device_id_type=MESH).wait_recv()
        pltpu.make_async_remote_copy(
            small_ref, smalls_ref.at[them], far_send.at[2 * k + 1], small_recv.at[them],
            device_id=twin, device_id_type=MESH).wait_recv()
    for push in pushes:
        push.wait_send()
    for copy in locals_:
        copy.wait()

    for z in range(n_ctx):
        b = (z * n_x + x) * 2 + core

        @pl.when((z <= ctx) & (ctx + 1 < n_ctx))
        def _():
            send(b, block_at(b), 0, up).wait_send()

        @pl.when((z >= ctx) & (ctx > 0))
        def _():
            send(b, block_at(b), 1, down).wait_send()

        send(b, block_at(b), 2, side).wait_send()
        send(b, block_at(b), 3, twin).wait_send()
        other = (z * n_x + (1 - x)) * 2 + core
        send(other, block_at(other), 3, twin).wait_send()


def gather_start(tokens, heads, small):
    n_ctx, n_x = lax.axis_size("ctx"), lax.axis_size("x")
    n = 2 * n_ctx * n_x
    slots, part, width = tokens.shape
    vmem = pl.BlockSpec(memory_space=pltpu.VMEM)
    anywhere = pl.BlockSpec(memory_space=pl.ANY)
    dma = pltpu.SemaphoreType.DMA
    return pl.pallas_call(
        partial(start_kernel, n_ctx=n_ctx, n_x=n_x),
        in_specs=[vmem, vmem, vmem],
        out_specs=[anywhere, vmem, vmem],
        out_shape=[
            jax.ShapeDtypeStruct((slots, n * part, width), tokens.dtype),
            jax.ShapeDtypeStruct(heads.shape, heads.dtype),
            jax.ShapeDtypeStruct((n,) + small.shape, small.dtype),
        ],
        scratch_shapes=[
            dma((2 * (n - 1),)), dma((4, n)), dma((3,)), dma((n,)), dma((n,)), dma((n,))
        ],
        compiler_params=pltpu.CompilerParams(
            collective_id=1, has_side_effects=True, vmem_limit_bytes=VMEM_LIMIT
        ),
        cost_estimate=pl.CostEstimate(
            flops=0, bytes_accessed=2 * n * tokens.size, transcendentals=0
        ),
        name="gather_start",
    )(tokens, heads, small)


def finish_kernel(
    out_ref, x_out, small_ref, qkv_ref, red_ref, join_ref, weight_ref, one_ref,
    g_down, g_up, g_out, g_small, g_qkv, g_bias, g_in,
    s_out, z_out, own_out, smalls, own_small, pair_small, pair_qkv, sum_qkv, qkvs,
    pair_down, pair_out, last_up, joins, partial_in, pair_in,
    join_send, join_recv, far_send, small_recv, qkv_recv, z_send, z_recv, y_send, y_recv,
    *, n_ctx, n_x
):
    ctx, x, core = (lax.axis_index(n) for n in GROUP)
    slot = lax.axis_index("slot")
    chip = ctx * n_x + x
    me = 2 * chip + core
    shard, width = g_out.shape
    part = g_down.shape[0] // 2
    peers = group_peers(n_ctx, n_x)
    lane_peers = [(z, a) for z, a, c in peers[1::2]]
    across = at_device(slot=1 - slot)
    corner = at_device(slot=1 - slot, core=1 - core)
    twin = at_device(core=1 - core)
    greet([at_device(ctx=z, x=a, core=c) for z, a, c in peers] + [across, corner])

    def remote(source, target_ref, send_sem, recv_sem, target):
        return pltpu.make_async_remote_copy(
            source, target_ref, send_sem, recv_sem, device_id=target, device_id_type=MESH)

    started = []

    def launch(copy):
        copy.start()
        started.append(copy)
        return copy

    def pair_copy(i, source, target_ref, target):
        return launch(remote(source, target_ref, y_send.at[i], y_recv.at[i], target))

    qkv_copy = pair_copy(0, qkv_ref, pair_qkv, across)
    mine = pl.multiple_of(part + core * shard, shard)
    theirs = pl.multiple_of(part + (1 - core) * shard, shard)
    for k, (z, a, c) in enumerate(peers):
        them = (z * n_x + a) * 2 + c
        launch(remote(
            small_ref.at[them], smalls.at[me], far_send.at[2 * k + 1], small_recv.at[me],
            at_device(ctx=z, x=a, core=c)))
    smalls[me] = small_ref[me]
    for k, (z, a) in enumerate(lane_peers):
        launch(remote(
            join_ref.at[z * n_x + a], joins.at[chip], join_send.at[k], join_recv.at[chip],
            at_device(ctx=z, x=a)))
    down_copy = pair_copy(4, red_ref.at[pl.ds(0, part)], pair_down, across)
    quarter_copies = [
        pair_copy(5, red_ref.at[pl.ds(theirs, shard)], last_up.at[0], twin),
        pair_copy(6, red_ref.at[pl.ds(mine, shard)], last_up.at[1], across),
        pair_copy(7, red_ref.at[pl.ds(theirs, shard)], last_up.at[2], corner),
    ]

    second_out = []
    for j in range(n_ctx):
        place = lax.rem(ctx + 1 + j, n_ctx)
        sum_out = out_ref[place].astype(F32) + x_out[place].astype(F32)
        if j < n_ctx - 1:
            s_out[j] = sum_out.astype(BF16)
            second_out.append(launch(remote(
                s_out.at[j], z_out.at[j], z_send.at[j], z_recv.at[j], at_device(ctx=place))))
        else:
            own_out[...] = sum_out

    qkv_copy.wait_recv()
    sum_qkv[...] = (qkv_ref[...].astype(F32) + pair_qkv[...].astype(F32)).astype(BF16)
    for k, (z, a, c) in enumerate(peers):
        them = (z * n_x + a) * 2 + c
        launch(remote(
            sum_qkv.at[them], qkvs.at[me], far_send.at[2 * k], qkv_recv.at[me],
            at_device(ctx=z, x=a, core=c)))
    qkvs[me] = sum_qkv[me]

    def add_head(source, rows_of, first):
        weight = jnp.concatenate(
            [weight_ref[b, source] for b in range(weight_ref.shape[0])], axis=0)
        for h in range(2):
            owner = core if h == 0 else 1 - core
            rows = rows_of(owner)
            cols = rows.shape[2] // 2
            rows = jnp.concatenate(
                [r for t in range(rows.shape[0]) for r in (rows[t, :, :cols], rows[t, :, cols:])],
                axis=0)
            term = contract(rows, weight, 1, 1)
            partial_in[h] = term if first else partial_in[h] + term

    add_head(chip, lambda owner: join_ref[chip, owner], True)

    half = pl.multiple_of(slot * part, part)
    other_half = pl.multiple_of((1 - slot) * part, part)
    g_down[pl.ds(half, part), :] = red_ref[pl.ds(0, part), :].astype(F32)
    down_copy.wait_recv()
    g_down[pl.ds(other_half, part), :] = pair_down[...].astype(F32)

    def place_quarter(rows, quarter_core, quarter_slot):
        for k in range(n_ctx * n_x):
            at = pl.multiple_of(((2 * k + quarter_core) * 2 + quarter_slot) * part, part)
            g_up[:, pl.ds(at, part)] = rows[:, k * part : (k + 1) * part].astype(F32)

    place_quarter(red_ref[pl.ds(mine, shard), :], core, slot)
    quarter_copies[0].wait_recv()
    place_quarter(last_up[0], 1 - core, slot)
    quarter_copies[1].wait_recv()
    place_quarter(last_up[1], core, 1 - slot)
    quarter_copies[2].wait_recv()
    place_quarter(last_up[2], 1 - core, 1 - slot)

    for z, a, c in peers:
        them = (z * n_x + a) * 2 + c
        remote(
            small_ref.at[them], smalls.at[them], far_send.at[1], small_recv.at[them], twin
        ).wait_recv()
    own_small[...] = jnp.sum(smalls[...].astype(F32), axis=0).astype(BF16)
    small_copy = pair_copy(1, own_small, pair_small, across)

    for k, (z, a) in enumerate(lane_peers):
        source = z * n_x + a
        remote(
            join_ref.at[source], joins.at[source], join_send.at[k], join_recv.at[source], twin
        ).wait_recv()
        add_head(source, lambda owner: joins[source, owner], False)
    in_copy = pair_copy(2, partial_in.at[1], pair_in, twin)

    for j in range(n_ctx - 1):
        second_out[j].wait_recv()
        own_out[...] += z_out[j].astype(F32)
    s_out[n_ctx - 1] = own_out[...].astype(BF16)
    out_copy = pair_copy(3, s_out.at[n_ctx - 1], pair_out, across)
    small_copy.wait_recv()
    g_small[...] = own_small[...].astype(F32) + pair_small[...].astype(F32)
    in_copy.wait_recv()
    g_in[...] = (partial_in[0] + pair_in[...] + one_ref[...]).astype(BF16)
    for z, a, c in peers:
        them = (z * n_x + a) * 2 + c
        remote(
            sum_qkv.at[them], qkvs.at[them], far_send.at[0], qkv_recv.at[them], twin
        ).wait_recv()
    for k in range(n_ctx * n_x):
        heads = [qkvs[2 * k + c, :shard, :].astype(F32) for c in range(2)]
        for t in range(3):
            at = t * width + 2 * HD * k
            g_qkv[:, at : at + 2 * HD] = jnp.concatenate(
                [h[:, t * HD : (t + 1) * HD] for h in heads], axis=1)
        for c in range(2):
            g_bias[2 * k + c : 2 * k + c + 1, :] = qkvs[2 * k + c, shard : shard + 1, :].astype(F32)
    out_copy.wait_recv()
    g_out[...] = s_out[n_ctx - 1].astype(F32) + pair_out[...].astype(F32)
    for copy in started:
        copy.wait_send()


def finish_grads(out, x_out, small, qkv, reduced, joined, weight, grad_one):
    n_ctx, n_x = lax.axis_size("ctx"), lax.axis_size("x")
    n = 2 * n_ctx * n_x
    shard, width = out.shape[1:]
    part = reduced.shape[0] // 2
    vmem = pl.BlockSpec(memory_space=pltpu.VMEM)
    dma = pltpu.SemaphoreType.DMA

    def low(*shape):
        return pltpu.VMEM(shape, BF16)

    def wide(*shape):
        return jax.ShapeDtypeStruct(shape, F32)

    return pl.pallas_call(
        partial(finish_kernel, n_ctx=n_ctx, n_x=n_x),
        in_specs=[vmem] * 8,
        out_specs=[vmem] * 7,
        out_shape=[
            wide(2 * part, width),
            wide(shard, 4 * width),
            wide(shard, width),
            wide(*small.shape[1:]),
            wide(shard, 3 * width),
            wide(n, qkv.shape[2]),
            jax.ShapeDtypeStruct(grad_one.shape, BF16),
        ],
        scratch_shapes=[
            low(n_ctx, *out.shape[1:]),
            low(n_ctx - 1, *out.shape[1:]),
            pltpu.VMEM(out.shape[1:], F32),
            low(*small.shape),
            low(*small.shape[1:]),
            low(*small.shape[1:]),
            low(*qkv.shape),
            low(*qkv.shape),
            low(*qkv.shape),
            low(part, width),
            low(*out.shape[1:]),
            low(3, shard, width),
            low(*joined.shape),
            pltpu.VMEM((2,) + grad_one.shape, F32),
            pltpu.VMEM(grad_one.shape, F32),
            dma((n_ctx * n_x - 1,)),
            dma((n_ctx * n_x,)),
            dma((2 * (n - 1),)),
            dma((n,)),
            dma((n,)),
            dma((n_ctx - 1,)),
            dma((n_ctx - 1,)),
            dma((8,)),
            dma((8,)),
        ],
        compiler_params=pltpu.CompilerParams(
            collective_id=2, has_side_effects=True, vmem_limit_bytes=VMEM_LIMIT
        ),
        cost_estimate=pl.CostEstimate(flops=0, bytes_accessed=16 * joined.size, transcendentals=0),
        name="finish_grads",
    )(out, x_out, small, qkv, reduced, joined, weight, grad_one)


def lane_gather(mine_ref, all_ref, send_sem, recv_sem, local_sem, n_ctx, n_x):
    ctx, x = lax.axis_index("ctx"), lax.axis_index("x")
    chip = ctx * n_x + x
    routes = (
        at_device(ctx=lax.rem(ctx + 1, n_ctx)),
        at_device(ctx=lax.rem(ctx + n_ctx - 1, n_ctx)),
        at_device(x=1 - x),
    )

    def send(k, lane, own=False):
        return pltpu.make_async_remote_copy(
            mine_ref if own else all_ref.at[k], all_ref.at[k], send_sem.at[lane, k], recv_sem.at[k],
            device_id=routes[lane], device_id_type=MESH)

    local = pltpu.make_async_copy(mine_ref, all_ref.at[chip], local_sem)

    def begin():
        @pl.when(ctx + 1 < n_ctx)
        def _():
            send(chip, 0, own=True).start()

        @pl.when(ctx > 0)
        def _():
            send(chip, 1, own=True).start()

        send(chip, 2, own=True).start()
        local.start()

    def relay(r):
        for sign, lane, more in ((-1, 0, ctx + 1 < n_ctx), (1, 1, ctx > 0)):
            z = ctx + sign * r

            @pl.when((z >= 0) & (z < n_ctx))
            def _():
                k = z * n_x + x
                send(k, 0).wait_recv()

                @pl.when(more)
                def _():
                    send(k, lane).start()

                send(k, 2).start()

    def end():
        for z in range(n_ctx):
            k = z * n_x + x
            send(z * n_x + 1 - x, 0).wait_recv()

            @pl.when((z <= ctx) & (ctx + 1 < n_ctx))
            def _():
                send(k, 0).wait_send()

            @pl.when((z >= ctx) & (ctx > 0))
            def _():
                send(k, 1).wait_send()

            send(k, 2).wait_send()
        local.wait()

    return begin, relay, end


QB = 512
KB = 512


def turn(pair, cosine, sine):
    half = HD // 2
    lanes = lax.broadcasted_iota(jnp.int32, (1, 2 * HD), 1)
    low = lax.rem(lanes, HD) < half
    swapped = jnp.where(low, pltpu.roll(pair, 2 * HD - half, 1), pltpu.roll(pair, half, 1))
    return pair * cosine + swapped * jnp.where(low, -sine, sine)


def heads_kernel(
    len_ref, tok_ref, w_ref, b_ref, cos_ref, sin_ref, wa_ref, wu_ref, wd_ref,
    q_ref, k_ref, v_ref, mix_ref, send_ref, norm_ref, fa_ref, fu_ref, fd_ref,
    a_send, a_recv, u_send, u_recv, d_send, d_recv, local_sem, *, n_ctx, n_x, part
):
    core = lax.axis_index("core")
    ctx, x = lax.axis_index("ctx"), lax.axis_index("x")
    greet([
        at_device(x=1 - x),
        at_device(ctx=lax.rem(ctx + 1, n_ctx)),
        at_device(ctx=lax.rem(ctx + n_ctx - 1, n_ctx)),
    ])
    flows = [
        lane_gather(wa_ref, fa_ref, a_send, a_recv, local_sem.at[0], n_ctx, n_x),
        lane_gather(wu_ref, fu_ref, u_send, u_recv, local_sem.at[1], n_ctx, n_x),
        lane_gather(wd_ref, fd_ref, d_send, d_recv, local_sem.at[2], n_ctx, n_x),
    ]
    for begin, _, _ in flows:
        begin()
    slots, seq, _ = q_ref.shape

    def relay(r):
        if r < n_ctx:
            for _, hop, _ in flows:
                hop(r)

    def project(s):
        @pl.loop(0, seq // QB)
        def _(i):
            at = pl.multiple_of(i * QB, QB)
            rows = pl.ds(at, QB)
            tokens = tok_ref[pl.ds(pl.multiple_of(s * seq + at, QB), QB), :]
            joined = mm(tokens, w_ref[...]) + b_ref[...]
            turned = turn(joined[:, : 2 * HD], cos_ref[rows, :], sin_ref[rows, :])
            q_ref[s, rows, :] = (turned[:, :HD].astype(BF16) * HD ** (-0.5)).astype(BF16)
            k_ref[s, rows, :] = turned[:, HD:].astype(BF16)
            v_ref[s, rows, :] = joined[:, 2 * HD :].astype(BF16)

    def attend(s, first, last):
        length = len_ref[s]

        @pl.loop(first, last)
        def _(i):
            rows = pl.ds(pl.multiple_of(i * QB, QB), QB)
            queries = q_ref[s, rows, :]

            def step(j, state):
                highest, total, mix = state
                start = pl.multiple_of(j * KB, KB)
                scores = contract(queries, k_ref[s, pl.ds(start, KB), :], 1, 1)
                ids = start + lax.broadcasted_iota(jnp.int32, (1, KB), 1)
                scores = jnp.where(ids < length, scores, NEG_FILL)
                higher = jnp.maximum(highest, jnp.max(scores, axis=1, keepdims=True))
                fade = jnp.exp(highest - higher)
                weights = jnp.exp(scores - higher)
                total = total * fade + jnp.sum(weights, axis=1, keepdims=True)
                mix = mix * fade + mm(weights.astype(BF16), v_ref[s, pl.ds(start, KB), :])
                return higher, total, mix

            highest, total, mix = lax.fori_loop(
                0,
                seq // KB,
                step,
                (
                    jnp.full((QB, 1), NEG_FILL, F32),
                    jnp.zeros((QB, 1), F32),
                    jnp.zeros((QB, HD), F32),
                ),
            )
            mix = mix / total
            mix_ref[s, rows, :] = mix
            log_norm = jnp.broadcast_to(highest + jnp.log(total), (QB, 128))
            norm_ref[s, :, rows] = jnp.transpose(log_norm)[0:1, :]
            low = mix.astype(BF16)
            chips = QB // (2 * part)
            for chip in range(chips):
                for half in range(2):
                    at = (2 * chip + half) * part
                    send_ref[i * chips + chip, half ^ core, s] = low[at : at + part]

    blocks = seq // QB
    for s in range(slots):
        project(s)
    relay(1)
    attend(0, 0, blocks)
    relay(2)
    for s in range(1, slots):
        attend(s, 0, blocks)
    for r in range(3, n_ctx):
        relay(r)
    for _, _, end in flows:
        end()


def heads(lengths, tokens, weight, bias, cosine, sine, part, *shards):
    n_ctx, n_x = lax.axis_size("ctx"), lax.axis_size("x")
    chips = n_ctx * n_x
    slots, seq = lengths.shape[0], cosine.shape[0]
    vmem = pl.BlockSpec(memory_space=pltpu.VMEM)
    anywhere = pl.BlockSpec(memory_space=pl.ANY)
    dma = pltpu.SemaphoreType.DMA
    head = jax.ShapeDtypeStruct((slots, seq, HD), BF16)
    return pl.pallas_call(
        partial(heads_kernel, n_ctx=n_ctx, n_x=n_x, part=part),
        in_specs=[pl.BlockSpec(memory_space=pltpu.SMEM)] + [vmem] * 8,
        out_specs=[vmem] * 6 + [anywhere] * 3,
        out_shape=[
            head,
            head,
            head,
            jax.ShapeDtypeStruct((slots, seq, HD), F32),
            jax.ShapeDtypeStruct((chips, 2, slots, part, HD), BF16),
            jax.ShapeDtypeStruct((slots, 1, seq), F32),
        ]
        + [jax.ShapeDtypeStruct((chips,) + w.shape, w.dtype) for w in shards],
        scratch_shapes=[dma((3, chips)), dma((chips,))] * 3 + [dma((3,))],
        compiler_params=pltpu.CompilerParams(
            collective_id=5, has_side_effects=True, vmem_limit_bytes=VMEM_LIMIT
        ),
        cost_estimate=pl.CostEstimate(
            flops=16 * slots * seq * seq * HD,
            bytes_accessed=2 * tokens.size,
            transcendentals=slots * seq * seq,
        ),
        name="heads",
    )(lengths, tokens, weight, bias, cosine, sine, *shards)


def backward_kernel(
    len_ref, q_ref, k_ref, v_ref, g_ref, norm_ref, dot_ref, dq_ref, dk_ref, dv_ref, dqt
):
    length = len_ref[pl.program_id(0)]
    j = pl.program_id(1)
    start = j * KB
    key_block = k_ref[0]
    value_block = v_ref[0]

    @pl.when(j == 0)
    def _():
        dqt[...] = jnp.zeros_like(dqt)

    turned = jnp.transpose(key_block.astype(F32)).astype(BF16)
    ids = start + lax.broadcasted_iota(jnp.int32, (KB, 1), 0)
    shift = jnp.where(ids < length, 0.0, NEG_FILL)

    def step(i, state):
        key_grad, value_grad = state
        at = pl.multiple_of(i * QB, QB)
        queries = q_ref[0, pl.ds(at, QB), :]
        grads = g_ref[0, pl.ds(at, QB), :]
        scores = contract(key_block, queries, 1, 1) + shift
        probs = jnp.exp(scores - norm_ref[0, :, pl.ds(at, QB)])
        grad_probs = contract(value_block, grads, 1, 1)
        grad_scores = (probs * (grad_probs - dot_ref[0, :, pl.ds(at, QB)])).astype(BF16)
        value_grad = value_grad + mm(probs.astype(BF16), grads)
        key_grad = key_grad + mm(grad_scores, queries)
        dqt[:, pl.ds(at, QB)] += mm(turned, grad_scores)
        return key_grad, value_grad

    blocks = jnp.where(start < length, (length + QB - 1) // QB, 0)
    zero = jnp.zeros((KB, HD), F32)
    key_grad, value_grad = lax.fori_loop(0, blocks, step, (zero, zero))
    dk_ref[0] = key_grad
    dv_ref[0] = value_grad

    @pl.when(j == pl.num_programs(1) - 1)
    def _():
        dq_ref[0] = jnp.transpose(dqt[...])


def attend_back(lengths, queries, keys, values, grads, norms, dots):
    slots, seq, _ = queries.shape
    whole = pl.BlockSpec((1, seq, HD), lambda s, j, *_: (s, 0, 0))
    block = pl.BlockSpec((1, KB, HD), lambda s, j, *_: (s, j, 0))
    row = pl.BlockSpec((1, 1, seq), lambda s, j, *_: (s, 0, 0))
    out = jax.ShapeDtypeStruct((slots, seq, HD), F32)
    return pl.pallas_call(
        backward_kernel,
        grid_spec=pltpu.PrefetchScalarGridSpec(
            num_scalar_prefetch=1,
            grid=(slots, seq // KB),
            in_specs=[whole, block, block, whole, row, row],
            out_specs=[whole, block, block],
            scratch_shapes=[pltpu.VMEM((HD, seq), F32)],
        ),
        out_shape=[out] * 3,
        compiler_params=pltpu.CompilerParams(vmem_limit_bytes=VMEM_LIMIT),
        cost_estimate=pl.CostEstimate(
            flops=40 * slots * seq * seq * HD,
            bytes_accessed=20 * slots * seq * HD,
            transcendentals=slots * seq * seq,
        ),
        name="attend_back",
    )(lengths, queries, keys, values, grads, norms, dots)


def join_kernel(
    q_ref, k_ref, v_ref, tok_ref, cos_ref, sin_ref, join_ref, grad_ref, total, bias, *, part
):
    i = pl.program_id(0)

    @pl.when(i == 0)
    def _():
        total[...] = jnp.zeros_like(total)
        bias[...] = jnp.zeros_like(bias)

    pair = jnp.concatenate([q_ref[...] * HD ** (-0.5), k_ref[...]], axis=1)
    turned = turn(pair, cos_ref[...], -sin_ref[...])
    joined = jnp.concatenate([turned, v_ref[...]], axis=1).astype(BF16)
    for chip in range(joined.shape[0] // (2 * part)):
        for core in range(2):
            at = (2 * chip + core) * part
            upper, lower = joined[at : at + part // 2], joined[at + part // 2 : at + part]
            join_ref[chip, core, 0] = jnp.concatenate([upper, lower], axis=1)
    total[...] += contract(joined, tok_ref[...], 0, 0)
    bias[...] += jnp.sum(joined.astype(F32), axis=0, keepdims=True)

    @pl.when(i == pl.num_programs(0) - 1)
    def _():
        turned_total = jnp.transpose(total[...])
        shard = turned_total.shape[0] // grad_ref.shape[0]
        extra = jnp.broadcast_to(bias[...], (grad_ref.shape[1] - shard, bias.shape[1]))
        for d in range(grad_ref.shape[0]):
            grad_ref[d, :shard] = turned_total[d * shard : (d + 1) * shard].astype(BF16)
            grad_ref[d, shard:] = extra.astype(BF16)


def join_grads(grad_q, grad_k, grad_v, tokens, cosine, sine, part, n_group):
    slots, seq, _ = grad_q.shape
    rows, width = tokens.shape
    block = min(512, seq)
    per_slot = seq // block
    cols = 3 * HD
    head = pl.BlockSpec((block, HD), lambda i: (i, 0))
    table = pl.BlockSpec((block, 2 * HD), lambda i: (i % per_slot, 0))
    chips = block // (2 * part)
    shard = width // n_group
    flat = [t.reshape(rows, HD) for t in (grad_q, grad_k, grad_v)]
    return pl.pallas_call(
        partial(join_kernel, part=part),
        grid=(rows // block,),
        in_specs=[
            head, head, head, pl.BlockSpec((block, width), lambda i: (i, 0)), table, table,
        ],
        out_specs=[
            pl.BlockSpec(
                (chips, 2, 1, part // 2, 2 * cols), lambda i: (i % per_slot, 0, i // per_slot, 0, 0)
            ),
            pl.BlockSpec((n_group, shard + 16, cols), lambda i: (0, 0, 0)),
        ],
        out_shape=[
            jax.ShapeDtypeStruct((seq // (2 * part), 2, slots, part // 2, 2 * cols), BF16),
            jax.ShapeDtypeStruct((n_group, shard + 16, cols), BF16),
        ],
        scratch_shapes=[pltpu.VMEM((cols, width), F32), pltpu.VMEM((1, cols), F32)],
        compiler_params=pltpu.CompilerParams(vmem_limit_bytes=VMEM_LIMIT),
        cost_estimate=pl.CostEstimate(
            flops=2 * rows * width * cols, bytes_accessed=2 * rows * width, transcendentals=0
        ),
        name="join_grads",
    )(*flat, tokens, cosine, sine)


def norm_forward(values, gain, shift):
    center = values - jnp.mean(values, axis=-1, keepdims=True)
    spread = jnp.mean(center * center, axis=-1, keepdims=True)
    root = lax.rsqrt(spread + LN_EPS)
    unit = center * root
    return unit * gain + shift, unit, root


def norm_backward(grad, unit, root, gain):
    scaled = grad * gain
    inner = scaled - jnp.mean(scaled, axis=-1, keepdims=True)
    inner = inner - unit * jnp.mean(scaled * unit, axis=-1, keepdims=True)
    return root * inner, jnp.sum(grad * unit, axis=0), jnp.sum(grad, axis=0)


def gelu_pair(values):
    half = 0.5 + 0.5 * lax.erf(values * 0.7071067811865476)
    bell = jnp.exp(-0.5 * values * values) * 0.3989422804014327
    return values * half, half + values * bell


def rope_rows(positions):
    halfway = HD // 2
    ladder = jnp.arange(halfway, dtype=F32) * (2.0 / HD)
    frequency = jnp.power(jnp.float32(10000.0), -ladder)
    angles = positions[:, None] * frequency[None, :]
    return jnp.cos(angles), jnp.sin(angles)


def layer_kernel(
    merged_ref, tok_ref, wo_ref, up_ref, down_ref, vec_ref, full_ref, lane_ref,
    out_ref, one_ref, gm_ref, att_ref, vecs_ref, act_out, hid_out, gdn_out, gup_out, lanes_out,
    first, first_in, hid, act, slope, gdn, gup, hidden, unit_one, two,
    roots, near, near_in, far, far_in, low_out, low_in, send_sem, recv_sem, out_sem,
    lane_send, lane_recv, *, n_ctx, n_x
):
    core, slot = lax.axis_index("core"), lax.axis_index("slot")
    twin, across = at_device(core=1 - core), at_device(slot=1 - slot)
    ctx, x = lax.axis_index("ctx"), lax.axis_index("x")
    greet([
        twin,
        across,
        at_device(x=1 - x),
        at_device(ctx=lax.rem(ctx + 1, n_ctx)),
        at_device(ctx=lax.rem(ctx + n_ctx - 1, n_ctx)),
    ])
    begin_lane, relay_lane, end_lane = lane_gather(
        lane_ref, lanes_out, lane_send, lane_recv, out_sem.at[4], n_ctx, n_x)
    begin_lane()
    rows, width = tok_ref.shape
    half = rows // 2
    tile = 256
    count = [0]
    started = []

    def launch(source, target_ref, target):
        i = count[0]
        count[0] += 1
        copy = pltpu.make_async_remote_copy(
            source, target_ref, send_sem.at[i], recv_sem.at[i],
            device_id=target, device_id_type=MESH)
        copy.start()
        started.append(copy)
        return copy

    def columns(body, n=width // tile):
        @pl.loop(0, n)
        def _(t):
            body(pl.ds(pl.multiple_of(t * tile, tile), tile))

    def chunks(body, size=64):
        @pl.loop(0, rows // size)
        def _(t):
            body(pl.ds(pl.multiple_of(t * size, size), size))

    def exchange(buf, turn, stage, product):
        halves = [
            launch(buf.at[pl.ds(h * half, half)], buf.at[pl.ds((2 + h) * rows, half)], across)
            for h in range(2)
        ]
        to_twin = launch(buf.at[pl.ds(0, rows)], buf.at[pl.ds(rows, rows)], twin)
        near_buf, far_buf = near.at[turn], far.at[turn]
        to_twin.wait_recv()
        stage(0, 2 * rows)
        product(0, 2 * rows, near_buf, 0)
        near_copy = launch(
            near_buf.at[pl.ds(rows, rows)], near_in.at[turn], twin)
        back = []
        for h in range(2):
            at = (2 + h) * rows
            halves[h].wait_recv()
            launch(
                buf.at[pl.ds(at, half)], buf.at[pl.ds(at + half, half)], twin).wait_recv()
            stage(at, rows)
            product(at, rows, far_buf, h * rows)
            i = 2 * turn + h
            launch(
                far_buf.at[pl.ds(h * rows + half, half)], far_in.at[i], twin).wait_recv()
            low_out[i] = (far_buf[pl.ds(h * rows, half), :] + far_in[i]).astype(BF16)
            back.append(launch(low_out.at[i], low_in.at[i], across))
        return near_copy, back

    def out_product(cols):
        first[:, cols] = mm(merged_ref[...], wo_ref[:, cols])

    columns(out_product)
    launch(first.at[pl.ds(rows, rows)], first_in, twin).wait_recv()

    def norm_one(at):
        values = tok_ref[at, :].astype(F32) + first[at, :] + first_in[at, :] + vec_ref[0:1, :]
        normed, unit, root = norm_forward(values, vec_ref[1:2, :], vec_ref[2:3, :])
        hidden[at, :] = normed
        unit_one[at, :] = unit
        roots[0, at, :] = jnp.broadcast_to(root, (root.shape[0], 128))
        hid[at, :] = normed.astype(BF16)

    chunks(norm_one)

    def up_stage(start, size):
        def body(cols):
            values = mm(hid[start : start + size, :], up_ref[:, cols]) + vec_ref[3:4, cols]
            active, bend = gelu_pair(values)
            act[start : start + size, cols] = active.astype(BF16)
            slope[start : start + size, cols] = bend

        columns(body)

    def down_product(start, size, target, at):
        def body(cols):
            target[at : at + size, cols] = mm(act[start : start + size, :], down_ref[:, cols])

        columns(body)

    near_copy, back = exchange(hid, 0, up_stage, down_product)
    relay_lane(1)
    out_copies = [
        pltpu.make_async_copy(hid, hid_out, out_sem.at[0]),
        pltpu.make_async_copy(act, act_out, out_sem.at[1]),
    ]
    for copy in out_copies:
        copy.start()
    vecs_ref[...] = jnp.zeros_like(vecs_ref)
    near_copy.wait_recv()

    def norm_two(at, h, local):
        downward = near[0, at, :] + near_in[0, at, :] + low_in[h, local, :].astype(F32)
        values = hidden[at, :] + downward + vec_ref[4:5, :]
        normed, unit, root = norm_forward(values, vec_ref[5:6, :], vec_ref[6:7, :])
        out_ref[at, :] = normed.astype(BF16)
        grad, gain, shift = norm_backward(full_ref[at, :], unit, root, vec_ref[5:6, :])
        two[at, :] = grad
        low = grad.astype(BF16)
        gdn[at, :] = low
        vecs_ref[5:6, :] += gain[None]
        vecs_ref[6:7, :] += shift[None]
        vecs_ref[4:5, :] += jnp.sum(low.astype(F32), axis=0, keepdims=True)

    def by_half(body, h, size=64):
        @pl.loop(0, half // size)
        def _(t):
            local = pl.multiple_of(t * size, size)
            body(pl.ds(h * half + local, size), h, pl.ds(local, size))

    for h in range(2):
        back[h].wait_recv()
        by_half(norm_two, h)

    def back_stage(start, size):
        def body(cols):
            grads = contract(gdn[start : start + size, :], down_ref[cols, :], 1, 1)
            low = (grads * slope[start : start + size, cols]).astype(BF16)
            gup[start : start + size, cols] = low
            vecs_ref[3:4, cols] += jnp.sum(low.astype(F32), axis=0, keepdims=True)

        columns(body)

    def back_product(start, size, target, at):
        def body(cols):
            target[at : at + size, cols] = contract(
                gup[start : start + size, :], up_ref[cols, :], 1, 1)

        columns(body)

    relay_lane(2)
    near_copy, back = exchange(gdn, 1, back_stage, back_product)
    for r in range(3, n_ctx):
        relay_lane(r)
    late_copies = [
        pltpu.make_async_copy(gdn, gdn_out, out_sem.at[2]),
        pltpu.make_async_copy(gup, gup_out, out_sem.at[3]),
    ]
    for copy in late_copies:
        copy.start()
    near_copy.wait_recv()

    def norm_back(at, h, local):
        grad = near[1, at, :] + near_in[1, at, :] + low_in[2 + h, local, :].astype(F32)
        grad = grad + two[at, :]
        root = roots[0, at, 0:1]
        one, gain, shift = norm_backward(grad, unit_one[at, :], root, vec_ref[1:2, :])
        one_ref[at, :] = one
        low = one.astype(BF16)
        att_ref[at, :] = low
        vecs_ref[1:2, :] += gain[None]
        vecs_ref[2:3, :] += shift[None]
        vecs_ref[0:1, :] += jnp.sum(low.astype(F32), axis=0, keepdims=True)

    for h in range(2):
        back[h].wait_recv()
        by_half(norm_back, h)
    launch(att_ref.at[pl.ds(0, rows)], att_ref.at[pl.ds(rows, rows)], twin).wait_recv()

    def merged_product(cols):
        gm_ref[:, cols] = contract(att_ref[...], wo_ref[cols, :], 1, 1).astype(BF16)

    columns(merged_product, wo_ref.shape[0] // tile)
    end_lane()
    for copy in started:
        copy.wait_send()
    for copy in out_copies + late_copies:
        copy.wait()


def layer(merged, tokens, w_out, up, down, vectors, grad_full, lane_shard):
    n_ctx, n_x = lax.axis_size("ctx"), lax.axis_size("x")
    chips = n_ctx * n_x
    rows, width = tokens.shape
    hidden = up.shape[1]
    lane = w_out.shape[0]
    vmem = pl.BlockSpec(memory_space=pltpu.VMEM)
    anywhere = pl.BlockSpec(memory_space=pl.ANY)
    dma = pltpu.SemaphoreType.DMA

    def shape(*dims, dtype=BF16):
        return jax.ShapeDtypeStruct(dims, dtype)

    def wide(*dims):
        return pltpu.VMEM(dims, F32)

    def low(*dims):
        return pltpu.VMEM(dims, BF16)

    return pl.pallas_call(
        partial(layer_kernel, n_ctx=n_ctx, n_x=n_x),
        in_specs=[vmem] * 8,
        out_specs=[vmem] * 5 + [anywhere] * 5,
        out_shape=[
            shape(rows, width),
            shape(rows, width, dtype=F32),
            shape(2 * rows, lane),
            shape(2 * rows, width),
            shape(8, width, dtype=F32),
            shape(4 * rows, hidden),
            shape(4 * rows, width),
            shape(4 * rows, width),
            shape(4 * rows, hidden),
            shape(chips, *lane_shard.shape),
        ],
        scratch_shapes=[
            wide(2 * rows, width),
            wide(rows, width),
            low(4 * rows, width),
            low(4 * rows, hidden),
            wide(4 * rows, hidden),
            low(4 * rows, width),
            low(4 * rows, hidden),
            wide(rows, width),
            wide(rows, width),
            wide(rows, width),
            wide(1, rows, 128),
            wide(2, 2 * rows, width),
            wide(2, rows, width),
            wide(2, 2 * rows, width),
            wide(4, rows // 2, width),
            low(4, rows // 2, width),
            low(4, rows // 2, width),
            dma((24,)),
            dma((24,)),
            dma((5,)),
            dma((3, chips)),
            dma((chips,)),
        ],
        compiler_params=pltpu.CompilerParams(
            collective_id=3, has_side_effects=True, vmem_limit_bytes=VMEM_LIMIT
        ),
        cost_estimate=pl.CostEstimate(
            flops=16 * rows * width * hidden, bytes_accessed=16 * rows * width, transcendentals=0
        ),
        name="layer",
    )(merged, tokens, w_out, up, down, vectors, grad_full, lane_shard)


def head_device(
    tokens,
    lengths,
    w_qkv,
    b_qkv,
    w_out,
    b_out,
    ln1_gain,
    ln1_bias,
    w_up,
    b_up,
    w_down,
    b_down,
    ln2_gain,
    ln2_bias,
    w_proj,
    cot_out,
    cot_emb,
):
    n_lane = lax.axis_size("ctx") * lax.axis_size("x")
    n_group = 2 * n_lane
    core = lax.axis_index("core")
    slot = lax.axis_index("slot")
    chip = lax.axis_index("ctx") * lax.axis_size("x") + lax.axis_index("x")
    me = 2 * chip + core
    slots, part, width = tokens.shape
    seq = part * n_group
    rows = slots * part
    shard = width // n_group
    ff_shard = w_down.shape[0]
    ff_half = ff_shard // 2
    proj = w_proj.shape[1]
    head_cols = 3 * HD

    small = jnp.concatenate(
        [b_qkv, b_out, ln1_gain, ln1_bias, b_up, b_down, ln2_gain, ln2_bias]
    )
    small_at = [0]
    for piece in (b_qkv, b_out, ln1_gain, ln1_bias, b_up, b_down, ln2_gain, ln2_bias):
        small_at.append(small_at[-1] + piece.shape[0])
    small_rows = -(-small.shape[0] // proj)
    small_rows = -(-small_rows // 16) * 16
    small = jnp.pad(small, (0, small_rows * proj - small.shape[0])).reshape(small_rows, proj)
    def two_lanes(mine, theirs):
        low_first = jnp.stack([mine, theirs], axis=0)
        high_first = jnp.stack([theirs, mine], axis=0)
        return jnp.where(core == 0, low_first, high_first)

    up_split = w_up.reshape(shard, n_lane, 2, 2, ff_half)
    up_mine = pick(up_split, core, 2)
    up_theirs = swap_core(pick(up_split, 1 - core, 2))
    up_chip = two_lanes(pick(up_mine, slot, 2), pick(up_theirs, slot, 2))
    down_split = w_down.reshape(2, ff_half, width)

    by_head = w_qkv.reshape(shard, 3, n_group, HD).transpose(2, 0, 1, 3)
    all_tokens, my_head, packed = gather_start(
        tokens,
        by_head.reshape(n_group, shard, head_cols),
        jnp.concatenate([w_proj, small], axis=0),
    )
    proj_full = packed[:, :shard].reshape(width, proj)
    smalls = packed[:, shard:].reshape(n_group, small_rows * proj).astype(F32)
    qkv_bias, out_bias, gain_one, shift_one, up_bias, down_bias, gain_two, shift_two = (
        smalls[:, a:b].reshape(-1) for a, b in zip(small_at[:-1], small_at[1:])
    )

    head_weight = my_head.reshape(width, head_cols)
    all_tokens = all_tokens.reshape(slots * seq, width)
    head_bias = pick(qkv_bias.reshape(1, 3, n_group, HD), me, 2).reshape(1, head_cols)
    cosine, sine = rope_rows(jnp.arange(seq, dtype=jnp.int32).astype(F32))
    cos_wide = jnp.tile(cosine, (1, 4))
    sin_wide = jnp.tile(sine, (1, 4))
    queries, keys, values, mixture, send, norms, out_lane, up, down = heads(
        lengths,
        all_tokens,
        head_weight,
        head_bias,
        cos_wide,
        sin_wide,
        part,
        w_out,
        up_chip.reshape(2 * shard, n_lane * ff_half),
        pick(down_split, slot, 0),
    )
    out_lane, up, down = (t.reshape(-1, t.shape[2]) for t in (out_lane, up, down))
    bias_lane = pick(up_bias.reshape(n_lane, 2, 2, ff_half), core, 1)
    up_bias_own = pick(bias_lane, slot, 1).reshape(-1)

    qkv_split = w_qkv.reshape(shard, 3, n_lane, 2, HD)
    qkv_mine = pick(qkv_split, core, 3)
    qkv_theirs = swap_core(pick(qkv_split, 1 - core, 3))
    qkv_chip = two_lanes(qkv_mine, qkv_theirs).transpose(3, 0, 1, 2, 4)
    qkv_chip = qkv_chip.reshape(n_lane, 2 * shard, head_cols)

    merged = lax.all_to_all(send, LANE, 0, 0, tiled=True)
    merged = merged.transpose(1, 2, 3, 0, 4).reshape(2 * rows, n_lane * HD)

    place = me * part + jnp.arange(part, dtype=jnp.int32)
    live = (place[None, :] < lengths[:, None]).reshape(rows, 1)
    grad_out = jnp.where(live, cot_out.reshape(rows, width).astype(F32), 0.0)
    grad_emb = jnp.where(live, cot_emb.reshape(rows, proj), 0)
    grad_full = grad_out + contract(grad_emb, proj_full, 1, 1)
    vectors = jnp.stack(
        [out_bias, gain_one, shift_one, up_bias_own, down_bias, gain_two, shift_two, shift_two]
    )
    (
        out_low,
        grad_one,
        grad_merged,
        grad_att,
        vector_grads,
        active,
        hidden_low,
        grad_down,
        grad_up,
        qkv_lane,
    ) = layer(
        merged, tokens.reshape(rows, width), out_lane, up, down, vectors, grad_full, qkv_chip
    )
    d_down = contract(active, grad_down, 0, 0).astype(BF16)
    d_up = contract(hidden_low, grad_up, 0, 0).astype(BF16)
    embeds = mm(out_low, proj_full).astype(BF16)
    d_proj = contract(out_low, grad_emb, 0, 0)
    (
        d_out_bias,
        d_gain_one,
        d_shift_one,
        up_bias_own_grad,
        d_down_bias,
        d_gain_two,
        d_shift_two,
    ) = (vector_grads[i] for i in range(7))
    grad_merged = grad_merged.reshape(2, slots, part, n_lane, HD).transpose(3, 0, 1, 2, 4)
    grad_heads = lax.all_to_all(grad_merged, LANE, 0, 0, tiled=True)

    def core_order(value):
        return jnp.where(core == 0, value, jnp.flip(value, axis=1))

    grad_heads = core_order(grad_heads).transpose(2, 0, 1, 3, 4).reshape(slots, seq, HD)

    d_out = contract(merged, grad_att, 0, 0).astype(BF16)

    both_ff = jnp.concatenate(
        [d_down.reshape(n_lane, 2 * shard, width), d_up.reshape(n_lane, 2 * shard, width)], axis=1
    )
    reduced = lax.psum_scatter(both_ff, LANE, scatter_dimension=0, tiled=False)
    x_at = lax.axis_index("x")
    out_rows_ = d_out.reshape(-1, 2, shard, width)
    keep_out = pick(out_rows_, x_at, 1)
    got_out = lax.ppermute(pick(out_rows_, 1 - x_at, 1), "x", SWAP)

    spread = (
        (jnp.arange(2) == core)[:, None, None] & (jnp.arange(2) == slot)[None, :, None]
    ).astype(F32)
    up_bias_grad = up_bias_own_grad.reshape(n_lane, 1, 1, ff_half) * spread[None]
    vectors = (
        d_out_bias,
        d_gain_one,
        d_shift_one,
        up_bias_grad.reshape(-1),
        d_down_bias,
        d_gain_two,
        d_shift_two,
    )
    small_grad = jnp.concatenate([v.reshape(n_group, -1) for v in vectors], axis=1)
    small_cols = small_grad.shape[1]
    vec_rows = -(-small_cols // proj)
    vec_rows = -(-(shard + vec_rows) // 16) * 16 - shard
    small_grad = jnp.pad(small_grad, ((0, 0), (0, vec_rows * proj - small_cols)))
    small_grad = jnp.concatenate(
        [d_proj.reshape(n_group, shard, proj), small_grad.reshape(n_group, vec_rows, proj)], axis=1
    )
    row_dots = jnp.sum(grad_heads.astype(F32) * mixture, axis=-1).reshape(slots, 1, seq)
    grad_q, grad_k, grad_v = attend_back(
        lengths, queries, keys, values, grad_heads, norms, row_dots
    )

    joined, d_qkv = join_grads(
        grad_q, grad_k, grad_v, all_tokens, cos_wide, sin_wide, part, n_group
    )
    grad_w_down, grad_w_up, grad_w_out, small_sum, grad_w_qkv, bias_rows, input_grad = finish_grads(
        keep_out,
        got_out,
        small_grad.astype(BF16),
        d_qkv,
        reduced,
        joined,
        qkv_lane,
        grad_one,
    )
    grad_w_proj = small_sum[:shard]
    vec_sum = small_sum[shard:].reshape(-1)
    vec_outs = []
    at = 0
    for v in vectors:
        size = v.size // n_group
        vec_outs.append(vec_sum[at : at + size])
        at += size
    (
        grad_b_out,
        grad_gain_one,
        grad_shift_one,
        grad_b_up,
        grad_b_down,
        grad_gain_two,
        grad_shift_two,
    ) = vec_outs

    qkv_bias_grad = bias_rows.reshape(n_group, 3, HD).transpose(1, 0, 2).reshape(-1)
    grad_b_qkv = lax.dynamic_slice(qkv_bias_grad, (me * b_qkv.shape[0],), (b_qkv.shape[0],))

    return (
        out_low.reshape(slots, part, width),
        embeds.reshape(slots, part, proj),
        input_grad.reshape(slots, part, width),
        grad_w_qkv,
        grad_b_qkv,
        grad_w_out,
        grad_b_out,
        grad_gain_one,
        grad_shift_one,
        grad_w_up,
        grad_b_up,
        grad_w_down,
        grad_b_down,
        grad_gain_two,
        grad_shift_two,
        grad_w_proj,
    )


def layer_norm(hidden, gain, shift):
    center = hidden - jnp.mean(hidden, axis=-1, keepdims=True)
    spread = jnp.mean(center * center, axis=-1, keepdims=True)
    return center * lax.rsqrt(spread + LN_EPS) * gain + shift


def rope_tables(positions, head_width):
    halfway = head_width // 2
    ladder = jnp.arange(halfway, dtype=jnp.float32) * (2.0 / head_width)
    frequency = jnp.power(jnp.float32(10000.0), -ladder)
    angles = positions[:, None] * frequency[None, :]
    return (jnp.cos(angles)[:, None, :], jnp.sin(angles)[:, None, :])


def rotate(values, cosine, sine_part):
    halfway = values.shape[-1] // 2
    first_half = values[..., :halfway]
    second_half = values[..., halfway:]
    return jnp.concatenate(
        [
            first_half * cosine - second_half * sine_part,
            second_half * cosine + first_half * sine_part,
        ],
        axis=-1,
    )


def block_scores(query_block, key_block, key_start, length, scale):
    scores = (
        jnp.einsum("qhd,khd->hqk", query_block, key_block, preferred_element_type=jnp.float32)
        * scale
    )
    key_ids = key_start + jnp.arange(key_block.shape[0], dtype=jnp.int32)
    return jnp.where((key_ids < length)[None, None, :], scores, NEG_FILL)


def per_device(
    tokens,
    lengths,
    w_qkv,
    b_qkv,
    w_out,
    b_out,
    ln1_gain,
    ln1_bias,
    w_up,
    b_up,
    w_down,
    b_down,
    ln2_gain,
    ln2_bias,
    w_proj,
    cot_out,
    cot_emb,
):
    n_fsdp = lax.axis_size("fsdp")
    n_ctx = lax.axis_size("ctx")
    ctx_at = lax.axis_index("ctx")
    fsdp_at = lax.axis_index("fsdp")
    groups, tok_slot, width = tokens.shape
    heads_here = H // n_fsdp
    lane_width = heads_here * HD
    span_rows = tok_slot * n_fsdp
    key_count = span_rows * n_ctx
    row_count = groups * tok_slot
    scale = HD ** (-0.5)
    query_rows = min(512, span_rows)
    key_rows = min(2048, key_count // 4)
    query_blocks = span_rows // query_rows
    key_blocks = key_count // key_rows
    key_starts = jnp.arange(key_blocks, dtype=jnp.int32) * key_rows
    qkv_full, qkv_bias, out_full, out_bias, gain_one, shift_one = (
        lax.all_gather(w_qkv, ("ctx", "fsdp"), axis=0, tiled=True),
        lax.all_gather(b_qkv, ("ctx", "fsdp"), axis=0, tiled=True),
        lax.all_gather(w_out, ("ctx", "fsdp"), axis=0, tiled=True),
        lax.all_gather(b_out, ("ctx", "fsdp"), axis=0, tiled=True),
        lax.all_gather(ln1_gain, ("ctx", "fsdp"), axis=0, tiled=True),
        lax.all_gather(ln1_bias, ("ctx", "fsdp"), axis=0, tiled=True),
    )
    token_pos = (ctx_at * n_fsdp + fsdp_at) * tok_slot + jnp.arange(tok_slot, dtype=jnp.int32)
    live_rows = (token_pos[None, :] < lengths[:, None]).reshape(row_count, 1)
    flat_tokens = tokens.reshape(row_count, width)
    joined = jnp.dot(flat_tokens, qkv_full, preferred_element_type=jnp.float32) + qkv_bias.astype(
        jnp.float32
    )
    cosine, sine_part = rope_tables(token_pos.astype(jnp.float32), HD)
    split_heads = joined.reshape(groups, tok_slot, 3, H, HD)
    rotated_query = rotate(split_heads[:, :, 0], cosine, sine_part)
    rotated_key = rotate(split_heads[:, :, 1], cosine, sine_part)
    packed = (
        jnp.stack([rotated_query, rotated_key, split_heads[:, :, 2]], axis=2)
        .astype(jnp.bfloat16)
        .reshape(groups, tok_slot, 3, n_fsdp, lane_width)
    )
    by_heads = lax.all_to_all(packed, "fsdp", split_axis=3, concat_axis=1, tiled=True)
    queries = by_heads[:, :, 0, 0]
    local_keys = by_heads[:, :, 1, 0]
    local_values = by_heads[:, :, 2, 0]
    all_keys, all_values = (
        lax.all_gather(local_keys, "ctx", axis=1, tiled=True),
        lax.all_gather(local_values, "ctx", axis=1, tiled=True),
    )

    def attend_slot(slot_item):
        slot_queries, slot_keys, slot_values, length = slot_item
        query_split = slot_queries.reshape(query_blocks, query_rows, heads_here, HD)
        key_split = slot_keys.reshape(key_blocks, key_rows, heads_here, HD)
        value_split = slot_values.reshape(key_blocks, key_rows, heads_here, HD)

        def per_query(query_block):

            def row_stats(state_pair, key_item):
                highest, running_sum = state_pair
                scores = block_scores(query_block, key_item[0], key_item[1], length, scale)
                new_high = jnp.maximum(highest, jnp.max(scores, axis=-1))
                running_sum = running_sum * jnp.exp(highest - new_high) + jnp.sum(
                    jnp.exp(scores - new_high[..., None]), axis=-1
                )
                return ((new_high, running_sum), None)

            start_state = (
                jnp.full((heads_here, query_rows), NEG_FILL, jnp.float32),
                jnp.zeros((heads_here, query_rows), jnp.float32),
            )
            highest, running_sum = lax.scan(row_stats, start_state, (key_split, key_starts))[0]
            log_norm = highest + jnp.log(running_sum)

            def weigh_values(accumulated, key_item):
                scores = block_scores(query_block, key_item[0], key_item[2], length, scale)
                weights = jnp.exp(scores - log_norm[..., None]).astype(jnp.bfloat16)
                return (
                    accumulated
                    + jnp.einsum(
                        "hqk,khd->qhd", weights, key_item[1], preferred_element_type=jnp.float32
                    ),
                    None,
                )

            mixture = lax.scan(
                weigh_values,
                jnp.zeros((query_rows, heads_here, HD), jnp.float32),
                (key_split, value_split, key_starts),
            )[0]
            return (mixture, log_norm)

        mixture, log_norm = lax.map(per_query, query_split)
        return (mixture.reshape(span_rows, lane_width), log_norm)

    mixture, log_norms = lax.map(attend_slot, (queries, all_keys, all_values, lengths))
    merged = lax.all_to_all(
        mixture.astype(jnp.bfloat16).reshape(groups, span_rows, 1, lane_width),
        "fsdp",
        split_axis=1,
        concat_axis=2,
        tiled=True,
    ).reshape(row_count, width)
    attended = jnp.dot(merged, out_full, preferred_element_type=jnp.float32) + out_bias.astype(
        jnp.float32
    )
    hidden_one, pull_one = jax.vjp(
        layer_norm,
        flat_tokens.astype(jnp.float32) + attended,
        gain_one.astype(jnp.float32),
        shift_one.astype(jnp.float32),
    )
    hidden_low = hidden_one.astype(jnp.bfloat16)
    up_full, up_bias, down_full, down_bias, gain_two, shift_two, proj_full = (
        lax.all_gather(w_up, ("ctx", "fsdp"), axis=0, tiled=True),
        lax.all_gather(b_up, ("ctx", "fsdp"), axis=0, tiled=True),
        lax.all_gather(w_down, ("ctx", "fsdp"), axis=0, tiled=True),
        lax.all_gather(b_down, ("ctx", "fsdp"), axis=0, tiled=True),
        lax.all_gather(ln2_gain, ("ctx", "fsdp"), axis=0, tiled=True),
        lax.all_gather(ln2_bias, ("ctx", "fsdp"), axis=0, tiled=True),
        lax.all_gather(w_proj, ("ctx", "fsdp"), axis=0, tiled=True),
    )
    upward = jnp.dot(hidden_low, up_full, preferred_element_type=jnp.float32) + up_bias.astype(
        jnp.float32
    )
    active_full, pull_gelu = jax.vjp(partial(jax.nn.gelu, approximate=False), upward)
    active = active_full.astype(jnp.bfloat16)
    downward = jnp.dot(active, down_full, preferred_element_type=jnp.float32) + down_bias.astype(
        jnp.float32
    )
    out_full_rows, pull_two = jax.vjp(
        layer_norm,
        hidden_one + downward,
        gain_two.astype(jnp.float32),
        shift_two.astype(jnp.float32),
    )
    out_low = out_full_rows.astype(jnp.bfloat16)
    projected = jnp.dot(out_low, proj_full, preferred_element_type=jnp.float32)
    back_qkv, back_qkv_bias, back_out, back_out_bias, back_gain_one, back_shift_one = (
        lax.all_gather(w_qkv, ("ctx", "fsdp"), axis=0, tiled=True),
        lax.all_gather(b_qkv, ("ctx", "fsdp"), axis=0, tiled=True),
        lax.all_gather(w_out, ("ctx", "fsdp"), axis=0, tiled=True),
        lax.all_gather(b_out, ("ctx", "fsdp"), axis=0, tiled=True),
        lax.all_gather(ln1_gain, ("ctx", "fsdp"), axis=0, tiled=True),
        lax.all_gather(ln1_bias, ("ctx", "fsdp"), axis=0, tiled=True),
    )
    back_up, back_up_bias, back_down, back_down_bias, back_gain_two, back_shift_two, back_proj = (
        lax.all_gather(w_up, ("ctx", "fsdp"), axis=0, tiled=True),
        lax.all_gather(b_up, ("ctx", "fsdp"), axis=0, tiled=True),
        lax.all_gather(w_down, ("ctx", "fsdp"), axis=0, tiled=True),
        lax.all_gather(b_down, ("ctx", "fsdp"), axis=0, tiled=True),
        lax.all_gather(ln2_gain, ("ctx", "fsdp"), axis=0, tiled=True),
        lax.all_gather(ln2_bias, ("ctx", "fsdp"), axis=0, tiled=True),
        lax.all_gather(w_proj, ("ctx", "fsdp"), axis=0, tiled=True),
    )
    grad_out = jnp.where(live_rows, cot_out.reshape(row_count, width).astype(jnp.float32), 0.0)
    grad_emb = jnp.where(live_rows, cot_emb.reshape(row_count, -1), 0)
    d_proj = jnp.einsum("rd,rp->dp", out_low, grad_emb, preferred_element_type=jnp.float32)
    grad_full = grad_out + jnp.einsum(
        "rp,dp->rd", grad_emb, back_proj, preferred_element_type=jnp.float32
    )
    grad_two, d_gain_two, d_shift_two = pull_two(grad_full)
    grad_down = grad_two.astype(jnp.bfloat16)
    d_down = jnp.einsum("rf,rd->fd", active, grad_down, preferred_element_type=jnp.float32)
    d_down_bias = jnp.sum(grad_down.astype(jnp.float32), axis=0)
    grad_act = jnp.einsum("rd,fd->rf", grad_down, back_down, preferred_element_type=jnp.float32)
    grad_up = pull_gelu(grad_act)[0].astype(jnp.bfloat16)
    d_up = jnp.einsum("rd,rf->df", hidden_low, grad_up, preferred_element_type=jnp.float32)
    d_up_bias = jnp.sum(grad_up.astype(jnp.float32), axis=0)
    grad_hidden = grad_two + jnp.einsum(
        "rf,df->rd", grad_up, back_up, preferred_element_type=jnp.float32
    )
    grad_one, d_gain_one, d_shift_one = pull_one(grad_hidden)
    grad_att = grad_one.astype(jnp.bfloat16)
    d_out = jnp.einsum("rd,re->de", merged, grad_att, preferred_element_type=jnp.float32)
    d_out_bias = jnp.sum(grad_att.astype(jnp.float32), axis=0)
    grad_merged = jnp.einsum(
        "re,de->rd", grad_att, back_out, preferred_element_type=jnp.float32
    ).astype(jnp.bfloat16)
    grad_heads = lax.all_to_all(
        grad_merged.reshape(groups, tok_slot, n_fsdp, lane_width),
        "fsdp",
        split_axis=2,
        concat_axis=1,
        tiled=True,
    ).reshape(groups, span_rows, lane_width)

    def attend_back(slot_item):
        slot_queries, slot_keys, slot_values, grad_mix, log_norm, length = slot_item
        query_split = slot_queries.reshape(query_blocks, query_rows, heads_here, HD)
        key_split = slot_keys.reshape(key_blocks, key_rows, heads_here, HD)
        value_split = slot_values.reshape(key_blocks, key_rows, heads_here, HD)
        grad_split = grad_mix.reshape(query_blocks, query_rows, heads_here, HD)

        def value_pass(value_total, query_item):
            query_block, grad_block, norm_block = query_item

            def value_per_key(row_dot, key_item):
                key_block, value_block, key_start = key_item
                scores = block_scores(query_block, key_block, key_start, length, scale)
                probability = jnp.exp(scores - norm_block[..., None])
                grad_probs = jnp.einsum(
                    "qhd,khd->hqk", grad_block, value_block, preferred_element_type=jnp.float32
                )
                value_part = jnp.einsum(
                    "hqk,qhd->khd",
                    probability.astype(jnp.bfloat16),
                    grad_block,
                    preferred_element_type=jnp.float32,
                )
                return (row_dot + jnp.sum(probability * grad_probs, axis=-1), value_part)

            row_dot, value_parts = lax.scan(
                value_per_key,
                jnp.zeros((heads_here, query_rows), jnp.float32),
                (key_split, value_split, key_starts),
            )
            return (value_total + value_parts.reshape(key_count, heads_here, HD), row_dot)

        value_grad, row_dots = lax.scan(
            value_pass,
            jnp.zeros((key_count, heads_here, HD), jnp.float32),
            (query_split, grad_split, log_norm),
        )

        def key_pass(key_total, query_item):
            query_block, grad_block, norm_block, dot_block = query_item

            def key_per_key(query_accum, key_item):
                key_block, value_block, key_start = key_item
                scores = block_scores(query_block, key_block, key_start, length, scale)
                probability = jnp.exp(scores - norm_block[..., None])
                grad_probs = jnp.einsum(
                    "qhd,khd->hqk", grad_block, value_block, preferred_element_type=jnp.float32
                )
                grad_scores = (probability * (grad_probs - dot_block[..., None])).astype(
                    jnp.bfloat16
                )
                query_accum = query_accum + jnp.einsum(
                    "hqk,khd->qhd", grad_scores, key_block, preferred_element_type=jnp.float32
                )
                key_part = jnp.einsum(
                    "hqk,qhd->khd", grad_scores, query_block, preferred_element_type=jnp.float32
                )
                return (query_accum, key_part)

            query_grad, key_parts = lax.scan(
                key_per_key,
                jnp.zeros((query_rows, heads_here, HD), jnp.float32),
                (key_split, value_split, key_starts),
            )
            return (key_total + key_parts.reshape(key_count, heads_here, HD), query_grad)

        key_grad, query_grads = lax.scan(
            key_pass,
            jnp.zeros((key_count, heads_here, HD), jnp.float32),
            (query_split, grad_split, log_norm, row_dots),
        )
        return (
            query_grads.reshape(span_rows, lane_width) * scale,
            key_grad.reshape(key_count, lane_width) * scale,
            value_grad.reshape(key_count, lane_width),
        )

    grad_queries, key_terms, value_terms = lax.map(
        attend_back, (queries, all_keys, all_values, grad_heads, log_norms, lengths)
    )
    grad_keys, grad_values = (
        lax.psum_scatter(
            key_terms.astype(jnp.bfloat16), "ctx", scatter_dimension=1, tiled=True
        ).astype(jnp.float32),
        lax.psum_scatter(
            value_terms.astype(jnp.bfloat16), "ctx", scatter_dimension=1, tiled=True
        ).astype(jnp.float32),
    )
    head_pos = (ctx_at * span_rows + jnp.arange(span_rows, dtype=jnp.int32)).astype(jnp.float32)
    head_cosine, head_sine = rope_tables(head_pos, HD)
    query_back = rotate(
        grad_queries.reshape(groups, span_rows, heads_here, HD), head_cosine, -head_sine
    )
    key_back = rotate(grad_keys.reshape(groups, span_rows, heads_here, HD), head_cosine, -head_sine)
    value_back = grad_values.reshape(groups, span_rows, heads_here, HD)
    grad_pack = (
        jnp.stack([query_back, key_back, value_back], axis=2)
        .astype(jnp.bfloat16)
        .reshape(groups, span_rows, 3, 1, lane_width)
    )
    grad_joined = lax.all_to_all(
        grad_pack, "fsdp", split_axis=1, concat_axis=3, tiled=True
    ).reshape(row_count, 3 * width)
    d_qkv = jnp.einsum("rd,re->de", flat_tokens, grad_joined, preferred_element_type=jnp.float32)
    d_qkv_bias = jnp.sum(grad_joined.astype(jnp.float32), axis=0)
    input_grad = (
        jnp.einsum("re,de->rd", grad_joined, back_qkv, preferred_element_type=jnp.float32)
        + grad_one
    ).astype(jnp.bfloat16)
    shards = (
        lax.psum_scatter(d_qkv, ("ctx", "fsdp"), scatter_dimension=0, tiled=True),
        lax.psum_scatter(d_qkv_bias, ("ctx", "fsdp"), scatter_dimension=0, tiled=True),
        lax.psum_scatter(d_out, ("ctx", "fsdp"), scatter_dimension=0, tiled=True),
        lax.psum_scatter(d_out_bias, ("ctx", "fsdp"), scatter_dimension=0, tiled=True),
        lax.psum_scatter(d_gain_one, ("ctx", "fsdp"), scatter_dimension=0, tiled=True),
        lax.psum_scatter(d_shift_one, ("ctx", "fsdp"), scatter_dimension=0, tiled=True),
        lax.psum_scatter(d_up, ("ctx", "fsdp"), scatter_dimension=0, tiled=True),
        lax.psum_scatter(d_up_bias, ("ctx", "fsdp"), scatter_dimension=0, tiled=True),
        lax.psum_scatter(d_down, ("ctx", "fsdp"), scatter_dimension=0, tiled=True),
        lax.psum_scatter(d_down_bias, ("ctx", "fsdp"), scatter_dimension=0, tiled=True),
        lax.psum_scatter(d_gain_two, ("ctx", "fsdp"), scatter_dimension=0, tiled=True),
        lax.psum_scatter(d_shift_two, ("ctx", "fsdp"), scatter_dimension=0, tiled=True),
        lax.psum_scatter(d_proj, ("ctx", "fsdp"), scatter_dimension=0, tiled=True),
    )
    totals = (
        lax.psum(shards[0].astype(jnp.bfloat16), "slot").astype(jnp.float32),
        lax.psum(shards[1].astype(jnp.bfloat16), "slot").astype(jnp.float32),
        lax.psum(shards[2].astype(jnp.bfloat16), "slot").astype(jnp.float32),
        lax.psum(shards[3].astype(jnp.bfloat16), "slot").astype(jnp.float32),
        lax.psum(shards[4].astype(jnp.bfloat16), "slot").astype(jnp.float32),
        lax.psum(shards[5].astype(jnp.bfloat16), "slot").astype(jnp.float32),
        lax.psum(shards[6].astype(jnp.bfloat16), "slot").astype(jnp.float32),
        lax.psum(shards[7].astype(jnp.bfloat16), "slot").astype(jnp.float32),
        lax.psum(shards[8].astype(jnp.bfloat16), "slot").astype(jnp.float32),
        lax.psum(shards[9].astype(jnp.bfloat16), "slot").astype(jnp.float32),
        lax.psum(shards[10].astype(jnp.bfloat16), "slot").astype(jnp.float32),
        lax.psum(shards[11].astype(jnp.bfloat16), "slot").astype(jnp.float32),
        lax.psum(shards[12].astype(jnp.bfloat16), "slot").astype(jnp.float32),
    )
    return (
        out_low.reshape(groups, tok_slot, width),
        projected.astype(jnp.bfloat16).reshape(groups, tok_slot, -1),
        input_grad.reshape(groups, tok_slot, width),
        totals[0],
        totals[1],
        totals[2],
        totals[3],
        totals[4],
        totals[5],
        totals[6],
        totals[7],
        totals[8],
        totals[9],
        totals[10],
        totals[11],
        totals[12],
    )


def solution(mesh):
    n_slot, n_ctx, n_fsdp = (mesh.shape[a] for a in ("slot", "ctx", "fsdp"))
    rows_axes = ("ctx", "fsdp")
    step = per_device
    if n_slot == 2 and n_fsdp % 2 == 0 and n_ctx * n_fsdp == H:
        mesh = Mesh(
            mesh.devices.reshape(n_slot, n_ctx, n_fsdp // 2, 2), ("slot", "ctx", "x", "core")
        )
        rows_axes = GROUP
        step = head_device
    in_specs = (
        P("slot", rows_axes, None),
        P("slot"),
        P(rows_axes, None),
        P(rows_axes),
        P(rows_axes, None),
        P(rows_axes),
        P(rows_axes),
        P(rows_axes),
        P(rows_axes, None),
        P(rows_axes),
        P(rows_axes, None),
        P(rows_axes),
        P(rows_axes),
        P(rows_axes),
        P(rows_axes, None),
        P("slot", rows_axes, None),
        P("slot", rows_axes, None),
    )
    out_specs = (
        P("slot", rows_axes, None),
        P("slot", rows_axes, None),
        P("slot", rows_axes, None),
        P(rows_axes, None),
        P(rows_axes),
        P(rows_axes, None),
        P(rows_axes),
        P(rows_axes),
        P(rows_axes),
        P(rows_axes, None),
        P(rows_axes),
        P(rows_axes, None),
        P(rows_axes),
        P(rows_axes),
        P(rows_axes),
        P(rows_axes, None),
    )
    return jax.shard_map(
        step, mesh=mesh, in_specs=in_specs, out_specs=out_specs, check_vma=False
    )
```

```python
from functools import partial

import jax
import jax.numpy as jnp
from jax import lax
from jax.experimental import pallas as pl
from jax.experimental.pallas import tpu as pltpu
from jax.sharding import Mesh
from jax.sharding import PartitionSpec as P

H = 16
HD = 64
LN_EPS = 1e-05
NEG_FILL = -1e30
F32 = jnp.float32
BF16 = jnp.bfloat16
GROUP = ("ctx", "x", "core")
LANE = ("ctx", "x")
SWAP = [(0, 1), (1, 0)]
VMEM_LIMIT = 60 * 1024 * 1024


def mm(left, right):
    return jnp.dot(left, right, preferred_element_type=F32)


def contract(left, right, left_dim, right_dim):
    return lax.dot_general(
        left, right, (((left_dim,), (right_dim,)), ((), ())), preferred_element_type=F32
    )


def swap_core(value):
    return lax.ppermute(value, "core", SWAP)


def swap_slot(value):
    return lax.ppermute(value, "slot", SWAP)


def pick(stacked, index, axis):
    return lax.dynamic_index_in_dim(stacked, index, axis, keepdims=False)


MESH = pl.DeviceIdType.MESH


def at_device(**where):
    names = ("slot", "ctx", "x", "core")
    return tuple(where[n] if n in where else lax.axis_index(n) for n in names)


def greet(peers):
    barrier = pltpu.get_barrier_semaphore()
    for peer in peers:
        pl.semaphore_signal(barrier, inc=1, device_id=peer, device_id_type=MESH)
    pl.semaphore_wait(barrier, len(peers))


def group_peers(n_ctx, n_x):
    ctx, x, core = (lax.axis_index(n) for n in GROUP)
    peers = []
    for dz in range(n_ctx):
        for dx in range(n_x):
            for dc in range(2):
                if dz or dx or dc:
                    where = (lax.rem(ctx + dz, n_ctx), lax.rem(x + dx, n_x), lax.rem(core + dc, 2))
                    peers.append(where)
    return peers


def start_kernel(
    tok_ref, head_ref, small_ref, all_ref, heads_ref, smalls_ref,
    far_send, block_send, local_sem, head_recv, small_recv, block_recv, *, n_ctx, n_x
):
    part = tok_ref.shape[1]
    ctx, x, core = (lax.axis_index(n) for n in GROUP)
    me = (ctx * n_x + x) * 2 + core
    peers = group_peers(n_ctx, n_x)
    greet([at_device(ctx=z, x=a, core=c) for z, a, c in peers])

    def block_at(b):
        return all_ref.at[:, pl.ds(pl.multiple_of(b * part, part), part), :]

    pushes = []
    for k, (z, a, c) in enumerate(peers):
        them = (z * n_x + a) * 2 + c
        target = at_device(ctx=z, x=a, core=c)
        pushes.append(pltpu.make_async_remote_copy(
            head_ref.at[them], heads_ref.at[me], far_send.at[2 * k], head_recv.at[me],
            device_id=target, device_id_type=MESH))
        pushes.append(pltpu.make_async_remote_copy(
            small_ref, smalls_ref.at[me], far_send.at[2 * k + 1], small_recv.at[me],
            device_id=target, device_id_type=MESH))
    locals_ = [
        pltpu.make_async_copy(tok_ref, block_at(me), local_sem.at[0]),
        pltpu.make_async_copy(head_ref.at[me], heads_ref.at[me], local_sem.at[1]),
        pltpu.make_async_copy(small_ref, smalls_ref.at[me], local_sem.at[2]),
    ]

    def send(b, source, lane, target):
        return pltpu.make_async_remote_copy(
            source, block_at(b), block_send.at[lane, b], block_recv.at[b],
            device_id=target, device_id_type=MESH)

    up = at_device(ctx=lax.rem(ctx + 1, n_ctx))
    down = at_device(ctx=lax.rem(ctx + n_ctx - 1, n_ctx))
    side = at_device(x=1 - x)
    twin = at_device(core=1 - core)

    def here(b):
        return send(b, block_at(b), 0, twin)

    @pl.when(ctx + 1 < n_ctx)
    def _():
        send(me, tok_ref, 0, up).start()

    @pl.when(ctx > 0)
    def _():
        send(me, tok_ref, 1, down).start()

    send(me, tok_ref, 2, side).start()
    send(me, tok_ref, 3, twin).start()
    for copy in locals_:
        copy.start()

    for r in range(1, n_ctx):
        if r == n_ctx - 1:
            for push in pushes:
                push.start()
        low = ctx - r
        high = ctx + r

        @pl.when(low >= 0)
        def _():
            b = (low * n_x + x) * 2 + core
            here(b).wait_recv()

            @pl.when(ctx + 1 < n_ctx)
            def _():
                send(b, block_at(b), 0, up).start()

            send(b, block_at(b), 2, side).start()
            send(b, block_at(b), 3, twin).start()

        @pl.when(high < n_ctx)
        def _():
            b = (high * n_x + x) * 2 + core
            here(b).wait_recv()

            @pl.when(ctx > 0)
            def _():
                send(b, block_at(b), 1, down).start()

            send(b, block_at(b), 2, side).start()
            send(b, block_at(b), 3, twin).start()

    def from_side(z):
        b = (z * n_x + (1 - x)) * 2 + core
        here(b).wait_recv()
        send(b, block_at(b), 3, twin).start()

    from_side(ctx)
    for r in range(1, n_ctx):
        @pl.when(ctx - r >= 0)
        def _():
            from_side(ctx - r)

        @pl.when(ctx + r < n_ctx)
        def _():
            from_side(ctx + r)

    for z in range(n_ctx):
        for a in range(n_x):
            here((z * n_x + a) * 2 + 1 - core).wait_recv()
    for k, (z, a, c) in enumerate(peers):
        them = (z * n_x + a) * 2 + c
        pltpu.make_async_remote_copy(
            head_ref.at[them], heads_ref.at[them], far_send.at[2 * k], head_recv.at[them],
            device_id=twin, device_id_type=MESH).wait_recv()
        pltpu.make_async_remote_copy(
            small_ref, smalls_ref.at[them], far_send.at[2 * k + 1], small_recv.at[them],
            device_id=twin, device_id_type=MESH).wait_recv()
    for push in pushes:
        push.wait_send()
    for copy in locals_:
        copy.wait()

    for z in range(n_ctx):
        b = (z * n_x + x) * 2 + core

        @pl.when((z <= ctx) & (ctx + 1 < n_ctx))
        def _():
            send(b, block_at(b), 0, up).wait_send()

        @pl.when((z >= ctx) & (ctx > 0))
        def _():
            send(b, block_at(b), 1, down).wait_send()

        send(b, block_at(b), 2, side).wait_send()
        send(b, block_at(b), 3, twin).wait_send()
        other = (z * n_x + (1 - x)) * 2 + core
        send(other, block_at(other), 3, twin).wait_send()


def gather_start(tokens, heads, small):
    n_ctx, n_x = lax.axis_size("ctx"), lax.axis_size("x")
    n = 2 * n_ctx * n_x
    slots, part, width = tokens.shape
    vmem = pl.BlockSpec(memory_space=pltpu.VMEM)
    anywhere = pl.BlockSpec(memory_space=pl.ANY)
    dma = pltpu.SemaphoreType.DMA
    return pl.pallas_call(
        partial(start_kernel, n_ctx=n_ctx, n_x=n_x),
        in_specs=[vmem, vmem, vmem],
        out_specs=[anywhere, vmem, vmem],
        out_shape=[
            jax.ShapeDtypeStruct((slots, n * part, width), tokens.dtype),
            jax.ShapeDtypeStruct(heads.shape, heads.dtype),
            jax.ShapeDtypeStruct((n,) + small.shape, small.dtype),
        ],
        scratch_shapes=[
            dma((2 * (n - 1),)), dma((4, n)), dma((3,)), dma((n,)), dma((n,)), dma((n,))
        ],
        compiler_params=pltpu.CompilerParams(
            collective_id=1, has_side_effects=True, vmem_limit_bytes=VMEM_LIMIT
        ),
        cost_estimate=pl.CostEstimate(
            flops=0, bytes_accessed=2 * n * tokens.size, transcendentals=0
        ),
        name="gather_start",
    )(tokens, heads, small)


def finish_kernel(
    out_ref, small_ref, qkv_ref, red_ref, join_ref, weight_ref, one_ref,
    g_down, g_up, g_out, g_small, g_qkv, g_bias, g_in,
    pair_small, pair_qkv, sum_qkv, qkvs,
    pair_down, pair_out, last_up, joins, partial_in, pair_in,
    join_send, join_recv, far_send, qkv_recv, y_send, y_recv,
    *, n_ctx, n_x
):
    ctx, x, core = (lax.axis_index(n) for n in GROUP)
    slot = lax.axis_index("slot")
    chip = ctx * n_x + x
    me = 2 * chip + core
    shard, width = g_out.shape
    part = g_down.shape[0] // 2
    peers = group_peers(n_ctx, n_x)
    lane_peers = [(z, a) for z, a, c in peers[1::2]]
    across = at_device(slot=1 - slot)
    corner = at_device(slot=1 - slot, core=1 - core)
    twin = at_device(core=1 - core)
    greet([at_device(ctx=z, x=a, core=c) for z, a, c in peers] + [across, corner])

    def remote(source, target_ref, send_sem, recv_sem, target):
        return pltpu.make_async_remote_copy(
            source, target_ref, send_sem, recv_sem, device_id=target, device_id_type=MESH)

    started = []

    def launch(copy):
        copy.start()
        started.append(copy)
        return copy

    def pair_copy(i, source, target_ref, target):
        return launch(remote(source, target_ref, y_send.at[i], y_recv.at[i], target))

    qkv_copy = pair_copy(0, qkv_ref, pair_qkv, across)
    mine = pl.multiple_of(part + core * shard, shard)
    theirs = pl.multiple_of(part + (1 - core) * shard, shard)
    for k, (z, a) in enumerate(lane_peers):
        launch(remote(
            join_ref.at[z * n_x + a], joins.at[chip], join_send.at[k], join_recv.at[chip],
            at_device(ctx=z, x=a)))
    down_copy = pair_copy(4, red_ref.at[pl.ds(0, part)], pair_down, across)
    quarter_copies = [
        pair_copy(5, red_ref.at[pl.ds(theirs, shard)], last_up.at[0], twin),
        pair_copy(6, red_ref.at[pl.ds(mine, shard)], last_up.at[1], across),
        pair_copy(7, red_ref.at[pl.ds(theirs, shard)], last_up.at[2], corner),
    ]

    small_copy = pair_copy(1, small_ref, pair_small, across)
    out_copy = pair_copy(3, out_ref, pair_out, across)
    qkv_copy.wait_recv()
    sum_qkv[...] = (qkv_ref[...].astype(F32) + pair_qkv[...].astype(F32)).astype(BF16)
    for k, (z, a, c) in enumerate(peers):
        them = (z * n_x + a) * 2 + c
        launch(remote(
            sum_qkv.at[them], qkvs.at[me], far_send.at[k], qkv_recv.at[me],
            at_device(ctx=z, x=a, core=c)))
    qkvs[me] = sum_qkv[me]

    def add_head(source, rows_of, first):
        weight = jnp.concatenate(
            [weight_ref[b, source] for b in range(weight_ref.shape[0])], axis=0)
        for h in range(2):
            owner = core if h == 0 else 1 - core
            rows = rows_of(owner)
            cols = rows.shape[2] // 2
            rows = jnp.concatenate(
                [r for t in range(rows.shape[0]) for r in (rows[t, :, :cols], rows[t, :, cols:])],
                axis=0)
            term = contract(rows, weight, 1, 1)
            partial_in[h] = term if first else partial_in[h] + term

    add_head(chip, lambda owner: join_ref[chip, owner], True)

    half = pl.multiple_of(slot * part, part)
    other_half = pl.multiple_of((1 - slot) * part, part)
    g_down[pl.ds(half, part), :] = red_ref[pl.ds(0, part), :].astype(F32)
    down_copy.wait_recv()
    g_down[pl.ds(other_half, part), :] = pair_down[...].astype(F32)

    def place_quarter(rows, quarter_core, quarter_slot):
        for k in range(n_ctx * n_x):
            at = pl.multiple_of(((2 * k + quarter_core) * 2 + quarter_slot) * part, part)
            g_up[:, pl.ds(at, part)] = rows[:, k * part : (k + 1) * part].astype(F32)

    place_quarter(red_ref[pl.ds(mine, shard), :], core, slot)
    quarter_copies[0].wait_recv()
    place_quarter(last_up[0], 1 - core, slot)
    quarter_copies[1].wait_recv()
    place_quarter(last_up[1], core, 1 - slot)
    quarter_copies[2].wait_recv()
    place_quarter(last_up[2], 1 - core, 1 - slot)

    for k, (z, a) in enumerate(lane_peers):
        source = z * n_x + a
        remote(
            join_ref.at[source], joins.at[source], join_send.at[k], join_recv.at[source], twin
        ).wait_recv()
        add_head(source, lambda owner: joins[source, owner], False)
    in_copy = pair_copy(2, partial_in.at[1], pair_in, twin)

    small_copy.wait_recv()
    g_small[...] = small_ref[...].astype(F32) + pair_small[...].astype(F32)
    in_copy.wait_recv()
    g_in[...] = (partial_in[0] + pair_in[...] + one_ref[...]).astype(BF16)
    for z, a, c in peers:
        them = (z * n_x + a) * 2 + c
        remote(
            sum_qkv.at[them], qkvs.at[them], far_send.at[0], qkv_recv.at[them], twin
        ).wait_recv()
    for k in range(n_ctx * n_x):
        heads = [qkvs[2 * k + c, :shard, :].astype(F32) for c in range(2)]
        for t in range(3):
            at = t * width + 2 * HD * k
            g_qkv[:, at : at + 2 * HD] = jnp.concatenate(
                [h[:, t * HD : (t + 1) * HD] for h in heads], axis=1)
        for c in range(2):
            g_bias[2 * k + c : 2 * k + c + 1, :] = qkvs[2 * k + c, shard : shard + 1, :].astype(F32)
    out_copy.wait_recv()
    g_out[...] = out_ref[...].astype(F32) + pair_out[...].astype(F32)
    for copy in started:
        copy.wait_send()


def finish_grads(out, small, qkv, reduced, joined, weight, grad_one):
    n_ctx, n_x = lax.axis_size("ctx"), lax.axis_size("x")
    n = 2 * n_ctx * n_x
    shard, width = out.shape
    part = reduced.shape[0] // 2
    vmem = pl.BlockSpec(memory_space=pltpu.VMEM)
    dma = pltpu.SemaphoreType.DMA

    def low(*shape):
        return pltpu.VMEM(shape, BF16)

    def wide(*shape):
        return jax.ShapeDtypeStruct(shape, F32)

    return pl.pallas_call(
        partial(finish_kernel, n_ctx=n_ctx, n_x=n_x),
        in_specs=[vmem] * 7,
        out_specs=[vmem] * 7,
        out_shape=[
            wide(2 * part, width),
            wide(shard, 4 * width),
            wide(shard, width),
            wide(*small.shape),
            wide(shard, 3 * width),
            wide(n, qkv.shape[2]),
            jax.ShapeDtypeStruct(grad_one.shape, BF16),
        ],
        scratch_shapes=[
            low(*small.shape),
            low(*qkv.shape),
            low(*qkv.shape),
            low(*qkv.shape),
            low(part, width),
            low(*out.shape),
            low(3, shard, width),
            low(*joined.shape),
            pltpu.VMEM((2,) + grad_one.shape, F32),
            pltpu.VMEM(grad_one.shape, F32),
            dma((n_ctx * n_x - 1,)),
            dma((n_ctx * n_x,)),
            dma((n - 1,)),
            dma((n,)),
            dma((8,)),
            dma((8,)),
        ],
        compiler_params=pltpu.CompilerParams(
            collective_id=2, has_side_effects=True, vmem_limit_bytes=VMEM_LIMIT
        ),
        cost_estimate=pl.CostEstimate(flops=0, bytes_accessed=16 * joined.size, transcendentals=0),
        name="finish_grads",
    )(out, small, qkv, reduced, joined, weight, grad_one)


def lane_gather(mine_ref, all_ref, send_sem, recv_sem, local_sem, n_ctx, n_x):
    ctx, x = lax.axis_index("ctx"), lax.axis_index("x")
    chip = ctx * n_x + x
    routes = (
        at_device(ctx=lax.rem(ctx + 1, n_ctx)),
        at_device(ctx=lax.rem(ctx + n_ctx - 1, n_ctx)),
        at_device(x=1 - x),
    )

    def send(k, lane, own=False):
        return pltpu.make_async_remote_copy(
            mine_ref if own else all_ref.at[k], all_ref.at[k], send_sem.at[lane, k], recv_sem.at[k],
            device_id=routes[lane], device_id_type=MESH)

    local = pltpu.make_async_copy(mine_ref, all_ref.at[chip], local_sem)

    def begin():
        @pl.when(ctx + 1 < n_ctx)
        def _():
            send(chip, 0, own=True).start()

        @pl.when(ctx > 0)
        def _():
            send(chip, 1, own=True).start()

        send(chip, 2, own=True).start()
        local.start()

    def relay(r):
        for sign, lane, more in ((-1, 0, ctx + 1 < n_ctx), (1, 1, ctx > 0)):
            z = ctx + sign * r

            @pl.when((z >= 0) & (z < n_ctx))
            def _():
                k = z * n_x + x
                send(k, 0).wait_recv()

                @pl.when(more)
                def _():
                    send(k, lane).start()

                send(k, 2).start()

    def end():
        for z in range(n_ctx):
            k = z * n_x + x
            send(z * n_x + 1 - x, 0).wait_recv()

            @pl.when((z <= ctx) & (ctx + 1 < n_ctx))
            def _():
                send(k, 0).wait_send()

            @pl.when((z >= ctx) & (ctx > 0))
            def _():
                send(k, 1).wait_send()

            send(k, 2).wait_send()
        local.wait()

    return begin, relay, end


QB = 512
KB = 512


def turn(pair, cosine, sine):
    half = HD // 2
    lanes = lax.broadcasted_iota(jnp.int32, (1, 2 * HD), 1)
    low = lax.rem(lanes, HD) < half
    swapped = jnp.where(low, pltpu.roll(pair, 2 * HD - half, 1), pltpu.roll(pair, half, 1))
    return pair * cosine + swapped * jnp.where(low, -sine, sine)


def heads_kernel(
    len_ref, tok_ref, w_ref, b_ref, cos_ref, sin_ref, wa_ref, wu_ref, wd_ref,
    q_ref, k_ref, v_ref, mix_ref, send_ref, norm_ref, fa_ref, fu_ref, fd_ref,
    a_send, a_recv, u_send, u_recv, d_send, d_recv, local_sem, *, n_ctx, n_x, part
):
    core = lax.axis_index("core")
    ctx, x = lax.axis_index("ctx"), lax.axis_index("x")
    greet([
        at_device(x=1 - x),
        at_device(ctx=lax.rem(ctx + 1, n_ctx)),
        at_device(ctx=lax.rem(ctx + n_ctx - 1, n_ctx)),
    ])
    flows = [
        lane_gather(wa_ref, fa_ref, a_send, a_recv, local_sem.at[0], n_ctx, n_x),
        lane_gather(wu_ref, fu_ref, u_send, u_recv, local_sem.at[1], n_ctx, n_x),
        lane_gather(wd_ref, fd_ref, d_send, d_recv, local_sem.at[2], n_ctx, n_x),
    ]
    for begin, _, _ in flows:
        begin()
    slots, seq, _ = q_ref.shape

    def relay(r):
        if r < n_ctx:
            for _, hop, _ in flows:
                hop(r)

    def project(s):
        @pl.loop(0, seq // QB)
        def _(i):
            at = pl.multiple_of(i * QB, QB)
            rows = pl.ds(at, QB)
            tokens = tok_ref[pl.ds(pl.multiple_of(s * seq + at, QB), QB), :]
            joined = mm(tokens, w_ref[...]) + b_ref[...]
            turned = turn(joined[:, : 2 * HD], cos_ref[rows, :], sin_ref[rows, :])
            q_ref[s, rows, :] = (turned[:, :HD].astype(BF16) * HD ** (-0.5)).astype(BF16)
            k_ref[s, rows, :] = turned[:, HD:].astype(BF16)
            v_ref[s, rows, :] = joined[:, 2 * HD :].astype(BF16)

    def attend(s, first, last):
        length = len_ref[s]

        @pl.loop(first, last)
        def _(i):
            rows = pl.ds(pl.multiple_of(i * QB, QB), QB)
            queries = q_ref[s, rows, :]

            def step(j, state):
                highest, total, mix = state
                start = pl.multiple_of(j * KB, KB)
                scores = contract(queries, k_ref[s, pl.ds(start, KB), :], 1, 1)
                ids = start + lax.broadcasted_iota(jnp.int32, (1, KB), 1)
                scores = jnp.where(ids < length, scores, NEG_FILL)
                higher = jnp.maximum(highest, jnp.max(scores, axis=1, keepdims=True))
                fade = jnp.exp(highest - higher)
                weights = jnp.exp(scores - higher)
                total = total * fade + jnp.sum(weights, axis=1, keepdims=True)
                mix = mix * fade + mm(weights.astype(BF16), v_ref[s, pl.ds(start, KB), :])
                return higher, total, mix

            highest, total, mix = lax.fori_loop(
                0,
                seq // KB,
                step,
                (
                    jnp.full((QB, 1), NEG_FILL, F32),
                    jnp.zeros((QB, 1), F32),
                    jnp.zeros((QB, HD), F32),
                ),
            )
            mix = mix / total
            mix_ref[s, rows, :] = mix
            log_norm = jnp.broadcast_to(highest + jnp.log(total), (QB, 128))
            norm_ref[s, :, rows] = jnp.transpose(log_norm)[0:1, :]
            low = mix.astype(BF16)
            chips = QB // (2 * part)
            for chip in range(chips):
                for half in range(2):
                    at = (2 * chip + half) * part
                    send_ref[i * chips + chip, half ^ core, s] = low[at : at + part]

    blocks = seq // QB
    for s in range(slots):
        project(s)
    relay(1)
    attend(0, 0, blocks)
    relay(2)
    for s in range(1, slots):
        attend(s, 0, blocks)
    for r in range(3, n_ctx):
        relay(r)
    for _, _, end in flows:
        end()


def heads(lengths, tokens, weight, bias, cosine, sine, part, *shards):
    n_ctx, n_x = lax.axis_size("ctx"), lax.axis_size("x")
    chips = n_ctx * n_x
    slots, seq = lengths.shape[0], cosine.shape[0]
    vmem = pl.BlockSpec(memory_space=pltpu.VMEM)
    anywhere = pl.BlockSpec(memory_space=pl.ANY)
    dma = pltpu.SemaphoreType.DMA
    head = jax.ShapeDtypeStruct((slots, seq, HD), BF16)
    return pl.pallas_call(
        partial(heads_kernel, n_ctx=n_ctx, n_x=n_x, part=part),
        in_specs=[pl.BlockSpec(memory_space=pltpu.SMEM)] + [vmem] * 8,
        out_specs=[vmem] * 6 + [anywhere] * 3,
        out_shape=[
            head,
            head,
            head,
            jax.ShapeDtypeStruct((slots, seq, HD), F32),
            jax.ShapeDtypeStruct((chips, 2, slots, part, HD), BF16),
            jax.ShapeDtypeStruct((slots, 1, seq), F32),
        ]
        + [jax.ShapeDtypeStruct((chips,) + w.shape, w.dtype) for w in shards],
        scratch_shapes=[dma((3, chips)), dma((chips,))] * 3 + [dma((3,))],
        compiler_params=pltpu.CompilerParams(
            collective_id=5, has_side_effects=True, vmem_limit_bytes=VMEM_LIMIT
        ),
        cost_estimate=pl.CostEstimate(
            flops=16 * slots * seq * seq * HD,
            bytes_accessed=2 * tokens.size,
            transcendentals=slots * seq * seq,
        ),
        name="heads",
    )(lengths, tokens, weight, bias, cosine, sine, *shards)


def grads_kernel(
    len_ref, q_ref, k_ref, v_ref, g_ref, norm_ref, dot_ref, tok_ref, cos_ref, sin_ref,
    down_ref, up_ref, out_ref, small_ref,
    join_ref, grad_ref, red_ref, sum_ref, small_sum,
    dqt, key_grads, value_grads, total, bias, x_down, x_up, x_out, s_down, s_up, s_out,
    z_down, z_up, z_out, own_down, own_up, own_out, smalls,
    x_send, x_recv, z_send, z_recv, small_send, small_recv, *, n_ctx, n_x, part
):
    ctx, x, core = (lax.axis_index(n) for n in GROUP)
    me = (ctx * n_x + x) * 2 + core
    peers = group_peers(n_ctx, n_x)
    greet([at_device(ctx=z, x=a, core=c) for z, a, c in peers])
    side = at_device(x=1 - x)
    arrays = (
        (down_ref, x_down, s_down, z_down, own_down),
        (up_ref, x_up, s_up, z_up, own_up),
        (out_ref, x_out, s_out, z_out, own_out),
    )

    def remote(source, target_ref, send_sem, recv_sem, target):
        return pltpu.make_async_remote_copy(
            source, target_ref, send_sem, recv_sem, device_id=target, device_id_type=MESH)

    places = [lax.rem(ctx + 1 + j, n_ctx) for j in range(n_ctx)]
    first = [
        [
            remote(
                ref.at[places[j] * n_x + 1 - x], x_in.at[j], x_send.at[i, j], x_recv.at[i, j], side)
            for i, (ref, x_in, _, _, _) in enumerate(arrays)
        ]
        for j in range(n_ctx)
    ]
    second = [
        [
            remote(
                s_out_.at[j], z_in.at[j], z_send.at[i, j], z_recv.at[i, j],
                at_device(ctx=places[j]))
            for i, (_, _, s_out_, z_in, _) in enumerate(arrays)
        ]
        for j in range(n_ctx - 1)
    ]
    pushes = []
    for k, (z, a, c) in enumerate(peers):
        them = (z * n_x + a) * 2 + c
        pushes.append(remote(
            small_ref.at[them], smalls.at[me], small_send.at[k], small_recv.at[me],
            at_device(ctx=z, x=a, core=c)))
    for copies in first:
        for copy in copies:
            copy.start()
    for copy in pushes:
        copy.start()
    smalls[me] = small_ref[me]

    def stage(j):
        for i, (ref, x_in, s_low, _, own) in enumerate(arrays):
            first[j][i].wait_recv()
            pair = ref[places[j] * n_x + x].astype(F32) + x_in[j].astype(F32)
            if j < n_ctx - 1:
                s_low[j] = pair.astype(BF16)
                second[j][i].start()
            else:
                own[...] = pair

    slots, seq, _ = q_ref.shape
    total[...] = jnp.zeros_like(total)
    bias[...] = jnp.zeros_like(bias)

    def attention(s, between):
        length = len_ref[s]
        dqt[...] = jnp.zeros_like(dqt)

        @pl.loop(0, seq // KB)
        def _(j):
            start = pl.multiple_of(j * KB, KB)
            key_block = k_ref[s, pl.ds(start, KB), :]
            value_block = v_ref[s, pl.ds(start, KB), :]
            turned = jnp.transpose(key_block.astype(F32)).astype(BF16)
            ids = start + lax.broadcasted_iota(jnp.int32, (KB, 1), 0)
            shift = jnp.where(ids < length, 0.0, NEG_FILL)
            for at_step, number in between:
                @pl.when(j == at_step)
                def _():
                    stage(number)

            def step(i, state):
                key_grad, value_grad = state
                at = pl.multiple_of(i * QB, QB)
                queries = q_ref[s, pl.ds(at, QB), :]
                grads = g_ref[s, pl.ds(at, QB), :]
                scores = contract(key_block, queries, 1, 1) + shift
                probs = jnp.exp(scores - norm_ref[s, :, pl.ds(at, QB)])
                grad_probs = contract(value_block, grads, 1, 1)
                grad_scores = (probs * (grad_probs - dot_ref[s, :, pl.ds(at, QB)])).astype(BF16)
                value_grad = value_grad + mm(probs.astype(BF16), grads)
                key_grad = key_grad + mm(grad_scores, queries)
                dqt[:, pl.ds(at, QB)] += mm(turned, grad_scores)
                return key_grad, value_grad

            zero = jnp.zeros((KB, HD), F32)
            key_grad, value_grad = lax.fori_loop(0, seq // QB, step, (zero, zero))
            key_grads[pl.ds(start, KB), :] = key_grad
            value_grads[pl.ds(start, KB), :] = value_grad

    def join(s):
        @pl.loop(0, seq // QB)
        def _(i):
            at = pl.multiple_of(i * QB, QB)
            rows = pl.ds(at, QB)
            query_grad = jnp.transpose(dqt[:, rows]) * HD ** (-0.5)
            pair = jnp.concatenate([query_grad, key_grads[rows, :]], axis=1)
            turned = turn(pair, cos_ref[rows, :], -sin_ref[rows, :])
            joined = jnp.concatenate([turned, value_grads[rows, :]], axis=1).astype(BF16)
            chips = QB // (2 * part)
            for chip in range(chips):
                for owner in range(2):
                    near = (2 * chip + owner) * part
                    upper = joined[near : near + part // 2]
                    lower = joined[near + part // 2 : near + part]
                    join_ref[i * chips + chip, owner, s] = jnp.concatenate([upper, lower], axis=1)
            tokens = tok_ref[pl.ds(pl.multiple_of(s * seq + at, QB), QB), :]
            total[...] += contract(joined, tokens, 0, 0)
            bias[...] += jnp.sum(joined.astype(F32), axis=0, keepdims=True)

    for s in range(slots):
        attention(s, [(1, 1)] if s == 1 else [])
        stage(0 if s == 0 else 2)
        join(s)
    turned_total = jnp.transpose(total[...])
    shard = turned_total.shape[0] // grad_ref.shape[0]
    extra = jnp.broadcast_to(bias[...], (grad_ref.shape[1] - shard, bias.shape[1]))
    for d in range(grad_ref.shape[0]):
        grad_ref[d, :shard] = turned_total[d * shard : (d + 1) * shard].astype(BF16)
        grad_ref[d, shard:] = extra.astype(BF16)
    for j in range(slots + 1, n_ctx):
        stage(j)
    for z, a, c in peers:
        them = (z * n_x + a) * 2 + c
        remote(
            small_ref.at[them], smalls.at[them], small_send.at[0], small_recv.at[them], side
        ).wait_recv()
    small_sum[...] = jnp.sum(smalls[...].astype(F32), axis=0).astype(BF16)
    for j in range(n_ctx - 1):
        for i, (_, _, _, z_in, own) in enumerate(arrays):
            second[j][i].wait_recv()
            own[...] += z_in[j].astype(F32)
    rows = own_down.shape[0]
    red_ref[:rows] = own_down[...].astype(BF16)
    red_ref[rows:] = own_up[...].astype(BF16)
    sum_ref[...] = own_out[...].astype(BF16)
    for copies in first + second + [pushes]:
        for copy in copies:
            copy.wait_send()


def grads(lengths, queries, keys, values, grad_heads, norms, dots, tokens, cosine, sine,
          down, up, out, small, part):
    n_ctx, n_x = lax.axis_size("ctx"), lax.axis_size("x")
    n = 2 * n_ctx * n_x
    slots, seq, _ = queries.shape
    width = tokens.shape[1]
    shard = width // n
    cols = 3 * HD
    vmem = pl.BlockSpec(memory_space=pltpu.VMEM)
    dma = pltpu.SemaphoreType.DMA
    parts = (down, up, out)

    def low(*dims):
        return jax.ShapeDtypeStruct(dims, BF16)

    return pl.pallas_call(
        partial(grads_kernel, n_ctx=n_ctx, n_x=n_x, part=part),
        in_specs=[pl.BlockSpec(memory_space=pltpu.SMEM)] + [vmem] * 13,
        out_specs=[vmem] * 5,
        out_shape=[
            low(seq // (2 * part), 2, slots, part // 2, 2 * cols),
            low(n, shard + 16, cols),
            low(down.shape[1] + up.shape[1], width),
            low(*out.shape[1:]),
            low(*small.shape[1:]),
        ],
        scratch_shapes=[
            pltpu.VMEM((HD, seq), F32),
            pltpu.VMEM((seq, HD), F32),
            pltpu.VMEM((seq, HD), F32),
            pltpu.VMEM((cols, width), F32),
            pltpu.VMEM((1, cols), F32),
        ]
        + [pltpu.VMEM((n_ctx,) + t.shape[1:], BF16) for t in parts]
        + [pltpu.VMEM((n_ctx - 1,) + t.shape[1:], BF16) for t in parts]
        + [pltpu.VMEM((n_ctx - 1,) + t.shape[1:], BF16) for t in parts]
        + [pltpu.VMEM(t.shape[1:], F32) for t in parts]
        + [
            pltpu.VMEM(small.shape, BF16),
            dma((3, n_ctx)),
            dma((3, n_ctx)),
            dma((3, n_ctx - 1)),
            dma((3, n_ctx - 1)),
            dma((n - 1,)),
            dma((n,)),
        ],
        compiler_params=pltpu.CompilerParams(
            collective_id=6, has_side_effects=True, vmem_limit_bytes=VMEM_LIMIT
        ),
        cost_estimate=pl.CostEstimate(
            flops=40 * slots * seq * seq * HD,
            bytes_accessed=4 * tokens.size,
            transcendentals=slots * seq * seq,
        ),
        name="grads",
    )(lengths, queries, keys, values, grad_heads, norms, dots, tokens, cosine, sine,
      down, up, out, small)


def norm_forward(values, gain, shift):
    center = values - jnp.mean(values, axis=-1, keepdims=True)
    spread = jnp.mean(center * center, axis=-1, keepdims=True)
    root = lax.rsqrt(spread + LN_EPS)
    unit = center * root
    return unit * gain + shift, unit, root


def norm_backward(grad, unit, root, gain):
    scaled = grad * gain
    inner = scaled - jnp.mean(scaled, axis=-1, keepdims=True)
    inner = inner - unit * jnp.mean(scaled * unit, axis=-1, keepdims=True)
    return root * inner, jnp.sum(grad * unit, axis=0), jnp.sum(grad, axis=0)


def gelu_pair(values):
    half = 0.5 + 0.5 * lax.erf(values * 0.7071067811865476)
    bell = jnp.exp(-0.5 * values * values) * 0.3989422804014327
    return values * half, half + values * bell


def rope_rows(positions):
    halfway = HD // 2
    ladder = jnp.arange(halfway, dtype=F32) * (2.0 / HD)
    frequency = jnp.power(jnp.float32(10000.0), -ladder)
    angles = positions[:, None] * frequency[None, :]
    return jnp.cos(angles), jnp.sin(angles)


def layer_kernel(
    merged_ref, tok_ref, wo_ref, up_ref, down_ref, vec_ref, full_ref, lane_ref,
    out_ref, one_ref, gm_ref, att_ref, vecs_ref, act_out, hid_out, gdn_out, gup_out, lanes_out,
    first, first_in, hid, act, slope, gdn, gup, hidden, unit_one, two,
    roots, near, near_in, far, far_in, low_out, low_in, send_sem, recv_sem, out_sem,
    lane_send, lane_recv, *, n_ctx, n_x
):
    core, slot = lax.axis_index("core"), lax.axis_index("slot")
    twin, across = at_device(core=1 - core), at_device(slot=1 - slot)
    ctx, x = lax.axis_index("ctx"), lax.axis_index("x")
    greet([
        twin,
        across,
        at_device(x=1 - x),
        at_device(ctx=lax.rem(ctx + 1, n_ctx)),
        at_device(ctx=lax.rem(ctx + n_ctx - 1, n_ctx)),
    ])
    begin_lane, relay_lane, end_lane = lane_gather(
        lane_ref, lanes_out, lane_send, lane_recv, out_sem.at[4], n_ctx, n_x)
    begin_lane()
    rows, width = tok_ref.shape
    half = rows // 2
    tile = 256
    count = [0]
    started = []

    def launch(source, target_ref, target):
        i = count[0]
        count[0] += 1
        copy = pltpu.make_async_remote_copy(
            source, target_ref, send_sem.at[i], recv_sem.at[i],
            device_id=target, device_id_type=MESH)
        copy.start()
        started.append(copy)
        return copy

    def columns(body, n=width // tile):
        @pl.loop(0, n)
        def _(t):
            body(pl.ds(pl.multiple_of(t * tile, tile), tile))

    def chunks(body, size=64):
        @pl.loop(0, rows // size)
        def _(t):
            body(pl.ds(pl.multiple_of(t * size, size), size))

    def exchange(buf, turn, stage, product):
        halves = [
            launch(buf.at[pl.ds(h * half, half)], buf.at[pl.ds((2 + h) * rows, half)], across)
            for h in range(2)
        ]
        to_twin = launch(buf.at[pl.ds(0, rows)], buf.at[pl.ds(rows, rows)], twin)
        near_buf, far_buf = near.at[turn], far.at[turn]
        to_twin.wait_recv()
        stage(0, 2 * rows)
        product(0, 2 * rows, near_buf, 0)
        near_copy = launch(
            near_buf.at[pl.ds(rows, rows)], near_in.at[turn], twin)
        back = []
        for h in range(2):
            at = (2 + h) * rows
            halves[h].wait_recv()
            launch(
                buf.at[pl.ds(at, half)], buf.at[pl.ds(at + half, half)], twin).wait_recv()
            stage(at, rows)
            product(at, rows, far_buf, h * rows)
            i = 2 * turn + h
            launch(
                far_buf.at[pl.ds(h * rows + half, half)], far_in.at[i], twin).wait_recv()
            low_out[i] = (far_buf[pl.ds(h * rows, half), :] + far_in[i]).astype(BF16)
            back.append(launch(low_out.at[i], low_in.at[i], across))
        return near_copy, back

    def out_product(cols):
        first[:, cols] = mm(merged_ref[...], wo_ref[:, cols])

    columns(out_product)
    launch(first.at[pl.ds(rows, rows)], first_in, twin).wait_recv()

    def norm_one(at):
        values = tok_ref[at, :].astype(F32) + first[at, :] + first_in[at, :] + vec_ref[0:1, :]
        normed, unit, root = norm_forward(values, vec_ref[1:2, :], vec_ref[2:3, :])
        hidden[at, :] = normed
        unit_one[at, :] = unit
        roots[0, at, :] = jnp.broadcast_to(root, (root.shape[0], 128))
        hid[at, :] = normed.astype(BF16)

    chunks(norm_one)

    def up_stage(start, size):
        def body(cols):
            values = mm(hid[start : start + size, :], up_ref[:, cols]) + vec_ref[3:4, cols]
            active, bend = gelu_pair(values)
            act[start : start + size, cols] = active.astype(BF16)
            slope[start : start + size, cols] = bend

        columns(body)

    def down_product(start, size, target, at):
        def body(cols):
            target[at : at + size, cols] = mm(act[start : start + size, :], down_ref[:, cols])

        columns(body)

    near_copy, back = exchange(hid, 0, up_stage, down_product)
    relay_lane(1)
    out_copies = [
        pltpu.make_async_copy(hid, hid_out, out_sem.at[0]),
        pltpu.make_async_copy(act, act_out, out_sem.at[1]),
    ]
    for copy in out_copies:
        copy.start()
    vecs_ref[...] = jnp.zeros_like(vecs_ref)
    near_copy.wait_recv()

    def norm_two(at, h, local):
        downward = near[0, at, :] + near_in[0, at, :] + low_in[h, local, :].astype(F32)
        values = hidden[at, :] + downward + vec_ref[4:5, :]
        normed, unit, root = norm_forward(values, vec_ref[5:6, :], vec_ref[6:7, :])
        out_ref[at, :] = normed.astype(BF16)
        grad, gain, shift = norm_backward(full_ref[at, :], unit, root, vec_ref[5:6, :])
        two[at, :] = grad
        low = grad.astype(BF16)
        gdn[at, :] = low
        vecs_ref[5:6, :] += gain[None]
        vecs_ref[6:7, :] += shift[None]
        vecs_ref[4:5, :] += jnp.sum(low.astype(F32), axis=0, keepdims=True)

    def by_half(body, h, size=64):
        @pl.loop(0, half // size)
        def _(t):
            local = pl.multiple_of(t * size, size)
            body(pl.ds(h * half + local, size), h, pl.ds(local, size))

    for h in range(2):
        back[h].wait_recv()
        by_half(norm_two, h)

    def back_stage(start, size):
        def body(cols):
            grads = contract(gdn[start : start + size, :], down_ref[cols, :], 1, 1)
            low = (grads * slope[start : start + size, cols]).astype(BF16)
            gup[start : start + size, cols] = low
            vecs_ref[3:4, cols] += jnp.sum(low.astype(F32), axis=0, keepdims=True)

        columns(body)

    def back_product(start, size, target, at):
        def body(cols):
            target[at : at + size, cols] = contract(
                gup[start : start + size, :], up_ref[cols, :], 1, 1)

        columns(body)

    relay_lane(2)
    near_copy, back = exchange(gdn, 1, back_stage, back_product)
    for r in range(3, n_ctx):
        relay_lane(r)
    late_copies = [
        pltpu.make_async_copy(gdn, gdn_out, out_sem.at[2]),
        pltpu.make_async_copy(gup, gup_out, out_sem.at[3]),
    ]
    for copy in late_copies:
        copy.start()
    near_copy.wait_recv()

    def norm_back(at, h, local):
        grad = near[1, at, :] + near_in[1, at, :] + low_in[2 + h, local, :].astype(F32)
        grad = grad + two[at, :]
        root = roots[0, at, 0:1]
        one, gain, shift = norm_backward(grad, unit_one[at, :], root, vec_ref[1:2, :])
        one_ref[at, :] = one
        low = one.astype(BF16)
        att_ref[at, :] = low
        vecs_ref[1:2, :] += gain[None]
        vecs_ref[2:3, :] += shift[None]
        vecs_ref[0:1, :] += jnp.sum(low.astype(F32), axis=0, keepdims=True)

    for h in range(2):
        back[h].wait_recv()
        by_half(norm_back, h)
    launch(att_ref.at[pl.ds(0, rows)], att_ref.at[pl.ds(rows, rows)], twin).wait_recv()

    def merged_product(cols):
        gm_ref[:, cols] = contract(att_ref[...], wo_ref[cols, :], 1, 1).astype(BF16)

    columns(merged_product, wo_ref.shape[0] // tile)
    end_lane()
    for copy in started:
        copy.wait_send()
    for copy in out_copies + late_copies:
        copy.wait()


def layer(merged, tokens, w_out, up, down, vectors, grad_full, lane_shard):
    n_ctx, n_x = lax.axis_size("ctx"), lax.axis_size("x")
    chips = n_ctx * n_x
    rows, width = tokens.shape
    hidden = up.shape[1]
    lane = w_out.shape[0]
    vmem = pl.BlockSpec(memory_space=pltpu.VMEM)
    anywhere = pl.BlockSpec(memory_space=pl.ANY)
    dma = pltpu.SemaphoreType.DMA

    def shape(*dims, dtype=BF16):
        return jax.ShapeDtypeStruct(dims, dtype)

    def wide(*dims):
        return pltpu.VMEM(dims, F32)

    def low(*dims):
        return pltpu.VMEM(dims, BF16)

    return pl.pallas_call(
        partial(layer_kernel, n_ctx=n_ctx, n_x=n_x),
        in_specs=[vmem] * 8,
        out_specs=[vmem] * 5 + [anywhere] * 5,
        out_shape=[
            shape(rows, width),
            shape(rows, width, dtype=F32),
            shape(2 * rows, lane),
            shape(2 * rows, width),
            shape(8, width, dtype=F32),
            shape(4 * rows, hidden),
            shape(4 * rows, width),
            shape(4 * rows, width),
            shape(4 * rows, hidden),
            shape(chips, *lane_shard.shape),
        ],
        scratch_shapes=[
            wide(2 * rows, width),
            wide(rows, width),
            low(4 * rows, width),
            low(4 * rows, hidden),
            wide(4 * rows, hidden),
            low(4 * rows, width),
            low(4 * rows, hidden),
            wide(rows, width),
            wide(rows, width),
            wide(rows, width),
            wide(1, rows, 128),
            wide(2, 2 * rows, width),
            wide(2, rows, width),
            wide(2, 2 * rows, width),
            wide(4, rows // 2, width),
            low(4, rows // 2, width),
            low(4, rows // 2, width),
            dma((24,)),
            dma((24,)),
            dma((5,)),
            dma((3, chips)),
            dma((chips,)),
        ],
        compiler_params=pltpu.CompilerParams(
            collective_id=3, has_side_effects=True, vmem_limit_bytes=VMEM_LIMIT
        ),
        cost_estimate=pl.CostEstimate(
            flops=16 * rows * width * hidden, bytes_accessed=16 * rows * width, transcendentals=0
        ),
        name="layer",
    )(merged, tokens, w_out, up, down, vectors, grad_full, lane_shard)


def head_device(
    tokens,
    lengths,
    w_qkv,
    b_qkv,
    w_out,
    b_out,
    ln1_gain,
    ln1_bias,
    w_up,
    b_up,
    w_down,
    b_down,
    ln2_gain,
    ln2_bias,
    w_proj,
    cot_out,
    cot_emb,
):
    n_lane = lax.axis_size("ctx") * lax.axis_size("x")
    n_group = 2 * n_lane
    core = lax.axis_index("core")
    slot = lax.axis_index("slot")
    chip = lax.axis_index("ctx") * lax.axis_size("x") + lax.axis_index("x")
    me = 2 * chip + core
    slots, part, width = tokens.shape
    seq = part * n_group
    rows = slots * part
    shard = width // n_group
    ff_shard = w_down.shape[0]
    ff_half = ff_shard // 2
    proj = w_proj.shape[1]
    head_cols = 3 * HD

    small = jnp.concatenate(
        [b_qkv, b_out, ln1_gain, ln1_bias, b_up, b_down, ln2_gain, ln2_bias]
    )
    small_at = [0]
    for piece in (b_qkv, b_out, ln1_gain, ln1_bias, b_up, b_down, ln2_gain, ln2_bias):
        small_at.append(small_at[-1] + piece.shape[0])
    small_rows = -(-small.shape[0] // proj)
    small_rows = -(-small_rows // 16) * 16
    small = jnp.pad(small, (0, small_rows * proj - small.shape[0])).reshape(small_rows, proj)
    def two_lanes(mine, theirs):
        low_first = jnp.stack([mine, theirs], axis=0)
        high_first = jnp.stack([theirs, mine], axis=0)
        return jnp.where(core == 0, low_first, high_first)

    up_split = w_up.reshape(shard, n_lane, 2, 2, ff_half)
    up_mine = pick(up_split, core, 2)
    up_theirs = swap_core(pick(up_split, 1 - core, 2))
    up_chip = two_lanes(pick(up_mine, slot, 2), pick(up_theirs, slot, 2))
    down_split = w_down.reshape(2, ff_half, width)

    by_head = w_qkv.reshape(shard, 3, n_group, HD).transpose(2, 0, 1, 3)
    all_tokens, my_head, packed = gather_start(
        tokens,
        by_head.reshape(n_group, shard, head_cols),
        jnp.concatenate([w_proj, small], axis=0),
    )
    proj_full = packed[:, :shard].reshape(width, proj)
    smalls = packed[:, shard:].reshape(n_group, small_rows * proj).astype(F32)
    qkv_bias, out_bias, gain_one, shift_one, up_bias, down_bias, gain_two, shift_two = (
        smalls[:, a:b].reshape(-1) for a, b in zip(small_at[:-1], small_at[1:])
    )

    head_weight = my_head.reshape(width, head_cols)
    all_tokens = all_tokens.reshape(slots * seq, width)
    head_bias = pick(qkv_bias.reshape(1, 3, n_group, HD), me, 2).reshape(1, head_cols)
    cosine, sine = rope_rows(jnp.arange(seq, dtype=jnp.int32).astype(F32))
    cos_wide = jnp.tile(cosine, (1, 4))
    sin_wide = jnp.tile(sine, (1, 4))
    queries, keys, values, mixture, send, norms, out_lane, up, down = heads(
        lengths,
        all_tokens,
        head_weight,
        head_bias,
        cos_wide,
        sin_wide,
        part,
        w_out,
        up_chip.reshape(2 * shard, n_lane * ff_half),
        pick(down_split, slot, 0),
    )
    out_lane, up, down = (t.reshape(-1, t.shape[2]) for t in (out_lane, up, down))
    bias_lane = pick(up_bias.reshape(n_lane, 2, 2, ff_half), core, 1)
    up_bias_own = pick(bias_lane, slot, 1).reshape(-1)

    qkv_split = w_qkv.reshape(shard, 3, n_lane, 2, HD)
    qkv_mine = pick(qkv_split, core, 3)
    qkv_theirs = swap_core(pick(qkv_split, 1 - core, 3))
    qkv_chip = two_lanes(qkv_mine, qkv_theirs).transpose(3, 0, 1, 2, 4)
    qkv_chip = qkv_chip.reshape(n_lane, 2 * shard, head_cols)

    merged = lax.all_to_all(send, LANE, 0, 0, tiled=True)
    merged = merged.transpose(1, 2, 3, 0, 4).reshape(2 * rows, n_lane * HD)

    place = me * part + jnp.arange(part, dtype=jnp.int32)
    live = (place[None, :] < lengths[:, None]).reshape(rows, 1)
    grad_out = jnp.where(live, cot_out.reshape(rows, width).astype(F32), 0.0)
    grad_emb = jnp.where(live, cot_emb.reshape(rows, proj), 0)
    grad_full = grad_out + contract(grad_emb, proj_full, 1, 1)
    vectors = jnp.stack(
        [out_bias, gain_one, shift_one, up_bias_own, down_bias, gain_two, shift_two, shift_two]
    )
    (
        out_low,
        grad_one,
        grad_merged,
        grad_att,
        vector_grads,
        active,
        hidden_low,
        grad_down,
        grad_up,
        qkv_lane,
    ) = layer(
        merged, tokens.reshape(rows, width), out_lane, up, down, vectors, grad_full, qkv_chip
    )
    d_down = contract(active, grad_down, 0, 0).astype(BF16)
    d_up = contract(hidden_low, grad_up, 0, 0).astype(BF16)
    embeds = mm(out_low, proj_full).astype(BF16)
    d_proj = contract(out_low, grad_emb, 0, 0)
    (
        d_out_bias,
        d_gain_one,
        d_shift_one,
        up_bias_own_grad,
        d_down_bias,
        d_gain_two,
        d_shift_two,
    ) = (vector_grads[i] for i in range(7))
    grad_merged = grad_merged.reshape(2, slots, part, n_lane, HD).transpose(3, 0, 1, 2, 4)
    grad_heads = lax.all_to_all(grad_merged, LANE, 0, 0, tiled=True)

    def core_order(value):
        return jnp.where(core == 0, value, jnp.flip(value, axis=1))

    grad_heads = core_order(grad_heads).transpose(2, 0, 1, 3, 4).reshape(slots, seq, HD)

    d_out = contract(merged, grad_att, 0, 0).astype(BF16)

    spread = (
        (jnp.arange(2) == core)[:, None, None] & (jnp.arange(2) == slot)[None, :, None]
    ).astype(F32)
    up_bias_grad = up_bias_own_grad.reshape(n_lane, 1, 1, ff_half) * spread[None]
    vectors = (
        d_out_bias,
        d_gain_one,
        d_shift_one,
        up_bias_grad.reshape(-1),
        d_down_bias,
        d_gain_two,
        d_shift_two,
    )
    small_grad = jnp.concatenate([v.reshape(n_group, -1) for v in vectors], axis=1)
    small_cols = small_grad.shape[1]
    vec_rows = -(-small_cols // proj)
    vec_rows = -(-(shard + vec_rows) // 16) * 16 - shard
    small_grad = jnp.pad(small_grad, ((0, 0), (0, vec_rows * proj - small_cols)))
    small_grad = jnp.concatenate(
        [d_proj.reshape(n_group, shard, proj), small_grad.reshape(n_group, vec_rows, proj)], axis=1
    )
    row_dots = jnp.sum(grad_heads.astype(F32) * mixture, axis=-1).reshape(slots, 1, seq)
    joined, d_qkv, reduced, out_sum, small_sum = grads(
        lengths,
        queries,
        keys,
        values,
        grad_heads,
        norms,
        row_dots,
        all_tokens,
        cos_wide,
        sin_wide,
        d_down.reshape(n_lane, 2 * shard, width),
        d_up.reshape(n_lane, 2 * shard, width),
        d_out.reshape(n_lane, shard, width),
        small_grad.astype(BF16),
        part,
    )
    grad_w_down, grad_w_up, grad_w_out, small_sum, grad_w_qkv, bias_rows, input_grad = finish_grads(
        out_sum,
        small_sum,
        d_qkv,
        reduced,
        joined,
        qkv_lane,
        grad_one,
    )
    grad_w_proj = small_sum[:shard]
    vec_sum = small_sum[shard:].reshape(-1)
    vec_outs = []
    at = 0
    for v in vectors:
        size = v.size // n_group
        vec_outs.append(vec_sum[at : at + size])
        at += size
    (
        grad_b_out,
        grad_gain_one,
        grad_shift_one,
        grad_b_up,
        grad_b_down,
        grad_gain_two,
        grad_shift_two,
    ) = vec_outs

    qkv_bias_grad = bias_rows.reshape(n_group, 3, HD).transpose(1, 0, 2).reshape(-1)
    grad_b_qkv = lax.dynamic_slice(qkv_bias_grad, (me * b_qkv.shape[0],), (b_qkv.shape[0],))

    return (
        out_low.reshape(slots, part, width),
        embeds.reshape(slots, part, proj),
        input_grad.reshape(slots, part, width),
        grad_w_qkv,
        grad_b_qkv,
        grad_w_out,
        grad_b_out,
        grad_gain_one,
        grad_shift_one,
        grad_w_up,
        grad_b_up,
        grad_w_down,
        grad_b_down,
        grad_gain_two,
        grad_shift_two,
        grad_w_proj,
    )


def layer_norm(hidden, gain, shift):
    center = hidden - jnp.mean(hidden, axis=-1, keepdims=True)
    spread = jnp.mean(center * center, axis=-1, keepdims=True)
    return center * lax.rsqrt(spread + LN_EPS) * gain + shift


def rope_tables(positions, head_width):
    halfway = head_width // 2
    ladder = jnp.arange(halfway, dtype=jnp.float32) * (2.0 / head_width)
    frequency = jnp.power(jnp.float32(10000.0), -ladder)
    angles = positions[:, None] * frequency[None, :]
    return (jnp.cos(angles)[:, None, :], jnp.sin(angles)[:, None, :])


def rotate(values, cosine, sine_part):
    halfway = values.shape[-1] // 2
    first_half = values[..., :halfway]
    second_half = values[..., halfway:]
    return jnp.concatenate(
        [
            first_half * cosine - second_half * sine_part,
            second_half * cosine + first_half * sine_part,
        ],
        axis=-1,
    )


def block_scores(query_block, key_block, key_start, length, scale):
    scores = (
        jnp.einsum("qhd,khd->hqk", query_block, key_block, preferred_element_type=jnp.float32)
        * scale
    )
    key_ids = key_start + jnp.arange(key_block.shape[0], dtype=jnp.int32)
    return jnp.where((key_ids < length)[None, None, :], scores, NEG_FILL)


def per_device(
    tokens,
    lengths,
    w_qkv,
    b_qkv,
    w_out,
    b_out,
    ln1_gain,
    ln1_bias,
    w_up,
    b_up,
    w_down,
    b_down,
    ln2_gain,
    ln2_bias,
    w_proj,
    cot_out,
    cot_emb,
):
    n_fsdp = lax.axis_size("fsdp")
    n_ctx = lax.axis_size("ctx")
    ctx_at = lax.axis_index("ctx")
    fsdp_at = lax.axis_index("fsdp")
    groups, tok_slot, width = tokens.shape
    heads_here = H // n_fsdp
    lane_width = heads_here * HD
    span_rows = tok_slot * n_fsdp
    key_count = span_rows * n_ctx
    row_count = groups * tok_slot
    scale = HD ** (-0.5)
    query_rows = min(512, span_rows)
    key_rows = min(2048, key_count // 4)
    query_blocks = span_rows // query_rows
    key_blocks = key_count // key_rows
    key_starts = jnp.arange(key_blocks, dtype=jnp.int32) * key_rows
    qkv_full, qkv_bias, out_full, out_bias, gain_one, shift_one = (
        lax.all_gather(w_qkv, ("ctx", "fsdp"), axis=0, tiled=True),
        lax.all_gather(b_qkv, ("ctx", "fsdp"), axis=0, tiled=True),
        lax.all_gather(w_out, ("ctx", "fsdp"), axis=0, tiled=True),
        lax.all_gather(b_out, ("ctx", "fsdp"), axis=0, tiled=True),
        lax.all_gather(ln1_gain, ("ctx", "fsdp"), axis=0, tiled=True),
        lax.all_gather(ln1_bias, ("ctx", "fsdp"), axis=0, tiled=True),
    )
    token_pos = (ctx_at * n_fsdp + fsdp_at) * tok_slot + jnp.arange(tok_slot, dtype=jnp.int32)
    live_rows = (token_pos[None, :] < lengths[:, None]).reshape(row_count, 1)
    flat_tokens = tokens.reshape(row_count, width)
    joined = jnp.dot(flat_tokens, qkv_full, preferred_element_type=jnp.float32) + qkv_bias.astype(
        jnp.float32
    )
    cosine, sine_part = rope_tables(token_pos.astype(jnp.float32), HD)
    split_heads = joined.reshape(groups, tok_slot, 3, H, HD)
    rotated_query = rotate(split_heads[:, :, 0], cosine, sine_part)
    rotated_key = rotate(split_heads[:, :, 1], cosine, sine_part)
    packed = (
        jnp.stack([rotated_query, rotated_key, split_heads[:, :, 2]], axis=2)
        .astype(jnp.bfloat16)
        .reshape(groups, tok_slot, 3, n_fsdp, lane_width)
    )
    by_heads = lax.all_to_all(packed, "fsdp", split_axis=3, concat_axis=1, tiled=True)
    queries = by_heads[:, :, 0, 0]
    local_keys = by_heads[:, :, 1, 0]
    local_values = by_heads[:, :, 2, 0]
    all_keys, all_values = (
        lax.all_gather(local_keys, "ctx", axis=1, tiled=True),
        lax.all_gather(local_values, "ctx", axis=1, tiled=True),
    )

    def attend_slot(slot_item):
        slot_queries, slot_keys, slot_values, length = slot_item
        query_split = slot_queries.reshape(query_blocks, query_rows, heads_here, HD)
        key_split = slot_keys.reshape(key_blocks, key_rows, heads_here, HD)
        value_split = slot_values.reshape(key_blocks, key_rows, heads_here, HD)

        def per_query(query_block):

            def row_stats(state_pair, key_item):
                highest, running_sum = state_pair
                scores = block_scores(query_block, key_item[0], key_item[1], length, scale)
                new_high = jnp.maximum(highest, jnp.max(scores, axis=-1))
                running_sum = running_sum * jnp.exp(highest - new_high) + jnp.sum(
                    jnp.exp(scores - new_high[..., None]), axis=-1
                )
                return ((new_high, running_sum), None)

            start_state = (
                jnp.full((heads_here, query_rows), NEG_FILL, jnp.float32),
                jnp.zeros((heads_here, query_rows), jnp.float32),
            )
            highest, running_sum = lax.scan(row_stats, start_state, (key_split, key_starts))[0]
            log_norm = highest + jnp.log(running_sum)

            def weigh_values(accumulated, key_item):
                scores = block_scores(query_block, key_item[0], key_item[2], length, scale)
                weights = jnp.exp(scores - log_norm[..., None]).astype(jnp.bfloat16)
                return (
                    accumulated
                    + jnp.einsum(
                        "hqk,khd->qhd", weights, key_item[1], preferred_element_type=jnp.float32
                    ),
                    None,
                )

            mixture = lax.scan(
                weigh_values,
                jnp.zeros((query_rows, heads_here, HD), jnp.float32),
                (key_split, value_split, key_starts),
            )[0]
            return (mixture, log_norm)

        mixture, log_norm = lax.map(per_query, query_split)
        return (mixture.reshape(span_rows, lane_width), log_norm)

    mixture, log_norms = lax.map(attend_slot, (queries, all_keys, all_values, lengths))
    merged = lax.all_to_all(
        mixture.astype(jnp.bfloat16).reshape(groups, span_rows, 1, lane_width),
        "fsdp",
        split_axis=1,
        concat_axis=2,
        tiled=True,
    ).reshape(row_count, width)
    attended = jnp.dot(merged, out_full, preferred_element_type=jnp.float32) + out_bias.astype(
        jnp.float32
    )
    hidden_one, pull_one = jax.vjp(
        layer_norm,
        flat_tokens.astype(jnp.float32) + attended,
        gain_one.astype(jnp.float32),
        shift_one.astype(jnp.float32),
    )
    hidden_low = hidden_one.astype(jnp.bfloat16)
    up_full, up_bias, down_full, down_bias, gain_two, shift_two, proj_full = (
        lax.all_gather(w_up, ("ctx", "fsdp"), axis=0, tiled=True),
        lax.all_gather(b_up, ("ctx", "fsdp"), axis=0, tiled=True),
        lax.all_gather(w_down, ("ctx", "fsdp"), axis=0, tiled=True),
        lax.all_gather(b_down, ("ctx", "fsdp"), axis=0, tiled=True),
        lax.all_gather(ln2_gain, ("ctx", "fsdp"), axis=0, tiled=True),
        lax.all_gather(ln2_bias, ("ctx", "fsdp"), axis=0, tiled=True),
        lax.all_gather(w_proj, ("ctx", "fsdp"), axis=0, tiled=True),
    )
    upward = jnp.dot(hidden_low, up_full, preferred_element_type=jnp.float32) + up_bias.astype(
        jnp.float32
    )
    active_full, pull_gelu = jax.vjp(partial(jax.nn.gelu, approximate=False), upward)
    active = active_full.astype(jnp.bfloat16)
    downward = jnp.dot(active, down_full, preferred_element_type=jnp.float32) + down_bias.astype(
        jnp.float32
    )
    out_full_rows, pull_two = jax.vjp(
        layer_norm,
        hidden_one + downward,
        gain_two.astype(jnp.float32),
        shift_two.astype(jnp.float32),
    )
    out_low = out_full_rows.astype(jnp.bfloat16)
    projected = jnp.dot(out_low, proj_full, preferred_element_type=jnp.float32)
    back_qkv, back_qkv_bias, back_out, back_out_bias, back_gain_one, back_shift_one = (
        lax.all_gather(w_qkv, ("ctx", "fsdp"), axis=0, tiled=True),
        lax.all_gather(b_qkv, ("ctx", "fsdp"), axis=0, tiled=True),
        lax.all_gather(w_out, ("ctx", "fsdp"), axis=0, tiled=True),
        lax.all_gather(b_out, ("ctx", "fsdp"), axis=0, tiled=True),
        lax.all_gather(ln1_gain, ("ctx", "fsdp"), axis=0, tiled=True),
        lax.all_gather(ln1_bias, ("ctx", "fsdp"), axis=0, tiled=True),
    )
    back_up, back_up_bias, back_down, back_down_bias, back_gain_two, back_shift_two, back_proj = (
        lax.all_gather(w_up, ("ctx", "fsdp"), axis=0, tiled=True),
        lax.all_gather(b_up, ("ctx", "fsdp"), axis=0, tiled=True),
        lax.all_gather(w_down, ("ctx", "fsdp"), axis=0, tiled=True),
        lax.all_gather(b_down, ("ctx", "fsdp"), axis=0, tiled=True),
        lax.all_gather(ln2_gain, ("ctx", "fsdp"), axis=0, tiled=True),
        lax.all_gather(ln2_bias, ("ctx", "fsdp"), axis=0, tiled=True),
        lax.all_gather(w_proj, ("ctx", "fsdp"), axis=0, tiled=True),
    )
    grad_out = jnp.where(live_rows, cot_out.reshape(row_count, width).astype(jnp.float32), 0.0)
    grad_emb = jnp.where(live_rows, cot_emb.reshape(row_count, -1), 0)
    d_proj = jnp.einsum("rd,rp->dp", out_low, grad_emb, preferred_element_type=jnp.float32)
    grad_full = grad_out + jnp.einsum(
        "rp,dp->rd", grad_emb, back_proj, preferred_element_type=jnp.float32
    )
    grad_two, d_gain_two, d_shift_two = pull_two(grad_full)
    grad_down = grad_two.astype(jnp.bfloat16)
    d_down = jnp.einsum("rf,rd->fd", active, grad_down, preferred_element_type=jnp.float32)
    d_down_bias = jnp.sum(grad_down.astype(jnp.float32), axis=0)
    grad_act = jnp.einsum("rd,fd->rf", grad_down, back_down, preferred_element_type=jnp.float32)
    grad_up = pull_gelu(grad_act)[0].astype(jnp.bfloat16)
    d_up = jnp.einsum("rd,rf->df", hidden_low, grad_up, preferred_element_type=jnp.float32)
    d_up_bias = jnp.sum(grad_up.astype(jnp.float32), axis=0)
    grad_hidden = grad_two + jnp.einsum(
        "rf,df->rd", grad_up, back_up, preferred_element_type=jnp.float32
    )
    grad_one, d_gain_one, d_shift_one = pull_one(grad_hidden)
    grad_att = grad_one.astype(jnp.bfloat16)
    d_out = jnp.einsum("rd,re->de", merged, grad_att, preferred_element_type=jnp.float32)
    d_out_bias = jnp.sum(grad_att.astype(jnp.float32), axis=0)
    grad_merged = jnp.einsum(
        "re,de->rd", grad_att, back_out, preferred_element_type=jnp.float32
    ).astype(jnp.bfloat16)
    grad_heads = lax.all_to_all(
        grad_merged.reshape(groups, tok_slot, n_fsdp, lane_width),
        "fsdp",
        split_axis=2,
        concat_axis=1,
        tiled=True,
    ).reshape(groups, span_rows, lane_width)

    def attend_back(slot_item):
        slot_queries, slot_keys, slot_values, grad_mix, log_norm, length = slot_item
        query_split = slot_queries.reshape(query_blocks, query_rows, heads_here, HD)
        key_split = slot_keys.reshape(key_blocks, key_rows, heads_here, HD)
        value_split = slot_values.reshape(key_blocks, key_rows, heads_here, HD)
        grad_split = grad_mix.reshape(query_blocks, query_rows, heads_here, HD)

        def value_pass(value_total, query_item):
            query_block, grad_block, norm_block = query_item

            def value_per_key(row_dot, key_item):
                key_block, value_block, key_start = key_item
                scores = block_scores(query_block, key_block, key_start, length, scale)
                probability = jnp.exp(scores - norm_block[..., None])
                grad_probs = jnp.einsum(
                    "qhd,khd->hqk", grad_block, value_block, preferred_element_type=jnp.float32
                )
                value_part = jnp.einsum(
                    "hqk,qhd->khd",
                    probability.astype(jnp.bfloat16),
                    grad_block,
                    preferred_element_type=jnp.float32,
                )
                return (row_dot + jnp.sum(probability * grad_probs, axis=-1), value_part)

            row_dot, value_parts = lax.scan(
                value_per_key,
                jnp.zeros((heads_here, query_rows), jnp.float32),
                (key_split, value_split, key_starts),
            )
            return (value_total + value_parts.reshape(key_count, heads_here, HD), row_dot)

        value_grad, row_dots = lax.scan(
            value_pass,
            jnp.zeros((key_count, heads_here, HD), jnp.float32),
            (query_split, grad_split, log_norm),
        )

        def key_pass(key_total, query_item):
            query_block, grad_block, norm_block, dot_block = query_item

            def key_per_key(query_accum, key_item):
                key_block, value_block, key_start = key_item
                scores = block_scores(query_block, key_block, key_start, length, scale)
                probability = jnp.exp(scores - norm_block[..., None])
                grad_probs = jnp.einsum(
                    "qhd,khd->hqk", grad_block, value_block, preferred_element_type=jnp.float32
                )
                grad_scores = (probability * (grad_probs - dot_block[..., None])).astype(
                    jnp.bfloat16
                )
                query_accum = query_accum + jnp.einsum(
                    "hqk,khd->qhd", grad_scores, key_block, preferred_element_type=jnp.float32
                )
                key_part = jnp.einsum(
                    "hqk,qhd->khd", grad_scores, query_block, preferred_element_type=jnp.float32
                )
                return (query_accum, key_part)

            query_grad, key_parts = lax.scan(
                key_per_key,
                jnp.zeros((query_rows, heads_here, HD), jnp.float32),
                (key_split, value_split, key_starts),
            )
            return (key_total + key_parts.reshape(key_count, heads_here, HD), query_grad)

        key_grad, query_grads = lax.scan(
            key_pass,
            jnp.zeros((key_count, heads_here, HD), jnp.float32),
            (query_split, grad_split, log_norm, row_dots),
        )
        return (
            query_grads.reshape(span_rows, lane_width) * scale,
            key_grad.reshape(key_count, lane_width) * scale,
            value_grad.reshape(key_count, lane_width),
        )

    grad_queries, key_terms, value_terms = lax.map(
        attend_back, (queries, all_keys, all_values, grad_heads, log_norms, lengths)
    )
    grad_keys, grad_values = (
        lax.psum_scatter(
            key_terms.astype(jnp.bfloat16), "ctx", scatter_dimension=1, tiled=True
        ).astype(jnp.float32),
        lax.psum_scatter(
            value_terms.astype(jnp.bfloat16), "ctx", scatter_dimension=1, tiled=True
        ).astype(jnp.float32),
    )
    head_pos = (ctx_at * span_rows + jnp.arange(span_rows, dtype=jnp.int32)).astype(jnp.float32)
    head_cosine, head_sine = rope_tables(head_pos, HD)
    query_back = rotate(
        grad_queries.reshape(groups, span_rows, heads_here, HD), head_cosine, -head_sine
    )
    key_back = rotate(grad_keys.reshape(groups, span_rows, heads_here, HD), head_cosine, -head_sine)
    value_back = grad_values.reshape(groups, span_rows, heads_here, HD)
    grad_pack = (
        jnp.stack([query_back, key_back, value_back], axis=2)
        .astype(jnp.bfloat16)
        .reshape(groups, span_rows, 3, 1, lane_width)
    )
    grad_joined = lax.all_to_all(
        grad_pack, "fsdp", split_axis=1, concat_axis=3, tiled=True
    ).reshape(row_count, 3 * width)
    d_qkv = jnp.einsum("rd,re->de", flat_tokens, grad_joined, preferred_element_type=jnp.float32)
    d_qkv_bias = jnp.sum(grad_joined.astype(jnp.float32), axis=0)
    input_grad = (
        jnp.einsum("re,de->rd", grad_joined, back_qkv, preferred_element_type=jnp.float32)
        + grad_one
    ).astype(jnp.bfloat16)
    shards = (
        lax.psum_scatter(d_qkv, ("ctx", "fsdp"), scatter_dimension=0, tiled=True),
        lax.psum_scatter(d_qkv_bias, ("ctx", "fsdp"), scatter_dimension=0, tiled=True),
        lax.psum_scatter(d_out, ("ctx", "fsdp"), scatter_dimension=0, tiled=True),
        lax.psum_scatter(d_out_bias, ("ctx", "fsdp"), scatter_dimension=0, tiled=True),
        lax.psum_scatter(d_gain_one, ("ctx", "fsdp"), scatter_dimension=0, tiled=True),
        lax.psum_scatter(d_shift_one, ("ctx", "fsdp"), scatter_dimension=0, tiled=True),
        lax.psum_scatter(d_up, ("ctx", "fsdp"), scatter_dimension=0, tiled=True),
        lax.psum_scatter(d_up_bias, ("ctx", "fsdp"), scatter_dimension=0, tiled=True),
        lax.psum_scatter(d_down, ("ctx", "fsdp"), scatter_dimension=0, tiled=True),
        lax.psum_scatter(d_down_bias, ("ctx", "fsdp"), scatter_dimension=0, tiled=True),
        lax.psum_scatter(d_gain_two, ("ctx", "fsdp"), scatter_dimension=0, tiled=True),
        lax.psum_scatter(d_shift_two, ("ctx", "fsdp"), scatter_dimension=0, tiled=True),
        lax.psum_scatter(d_proj, ("ctx", "fsdp"), scatter_dimension=0, tiled=True),
    )
    totals = (
        lax.psum(shards[0].astype(jnp.bfloat16), "slot").astype(jnp.float32),
        lax.psum(shards[1].astype(jnp.bfloat16), "slot").astype(jnp.float32),
        lax.psum(shards[2].astype(jnp.bfloat16), "slot").astype(jnp.float32),
        lax.psum(shards[3].astype(jnp.bfloat16), "slot").astype(jnp.float32),
        lax.psum(shards[4].astype(jnp.bfloat16), "slot").astype(jnp.float32),
        lax.psum(shards[5].astype(jnp.bfloat16), "slot").astype(jnp.float32),
        lax.psum(shards[6].astype(jnp.bfloat16), "slot").astype(jnp.float32),
        lax.psum(shards[7].astype(jnp.bfloat16), "slot").astype(jnp.float32),
        lax.psum(shards[8].astype(jnp.bfloat16), "slot").astype(jnp.float32),
        lax.psum(shards[9].astype(jnp.bfloat16), "slot").astype(jnp.float32),
        lax.psum(shards[10].astype(jnp.bfloat16), "slot").astype(jnp.float32),
        lax.psum(shards[11].astype(jnp.bfloat16), "slot").astype(jnp.float32),
        lax.psum(shards[12].astype(jnp.bfloat16), "slot").astype(jnp.float32),
    )
    return (
        out_low.reshape(groups, tok_slot, width),
        projected.astype(jnp.bfloat16).reshape(groups, tok_slot, -1),
        input_grad.reshape(groups, tok_slot, width),
        totals[0],
        totals[1],
        totals[2],
        totals[3],
        totals[4],
        totals[5],
        totals[6],
        totals[7],
        totals[8],
        totals[9],
        totals[10],
        totals[11],
        totals[12],
    )


def solution(mesh):
    n_slot, n_ctx, n_fsdp = (mesh.shape[a] for a in ("slot", "ctx", "fsdp"))
    rows_axes = ("ctx", "fsdp")
    step = per_device
    if n_slot == 2 and n_fsdp % 2 == 0 and n_ctx * n_fsdp == H:
        mesh = Mesh(
            mesh.devices.reshape(n_slot, n_ctx, n_fsdp // 2, 2), ("slot", "ctx", "x", "core")
        )
        rows_axes = GROUP
        step = head_device
    in_specs = (
        P("slot", rows_axes, None),
        P("slot"),
        P(rows_axes, None),
        P(rows_axes),
        P(rows_axes, None),
        P(rows_axes),
        P(rows_axes),
        P(rows_axes),
        P(rows_axes, None),
        P(rows_axes),
        P(rows_axes, None),
        P(rows_axes),
        P(rows_axes),
        P(rows_axes),
        P(rows_axes, None),
        P("slot", rows_axes, None),
        P("slot", rows_axes, None),
    )
    out_specs = (
        P("slot", rows_axes, None),
        P("slot", rows_axes, None),
        P("slot", rows_axes, None),
        P(rows_axes, None),
        P(rows_axes),
        P(rows_axes, None),
        P(rows_axes),
        P(rows_axes),
        P(rows_axes),
        P(rows_axes, None),
        P(rows_axes),
        P(rows_axes, None),
        P(rows_axes),
        P(rows_axes),
        P(rows_axes),
        P(rows_axes, None),
    )
    return jax.shard_map(
        step, mesh=mesh, in_specs=in_specs, out_specs=out_specs, check_vma=False
    )
```

```python
from functools import partial

import jax
import jax.numpy as jnp
from jax import lax
from jax.experimental import pallas as pl
from jax.experimental.pallas import tpu as pltpu
from jax.sharding import Mesh
from jax.sharding import PartitionSpec as P

H = 16
HD = 64
LN_EPS = 1e-05
NEG_FILL = -1e30
F32 = jnp.float32
BF16 = jnp.bfloat16
GROUP = ("ctx", "x", "core")
LANE = ("ctx", "x")
SWAP = [(0, 1), (1, 0)]
VMEM_LIMIT = 60 * 1024 * 1024


def mm(left, right):
    return jnp.dot(left, right, preferred_element_type=F32)


def contract(left, right, left_dim, right_dim):
    return lax.dot_general(
        left, right, (((left_dim,), (right_dim,)), ((), ())), preferred_element_type=F32
    )


def swap_core(value):
    return lax.ppermute(value, "core", SWAP)


def swap_slot(value):
    return lax.ppermute(value, "slot", SWAP)


def pick(stacked, index, axis):
    return lax.dynamic_index_in_dim(stacked, index, axis, keepdims=False)


MESH = pl.DeviceIdType.MESH


def at_device(**where):
    names = ("slot", "ctx", "x", "core")
    return tuple(where[n] if n in where else lax.axis_index(n) for n in names)


def greet(peers):
    barrier = pltpu.get_barrier_semaphore()
    for peer in peers:
        pl.semaphore_signal(barrier, inc=1, device_id=peer, device_id_type=MESH)
    pl.semaphore_wait(barrier, len(peers))


def group_peers(n_ctx, n_x):
    ctx, x, core = (lax.axis_index(n) for n in GROUP)
    peers = []
    for dz in range(n_ctx):
        for dx in range(n_x):
            for dc in range(2):
                if dz or dx or dc:
                    where = (lax.rem(ctx + dz, n_ctx), lax.rem(x + dx, n_x), lax.rem(core + dc, 2))
                    peers.append(where)
    return peers


def start_kernel(
    tok_ref, head_ref, small_ref, all_ref, heads_ref, smalls_ref,
    far_send, block_send, local_sem, head_recv, small_recv, block_recv, *, n_ctx, n_x
):
    part = tok_ref.shape[1]
    ctx, x, core = (lax.axis_index(n) for n in GROUP)
    me = (ctx * n_x + x) * 2 + core
    peers = group_peers(n_ctx, n_x)
    greet([at_device(ctx=z, x=a, core=c) for z, a, c in peers])

    def block_at(b):
        return all_ref.at[:, pl.ds(pl.multiple_of(b * part, part), part), :]

    pushes = []
    for k, (z, a, c) in enumerate(peers):
        them = (z * n_x + a) * 2 + c
        target = at_device(ctx=z, x=a, core=c)
        pushes.append(pltpu.make_async_remote_copy(
            head_ref.at[them], heads_ref.at[me], far_send.at[2 * k], head_recv.at[me],
            device_id=target, device_id_type=MESH))
        pushes.append(pltpu.make_async_remote_copy(
            small_ref, smalls_ref.at[me], far_send.at[2 * k + 1], small_recv.at[me],
            device_id=target, device_id_type=MESH))
    locals_ = [
        pltpu.make_async_copy(tok_ref, block_at(me), local_sem.at[0]),
        pltpu.make_async_copy(head_ref.at[me], heads_ref.at[me], local_sem.at[1]),
        pltpu.make_async_copy(small_ref, smalls_ref.at[me], local_sem.at[2]),
    ]

    def send(b, source, lane, target):
        return pltpu.make_async_remote_copy(
            source, block_at(b), block_send.at[lane, b], block_recv.at[b],
            device_id=target, device_id_type=MESH)

    up = at_device(ctx=lax.rem(ctx + 1, n_ctx))
    down = at_device(ctx=lax.rem(ctx + n_ctx - 1, n_ctx))
    side = at_device(x=1 - x)
    twin = at_device(core=1 - core)

    def here(b):
        return send(b, block_at(b), 0, twin)

    @pl.when(ctx + 1 < n_ctx)
    def _():
        send(me, tok_ref, 0, up).start()

    @pl.when(ctx > 0)
    def _():
        send(me, tok_ref, 1, down).start()

    send(me, tok_ref, 2, side).start()
    send(me, tok_ref, 3, twin).start()
    for copy in locals_:
        copy.start()

    for r in range(1, n_ctx):
        if r == n_ctx - 1:
            for push in pushes:
                push.start()
        low = ctx - r
        high = ctx + r

        @pl.when(low >= 0)
        def _():
            b = (low * n_x + x) * 2 + core
            here(b).wait_recv()

            @pl.when(ctx + 1 < n_ctx)
            def _():
                send(b, block_at(b), 0, up).start()

            send(b, block_at(b), 2, side).start()
            send(b, block_at(b), 3, twin).start()

        @pl.when(high < n_ctx)
        def _():
            b = (high * n_x + x) * 2 + core
            here(b).wait_recv()

            @pl.when(ctx > 0)
            def _():
                send(b, block_at(b), 1, down).start()

            send(b, block_at(b), 2, side).start()
            send(b, block_at(b), 3, twin).start()

    def from_side(z):
        b = (z * n_x + (1 - x)) * 2 + core
        here(b).wait_recv()
        send(b, block_at(b), 3, twin).start()

    from_side(ctx)
    for r in range(1, n_ctx):
        @pl.when(ctx - r >= 0)
        def _():
            from_side(ctx - r)

        @pl.when(ctx + r < n_ctx)
        def _():
            from_side(ctx + r)

    for z in range(n_ctx):
        for a in range(n_x):
            here((z * n_x + a) * 2 + 1 - core).wait_recv()
    for k, (z, a, c) in enumerate(peers):
        them = (z * n_x + a) * 2 + c
        pltpu.make_async_remote_copy(
            head_ref.at[them], heads_ref.at[them], far_send.at[2 * k], head_recv.at[them],
            device_id=twin, device_id_type=MESH).wait_recv()
        pltpu.make_async_remote_copy(
            small_ref, smalls_ref.at[them], far_send.at[2 * k + 1], small_recv.at[them],
            device_id=twin, device_id_type=MESH).wait_recv()
    for push in pushes:
        push.wait_send()
    for copy in locals_:
        copy.wait()

    for z in range(n_ctx):
        b = (z * n_x + x) * 2 + core

        @pl.when((z <= ctx) & (ctx + 1 < n_ctx))
        def _():
            send(b, block_at(b), 0, up).wait_send()

        @pl.when((z >= ctx) & (ctx > 0))
        def _():
            send(b, block_at(b), 1, down).wait_send()

        send(b, block_at(b), 2, side).wait_send()
        send(b, block_at(b), 3, twin).wait_send()
        other = (z * n_x + (1 - x)) * 2 + core
        send(other, block_at(other), 3, twin).wait_send()


def gather_start(tokens, heads, small):
    n_ctx, n_x = lax.axis_size("ctx"), lax.axis_size("x")
    n = 2 * n_ctx * n_x
    slots, part, width = tokens.shape
    vmem = pl.BlockSpec(memory_space=pltpu.VMEM)
    anywhere = pl.BlockSpec(memory_space=pl.ANY)
    dma = pltpu.SemaphoreType.DMA
    return pl.pallas_call(
        partial(start_kernel, n_ctx=n_ctx, n_x=n_x),
        in_specs=[vmem, vmem, vmem],
        out_specs=[anywhere, vmem, vmem],
        out_shape=[
            jax.ShapeDtypeStruct((slots, n * part, width), tokens.dtype),
            jax.ShapeDtypeStruct(heads.shape, heads.dtype),
            jax.ShapeDtypeStruct((n,) + small.shape, small.dtype),
        ],
        scratch_shapes=[
            dma((2 * (n - 1),)), dma((4, n)), dma((3,)), dma((n,)), dma((n,)), dma((n,))
        ],
        compiler_params=pltpu.CompilerParams(
            collective_id=1, has_side_effects=True, vmem_limit_bytes=VMEM_LIMIT
        ),
        cost_estimate=pl.CostEstimate(
            flops=0, bytes_accessed=2 * n * tokens.size, transcendentals=0
        ),
        name="gather_start",
    )(tokens, heads, small)


def finish_kernel(
    out_ref, small_ref, qkv_ref, red_ref, join_ref, weight_ref, one_ref,
    g_down, g_up, g_out, g_small, g_qkv, g_bias, g_in,
    pair_small, pair_qkv, sum_qkv, qkvs,
    pair_down, pair_out, last_up, joins, partial_in, pair_in,
    join_send, join_recv, far_send, qkv_recv, y_send, y_recv,
    *, n_ctx, n_x
):
    ctx, x, core = (lax.axis_index(n) for n in GROUP)
    slot = lax.axis_index("slot")
    chip = ctx * n_x + x
    me = 2 * chip + core
    shard, width = g_out.shape
    part = g_down.shape[0] // 2
    peers = group_peers(n_ctx, n_x)
    lane_peers = [(z, a) for z, a, c in peers[1::2]]
    across = at_device(slot=1 - slot)
    corner = at_device(slot=1 - slot, core=1 - core)
    twin = at_device(core=1 - core)
    greet([at_device(ctx=z, x=a, core=c) for z, a, c in peers] + [across, corner])

    def remote(source, target_ref, send_sem, recv_sem, target):
        return pltpu.make_async_remote_copy(
            source, target_ref, send_sem, recv_sem, device_id=target, device_id_type=MESH)

    started = []

    def launch(copy):
        copy.start()
        started.append(copy)
        return copy

    def pair_copy(i, source, target_ref, target):
        return launch(remote(source, target_ref, y_send.at[i], y_recv.at[i], target))

    qkv_copy = pair_copy(0, qkv_ref, pair_qkv, across)
    mine = pl.multiple_of(part + core * shard, shard)
    theirs = pl.multiple_of(part + (1 - core) * shard, shard)
    for k, (z, a) in enumerate(lane_peers):
        launch(remote(
            join_ref.at[z * n_x + a], joins.at[chip], join_send.at[k], join_recv.at[chip],
            at_device(ctx=z, x=a)))
    down_copy = pair_copy(4, red_ref.at[pl.ds(0, part)], pair_down, across)
    quarter_copies = [
        pair_copy(5, red_ref.at[pl.ds(theirs, shard)], last_up.at[0], twin),
        pair_copy(6, red_ref.at[pl.ds(mine, shard)], last_up.at[1], across),
        pair_copy(7, red_ref.at[pl.ds(theirs, shard)], last_up.at[2], corner),
    ]

    small_copy = pair_copy(1, small_ref, pair_small, across)
    out_copy = pair_copy(3, out_ref, pair_out, across)
    qkv_copy.wait_recv()
    sum_qkv[...] = (qkv_ref[...].astype(F32) + pair_qkv[...].astype(F32)).astype(BF16)
    for k, (z, a, c) in enumerate(peers):
        them = (z * n_x + a) * 2 + c
        launch(remote(
            sum_qkv.at[them], qkvs.at[me], far_send.at[k], qkv_recv.at[me],
            at_device(ctx=z, x=a, core=c)))
    qkvs[me] = sum_qkv[me]

    def add_head(source, rows_of, first):
        weight = jnp.concatenate(
            [weight_ref[b, source] for b in range(weight_ref.shape[0])], axis=0)
        for h in range(2):
            owner = core if h == 0 else 1 - core
            rows = rows_of(owner)
            cols = rows.shape[2] // 2
            rows = jnp.concatenate(
                [r for t in range(rows.shape[0]) for r in (rows[t, :, :cols], rows[t, :, cols:])],
                axis=0)
            term = contract(rows, weight, 1, 1)
            partial_in[h] = term if first else partial_in[h] + term

    add_head(chip, lambda owner: join_ref[chip, owner], True)

    half = pl.multiple_of(slot * part, part)
    other_half = pl.multiple_of((1 - slot) * part, part)
    g_down[pl.ds(half, part), :] = red_ref[pl.ds(0, part), :].astype(F32)
    down_copy.wait_recv()
    g_down[pl.ds(other_half, part), :] = pair_down[...].astype(F32)

    def place_quarter(rows, quarter_core, quarter_slot):
        for k in range(n_ctx * n_x):
            at = pl.multiple_of(((2 * k + quarter_core) * 2 + quarter_slot) * part, part)
            g_up[:, pl.ds(at, part)] = rows[:, k * part : (k + 1) * part].astype(F32)

    place_quarter(red_ref[pl.ds(mine, shard), :], core, slot)
    quarter_copies[0].wait_recv()
    place_quarter(last_up[0], 1 - core, slot)
    quarter_copies[1].wait_recv()
    place_quarter(last_up[1], core, 1 - slot)
    quarter_copies[2].wait_recv()
    place_quarter(last_up[2], 1 - core, 1 - slot)

    @pl.loop(1, n_ctx * n_x)
    def _(o):
        source = lax.rem(ctx + o // n_x, n_ctx) * n_x + lax.rem(x + o % n_x, n_x)
        remote(
            join_ref.at[source], joins.at[source], join_send.at[0], join_recv.at[source], twin
        ).wait_recv()
        add_head(source, lambda owner: joins[source, owner], False)

    in_copy = pair_copy(2, partial_in.at[1], pair_in, twin)

    small_copy.wait_recv()
    g_small[...] = small_ref[...].astype(F32) + pair_small[...].astype(F32)
    in_copy.wait_recv()
    g_in[...] = (partial_in[0] + pair_in[...] + one_ref[...]).astype(BF16)
    for z, a, c in peers:
        them = (z * n_x + a) * 2 + c
        remote(
            sum_qkv.at[them], qkvs.at[them], far_send.at[0], qkv_recv.at[them], twin
        ).wait_recv()
    for k in range(n_ctx * n_x):
        heads = [qkvs[2 * k + c, :shard, :].astype(F32) for c in range(2)]
        for t in range(3):
            at = t * width + 2 * HD * k
            g_qkv[:, at : at + 2 * HD] = jnp.concatenate(
                [h[:, t * HD : (t + 1) * HD] for h in heads], axis=1)
        for c in range(2):
            g_bias[2 * k + c : 2 * k + c + 1, :] = qkvs[2 * k + c, shard : shard + 1, :].astype(F32)
    out_copy.wait_recv()
    g_out[...] = out_ref[...].astype(F32) + pair_out[...].astype(F32)
    for copy in started:
        copy.wait_send()


def finish_grads(out, small, qkv, reduced, joined, weight, grad_one):
    n_ctx, n_x = lax.axis_size("ctx"), lax.axis_size("x")
    n = 2 * n_ctx * n_x
    shard, width = out.shape
    part = reduced.shape[0] // 2
    vmem = pl.BlockSpec(memory_space=pltpu.VMEM)
    dma = pltpu.SemaphoreType.DMA

    def low(*shape):
        return pltpu.VMEM(shape, BF16)

    def wide(*shape):
        return jax.ShapeDtypeStruct(shape, F32)

    return pl.pallas_call(
        partial(finish_kernel, n_ctx=n_ctx, n_x=n_x),
        in_specs=[vmem] * 7,
        out_specs=[vmem] * 7,
        out_shape=[
            wide(2 * part, width),
            wide(shard, 4 * width),
            wide(shard, width),
            wide(*small.shape),
            wide(shard, 3 * width),
            wide(n, qkv.shape[2]),
            jax.ShapeDtypeStruct(grad_one.shape, BF16),
        ],
        scratch_shapes=[
            low(*small.shape),
            low(*qkv.shape),
            low(*qkv.shape),
            low(*qkv.shape),
            low(part, width),
            low(*out.shape),
            low(3, shard, width),
            low(*joined.shape),
            pltpu.VMEM((2,) + grad_one.shape, F32),
            pltpu.VMEM(grad_one.shape, F32),
            dma((n_ctx * n_x - 1,)),
            dma((n_ctx * n_x,)),
            dma((n - 1,)),
            dma((n,)),
            dma((8,)),
            dma((8,)),
        ],
        compiler_params=pltpu.CompilerParams(
            collective_id=2, has_side_effects=True, vmem_limit_bytes=VMEM_LIMIT
        ),
        cost_estimate=pl.CostEstimate(flops=0, bytes_accessed=16 * joined.size, transcendentals=0),
        name="finish_grads",
    )(out, small, qkv, reduced, joined, weight, grad_one)


def lane_gather(mine_ref, all_ref, send_sem, recv_sem, local_sem, n_ctx, n_x):
    ctx, x = lax.axis_index("ctx"), lax.axis_index("x")
    chip = ctx * n_x + x
    routes = (
        at_device(ctx=lax.rem(ctx + 1, n_ctx)),
        at_device(ctx=lax.rem(ctx + n_ctx - 1, n_ctx)),
        at_device(x=1 - x),
    )

    def send(k, lane, own=False):
        return pltpu.make_async_remote_copy(
            mine_ref if own else all_ref.at[k], all_ref.at[k], send_sem.at[lane, k], recv_sem.at[k],
            device_id=routes[lane], device_id_type=MESH)

    local = pltpu.make_async_copy(mine_ref, all_ref.at[chip], local_sem)

    def begin():
        @pl.when(ctx + 1 < n_ctx)
        def _():
            send(chip, 0, own=True).start()

        @pl.when(ctx > 0)
        def _():
            send(chip, 1, own=True).start()

        send(chip, 2, own=True).start()
        local.start()

    def relay(r):
        for sign, lane, more in ((-1, 0, ctx + 1 < n_ctx), (1, 1, ctx > 0)):
            z = ctx + sign * r

            @pl.when((z >= 0) & (z < n_ctx))
            def _():
                k = z * n_x + x
                send(k, 0).wait_recv()

                @pl.when(more)
                def _():
                    send(k, lane).start()

                send(k, 2).start()

    def end():
        for z in range(n_ctx):
            k = z * n_x + x
            send(z * n_x + 1 - x, 0).wait_recv()

            @pl.when((z <= ctx) & (ctx + 1 < n_ctx))
            def _():
                send(k, 0).wait_send()

            @pl.when((z >= ctx) & (ctx > 0))
            def _():
                send(k, 1).wait_send()

            send(k, 2).wait_send()
        local.wait()

    return begin, relay, end


QB = 512
KB = 512


def turn(pair, cosine, sine):
    half = HD // 2
    lanes = lax.broadcasted_iota(jnp.int32, (1, 2 * HD), 1)
    low = lax.rem(lanes, HD) < half
    swapped = jnp.where(low, pltpu.roll(pair, 2 * HD - half, 1), pltpu.roll(pair, half, 1))
    return pair * cosine + swapped * jnp.where(low, -sine, sine)


def heads_kernel(
    len_ref, tok_ref, w_ref, b_ref, cos_ref, sin_ref, wa_ref, wu_ref, wd_ref,
    q_ref, k_ref, v_ref, mix_ref, send_ref, norm_ref, fa_ref, fu_ref, fd_ref,
    a_send, a_recv, u_send, u_recv, d_send, d_recv, local_sem, *, n_ctx, n_x, part
):
    core = lax.axis_index("core")
    ctx, x = lax.axis_index("ctx"), lax.axis_index("x")
    greet([
        at_device(x=1 - x),
        at_device(ctx=lax.rem(ctx + 1, n_ctx)),
        at_device(ctx=lax.rem(ctx + n_ctx - 1, n_ctx)),
    ])
    flows = [
        lane_gather(wa_ref, fa_ref, a_send, a_recv, local_sem.at[0], n_ctx, n_x),
        lane_gather(wu_ref, fu_ref, u_send, u_recv, local_sem.at[1], n_ctx, n_x),
        lane_gather(wd_ref, fd_ref, d_send, d_recv, local_sem.at[2], n_ctx, n_x),
    ]
    for begin, _, _ in flows:
        begin()
    slots, seq, _ = q_ref.shape

    def relay(r):
        if r < n_ctx:
            for _, hop, _ in flows:
                hop(r)

    blocks = seq // QB

    def project():
        @pl.loop(0, slots * blocks)
        def _(n):
            s, i = n // blocks, lax.rem(n, blocks)
            rows = pl.ds(pl.multiple_of(i * QB, QB), QB)
            tokens = tok_ref[pl.ds(pl.multiple_of(n * QB, QB), QB), :]
            joined = mm(tokens, w_ref[...]) + b_ref[...]
            turned = turn(joined[:, : 2 * HD], cos_ref[rows, :], sin_ref[rows, :])
            q_ref[s, rows, :] = (turned[:, :HD].astype(BF16) * HD ** (-0.5)).astype(BF16)
            k_ref[s, rows, :] = turned[:, HD:].astype(BF16)
            v_ref[s, rows, :] = joined[:, 2 * HD :].astype(BF16)

    def attend():
        @pl.loop(0, slots * blocks)
        def _(n):
            s, i = n // blocks, lax.rem(n, blocks)
            length = len_ref[s]
            rows = pl.ds(pl.multiple_of(i * QB, QB), QB)
            queries = q_ref[s, rows, :]

            @pl.when(n == blocks)
            def _():
                relay(2)

            def step(j, state):
                highest, total, mix = state
                start = pl.multiple_of(j * KB, KB)
                scores = contract(queries, k_ref[s, pl.ds(start, KB), :], 1, 1)
                ids = start + lax.broadcasted_iota(jnp.int32, (1, KB), 1)
                scores = jnp.where(ids < length, scores, NEG_FILL)
                higher = jnp.maximum(highest, jnp.max(scores, axis=1, keepdims=True))
                fade = jnp.exp(highest - higher)
                weights = jnp.exp(scores - higher)
                total = total * fade + jnp.sum(weights, axis=1, keepdims=True)
                mix = mix * fade + mm(weights.astype(BF16), v_ref[s, pl.ds(start, KB), :])
                return higher, total, mix

            highest, total, mix = lax.fori_loop(
                0,
                seq // KB,
                step,
                (
                    jnp.full((QB, 1), NEG_FILL, F32),
                    jnp.zeros((QB, 1), F32),
                    jnp.zeros((QB, HD), F32),
                ),
            )
            mix = mix / total
            mix_ref[s, rows, :] = mix
            log_norm = jnp.broadcast_to(highest + jnp.log(total), (QB, 128))
            norm_ref[s, :, rows] = jnp.transpose(log_norm)[0:1, :]
            low = mix.astype(BF16)
            chips = QB // (2 * part)
            for chip in range(chips):
                for half in range(2):
                    at = (2 * chip + half) * part
                    send_ref[i * chips + chip, half ^ core, s] = low[at : at + part]

    project()
    relay(1)
    attend()
    for r in range(3, n_ctx):
        relay(r)
    for _, _, end in flows:
        end()


def heads(lengths, tokens, weight, bias, cosine, sine, part, *shards):
    n_ctx, n_x = lax.axis_size("ctx"), lax.axis_size("x")
    chips = n_ctx * n_x
    slots, seq = lengths.shape[0], cosine.shape[0]
    vmem = pl.BlockSpec(memory_space=pltpu.VMEM)
    anywhere = pl.BlockSpec(memory_space=pl.ANY)
    dma = pltpu.SemaphoreType.DMA
    head = jax.ShapeDtypeStruct((slots, seq, HD), BF16)
    return pl.pallas_call(
        partial(heads_kernel, n_ctx=n_ctx, n_x=n_x, part=part),
        in_specs=[pl.BlockSpec(memory_space=pltpu.SMEM)] + [vmem] * 8,
        out_specs=[vmem] * 6 + [anywhere] * 3,
        out_shape=[
            head,
            head,
            head,
            jax.ShapeDtypeStruct((slots, seq, HD), F32),
            jax.ShapeDtypeStruct((chips, 2, slots, part, HD), BF16),
            jax.ShapeDtypeStruct((slots, 1, seq), F32),
        ]
        + [jax.ShapeDtypeStruct((chips,) + w.shape, w.dtype) for w in shards],
        scratch_shapes=[dma((3, chips)), dma((chips,))] * 3 + [dma((3,))],
        compiler_params=pltpu.CompilerParams(
            collective_id=5, has_side_effects=True, vmem_limit_bytes=VMEM_LIMIT
        ),
        cost_estimate=pl.CostEstimate(
            flops=16 * slots * seq * seq * HD,
            bytes_accessed=2 * tokens.size,
            transcendentals=slots * seq * seq,
        ),
        name="heads",
    )(lengths, tokens, weight, bias, cosine, sine, *shards)


def grads_kernel(
    len_ref, q_ref, k_ref, v_ref, g_ref, norm_ref, dot_ref, tok_ref, cos_ref, sin_ref,
    down_ref, up_ref, out_ref, small_ref,
    join_ref, grad_ref, red_ref, sum_ref, small_sum,
    dqt, key_grads, value_grads, total, bias, x_down, x_up, x_out, s_down, s_up, s_out,
    z_down, z_up, z_out, top_down, top_up, top_out, own_down, own_up, own_out, smalls,
    x_send, x_recv, z_send, z_recv, top_recv, small_send, small_recv, *, n_ctx, n_x, part
):
    ctx, x, core = (lax.axis_index(n) for n in GROUP)
    me = (ctx * n_x + x) * 2 + core
    peers = group_peers(n_ctx, n_x)
    greet([at_device(ctx=z, x=a, core=c) for z, a, c in peers])
    side = at_device(x=1 - x)
    arrays = (
        (down_ref, x_down, s_down, z_down, top_down, own_down),
        (up_ref, x_up, s_up, z_up, top_up, own_up),
        (out_ref, x_out, s_out, z_out, top_out, own_out),
    )

    def remote(source, target_ref, send_sem, recv_sem, target):
        return pltpu.make_async_remote_copy(
            source, target_ref, send_sem, recv_sem, device_id=target, device_id_type=MESH)

    orders = [
        sorted(range(n_ctx), key=lambda p, z=z: (p == z, -abs(p - z), -p)) for z in range(n_ctx)
    ]
    places = [
        sum(jnp.where(ctx == z, orders[z][j], 0) for z in range(n_ctx)) for j in range(n_ctx)
    ]
    above = at_device(ctx=lax.rem(ctx + 1, n_ctx))
    below = at_device(ctx=lax.rem(ctx + n_ctx - 1, n_ctx))
    first = [
        [
            remote(
                ref.at[places[j] * n_x + 1 - x], x_in.at[j], x_send.at[i, j], x_recv.at[i, j], side)
            for i, (ref, x_in, _, _, _, _) in enumerate(arrays)
        ]
        for j in range(n_ctx)
    ]

    def hop(j, i, target, last=False):
        _, _, s_low, z_in, top, _ = arrays[i]
        p = places[j]
        return remote(
            s_low.at[min(j, n_ctx - 2)], top if last else z_in.at[p], z_send.at[i, min(j, n_ctx - 2)],
            top_recv.at[i] if last else z_recv.at[i, p], target)

    pushes = []
    for k, (z, a, c) in enumerate(peers):
        them = (z * n_x + a) * 2 + c
        pushes.append(remote(
            small_ref.at[them], smalls.at[me], small_send.at[k], small_recv.at[me],
            at_device(ctx=z, x=a, core=c)))
    for copies in first:
        for copy in copies:
            copy.start()
    for copy in pushes:
        copy.start()
    smalls[me] = small_ref[me]

    def stage(j):
        p = places[j]
        going_up = p > ctx
        for i, (ref, x_in, s_low, z_in, _, own) in enumerate(arrays):
            first[j][i].wait_recv()
            own[...] = ref[p * n_x + x].astype(F32) + x_in[j].astype(F32)
            if j == n_ctx - 1:
                continue

            @pl.when((going_up & (ctx > 0)) | ((p < ctx) & (ctx < n_ctx - 1)))
            def _():
                hop(j, i, above).wait_recv()
                own[...] += z_in[p].astype(F32)

            s_low[j] = own[...].astype(BF16)

            @pl.when(going_up)
            def _():
                hop(j, i, above).start()

            @pl.when(p < ctx - 1)
            def _():
                hop(j, i, below).start()

            @pl.when(p == ctx - 1)
            def _():
                hop(j, i, below, last=True).start()

    slots, seq, _ = q_ref.shape
    total[...] = jnp.zeros_like(total)
    bias[...] = jnp.zeros_like(bias)

    def attention(s, between):
        length = len_ref[s]
        dqt[...] = jnp.zeros_like(dqt)

        @pl.loop(0, seq // KB)
        def _(j):
            start = pl.multiple_of(j * KB, KB)
            key_block = k_ref[s, pl.ds(start, KB), :]
            value_block = v_ref[s, pl.ds(start, KB), :]
            turned = jnp.transpose(key_block.astype(F32)).astype(BF16)
            ids = start + lax.broadcasted_iota(jnp.int32, (KB, 1), 0)
            shift = jnp.where(ids < length, 0.0, NEG_FILL)
            for at_step, number in between:
                @pl.when(j == at_step)
                def _():
                    stage(number)

            def step(i, state):
                key_grad, value_grad = state
                at = pl.multiple_of(i * QB, QB)
                queries = q_ref[s, pl.ds(at, QB), :]
                grads = g_ref[s, pl.ds(at, QB), :]
                scores = contract(key_block, queries, 1, 1) + shift
                probs = jnp.exp(scores - norm_ref[s, :, pl.ds(at, QB)])
                grad_probs = contract(value_block, grads, 1, 1)
                grad_scores = (probs * (grad_probs - dot_ref[s, :, pl.ds(at, QB)])).astype(BF16)
                value_grad = value_grad + mm(probs.astype(BF16), grads)
                key_grad = key_grad + mm(grad_scores, queries)
                dqt[:, pl.ds(at, QB)] += mm(turned, grad_scores)
                return key_grad, value_grad

            zero = jnp.zeros((KB, HD), F32)
            key_grad, value_grad = lax.fori_loop(0, seq // QB, step, (zero, zero))
            key_grads[pl.ds(start, KB), :] = key_grad
            value_grads[pl.ds(start, KB), :] = value_grad

    def join(s):
        @pl.loop(0, seq // QB)
        def _(i):
            at = pl.multiple_of(i * QB, QB)
            rows = pl.ds(at, QB)
            query_grad = jnp.transpose(dqt[:, rows]) * HD ** (-0.5)
            pair = jnp.concatenate([query_grad, key_grads[rows, :]], axis=1)
            turned = turn(pair, cos_ref[rows, :], -sin_ref[rows, :])
            joined = jnp.concatenate([turned, value_grads[rows, :]], axis=1).astype(BF16)
            chips = QB // (2 * part)
            for chip in range(chips):
                for owner in range(2):
                    near = (2 * chip + owner) * part
                    upper = joined[near : near + part // 2]
                    lower = joined[near + part // 2 : near + part]
                    join_ref[i * chips + chip, owner, s] = jnp.concatenate([upper, lower], axis=1)
            tokens = tok_ref[pl.ds(pl.multiple_of(s * seq + at, QB), QB), :]
            total[...] += contract(joined, tokens, 0, 0)
            bias[...] += jnp.sum(joined.astype(F32), axis=0, keepdims=True)

    for s in range(slots):
        attention(s, [(1, 1)] if s == 1 else [])
        stage(0 if s == 0 else 2)
        join(s)
    turned_total = jnp.transpose(total[...])
    shard = turned_total.shape[0] // grad_ref.shape[0]
    extra = jnp.broadcast_to(bias[...], (grad_ref.shape[1] - shard, bias.shape[1]))
    for d in range(grad_ref.shape[0]):
        grad_ref[d, :shard] = turned_total[d * shard : (d + 1) * shard].astype(BF16)
        grad_ref[d, shard:] = extra.astype(BF16)
    for j in range(slots + 1, n_ctx):
        stage(j)
    for z, a, c in peers:
        them = (z * n_x + a) * 2 + c
        remote(
            small_ref.at[them], smalls.at[them], small_send.at[0], small_recv.at[them], side
        ).wait_recv()
    small_sum[...] = jnp.sum(smalls[...].astype(F32), axis=0).astype(BF16)
    for i, (_, _, _, z_in, top, own) in enumerate(arrays):
        @pl.when(ctx > 0)
        def _():
            hop(n_ctx - 1, i, above).wait_recv()
            own[...] += z_in[ctx].astype(F32)

        @pl.when(ctx < n_ctx - 1)
        def _():
            hop(0, i, below, last=True).wait_recv()
            own[...] += top[...].astype(F32)

    rows = own_down.shape[0]
    red_ref[:rows] = own_down[...].astype(BF16)
    red_ref[rows:] = own_up[...].astype(BF16)
    sum_ref[...] = own_out[...].astype(BF16)
    for copies in first + [pushes]:
        for copy in copies:
            copy.wait_send()
    for j in range(n_ctx - 1):
        for i in range(len(arrays)):
            hop(j, i, above).wait_send()


def grads(lengths, queries, keys, values, grad_heads, norms, dots, tokens, cosine, sine,
          down, up, out, small, part):
    n_ctx, n_x = lax.axis_size("ctx"), lax.axis_size("x")
    n = 2 * n_ctx * n_x
    slots, seq, _ = queries.shape
    width = tokens.shape[1]
    shard = width // n
    cols = 3 * HD
    vmem = pl.BlockSpec(memory_space=pltpu.VMEM)
    dma = pltpu.SemaphoreType.DMA
    parts = (down, up, out)

    def low(*dims):
        return jax.ShapeDtypeStruct(dims, BF16)

    return pl.pallas_call(
        partial(grads_kernel, n_ctx=n_ctx, n_x=n_x, part=part),
        in_specs=[pl.BlockSpec(memory_space=pltpu.SMEM)] + [vmem] * 13,
        out_specs=[vmem] * 5,
        out_shape=[
            low(seq // (2 * part), 2, slots, part // 2, 2 * cols),
            low(n, shard + 16, cols),
            low(down.shape[1] + up.shape[1], width),
            low(*out.shape[1:]),
            low(*small.shape[1:]),
        ],
        scratch_shapes=[
            pltpu.VMEM((HD, seq), F32),
            pltpu.VMEM((seq, HD), F32),
            pltpu.VMEM((seq, HD), F32),
            pltpu.VMEM((cols, width), F32),
            pltpu.VMEM((1, cols), F32),
        ]
        + [pltpu.VMEM((n_ctx,) + t.shape[1:], BF16) for t in parts]
        + [pltpu.VMEM((n_ctx - 1,) + t.shape[1:], BF16) for t in parts]
        + [pltpu.VMEM((n_ctx,) + t.shape[1:], BF16) for t in parts]
        + [pltpu.VMEM(t.shape[1:], BF16) for t in parts]
        + [pltpu.VMEM(t.shape[1:], F32) for t in parts]
        + [
            pltpu.VMEM(small.shape, BF16),
            dma((3, n_ctx)),
            dma((3, n_ctx)),
            dma((3, n_ctx - 1)),
            dma((3, n_ctx)),
            dma((3,)),
            dma((n - 1,)),
            dma((n,)),
        ],
        compiler_params=pltpu.CompilerParams(
            collective_id=6, has_side_effects=True, vmem_limit_bytes=VMEM_LIMIT
        ),
        cost_estimate=pl.CostEstimate(
            flops=40 * slots * seq * seq * HD,
            bytes_accessed=4 * tokens.size,
            transcendentals=slots * seq * seq,
        ),
        name="grads",
    )(lengths, queries, keys, values, grad_heads, norms, dots, tokens, cosine, sine,
      down, up, out, small)


def norm_forward(values, gain, shift):
    center = values - jnp.mean(values, axis=-1, keepdims=True)
    spread = jnp.mean(center * center, axis=-1, keepdims=True)
    root = lax.rsqrt(spread + LN_EPS)
    unit = center * root
    return unit * gain + shift, unit, root


def norm_backward(grad, unit, root, gain):
    scaled = grad * gain
    inner = scaled - jnp.mean(scaled, axis=-1, keepdims=True)
    inner = inner - unit * jnp.mean(scaled * unit, axis=-1, keepdims=True)
    return root * inner, jnp.sum(grad * unit, axis=0), jnp.sum(grad, axis=0)


def gelu_pair(values):
    half = 0.5 + 0.5 * lax.erf(values * 0.7071067811865476)
    bell = jnp.exp(-0.5 * values * values) * 0.3989422804014327
    return values * half, half + values * bell


def rope_rows(positions):
    halfway = HD // 2
    ladder = jnp.arange(halfway, dtype=F32) * (2.0 / HD)
    frequency = jnp.power(jnp.float32(10000.0), -ladder)
    angles = positions[:, None] * frequency[None, :]
    return jnp.cos(angles), jnp.sin(angles)


def layer_kernel(
    merged_ref, tok_ref, wo_ref, up_ref, down_ref, vec_ref, full_ref, lane_ref,
    out_ref, one_ref, gm_ref, att_ref, vecs_ref, act_out, hid_out, gdn_out, gup_out, lanes_out,
    first, first_in, hid, act, slope, gdn, gup, hidden, unit_one, two,
    roots, near, near_in, far, far_in, low_out, low_in, send_sem, recv_sem, out_sem,
    lane_send, lane_recv, *, n_ctx, n_x
):
    core, slot = lax.axis_index("core"), lax.axis_index("slot")
    twin, across = at_device(core=1 - core), at_device(slot=1 - slot)
    ctx, x = lax.axis_index("ctx"), lax.axis_index("x")
    greet([
        twin,
        across,
        at_device(x=1 - x),
        at_device(ctx=lax.rem(ctx + 1, n_ctx)),
        at_device(ctx=lax.rem(ctx + n_ctx - 1, n_ctx)),
    ])
    begin_lane, relay_lane, end_lane = lane_gather(
        lane_ref, lanes_out, lane_send, lane_recv, out_sem.at[4], n_ctx, n_x)
    begin_lane()
    rows, width = tok_ref.shape
    half = rows // 2
    tile = 256
    count = [0]
    started = []

    def launch(source, target_ref, target):
        i = count[0]
        count[0] += 1
        copy = pltpu.make_async_remote_copy(
            source, target_ref, send_sem.at[i], recv_sem.at[i],
            device_id=target, device_id_type=MESH)
        copy.start()
        started.append(copy)
        return copy

    def columns(body, n=width // tile):
        @pl.loop(0, n)
        def _(t):
            body(pl.ds(pl.multiple_of(t * tile, tile), tile))

    def chunks(body, size=64):
        @pl.loop(0, rows // size)
        def _(t):
            body(pl.ds(pl.multiple_of(t * size, size), size))

    def exchange(buf, turn, stage, product):
        halves = [
            launch(buf.at[pl.ds(h * half, half)], buf.at[pl.ds((2 + h) * rows, half)], across)
            for h in range(2)
        ]
        to_twin = launch(buf.at[pl.ds(0, rows)], buf.at[pl.ds(rows, rows)], twin)
        near_buf, far_buf = near.at[turn], far.at[turn]
        to_twin.wait_recv()
        stage(0, 2 * rows)
        product(0, 2 * rows, near_buf, 0)
        near_copy = launch(
            near_buf.at[pl.ds(rows, rows)], near_in.at[turn], twin)
        back = []
        for h in range(2):
            at = (2 + h) * rows
            halves[h].wait_recv()
            launch(
                buf.at[pl.ds(at, half)], buf.at[pl.ds(at + half, half)], twin).wait_recv()
            stage(at, rows)
            product(at, rows, far_buf, h * rows)
            i = 2 * turn + h
            launch(
                far_buf.at[pl.ds(h * rows + half, half)], far_in.at[i], twin).wait_recv()
            low_out[i] = (far_buf[pl.ds(h * rows, half), :] + far_in[i]).astype(BF16)
            back.append(launch(low_out.at[i], low_in.at[i], across))
        return near_copy, back

    def out_product(cols):
        first[:, cols] = mm(merged_ref[...], wo_ref[:, cols])

    columns(out_product)
    launch(first.at[pl.ds(rows, rows)], first_in, twin).wait_recv()

    def norm_one(at):
        values = tok_ref[at, :].astype(F32) + first[at, :] + first_in[at, :] + vec_ref[0:1, :]
        normed, unit, root = norm_forward(values, vec_ref[1:2, :], vec_ref[2:3, :])
        hidden[at, :] = normed
        unit_one[at, :] = unit
        roots[0, at, :] = jnp.broadcast_to(root, (root.shape[0], 128))
        hid[at, :] = normed.astype(BF16)

    chunks(norm_one)

    def up_stage(start, size):
        def body(cols):
            values = mm(hid[start : start + size, :], up_ref[:, cols]) + vec_ref[3:4, cols]
            active, bend = gelu_pair(values)
            act[start : start + size, cols] = active.astype(BF16)
            slope[start : start + size, cols] = bend

        columns(body)

    def down_product(start, size, target, at):
        def body(cols):
            target[at : at + size, cols] = mm(act[start : start + size, :], down_ref[:, cols])

        columns(body)

    near_copy, back = exchange(hid, 0, up_stage, down_product)
    relay_lane(1)
    out_copies = [
        pltpu.make_async_copy(hid, hid_out, out_sem.at[0]),
        pltpu.make_async_copy(act, act_out, out_sem.at[1]),
    ]
    for copy in out_copies:
        copy.start()
    vecs_ref[...] = jnp.zeros_like(vecs_ref)
    near_copy.wait_recv()

    def norm_two(at, h, local):
        downward = near[0, at, :] + near_in[0, at, :] + low_in[h, local, :].astype(F32)
        values = hidden[at, :] + downward + vec_ref[4:5, :]
        normed, unit, root = norm_forward(values, vec_ref[5:6, :], vec_ref[6:7, :])
        out_ref[at, :] = normed.astype(BF16)
        grad, gain, shift = norm_backward(full_ref[at, :], unit, root, vec_ref[5:6, :])
        two[at, :] = grad
        low = grad.astype(BF16)
        gdn[at, :] = low
        vecs_ref[5:6, :] += gain[None]
        vecs_ref[6:7, :] += shift[None]
        vecs_ref[4:5, :] += jnp.sum(low.astype(F32), axis=0, keepdims=True)

    def by_half(body, h, size=64):
        @pl.loop(0, half // size)
        def _(t):
            local = pl.multiple_of(t * size, size)
            body(pl.ds(h * half + local, size), h, pl.ds(local, size))

    for h in range(2):
        back[h].wait_recv()
        by_half(norm_two, h)

    def back_stage(start, size):
        def body(cols):
            grads = contract(gdn[start : start + size, :], down_ref[cols, :], 1, 1)
            low = (grads * slope[start : start + size, cols]).astype(BF16)
            gup[start : start + size, cols] = low
            vecs_ref[3:4, cols] += jnp.sum(low.astype(F32), axis=0, keepdims=True)

        columns(body)

    def back_product(start, size, target, at):
        def body(cols):
            target[at : at + size, cols] = contract(
                gup[start : start + size, :], up_ref[cols, :], 1, 1)

        columns(body)

    relay_lane(2)
    near_copy, back = exchange(gdn, 1, back_stage, back_product)
    for r in range(3, n_ctx):
        relay_lane(r)
    late_copies = [
        pltpu.make_async_copy(gdn, gdn_out, out_sem.at[2]),
        pltpu.make_async_copy(gup, gup_out, out_sem.at[3]),
    ]
    for copy in late_copies:
        copy.start()
    near_copy.wait_recv()

    def norm_back(at, h, local):
        grad = near[1, at, :] + near_in[1, at, :] + low_in[2 + h, local, :].astype(F32)
        grad = grad + two[at, :]
        root = roots[0, at, 0:1]
        one, gain, shift = norm_backward(grad, unit_one[at, :], root, vec_ref[1:2, :])
        one_ref[at, :] = one
        low = one.astype(BF16)
        att_ref[at, :] = low
        vecs_ref[1:2, :] += gain[None]
        vecs_ref[2:3, :] += shift[None]
        vecs_ref[0:1, :] += jnp.sum(low.astype(F32), axis=0, keepdims=True)

    for h in range(2):
        back[h].wait_recv()
        by_half(norm_back, h)
    launch(att_ref.at[pl.ds(0, rows)], att_ref.at[pl.ds(rows, rows)], twin).wait_recv()

    def merged_product(cols):
        gm_ref[:, cols] = contract(att_ref[...], wo_ref[cols, :], 1, 1).astype(BF16)

    columns(merged_product, wo_ref.shape[0] // tile)
    end_lane()
    for copy in started:
        copy.wait_send()
    for copy in out_copies + late_copies:
        copy.wait()


def layer(merged, tokens, w_out, up, down, vectors, grad_full, lane_shard):
    n_ctx, n_x = lax.axis_size("ctx"), lax.axis_size("x")
    chips = n_ctx * n_x
    rows, width = tokens.shape
    hidden = up.shape[1]
    lane = w_out.shape[0]
    vmem = pl.BlockSpec(memory_space=pltpu.VMEM)
    anywhere = pl.BlockSpec(memory_space=pl.ANY)
    dma = pltpu.SemaphoreType.DMA

    def shape(*dims, dtype=BF16):
        return jax.ShapeDtypeStruct(dims, dtype)

    def wide(*dims):
        return pltpu.VMEM(dims, F32)

    def low(*dims):
        return pltpu.VMEM(dims, BF16)

    return pl.pallas_call(
        partial(layer_kernel, n_ctx=n_ctx, n_x=n_x),
        in_specs=[vmem] * 8,
        out_specs=[vmem] * 5 + [anywhere] * 5,
        out_shape=[
            shape(rows, width),
            shape(rows, width, dtype=F32),
            shape(2 * rows, lane),
            shape(2 * rows, width),
            shape(8, width, dtype=F32),
            shape(4 * rows, hidden),
            shape(4 * rows, width),
            shape(4 * rows, width),
            shape(4 * rows, hidden),
            shape(chips, *lane_shard.shape),
        ],
        scratch_shapes=[
            wide(2 * rows, width),
            wide(rows, width),
            low(4 * rows, width),
            low(4 * rows, hidden),
            wide(4 * rows, hidden),
            low(4 * rows, width),
            low(4 * rows, hidden),
            wide(rows, width),
            wide(rows, width),
            wide(rows, width),
            wide(1, rows, 128),
            wide(2, 2 * rows, width),
            wide(2, rows, width),
            wide(2, 2 * rows, width),
            wide(4, rows // 2, width),
            low(4, rows // 2, width),
            low(4, rows // 2, width),
            dma((24,)),
            dma((24,)),
            dma((5,)),
            dma((3, chips)),
            dma((chips,)),
        ],
        compiler_params=pltpu.CompilerParams(
            collective_id=3, has_side_effects=True, vmem_limit_bytes=VMEM_LIMIT
        ),
        cost_estimate=pl.CostEstimate(
            flops=16 * rows * width * hidden, bytes_accessed=16 * rows * width, transcendentals=0
        ),
        name="layer",
    )(merged, tokens, w_out, up, down, vectors, grad_full, lane_shard)


def head_device(
    tokens,
    lengths,
    w_qkv,
    b_qkv,
    w_out,
    b_out,
    ln1_gain,
    ln1_bias,
    w_up,
    b_up,
    w_down,
    b_down,
    ln2_gain,
    ln2_bias,
    w_proj,
    cot_out,
    cot_emb,
):
    n_lane = lax.axis_size("ctx") * lax.axis_size("x")
    n_group = 2 * n_lane
    core = lax.axis_index("core")
    slot = lax.axis_index("slot")
    chip = lax.axis_index("ctx") * lax.axis_size("x") + lax.axis_index("x")
    me = 2 * chip + core
    slots, part, width = tokens.shape
    seq = part * n_group
    rows = slots * part
    shard = width // n_group
    ff_shard = w_down.shape[0]
    ff_half = ff_shard // 2
    proj = w_proj.shape[1]
    head_cols = 3 * HD

    small = jnp.concatenate(
        [b_qkv, b_out, ln1_gain, ln1_bias, b_up, b_down, ln2_gain, ln2_bias]
    )
    small_at = [0]
    for piece in (b_qkv, b_out, ln1_gain, ln1_bias, b_up, b_down, ln2_gain, ln2_bias):
        small_at.append(small_at[-1] + piece.shape[0])
    small_rows = -(-small.shape[0] // proj)
    small_rows = -(-small_rows // 16) * 16
    small = jnp.pad(small, (0, small_rows * proj - small.shape[0])).reshape(small_rows, proj)
    def two_lanes(mine, theirs):
        low_first = jnp.stack([mine, theirs], axis=0)
        high_first = jnp.stack([theirs, mine], axis=0)
        return jnp.where(core == 0, low_first, high_first)

    up_split = w_up.reshape(shard, n_lane, 2, 2, ff_half)
    up_mine = pick(up_split, core, 2)
    up_theirs = swap_core(pick(up_split, 1 - core, 2))
    up_chip = two_lanes(pick(up_mine, slot, 2), pick(up_theirs, slot, 2))
    down_split = w_down.reshape(2, ff_half, width)

    by_head = w_qkv.reshape(shard, 3, n_group, HD).transpose(2, 0, 1, 3)
    all_tokens, my_head, packed = gather_start(
        tokens,
        by_head.reshape(n_group, shard, head_cols),
        jnp.concatenate([w_proj, small], axis=0),
    )
    proj_full = packed[:, :shard].reshape(width, proj)
    smalls = packed[:, shard:].reshape(n_group, small_rows * proj).astype(F32)
    qkv_bias, out_bias, gain_one, shift_one, up_bias, down_bias, gain_two, shift_two = (
        smalls[:, a:b].reshape(-1) for a, b in zip(small_at[:-1], small_at[1:])
    )

    head_weight = my_head.reshape(width, head_cols)
    all_tokens = all_tokens.reshape(slots * seq, width)
    head_bias = pick(qkv_bias.reshape(1, 3, n_group, HD), me, 2).reshape(1, head_cols)
    cosine, sine = rope_rows(jnp.arange(seq, dtype=jnp.int32).astype(F32))
    cos_wide = jnp.tile(cosine, (1, 4))
    sin_wide = jnp.tile(sine, (1, 4))
    queries, keys, values, mixture, send, norms, out_lane, up, down = heads(
        lengths,
        all_tokens,
        head_weight,
        head_bias,
        cos_wide,
        sin_wide,
        part,
        w_out,
        up_chip.reshape(2 * shard, n_lane * ff_half),
        pick(down_split, slot, 0),
    )
    out_lane, up, down = (t.reshape(-1, t.shape[2]) for t in (out_lane, up, down))
    bias_lane = pick(up_bias.reshape(n_lane, 2, 2, ff_half), core, 1)
    up_bias_own = pick(bias_lane, slot, 1).reshape(-1)

    qkv_split = w_qkv.reshape(shard, 3, n_lane, 2, HD)
    qkv_mine = pick(qkv_split, core, 3)
    qkv_theirs = swap_core(pick(qkv_split, 1 - core, 3))
    qkv_chip = two_lanes(qkv_mine, qkv_theirs).transpose(3, 0, 1, 2, 4)
    qkv_chip = qkv_chip.reshape(n_lane, 2 * shard, head_cols)

    merged = lax.all_to_all(send, LANE, 0, 0, tiled=True)
    merged = merged.transpose(1, 2, 3, 0, 4).reshape(2 * rows, n_lane * HD)

    place = me * part + jnp.arange(part, dtype=jnp.int32)
    live = (place[None, :] < lengths[:, None]).reshape(rows, 1)
    grad_out = jnp.where(live, cot_out.reshape(rows, width).astype(F32), 0.0)
    grad_emb = jnp.where(live, cot_emb.reshape(rows, proj), 0)
    grad_full = grad_out + contract(grad_emb, proj_full, 1, 1)
    vectors = jnp.stack(
        [out_bias, gain_one, shift_one, up_bias_own, down_bias, gain_two, shift_two, shift_two]
    )
    (
        out_low,
        grad_one,
        grad_merged,
        grad_att,
        vector_grads,
        active,
        hidden_low,
        grad_down,
        grad_up,
        qkv_lane,
    ) = layer(
        merged, tokens.reshape(rows, width), out_lane, up, down, vectors, grad_full, qkv_chip
    )
    d_down = contract(active, grad_down, 0, 0).astype(BF16)
    d_up = contract(hidden_low, grad_up, 0, 0).astype(BF16)
    embeds = mm(out_low, proj_full).astype(BF16)
    d_proj = contract(out_low, grad_emb, 0, 0)
    (
        d_out_bias,
        d_gain_one,
        d_shift_one,
        up_bias_own_grad,
        d_down_bias,
        d_gain_two,
        d_shift_two,
    ) = (vector_grads[i] for i in range(7))
    grad_merged = grad_merged.reshape(2, slots, part, n_lane, HD).transpose(3, 0, 1, 2, 4)
    grad_heads = lax.all_to_all(grad_merged, LANE, 0, 0, tiled=True)

    def core_order(value):
        return jnp.where(core == 0, value, jnp.flip(value, axis=1))

    grad_heads = core_order(grad_heads).transpose(2, 0, 1, 3, 4).reshape(slots, seq, HD)

    d_out = contract(merged, grad_att, 0, 0).astype(BF16)

    spread = (
        (jnp.arange(2) == core)[:, None, None] & (jnp.arange(2) == slot)[None, :, None]
    ).astype(F32)
    up_bias_grad = up_bias_own_grad.reshape(n_lane, 1, 1, ff_half) * spread[None]
    vectors = (
        d_out_bias,
        d_gain_one,
        d_shift_one,
        up_bias_grad.reshape(-1),
        d_down_bias,
        d_gain_two,
        d_shift_two,
    )
    small_grad = jnp.concatenate([v.reshape(n_group, -1) for v in vectors], axis=1)
    small_cols = small_grad.shape[1]
    vec_rows = -(-small_cols // proj)
    vec_rows = -(-(shard + vec_rows) // 16) * 16 - shard
    small_grad = jnp.pad(small_grad, ((0, 0), (0, vec_rows * proj - small_cols)))
    small_grad = jnp.concatenate(
        [d_proj.reshape(n_group, shard, proj), small_grad.reshape(n_group, vec_rows, proj)], axis=1
    )
    row_dots = jnp.sum(grad_heads.astype(F32) * mixture, axis=-1).reshape(slots, 1, seq)
    joined, d_qkv, reduced, out_sum, small_sum = grads(
        lengths,
        queries,
        keys,
        values,
        grad_heads,
        norms,
        row_dots,
        all_tokens,
        cos_wide,
        sin_wide,
        d_down.reshape(n_lane, 2 * shard, width),
        d_up.reshape(n_lane, 2 * shard, width),
        d_out.reshape(n_lane, shard, width),
        small_grad.astype(BF16),
        part,
    )
    grad_w_down, grad_w_up, grad_w_out, small_sum, grad_w_qkv, bias_rows, input_grad = finish_grads(
        out_sum,
        small_sum,
        d_qkv,
        reduced,
        joined,
        qkv_lane,
        grad_one,
    )
    grad_w_proj = small_sum[:shard]
    vec_sum = small_sum[shard:].reshape(-1)
    vec_outs = []
    at = 0
    for v in vectors:
        size = v.size // n_group
        vec_outs.append(vec_sum[at : at + size])
        at += size
    (
        grad_b_out,
        grad_gain_one,
        grad_shift_one,
        grad_b_up,
        grad_b_down,
        grad_gain_two,
        grad_shift_two,
    ) = vec_outs

    qkv_bias_grad = bias_rows.reshape(n_group, 3, HD).transpose(1, 0, 2).reshape(-1)
    grad_b_qkv = lax.dynamic_slice(qkv_bias_grad, (me * b_qkv.shape[0],), (b_qkv.shape[0],))

    return (
        out_low.reshape(slots, part, width),
        embeds.reshape(slots, part, proj),
        input_grad.reshape(slots, part, width),
        grad_w_qkv,
        grad_b_qkv,
        grad_w_out,
        grad_b_out,
        grad_gain_one,
        grad_shift_one,
        grad_w_up,
        grad_b_up,
        grad_w_down,
        grad_b_down,
        grad_gain_two,
        grad_shift_two,
        grad_w_proj,
    )


def layer_norm(hidden, gain, shift):
    center = hidden - jnp.mean(hidden, axis=-1, keepdims=True)
    spread = jnp.mean(center * center, axis=-1, keepdims=True)
    return center * lax.rsqrt(spread + LN_EPS) * gain + shift


def rope_tables(positions, head_width):
    halfway = head_width // 2
    ladder = jnp.arange(halfway, dtype=jnp.float32) * (2.0 / head_width)
    frequency = jnp.power(jnp.float32(10000.0), -ladder)
    angles = positions[:, None] * frequency[None, :]
    return (jnp.cos(angles)[:, None, :], jnp.sin(angles)[:, None, :])


def rotate(values, cosine, sine_part):
    halfway = values.shape[-1] // 2
    first_half = values[..., :halfway]
    second_half = values[..., halfway:]
    return jnp.concatenate(
        [
            first_half * cosine - second_half * sine_part,
            second_half * cosine + first_half * sine_part,
        ],
        axis=-1,
    )


def block_scores(query_block, key_block, key_start, length, scale):
    scores = (
        jnp.einsum("qhd,khd->hqk", query_block, key_block, preferred_element_type=jnp.float32)
        * scale
    )
    key_ids = key_start + jnp.arange(key_block.shape[0], dtype=jnp.int32)
    return jnp.where((key_ids < length)[None, None, :], scores, NEG_FILL)


def per_device(
    tokens,
    lengths,
    w_qkv,
    b_qkv,
    w_out,
    b_out,
    ln1_gain,
    ln1_bias,
    w_up,
    b_up,
    w_down,
    b_down,
    ln2_gain,
    ln2_bias,
    w_proj,
    cot_out,
    cot_emb,
):
    n_fsdp = lax.axis_size("fsdp")
    n_ctx = lax.axis_size("ctx")
    ctx_at = lax.axis_index("ctx")
    fsdp_at = lax.axis_index("fsdp")
    groups, tok_slot, width = tokens.shape
    heads_here = H // n_fsdp
    lane_width = heads_here * HD
    span_rows = tok_slot * n_fsdp
    key_count = span_rows * n_ctx
    row_count = groups * tok_slot
    scale = HD ** (-0.5)
    query_rows = min(512, span_rows)
    key_rows = min(2048, key_count // 4)
    query_blocks = span_rows // query_rows
    key_blocks = key_count // key_rows
    key_starts = jnp.arange(key_blocks, dtype=jnp.int32) * key_rows
    qkv_full, qkv_bias, out_full, out_bias, gain_one, shift_one = (
        lax.all_gather(w_qkv, ("ctx", "fsdp"), axis=0, tiled=True),
        lax.all_gather(b_qkv, ("ctx", "fsdp"), axis=0, tiled=True),
        lax.all_gather(w_out, ("ctx", "fsdp"), axis=0, tiled=True),
        lax.all_gather(b_out, ("ctx", "fsdp"), axis=0, tiled=True),
        lax.all_gather(ln1_gain, ("ctx", "fsdp"), axis=0, tiled=True),
        lax.all_gather(ln1_bias, ("ctx", "fsdp"), axis=0, tiled=True),
    )
    token_pos = (ctx_at * n_fsdp + fsdp_at) * tok_slot + jnp.arange(tok_slot, dtype=jnp.int32)
    live_rows = (token_pos[None, :] < lengths[:, None]).reshape(row_count, 1)
    flat_tokens = tokens.reshape(row_count, width)
    joined = jnp.dot(flat_tokens, qkv_full, preferred_element_type=jnp.float32) + qkv_bias.astype(
        jnp.float32
    )
    cosine, sine_part = rope_tables(token_pos.astype(jnp.float32), HD)
    split_heads = joined.reshape(groups, tok_slot, 3, H, HD)
    rotated_query = rotate(split_heads[:, :, 0], cosine, sine_part)
    rotated_key = rotate(split_heads[:, :, 1], cosine, sine_part)
    packed = (
        jnp.stack([rotated_query, rotated_key, split_heads[:, :, 2]], axis=2)
        .astype(jnp.bfloat16)
        .reshape(groups, tok_slot, 3, n_fsdp, lane_width)
    )
    by_heads = lax.all_to_all(packed, "fsdp", split_axis=3, concat_axis=1, tiled=True)
    queries = by_heads[:, :, 0, 0]
    local_keys = by_heads[:, :, 1, 0]
    local_values = by_heads[:, :, 2, 0]
    all_keys, all_values = (
        lax.all_gather(local_keys, "ctx", axis=1, tiled=True),
        lax.all_gather(local_values, "ctx", axis=1, tiled=True),
    )

    def attend_slot(slot_item):
        slot_queries, slot_keys, slot_values, length = slot_item
        query_split = slot_queries.reshape(query_blocks, query_rows, heads_here, HD)
        key_split = slot_keys.reshape(key_blocks, key_rows, heads_here, HD)
        value_split = slot_values.reshape(key_blocks, key_rows, heads_here, HD)

        def per_query(query_block):

            def row_stats(state_pair, key_item):
                highest, running_sum = state_pair
                scores = block_scores(query_block, key_item[0], key_item[1], length, scale)
                new_high = jnp.maximum(highest, jnp.max(scores, axis=-1))
                running_sum = running_sum * jnp.exp(highest - new_high) + jnp.sum(
                    jnp.exp(scores - new_high[..., None]), axis=-1
                )
                return ((new_high, running_sum), None)

            start_state = (
                jnp.full((heads_here, query_rows), NEG_FILL, jnp.float32),
                jnp.zeros((heads_here, query_rows), jnp.float32),
            )
            highest, running_sum = lax.scan(row_stats, start_state, (key_split, key_starts))[0]
            log_norm = highest + jnp.log(running_sum)

            def weigh_values(accumulated, key_item):
                scores = block_scores(query_block, key_item[0], key_item[2], length, scale)
                weights = jnp.exp(scores - log_norm[..., None]).astype(jnp.bfloat16)
                return (
                    accumulated
                    + jnp.einsum(
                        "hqk,khd->qhd", weights, key_item[1], preferred_element_type=jnp.float32
                    ),
                    None,
                )

            mixture = lax.scan(
                weigh_values,
                jnp.zeros((query_rows, heads_here, HD), jnp.float32),
                (key_split, value_split, key_starts),
            )[0]
            return (mixture, log_norm)

        mixture, log_norm = lax.map(per_query, query_split)
        return (mixture.reshape(span_rows, lane_width), log_norm)

    mixture, log_norms = lax.map(attend_slot, (queries, all_keys, all_values, lengths))
    merged = lax.all_to_all(
        mixture.astype(jnp.bfloat16).reshape(groups, span_rows, 1, lane_width),
        "fsdp",
        split_axis=1,
        concat_axis=2,
        tiled=True,
    ).reshape(row_count, width)
    attended = jnp.dot(merged, out_full, preferred_element_type=jnp.float32) + out_bias.astype(
        jnp.float32
    )
    hidden_one, pull_one = jax.vjp(
        layer_norm,
        flat_tokens.astype(jnp.float32) + attended,
        gain_one.astype(jnp.float32),
        shift_one.astype(jnp.float32),
    )
    hidden_low = hidden_one.astype(jnp.bfloat16)
    up_full, up_bias, down_full, down_bias, gain_two, shift_two, proj_full = (
        lax.all_gather(w_up, ("ctx", "fsdp"), axis=0, tiled=True),
        lax.all_gather(b_up, ("ctx", "fsdp"), axis=0, tiled=True),
        lax.all_gather(w_down, ("ctx", "fsdp"), axis=0, tiled=True),
        lax.all_gather(b_down, ("ctx", "fsdp"), axis=0, tiled=True),
        lax.all_gather(ln2_gain, ("ctx", "fsdp"), axis=0, tiled=True),
        lax.all_gather(ln2_bias, ("ctx", "fsdp"), axis=0, tiled=True),
        lax.all_gather(w_proj, ("ctx", "fsdp"), axis=0, tiled=True),
    )
    upward = jnp.dot(hidden_low, up_full, preferred_element_type=jnp.float32) + up_bias.astype(
        jnp.float32
    )
    active_full, pull_gelu = jax.vjp(partial(jax.nn.gelu, approximate=False), upward)
    active = active_full.astype(jnp.bfloat16)
    downward = jnp.dot(active, down_full, preferred_element_type=jnp.float32) + down_bias.astype(
        jnp.float32
    )
    out_full_rows, pull_two = jax.vjp(
        layer_norm,
        hidden_one + downward,
        gain_two.astype(jnp.float32),
        shift_two.astype(jnp.float32),
    )
    out_low = out_full_rows.astype(jnp.bfloat16)
    projected = jnp.dot(out_low, proj_full, preferred_element_type=jnp.float32)
    back_qkv, back_qkv_bias, back_out, back_out_bias, back_gain_one, back_shift_one = (
        lax.all_gather(w_qkv, ("ctx", "fsdp"), axis=0, tiled=True),
        lax.all_gather(b_qkv, ("ctx", "fsdp"), axis=0, tiled=True),
        lax.all_gather(w_out, ("ctx", "fsdp"), axis=0, tiled=True),
        lax.all_gather(b_out, ("ctx", "fsdp"), axis=0, tiled=True),
        lax.all_gather(ln1_gain, ("ctx", "fsdp"), axis=0, tiled=True),
        lax.all_gather(ln1_bias, ("ctx", "fsdp"), axis=0, tiled=True),
    )
    back_up, back_up_bias, back_down, back_down_bias, back_gain_two, back_shift_two, back_proj = (
        lax.all_gather(w_up, ("ctx", "fsdp"), axis=0, tiled=True),
        lax.all_gather(b_up, ("ctx", "fsdp"), axis=0, tiled=True),
        lax.all_gather(w_down, ("ctx", "fsdp"), axis=0, tiled=True),
        lax.all_gather(b_down, ("ctx", "fsdp"), axis=0, tiled=True),
        lax.all_gather(ln2_gain, ("ctx", "fsdp"), axis=0, tiled=True),
        lax.all_gather(ln2_bias, ("ctx", "fsdp"), axis=0, tiled=True),
        lax.all_gather(w_proj, ("ctx", "fsdp"), axis=0, tiled=True),
    )
    grad_out = jnp.where(live_rows, cot_out.reshape(row_count, width).astype(jnp.float32), 0.0)
    grad_emb = jnp.where(live_rows, cot_emb.reshape(row_count, -1), 0)
    d_proj = jnp.einsum("rd,rp->dp", out_low, grad_emb, preferred_element_type=jnp.float32)
    grad_full = grad_out + jnp.einsum(
        "rp,dp->rd", grad_emb, back_proj, preferred_element_type=jnp.float32
    )
    grad_two, d_gain_two, d_shift_two = pull_two(grad_full)
    grad_down = grad_two.astype(jnp.bfloat16)
    d_down = jnp.einsum("rf,rd->fd", active, grad_down, preferred_element_type=jnp.float32)
    d_down_bias = jnp.sum(grad_down.astype(jnp.float32), axis=0)
    grad_act = jnp.einsum("rd,fd->rf", grad_down, back_down, preferred_element_type=jnp.float32)
    grad_up = pull_gelu(grad_act)[0].astype(jnp.bfloat16)
    d_up = jnp.einsum("rd,rf->df", hidden_low, grad_up, preferred_element_type=jnp.float32)
    d_up_bias = jnp.sum(grad_up.astype(jnp.float32), axis=0)
    grad_hidden = grad_two + jnp.einsum(
        "rf,df->rd", grad_up, back_up, preferred_element_type=jnp.float32
    )
    grad_one, d_gain_one, d_shift_one = pull_one(grad_hidden)
    grad_att = grad_one.astype(jnp.bfloat16)
    d_out = jnp.einsum("rd,re->de", merged, grad_att, preferred_element_type=jnp.float32)
    d_out_bias = jnp.sum(grad_att.astype(jnp.float32), axis=0)
    grad_merged = jnp.einsum(
        "re,de->rd", grad_att, back_out, preferred_element_type=jnp.float32
    ).astype(jnp.bfloat16)
    grad_heads = lax.all_to_all(
        grad_merged.reshape(groups, tok_slot, n_fsdp, lane_width),
        "fsdp",
        split_axis=2,
        concat_axis=1,
        tiled=True,
    ).reshape(groups, span_rows, lane_width)

    def attend_back(slot_item):
        slot_queries, slot_keys, slot_values, grad_mix, log_norm, length = slot_item
        query_split = slot_queries.reshape(query_blocks, query_rows, heads_here, HD)
        key_split = slot_keys.reshape(key_blocks, key_rows, heads_here, HD)
        value_split = slot_values.reshape(key_blocks, key_rows, heads_here, HD)
        grad_split = grad_mix.reshape(query_blocks, query_rows, heads_here, HD)

        def value_pass(value_total, query_item):
            query_block, grad_block, norm_block = query_item

            def value_per_key(row_dot, key_item):
                key_block, value_block, key_start = key_item
                scores = block_scores(query_block, key_block, key_start, length, scale)
                probability = jnp.exp(scores - norm_block[..., None])
                grad_probs = jnp.einsum(
                    "qhd,khd->hqk", grad_block, value_block, preferred_element_type=jnp.float32
                )
                value_part = jnp.einsum(
                    "hqk,qhd->khd",
                    probability.astype(jnp.bfloat16),
                    grad_block,
                    preferred_element_type=jnp.float32,
                )
                return (row_dot + jnp.sum(probability * grad_probs, axis=-1), value_part)

            row_dot, value_parts = lax.scan(
                value_per_key,
                jnp.zeros((heads_here, query_rows), jnp.float32),
                (key_split, value_split, key_starts),
            )
            return (value_total + value_parts.reshape(key_count, heads_here, HD), row_dot)

        value_grad, row_dots = lax.scan(
            value_pass,
            jnp.zeros((key_count, heads_here, HD), jnp.float32),
            (query_split, grad_split, log_norm),
        )

        def key_pass(key_total, query_item):
            query_block, grad_block, norm_block, dot_block = query_item

            def key_per_key(query_accum, key_item):
                key_block, value_block, key_start = key_item
                scores = block_scores(query_block, key_block, key_start, length, scale)
                probability = jnp.exp(scores - norm_block[..., None])
                grad_probs = jnp.einsum(
                    "qhd,khd->hqk", grad_block, value_block, preferred_element_type=jnp.float32
                )
                grad_scores = (probability * (grad_probs - dot_block[..., None])).astype(
                    jnp.bfloat16
                )
                query_accum = query_accum + jnp.einsum(
                    "hqk,khd->qhd", grad_scores, key_block, preferred_element_type=jnp.float32
                )
                key_part = jnp.einsum(
                    "hqk,qhd->khd", grad_scores, query_block, preferred_element_type=jnp.float32
                )
                return (query_accum, key_part)

            query_grad, key_parts = lax.scan(
                key_per_key,
                jnp.zeros((query_rows, heads_here, HD), jnp.float32),
                (key_split, value_split, key_starts),
            )
            return (key_total + key_parts.reshape(key_count, heads_here, HD), query_grad)

        key_grad, query_grads = lax.scan(
            key_pass,
            jnp.zeros((key_count, heads_here, HD), jnp.float32),
            (query_split, grad_split, log_norm, row_dots),
        )
        return (
            query_grads.reshape(span_rows, lane_width) * scale,
            key_grad.reshape(key_count, lane_width) * scale,
            value_grad.reshape(key_count, lane_width),
        )

    grad_queries, key_terms, value_terms = lax.map(
        attend_back, (queries, all_keys, all_values, grad_heads, log_norms, lengths)
    )
    grad_keys, grad_values = (
        lax.psum_scatter(
            key_terms.astype(jnp.bfloat16), "ctx", scatter_dimension=1, tiled=True
        ).astype(jnp.float32),
        lax.psum_scatter(
            value_terms.astype(jnp.bfloat16), "ctx", scatter_dimension=1, tiled=True
        ).astype(jnp.float32),
    )
    head_pos = (ctx_at * span_rows + jnp.arange(span_rows, dtype=jnp.int32)).astype(jnp.float32)
    head_cosine, head_sine = rope_tables(head_pos, HD)
    query_back = rotate(
        grad_queries.reshape(groups, span_rows, heads_here, HD), head_cosine, -head_sine
    )
    key_back = rotate(grad_keys.reshape(groups, span_rows, heads_here, HD), head_cosine, -head_sine)
    value_back = grad_values.reshape(groups, span_rows, heads_here, HD)
    grad_pack = (
        jnp.stack([query_back, key_back, value_back], axis=2)
        .astype(jnp.bfloat16)
        .reshape(groups, span_rows, 3, 1, lane_width)
    )
    grad_joined = lax.all_to_all(
        grad_pack, "fsdp", split_axis=1, concat_axis=3, tiled=True
    ).reshape(row_count, 3 * width)
    d_qkv = jnp.einsum("rd,re->de", flat_tokens, grad_joined, preferred_element_type=jnp.float32)
    d_qkv_bias = jnp.sum(grad_joined.astype(jnp.float32), axis=0)
    input_grad = (
        jnp.einsum("re,de->rd", grad_joined, back_qkv, preferred_element_type=jnp.float32)
        + grad_one
    ).astype(jnp.bfloat16)
    shards = (
        lax.psum_scatter(d_qkv, ("ctx", "fsdp"), scatter_dimension=0, tiled=True),
        lax.psum_scatter(d_qkv_bias, ("ctx", "fsdp"), scatter_dimension=0, tiled=True),
        lax.psum_scatter(d_out, ("ctx", "fsdp"), scatter_dimension=0, tiled=True),
        lax.psum_scatter(d_out_bias, ("ctx", "fsdp"), scatter_dimension=0, tiled=True),
        lax.psum_scatter(d_gain_one, ("ctx", "fsdp"), scatter_dimension=0, tiled=True),
        lax.psum_scatter(d_shift_one, ("ctx", "fsdp"), scatter_dimension=0, tiled=True),
        lax.psum_scatter(d_up, ("ctx", "fsdp"), scatter_dimension=0, tiled=True),
        lax.psum_scatter(d_up_bias, ("ctx", "fsdp"), scatter_dimension=0, tiled=True),
        lax.psum_scatter(d_down, ("ctx", "fsdp"), scatter_dimension=0, tiled=True),
        lax.psum_scatter(d_down_bias, ("ctx", "fsdp"), scatter_dimension=0, tiled=True),
        lax.psum_scatter(d_gain_two, ("ctx", "fsdp"), scatter_dimension=0, tiled=True),
        lax.psum_scatter(d_shift_two, ("ctx", "fsdp"), scatter_dimension=0, tiled=True),
        lax.psum_scatter(d_proj, ("ctx", "fsdp"), scatter_dimension=0, tiled=True),
    )
    totals = (
        lax.psum(shards[0].astype(jnp.bfloat16), "slot").astype(jnp.float32),
        lax.psum(shards[1].astype(jnp.bfloat16), "slot").astype(jnp.float32),
        lax.psum(shards[2].astype(jnp.bfloat16), "slot").astype(jnp.float32),
        lax.psum(shards[3].astype(jnp.bfloat16), "slot").astype(jnp.float32),
        lax.psum(shards[4].astype(jnp.bfloat16), "slot").astype(jnp.float32),
        lax.psum(shards[5].astype(jnp.bfloat16), "slot").astype(jnp.float32),
        lax.psum(shards[6].astype(jnp.bfloat16), "slot").astype(jnp.float32),
        lax.psum(shards[7].astype(jnp.bfloat16), "slot").astype(jnp.float32),
        lax.psum(shards[8].astype(jnp.bfloat16), "slot").astype(jnp.float32),
        lax.psum(shards[9].astype(jnp.bfloat16), "slot").astype(jnp.float32),
        lax.psum(shards[10].astype(jnp.bfloat16), "slot").astype(jnp.float32),
        lax.psum(shards[11].astype(jnp.bfloat16), "slot").astype(jnp.float32),
        lax.psum(shards[12].astype(jnp.bfloat16), "slot").astype(jnp.float32),
    )
    return (
        out_low.reshape(groups, tok_slot, width),
        projected.astype(jnp.bfloat16).reshape(groups, tok_slot, -1),
        input_grad.reshape(groups, tok_slot, width),
        totals[0],
        totals[1],
        totals[2],
        totals[3],
        totals[4],
        totals[5],
        totals[6],
        totals[7],
        totals[8],
        totals[9],
        totals[10],
        totals[11],
        totals[12],
    )


def solution(mesh):
    n_slot, n_ctx, n_fsdp = (mesh.shape[a] for a in ("slot", "ctx", "fsdp"))
    rows_axes = ("ctx", "fsdp")
    step = per_device
    if n_slot == 2 and n_fsdp % 2 == 0 and n_ctx * n_fsdp == H:
        mesh = Mesh(
            mesh.devices.reshape(n_slot, n_ctx, n_fsdp // 2, 2), ("slot", "ctx", "x", "core")
        )
        rows_axes = GROUP
        step = head_device
    in_specs = (
        P("slot", rows_axes, None),
        P("slot"),
        P(rows_axes, None),
        P(rows_axes),
        P(rows_axes, None),
        P(rows_axes),
        P(rows_axes),
        P(rows_axes),
        P(rows_axes, None),
        P(rows_axes),
        P(rows_axes, None),
        P(rows_axes),
        P(rows_axes),
        P(rows_axes),
        P(rows_axes, None),
        P("slot", rows_axes, None),
        P("slot", rows_axes, None),
    )
    out_specs = (
        P("slot", rows_axes, None),
        P("slot", rows_axes, None),
        P("slot", rows_axes, None),
        P(rows_axes, None),
        P(rows_axes),
        P(rows_axes, None),
        P(rows_axes),
        P(rows_axes),
        P(rows_axes),
        P(rows_axes, None),
        P(rows_axes),
        P(rows_axes, None),
        P(rows_axes),
        P(rows_axes),
        P(rows_axes),
        P(rows_axes, None),
    )
    return jax.shard_map(
        step, mesh=mesh, in_specs=in_specs, out_specs=out_specs, check_vma=False
    )
```

```python
from functools import partial

import jax
import jax.numpy as jnp
from jax import lax
from jax.experimental import pallas as pl
from jax.experimental.pallas import tpu as pltpu
from jax.sharding import Mesh
from jax.sharding import PartitionSpec as P

H = 16
HD = 64
LN_EPS = 1e-05
NEG_FILL = -1e30
F32 = jnp.float32
BF16 = jnp.bfloat16
GROUP = ("ctx", "x", "core")
LANE = ("ctx", "x")
SWAP = [(0, 1), (1, 0)]
VMEM_LIMIT = 60 * 1024 * 1024


def mm(left, right):
    return jnp.dot(left, right, preferred_element_type=F32)


def contract(left, right, left_dim, right_dim):
    return lax.dot_general(
        left, right, (((left_dim,), (right_dim,)), ((), ())), preferred_element_type=F32
    )


def swap_core(value):
    return lax.ppermute(value, "core", SWAP)


def swap_slot(value):
    return lax.ppermute(value, "slot", SWAP)


def pick(stacked, index, axis):
    return lax.dynamic_index_in_dim(stacked, index, axis, keepdims=False)


MESH = pl.DeviceIdType.MESH


def at_device(**where):
    names = ("slot", "ctx", "x", "core")
    return tuple(where[n] if n in where else lax.axis_index(n) for n in names)


def greet(peers):
    barrier = pltpu.get_barrier_semaphore()
    for peer in peers:
        pl.semaphore_signal(barrier, inc=1, device_id=peer, device_id_type=MESH)
    pl.semaphore_wait(barrier, len(peers))


def group_peers(n_ctx, n_x):
    ctx, x, core = (lax.axis_index(n) for n in GROUP)
    peers = []
    for dz in range(n_ctx):
        for dx in range(n_x):
            for dc in range(2):
                if dz or dx or dc:
                    where = (lax.rem(ctx + dz, n_ctx), lax.rem(x + dx, n_x), lax.rem(core + dc, 2))
                    peers.append(where)
    return peers


def start_kernel(
    tok_ref, head_ref, small_ref, all_ref, heads_ref, smalls_ref,
    far_send, block_send, local_sem, head_recv, small_recv, block_recv, *, n_ctx, n_x
):
    part = tok_ref.shape[1]
    ctx, x, core = (lax.axis_index(n) for n in GROUP)
    me = (ctx * n_x + x) * 2 + core
    peers = group_peers(n_ctx, n_x)
    greet([at_device(ctx=z, x=a, core=c) for z, a, c in peers])

    def block_at(b):
        return all_ref.at[:, pl.ds(pl.multiple_of(b * part, part), part), :]

    pushes = []
    for k, (z, a, c) in enumerate(peers):
        them = (z * n_x + a) * 2 + c
        target = at_device(ctx=z, x=a, core=c)
        pushes.append(pltpu.make_async_remote_copy(
            head_ref.at[them], heads_ref.at[me], far_send.at[2 * k], head_recv.at[me],
            device_id=target, device_id_type=MESH))
        pushes.append(pltpu.make_async_remote_copy(
            small_ref, smalls_ref.at[me], far_send.at[2 * k + 1], small_recv.at[me],
            device_id=target, device_id_type=MESH))
    locals_ = [
        pltpu.make_async_copy(tok_ref, block_at(me), local_sem.at[0]),
        pltpu.make_async_copy(head_ref.at[me], heads_ref.at[me], local_sem.at[1]),
        pltpu.make_async_copy(small_ref, smalls_ref.at[me], local_sem.at[2]),
    ]

    def send(b, source, lane, target):
        return pltpu.make_async_remote_copy(
            source, block_at(b), block_send.at[lane, b], block_recv.at[b],
            device_id=target, device_id_type=MESH)

    up = at_device(ctx=lax.rem(ctx + 1, n_ctx))
    down = at_device(ctx=lax.rem(ctx + n_ctx - 1, n_ctx))
    side = at_device(x=1 - x)
    twin = at_device(core=1 - core)

    def here(b):
        return send(b, block_at(b), 0, twin)

    @pl.when(ctx + 1 < n_ctx)
    def _():
        send(me, tok_ref, 0, up).start()

    @pl.when(ctx > 0)
    def _():
        send(me, tok_ref, 1, down).start()

    send(me, tok_ref, 2, side).start()
    send(me, tok_ref, 3, twin).start()
    for copy in locals_:
        copy.start()

    for r in range(1, n_ctx):
        if r == n_ctx - 1:
            for push in pushes:
                push.start()
        low = ctx - r
        high = ctx + r

        @pl.when(low >= 0)
        def _():
            b = (low * n_x + x) * 2 + core
            here(b).wait_recv()

            @pl.when(ctx + 1 < n_ctx)
            def _():
                send(b, block_at(b), 0, up).start()

            send(b, block_at(b), 2, side).start()
            send(b, block_at(b), 3, twin).start()

        @pl.when(high < n_ctx)
        def _():
            b = (high * n_x + x) * 2 + core
            here(b).wait_recv()

            @pl.when(ctx > 0)
            def _():
                send(b, block_at(b), 1, down).start()

            send(b, block_at(b), 2, side).start()
            send(b, block_at(b), 3, twin).start()

    def from_side(z):
        b = (z * n_x + (1 - x)) * 2 + core
        here(b).wait_recv()
        send(b, block_at(b), 3, twin).start()

    from_side(ctx)
    for r in range(1, n_ctx):
        @pl.when(ctx - r >= 0)
        def _():
            from_side(ctx - r)

        @pl.when(ctx + r < n_ctx)
        def _():
            from_side(ctx + r)

    for z in range(n_ctx):
        for a in range(n_x):
            here((z * n_x + a) * 2 + 1 - core).wait_recv()
    for k, (z, a, c) in enumerate(peers):
        them = (z * n_x + a) * 2 + c
        pltpu.make_async_remote_copy(
            head_ref.at[them], heads_ref.at[them], far_send.at[2 * k], head_recv.at[them],
            device_id=twin, device_id_type=MESH).wait_recv()
        pltpu.make_async_remote_copy(
            small_ref, smalls_ref.at[them], far_send.at[2 * k + 1], small_recv.at[them],
            device_id=twin, device_id_type=MESH).wait_recv()
    for push in pushes:
        push.wait_send()
    for copy in locals_:
        copy.wait()

    for z in range(n_ctx):
        b = (z * n_x + x) * 2 + core

        @pl.when((z <= ctx) & (ctx + 1 < n_ctx))
        def _():
            send(b, block_at(b), 0, up).wait_send()

        @pl.when((z >= ctx) & (ctx > 0))
        def _():
            send(b, block_at(b), 1, down).wait_send()

        send(b, block_at(b), 2, side).wait_send()
        send(b, block_at(b), 3, twin).wait_send()
        other = (z * n_x + (1 - x)) * 2 + core
        send(other, block_at(other), 3, twin).wait_send()


def gather_start(tokens, heads, small):
    n_ctx, n_x = lax.axis_size("ctx"), lax.axis_size("x")
    n = 2 * n_ctx * n_x
    slots, part, width = tokens.shape
    vmem = pl.BlockSpec(memory_space=pltpu.VMEM)
    anywhere = pl.BlockSpec(memory_space=pl.ANY)
    dma = pltpu.SemaphoreType.DMA
    return pl.pallas_call(
        partial(start_kernel, n_ctx=n_ctx, n_x=n_x),
        in_specs=[vmem, vmem, vmem],
        out_specs=[anywhere, vmem, vmem],
        out_shape=[
            jax.ShapeDtypeStruct((slots, n * part, width), tokens.dtype),
            jax.ShapeDtypeStruct(heads.shape, heads.dtype),
            jax.ShapeDtypeStruct((n,) + small.shape, small.dtype),
        ],
        scratch_shapes=[
            dma((2 * (n - 1),)), dma((4, n)), dma((3,)), dma((n,)), dma((n,)), dma((n,))
        ],
        compiler_params=pltpu.CompilerParams(
            collective_id=1, has_side_effects=True, vmem_limit_bytes=VMEM_LIMIT
        ),
        cost_estimate=pl.CostEstimate(
            flops=0, bytes_accessed=2 * n * tokens.size, transcendentals=0
        ),
        name="gather_start",
    )(tokens, heads, small)


def finish_kernel(
    out_ref, small_ref, qkv_ref, red_ref, join_ref, weight_ref, one_ref,
    g_down, g_up, g_out, g_small, g_qkv, g_bias, g_in,
    pair_small, pair_qkv, sum_qkv, qkvs,
    pair_down, pair_out, last_up, joins, partial_in, pair_in,
    join_send, join_recv, far_send, qkv_recv, y_send, y_recv,
    *, n_ctx, n_x
):
    ctx, x, core = (lax.axis_index(n) for n in GROUP)
    slot = lax.axis_index("slot")
    chip = ctx * n_x + x
    me = 2 * chip + core
    shard, width = g_out.shape
    part = g_down.shape[0] // 2
    peers = group_peers(n_ctx, n_x)
    lane_peers = [(z, a) for z, a, c in peers[1::2]]
    across = at_device(slot=1 - slot)
    corner = at_device(slot=1 - slot, core=1 - core)
    twin = at_device(core=1 - core)
    greet([at_device(ctx=z, x=a, core=c) for z, a, c in peers] + [across, corner])

    def remote(source, target_ref, send_sem, recv_sem, target):
        return pltpu.make_async_remote_copy(
            source, target_ref, send_sem, recv_sem, device_id=target, device_id_type=MESH)

    started = []

    def launch(copy):
        copy.start()
        started.append(copy)
        return copy

    def pair_copy(i, source, target_ref, target):
        return launch(remote(source, target_ref, y_send.at[i], y_recv.at[i], target))

    qkv_copy = pair_copy(0, qkv_ref, pair_qkv, across)
    mine = pl.multiple_of(part + core * shard, shard)
    theirs = pl.multiple_of(part + (1 - core) * shard, shard)
    for k, (z, a) in enumerate(lane_peers):
        launch(remote(
            join_ref.at[z * n_x + a], joins.at[chip], join_send.at[k], join_recv.at[chip],
            at_device(ctx=z, x=a)))
    down_copy = pair_copy(4, red_ref.at[pl.ds(0, part)], pair_down, across)
    quarter_copies = [
        pair_copy(5, red_ref.at[pl.ds(theirs, shard)], last_up.at[0], twin),
        pair_copy(6, red_ref.at[pl.ds(mine, shard)], last_up.at[1], across),
        pair_copy(7, red_ref.at[pl.ds(theirs, shard)], last_up.at[2], corner),
    ]

    small_copy = pair_copy(1, small_ref, pair_small, across)
    out_copy = pair_copy(3, out_ref, pair_out, across)
    qkv_copy.wait_recv()
    sum_qkv[...] = (qkv_ref[...].astype(F32) + pair_qkv[...].astype(F32)).astype(BF16)
    for k, (z, a, c) in enumerate(peers):
        them = (z * n_x + a) * 2 + c
        launch(remote(
            sum_qkv.at[them], qkvs.at[me], far_send.at[k], qkv_recv.at[me],
            at_device(ctx=z, x=a, core=c)))
    qkvs[me] = sum_qkv[me]

    def add_head(source, rows_of, first):
        weight = jnp.concatenate(
            [weight_ref[b, source] for b in range(weight_ref.shape[0])], axis=0)
        for h in range(2):
            owner = core if h == 0 else 1 - core
            rows = rows_of(owner)
            cols = rows.shape[2] // 2
            rows = jnp.concatenate(
                [r for t in range(rows.shape[0]) for r in (rows[t, :, :cols], rows[t, :, cols:])],
                axis=0)
            term = contract(rows, weight, 1, 1)
            partial_in[h] = term if first else partial_in[h] + term

    add_head(chip, lambda owner: join_ref[chip, owner], True)

    half = pl.multiple_of(slot * part, part)
    other_half = pl.multiple_of((1 - slot) * part, part)
    g_down[pl.ds(half, part), :] = red_ref[pl.ds(0, part), :].astype(F32)
    down_copy.wait_recv()
    g_down[pl.ds(other_half, part), :] = pair_down[...].astype(F32)

    def place_quarter(rows, quarter_core, quarter_slot):
        for k in range(n_ctx * n_x):
            at = pl.multiple_of(((2 * k + quarter_core) * 2 + quarter_slot) * part, part)
            g_up[:, pl.ds(at, part)] = rows[:, k * part : (k + 1) * part].astype(F32)

    place_quarter(red_ref[pl.ds(mine, shard), :], core, slot)
    quarter_copies[0].wait_recv()
    place_quarter(last_up[0], 1 - core, slot)
    quarter_copies[1].wait_recv()
    place_quarter(last_up[1], core, 1 - slot)
    quarter_copies[2].wait_recv()
    place_quarter(last_up[2], 1 - core, 1 - slot)

    @pl.loop(1, n_ctx * n_x)
    def _(o):
        source = lax.rem(ctx + o // n_x, n_ctx) * n_x + lax.rem(x + o % n_x, n_x)
        remote(
            join_ref.at[source], joins.at[source], join_send.at[0], join_recv.at[source], twin
        ).wait_recv()
        add_head(source, lambda owner: joins[source, owner], False)

    in_copy = pair_copy(2, partial_in.at[1], pair_in, twin)

    small_copy.wait_recv()
    g_small[...] = small_ref[...].astype(F32) + pair_small[...].astype(F32)
    in_copy.wait_recv()
    g_in[...] = (partial_in[0] + pair_in[...] + one_ref[...]).astype(BF16)
    for z, a, c in peers:
        them = (z * n_x + a) * 2 + c
        remote(
            sum_qkv.at[them], qkvs.at[them], far_send.at[0], qkv_recv.at[them], twin
        ).wait_recv()
    for k in range(n_ctx * n_x):
        heads = [qkvs[2 * k + c, :shard, :].astype(F32) for c in range(2)]
        for t in range(3):
            at = t * width + 2 * HD * k
            g_qkv[:, at : at + 2 * HD] = jnp.concatenate(
                [h[:, t * HD : (t + 1) * HD] for h in heads], axis=1)
        for c in range(2):
            g_bias[2 * k + c : 2 * k + c + 1, :] = qkvs[2 * k + c, shard : shard + 1, :].astype(F32)
    out_copy.wait_recv()
    g_out[...] = out_ref[...].astype(F32) + pair_out[...].astype(F32)
    for copy in started:
        copy.wait_send()


def finish_grads(out, small, qkv, reduced, joined, weight, grad_one):
    n_ctx, n_x = lax.axis_size("ctx"), lax.axis_size("x")
    n = 2 * n_ctx * n_x
    shard, width = out.shape
    part = reduced.shape[0] // 2
    vmem = pl.BlockSpec(memory_space=pltpu.VMEM)
    dma = pltpu.SemaphoreType.DMA

    def low(*shape):
        return pltpu.VMEM(shape, BF16)

    def wide(*shape):
        return jax.ShapeDtypeStruct(shape, F32)

    return pl.pallas_call(
        partial(finish_kernel, n_ctx=n_ctx, n_x=n_x),
        in_specs=[vmem] * 7,
        out_specs=[vmem] * 7,
        out_shape=[
            wide(2 * part, width),
            wide(shard, 4 * width),
            wide(shard, width),
            wide(*small.shape),
            wide(shard, 3 * width),
            wide(n, qkv.shape[2]),
            jax.ShapeDtypeStruct(grad_one.shape, BF16),
        ],
        scratch_shapes=[
            low(*small.shape),
            low(*qkv.shape),
            low(*qkv.shape),
            low(*qkv.shape),
            low(part, width),
            low(*out.shape),
            low(3, shard, width),
            low(*joined.shape),
            pltpu.VMEM((2,) + grad_one.shape, F32),
            pltpu.VMEM(grad_one.shape, F32),
            dma((n_ctx * n_x - 1,)),
            dma((n_ctx * n_x,)),
            dma((n - 1,)),
            dma((n,)),
            dma((8,)),
            dma((8,)),
        ],
        compiler_params=pltpu.CompilerParams(
            collective_id=2, has_side_effects=True, vmem_limit_bytes=VMEM_LIMIT
        ),
        cost_estimate=pl.CostEstimate(flops=0, bytes_accessed=16 * joined.size, transcendentals=0),
        name="finish_grads",
    )(out, small, qkv, reduced, joined, weight, grad_one)


def lane_gather(mine_ref, all_ref, send_sem, recv_sem, local_sem, n_ctx, n_x):
    ctx, x = lax.axis_index("ctx"), lax.axis_index("x")
    chip = ctx * n_x + x
    routes = (
        at_device(ctx=lax.rem(ctx + 1, n_ctx)),
        at_device(ctx=lax.rem(ctx + n_ctx - 1, n_ctx)),
        at_device(x=1 - x),
    )

    def send(k, lane, own=False):
        return pltpu.make_async_remote_copy(
            mine_ref if own else all_ref.at[k], all_ref.at[k], send_sem.at[lane, k], recv_sem.at[k],
            device_id=routes[lane], device_id_type=MESH)

    local = pltpu.make_async_copy(mine_ref, all_ref.at[chip], local_sem)

    def begin():
        @pl.when(ctx + 1 < n_ctx)
        def _():
            send(chip, 0, own=True).start()

        @pl.when(ctx > 0)
        def _():
            send(chip, 1, own=True).start()

        send(chip, 2, own=True).start()
        local.start()

    def relay(r):
        for sign, lane, more in ((-1, 0, ctx + 1 < n_ctx), (1, 1, ctx > 0)):
            z = ctx + sign * r

            @pl.when((z >= 0) & (z < n_ctx))
            def _():
                k = z * n_x + x
                send(k, 0).wait_recv()

                @pl.when(more)
                def _():
                    send(k, lane).start()

                send(k, 2).start()

    def end():
        for z in range(n_ctx):
            k = z * n_x + x
            send(z * n_x + 1 - x, 0).wait_recv()

            @pl.when((z <= ctx) & (ctx + 1 < n_ctx))
            def _():
                send(k, 0).wait_send()

            @pl.when((z >= ctx) & (ctx > 0))
            def _():
                send(k, 1).wait_send()

            send(k, 2).wait_send()
        local.wait()

    return begin, relay, end


def lane_gather_x_first(mine_ref, all_ref, send_sem, recv_sem, local_sem, n_ctx, n_x):
    ctx, x = lax.axis_index("ctx"), lax.axis_index("x")
    chip = ctx * n_x + x
    pair = ctx * n_x + 1 - x
    routes = (
        at_device(ctx=lax.rem(ctx + 1, n_ctx)),
        at_device(ctx=lax.rem(ctx + n_ctx - 1, n_ctx)),
        at_device(x=1 - x),
    )
    ways = ((-1, 0, ctx + 1 < n_ctx), (1, 1, ctx > 0))

    def send(k, lane, own=False):
        return pltpu.make_async_remote_copy(
            mine_ref if own else all_ref.at[k], all_ref.at[k], send_sem.at[lane, k], recv_sem.at[k],
            device_id=routes[lane], device_id_type=MESH)

    local = pltpu.make_async_copy(mine_ref, all_ref.at[chip], local_sem)

    def along(k, own=False):
        for _, lane, more in ways:
            @pl.when(more)
            def _():
                send(k, lane, own).start()

    def begin():
        send(chip, 2, own=True).start()
        along(chip, own=True)
        local.start()

    def pass_on(r, line):
        for sign, lane, more in ways:
            z = ctx + sign * r

            @pl.when((z >= 0) & (z < n_ctx))
            def _():
                k = z * n_x + line
                send(k, lane).wait_recv()

                @pl.when(more)
                def _():
                    send(k, lane).start()

    def relay(r):
        if r == 1:
            send(pair, 2).wait_recv()
            along(pair)
        else:
            pass_on(r - 1, 1 - x)
        pass_on(r, x)

    def end():
        pass_on(n_ctx - 1, 1 - x)
        send(chip, 2).wait_send()
        for z in range(n_ctx):
            for line in range(n_x):
                @pl.when((z <= ctx) & (ctx + 1 < n_ctx))
                def _():
                    send(z * n_x + line, 0).wait_send()

                @pl.when((z >= ctx) & (ctx > 0))
                def _():
                    send(z * n_x + line, 1).wait_send()

        local.wait()

    return begin, relay, end


QB = 512
KB = 512


def turn(pair, cosine, sine):
    half = HD // 2
    lanes = lax.broadcasted_iota(jnp.int32, (1, 2 * HD), 1)
    low = lax.rem(lanes, HD) < half
    swapped = jnp.where(low, pltpu.roll(pair, 2 * HD - half, 1), pltpu.roll(pair, half, 1))
    return pair * cosine + swapped * jnp.where(low, -sine, sine)


def heads_kernel(
    len_ref, tok_ref, w_ref, b_ref, cos_ref, sin_ref, wa_ref, wu_ref, wd_ref,
    q_ref, k_ref, v_ref, mix_ref, send_ref, norm_ref, fa_ref, fu_ref, fd_ref,
    a_send, a_recv, u_send, u_recv, d_send, d_recv, local_sem, *, n_ctx, n_x, part
):
    core = lax.axis_index("core")
    ctx, x = lax.axis_index("ctx"), lax.axis_index("x")
    greet([
        at_device(x=1 - x),
        at_device(ctx=lax.rem(ctx + 1, n_ctx)),
        at_device(ctx=lax.rem(ctx + n_ctx - 1, n_ctx)),
    ])
    flows = [
        lane_gather_x_first(wa_ref, fa_ref, a_send, a_recv, local_sem.at[0], n_ctx, n_x),
        lane_gather(wu_ref, fu_ref, u_send, u_recv, local_sem.at[1], n_ctx, n_x),
        lane_gather(wd_ref, fd_ref, d_send, d_recv, local_sem.at[2], n_ctx, n_x),
    ]
    for begin, _, _ in flows:
        begin()
    slots, seq, _ = q_ref.shape

    def relay(r):
        if r < n_ctx:
            for _, hop, _ in flows:
                hop(r)

    blocks = seq // QB

    def project():
        @pl.loop(0, slots * blocks)
        def _(n):
            s, i = n // blocks, lax.rem(n, blocks)
            rows = pl.ds(pl.multiple_of(i * QB, QB), QB)
            tokens = tok_ref[pl.ds(pl.multiple_of(n * QB, QB), QB), :]
            joined = mm(tokens, w_ref[...]) + b_ref[...]
            turned = turn(joined[:, : 2 * HD], cos_ref[rows, :], sin_ref[rows, :])
            q_ref[s, rows, :] = (turned[:, :HD].astype(BF16) * HD ** (-0.5)).astype(BF16)
            k_ref[s, rows, :] = turned[:, HD:].astype(BF16)
            v_ref[s, rows, :] = joined[:, 2 * HD :].astype(BF16)

    def attend():
        @pl.loop(0, slots * blocks)
        def _(n):
            s, i = n // blocks, lax.rem(n, blocks)
            length = len_ref[s]
            rows = pl.ds(pl.multiple_of(i * QB, QB), QB)
            queries = q_ref[s, rows, :]

            @pl.when(n == blocks)
            def _():
                relay(2)

            def step(j, state):
                highest, total, mix = state
                start = pl.multiple_of(j * KB, KB)
                scores = contract(queries, k_ref[s, pl.ds(start, KB), :], 1, 1)
                ids = start + lax.broadcasted_iota(jnp.int32, (1, KB), 1)
                scores = jnp.where(ids < length, scores, NEG_FILL)
                higher = jnp.maximum(highest, jnp.max(scores, axis=1, keepdims=True))
                fade = jnp.exp(highest - higher)
                weights = jnp.exp(scores - higher)
                total = total * fade + jnp.sum(weights, axis=1, keepdims=True)
                mix = mix * fade + mm(weights.astype(BF16), v_ref[s, pl.ds(start, KB), :])
                return higher, total, mix

            highest, total, mix = lax.fori_loop(
                0,
                seq // KB,
                step,
                (
                    jnp.full((QB, 1), NEG_FILL, F32),
                    jnp.zeros((QB, 1), F32),
                    jnp.zeros((QB, HD), F32),
                ),
            )
            mix = mix / total
            mix_ref[s, rows, :] = mix
            log_norm = jnp.broadcast_to(highest + jnp.log(total), (QB, 128))
            norm_ref[s, :, rows] = jnp.transpose(log_norm)[0:1, :]
            low = mix.astype(BF16)
            chips = QB // (2 * part)
            for chip in range(chips):
                for half in range(2):
                    at = (2 * chip + half) * part
                    upper, lower = low[at : at + part // 2], low[at + part // 2 : at + part]
                    send_ref[i * chips + chip, half ^ core, s] = jnp.concatenate(
                        [upper, lower], axis=1)

    project()
    relay(1)
    attend()
    for r in range(3, n_ctx):
        relay(r)
    for _, _, end in flows:
        end()


def heads(lengths, tokens, weight, bias, cosine, sine, part, *shards):
    n_ctx, n_x = lax.axis_size("ctx"), lax.axis_size("x")
    chips = n_ctx * n_x
    slots, seq = lengths.shape[0], cosine.shape[0]
    vmem = pl.BlockSpec(memory_space=pltpu.VMEM)
    anywhere = pl.BlockSpec(memory_space=pl.ANY)
    dma = pltpu.SemaphoreType.DMA
    head = jax.ShapeDtypeStruct((slots, seq, HD), BF16)
    return pl.pallas_call(
        partial(heads_kernel, n_ctx=n_ctx, n_x=n_x, part=part),
        in_specs=[pl.BlockSpec(memory_space=pltpu.SMEM)] + [vmem] * 8,
        out_specs=[vmem] * 6 + [anywhere] * 3,
        out_shape=[
            head,
            head,
            head,
            jax.ShapeDtypeStruct((slots, seq, HD), F32),
            jax.ShapeDtypeStruct((chips, 2, slots, part // 2, 2 * HD), BF16),
            jax.ShapeDtypeStruct((slots, 1, seq), F32),
        ]
        + [jax.ShapeDtypeStruct((chips,) + w.shape, w.dtype) for w in shards],
        scratch_shapes=[dma((3, chips)), dma((chips,))] * 3 + [dma((3,))],
        compiler_params=pltpu.CompilerParams(
            collective_id=5, has_side_effects=True, vmem_limit_bytes=VMEM_LIMIT
        ),
        cost_estimate=pl.CostEstimate(
            flops=16 * slots * seq * seq * HD,
            bytes_accessed=2 * tokens.size,
            transcendentals=slots * seq * seq,
        ),
        name="heads",
    )(lengths, tokens, weight, bias, cosine, sine, *shards)


def grads_kernel(
    len_ref, q_ref, k_ref, v_ref, g_ref, norm_ref, dot_ref, tok_ref, cos_ref, sin_ref,
    down_ref, up_ref, out_ref, small_ref,
    join_ref, grad_ref, red_ref, sum_ref, small_sum,
    dqt, key_grads, value_grads, total, bias, x_down, x_up, x_out, s_down, s_up, s_out,
    z_down, z_up, z_out, top_down, top_up, top_out, own_down, own_up, own_out, smalls,
    x_send, x_recv, z_send, z_recv, top_recv, small_send, small_recv, *, n_ctx, n_x, part
):
    ctx, x, core = (lax.axis_index(n) for n in GROUP)
    me = (ctx * n_x + x) * 2 + core
    peers = group_peers(n_ctx, n_x)
    greet([at_device(ctx=z, x=a, core=c) for z, a, c in peers])
    side = at_device(x=1 - x)
    arrays = (
        (down_ref, x_down, s_down, z_down, top_down, own_down),
        (up_ref, x_up, s_up, z_up, top_up, own_up),
        (out_ref, x_out, s_out, z_out, top_out, own_out),
    )

    def remote(source, target_ref, send_sem, recv_sem, target):
        return pltpu.make_async_remote_copy(
            source, target_ref, send_sem, recv_sem, device_id=target, device_id_type=MESH)

    orders = [
        sorted(range(n_ctx), key=lambda p, z=z: (p == z, -abs(p - z), min(p, n_ctx - 1 - p))) for z in range(n_ctx)
    ]
    places = [
        sum(jnp.where(ctx == z, orders[z][j], 0) for z in range(n_ctx)) for j in range(n_ctx)
    ]
    above = at_device(ctx=lax.rem(ctx + 1, n_ctx))
    below = at_device(ctx=lax.rem(ctx + n_ctx - 1, n_ctx))
    first = [
        [
            remote(
                ref.at[places[j] * n_x + 1 - x], x_in.at[j], x_send.at[i, j], x_recv.at[i, j], side)
            for i, (ref, x_in, _, _, _, _) in enumerate(arrays)
        ]
        for j in range(n_ctx)
    ]

    def hop(j, i, target, last=False):
        _, _, s_low, z_in, top, _ = arrays[i]
        p = places[j]
        return remote(
            s_low.at[min(j, n_ctx - 2)], top if last else z_in.at[p], z_send.at[i, min(j, n_ctx - 2)],
            top_recv.at[i] if last else z_recv.at[i, p], target)

    pushes = []
    for k, (z, a, c) in enumerate(peers):
        them = (z * n_x + a) * 2 + c
        pushes.append(remote(
            small_ref.at[them], smalls.at[me], small_send.at[k], small_recv.at[me],
            at_device(ctx=z, x=a, core=c)))
    for copies in first:
        for copy in copies:
            copy.start()
    for copy in pushes:
        copy.start()
    smalls[me] = small_ref[me]

    def stage(j):
        p = places[j]
        going_up = p > ctx
        for i, (ref, x_in, s_low, z_in, _, own) in enumerate(arrays):
            first[j][i].wait_recv()
            own[...] = ref[p * n_x + x].astype(F32) + x_in[j].astype(F32)
            if j == n_ctx - 1:
                continue

            @pl.when((going_up & (ctx > 0)) | ((p < ctx) & (ctx < n_ctx - 1)))
            def _():
                hop(j, i, above).wait_recv()
                own[...] += z_in[p].astype(F32)

            s_low[j] = own[...].astype(BF16)

            @pl.when(going_up)
            def _():
                hop(j, i, above).start()

            @pl.when(p < ctx - 1)
            def _():
                hop(j, i, below).start()

            @pl.when(p == ctx - 1)
            def _():
                hop(j, i, below, last=True).start()

    slots, seq, _ = q_ref.shape
    total[...] = jnp.zeros_like(total)
    bias[...] = jnp.zeros_like(bias)

    def attention(s, between):
        length = len_ref[s]
        dqt[...] = jnp.zeros_like(dqt)

        @pl.loop(0, seq // KB)
        def _(j):
            start = pl.multiple_of(j * KB, KB)
            key_block = k_ref[s, pl.ds(start, KB), :]
            value_block = v_ref[s, pl.ds(start, KB), :]
            turned = jnp.transpose(key_block.astype(F32)).astype(BF16)
            ids = start + lax.broadcasted_iota(jnp.int32, (KB, 1), 0)
            shift = jnp.where(ids < length, 0.0, NEG_FILL)
            for at_step, number in between:
                @pl.when(j == at_step)
                def _():
                    stage(number)

            def step(i, state):
                key_grad, value_grad = state
                at = pl.multiple_of(i * QB, QB)
                queries = q_ref[s, pl.ds(at, QB), :]
                grads = g_ref[s, pl.ds(at, QB), :]
                scores = contract(key_block, queries, 1, 1) + shift
                probs = jnp.exp(scores - norm_ref[s, :, pl.ds(at, QB)])
                grad_probs = contract(value_block, grads, 1, 1)
                grad_scores = (probs * (grad_probs - dot_ref[s, :, pl.ds(at, QB)])).astype(BF16)
                value_grad = value_grad + mm(probs.astype(BF16), grads)
                key_grad = key_grad + mm(grad_scores, queries)
                dqt[:, pl.ds(at, QB)] += mm(turned, grad_scores)
                return key_grad, value_grad

            zero = jnp.zeros((KB, HD), F32)
            key_grad, value_grad = lax.fori_loop(0, seq // QB, step, (zero, zero))
            key_grads[pl.ds(start, KB), :] = key_grad
            value_grads[pl.ds(start, KB), :] = value_grad

    def join(s):
        @pl.loop(0, seq // QB)
        def _(i):
            at = pl.multiple_of(i * QB, QB)
            rows = pl.ds(at, QB)
            query_grad = jnp.transpose(dqt[:, rows]) * HD ** (-0.5)
            pair = jnp.concatenate([query_grad, key_grads[rows, :]], axis=1)
            turned = turn(pair, cos_ref[rows, :], -sin_ref[rows, :])
            joined = jnp.concatenate([turned, value_grads[rows, :]], axis=1).astype(BF16)
            chips = QB // (2 * part)
            for chip in range(chips):
                for owner in range(2):
                    near = (2 * chip + owner) * part
                    upper = joined[near : near + part // 2]
                    lower = joined[near + part // 2 : near + part]
                    join_ref[i * chips + chip, owner, s] = jnp.concatenate([upper, lower], axis=1)
            tokens = tok_ref[pl.ds(pl.multiple_of(s * seq + at, QB), QB), :]
            total[...] += contract(joined, tokens, 0, 0)
            bias[...] += jnp.sum(joined.astype(F32), axis=0, keepdims=True)

    for s in range(slots):
        attention(s, [(1, 1)] if s == 1 else [])
        stage(0 if s == 0 else 2)
        join(s)
    turned_total = jnp.transpose(total[...])
    shard = turned_total.shape[0] // grad_ref.shape[0]
    extra = jnp.broadcast_to(bias[...], (grad_ref.shape[1] - shard, bias.shape[1]))
    for d in range(grad_ref.shape[0]):
        grad_ref[d, :shard] = turned_total[d * shard : (d + 1) * shard].astype(BF16)
        grad_ref[d, shard:] = extra.astype(BF16)
    for j in range(slots + 1, n_ctx):
        stage(j)
    for z, a, c in peers:
        them = (z * n_x + a) * 2 + c
        remote(
            small_ref.at[them], smalls.at[them], small_send.at[0], small_recv.at[them], side
        ).wait_recv()
    small_sum[...] = jnp.sum(smalls[...].astype(F32), axis=0).astype(BF16)
    for i, (_, _, _, z_in, top, own) in enumerate(arrays):
        @pl.when(ctx > 0)
        def _():
            hop(n_ctx - 1, i, above).wait_recv()
            own[...] += z_in[ctx].astype(F32)

        @pl.when(ctx < n_ctx - 1)
        def _():
            hop(0, i, below, last=True).wait_recv()
            own[...] += top[...].astype(F32)

    rows = own_down.shape[0]
    red_ref[:rows] = own_down[...].astype(BF16)
    red_ref[rows:] = own_up[...].astype(BF16)
    sum_ref[...] = own_out[...].astype(BF16)
    for copies in first + [pushes]:
        for copy in copies:
            copy.wait_send()
    for j in range(n_ctx - 1):
        for i in range(len(arrays)):
            hop(j, i, above).wait_send()


def grads(lengths, queries, keys, values, grad_heads, norms, dots, tokens, cosine, sine,
          down, up, out, small, part):
    n_ctx, n_x = lax.axis_size("ctx"), lax.axis_size("x")
    n = 2 * n_ctx * n_x
    slots, seq, _ = queries.shape
    width = tokens.shape[1]
    shard = width // n
    cols = 3 * HD
    vmem = pl.BlockSpec(memory_space=pltpu.VMEM)
    dma = pltpu.SemaphoreType.DMA
    parts = (down, up, out)

    def low(*dims):
        return jax.ShapeDtypeStruct(dims, BF16)

    return pl.pallas_call(
        partial(grads_kernel, n_ctx=n_ctx, n_x=n_x, part=part),
        in_specs=[pl.BlockSpec(memory_space=pltpu.SMEM)] + [vmem] * 13,
        out_specs=[vmem] * 5,
        out_shape=[
            low(seq // (2 * part), 2, slots, part // 2, 2 * cols),
            low(n, shard + 16, cols),
            low(down.shape[1] + up.shape[1], width),
            low(*out.shape[1:]),
            low(*small.shape[1:]),
        ],
        scratch_shapes=[
            pltpu.VMEM((HD, seq), F32),
            pltpu.VMEM((seq, HD), F32),
            pltpu.VMEM((seq, HD), F32),
            pltpu.VMEM((cols, width), F32),
            pltpu.VMEM((1, cols), F32),
        ]
        + [pltpu.VMEM((n_ctx,) + t.shape[1:], BF16) for t in parts]
        + [pltpu.VMEM((n_ctx - 1,) + t.shape[1:], BF16) for t in parts]
        + [pltpu.VMEM((n_ctx,) + t.shape[1:], BF16) for t in parts]
        + [pltpu.VMEM(t.shape[1:], BF16) for t in parts]
        + [pltpu.VMEM(t.shape[1:], F32) for t in parts]
        + [
            pltpu.VMEM(small.shape, BF16),
            dma((3, n_ctx)),
            dma((3, n_ctx)),
            dma((3, n_ctx - 1)),
            dma((3, n_ctx)),
            dma((3,)),
            dma((n - 1,)),
            dma((n,)),
        ],
        compiler_params=pltpu.CompilerParams(
            collective_id=6, has_side_effects=True, vmem_limit_bytes=VMEM_LIMIT
        ),
        cost_estimate=pl.CostEstimate(
            flops=40 * slots * seq * seq * HD,
            bytes_accessed=4 * tokens.size,
            transcendentals=slots * seq * seq,
        ),
        name="grads",
    )(lengths, queries, keys, values, grad_heads, norms, dots, tokens, cosine, sine,
      down, up, out, small)


def norm_forward(values, gain, shift):
    center = values - jnp.mean(values, axis=-1, keepdims=True)
    spread = jnp.mean(center * center, axis=-1, keepdims=True)
    root = lax.rsqrt(spread + LN_EPS)
    unit = center * root
    return unit * gain + shift, unit, root


def norm_backward(grad, unit, root, gain):
    scaled = grad * gain
    inner = scaled - jnp.mean(scaled, axis=-1, keepdims=True)
    inner = inner - unit * jnp.mean(scaled * unit, axis=-1, keepdims=True)
    return root * inner, jnp.sum(grad * unit, axis=0), jnp.sum(grad, axis=0)


def gelu_pair(values):
    half = 0.5 + 0.5 * lax.erf(values * 0.7071067811865476)
    bell = jnp.exp(-0.5 * values * values) * 0.3989422804014327
    return values * half, half + values * bell


def rope_rows(positions):
    halfway = HD // 2
    ladder = jnp.arange(halfway, dtype=F32) * (2.0 / HD)
    frequency = jnp.power(jnp.float32(10000.0), -ladder)
    angles = positions[:, None] * frequency[None, :]
    return jnp.cos(angles), jnp.sin(angles)


def layer_kernel(
    sent_ref, tok_ref, wo_ref, up_ref, down_ref, vec_ref, full_ref, lane_ref,
    merged_ref, out_ref, one_ref, gm_ref, att_ref, vecs_ref, act_out, hid_out, gdn_out, gup_out, lanes_out,
    first, first_in, hid, act, slope, gdn, gup, hidden, unit_one, two,
    roots, near, near_in, far, far_in, low_out, low_in, send_sem, recv_sem, out_sem,
    lane_send, lane_recv, heads_in, push_send, push_recv, *, n_ctx, n_x
):
    core, slot = lax.axis_index("core"), lax.axis_index("slot")
    twin, across = at_device(core=1 - core), at_device(slot=1 - slot)
    ctx, x = lax.axis_index("ctx"), lax.axis_index("x")
    chip = ctx * n_x + x
    others = [
        (lax.rem(ctx + o // n_x, n_ctx), lax.rem(x + o % n_x, n_x)) for o in range(1, n_ctx * n_x)
    ]
    greet([twin, across] + [at_device(ctx=z, x=a) for z, a in others])
    pushes = [
        pltpu.make_async_remote_copy(
            sent_ref.at[z * n_x + a], heads_in.at[chip], push_send.at[o], push_recv.at[chip],
            device_id=at_device(ctx=z, x=a), device_id_type=MESH)
        for o, (z, a) in enumerate(others)
    ]
    for push in pushes:
        push.start()
    heads_in[chip] = sent_ref[chip]
    begin_lane, relay_lane, end_lane = lane_gather(
        lane_ref, lanes_out, lane_send, lane_recv, out_sem.at[4], n_ctx, n_x)
    begin_lane()
    rows, width = tok_ref.shape
    half = rows // 2
    tile = 256
    count = [0]
    started = []

    def launch(source, target_ref, target):
        i = count[0]
        count[0] += 1
        copy = pltpu.make_async_remote_copy(
            source, target_ref, send_sem.at[i], recv_sem.at[i],
            device_id=target, device_id_type=MESH)
        copy.start()
        started.append(copy)
        return copy

    def columns(body, n=width // tile):
        @pl.loop(0, n)
        def _(t):
            body(pl.ds(pl.multiple_of(t * tile, tile), tile))

    def chunks(body, size=64):
        @pl.loop(0, rows // size)
        def _(t):
            body(pl.ds(pl.multiple_of(t * size, size), size))

    def exchange(buf, turn, stage, product):
        halves = [
            launch(buf.at[pl.ds(h * half, half)], buf.at[pl.ds((2 + h) * rows, half)], across)
            for h in range(2)
        ]
        to_twin = launch(buf.at[pl.ds(0, rows)], buf.at[pl.ds(rows, rows)], twin)
        near_buf, far_buf = near.at[turn], far.at[turn]
        to_twin.wait_recv()
        stage(0, 2 * rows)
        product(0, 2 * rows, near_buf, 0)
        near_copy = launch(
            near_buf.at[pl.ds(rows, rows)], near_in.at[turn], twin)
        back = []
        for h in range(2):
            at = (2 + h) * rows
            halves[h].wait_recv()
            launch(
                buf.at[pl.ds(at, half)], buf.at[pl.ds(at + half, half)], twin).wait_recv()
            stage(at, rows)
            product(at, rows, far_buf, h * rows)
            i = 2 * turn + h
            launch(
                far_buf.at[pl.ds(h * rows + half, half)], far_in.at[i], twin).wait_recv()
            low_out[i] = (far_buf[pl.ds(h * rows, half), :] + far_in[i]).astype(BF16)
            back.append(launch(low_out.at[i], low_in.at[i], across))
        return near_copy, back

    for o, (z, a) in enumerate(others):
        source = z * n_x + a
        pltpu.make_async_remote_copy(
            sent_ref.at[source], heads_in.at[source], push_send.at[o], push_recv.at[source],
            device_id=twin, device_id_type=MESH).wait_recv()
    _, owners, slots, packed, pair_width = heads_in.shape
    for k in range(0, n_ctx * n_x, 2):
        for h in range(owners):
            for t in range(slots):
                left, right = heads_in[k, h, t], heads_in[k + 1, h, t]
                for piece in range(2):
                    at = ((h * slots + t) * 2 + piece) * packed
                    of = slice(piece * HD, (piece + 1) * HD)
                    merged_ref[at : at + packed, k * HD : (k + 2) * HD] = jnp.concatenate(
                        [left[:, of], right[:, of]], axis=1)

    def out_product(cols):
        first[:, cols] = mm(merged_ref[...], wo_ref[:, cols])

    columns(out_product)
    launch(first.at[pl.ds(rows, rows)], first_in, twin).wait_recv()

    def norm_one(at):
        values = tok_ref[at, :].astype(F32) + first[at, :] + first_in[at, :] + vec_ref[0:1, :]
        normed, unit, root = norm_forward(values, vec_ref[1:2, :], vec_ref[2:3, :])
        hidden[at, :] = normed
        unit_one[at, :] = unit
        roots[0, at, :] = jnp.broadcast_to(root, (root.shape[0], 128))
        hid[at, :] = normed.astype(BF16)

    chunks(norm_one)

    def up_stage(start, size):
        def body(cols):
            values = mm(hid[start : start + size, :], up_ref[:, cols]) + vec_ref[3:4, cols]
            active, bend = gelu_pair(values)
            act[start : start + size, cols] = active.astype(BF16)
            slope[start : start + size, cols] = bend

        columns(body)

    def down_product(start, size, target, at):
        def body(cols):
            target[at : at + size, cols] = mm(act[start : start + size, :], down_ref[:, cols])

        columns(body)

    near_copy, back = exchange(hid, 0, up_stage, down_product)
    relay_lane(1)
    out_copies = [
        pltpu.make_async_copy(hid, hid_out, out_sem.at[0]),
        pltpu.make_async_copy(act, act_out, out_sem.at[1]),
    ]
    for copy in out_copies:
        copy.start()
    vecs_ref[...] = jnp.zeros_like(vecs_ref)
    near_copy.wait_recv()

    def norm_two(at, h, local):
        downward = near[0, at, :] + near_in[0, at, :] + low_in[h, local, :].astype(F32)
        values = hidden[at, :] + downward + vec_ref[4:5, :]
        normed, unit, root = norm_forward(values, vec_ref[5:6, :], vec_ref[6:7, :])
        out_ref[at, :] = normed.astype(BF16)
        grad, gain, shift = norm_backward(full_ref[at, :], unit, root, vec_ref[5:6, :])
        two[at, :] = grad
        low = grad.astype(BF16)
        gdn[at, :] = low
        vecs_ref[5:6, :] += gain[None]
        vecs_ref[6:7, :] += shift[None]
        vecs_ref[4:5, :] += jnp.sum(low.astype(F32), axis=0, keepdims=True)

    def by_half(body, h, size=64):
        @pl.loop(0, half // size)
        def _(t):
            local = pl.multiple_of(t * size, size)
            body(pl.ds(h * half + local, size), h, pl.ds(local, size))

    for h in range(2):
        back[h].wait_recv()
        by_half(norm_two, h)

    def back_stage(start, size):
        def body(cols):
            grads = contract(gdn[start : start + size, :], down_ref[cols, :], 1, 1)
            low = (grads * slope[start : start + size, cols]).astype(BF16)
            gup[start : start + size, cols] = low
            vecs_ref[3:4, cols] += jnp.sum(low.astype(F32), axis=0, keepdims=True)

        columns(body)

    def back_product(start, size, target, at):
        def body(cols):
            target[at : at + size, cols] = contract(
                gup[start : start + size, :], up_ref[cols, :], 1, 1)

        columns(body)

    relay_lane(2)
    near_copy, back = exchange(gdn, 1, back_stage, back_product)
    for r in range(3, n_ctx):
        relay_lane(r)
    late_copies = [
        pltpu.make_async_copy(gdn, gdn_out, out_sem.at[2]),
        pltpu.make_async_copy(gup, gup_out, out_sem.at[3]),
    ]
    for copy in late_copies:
        copy.start()
    near_copy.wait_recv()

    def norm_back(at, h, local):
        grad = near[1, at, :] + near_in[1, at, :] + low_in[2 + h, local, :].astype(F32)
        grad = grad + two[at, :]
        root = roots[0, at, 0:1]
        one, gain, shift = norm_backward(grad, unit_one[at, :], root, vec_ref[1:2, :])
        one_ref[at, :] = one
        low = one.astype(BF16)
        att_ref[at, :] = low
        vecs_ref[1:2, :] += gain[None]
        vecs_ref[2:3, :] += shift[None]
        vecs_ref[0:1, :] += jnp.sum(low.astype(F32), axis=0, keepdims=True)

    for h in range(2):
        back[h].wait_recv()
        by_half(norm_back, h)
    launch(att_ref.at[pl.ds(0, rows)], att_ref.at[pl.ds(rows, rows)], twin).wait_recv()

    def merged_product(cols):
        gm_ref[:, cols] = contract(att_ref[...], wo_ref[cols, :], 1, 1).astype(BF16)

    columns(merged_product, wo_ref.shape[0] // tile)
    end_lane()
    for copy in started + pushes:
        copy.wait_send()
    for copy in out_copies + late_copies:
        copy.wait()


def layer(sent, tokens, w_out, up, down, vectors, grad_full, lane_shard):
    n_ctx, n_x = lax.axis_size("ctx"), lax.axis_size("x")
    chips = n_ctx * n_x
    rows, width = tokens.shape
    hidden = up.shape[1]
    lane = w_out.shape[0]
    vmem = pl.BlockSpec(memory_space=pltpu.VMEM)
    anywhere = pl.BlockSpec(memory_space=pl.ANY)
    dma = pltpu.SemaphoreType.DMA

    def shape(*dims, dtype=BF16):
        return jax.ShapeDtypeStruct(dims, dtype)

    def wide(*dims):
        return pltpu.VMEM(dims, F32)

    def low(*dims):
        return pltpu.VMEM(dims, BF16)

    return pl.pallas_call(
        partial(layer_kernel, n_ctx=n_ctx, n_x=n_x),
        in_specs=[vmem] * 8,
        out_specs=[vmem] * 6 + [anywhere] * 5,
        out_shape=[
            shape(2 * rows, lane),
            shape(rows, width),
            shape(rows, width, dtype=F32),
            shape(2 * rows, lane),
            shape(2 * rows, width),
            shape(8, width, dtype=F32),
            shape(4 * rows, hidden),
            shape(4 * rows, width),
            shape(4 * rows, width),
            shape(4 * rows, hidden),
            shape(chips, *lane_shard.shape),
        ],
        scratch_shapes=[
            wide(2 * rows, width),
            wide(rows, width),
            low(4 * rows, width),
            low(4 * rows, hidden),
            wide(4 * rows, hidden),
            low(4 * rows, width),
            low(4 * rows, hidden),
            wide(rows, width),
            wide(rows, width),
            wide(rows, width),
            wide(1, rows, 128),
            wide(2, 2 * rows, width),
            wide(2, rows, width),
            wide(2, 2 * rows, width),
            wide(4, rows // 2, width),
            low(4, rows // 2, width),
            low(4, rows // 2, width),
            dma((24,)),
            dma((24,)),
            dma((5,)),
            dma((3, chips)),
            dma((chips,)),
            low(*sent.shape),
            dma((chips - 1,)),
            dma((chips,)),
        ],
        compiler_params=pltpu.CompilerParams(
            collective_id=3, has_side_effects=True, vmem_limit_bytes=VMEM_LIMIT
        ),
        cost_estimate=pl.CostEstimate(
            flops=16 * rows * width * hidden, bytes_accessed=16 * rows * width, transcendentals=0
        ),
        name="layer",
    )(sent, tokens, w_out, up, down, vectors, grad_full, lane_shard)


def head_device(
    tokens,
    lengths,
    w_qkv,
    b_qkv,
    w_out,
    b_out,
    ln1_gain,
    ln1_bias,
    w_up,
    b_up,
    w_down,
    b_down,
    ln2_gain,
    ln2_bias,
    w_proj,
    cot_out,
    cot_emb,
):
    n_lane = lax.axis_size("ctx") * lax.axis_size("x")
    n_group = 2 * n_lane
    core = lax.axis_index("core")
    slot = lax.axis_index("slot")
    chip = lax.axis_index("ctx") * lax.axis_size("x") + lax.axis_index("x")
    me = 2 * chip + core
    slots, part, width = tokens.shape
    seq = part * n_group
    rows = slots * part
    shard = width // n_group
    ff_shard = w_down.shape[0]
    ff_half = ff_shard // 2
    proj = w_proj.shape[1]
    head_cols = 3 * HD

    small = jnp.concatenate(
        [b_qkv, b_out, ln1_gain, ln1_bias, b_up, b_down, ln2_gain, ln2_bias]
    )
    small_at = [0]
    for piece in (b_qkv, b_out, ln1_gain, ln1_bias, b_up, b_down, ln2_gain, ln2_bias):
        small_at.append(small_at[-1] + piece.shape[0])
    small_rows = -(-small.shape[0] // proj)
    small_rows = -(-small_rows // 16) * 16
    small = jnp.pad(small, (0, small_rows * proj - small.shape[0])).reshape(small_rows, proj)
    def two_lanes(mine, theirs):
        low_first = jnp.stack([mine, theirs], axis=0)
        high_first = jnp.stack([theirs, mine], axis=0)
        return jnp.where(core == 0, low_first, high_first)

    up_split = w_up.reshape(shard, n_lane, 2, 2, ff_half)
    up_mine = pick(up_split, core, 2)
    up_theirs = swap_core(pick(up_split, 1 - core, 2))
    up_chip = two_lanes(pick(up_mine, slot, 2), pick(up_theirs, slot, 2))
    down_split = w_down.reshape(2, ff_half, width)

    by_head = w_qkv.reshape(shard, 3, n_group, HD).transpose(2, 0, 1, 3)
    all_tokens, my_head, packed = gather_start(
        tokens,
        by_head.reshape(n_group, shard, head_cols),
        jnp.concatenate([w_proj, small], axis=0),
    )
    proj_full = packed[:, :shard].reshape(width, proj)
    smalls = packed[:, shard:].reshape(n_group, small_rows * proj).astype(F32)
    qkv_bias, out_bias, gain_one, shift_one, up_bias, down_bias, gain_two, shift_two = (
        smalls[:, a:b].reshape(-1) for a, b in zip(small_at[:-1], small_at[1:])
    )

    head_weight = my_head.reshape(width, head_cols)
    all_tokens = all_tokens.reshape(slots * seq, width)
    head_bias = pick(qkv_bias.reshape(1, 3, n_group, HD), me, 2).reshape(1, head_cols)
    cosine, sine = rope_rows(jnp.arange(seq, dtype=jnp.int32).astype(F32))
    cos_wide = jnp.tile(cosine, (1, 4))
    sin_wide = jnp.tile(sine, (1, 4))
    queries, keys, values, mixture, send, norms, out_lane, up, down = heads(
        lengths,
        all_tokens,
        head_weight,
        head_bias,
        cos_wide,
        sin_wide,
        part,
        w_out,
        up_chip.reshape(2 * shard, n_lane * ff_half),
        pick(down_split, slot, 0),
    )
    out_lane, up, down = (t.reshape(-1, t.shape[2]) for t in (out_lane, up, down))
    bias_lane = pick(up_bias.reshape(n_lane, 2, 2, ff_half), core, 1)
    up_bias_own = pick(bias_lane, slot, 1).reshape(-1)

    qkv_split = w_qkv.reshape(shard, 3, n_lane, 2, HD)
    qkv_mine = pick(qkv_split, core, 3)
    qkv_theirs = swap_core(pick(qkv_split, 1 - core, 3))
    qkv_chip = two_lanes(qkv_mine, qkv_theirs).transpose(3, 0, 1, 2, 4)
    qkv_chip = qkv_chip.reshape(n_lane, 2 * shard, head_cols)

    place = me * part + jnp.arange(part, dtype=jnp.int32)
    live = (place[None, :] < lengths[:, None]).reshape(rows, 1)
    grad_out = jnp.where(live, cot_out.reshape(rows, width).astype(F32), 0.0)
    grad_emb = jnp.where(live, cot_emb.reshape(rows, proj), 0)
    grad_full = grad_out + contract(grad_emb, proj_full, 1, 1)
    vectors = jnp.stack(
        [out_bias, gain_one, shift_one, up_bias_own, down_bias, gain_two, shift_two, shift_two]
    )
    (
        merged,
        out_low,
        grad_one,
        grad_merged,
        grad_att,
        vector_grads,
        active,
        hidden_low,
        grad_down,
        grad_up,
        qkv_lane,
    ) = layer(
        send, tokens.reshape(rows, width), out_lane, up, down, vectors, grad_full, qkv_chip
    )
    d_down = contract(active, grad_down, 0, 0).astype(BF16)
    d_up = contract(hidden_low, grad_up, 0, 0).astype(BF16)
    embeds = mm(out_low, proj_full).astype(BF16)
    d_proj = contract(out_low, grad_emb, 0, 0)
    (
        d_out_bias,
        d_gain_one,
        d_shift_one,
        up_bias_own_grad,
        d_down_bias,
        d_gain_two,
        d_shift_two,
    ) = (vector_grads[i] for i in range(7))
    grad_merged = grad_merged.reshape(2, slots, part, n_lane, HD).transpose(3, 0, 1, 2, 4)
    grad_heads = lax.all_to_all(grad_merged, LANE, 0, 0, tiled=True)

    def core_order(value):
        return jnp.where(core == 0, value, jnp.flip(value, axis=1))

    grad_heads = core_order(grad_heads).transpose(2, 0, 1, 3, 4).reshape(slots, seq, HD)

    d_out = contract(merged, grad_att, 0, 0).astype(BF16)

    spread = (
        (jnp.arange(2) == core)[:, None, None] & (jnp.arange(2) == slot)[None, :, None]
    ).astype(F32)
    up_bias_grad = up_bias_own_grad.reshape(n_lane, 1, 1, ff_half) * spread[None]
    vectors = (
        d_out_bias,
        d_gain_one,
        d_shift_one,
        up_bias_grad.reshape(-1),
        d_down_bias,
        d_gain_two,
        d_shift_two,
    )
    small_grad = jnp.concatenate([v.reshape(n_group, -1) for v in vectors], axis=1)
    small_cols = small_grad.shape[1]
    vec_rows = -(-small_cols // proj)
    vec_rows = -(-(shard + vec_rows) // 16) * 16 - shard
    small_grad = jnp.pad(small_grad, ((0, 0), (0, vec_rows * proj - small_cols)))
    small_grad = jnp.concatenate(
        [d_proj.reshape(n_group, shard, proj), small_grad.reshape(n_group, vec_rows, proj)], axis=1
    )
    row_dots = jnp.sum(grad_heads.astype(F32) * mixture, axis=-1).reshape(slots, 1, seq)
    joined, d_qkv, reduced, out_sum, small_sum = grads(
        lengths,
        queries,
        keys,
        values,
        grad_heads,
        norms,
        row_dots,
        all_tokens,
        cos_wide,
        sin_wide,
        d_down.reshape(n_lane, 2 * shard, width),
        d_up.reshape(n_lane, 2 * shard, width),
        d_out.reshape(n_lane, shard, width),
        small_grad.astype(BF16),
        part,
    )
    grad_w_down, grad_w_up, grad_w_out, small_sum, grad_w_qkv, bias_rows, input_grad = finish_grads(
        out_sum,
        small_sum,
        d_qkv,
        reduced,
        joined,
        qkv_lane,
        grad_one,
    )
    grad_w_proj = small_sum[:shard]
    vec_sum = small_sum[shard:].reshape(-1)
    vec_outs = []
    at = 0
    for v in vectors:
        size = v.size // n_group
        vec_outs.append(vec_sum[at : at + size])
        at += size
    (
        grad_b_out,
        grad_gain_one,
        grad_shift_one,
        grad_b_up,
        grad_b_down,
        grad_gain_two,
        grad_shift_two,
    ) = vec_outs

    qkv_bias_grad = bias_rows.reshape(n_group, 3, HD).transpose(1, 0, 2).reshape(-1)
    grad_b_qkv = lax.dynamic_slice(qkv_bias_grad, (me * b_qkv.shape[0],), (b_qkv.shape[0],))

    return (
        out_low.reshape(slots, part, width),
        embeds.reshape(slots, part, proj),
        input_grad.reshape(slots, part, width),
        grad_w_qkv,
        grad_b_qkv,
        grad_w_out,
        grad_b_out,
        grad_gain_one,
        grad_shift_one,
        grad_w_up,
        grad_b_up,
        grad_w_down,
        grad_b_down,
        grad_gain_two,
        grad_shift_two,
        grad_w_proj,
    )


def layer_norm(hidden, gain, shift):
    center = hidden - jnp.mean(hidden, axis=-1, keepdims=True)
    spread = jnp.mean(center * center, axis=-1, keepdims=True)
    return center * lax.rsqrt(spread + LN_EPS) * gain + shift


def rope_tables(positions, head_width):
    halfway = head_width // 2
    ladder = jnp.arange(halfway, dtype=jnp.float32) * (2.0 / head_width)
    frequency = jnp.power(jnp.float32(10000.0), -ladder)
    angles = positions[:, None] * frequency[None, :]
    return (jnp.cos(angles)[:, None, :], jnp.sin(angles)[:, None, :])


def rotate(values, cosine, sine_part):
    halfway = values.shape[-1] // 2
    first_half = values[..., :halfway]
    second_half = values[..., halfway:]
    return jnp.concatenate(
        [
            first_half * cosine - second_half * sine_part,
            second_half * cosine + first_half * sine_part,
        ],
        axis=-1,
    )


def block_scores(query_block, key_block, key_start, length, scale):
    scores = (
        jnp.einsum("qhd,khd->hqk", query_block, key_block, preferred_element_type=jnp.float32)
        * scale
    )
    key_ids = key_start + jnp.arange(key_block.shape[0], dtype=jnp.int32)
    return jnp.where((key_ids < length)[None, None, :], scores, NEG_FILL)


def per_device(
    tokens,
    lengths,
    w_qkv,
    b_qkv,
    w_out,
    b_out,
    ln1_gain,
    ln1_bias,
    w_up,
    b_up,
    w_down,
    b_down,
    ln2_gain,
    ln2_bias,
    w_proj,
    cot_out,
    cot_emb,
):
    n_fsdp = lax.axis_size("fsdp")
    n_ctx = lax.axis_size("ctx")
    ctx_at = lax.axis_index("ctx")
    fsdp_at = lax.axis_index("fsdp")
    groups, tok_slot, width = tokens.shape
    heads_here = H // n_fsdp
    lane_width = heads_here * HD
    span_rows = tok_slot * n_fsdp
    key_count = span_rows * n_ctx
    row_count = groups * tok_slot
    scale = HD ** (-0.5)
    query_rows = min(512, span_rows)
    key_rows = min(2048, key_count // 4)
    query_blocks = span_rows // query_rows
    key_blocks = key_count // key_rows
    key_starts = jnp.arange(key_blocks, dtype=jnp.int32) * key_rows
    qkv_full, qkv_bias, out_full, out_bias, gain_one, shift_one = (
        lax.all_gather(w_qkv, ("ctx", "fsdp"), axis=0, tiled=True),
        lax.all_gather(b_qkv, ("ctx", "fsdp"), axis=0, tiled=True),
        lax.all_gather(w_out, ("ctx", "fsdp"), axis=0, tiled=True),
        lax.all_gather(b_out, ("ctx", "fsdp"), axis=0, tiled=True),
        lax.all_gather(ln1_gain, ("ctx", "fsdp"), axis=0, tiled=True),
        lax.all_gather(ln1_bias, ("ctx", "fsdp"), axis=0, tiled=True),
    )
    token_pos = (ctx_at * n_fsdp + fsdp_at) * tok_slot + jnp.arange(tok_slot, dtype=jnp.int32)
    live_rows = (token_pos[None, :] < lengths[:, None]).reshape(row_count, 1)
    flat_tokens = tokens.reshape(row_count, width)
    joined = jnp.dot(flat_tokens, qkv_full, preferred_element_type=jnp.float32) + qkv_bias.astype(
        jnp.float32
    )
    cosine, sine_part = rope_tables(token_pos.astype(jnp.float32), HD)
    split_heads = joined.reshape(groups, tok_slot, 3, H, HD)
    rotated_query = rotate(split_heads[:, :, 0], cosine, sine_part)
    rotated_key = rotate(split_heads[:, :, 1], cosine, sine_part)
    packed = (
        jnp.stack([rotated_query, rotated_key, split_heads[:, :, 2]], axis=2)
        .astype(jnp.bfloat16)
        .reshape(groups, tok_slot, 3, n_fsdp, lane_width)
    )
    by_heads = lax.all_to_all(packed, "fsdp", split_axis=3, concat_axis=1, tiled=True)
    queries = by_heads[:, :, 0, 0]
    local_keys = by_heads[:, :, 1, 0]
    local_values = by_heads[:, :, 2, 0]
    all_keys, all_values = (
        lax.all_gather(local_keys, "ctx", axis=1, tiled=True),
        lax.all_gather(local_values, "ctx", axis=1, tiled=True),
    )

    def attend_slot(slot_item):
        slot_queries, slot_keys, slot_values, length = slot_item
        query_split = slot_queries.reshape(query_blocks, query_rows, heads_here, HD)
        key_split = slot_keys.reshape(key_blocks, key_rows, heads_here, HD)
        value_split = slot_values.reshape(key_blocks, key_rows, heads_here, HD)

        def per_query(query_block):

            def row_stats(state_pair, key_item):
                highest, running_sum = state_pair
                scores = block_scores(query_block, key_item[0], key_item[1], length, scale)
                new_high = jnp.maximum(highest, jnp.max(scores, axis=-1))
                running_sum = running_sum * jnp.exp(highest - new_high) + jnp.sum(
                    jnp.exp(scores - new_high[..., None]), axis=-1
                )
                return ((new_high, running_sum), None)

            start_state = (
                jnp.full((heads_here, query_rows), NEG_FILL, jnp.float32),
                jnp.zeros((heads_here, query_rows), jnp.float32),
            )
            highest, running_sum = lax.scan(row_stats, start_state, (key_split, key_starts))[0]
            log_norm = highest + jnp.log(running_sum)

            def weigh_values(accumulated, key_item):
                scores = block_scores(query_block, key_item[0], key_item[2], length, scale)
                weights = jnp.exp(scores - log_norm[..., None]).astype(jnp.bfloat16)
                return (
                    accumulated
                    + jnp.einsum(
                        "hqk,khd->qhd", weights, key_item[1], preferred_element_type=jnp.float32
                    ),
                    None,
                )

            mixture = lax.scan(
                weigh_values,
                jnp.zeros((query_rows, heads_here, HD), jnp.float32),
                (key_split, value_split, key_starts),
            )[0]
            return (mixture, log_norm)

        mixture, log_norm = lax.map(per_query, query_split)
        return (mixture.reshape(span_rows, lane_width), log_norm)

    mixture, log_norms = lax.map(attend_slot, (queries, all_keys, all_values, lengths))
    merged = lax.all_to_all(
        mixture.astype(jnp.bfloat16).reshape(groups, span_rows, 1, lane_width),
        "fsdp",
        split_axis=1,
        concat_axis=2,
        tiled=True,
    ).reshape(row_count, width)
    attended = jnp.dot(merged, out_full, preferred_element_type=jnp.float32) + out_bias.astype(
        jnp.float32
    )
    hidden_one, pull_one = jax.vjp(
        layer_norm,
        flat_tokens.astype(jnp.float32) + attended,
        gain_one.astype(jnp.float32),
        shift_one.astype(jnp.float32),
    )
    hidden_low = hidden_one.astype(jnp.bfloat16)
    up_full, up_bias, down_full, down_bias, gain_two, shift_two, proj_full = (
        lax.all_gather(w_up, ("ctx", "fsdp"), axis=0, tiled=True),
        lax.all_gather(b_up, ("ctx", "fsdp"), axis=0, tiled=True),
        lax.all_gather(w_down, ("ctx", "fsdp"), axis=0, tiled=True),
        lax.all_gather(b_down, ("ctx", "fsdp"), axis=0, tiled=True),
        lax.all_gather(ln2_gain, ("ctx", "fsdp"), axis=0, tiled=True),
        lax.all_gather(ln2_bias, ("ctx", "fsdp"), axis=0, tiled=True),
        lax.all_gather(w_proj, ("ctx", "fsdp"), axis=0, tiled=True),
    )
    upward = jnp.dot(hidden_low, up_full, preferred_element_type=jnp.float32) + up_bias.astype(
        jnp.float32
    )
    active_full, pull_gelu = jax.vjp(partial(jax.nn.gelu, approximate=False), upward)
    active = active_full.astype(jnp.bfloat16)
    downward = jnp.dot(active, down_full, preferred_element_type=jnp.float32) + down_bias.astype(
        jnp.float32
    )
    out_full_rows, pull_two = jax.vjp(
        layer_norm,
        hidden_one + downward,
        gain_two.astype(jnp.float32),
        shift_two.astype(jnp.float32),
    )
    out_low = out_full_rows.astype(jnp.bfloat16)
    projected = jnp.dot(out_low, proj_full, preferred_element_type=jnp.float32)
    back_qkv, back_qkv_bias, back_out, back_out_bias, back_gain_one, back_shift_one = (
        lax.all_gather(w_qkv, ("ctx", "fsdp"), axis=0, tiled=True),
        lax.all_gather(b_qkv, ("ctx", "fsdp"), axis=0, tiled=True),
        lax.all_gather(w_out, ("ctx", "fsdp"), axis=0, tiled=True),
        lax.all_gather(b_out, ("ctx", "fsdp"), axis=0, tiled=True),
        lax.all_gather(ln1_gain, ("ctx", "fsdp"), axis=0, tiled=True),
        lax.all_gather(ln1_bias, ("ctx", "fsdp"), axis=0, tiled=True),
    )
    back_up, back_up_bias, back_down, back_down_bias, back_gain_two, back_shift_two, back_proj = (
        lax.all_gather(w_up, ("ctx", "fsdp"), axis=0, tiled=True),
        lax.all_gather(b_up, ("ctx", "fsdp"), axis=0, tiled=True),
        lax.all_gather(w_down, ("ctx", "fsdp"), axis=0, tiled=True),
        lax.all_gather(b_down, ("ctx", "fsdp"), axis=0, tiled=True),
        lax.all_gather(ln2_gain, ("ctx", "fsdp"), axis=0, tiled=True),
        lax.all_gather(ln2_bias, ("ctx", "fsdp"), axis=0, tiled=True),
        lax.all_gather(w_proj, ("ctx", "fsdp"), axis=0, tiled=True),
    )
    grad_out = jnp.where(live_rows, cot_out.reshape(row_count, width).astype(jnp.float32), 0.0)
    grad_emb = jnp.where(live_rows, cot_emb.reshape(row_count, -1), 0)
    d_proj = jnp.einsum("rd,rp->dp", out_low, grad_emb, preferred_element_type=jnp.float32)
    grad_full = grad_out + jnp.einsum(
        "rp,dp->rd", grad_emb, back_proj, preferred_element_type=jnp.float32
    )
    grad_two, d_gain_two, d_shift_two = pull_two(grad_full)
    grad_down = grad_two.astype(jnp.bfloat16)
    d_down = jnp.einsum("rf,rd->fd", active, grad_down, preferred_element_type=jnp.float32)
    d_down_bias = jnp.sum(grad_down.astype(jnp.float32), axis=0)
    grad_act = jnp.einsum("rd,fd->rf", grad_down, back_down, preferred_element_type=jnp.float32)
    grad_up = pull_gelu(grad_act)[0].astype(jnp.bfloat16)
    d_up = jnp.einsum("rd,rf->df", hidden_low, grad_up, preferred_element_type=jnp.float32)
    d_up_bias = jnp.sum(grad_up.astype(jnp.float32), axis=0)
    grad_hidden = grad_two + jnp.einsum(
        "rf,df->rd", grad_up, back_up, preferred_element_type=jnp.float32
    )
    grad_one, d_gain_one, d_shift_one = pull_one(grad_hidden)
    grad_att = grad_one.astype(jnp.bfloat16)
    d_out = jnp.einsum("rd,re->de", merged, grad_att, preferred_element_type=jnp.float32)
    d_out_bias = jnp.sum(grad_att.astype(jnp.float32), axis=0)
    grad_merged = jnp.einsum(
        "re,de->rd", grad_att, back_out, preferred_element_type=jnp.float32
    ).astype(jnp.bfloat16)
    grad_heads = lax.all_to_all(
        grad_merged.reshape(groups, tok_slot, n_fsdp, lane_width),
        "fsdp",
        split_axis=2,
        concat_axis=1,
        tiled=True,
    ).reshape(groups, span_rows, lane_width)

    def attend_back(slot_item):
        slot_queries, slot_keys, slot_values, grad_mix, log_norm, length = slot_item
        query_split = slot_queries.reshape(query_blocks, query_rows, heads_here, HD)
        key_split = slot_keys.reshape(key_blocks, key_rows, heads_here, HD)
        value_split = slot_values.reshape(key_blocks, key_rows, heads_here, HD)
        grad_split = grad_mix.reshape(query_blocks, query_rows, heads_here, HD)

        def value_pass(value_total, query_item):
            query_block, grad_block, norm_block = query_item

            def value_per_key(row_dot, key_item):
                key_block, value_block, key_start = key_item
                scores = block_scores(query_block, key_block, key_start, length, scale)
                probability = jnp.exp(scores - norm_block[..., None])
                grad_probs = jnp.einsum(
                    "qhd,khd->hqk", grad_block, value_block, preferred_element_type=jnp.float32
                )
                value_part = jnp.einsum(
                    "hqk,qhd->khd",
                    probability.astype(jnp.bfloat16),
                    grad_block,
                    preferred_element_type=jnp.float32,
                )
                return (row_dot + jnp.sum(probability * grad_probs, axis=-1), value_part)

            row_dot, value_parts = lax.scan(
                value_per_key,
                jnp.zeros((heads_here, query_rows), jnp.float32),
                (key_split, value_split, key_starts),
            )
            return (value_total + value_parts.reshape(key_count, heads_here, HD), row_dot)

        value_grad, row_dots = lax.scan(
            value_pass,
            jnp.zeros((key_count, heads_here, HD), jnp.float32),
            (query_split, grad_split, log_norm),
        )

        def key_pass(key_total, query_item):
            query_block, grad_block, norm_block, dot_block = query_item

            def key_per_key(query_accum, key_item):
                key_block, value_block, key_start = key_item
                scores = block_scores(query_block, key_block, key_start, length, scale)
                probability = jnp.exp(scores - norm_block[..., None])
                grad_probs = jnp.einsum(
                    "qhd,khd->hqk", grad_block, value_block, preferred_element_type=jnp.float32
                )
                grad_scores = (probability * (grad_probs - dot_block[..., None])).astype(
                    jnp.bfloat16
                )
                query_accum = query_accum + jnp.einsum(
                    "hqk,khd->qhd", grad_scores, key_block, preferred_element_type=jnp.float32
                )
                key_part = jnp.einsum(
                    "hqk,qhd->khd", grad_scores, query_block, preferred_element_type=jnp.float32
                )
                return (query_accum, key_part)

            query_grad, key_parts = lax.scan(
                key_per_key,
                jnp.zeros((query_rows, heads_here, HD), jnp.float32),
                (key_split, value_split, key_starts),
            )
            return (key_total + key_parts.reshape(key_count, heads_here, HD), query_grad)

        key_grad, query_grads = lax.scan(
            key_pass,
            jnp.zeros((key_count, heads_here, HD), jnp.float32),
            (query_split, grad_split, log_norm, row_dots),
        )
        return (
            query_grads.reshape(span_rows, lane_width) * scale,
            key_grad.reshape(key_count, lane_width) * scale,
            value_grad.reshape(key_count, lane_width),
        )

    grad_queries, key_terms, value_terms = lax.map(
        attend_back, (queries, all_keys, all_values, grad_heads, log_norms, lengths)
    )
    grad_keys, grad_values = (
        lax.psum_scatter(
            key_terms.astype(jnp.bfloat16), "ctx", scatter_dimension=1, tiled=True
        ).astype(jnp.float32),
        lax.psum_scatter(
            value_terms.astype(jnp.bfloat16), "ctx", scatter_dimension=1, tiled=True
        ).astype(jnp.float32),
    )
    head_pos = (ctx_at * span_rows + jnp.arange(span_rows, dtype=jnp.int32)).astype(jnp.float32)
    head_cosine, head_sine = rope_tables(head_pos, HD)
    query_back = rotate(
        grad_queries.reshape(groups, span_rows, heads_here, HD), head_cosine, -head_sine
    )
    key_back = rotate(grad_keys.reshape(groups, span_rows, heads_here, HD), head_cosine, -head_sine)
    value_back = grad_values.reshape(groups, span_rows, heads_here, HD)
    grad_pack = (
        jnp.stack([query_back, key_back, value_back], axis=2)
        .astype(jnp.bfloat16)
        .reshape(groups, span_rows, 3, 1, lane_width)
    )
    grad_joined = lax.all_to_all(
        grad_pack, "fsdp", split_axis=1, concat_axis=3, tiled=True
    ).reshape(row_count, 3 * width)
    d_qkv = jnp.einsum("rd,re->de", flat_tokens, grad_joined, preferred_element_type=jnp.float32)
    d_qkv_bias = jnp.sum(grad_joined.astype(jnp.float32), axis=0)
    input_grad = (
        jnp.einsum("re,de->rd", grad_joined, back_qkv, preferred_element_type=jnp.float32)
        + grad_one
    ).astype(jnp.bfloat16)
    shards = (
        lax.psum_scatter(d_qkv, ("ctx", "fsdp"), scatter_dimension=0, tiled=True),
        lax.psum_scatter(d_qkv_bias, ("ctx", "fsdp"), scatter_dimension=0, tiled=True),
        lax.psum_scatter(d_out, ("ctx", "fsdp"), scatter_dimension=0, tiled=True),
        lax.psum_scatter(d_out_bias, ("ctx", "fsdp"), scatter_dimension=0, tiled=True),
        lax.psum_scatter(d_gain_one, ("ctx", "fsdp"), scatter_dimension=0, tiled=True),
        lax.psum_scatter(d_shift_one, ("ctx", "fsdp"), scatter_dimension=0, tiled=True),
        lax.psum_scatter(d_up, ("ctx", "fsdp"), scatter_dimension=0, tiled=True),
        lax.psum_scatter(d_up_bias, ("ctx", "fsdp"), scatter_dimension=0, tiled=True),
        lax.psum_scatter(d_down, ("ctx", "fsdp"), scatter_dimension=0, tiled=True),
        lax.psum_scatter(d_down_bias, ("ctx", "fsdp"), scatter_dimension=0, tiled=True),
        lax.psum_scatter(d_gain_two, ("ctx", "fsdp"), scatter_dimension=0, tiled=True),
        lax.psum_scatter(d_shift_two, ("ctx", "fsdp"), scatter_dimension=0, tiled=True),
        lax.psum_scatter(d_proj, ("ctx", "fsdp"), scatter_dimension=0, tiled=True),
    )
    totals = (
        lax.psum(shards[0].astype(jnp.bfloat16), "slot").astype(jnp.float32),
        lax.psum(shards[1].astype(jnp.bfloat16), "slot").astype(jnp.float32),
        lax.psum(shards[2].astype(jnp.bfloat16), "slot").astype(jnp.float32),
        lax.psum(shards[3].astype(jnp.bfloat16), "slot").astype(jnp.float32),
        lax.psum(shards[4].astype(jnp.bfloat16), "slot").astype(jnp.float32),
        lax.psum(shards[5].astype(jnp.bfloat16), "slot").astype(jnp.float32),
        lax.psum(shards[6].astype(jnp.bfloat16), "slot").astype(jnp.float32),
        lax.psum(shards[7].astype(jnp.bfloat16), "slot").astype(jnp.float32),
        lax.psum(shards[8].astype(jnp.bfloat16), "slot").astype(jnp.float32),
        lax.psum(shards[9].astype(jnp.bfloat16), "slot").astype(jnp.float32),
        lax.psum(shards[10].astype(jnp.bfloat16), "slot").astype(jnp.float32),
        lax.psum(shards[11].astype(jnp.bfloat16), "slot").astype(jnp.float32),
        lax.psum(shards[12].astype(jnp.bfloat16), "slot").astype(jnp.float32),
    )
    return (
        out_low.reshape(groups, tok_slot, width),
        projected.astype(jnp.bfloat16).reshape(groups, tok_slot, -1),
        input_grad.reshape(groups, tok_slot, width),
        totals[0],
        totals[1],
        totals[2],
        totals[3],
        totals[4],
        totals[5],
        totals[6],
        totals[7],
        totals[8],
        totals[9],
        totals[10],
        totals[11],
        totals[12],
    )


def solution(mesh):
    n_slot, n_ctx, n_fsdp = (mesh.shape[a] for a in ("slot", "ctx", "fsdp"))
    rows_axes = ("ctx", "fsdp")
    step = per_device
    if n_slot == 2 and n_fsdp % 2 == 0 and n_ctx * n_fsdp == H:
        mesh = Mesh(
            mesh.devices.reshape(n_slot, n_ctx, n_fsdp // 2, 2), ("slot", "ctx", "x", "core")
        )
        rows_axes = GROUP
        step = head_device
    in_specs = (
        P("slot", rows_axes, None),
        P("slot"),
        P(rows_axes, None),
        P(rows_axes),
        P(rows_axes, None),
        P(rows_axes),
        P(rows_axes),
        P(rows_axes),
        P(rows_axes, None),
        P(rows_axes),
        P(rows_axes, None),
        P(rows_axes),
        P(rows_axes),
        P(rows_axes),
        P(rows_axes, None),
        P("slot", rows_axes, None),
        P("slot", rows_axes, None),
    )
    out_specs = (
        P("slot", rows_axes, None),
        P("slot", rows_axes, None),
        P("slot", rows_axes, None),
        P(rows_axes, None),
        P(rows_axes),
        P(rows_axes, None),
        P(rows_axes),
        P(rows_axes),
        P(rows_axes),
        P(rows_axes, None),
        P(rows_axes),
        P(rows_axes, None),
        P(rows_axes),
        P(rows_axes),
        P(rows_axes),
        P(rows_axes, None),
    )
    return jax.shard_map(
        step, mesh=mesh, in_specs=in_specs, out_specs=out_specs, check_vma=False
    )
```

```python
from functools import partial

import jax
import jax.numpy as jnp
from jax import lax
from jax.experimental import pallas as pl
from jax.experimental.pallas import tpu as pltpu
from jax.sharding import Mesh
from jax.sharding import PartitionSpec as P

H = 16
HD = 64
LN_EPS = 1e-05
NEG_FILL = -1e30
F32 = jnp.float32
BF16 = jnp.bfloat16
GROUP = ("ctx", "x", "core")
LANE = ("ctx", "x")
SWAP = [(0, 1), (1, 0)]
VMEM_LIMIT = 60 * 1024 * 1024


def mm(left, right):
    return jnp.dot(left, right, preferred_element_type=F32)


def contract(left, right, left_dim, right_dim):
    return lax.dot_general(
        left, right, (((left_dim,), (right_dim,)), ((), ())), preferred_element_type=F32
    )


def swap_core(value):
    return lax.ppermute(value, "core", SWAP)


def swap_slot(value):
    return lax.ppermute(value, "slot", SWAP)


def pick(stacked, index, axis):
    return lax.dynamic_index_in_dim(stacked, index, axis, keepdims=False)


MESH = pl.DeviceIdType.MESH


def at_device(**where):
    names = ("slot", "ctx", "x", "core")
    return tuple(where[n] if n in where else lax.axis_index(n) for n in names)


def greet(peers):
    barrier = pltpu.get_barrier_semaphore()
    for peer in peers:
        pl.semaphore_signal(barrier, inc=1, device_id=peer, device_id_type=MESH)
    pl.semaphore_wait(barrier, len(peers))


def group_peers(n_ctx, n_x):
    ctx, x, core = (lax.axis_index(n) for n in GROUP)
    peers = []
    for dz in range(n_ctx):
        for dx in range(n_x):
            for dc in range(2):
                if dz or dx or dc:
                    where = (lax.rem(ctx + dz, n_ctx), lax.rem(x + dx, n_x), lax.rem(core + dc, 2))
                    peers.append(where)
    return peers


def start_kernel(
    tok_ref, head_ref, small_ref, all_ref, heads_ref, smalls_ref,
    far_send, block_send, local_sem, head_recv, small_recv, block_recv, *, n_ctx, n_x
):
    part = tok_ref.shape[1]
    ctx, x, core = (lax.axis_index(n) for n in GROUP)
    me = (ctx * n_x + x) * 2 + core
    peers = group_peers(n_ctx, n_x)
    greet([at_device(ctx=z, x=a, core=c) for z, a, c in peers])

    def block_at(b):
        return all_ref.at[:, pl.ds(pl.multiple_of(b * part, part), part), :]

    pushes = []
    for k, (z, a, c) in enumerate(peers):
        them = (z * n_x + a) * 2 + c
        target = at_device(ctx=z, x=a, core=c)
        pushes.append(pltpu.make_async_remote_copy(
            head_ref.at[them], heads_ref.at[me], far_send.at[2 * k], head_recv.at[me],
            device_id=target, device_id_type=MESH))
        pushes.append(pltpu.make_async_remote_copy(
            small_ref, smalls_ref.at[me], far_send.at[2 * k + 1], small_recv.at[me],
            device_id=target, device_id_type=MESH))
    locals_ = [
        pltpu.make_async_copy(tok_ref, block_at(me), local_sem.at[0]),
        pltpu.make_async_copy(head_ref.at[me], heads_ref.at[me], local_sem.at[1]),
        pltpu.make_async_copy(small_ref, smalls_ref.at[me], local_sem.at[2]),
    ]

    def send(b, source, lane, target):
        return pltpu.make_async_remote_copy(
            source, block_at(b), block_send.at[lane, b], block_recv.at[b],
            device_id=target, device_id_type=MESH)

    up = at_device(ctx=lax.rem(ctx + 1, n_ctx))
    down = at_device(ctx=lax.rem(ctx + n_ctx - 1, n_ctx))
    side = at_device(x=1 - x)
    twin = at_device(core=1 - core)

    def here(b):
        return send(b, block_at(b), 0, twin)

    @pl.when(ctx + 1 < n_ctx)
    def _():
        send(me, tok_ref, 0, up).start()

    @pl.when(ctx > 0)
    def _():
        send(me, tok_ref, 1, down).start()

    send(me, tok_ref, 2, side).start()
    send(me, tok_ref, 3, twin).start()
    for copy in locals_:
        copy.start()

    for r in range(1, n_ctx):
        if r == n_ctx - 1:
            for push in pushes:
                push.start()
        low = ctx - r
        high = ctx + r

        @pl.when(low >= 0)
        def _():
            b = (low * n_x + x) * 2 + core
            here(b).wait_recv()

            @pl.when(ctx + 1 < n_ctx)
            def _():
                send(b, block_at(b), 0, up).start()

            send(b, block_at(b), 2, side).start()
            send(b, block_at(b), 3, twin).start()

        @pl.when(high < n_ctx)
        def _():
            b = (high * n_x + x) * 2 + core
            here(b).wait_recv()

            @pl.when(ctx > 0)
            def _():
                send(b, block_at(b), 1, down).start()

            send(b, block_at(b), 2, side).start()
            send(b, block_at(b), 3, twin).start()

    def from_side(z):
        b = (z * n_x + (1 - x)) * 2 + core
        here(b).wait_recv()
        send(b, block_at(b), 3, twin).start()

    from_side(ctx)
    for r in range(1, n_ctx):
        @pl.when(ctx - r >= 0)
        def _():
            from_side(ctx - r)

        @pl.when(ctx + r < n_ctx)
        def _():
            from_side(ctx + r)

    for z in range(n_ctx):
        for a in range(n_x):
            here((z * n_x + a) * 2 + 1 - core).wait_recv()
    for k, (z, a, c) in enumerate(peers):
        them = (z * n_x + a) * 2 + c
        pltpu.make_async_remote_copy(
            head_ref.at[them], heads_ref.at[them], far_send.at[2 * k], head_recv.at[them],
            device_id=twin, device_id_type=MESH).wait_recv()
        pltpu.make_async_remote_copy(
            small_ref, smalls_ref.at[them], far_send.at[2 * k + 1], small_recv.at[them],
            device_id=twin, device_id_type=MESH).wait_recv()
    for push in pushes:
        push.wait_send()
    for copy in locals_:
        copy.wait()

    for z in range(n_ctx):
        b = (z * n_x + x) * 2 + core

        @pl.when((z <= ctx) & (ctx + 1 < n_ctx))
        def _():
            send(b, block_at(b), 0, up).wait_send()

        @pl.when((z >= ctx) & (ctx > 0))
        def _():
            send(b, block_at(b), 1, down).wait_send()

        send(b, block_at(b), 2, side).wait_send()
        send(b, block_at(b), 3, twin).wait_send()
        other = (z * n_x + (1 - x)) * 2 + core
        send(other, block_at(other), 3, twin).wait_send()


def gather_start(tokens, heads, small):
    n_ctx, n_x = lax.axis_size("ctx"), lax.axis_size("x")
    n = 2 * n_ctx * n_x
    slots, part, width = tokens.shape
    vmem = pl.BlockSpec(memory_space=pltpu.VMEM)
    anywhere = pl.BlockSpec(memory_space=pl.ANY)
    dma = pltpu.SemaphoreType.DMA
    return pl.pallas_call(
        partial(start_kernel, n_ctx=n_ctx, n_x=n_x),
        in_specs=[vmem, vmem, vmem],
        out_specs=[anywhere, vmem, vmem],
        out_shape=[
            jax.ShapeDtypeStruct((slots, n * part, width), tokens.dtype),
            jax.ShapeDtypeStruct(heads.shape, heads.dtype),
            jax.ShapeDtypeStruct((n,) + small.shape, small.dtype),
        ],
        scratch_shapes=[
            dma((2 * (n - 1),)), dma((4, n)), dma((3,)), dma((n,)), dma((n,)), dma((n,))
        ],
        compiler_params=pltpu.CompilerParams(
            collective_id=1, has_side_effects=True, vmem_limit_bytes=VMEM_LIMIT
        ),
        cost_estimate=pl.CostEstimate(
            flops=0, bytes_accessed=2 * n * tokens.size, transcendentals=0
        ),
        name="gather_start",
    )(tokens, heads, small)


def finish_kernel(
    out_ref, small_ref, qkv_ref, red_ref, join_ref, weight_ref, one_ref,
    g_down, g_up, g_out, g_small, g_qkv, g_bias, g_in,
    pair_small, pair_qkv, sum_qkv, qkvs,
    pair_down, pair_out, last_up, joins, partial_in, pair_in,
    join_send, join_recv, far_send, qkv_recv, y_send, y_recv,
    *, n_ctx, n_x
):
    ctx, x, core = (lax.axis_index(n) for n in GROUP)
    slot = lax.axis_index("slot")
    chip = ctx * n_x + x
    me = 2 * chip + core
    shard, width = g_out.shape
    part = g_down.shape[0] // 2
    peers = group_peers(n_ctx, n_x)
    lane_peers = [(z, a) for z, a, c in peers[1::2]]
    across = at_device(slot=1 - slot)
    corner = at_device(slot=1 - slot, core=1 - core)
    twin = at_device(core=1 - core)
    greet([at_device(ctx=z, x=a, core=c) for z, a, c in peers] + [across, corner])

    def remote(source, target_ref, send_sem, recv_sem, target):
        return pltpu.make_async_remote_copy(
            source, target_ref, send_sem, recv_sem, device_id=target, device_id_type=MESH)

    started = []

    def launch(copy):
        copy.start()
        started.append(copy)
        return copy

    def pair_copy(i, source, target_ref, target):
        return launch(remote(source, target_ref, y_send.at[i], y_recv.at[i], target))

    qkv_copy = pair_copy(0, qkv_ref, pair_qkv, across)
    mine = pl.multiple_of(part + core * shard, shard)
    theirs = pl.multiple_of(part + (1 - core) * shard, shard)
    for k, (z, a) in enumerate(lane_peers):
        launch(remote(
            join_ref.at[z * n_x + a], joins.at[chip], join_send.at[k], join_recv.at[chip],
            at_device(ctx=z, x=a)))
    down_copy = pair_copy(4, red_ref.at[pl.ds(0, part)], pair_down, across)
    quarter_copies = [
        pair_copy(5, red_ref.at[pl.ds(theirs, shard)], last_up.at[0], twin),
        pair_copy(6, red_ref.at[pl.ds(mine, shard)], last_up.at[1], across),
        pair_copy(7, red_ref.at[pl.ds(theirs, shard)], last_up.at[2], corner),
    ]

    small_copy = pair_copy(1, small_ref, pair_small, across)
    out_copy = pair_copy(3, out_ref, pair_out, across)
    qkv_copy.wait_recv()
    sum_qkv[...] = (qkv_ref[...].astype(F32) + pair_qkv[...].astype(F32)).astype(BF16)
    for k, (z, a, c) in enumerate(peers):
        them = (z * n_x + a) * 2 + c
        launch(remote(
            sum_qkv.at[them], qkvs.at[me], far_send.at[k], qkv_recv.at[me],
            at_device(ctx=z, x=a, core=c)))
    qkvs[me] = sum_qkv[me]

    def add_head(source, rows_of, first):
        weight = jnp.concatenate(
            [weight_ref[b, source] for b in range(weight_ref.shape[0])], axis=0)
        for h in range(2):
            owner = core if h == 0 else 1 - core
            rows = rows_of(owner)
            cols = rows.shape[2] // 2
            rows = jnp.concatenate(
                [r for t in range(rows.shape[0]) for r in (rows[t, :, :cols], rows[t, :, cols:])],
                axis=0)
            term = contract(rows, weight, 1, 1)
            partial_in[h] = term if first else partial_in[h] + term

    add_head(chip, lambda owner: join_ref[chip, owner], True)

    half = pl.multiple_of(slot * part, part)
    other_half = pl.multiple_of((1 - slot) * part, part)
    g_down[pl.ds(half, part), :] = red_ref[pl.ds(0, part), :].astype(F32)
    down_copy.wait_recv()
    g_down[pl.ds(other_half, part), :] = pair_down[...].astype(F32)

    def place_quarter(rows, quarter_core, quarter_slot):
        for k in range(n_ctx * n_x):
            at = pl.multiple_of(((2 * k + quarter_core) * 2 + quarter_slot) * part, part)
            g_up[:, pl.ds(at, part)] = rows[:, k * part : (k + 1) * part].astype(F32)

    place_quarter(red_ref[pl.ds(mine, shard), :], core, slot)
    quarter_copies[0].wait_recv()
    place_quarter(last_up[0], 1 - core, slot)
    quarter_copies[1].wait_recv()
    place_quarter(last_up[1], core, 1 - slot)
    quarter_copies[2].wait_recv()
    place_quarter(last_up[2], 1 - core, 1 - slot)

    @pl.loop(1, n_ctx * n_x)
    def _(o):
        source = lax.rem(ctx + o // n_x, n_ctx) * n_x + lax.rem(x + o % n_x, n_x)
        remote(
            join_ref.at[source], joins.at[source], join_send.at[0], join_recv.at[source], twin
        ).wait_recv()
        add_head(source, lambda owner: joins[source, owner], False)

    in_copy = pair_copy(2, partial_in.at[1], pair_in, twin)

    small_copy.wait_recv()
    g_small[...] = small_ref[...].astype(F32) + pair_small[...].astype(F32)
    in_copy.wait_recv()
    g_in[...] = (partial_in[0] + pair_in[...] + one_ref[...]).astype(BF16)
    for z, a, c in peers:
        them = (z * n_x + a) * 2 + c
        remote(
            sum_qkv.at[them], qkvs.at[them], far_send.at[0], qkv_recv.at[them], twin
        ).wait_recv()
    for k in range(n_ctx * n_x):
        heads = [qkvs[2 * k + c, :shard, :].astype(F32) for c in range(2)]
        for t in range(3):
            at = t * width + 2 * HD * k
            g_qkv[:, at : at + 2 * HD] = jnp.concatenate(
                [h[:, t * HD : (t + 1) * HD] for h in heads], axis=1)
        for c in range(2):
            g_bias[2 * k + c : 2 * k + c + 1, :] = qkvs[2 * k + c, shard : shard + 1, :].astype(F32)
    out_copy.wait_recv()
    g_out[...] = out_ref[...].astype(F32) + pair_out[...].astype(F32)
    for copy in started:
        copy.wait_send()


def finish_grads(out, small, qkv, reduced, joined, weight, grad_one):
    n_ctx, n_x = lax.axis_size("ctx"), lax.axis_size("x")
    n = 2 * n_ctx * n_x
    shard, width = out.shape
    part = reduced.shape[0] // 2
    vmem = pl.BlockSpec(memory_space=pltpu.VMEM)
    dma = pltpu.SemaphoreType.DMA

    def low(*shape):
        return pltpu.VMEM(shape, BF16)

    def wide(*shape):
        return jax.ShapeDtypeStruct(shape, F32)

    return pl.pallas_call(
        partial(finish_kernel, n_ctx=n_ctx, n_x=n_x),
        in_specs=[vmem] * 7,
        out_specs=[vmem] * 7,
        out_shape=[
            wide(2 * part, width),
            wide(shard, 4 * width),
            wide(shard, width),
            wide(*small.shape),
            wide(shard, 3 * width),
            wide(n, qkv.shape[2]),
            jax.ShapeDtypeStruct(grad_one.shape, BF16),
        ],
        scratch_shapes=[
            low(*small.shape),
            low(*qkv.shape),
            low(*qkv.shape),
            low(*qkv.shape),
            low(part, width),
            low(*out.shape),
            low(3, shard, width),
            low(*joined.shape),
            pltpu.VMEM((2,) + grad_one.shape, F32),
            pltpu.VMEM(grad_one.shape, F32),
            dma((n_ctx * n_x - 1,)),
            dma((n_ctx * n_x,)),
            dma((n - 1,)),
            dma((n,)),
            dma((8,)),
            dma((8,)),
        ],
        compiler_params=pltpu.CompilerParams(
            collective_id=2, has_side_effects=True, vmem_limit_bytes=VMEM_LIMIT
        ),
        cost_estimate=pl.CostEstimate(flops=0, bytes_accessed=16 * joined.size, transcendentals=0),
        name="finish_grads",
    )(out, small, qkv, reduced, joined, weight, grad_one)


def lane_gather(mine_ref, all_ref, send_sem, recv_sem, local_sem, n_ctx, n_x):
    ctx, x = lax.axis_index("ctx"), lax.axis_index("x")
    chip = ctx * n_x + x
    routes = (
        at_device(ctx=lax.rem(ctx + 1, n_ctx)),
        at_device(ctx=lax.rem(ctx + n_ctx - 1, n_ctx)),
        at_device(x=1 - x),
    )

    def send(k, lane, own=False):
        return pltpu.make_async_remote_copy(
            mine_ref if own else all_ref.at[k], all_ref.at[k], send_sem.at[lane, k], recv_sem.at[k],
            device_id=routes[lane], device_id_type=MESH)

    local = pltpu.make_async_copy(mine_ref, all_ref.at[chip], local_sem)

    def begin():
        @pl.when(ctx + 1 < n_ctx)
        def _():
            send(chip, 0, own=True).start()

        @pl.when(ctx > 0)
        def _():
            send(chip, 1, own=True).start()

        send(chip, 2, own=True).start()
        local.start()

    def relay(r):
        for sign, lane, more in ((-1, 0, ctx + 1 < n_ctx), (1, 1, ctx > 0)):
            z = ctx + sign * r

            @pl.when((z >= 0) & (z < n_ctx))
            def _():
                k = z * n_x + x
                send(k, 0).wait_recv()

                @pl.when(more)
                def _():
                    send(k, lane).start()

                send(k, 2).start()

    def end():
        for z in range(n_ctx):
            k = z * n_x + x
            send(z * n_x + 1 - x, 0).wait_recv()

            @pl.when((z <= ctx) & (ctx + 1 < n_ctx))
            def _():
                send(k, 0).wait_send()

            @pl.when((z >= ctx) & (ctx > 0))
            def _():
                send(k, 1).wait_send()

            send(k, 2).wait_send()
        local.wait()

    return begin, relay, end


def lane_gather_x_first(mine_ref, all_ref, send_sem, recv_sem, local_sem, n_ctx, n_x):
    ctx, x = lax.axis_index("ctx"), lax.axis_index("x")
    chip = ctx * n_x + x
    pair = ctx * n_x + 1 - x
    routes = (
        at_device(ctx=lax.rem(ctx + 1, n_ctx)),
        at_device(ctx=lax.rem(ctx + n_ctx - 1, n_ctx)),
        at_device(x=1 - x),
    )
    ways = ((-1, 0, ctx + 1 < n_ctx), (1, 1, ctx > 0))

    def send(k, lane, own=False):
        return pltpu.make_async_remote_copy(
            mine_ref if own else all_ref.at[k], all_ref.at[k], send_sem.at[lane, k], recv_sem.at[k],
            device_id=routes[lane], device_id_type=MESH)

    local = pltpu.make_async_copy(mine_ref, all_ref.at[chip], local_sem)

    def along(k, own=False):
        for _, lane, more in ways:
            @pl.when(more)
            def _():
                send(k, lane, own).start()

    def begin():
        send(chip, 2, own=True).start()
        along(chip, own=True)
        local.start()

    def pass_on(r, line):
        for sign, lane, more in ways:
            z = ctx + sign * r

            @pl.when((z >= 0) & (z < n_ctx))
            def _():
                k = z * n_x + line
                send(k, lane).wait_recv()

                @pl.when(more)
                def _():
                    send(k, lane).start()

    def relay(r):
        if r == 1:
            send(pair, 2).wait_recv()
            along(pair)
        else:
            pass_on(r - 1, 1 - x)
        pass_on(r, x)

    def end():
        pass_on(n_ctx - 1, 1 - x)
        send(chip, 2).wait_send()
        for z in range(n_ctx):
            for line in range(n_x):
                @pl.when((z <= ctx) & (ctx + 1 < n_ctx))
                def _():
                    send(z * n_x + line, 0).wait_send()

                @pl.when((z >= ctx) & (ctx > 0))
                def _():
                    send(z * n_x + line, 1).wait_send()

        local.wait()

    return begin, relay, end


QB = 512
KB = 512


def turn(pair, cosine, sine):
    half = HD // 2
    lanes = lax.broadcasted_iota(jnp.int32, (1, 2 * HD), 1)
    low = lax.rem(lanes, HD) < half
    swapped = jnp.where(low, pltpu.roll(pair, 2 * HD - half, 1), pltpu.roll(pair, half, 1))
    return pair * cosine + swapped * jnp.where(low, -sine, sine)


def heads_kernel(
    len_ref, tok_ref, w_ref, b_ref, cos_ref, sin_ref, wa_ref, wu_ref, wd_ref,
    q_ref, k_ref, v_ref, mix_ref, send_ref, norm_ref, fa_ref, fu_ref, fd_ref,
    a_send, a_recv, u_send, u_recv, d_send, d_recv, local_sem, *, n_ctx, n_x, part
):
    core = lax.axis_index("core")
    ctx, x = lax.axis_index("ctx"), lax.axis_index("x")
    greet([
        at_device(x=1 - x),
        at_device(ctx=lax.rem(ctx + 1, n_ctx)),
        at_device(ctx=lax.rem(ctx + n_ctx - 1, n_ctx)),
    ])
    flows = [
        lane_gather_x_first(wa_ref, fa_ref, a_send, a_recv, local_sem.at[0], n_ctx, n_x),
        lane_gather(wu_ref, fu_ref, u_send, u_recv, local_sem.at[1], n_ctx, n_x),
        lane_gather(wd_ref, fd_ref, d_send, d_recv, local_sem.at[2], n_ctx, n_x),
    ]
    for begin, _, _ in flows:
        begin()
    slots, seq, _ = q_ref.shape

    def relay(r):
        if r < n_ctx:
            for _, hop, _ in flows:
                hop(r)

    blocks = seq // QB

    def project():
        @pl.loop(0, slots * blocks)
        def _(n):
            s, i = n // blocks, lax.rem(n, blocks)
            rows = pl.ds(pl.multiple_of(i * QB, QB), QB)
            tokens = tok_ref[pl.ds(pl.multiple_of(n * QB, QB), QB), :]
            joined = mm(tokens, w_ref[...]) + b_ref[...]
            turned = turn(joined[:, : 2 * HD], cos_ref[rows, :], sin_ref[rows, :])
            q_ref[s, rows, :] = (turned[:, :HD].astype(BF16) * HD ** (-0.5)).astype(BF16)
            k_ref[s, rows, :] = turned[:, HD:].astype(BF16)
            v_ref[s, rows, :] = joined[:, 2 * HD :].astype(BF16)

    def attend():
        @pl.loop(0, slots * blocks)
        def _(n):
            s, i = n // blocks, lax.rem(n, blocks)
            length = len_ref[s]
            rows = pl.ds(pl.multiple_of(i * QB, QB), QB)
            queries = q_ref[s, rows, :]

            @pl.when(n == blocks)
            def _():
                relay(2)

            def step(j, state):
                highest, total, mix = state
                start = pl.multiple_of(j * KB, KB)
                scores = contract(queries, k_ref[s, pl.ds(start, KB), :], 1, 1)
                ids = start + lax.broadcasted_iota(jnp.int32, (1, KB), 1)
                scores = jnp.where(ids < length, scores, NEG_FILL)
                higher = jnp.maximum(highest, jnp.max(scores, axis=1, keepdims=True))
                fade = jnp.exp(highest - higher)
                weights = jnp.exp(scores - higher)
                total = total * fade + jnp.sum(weights, axis=1, keepdims=True)
                mix = mix * fade + mm(weights.astype(BF16), v_ref[s, pl.ds(start, KB), :])
                return higher, total, mix

            highest, total, mix = lax.fori_loop(
                0,
                seq // KB,
                step,
                (
                    jnp.full((QB, 1), NEG_FILL, F32),
                    jnp.zeros((QB, 1), F32),
                    jnp.zeros((QB, HD), F32),
                ),
            )
            mix = mix / total
            mix_ref[s, rows, :] = mix
            log_norm = jnp.broadcast_to(highest + jnp.log(total), (QB, 128))
            norm_ref[s, :, rows] = jnp.transpose(log_norm)[0:1, :]
            low = mix.astype(BF16)
            chips = QB // (2 * part)
            for chip in range(chips):
                for half in range(2):
                    at = (2 * chip + half) * part
                    upper, lower = low[at : at + part // 2], low[at + part // 2 : at + part]
                    send_ref[i * chips + chip, half ^ core, s] = jnp.concatenate(
                        [upper, lower], axis=1)

    project()
    relay(1)
    attend()
    for r in range(3, n_ctx):
        relay(r)
    for _, _, end in flows:
        end()


def heads(lengths, tokens, weight, bias, cosine, sine, part, *shards):
    n_ctx, n_x = lax.axis_size("ctx"), lax.axis_size("x")
    chips = n_ctx * n_x
    slots, seq = lengths.shape[0], cosine.shape[0]
    vmem = pl.BlockSpec(memory_space=pltpu.VMEM)
    anywhere = pl.BlockSpec(memory_space=pl.ANY)
    dma = pltpu.SemaphoreType.DMA
    head = jax.ShapeDtypeStruct((slots, seq, HD), BF16)
    return pl.pallas_call(
        partial(heads_kernel, n_ctx=n_ctx, n_x=n_x, part=part),
        in_specs=[pl.BlockSpec(memory_space=pltpu.SMEM)] + [vmem] * 8,
        out_specs=[vmem] * 6 + [anywhere] * 3,
        out_shape=[
            head,
            head,
            head,
            jax.ShapeDtypeStruct((slots, seq, HD), F32),
            jax.ShapeDtypeStruct((chips, 2, slots, part // 2, 2 * HD), BF16),
            jax.ShapeDtypeStruct((slots, 1, seq), F32),
        ]
        + [jax.ShapeDtypeStruct((chips,) + w.shape, w.dtype) for w in shards],
        scratch_shapes=[dma((3, chips)), dma((chips,))] * 3 + [dma((3,))],
        compiler_params=pltpu.CompilerParams(
            collective_id=5, has_side_effects=True, vmem_limit_bytes=VMEM_LIMIT
        ),
        cost_estimate=pl.CostEstimate(
            flops=16 * slots * seq * seq * HD,
            bytes_accessed=2 * tokens.size,
            transcendentals=slots * seq * seq,
        ),
        name="heads",
    )(lengths, tokens, weight, bias, cosine, sine, *shards)


def grads_kernel(
    len_ref, q_ref, k_ref, v_ref, g_ref, norm_ref, dot_ref, tok_ref, cos_ref, sin_ref,
    down_ref, up_ref, out_ref, small_ref,
    join_ref, grad_ref, red_ref, sum_ref, small_sum,
    dqt, key_grads, value_grads, total, bias, x_down, x_up, x_out, s_down, s_up, s_out,
    z_down, z_up, z_out, top_down, top_up, top_out, own_down, own_up, own_out, smalls,
    x_send, x_recv, z_send, z_recv, top_recv, small_send, small_recv, *, n_ctx, n_x, part
):
    ctx, x, core = (lax.axis_index(n) for n in GROUP)
    me = (ctx * n_x + x) * 2 + core
    peers = group_peers(n_ctx, n_x)
    greet([at_device(ctx=z, x=a, core=c) for z, a, c in peers])
    side = at_device(x=1 - x)
    arrays = (
        (down_ref, x_down, s_down, z_down, top_down, own_down),
        (up_ref, x_up, s_up, z_up, top_up, own_up),
        (out_ref, x_out, s_out, z_out, top_out, own_out),
    )

    def remote(source, target_ref, send_sem, recv_sem, target):
        return pltpu.make_async_remote_copy(
            source, target_ref, send_sem, recv_sem, device_id=target, device_id_type=MESH)

    orders = [
        sorted(range(n_ctx), key=lambda p, z=z: (p == z, -abs(p - z), min(p, n_ctx - 1 - p))) for z in range(n_ctx)
    ]
    places = [
        sum(jnp.where(ctx == z, orders[z][j], 0) for z in range(n_ctx)) for j in range(n_ctx)
    ]
    above = at_device(ctx=lax.rem(ctx + 1, n_ctx))
    below = at_device(ctx=lax.rem(ctx + n_ctx - 1, n_ctx))
    first = [
        [
            remote(
                ref.at[places[j] * n_x + 1 - x], x_in.at[j], x_send.at[i, j], x_recv.at[i, j], side)
            for i, (ref, x_in, _, _, _, _) in enumerate(arrays)
        ]
        for j in range(n_ctx)
    ]

    def hop(j, i, target, last=False):
        _, _, s_low, z_in, top, _ = arrays[i]
        p = places[j]
        return remote(
            s_low.at[min(j, n_ctx - 2)], top if last else z_in.at[p], z_send.at[i, min(j, n_ctx - 2)],
            top_recv.at[i] if last else z_recv.at[i, p], target)

    pushes = []
    for k, (z, a, c) in enumerate(peers):
        them = (z * n_x + a) * 2 + c
        pushes.append(remote(
            small_ref.at[them], smalls.at[me], small_send.at[k], small_recv.at[me],
            at_device(ctx=z, x=a, core=c)))
    for copies in first:
        for copy in copies:
            copy.start()
    for copy in pushes:
        copy.start()
    smalls[me] = small_ref[me]

    def stage(j):
        p = places[j]
        going_up = p > ctx
        for i, (ref, x_in, s_low, z_in, _, own) in enumerate(arrays):
            first[j][i].wait_recv()
            own[...] = ref[p * n_x + x].astype(F32) + x_in[j].astype(F32)
            if j == n_ctx - 1:
                continue

            @pl.when((going_up & (ctx > 0)) | ((p < ctx) & (ctx < n_ctx - 1)))
            def _():
                hop(j, i, above).wait_recv()
                own[...] += z_in[p].astype(F32)

            s_low[j] = own[...].astype(BF16)

            @pl.when(going_up)
            def _():
                hop(j, i, above).start()

            @pl.when(p < ctx - 1)
            def _():
                hop(j, i, below).start()

            @pl.when(p == ctx - 1)
            def _():
                hop(j, i, below, last=True).start()

    slots, seq, _ = q_ref.shape
    total[...] = jnp.zeros_like(total)
    bias[...] = jnp.zeros_like(bias)

    def attention(s, between):
        length = len_ref[s]
        dqt[...] = jnp.zeros_like(dqt)

        @pl.loop(0, seq // KB)
        def _(j):
            start = pl.multiple_of(j * KB, KB)
            key_block = k_ref[s, pl.ds(start, KB), :]
            value_block = v_ref[s, pl.ds(start, KB), :]
            turned = jnp.transpose(key_block.astype(F32)).astype(BF16)
            ids = start + lax.broadcasted_iota(jnp.int32, (KB, 1), 0)
            shift = jnp.where(ids < length, 0.0, NEG_FILL)
            for at_step, number in between:
                @pl.when(j == at_step)
                def _():
                    stage(number)

            def step(i, state):
                key_grad, value_grad = state
                at = pl.multiple_of(i * QB, QB)
                queries = q_ref[s, pl.ds(at, QB), :]
                grads = g_ref[s, pl.ds(at, QB), :]
                scores = contract(key_block, queries, 1, 1) + shift
                probs = jnp.exp(scores - norm_ref[s, :, pl.ds(at, QB)])
                grad_probs = contract(value_block, grads, 1, 1)
                grad_scores = (probs * (grad_probs - dot_ref[s, :, pl.ds(at, QB)])).astype(BF16)
                value_grad = value_grad + mm(probs.astype(BF16), grads)
                key_grad = key_grad + mm(grad_scores, queries)
                dqt[:, pl.ds(at, QB)] += mm(turned, grad_scores)
                return key_grad, value_grad

            zero = jnp.zeros((KB, HD), F32)
            key_grad, value_grad = lax.fori_loop(0, seq // QB, step, (zero, zero))
            key_grads[pl.ds(start, KB), :] = key_grad
            value_grads[pl.ds(start, KB), :] = value_grad

    def join(s):
        @pl.loop(0, seq // QB)
        def _(i):
            at = pl.multiple_of(i * QB, QB)
            rows = pl.ds(at, QB)
            query_grad = jnp.transpose(dqt[:, rows]) * HD ** (-0.5)
            pair = jnp.concatenate([query_grad, key_grads[rows, :]], axis=1)
            turned = turn(pair, cos_ref[rows, :], -sin_ref[rows, :])
            joined = jnp.concatenate([turned, value_grads[rows, :]], axis=1).astype(BF16)
            chips = QB // (2 * part)
            for chip in range(chips):
                for owner in range(2):
                    near = (2 * chip + owner) * part
                    upper = joined[near : near + part // 2]
                    lower = joined[near + part // 2 : near + part]
                    join_ref[i * chips + chip, owner, s] = jnp.concatenate([upper, lower], axis=1)
            tokens = tok_ref[pl.ds(pl.multiple_of(s * seq + at, QB), QB), :]
            total[...] += contract(joined, tokens, 0, 0)
            bias[...] += jnp.sum(joined.astype(F32), axis=0, keepdims=True)

    for s in range(slots):
        attention(s, [(1, 1)] if s == 1 else [])
        stage(0 if s == 0 else 2)
        join(s)
    turned_total = jnp.transpose(total[...])
    shard = turned_total.shape[0] // grad_ref.shape[0]
    extra = jnp.broadcast_to(bias[...], (grad_ref.shape[1] - shard, bias.shape[1]))
    for d in range(grad_ref.shape[0]):
        grad_ref[d, :shard] = turned_total[d * shard : (d + 1) * shard].astype(BF16)
        grad_ref[d, shard:] = extra.astype(BF16)
    for j in range(slots + 1, n_ctx):
        stage(j)
    for z, a, c in peers:
        them = (z * n_x + a) * 2 + c
        remote(
            small_ref.at[them], smalls.at[them], small_send.at[0], small_recv.at[them], side
        ).wait_recv()
    small_sum[...] = jnp.sum(smalls[...].astype(F32), axis=0).astype(BF16)
    for i, (_, _, _, z_in, top, own) in enumerate(arrays):
        @pl.when(ctx > 0)
        def _():
            hop(n_ctx - 1, i, above).wait_recv()
            own[...] += z_in[ctx].astype(F32)

        @pl.when(ctx < n_ctx - 1)
        def _():
            hop(0, i, below, last=True).wait_recv()
            own[...] += top[...].astype(F32)

    rows = own_down.shape[0]
    red_ref[:rows] = own_down[...].astype(BF16)
    red_ref[rows:] = own_up[...].astype(BF16)
    sum_ref[...] = own_out[...].astype(BF16)
    for copies in first + [pushes]:
        for copy in copies:
            copy.wait_send()
    for j in range(n_ctx - 1):
        for i in range(len(arrays)):
            hop(j, i, above).wait_send()


def grads(lengths, queries, keys, values, grad_heads, norms, dots, tokens, cosine, sine,
          down, up, out, small, part):
    n_ctx, n_x = lax.axis_size("ctx"), lax.axis_size("x")
    n = 2 * n_ctx * n_x
    slots, seq, _ = queries.shape
    width = tokens.shape[1]
    shard = width // n
    cols = 3 * HD
    vmem = pl.BlockSpec(memory_space=pltpu.VMEM)
    dma = pltpu.SemaphoreType.DMA
    parts = (down, up, out)

    def low(*dims):
        return jax.ShapeDtypeStruct(dims, BF16)

    return pl.pallas_call(
        partial(grads_kernel, n_ctx=n_ctx, n_x=n_x, part=part),
        in_specs=[pl.BlockSpec(memory_space=pltpu.SMEM)] + [vmem] * 13,
        out_specs=[vmem] * 5,
        out_shape=[
            low(seq // (2 * part), 2, slots, part // 2, 2 * cols),
            low(n, shard + 16, cols),
            low(down.shape[1] + up.shape[1], width),
            low(*out.shape[1:]),
            low(*small.shape[1:]),
        ],
        scratch_shapes=[
            pltpu.VMEM((HD, seq), F32),
            pltpu.VMEM((seq, HD), F32),
            pltpu.VMEM((seq, HD), F32),
            pltpu.VMEM((cols, width), F32),
            pltpu.VMEM((1, cols), F32),
        ]
        + [pltpu.VMEM((n_ctx,) + t.shape[1:], BF16) for t in parts]
        + [pltpu.VMEM((n_ctx - 1,) + t.shape[1:], BF16) for t in parts]
        + [pltpu.VMEM((n_ctx,) + t.shape[1:], BF16) for t in parts]
        + [pltpu.VMEM(t.shape[1:], BF16) for t in parts]
        + [pltpu.VMEM(t.shape[1:], F32) for t in parts]
        + [
            pltpu.VMEM(small.shape, BF16),
            dma((3, n_ctx)),
            dma((3, n_ctx)),
            dma((3, n_ctx - 1)),
            dma((3, n_ctx)),
            dma((3,)),
            dma((n - 1,)),
            dma((n,)),
        ],
        compiler_params=pltpu.CompilerParams(
            collective_id=6, has_side_effects=True, vmem_limit_bytes=VMEM_LIMIT
        ),
        cost_estimate=pl.CostEstimate(
            flops=40 * slots * seq * seq * HD,
            bytes_accessed=4 * tokens.size,
            transcendentals=slots * seq * seq,
        ),
        name="grads",
    )(lengths, queries, keys, values, grad_heads, norms, dots, tokens, cosine, sine,
      down, up, out, small)


def norm_forward(values, gain, shift):
    center = values - jnp.mean(values, axis=-1, keepdims=True)
    spread = jnp.mean(center * center, axis=-1, keepdims=True)
    root = lax.rsqrt(spread + LN_EPS)
    unit = center * root
    return unit * gain + shift, unit, root


def norm_backward(grad, unit, root, gain):
    scaled = grad * gain
    inner = scaled - jnp.mean(scaled, axis=-1, keepdims=True)
    inner = inner - unit * jnp.mean(scaled * unit, axis=-1, keepdims=True)
    return root * inner, jnp.sum(grad * unit, axis=0), jnp.sum(grad, axis=0)


def gelu_pair(values):
    half = 0.5 + 0.5 * lax.erf(values * 0.7071067811865476)
    bell = jnp.exp(-0.5 * values * values) * 0.3989422804014327
    return values * half, half + values * bell


def rope_rows(positions):
    halfway = HD // 2
    ladder = jnp.arange(halfway, dtype=F32) * (2.0 / HD)
    frequency = jnp.power(jnp.float32(10000.0), -ladder)
    angles = positions[:, None] * frequency[None, :]
    return jnp.cos(angles), jnp.sin(angles)


def layer_kernel(
    sent_ref, tok_ref, wo_ref, up_ref, down_ref, vec_ref, full_ref, lane_ref,
    merged_ref, out_ref, one_ref, ghead_ref, att_ref, vecs_ref, d_down_ref, d_up_ref, lanes_out,
    first, first_in, hid, act, slope, gdn, gup, hidden, unit_one, two,
    roots, near, near_in, far, far_in, low_out, low_in, send_sem, recv_sem, out_sem,
    lane_send, lane_recv, heads_in, push_send, push_recv,
    gm, heads_out, heads_back, back_send, back_recv, *, n_ctx, n_x
):
    core, slot = lax.axis_index("core"), lax.axis_index("slot")
    twin, across = at_device(core=1 - core), at_device(slot=1 - slot)
    ctx, x = lax.axis_index("ctx"), lax.axis_index("x")
    chip = ctx * n_x + x
    others = [
        (lax.rem(ctx + o // n_x, n_ctx), lax.rem(x + o % n_x, n_x)) for o in range(1, n_ctx * n_x)
    ]
    greet([twin, across] + [at_device(ctx=z, x=a) for z, a in others])
    pushes = [
        pltpu.make_async_remote_copy(
            sent_ref.at[z * n_x + a], heads_in.at[chip], push_send.at[o], push_recv.at[chip],
            device_id=at_device(ctx=z, x=a), device_id_type=MESH)
        for o, (z, a) in enumerate(others)
    ]
    for push in pushes:
        push.start()
    heads_in[chip] = sent_ref[chip]
    begin_lane, relay_lane, end_lane = lane_gather(
        lane_ref, lanes_out, lane_send, lane_recv, out_sem.at[0], n_ctx, n_x)
    begin_lane()
    rows, width = tok_ref.shape
    half = rows // 2
    tile = 256
    count = [0]
    started = []

    def launch(source, target_ref, target):
        i = count[0]
        count[0] += 1
        copy = pltpu.make_async_remote_copy(
            source, target_ref, send_sem.at[i], recv_sem.at[i],
            device_id=target, device_id_type=MESH)
        copy.start()
        started.append(copy)
        return copy

    def columns(body, n=width // tile):
        @pl.loop(0, n)
        def _(t):
            body(pl.ds(pl.multiple_of(t * tile, tile), tile))

    def chunks(body, size=64):
        @pl.loop(0, rows // size)
        def _(t):
            body(pl.ds(pl.multiple_of(t * size, size), size))

    def exchange(buf, turn, stage, product, between):
        halves = [
            launch(buf.at[pl.ds(h * half, half)], buf.at[pl.ds((2 + h) * rows, half)], across)
            for h in range(2)
        ]
        to_twin = launch(buf.at[pl.ds(0, rows)], buf.at[pl.ds(rows, rows)], twin)
        near_buf, far_buf = near.at[turn], far.at[turn]
        to_twin.wait_recv()
        stage(0, 2 * rows)
        product(0, 2 * rows, near_buf, 0)
        near_copy = launch(
            near_buf.at[pl.ds(rows, rows)], near_in.at[turn], twin)
        between()
        back = []
        for h in range(2):
            at = (2 + h) * rows
            halves[h].wait_recv()
            launch(
                buf.at[pl.ds(at, half)], buf.at[pl.ds(at + half, half)], twin).wait_recv()
            stage(at, rows)
            product(at, rows, far_buf, h * rows)
            i = 2 * turn + h
            launch(
                far_buf.at[pl.ds(h * rows + half, half)], far_in.at[i], twin).wait_recv()
            low_out[i] = (far_buf[pl.ds(h * rows, half), :] + far_in[i]).astype(BF16)
            back.append(launch(low_out.at[i], low_in.at[i], across))
        return near_copy, back

    for o, (z, a) in enumerate(others):
        source = z * n_x + a
        pltpu.make_async_remote_copy(
            sent_ref.at[source], heads_in.at[source], push_send.at[o], push_recv.at[source],
            device_id=twin, device_id_type=MESH).wait_recv()
    _, owners, slots, packed, pair_width = heads_in.shape
    for k in range(0, n_ctx * n_x, 2):
        for h in range(owners):
            for t in range(slots):
                left, right = heads_in[k, h, t], heads_in[k + 1, h, t]
                for piece in range(2):
                    at = ((h * slots + t) * 2 + piece) * packed
                    of = slice(piece * HD, (piece + 1) * HD)
                    merged_ref[at : at + packed, k * HD : (k + 2) * HD] = jnp.concatenate(
                        [left[:, of], right[:, of]], axis=1)

    def out_product(cols):
        first[:, cols] = mm(merged_ref[...], wo_ref[:, cols])

    columns(out_product)
    launch(first.at[pl.ds(rows, rows)], first_in, twin).wait_recv()

    def norm_one(at):
        values = tok_ref[at, :].astype(F32) + first[at, :] + first_in[at, :] + vec_ref[0:1, :]
        normed, unit, root = norm_forward(values, vec_ref[1:2, :], vec_ref[2:3, :])
        hidden[at, :] = normed
        unit_one[at, :] = unit
        roots[0, at, :] = jnp.broadcast_to(root, (root.shape[0], 128))
        hid[at, :] = normed.astype(BF16)

    chunks(norm_one)

    def up_stage(start, size):
        def body(cols):
            values = mm(hid[start : start + size, :], up_ref[:, cols]) + vec_ref[3:4, cols]
            active, bend = gelu_pair(values)
            act[start : start + size, cols] = active.astype(BF16)
            slope[start : start + size, cols] = bend

        columns(body)

    def down_product(start, size, target, at):
        def body(cols):
            target[at : at + size, cols] = mm(act[start : start + size, :], down_ref[:, cols])

        columns(body)

    near_copy, back = exchange(hid, 0, up_stage, down_product, lambda: relay_lane(1))
    relay_lane(2)
    vecs_ref[...] = jnp.zeros_like(vecs_ref)
    near_copy.wait_recv()

    def norm_two(at, h, local):
        downward = near[0, at, :] + near_in[0, at, :] + low_in[h, local, :].astype(F32)
        values = hidden[at, :] + downward + vec_ref[4:5, :]
        normed, unit, root = norm_forward(values, vec_ref[5:6, :], vec_ref[6:7, :])
        out_ref[at, :] = normed.astype(BF16)
        grad, gain, shift = norm_backward(full_ref[at, :], unit, root, vec_ref[5:6, :])
        two[at, :] = grad
        low = grad.astype(BF16)
        gdn[at, :] = low
        vecs_ref[5:6, :] += gain[None]
        vecs_ref[6:7, :] += shift[None]
        vecs_ref[4:5, :] += jnp.sum(low.astype(F32), axis=0, keepdims=True)

    def by_half(body, h, size=64):
        @pl.loop(0, half // size)
        def _(t):
            local = pl.multiple_of(t * size, size)
            body(pl.ds(h * half + local, size), h, pl.ds(local, size))

    for h in range(2):
        back[h].wait_recv()
        by_half(norm_two, h)

    def back_stage(start, size):
        def body(cols):
            grads = contract(gdn[start : start + size, :], down_ref[cols, :], 1, 1)
            low = (grads * slope[start : start + size, cols]).astype(BF16)
            gup[start : start + size, cols] = low
            vecs_ref[3:4, cols] += jnp.sum(low.astype(F32), axis=0, keepdims=True)

        columns(body)

    def back_product(start, size, target, at):
        def body(cols):
            target[at : at + size, cols] = contract(
                gup[start : start + size, :], up_ref[cols, :], 1, 1)

        columns(body)

    def last_relays():
        for r in range(3, n_ctx):
            relay_lane(r)

    near_copy, back = exchange(gdn, 1, back_stage, back_product, last_relays)
    near_copy.wait_recv()

    def norm_back(at, h, local):
        grad = near[1, at, :] + near_in[1, at, :] + low_in[2 + h, local, :].astype(F32)
        grad = grad + two[at, :]
        root = roots[0, at, 0:1]
        one, gain, shift = norm_backward(grad, unit_one[at, :], root, vec_ref[1:2, :])
        one_ref[at, :] = one
        low = one.astype(BF16)
        att_ref[at, :] = low
        vecs_ref[1:2, :] += gain[None]
        vecs_ref[2:3, :] += shift[None]
        vecs_ref[0:1, :] += jnp.sum(low.astype(F32), axis=0, keepdims=True)

    for h in range(2):
        back[h].wait_recv()
        by_half(norm_back, h)
    launch(att_ref.at[pl.ds(0, rows)], att_ref.at[pl.ds(rows, rows)], twin).wait_recv()

    def merged_product(cols):
        gm[:, cols] = contract(att_ref[...], wo_ref[cols, :], 1, 1).astype(BF16)

    columns(merged_product, wo_ref.shape[0] // tile)
    for k in range(n_ctx * n_x):
        of = slice(k * HD, (k + 1) * HD)
        for h in range(owners):
            for t in range(slots):
                at = (h * slots + t) * 2 * packed
                heads_out[k, h, t] = jnp.concatenate(
                    [gm[at : at + packed, of], gm[at + packed : at + 2 * packed, of]], axis=1)
    returns = [
        pltpu.make_async_remote_copy(
            heads_out.at[z * n_x + a], heads_back.at[chip], back_send.at[o], back_recv.at[chip],
            device_id=at_device(ctx=z, x=a), device_id_type=MESH)
        for o, (z, a) in enumerate(others)
    ]
    for copy in returns:
        copy.start()
    heads_back[chip] = heads_out[chip]

    half_tile = tile // 2

    @pl.loop(0, width // tile)
    def _(t):
        cols = pl.ds(pl.multiple_of(t * tile, tile), tile)
        down_grad = contract(act[:, cols], gdn[...], 0, 0).astype(BF16)
        up_grad = contract(hid[:, cols], gup[...], 0, 0).astype(BF16)
        for piece in range(2):
            of = slice(piece * half_tile, (piece + 1) * half_tile)
            d_down_ref[2 * t + piece] = down_grad[of]
            d_up_ref[2 * t + piece] = up_grad[of]

    for o, (z, a) in enumerate(others):
        source = z * n_x + a
        pltpu.make_async_remote_copy(
            heads_out.at[source], heads_back.at[source], back_send.at[o], back_recv.at[source],
            device_id=twin, device_id_type=MESH).wait_recv()
    for k in range(n_ctx * n_x):
        for h in range(owners):
            owner = core if h == 0 else 1 - core
            at = pl.multiple_of((2 * k + owner) * 2 * packed, 2 * packed)
            for t in range(slots):
                block = heads_back[k, h, t]
                ghead_ref[t, pl.ds(at, packed), :] = block[:, :HD]
                ghead_ref[t, pl.ds(at + packed, packed), :] = block[:, HD:]
    end_lane()
    for copy in started + pushes + returns:
        copy.wait_send()


def layer(sent, tokens, w_out, up, down, vectors, grad_full, lane_shard):
    n_ctx, n_x = lax.axis_size("ctx"), lax.axis_size("x")
    chips = n_ctx * n_x
    rows, width = tokens.shape
    hidden = up.shape[1]
    lane = w_out.shape[0]
    slots = sent.shape[2]
    vmem = pl.BlockSpec(memory_space=pltpu.VMEM)
    anywhere = pl.BlockSpec(memory_space=pl.ANY)
    dma = pltpu.SemaphoreType.DMA

    def shape(*dims, dtype=BF16):
        return jax.ShapeDtypeStruct(dims, dtype)

    def wide(*dims):
        return pltpu.VMEM(dims, F32)

    def low(*dims):
        return pltpu.VMEM(dims, BF16)

    return pl.pallas_call(
        partial(layer_kernel, n_ctx=n_ctx, n_x=n_x),
        in_specs=[vmem] * 8,
        out_specs=[vmem] * 8 + [anywhere],
        out_shape=[
            shape(2 * rows, lane),
            shape(rows, width),
            shape(rows, width, dtype=F32),
            shape(slots, 2 * chips * (rows // slots), HD),
            shape(2 * rows, width),
            shape(8, width, dtype=F32),
            shape(chips, hidden // chips, width),
            shape(chips, width // chips, hidden),
            shape(chips, *lane_shard.shape),
        ],
        scratch_shapes=[
            wide(2 * rows, width),
            wide(rows, width),
            low(4 * rows, width),
            low(4 * rows, hidden),
            wide(4 * rows, hidden),
            low(4 * rows, width),
            low(4 * rows, hidden),
            wide(rows, width),
            wide(rows, width),
            wide(rows, width),
            wide(1, rows, 128),
            wide(2, 2 * rows, width),
            wide(2, rows, width),
            wide(2, 2 * rows, width),
            wide(4, rows // 2, width),
            low(4, rows // 2, width),
            low(4, rows // 2, width),
            dma((24,)),
            dma((24,)),
            dma((5,)),
            dma((3, chips)),
            dma((chips,)),
            low(*sent.shape),
            dma((chips - 1,)),
            dma((chips,)),
            low(2 * rows, lane),
            low(*sent.shape),
            low(*sent.shape),
            dma((chips - 1,)),
            dma((chips,)),
        ],
        compiler_params=pltpu.CompilerParams(
            collective_id=3, has_side_effects=True, vmem_limit_bytes=VMEM_LIMIT
        ),
        cost_estimate=pl.CostEstimate(
            flops=16 * rows * width * hidden, bytes_accessed=16 * rows * width, transcendentals=0
        ),
        name="layer",
    )(sent, tokens, w_out, up, down, vectors, grad_full, lane_shard)


def head_device(
    tokens,
    lengths,
    w_qkv,
    b_qkv,
    w_out,
    b_out,
    ln1_gain,
    ln1_bias,
    w_up,
    b_up,
    w_down,
    b_down,
    ln2_gain,
    ln2_bias,
    w_proj,
    cot_out,
    cot_emb,
):
    n_lane = lax.axis_size("ctx") * lax.axis_size("x")
    n_group = 2 * n_lane
    core = lax.axis_index("core")
    slot = lax.axis_index("slot")
    chip = lax.axis_index("ctx") * lax.axis_size("x") + lax.axis_index("x")
    me = 2 * chip + core
    slots, part, width = tokens.shape
    seq = part * n_group
    rows = slots * part
    shard = width // n_group
    ff_shard = w_down.shape[0]
    ff_half = ff_shard // 2
    proj = w_proj.shape[1]
    head_cols = 3 * HD

    small = jnp.concatenate(
        [b_qkv, b_out, ln1_gain, ln1_bias, b_up, b_down, ln2_gain, ln2_bias]
    )
    small_at = [0]
    for piece in (b_qkv, b_out, ln1_gain, ln1_bias, b_up, b_down, ln2_gain, ln2_bias):
        small_at.append(small_at[-1] + piece.shape[0])
    small_rows = -(-small.shape[0] // proj)
    small_rows = -(-small_rows // 16) * 16
    small = jnp.pad(small, (0, small_rows * proj - small.shape[0])).reshape(small_rows, proj)
    def two_lanes(mine, theirs):
        low_first = jnp.stack([mine, theirs], axis=0)
        high_first = jnp.stack([theirs, mine], axis=0)
        return jnp.where(core == 0, low_first, high_first)

    up_split = w_up.reshape(shard, n_lane, 2, 2, ff_half)
    up_mine = pick(up_split, core, 2)
    up_theirs = swap_core(pick(up_split, 1 - core, 2))
    up_chip = two_lanes(pick(up_mine, slot, 2), pick(up_theirs, slot, 2))
    down_split = w_down.reshape(2, ff_half, width)

    by_head = w_qkv.reshape(shard, 3, n_group, HD).transpose(2, 0, 1, 3)
    all_tokens, my_head, packed = gather_start(
        tokens,
        by_head.reshape(n_group, shard, head_cols),
        jnp.concatenate([w_proj, small], axis=0),
    )
    proj_full = packed[:, :shard].reshape(width, proj)
    smalls = packed[:, shard:].reshape(n_group, small_rows * proj).astype(F32)
    qkv_bias, out_bias, gain_one, shift_one, up_bias, down_bias, gain_two, shift_two = (
        smalls[:, a:b].reshape(-1) for a, b in zip(small_at[:-1], small_at[1:])
    )

    head_weight = my_head.reshape(width, head_cols)
    all_tokens = all_tokens.reshape(slots * seq, width)
    head_bias = pick(qkv_bias.reshape(1, 3, n_group, HD), me, 2).reshape(1, head_cols)
    cosine, sine = rope_rows(jnp.arange(seq, dtype=jnp.int32).astype(F32))
    cos_wide = jnp.tile(cosine, (1, 4))
    sin_wide = jnp.tile(sine, (1, 4))
    queries, keys, values, mixture, send, norms, out_lane, up, down = heads(
        lengths,
        all_tokens,
        head_weight,
        head_bias,
        cos_wide,
        sin_wide,
        part,
        w_out,
        up_chip.reshape(2 * shard, n_lane * ff_half),
        pick(down_split, slot, 0),
    )
    out_lane, up, down = (t.reshape(-1, t.shape[2]) for t in (out_lane, up, down))
    bias_lane = pick(up_bias.reshape(n_lane, 2, 2, ff_half), core, 1)
    up_bias_own = pick(bias_lane, slot, 1).reshape(-1)

    qkv_split = w_qkv.reshape(shard, 3, n_lane, 2, HD)
    qkv_mine = pick(qkv_split, core, 3)
    qkv_theirs = swap_core(pick(qkv_split, 1 - core, 3))
    qkv_chip = two_lanes(qkv_mine, qkv_theirs).transpose(3, 0, 1, 2, 4)
    qkv_chip = qkv_chip.reshape(n_lane, 2 * shard, head_cols)

    place = me * part + jnp.arange(part, dtype=jnp.int32)
    live = (place[None, :] < lengths[:, None]).reshape(rows, 1)
    grad_out = jnp.where(live, cot_out.reshape(rows, width).astype(F32), 0.0)
    grad_emb = jnp.where(live, cot_emb.reshape(rows, proj), 0)
    grad_full = grad_out + contract(grad_emb, proj_full, 1, 1)
    vectors = jnp.stack(
        [out_bias, gain_one, shift_one, up_bias_own, down_bias, gain_two, shift_two, shift_two]
    )
    (
        merged,
        out_low,
        grad_one,
        grad_heads,
        grad_att,
        vector_grads,
        d_down,
        d_up,
        qkv_lane,
    ) = layer(
        send, tokens.reshape(rows, width), out_lane, up, down, vectors, grad_full, qkv_chip
    )
    embeds = mm(out_low, proj_full).astype(BF16)
    d_proj = contract(out_low, grad_emb, 0, 0)
    (
        d_out_bias,
        d_gain_one,
        d_shift_one,
        up_bias_own_grad,
        d_down_bias,
        d_gain_two,
        d_shift_two,
    ) = (vector_grads[i] for i in range(7))
    d_out = contract(merged, grad_att, 0, 0).astype(BF16)

    spread = (
        (jnp.arange(2) == core)[:, None, None] & (jnp.arange(2) == slot)[None, :, None]
    ).astype(F32)
    up_bias_grad = up_bias_own_grad.reshape(n_lane, 1, 1, ff_half) * spread[None]
    vectors = (
        d_out_bias,
        d_gain_one,
        d_shift_one,
        up_bias_grad.reshape(-1),
        d_down_bias,
        d_gain_two,
        d_shift_two,
    )
    small_grad = jnp.concatenate([v.reshape(n_group, -1) for v in vectors], axis=1)
    small_cols = small_grad.shape[1]
    vec_rows = -(-small_cols // proj)
    vec_rows = -(-(shard + vec_rows) // 16) * 16 - shard
    small_grad = jnp.pad(small_grad, ((0, 0), (0, vec_rows * proj - small_cols)))
    small_grad = jnp.concatenate(
        [d_proj.reshape(n_group, shard, proj), small_grad.reshape(n_group, vec_rows, proj)], axis=1
    )
    row_dots = jnp.sum(grad_heads.astype(F32) * mixture, axis=-1).reshape(slots, 1, seq)
    joined, d_qkv, reduced, out_sum, small_sum = grads(
        lengths,
        queries,
        keys,
        values,
        grad_heads,
        norms,
        row_dots,
        all_tokens,
        cos_wide,
        sin_wide,
        d_down,
        d_up,
        d_out.reshape(n_lane, shard, width),
        small_grad.astype(BF16),
        part,
    )
    grad_w_down, grad_w_up, grad_w_out, small_sum, grad_w_qkv, bias_rows, input_grad = finish_grads(
        out_sum,
        small_sum,
        d_qkv,
        reduced,
        joined,
        qkv_lane,
        grad_one,
    )
    grad_w_proj = small_sum[:shard]
    vec_sum = small_sum[shard:].reshape(-1)
    vec_outs = []
    at = 0
    for v in vectors:
        size = v.size // n_group
        vec_outs.append(vec_sum[at : at + size])
        at += size
    (
        grad_b_out,
        grad_gain_one,
        grad_shift_one,
        grad_b_up,
        grad_b_down,
        grad_gain_two,
        grad_shift_two,
    ) = vec_outs

    qkv_bias_grad = bias_rows.reshape(n_group, 3, HD).transpose(1, 0, 2).reshape(-1)
    grad_b_qkv = lax.dynamic_slice(qkv_bias_grad, (me * b_qkv.shape[0],), (b_qkv.shape[0],))

    return (
        out_low.reshape(slots, part, width),
        embeds.reshape(slots, part, proj),
        input_grad.reshape(slots, part, width),
        grad_w_qkv,
        grad_b_qkv,
        grad_w_out,
        grad_b_out,
        grad_gain_one,
        grad_shift_one,
        grad_w_up,
        grad_b_up,
        grad_w_down,
        grad_b_down,
        grad_gain_two,
        grad_shift_two,
        grad_w_proj,
    )


def layer_norm(hidden, gain, shift):
    center = hidden - jnp.mean(hidden, axis=-1, keepdims=True)
    spread = jnp.mean(center * center, axis=-1, keepdims=True)
    return center * lax.rsqrt(spread + LN_EPS) * gain + shift


def rope_tables(positions, head_width):
    halfway = head_width // 2
    ladder = jnp.arange(halfway, dtype=jnp.float32) * (2.0 / head_width)
    frequency = jnp.power(jnp.float32(10000.0), -ladder)
    angles = positions[:, None] * frequency[None, :]
    return (jnp.cos(angles)[:, None, :], jnp.sin(angles)[:, None, :])


def rotate(values, cosine, sine_part):
    halfway = values.shape[-1] // 2
    first_half = values[..., :halfway]
    second_half = values[..., halfway:]
    return jnp.concatenate(
        [
            first_half * cosine - second_half * sine_part,
            second_half * cosine + first_half * sine_part,
        ],
        axis=-1,
    )


def block_scores(query_block, key_block, key_start, length, scale):
    scores = (
        jnp.einsum("qhd,khd->hqk", query_block, key_block, preferred_element_type=jnp.float32)
        * scale
    )
    key_ids = key_start + jnp.arange(key_block.shape[0], dtype=jnp.int32)
    return jnp.where((key_ids < length)[None, None, :], scores, NEG_FILL)


def per_device(
    tokens,
    lengths,
    w_qkv,
    b_qkv,
    w_out,
    b_out,
    ln1_gain,
    ln1_bias,
    w_up,
    b_up,
    w_down,
    b_down,
    ln2_gain,
    ln2_bias,
    w_proj,
    cot_out,
    cot_emb,
):
    n_fsdp = lax.axis_size("fsdp")
    n_ctx = lax.axis_size("ctx")
    ctx_at = lax.axis_index("ctx")
    fsdp_at = lax.axis_index("fsdp")
    groups, tok_slot, width = tokens.shape
    heads_here = H // n_fsdp
    lane_width = heads_here * HD
    span_rows = tok_slot * n_fsdp
    key_count = span_rows * n_ctx
    row_count = groups * tok_slot
    scale = HD ** (-0.5)
    query_rows = min(512, span_rows)
    key_rows = min(2048, key_count // 4)
    query_blocks = span_rows // query_rows
    key_blocks = key_count // key_rows
    key_starts = jnp.arange(key_blocks, dtype=jnp.int32) * key_rows
    qkv_full, qkv_bias, out_full, out_bias, gain_one, shift_one = (
        lax.all_gather(w_qkv, ("ctx", "fsdp"), axis=0, tiled=True),
        lax.all_gather(b_qkv, ("ctx", "fsdp"), axis=0, tiled=True),
        lax.all_gather(w_out, ("ctx", "fsdp"), axis=0, tiled=True),
        lax.all_gather(b_out, ("ctx", "fsdp"), axis=0, tiled=True),
        lax.all_gather(ln1_gain, ("ctx", "fsdp"), axis=0, tiled=True),
        lax.all_gather(ln1_bias, ("ctx", "fsdp"), axis=0, tiled=True),
    )
    token_pos = (ctx_at * n_fsdp + fsdp_at) * tok_slot + jnp.arange(tok_slot, dtype=jnp.int32)
    live_rows = (token_pos[None, :] < lengths[:, None]).reshape(row_count, 1)
    flat_tokens = tokens.reshape(row_count, width)
    joined = jnp.dot(flat_tokens, qkv_full, preferred_element_type=jnp.float32) + qkv_bias.astype(
        jnp.float32
    )
    cosine, sine_part = rope_tables(token_pos.astype(jnp.float32), HD)
    split_heads = joined.reshape(groups, tok_slot, 3, H, HD)
    rotated_query = rotate(split_heads[:, :, 0], cosine, sine_part)
    rotated_key = rotate(split_heads[:, :, 1], cosine, sine_part)
    packed = (
        jnp.stack([rotated_query, rotated_key, split_heads[:, :, 2]], axis=2)
        .astype(jnp.bfloat16)
        .reshape(groups, tok_slot, 3, n_fsdp, lane_width)
    )
    by_heads = lax.all_to_all(packed, "fsdp", split_axis=3, concat_axis=1, tiled=True)
    queries = by_heads[:, :, 0, 0]
    local_keys = by_heads[:, :, 1, 0]
    local_values = by_heads[:, :, 2, 0]
    all_keys, all_values = (
        lax.all_gather(local_keys, "ctx", axis=1, tiled=True),
        lax.all_gather(local_values, "ctx", axis=1, tiled=True),
    )

    def attend_slot(slot_item):
        slot_queries, slot_keys, slot_values, length = slot_item
        query_split = slot_queries.reshape(query_blocks, query_rows, heads_here, HD)
        key_split = slot_keys.reshape(key_blocks, key_rows, heads_here, HD)
        value_split = slot_values.reshape(key_blocks, key_rows, heads_here, HD)

        def per_query(query_block):

            def row_stats(state_pair, key_item):
                highest, running_sum = state_pair
                scores = block_scores(query_block, key_item[0], key_item[1], length, scale)
                new_high = jnp.maximum(highest, jnp.max(scores, axis=-1))
                running_sum = running_sum * jnp.exp(highest - new_high) + jnp.sum(
                    jnp.exp(scores - new_high[..., None]), axis=-1
                )
                return ((new_high, running_sum), None)

            start_state = (
                jnp.full((heads_here, query_rows), NEG_FILL, jnp.float32),
                jnp.zeros((heads_here, query_rows), jnp.float32),
            )
            highest, running_sum = lax.scan(row_stats, start_state, (key_split, key_starts))[0]
            log_norm = highest + jnp.log(running_sum)

            def weigh_values(accumulated, key_item):
                scores = block_scores(query_block, key_item[0], key_item[2], length, scale)
                weights = jnp.exp(scores - log_norm[..., None]).astype(jnp.bfloat16)
                return (
                    accumulated
                    + jnp.einsum(
                        "hqk,khd->qhd", weights, key_item[1], preferred_element_type=jnp.float32
                    ),
                    None,
                )

            mixture = lax.scan(
                weigh_values,
                jnp.zeros((query_rows, heads_here, HD), jnp.float32),
                (key_split, value_split, key_starts),
            )[0]
            return (mixture, log_norm)

        mixture, log_norm = lax.map(per_query, query_split)
        return (mixture.reshape(span_rows, lane_width), log_norm)

    mixture, log_norms = lax.map(attend_slot, (queries, all_keys, all_values, lengths))
    merged = lax.all_to_all(
        mixture.astype(jnp.bfloat16).reshape(groups, span_rows, 1, lane_width),
        "fsdp",
        split_axis=1,
        concat_axis=2,
        tiled=True,
    ).reshape(row_count, width)
    attended = jnp.dot(merged, out_full, preferred_element_type=jnp.float32) + out_bias.astype(
        jnp.float32
    )
    hidden_one, pull_one = jax.vjp(
        layer_norm,
        flat_tokens.astype(jnp.float32) + attended,
        gain_one.astype(jnp.float32),
        shift_one.astype(jnp.float32),
    )
    hidden_low = hidden_one.astype(jnp.bfloat16)
    up_full, up_bias, down_full, down_bias, gain_two, shift_two, proj_full = (
        lax.all_gather(w_up, ("ctx", "fsdp"), axis=0, tiled=True),
        lax.all_gather(b_up, ("ctx", "fsdp"), axis=0, tiled=True),
        lax.all_gather(w_down, ("ctx", "fsdp"), axis=0, tiled=True),
        lax.all_gather(b_down, ("ctx", "fsdp"), axis=0, tiled=True),
        lax.all_gather(ln2_gain, ("ctx", "fsdp"), axis=0, tiled=True),
        lax.all_gather(ln2_bias, ("ctx", "fsdp"), axis=0, tiled=True),
        lax.all_gather(w_proj, ("ctx", "fsdp"), axis=0, tiled=True),
    )
    upward = jnp.dot(hidden_low, up_full, preferred_element_type=jnp.float32) + up_bias.astype(
        jnp.float32
    )
    active_full, pull_gelu = jax.vjp(partial(jax.nn.gelu, approximate=False), upward)
    active = active_full.astype(jnp.bfloat16)
    downward = jnp.dot(active, down_full, preferred_element_type=jnp.float32) + down_bias.astype(
        jnp.float32
    )
    out_full_rows, pull_two = jax.vjp(
        layer_norm,
        hidden_one + downward,
        gain_two.astype(jnp.float32),
        shift_two.astype(jnp.float32),
    )
    out_low = out_full_rows.astype(jnp.bfloat16)
    projected = jnp.dot(out_low, proj_full, preferred_element_type=jnp.float32)
    back_qkv, back_qkv_bias, back_out, back_out_bias, back_gain_one, back_shift_one = (
        lax.all_gather(w_qkv, ("ctx", "fsdp"), axis=0, tiled=True),
        lax.all_gather(b_qkv, ("ctx", "fsdp"), axis=0, tiled=True),
        lax.all_gather(w_out, ("ctx", "fsdp"), axis=0, tiled=True),
        lax.all_gather(b_out, ("ctx", "fsdp"), axis=0, tiled=True),
        lax.all_gather(ln1_gain, ("ctx", "fsdp"), axis=0, tiled=True),
        lax.all_gather(ln1_bias, ("ctx", "fsdp"), axis=0, tiled=True),
    )
    back_up, back_up_bias, back_down, back_down_bias, back_gain_two, back_shift_two, back_proj = (
        lax.all_gather(w_up, ("ctx", "fsdp"), axis=0, tiled=True),
        lax.all_gather(b_up, ("ctx", "fsdp"), axis=0, tiled=True),
        lax.all_gather(w_down, ("ctx", "fsdp"), axis=0, tiled=True),
        lax.all_gather(b_down, ("ctx", "fsdp"), axis=0, tiled=True),
        lax.all_gather(ln2_gain, ("ctx", "fsdp"), axis=0, tiled=True),
        lax.all_gather(ln2_bias, ("ctx", "fsdp"), axis=0, tiled=True),
        lax.all_gather(w_proj, ("ctx", "fsdp"), axis=0, tiled=True),
    )
    grad_out = jnp.where(live_rows, cot_out.reshape(row_count, width).astype(jnp.float32), 0.0)
    grad_emb = jnp.where(live_rows, cot_emb.reshape(row_count, -1), 0)
    d_proj = jnp.einsum("rd,rp->dp", out_low, grad_emb, preferred_element_type=jnp.float32)
    grad_full = grad_out + jnp.einsum(
        "rp,dp->rd", grad_emb, back_proj, preferred_element_type=jnp.float32
    )
    grad_two, d_gain_two, d_shift_two = pull_two(grad_full)
    grad_down = grad_two.astype(jnp.bfloat16)
    d_down = jnp.einsum("rf,rd->fd", active, grad_down, preferred_element_type=jnp.float32)
    d_down_bias = jnp.sum(grad_down.astype(jnp.float32), axis=0)
    grad_act = jnp.einsum("rd,fd->rf", grad_down, back_down, preferred_element_type=jnp.float32)
    grad_up = pull_gelu(grad_act)[0].astype(jnp.bfloat16)
    d_up = jnp.einsum("rd,rf->df", hidden_low, grad_up, preferred_element_type=jnp.float32)
    d_up_bias = jnp.sum(grad_up.astype(jnp.float32), axis=0)
    grad_hidden = grad_two + jnp.einsum(
        "rf,df->rd", grad_up, back_up, preferred_element_type=jnp.float32
    )
    grad_one, d_gain_one, d_shift_one = pull_one(grad_hidden)
    grad_att = grad_one.astype(jnp.bfloat16)
    d_out = jnp.einsum("rd,re->de", merged, grad_att, preferred_element_type=jnp.float32)
    d_out_bias = jnp.sum(grad_att.astype(jnp.float32), axis=0)
    grad_merged = jnp.einsum(
        "re,de->rd", grad_att, back_out, preferred_element_type=jnp.float32
    ).astype(jnp.bfloat16)
    grad_heads = lax.all_to_all(
        grad_merged.reshape(groups, tok_slot, n_fsdp, lane_width),
        "fsdp",
        split_axis=2,
        concat_axis=1,
        tiled=True,
    ).reshape(groups, span_rows, lane_width)

    def attend_back(slot_item):
        slot_queries, slot_keys, slot_values, grad_mix, log_norm, length = slot_item
        query_split = slot_queries.reshape(query_blocks, query_rows, heads_here, HD)
        key_split = slot_keys.reshape(key_blocks, key_rows, heads_here, HD)
        value_split = slot_values.reshape(key_blocks, key_rows, heads_here, HD)
        grad_split = grad_mix.reshape(query_blocks, query_rows, heads_here, HD)

        def value_pass(value_total, query_item):
            query_block, grad_block, norm_block = query_item

            def value_per_key(row_dot, key_item):
                key_block, value_block, key_start = key_item
                scores = block_scores(query_block, key_block, key_start, length, scale)
                probability = jnp.exp(scores - norm_block[..., None])
                grad_probs = jnp.einsum(
                    "qhd,khd->hqk", grad_block, value_block, preferred_element_type=jnp.float32
                )
                value_part = jnp.einsum(
                    "hqk,qhd->khd",
                    probability.astype(jnp.bfloat16),
                    grad_block,
                    preferred_element_type=jnp.float32,
                )
                return (row_dot + jnp.sum(probability * grad_probs, axis=-1), value_part)

            row_dot, value_parts = lax.scan(
                value_per_key,
                jnp.zeros((heads_here, query_rows), jnp.float32),
                (key_split, value_split, key_starts),
            )
            return (value_total + value_parts.reshape(key_count, heads_here, HD), row_dot)

        value_grad, row_dots = lax.scan(
            value_pass,
            jnp.zeros((key_count, heads_here, HD), jnp.float32),
            (query_split, grad_split, log_norm),
        )

        def key_pass(key_total, query_item):
            query_block, grad_block, norm_block, dot_block = query_item

            def key_per_key(query_accum, key_item):
                key_block, value_block, key_start = key_item
                scores = block_scores(query_block, key_block, key_start, length, scale)
                probability = jnp.exp(scores - norm_block[..., None])
                grad_probs = jnp.einsum(
                    "qhd,khd->hqk", grad_block, value_block, preferred_element_type=jnp.float32
                )
                grad_scores = (probability * (grad_probs - dot_block[..., None])).astype(
                    jnp.bfloat16
                )
                query_accum = query_accum + jnp.einsum(
                    "hqk,khd->qhd", grad_scores, key_block, preferred_element_type=jnp.float32
                )
                key_part = jnp.einsum(
                    "hqk,qhd->khd", grad_scores, query_block, preferred_element_type=jnp.float32
                )
                return (query_accum, key_part)

            query_grad, key_parts = lax.scan(
                key_per_key,
                jnp.zeros((query_rows, heads_here, HD), jnp.float32),
                (key_split, value_split, key_starts),
            )
            return (key_total + key_parts.reshape(key_count, heads_here, HD), query_grad)

        key_grad, query_grads = lax.scan(
            key_pass,
            jnp.zeros((key_count, heads_here, HD), jnp.float32),
            (query_split, grad_split, log_norm, row_dots),
        )
        return (
            query_grads.reshape(span_rows, lane_width) * scale,
            key_grad.reshape(key_count, lane_width) * scale,
            value_grad.reshape(key_count, lane_width),
        )

    grad_queries, key_terms, value_terms = lax.map(
        attend_back, (queries, all_keys, all_values, grad_heads, log_norms, lengths)
    )
    grad_keys, grad_values = (
        lax.psum_scatter(
            key_terms.astype(jnp.bfloat16), "ctx", scatter_dimension=1, tiled=True
        ).astype(jnp.float32),
        lax.psum_scatter(
            value_terms.astype(jnp.bfloat16), "ctx", scatter_dimension=1, tiled=True
        ).astype(jnp.float32),
    )
    head_pos = (ctx_at * span_rows + jnp.arange(span_rows, dtype=jnp.int32)).astype(jnp.float32)
    head_cosine, head_sine = rope_tables(head_pos, HD)
    query_back = rotate(
        grad_queries.reshape(groups, span_rows, heads_here, HD), head_cosine, -head_sine
    )
    key_back = rotate(grad_keys.reshape(groups, span_rows, heads_here, HD), head_cosine, -head_sine)
    value_back = grad_values.reshape(groups, span_rows, heads_here, HD)
    grad_pack = (
        jnp.stack([query_back, key_back, value_back], axis=2)
        .astype(jnp.bfloat16)
        .reshape(groups, span_rows, 3, 1, lane_width)
    )
    grad_joined = lax.all_to_all(
        grad_pack, "fsdp", split_axis=1, concat_axis=3, tiled=True
    ).reshape(row_count, 3 * width)
    d_qkv = jnp.einsum("rd,re->de", flat_tokens, grad_joined, preferred_element_type=jnp.float32)
    d_qkv_bias = jnp.sum(grad_joined.astype(jnp.float32), axis=0)
    input_grad = (
        jnp.einsum("re,de->rd", grad_joined, back_qkv, preferred_element_type=jnp.float32)
        + grad_one
    ).astype(jnp.bfloat16)
    shards = (
        lax.psum_scatter(d_qkv, ("ctx", "fsdp"), scatter_dimension=0, tiled=True),
        lax.psum_scatter(d_qkv_bias, ("ctx", "fsdp"), scatter_dimension=0, tiled=True),
        lax.psum_scatter(d_out, ("ctx", "fsdp"), scatter_dimension=0, tiled=True),
        lax.psum_scatter(d_out_bias, ("ctx", "fsdp"), scatter_dimension=0, tiled=True),
        lax.psum_scatter(d_gain_one, ("ctx", "fsdp"), scatter_dimension=0, tiled=True),
        lax.psum_scatter(d_shift_one, ("ctx", "fsdp"), scatter_dimension=0, tiled=True),
        lax.psum_scatter(d_up, ("ctx", "fsdp"), scatter_dimension=0, tiled=True),
        lax.psum_scatter(d_up_bias, ("ctx", "fsdp"), scatter_dimension=0, tiled=True),
        lax.psum_scatter(d_down, ("ctx", "fsdp"), scatter_dimension=0, tiled=True),
        lax.psum_scatter(d_down_bias, ("ctx", "fsdp"), scatter_dimension=0, tiled=True),
        lax.psum_scatter(d_gain_two, ("ctx", "fsdp"), scatter_dimension=0, tiled=True),
        lax.psum_scatter(d_shift_two, ("ctx", "fsdp"), scatter_dimension=0, tiled=True),
        lax.psum_scatter(d_proj, ("ctx", "fsdp"), scatter_dimension=0, tiled=True),
    )
    totals = (
        lax.psum(shards[0].astype(jnp.bfloat16), "slot").astype(jnp.float32),
        lax.psum(shards[1].astype(jnp.bfloat16), "slot").astype(jnp.float32),
        lax.psum(shards[2].astype(jnp.bfloat16), "slot").astype(jnp.float32),
        lax.psum(shards[3].astype(jnp.bfloat16), "slot").astype(jnp.float32),
        lax.psum(shards[4].astype(jnp.bfloat16), "slot").astype(jnp.float32),
        lax.psum(shards[5].astype(jnp.bfloat16), "slot").astype(jnp.float32),
        lax.psum(shards[6].astype(jnp.bfloat16), "slot").astype(jnp.float32),
        lax.psum(shards[7].astype(jnp.bfloat16), "slot").astype(jnp.float32),
        lax.psum(shards[8].astype(jnp.bfloat16), "slot").astype(jnp.float32),
        lax.psum(shards[9].astype(jnp.bfloat16), "slot").astype(jnp.float32),
        lax.psum(shards[10].astype(jnp.bfloat16), "slot").astype(jnp.float32),
        lax.psum(shards[11].astype(jnp.bfloat16), "slot").astype(jnp.float32),
        lax.psum(shards[12].astype(jnp.bfloat16), "slot").astype(jnp.float32),
    )
    return (
        out_low.reshape(groups, tok_slot, width),
        projected.astype(jnp.bfloat16).reshape(groups, tok_slot, -1),
        input_grad.reshape(groups, tok_slot, width),
        totals[0],
        totals[1],
        totals[2],
        totals[3],
        totals[4],
        totals[5],
        totals[6],
        totals[7],
        totals[8],
        totals[9],
        totals[10],
        totals[11],
        totals[12],
    )


def solution(mesh):
    n_slot, n_ctx, n_fsdp = (mesh.shape[a] for a in ("slot", "ctx", "fsdp"))
    rows_axes = ("ctx", "fsdp")
    step = per_device
    if n_slot == 2 and n_fsdp % 2 == 0 and n_ctx * n_fsdp == H:
        mesh = Mesh(
            mesh.devices.reshape(n_slot, n_ctx, n_fsdp // 2, 2), ("slot", "ctx", "x", "core")
        )
        rows_axes = GROUP
        step = head_device
    in_specs = (
        P("slot", rows_axes, None),
        P("slot"),
        P(rows_axes, None),
        P(rows_axes),
        P(rows_axes, None),
        P(rows_axes),
        P(rows_axes),
        P(rows_axes),
        P(rows_axes, None),
        P(rows_axes),
        P(rows_axes, None),
        P(rows_axes),
        P(rows_axes),
        P(rows_axes),
        P(rows_axes, None),
        P("slot", rows_axes, None),
        P("slot", rows_axes, None),
    )
    out_specs = (
        P("slot", rows_axes, None),
        P("slot", rows_axes, None),
        P("slot", rows_axes, None),
        P(rows_axes, None),
        P(rows_axes),
        P(rows_axes, None),
        P(rows_axes),
        P(rows_axes),
        P(rows_axes),
        P(rows_axes, None),
        P(rows_axes),
        P(rows_axes, None),
        P(rows_axes),
        P(rows_axes),
        P(rows_axes),
        P(rows_axes, None),
    )
    return jax.shard_map(
        step, mesh=mesh, in_specs=in_specs, out_specs=out_specs, check_vma=False
    )
```

```python
from functools import partial

import jax
import jax.numpy as jnp
from jax import lax
from jax.experimental import pallas as pl
from jax.experimental.pallas import tpu as pltpu
from jax.sharding import Mesh
from jax.sharding import PartitionSpec as P

H = 16
HD = 64
LN_EPS = 1e-05
NEG_FILL = -1e30
F32 = jnp.float32
BF16 = jnp.bfloat16
GROUP = ("ctx", "x", "core")
LANE = ("ctx", "x")
SWAP = [(0, 1), (1, 0)]
VMEM_LIMIT = 60 * 1024 * 1024


def mm(left, right):
    return jnp.dot(left, right, preferred_element_type=F32)


def contract(left, right, left_dim, right_dim):
    return lax.dot_general(
        left, right, (((left_dim,), (right_dim,)), ((), ())), preferred_element_type=F32
    )


def swap_core(value):
    return lax.ppermute(value, "core", SWAP)


def swap_slot(value):
    return lax.ppermute(value, "slot", SWAP)


def pick(stacked, index, axis):
    return lax.dynamic_index_in_dim(stacked, index, axis, keepdims=False)


MESH = pl.DeviceIdType.MESH


def at_device(**where):
    names = ("slot", "ctx", "x", "core")
    return tuple(where[n] if n in where else lax.axis_index(n) for n in names)


def greet(peers):
    barrier = pltpu.get_barrier_semaphore()
    for peer in peers:
        pl.semaphore_signal(barrier, inc=1, device_id=peer, device_id_type=MESH)
    pl.semaphore_wait(barrier, len(peers))


def group_peers(n_ctx, n_x):
    ctx, x, core = (lax.axis_index(n) for n in GROUP)
    peers = []
    for dz in range(n_ctx):
        for dx in range(n_x):
            for dc in range(2):
                if dz or dx or dc:
                    where = (lax.rem(ctx + dz, n_ctx), lax.rem(x + dx, n_x), lax.rem(core + dc, 2))
                    peers.append(where)
    return peers


def start_kernel(
    tok_ref, head_ref, small_ref, all_ref, heads_ref, smalls_ref,
    far_send, block_send, local_sem, head_recv, small_recv, block_recv, *, n_ctx, n_x
):
    part = tok_ref.shape[1]
    ctx, x, core = (lax.axis_index(n) for n in GROUP)
    me = (ctx * n_x + x) * 2 + core
    peers = group_peers(n_ctx, n_x)
    greet([at_device(ctx=z, x=a, core=c) for z, a, c in peers])

    def block_at(b):
        return all_ref.at[:, pl.ds(pl.multiple_of(b * part, part), part), :]

    pushes = []
    for k, (z, a, c) in enumerate(peers):
        them = (z * n_x + a) * 2 + c
        target = at_device(ctx=z, x=a, core=c)
        pushes.append(pltpu.make_async_remote_copy(
            head_ref.at[them], heads_ref.at[me], far_send.at[2 * k], head_recv.at[me],
            device_id=target, device_id_type=MESH))
        pushes.append(pltpu.make_async_remote_copy(
            small_ref, smalls_ref.at[me], far_send.at[2 * k + 1], small_recv.at[me],
            device_id=target, device_id_type=MESH))
    locals_ = [
        pltpu.make_async_copy(tok_ref, block_at(me), local_sem.at[0]),
        pltpu.make_async_copy(head_ref.at[me], heads_ref.at[me], local_sem.at[1]),
        pltpu.make_async_copy(small_ref, smalls_ref.at[me], local_sem.at[2]),
    ]

    def send(b, source, lane, target):
        return pltpu.make_async_remote_copy(
            source, block_at(b), block_send.at[lane, b], block_recv.at[b],
            device_id=target, device_id_type=MESH)

    up = at_device(ctx=lax.rem(ctx + 1, n_ctx))
    down = at_device(ctx=lax.rem(ctx + n_ctx - 1, n_ctx))
    side = at_device(x=1 - x)
    twin = at_device(core=1 - core)

    def here(b):
        return send(b, block_at(b), 0, twin)

    @pl.when(ctx + 1 < n_ctx)
    def _():
        send(me, tok_ref, 0, up).start()

    @pl.when(ctx > 0)
    def _():
        send(me, tok_ref, 1, down).start()

    send(me, tok_ref, 2, side).start()
    send(me, tok_ref, 3, twin).start()
    for copy in locals_:
        copy.start()

    for r in range(1, n_ctx):
        if r == n_ctx - 1:
            for push in pushes:
                push.start()
        low = ctx - r
        high = ctx + r

        @pl.when(low >= 0)
        def _():
            b = (low * n_x + x) * 2 + core
            here(b).wait_recv()

            @pl.when(ctx + 1 < n_ctx)
            def _():
                send(b, block_at(b), 0, up).start()

            send(b, block_at(b), 2, side).start()
            send(b, block_at(b), 3, twin).start()

        @pl.when(high < n_ctx)
        def _():
            b = (high * n_x + x) * 2 + core
            here(b).wait_recv()

            @pl.when(ctx > 0)
            def _():
                send(b, block_at(b), 1, down).start()

            send(b, block_at(b), 2, side).start()
            send(b, block_at(b), 3, twin).start()

    def from_side(z):
        b = (z * n_x + (1 - x)) * 2 + core
        here(b).wait_recv()
        send(b, block_at(b), 3, twin).start()

    from_side(ctx)
    for r in range(1, n_ctx):
        @pl.when(ctx - r >= 0)
        def _():
            from_side(ctx - r)

        @pl.when(ctx + r < n_ctx)
        def _():
            from_side(ctx + r)

    for z in range(n_ctx):
        for a in range(n_x):
            here((z * n_x + a) * 2 + 1 - core).wait_recv()
    for k, (z, a, c) in enumerate(peers):
        them = (z * n_x + a) * 2 + c
        pltpu.make_async_remote_copy(
            head_ref.at[them], heads_ref.at[them], far_send.at[2 * k], head_recv.at[them],
            device_id=twin, device_id_type=MESH).wait_recv()
        pltpu.make_async_remote_copy(
            small_ref, smalls_ref.at[them], far_send.at[2 * k + 1], small_recv.at[them],
            device_id=twin, device_id_type=MESH).wait_recv()
    for push in pushes:
        push.wait_send()
    for copy in locals_:
        copy.wait()

    for z in range(n_ctx):
        b = (z * n_x + x) * 2 + core

        @pl.when((z <= ctx) & (ctx + 1 < n_ctx))
        def _():
            send(b, block_at(b), 0, up).wait_send()

        @pl.when((z >= ctx) & (ctx > 0))
        def _():
            send(b, block_at(b), 1, down).wait_send()

        send(b, block_at(b), 2, side).wait_send()
        send(b, block_at(b), 3, twin).wait_send()
        other = (z * n_x + (1 - x)) * 2 + core
        send(other, block_at(other), 3, twin).wait_send()


def gather_start(tokens, heads, small):
    n_ctx, n_x = lax.axis_size("ctx"), lax.axis_size("x")
    n = 2 * n_ctx * n_x
    slots, part, width = tokens.shape
    vmem = pl.BlockSpec(memory_space=pltpu.VMEM)
    anywhere = pl.BlockSpec(memory_space=pl.ANY)
    dma = pltpu.SemaphoreType.DMA
    return pl.pallas_call(
        partial(start_kernel, n_ctx=n_ctx, n_x=n_x),
        in_specs=[vmem, vmem, vmem],
        out_specs=[anywhere, vmem, vmem],
        out_shape=[
            jax.ShapeDtypeStruct((slots, n * part, width), tokens.dtype),
            jax.ShapeDtypeStruct(heads.shape, heads.dtype),
            jax.ShapeDtypeStruct((n,) + small.shape, small.dtype),
        ],
        scratch_shapes=[
            dma((2 * (n - 1),)), dma((4, n)), dma((3,)), dma((n,)), dma((n,)), dma((n,))
        ],
        compiler_params=pltpu.CompilerParams(
            collective_id=1, has_side_effects=True, vmem_limit_bytes=VMEM_LIMIT
        ),
        cost_estimate=pl.CostEstimate(
            flops=0, bytes_accessed=2 * n * tokens.size, transcendentals=0
        ),
        name="gather_start",
    )(tokens, heads, small)


def finish_kernel(
    out_ref, small_ref, qkv_ref, red_ref, join_ref, weight_ref, one_ref,
    g_down, g_up, g_out, g_small, g_qkv, g_bias, g_in,
    pair_small, pair_qkv, sum_qkv, qkvs,
    pair_down, pair_out, last_up, joins, partial_in, pair_in,
    join_send, join_recv, far_send, qkv_recv, y_send, y_recv,
    *, n_ctx, n_x
):
    ctx, x, core = (lax.axis_index(n) for n in GROUP)
    slot = lax.axis_index("slot")
    chip = ctx * n_x + x
    me = 2 * chip + core
    shard, width = g_out.shape
    part = g_down.shape[0] // 2
    peers = group_peers(n_ctx, n_x)
    lane_peers = [(z, a) for z, a, c in peers[1::2]]
    across = at_device(slot=1 - slot)
    corner = at_device(slot=1 - slot, core=1 - core)
    twin = at_device(core=1 - core)
    greet([at_device(ctx=z, x=a, core=c) for z, a, c in peers] + [across, corner])

    def remote(source, target_ref, send_sem, recv_sem, target):
        return pltpu.make_async_remote_copy(
            source, target_ref, send_sem, recv_sem, device_id=target, device_id_type=MESH)

    started = []

    def launch(copy):
        copy.start()
        started.append(copy)
        return copy

    def pair_copy(i, source, target_ref, target):
        return launch(remote(source, target_ref, y_send.at[i], y_recv.at[i], target))

    qkv_copy = pair_copy(0, qkv_ref, pair_qkv, across)
    mine = pl.multiple_of(part + core * shard, shard)
    theirs = pl.multiple_of(part + (1 - core) * shard, shard)
    for k, (z, a) in enumerate(lane_peers):
        launch(remote(
            join_ref.at[z * n_x + a], joins.at[chip], join_send.at[k], join_recv.at[chip],
            at_device(ctx=z, x=a)))
    down_copy = pair_copy(4, red_ref.at[pl.ds(0, part)], pair_down, across)
    quarter_copies = [
        pair_copy(5, red_ref.at[pl.ds(theirs, shard)], last_up.at[0], twin),
        pair_copy(6, red_ref.at[pl.ds(mine, shard)], last_up.at[1], across),
        pair_copy(7, red_ref.at[pl.ds(theirs, shard)], last_up.at[2], corner),
    ]

    small_copy = pair_copy(1, small_ref, pair_small, across)
    out_copy = pair_copy(3, out_ref, pair_out, across)
    qkv_copy.wait_recv()
    sum_qkv[...] = (qkv_ref[...].astype(F32) + pair_qkv[...].astype(F32)).astype(BF16)
    for k, (z, a, c) in enumerate(peers):
        them = (z * n_x + a) * 2 + c
        launch(remote(
            sum_qkv.at[them], qkvs.at[me], far_send.at[k], qkv_recv.at[me],
            at_device(ctx=z, x=a, core=c)))
    qkvs[me] = sum_qkv[me]

    def add_head(source, rows_of, first):
        weight = weight_ref[source]
        for h in range(2):
            owner = core if h == 0 else 1 - core
            rows = rows_of(owner)
            cols = rows.shape[2] // 2
            rows = jnp.concatenate(
                [r for t in range(rows.shape[0]) for r in (rows[t, :, :cols], rows[t, :, cols:])],
                axis=0)
            term = contract(rows, weight, 1, 1)
            partial_in[h] = term if first else partial_in[h] + term

    add_head(chip, lambda owner: join_ref[chip, owner], True)

    half = pl.multiple_of(slot * part, part)
    other_half = pl.multiple_of((1 - slot) * part, part)
    g_down[pl.ds(half, part), :] = red_ref[pl.ds(0, part), :].astype(F32)
    down_copy.wait_recv()
    g_down[pl.ds(other_half, part), :] = pair_down[...].astype(F32)

    def place_quarter(rows, quarter_core, quarter_slot):
        for k in range(n_ctx * n_x):
            at = pl.multiple_of(((2 * k + quarter_core) * 2 + quarter_slot) * part, part)
            g_up[:, pl.ds(at, part)] = rows[:, k * part : (k + 1) * part].astype(F32)

    place_quarter(red_ref[pl.ds(mine, shard), :], core, slot)
    quarter_copies[0].wait_recv()
    place_quarter(last_up[0], 1 - core, slot)
    quarter_copies[1].wait_recv()
    place_quarter(last_up[1], core, 1 - slot)
    quarter_copies[2].wait_recv()
    place_quarter(last_up[2], 1 - core, 1 - slot)

    @pl.loop(1, n_ctx * n_x)
    def _(o):
        source = lax.rem(ctx + o // n_x, n_ctx) * n_x + lax.rem(x + o % n_x, n_x)
        remote(
            join_ref.at[source], joins.at[source], join_send.at[0], join_recv.at[source], twin
        ).wait_recv()
        add_head(source, lambda owner: joins[source, owner], False)

    in_copy = pair_copy(2, partial_in.at[1], pair_in, twin)

    small_copy.wait_recv()
    g_small[...] = small_ref[...].astype(F32) + pair_small[...].astype(F32)
    in_copy.wait_recv()
    g_in[...] = (partial_in[0] + pair_in[...] + one_ref[...]).astype(BF16)
    for z, a, c in peers:
        them = (z * n_x + a) * 2 + c
        remote(
            sum_qkv.at[them], qkvs.at[them], far_send.at[0], qkv_recv.at[them], twin
        ).wait_recv()
    for k in range(n_ctx * n_x):
        heads = [qkvs[2 * k + c, :shard, :].astype(F32) for c in range(2)]
        for t in range(3):
            at = t * width + 2 * HD * k
            g_qkv[:, at : at + 2 * HD] = jnp.concatenate(
                [h[:, t * HD : (t + 1) * HD] for h in heads], axis=1)
        for c in range(2):
            g_bias[2 * k + c : 2 * k + c + 1, :] = qkvs[2 * k + c, shard : shard + 1, :].astype(F32)
    out_copy.wait_recv()
    g_out[...] = out_ref[...].astype(F32) + pair_out[...].astype(F32)
    for copy in started:
        copy.wait_send()


def finish_grads(out, small, qkv, reduced, joined, weight, grad_one):
    n_ctx, n_x = lax.axis_size("ctx"), lax.axis_size("x")
    n = 2 * n_ctx * n_x
    shard, width = out.shape
    part = reduced.shape[0] // 2
    vmem = pl.BlockSpec(memory_space=pltpu.VMEM)
    dma = pltpu.SemaphoreType.DMA

    def low(*shape):
        return pltpu.VMEM(shape, BF16)

    def wide(*shape):
        return jax.ShapeDtypeStruct(shape, F32)

    return pl.pallas_call(
        partial(finish_kernel, n_ctx=n_ctx, n_x=n_x),
        in_specs=[vmem] * 7,
        out_specs=[vmem] * 7,
        out_shape=[
            wide(2 * part, width),
            wide(shard, 4 * width),
            wide(shard, width),
            wide(*small.shape),
            wide(shard, 3 * width),
            wide(n, qkv.shape[2]),
            jax.ShapeDtypeStruct(grad_one.shape, BF16),
        ],
        scratch_shapes=[
            low(*small.shape),
            low(*qkv.shape),
            low(*qkv.shape),
            low(*qkv.shape),
            low(part, width),
            low(*out.shape),
            low(3, shard, width),
            low(*joined.shape),
            pltpu.VMEM((2,) + grad_one.shape, F32),
            pltpu.VMEM(grad_one.shape, F32),
            dma((n_ctx * n_x - 1,)),
            dma((n_ctx * n_x,)),
            dma((n - 1,)),
            dma((n,)),
            dma((8,)),
            dma((8,)),
        ],
        compiler_params=pltpu.CompilerParams(
            collective_id=2, has_side_effects=True, vmem_limit_bytes=VMEM_LIMIT
        ),
        cost_estimate=pl.CostEstimate(flops=0, bytes_accessed=16 * joined.size, transcendentals=0),
        name="finish_grads",
    )(out, small, qkv, reduced, joined, weight, grad_one)


def lane_gather(mine_ref, all_ref, send_sem, recv_sem, local_sem, n_ctx, n_x):
    ctx, x = lax.axis_index("ctx"), lax.axis_index("x")
    chip = ctx * n_x + x
    routes = (
        at_device(ctx=lax.rem(ctx + 1, n_ctx)),
        at_device(ctx=lax.rem(ctx + n_ctx - 1, n_ctx)),
        at_device(x=1 - x),
    )

    def send(k, lane, own=False):
        return pltpu.make_async_remote_copy(
            mine_ref if own else all_ref.at[k], all_ref.at[k], send_sem.at[lane, k], recv_sem.at[k],
            device_id=routes[lane], device_id_type=MESH)

    local = pltpu.make_async_copy(mine_ref, all_ref.at[chip], local_sem)

    def begin():
        @pl.when(ctx + 1 < n_ctx)
        def _():
            send(chip, 0, own=True).start()

        @pl.when(ctx > 0)
        def _():
            send(chip, 1, own=True).start()

        send(chip, 2, own=True).start()
        local.start()

    def relay(r):
        for sign, lane, more in ((-1, 0, ctx + 1 < n_ctx), (1, 1, ctx > 0)):
            z = ctx + sign * r

            @pl.when((z >= 0) & (z < n_ctx))
            def _():
                k = z * n_x + x
                send(k, 0).wait_recv()

                @pl.when(more)
                def _():
                    send(k, lane).start()

                send(k, 2).start()

    def end():
        for z in range(n_ctx):
            k = z * n_x + x
            send(z * n_x + 1 - x, 0).wait_recv()

            @pl.when((z <= ctx) & (ctx + 1 < n_ctx))
            def _():
                send(k, 0).wait_send()

            @pl.when((z >= ctx) & (ctx > 0))
            def _():
                send(k, 1).wait_send()

            send(k, 2).wait_send()
        local.wait()

    return begin, relay, end


def lane_gather_x_first(mine_ref, all_ref, send_sem, recv_sem, local_sem, n_ctx, n_x):
    ctx, x = lax.axis_index("ctx"), lax.axis_index("x")
    chip = ctx * n_x + x
    pair = ctx * n_x + 1 - x
    routes = (
        at_device(ctx=lax.rem(ctx + 1, n_ctx)),
        at_device(ctx=lax.rem(ctx + n_ctx - 1, n_ctx)),
        at_device(x=1 - x),
    )
    ways = ((-1, 0, ctx + 1 < n_ctx), (1, 1, ctx > 0))

    def send(k, lane, own=False):
        return pltpu.make_async_remote_copy(
            mine_ref if own else all_ref.at[k], all_ref.at[k], send_sem.at[lane, k], recv_sem.at[k],
            device_id=routes[lane], device_id_type=MESH)

    local = pltpu.make_async_copy(mine_ref, all_ref.at[chip], local_sem)

    def along(k, own=False):
        for _, lane, more in ways:
            @pl.when(more)
            def _():
                send(k, lane, own).start()

    def begin():
        send(chip, 2, own=True).start()
        along(chip, own=True)
        local.start()

    def pass_on(r, line):
        for sign, lane, more in ways:
            z = ctx + sign * r

            @pl.when((z >= 0) & (z < n_ctx))
            def _():
                k = z * n_x + line
                send(k, lane).wait_recv()

                @pl.when(more)
                def _():
                    send(k, lane).start()

    def relay(r):
        if r == 1:
            send(pair, 2).wait_recv()
            along(pair)
        else:
            pass_on(r - 1, 1 - x)
        pass_on(r, x)

    def end():
        pass_on(n_ctx - 1, 1 - x)
        send(chip, 2).wait_send()
        for z in range(n_ctx):
            for line in range(n_x):
                @pl.when((z <= ctx) & (ctx + 1 < n_ctx))
                def _():
                    send(z * n_x + line, 0).wait_send()

                @pl.when((z >= ctx) & (ctx > 0))
                def _():
                    send(z * n_x + line, 1).wait_send()

        local.wait()

    return begin, relay, end


QB = 512
KB = 512


def turn(pair, cosine, sine):
    half = HD // 2
    lanes = lax.broadcasted_iota(jnp.int32, (1, 2 * HD), 1)
    low = lax.rem(lanes, HD) < half
    swapped = jnp.where(low, pltpu.roll(pair, 2 * HD - half, 1), pltpu.roll(pair, half, 1))
    return pair * cosine + swapped * jnp.where(low, -sine, sine)


def heads_kernel(
    len_ref, tok_ref, w_ref, b_ref, cos_ref, sin_ref, wa_ref, wu_ref, wd_ref,
    q_ref, k_ref, v_ref, mix_ref, send_ref, norm_ref, fa_ref, fu_ref, fd_ref,
    a_send, a_recv, u_send, u_recv, d_send, d_recv, local_sem, *, n_ctx, n_x, part
):
    core = lax.axis_index("core")
    ctx, x = lax.axis_index("ctx"), lax.axis_index("x")
    greet([
        at_device(x=1 - x),
        at_device(ctx=lax.rem(ctx + 1, n_ctx)),
        at_device(ctx=lax.rem(ctx + n_ctx - 1, n_ctx)),
    ])
    flows = [
        lane_gather_x_first(wa_ref, fa_ref, a_send, a_recv, local_sem.at[0], n_ctx, n_x),
        lane_gather(wu_ref, fu_ref, u_send, u_recv, local_sem.at[1], n_ctx, n_x),
        lane_gather(wd_ref, fd_ref, d_send, d_recv, local_sem.at[2], n_ctx, n_x),
    ]
    for begin, _, _ in flows:
        begin()
    slots, seq, _ = q_ref.shape

    def relay(r):
        if r < n_ctx:
            for _, hop, _ in flows:
                hop(r)

    blocks = seq // QB

    def project():
        @pl.loop(0, slots * blocks)
        def _(n):
            s, i = n // blocks, lax.rem(n, blocks)
            rows = pl.ds(pl.multiple_of(i * QB, QB), QB)
            tokens = tok_ref[pl.ds(pl.multiple_of(n * QB, QB), QB), :]
            joined = mm(tokens, w_ref[...]) + b_ref[...]
            turned = turn(joined[:, : 2 * HD], cos_ref[rows, :], sin_ref[rows, :])
            q_ref[s, rows, :] = (turned[:, :HD].astype(BF16) * HD ** (-0.5)).astype(BF16)
            k_ref[s, rows, :] = turned[:, HD:].astype(BF16)
            v_ref[s, rows, :] = joined[:, 2 * HD :].astype(BF16)

    def attend():
        @pl.loop(0, slots * blocks)
        def _(n):
            s, i = n // blocks, lax.rem(n, blocks)
            length = len_ref[s]
            rows = pl.ds(pl.multiple_of(i * QB, QB), QB)
            queries = q_ref[s, rows, :]

            @pl.when(n == blocks)
            def _():
                relay(2)

            def step(j, state):
                highest, total, mix = state
                start = pl.multiple_of(j * KB, KB)
                scores = contract(queries, k_ref[s, pl.ds(start, KB), :], 1, 1)
                ids = start + lax.broadcasted_iota(jnp.int32, (1, KB), 1)
                scores = jnp.where(ids < length, scores, NEG_FILL)
                higher = jnp.maximum(highest, jnp.max(scores, axis=1, keepdims=True))
                fade = jnp.exp(highest - higher)
                weights = jnp.exp(scores - higher)
                total = total * fade + jnp.sum(weights, axis=1, keepdims=True)
                mix = mix * fade + mm(weights.astype(BF16), v_ref[s, pl.ds(start, KB), :])
                return higher, total, mix

            highest, total, mix = lax.fori_loop(
                0,
                seq // KB,
                step,
                (
                    jnp.full((QB, 1), NEG_FILL, F32),
                    jnp.zeros((QB, 1), F32),
                    jnp.zeros((QB, HD), F32),
                ),
            )
            mix = mix / total
            mix_ref[s, rows, :] = mix
            log_norm = jnp.broadcast_to(highest + jnp.log(total), (QB, 128))
            norm_ref[s, :, rows] = jnp.transpose(log_norm)[0:1, :]
            low = mix.astype(BF16)
            chips = QB // (2 * part)
            for chip in range(chips):
                for half in range(2):
                    at = (2 * chip + half) * part
                    upper, lower = low[at : at + part // 2], low[at + part // 2 : at + part]
                    send_ref[i * chips + chip, half ^ core, s] = jnp.concatenate(
                        [upper, lower], axis=1)

    project()
    relay(1)
    attend()
    for r in range(3, n_ctx):
        relay(r)
    for _, _, end in flows:
        end()


def heads(lengths, tokens, weight, bias, cosine, sine, part, *shards):
    n_ctx, n_x = lax.axis_size("ctx"), lax.axis_size("x")
    chips = n_ctx * n_x
    slots, seq = lengths.shape[0], cosine.shape[0]
    vmem = pl.BlockSpec(memory_space=pltpu.VMEM)
    anywhere = pl.BlockSpec(memory_space=pl.ANY)
    dma = pltpu.SemaphoreType.DMA
    head = jax.ShapeDtypeStruct((slots, seq, HD), BF16)
    return pl.pallas_call(
        partial(heads_kernel, n_ctx=n_ctx, n_x=n_x, part=part),
        in_specs=[pl.BlockSpec(memory_space=pltpu.SMEM)] + [vmem] * 8,
        out_specs=[vmem] * 6 + [anywhere] * 3,
        out_shape=[
            head,
            head,
            head,
            jax.ShapeDtypeStruct((slots, seq, HD), F32),
            jax.ShapeDtypeStruct((chips, 2, slots, part // 2, 2 * HD), BF16),
            jax.ShapeDtypeStruct((slots, 1, seq), F32),
        ]
        + [jax.ShapeDtypeStruct((chips,) + w.shape, w.dtype) for w in shards],
        scratch_shapes=[dma((3, chips)), dma((chips,))] * 3 + [dma((3,))],
        compiler_params=pltpu.CompilerParams(
            collective_id=5, has_side_effects=True, vmem_limit_bytes=VMEM_LIMIT
        ),
        cost_estimate=pl.CostEstimate(
            flops=16 * slots * seq * seq * HD,
            bytes_accessed=2 * tokens.size,
            transcendentals=slots * seq * seq,
        ),
        name="heads",
    )(lengths, tokens, weight, bias, cosine, sine, *shards)


def grads_kernel(
    len_ref, q_ref, k_ref, v_ref, g_ref, norm_ref, dot_ref, tok_ref, cos_ref, sin_ref,
    down_ref, up_ref, out_ref, small_ref,
    join_ref, grad_ref, red_ref, sum_ref, small_sum,
    dqt, key_grads, value_grads, total, bias, x_down, x_up, x_out, s_down, s_up, s_out,
    z_down, z_up, z_out, top_down, top_up, top_out, own_down, own_up, own_out, smalls,
    x_send, x_recv, z_send, z_recv, top_recv, small_send, small_recv, *, n_ctx, n_x, part
):
    ctx, x, core = (lax.axis_index(n) for n in GROUP)
    me = (ctx * n_x + x) * 2 + core
    peers = group_peers(n_ctx, n_x)
    greet([at_device(ctx=z, x=a, core=c) for z, a, c in peers])
    side = at_device(x=1 - x)
    arrays = (
        (down_ref, x_down, s_down, z_down, top_down, own_down),
        (up_ref, x_up, s_up, z_up, top_up, own_up),
        (out_ref, x_out, s_out, z_out, top_out, own_out),
    )

    def remote(source, target_ref, send_sem, recv_sem, target):
        return pltpu.make_async_remote_copy(
            source, target_ref, send_sem, recv_sem, device_id=target, device_id_type=MESH)

    orders = [
        sorted(range(n_ctx), key=lambda p, z=z: (p == z, -abs(p - z), min(p, n_ctx - 1 - p))) for z in range(n_ctx)
    ]
    places = [
        sum(jnp.where(ctx == z, orders[z][j], 0) for z in range(n_ctx)) for j in range(n_ctx)
    ]
    above = at_device(ctx=lax.rem(ctx + 1, n_ctx))
    below = at_device(ctx=lax.rem(ctx + n_ctx - 1, n_ctx))
    first = [
        [
            remote(
                ref.at[places[j] * n_x + 1 - x], x_in.at[j], x_send.at[i, j], x_recv.at[i, j], side)
            for i, (ref, x_in, _, _, _, _) in enumerate(arrays)
        ]
        for j in range(n_ctx)
    ]

    def hop(j, i, target, last=False):
        _, _, s_low, z_in, top, _ = arrays[i]
        p = places[j]
        return remote(
            s_low.at[min(j, n_ctx - 2)], top if last else z_in.at[p], z_send.at[i, min(j, n_ctx - 2)],
            top_recv.at[i] if last else z_recv.at[i, p], target)

    pushes = []
    for k, (z, a, c) in enumerate(peers):
        them = (z * n_x + a) * 2 + c
        pushes.append(remote(
            small_ref.at[them], smalls.at[me], small_send.at[k], small_recv.at[me],
            at_device(ctx=z, x=a, core=c)))
    for copies in first:
        for copy in copies:
            copy.start()
    for copy in pushes:
        copy.start()
    smalls[me] = small_ref[me]

    def stage(j):
        p = places[j]
        going_up = p > ctx
        for i, (ref, x_in, s_low, z_in, _, own) in enumerate(arrays):
            first[j][i].wait_recv()
            own[...] = ref[p * n_x + x].astype(F32) + x_in[j].astype(F32)
            if j == n_ctx - 1:
                continue

            @pl.when((going_up & (ctx > 0)) | ((p < ctx) & (ctx < n_ctx - 1)))
            def _():
                hop(j, i, above).wait_recv()
                own[...] += z_in[p].astype(F32)

            s_low[j] = own[...].astype(BF16)

            @pl.when(going_up)
            def _():
                hop(j, i, above).start()

            @pl.when(p < ctx - 1)
            def _():
                hop(j, i, below).start()

            @pl.when(p == ctx - 1)
            def _():
                hop(j, i, below, last=True).start()

    slots, seq, _ = q_ref.shape
    total[...] = jnp.zeros_like(total)
    bias[...] = jnp.zeros_like(bias)

    def attention(s, between):
        length = len_ref[s]
        dqt[...] = jnp.zeros_like(dqt)

        @pl.loop(0, seq // KB)
        def _(j):
            start = pl.multiple_of(j * KB, KB)
            key_block = k_ref[s, pl.ds(start, KB), :]
            value_block = v_ref[s, pl.ds(start, KB), :]
            turned = jnp.transpose(key_block.astype(F32)).astype(BF16)
            ids = start + lax.broadcasted_iota(jnp.int32, (KB, 1), 0)
            shift = jnp.where(ids < length, 0.0, NEG_FILL)
            for at_step, number in between:
                @pl.when(j == at_step)
                def _():
                    stage(number)

            def step(i, state):
                key_grad, value_grad = state
                at = pl.multiple_of(i * QB, QB)
                queries = q_ref[s, pl.ds(at, QB), :]
                grads = g_ref[s, pl.ds(at, QB), :]
                scores = contract(key_block, queries, 1, 1) + shift
                probs = jnp.exp(scores - norm_ref[s, :, pl.ds(at, QB)])
                grad_probs = contract(value_block, grads, 1, 1)
                grad_scores = (probs * (grad_probs - dot_ref[s, :, pl.ds(at, QB)])).astype(BF16)
                value_grad = value_grad + mm(probs.astype(BF16), grads)
                key_grad = key_grad + mm(grad_scores, queries)
                dqt[:, pl.ds(at, QB)] += mm(turned, grad_scores)
                return key_grad, value_grad

            zero = jnp.zeros((KB, HD), F32)
            key_grad, value_grad = lax.fori_loop(0, seq // QB, step, (zero, zero))
            key_grads[pl.ds(start, KB), :] = key_grad
            value_grads[pl.ds(start, KB), :] = value_grad

    def join(s):
        @pl.loop(0, seq // QB)
        def _(i):
            at = pl.multiple_of(i * QB, QB)
            rows = pl.ds(at, QB)
            query_grad = jnp.transpose(dqt[:, rows]) * HD ** (-0.5)
            pair = jnp.concatenate([query_grad, key_grads[rows, :]], axis=1)
            turned = turn(pair, cos_ref[rows, :], -sin_ref[rows, :])
            joined = jnp.concatenate([turned, value_grads[rows, :]], axis=1).astype(BF16)
            chips = QB // (2 * part)
            for chip in range(chips):
                for owner in range(2):
                    near = (2 * chip + owner) * part
                    upper = joined[near : near + part // 2]
                    lower = joined[near + part // 2 : near + part]
                    join_ref[i * chips + chip, owner, s] = jnp.concatenate([upper, lower], axis=1)
            tokens = tok_ref[pl.ds(pl.multiple_of(s * seq + at, QB), QB), :]
            total[...] += contract(joined, tokens, 0, 0)
            bias[...] += jnp.sum(joined.astype(F32), axis=0, keepdims=True)

    for s in range(slots):
        attention(s, [(1, 1)] if s == 1 else [])
        stage(0 if s == 0 else 2)
        join(s)
    turned_total = jnp.transpose(total[...])
    shard = turned_total.shape[0] // grad_ref.shape[0]
    extra = jnp.broadcast_to(bias[...], (grad_ref.shape[1] - shard, bias.shape[1]))
    for d in range(grad_ref.shape[0]):
        grad_ref[d, :shard] = turned_total[d * shard : (d + 1) * shard].astype(BF16)
        grad_ref[d, shard:] = extra.astype(BF16)
    for j in range(slots + 1, n_ctx):
        stage(j)
    for z, a, c in peers:
        them = (z * n_x + a) * 2 + c
        remote(
            small_ref.at[them], smalls.at[them], small_send.at[0], small_recv.at[them], side
        ).wait_recv()
    small_sum[...] = jnp.sum(smalls[...].astype(F32), axis=0).astype(BF16)
    for i, (_, _, _, z_in, top, own) in enumerate(arrays):
        @pl.when(ctx > 0)
        def _():
            hop(n_ctx - 1, i, above).wait_recv()
            own[...] += z_in[ctx].astype(F32)

        @pl.when(ctx < n_ctx - 1)
        def _():
            hop(0, i, below, last=True).wait_recv()
            own[...] += top[...].astype(F32)

    rows = own_down.shape[0]
    red_ref[:rows] = own_down[...].astype(BF16)
    red_ref[rows:] = own_up[...].astype(BF16)
    sum_ref[...] = own_out[...].astype(BF16)
    for copies in first + [pushes]:
        for copy in copies:
            copy.wait_send()
    for j in range(n_ctx - 1):
        for i in range(len(arrays)):
            hop(j, i, above).wait_send()


def grads(lengths, queries, keys, values, grad_heads, norms, dots, tokens, cosine, sine,
          down, up, out, small, part):
    n_ctx, n_x = lax.axis_size("ctx"), lax.axis_size("x")
    n = 2 * n_ctx * n_x
    slots, seq, _ = queries.shape
    width = tokens.shape[1]
    shard = width // n
    cols = 3 * HD
    vmem = pl.BlockSpec(memory_space=pltpu.VMEM)
    dma = pltpu.SemaphoreType.DMA
    parts = (down, up, out)

    def low(*dims):
        return jax.ShapeDtypeStruct(dims, BF16)

    return pl.pallas_call(
        partial(grads_kernel, n_ctx=n_ctx, n_x=n_x, part=part),
        in_specs=[pl.BlockSpec(memory_space=pltpu.SMEM)] + [vmem] * 13,
        out_specs=[vmem] * 5,
        out_shape=[
            low(seq // (2 * part), 2, slots, part // 2, 2 * cols),
            low(n, shard + 16, cols),
            low(down.shape[1] + up.shape[1], width),
            low(*out.shape[1:]),
            low(*small.shape[1:]),
        ],
        scratch_shapes=[
            pltpu.VMEM((HD, seq), F32),
            pltpu.VMEM((seq, HD), F32),
            pltpu.VMEM((seq, HD), F32),
            pltpu.VMEM((cols, width), F32),
            pltpu.VMEM((1, cols), F32),
        ]
        + [pltpu.VMEM((n_ctx,) + t.shape[1:], BF16) for t in parts]
        + [pltpu.VMEM((n_ctx - 1,) + t.shape[1:], BF16) for t in parts]
        + [pltpu.VMEM((n_ctx,) + t.shape[1:], BF16) for t in parts]
        + [pltpu.VMEM(t.shape[1:], BF16) for t in parts]
        + [pltpu.VMEM(t.shape[1:], F32) for t in parts]
        + [
            pltpu.VMEM(small.shape, BF16),
            dma((3, n_ctx)),
            dma((3, n_ctx)),
            dma((3, n_ctx - 1)),
            dma((3, n_ctx)),
            dma((3,)),
            dma((n - 1,)),
            dma((n,)),
        ],
        compiler_params=pltpu.CompilerParams(
            collective_id=6, has_side_effects=True, vmem_limit_bytes=VMEM_LIMIT
        ),
        cost_estimate=pl.CostEstimate(
            flops=40 * slots * seq * seq * HD,
            bytes_accessed=4 * tokens.size,
            transcendentals=slots * seq * seq,
        ),
        name="grads",
    )(lengths, queries, keys, values, grad_heads, norms, dots, tokens, cosine, sine,
      down, up, out, small)


def norm_forward(values, gain, shift):
    center = values - jnp.mean(values, axis=-1, keepdims=True)
    spread = jnp.mean(center * center, axis=-1, keepdims=True)
    root = lax.rsqrt(spread + LN_EPS)
    unit = center * root
    return unit * gain + shift, unit, root


def norm_backward(grad, unit, root, gain):
    scaled = grad * gain
    inner = scaled - jnp.mean(scaled, axis=-1, keepdims=True)
    inner = inner - unit * jnp.mean(scaled * unit, axis=-1, keepdims=True)
    return root * inner, jnp.sum(grad * unit, axis=0), jnp.sum(grad, axis=0)


def gelu_pair(values):
    half = 0.5 + 0.5 * lax.erf(values * 0.7071067811865476)
    bell = jnp.exp(-0.5 * values * values) * 0.3989422804014327
    return values * half, half + values * bell


def rope_rows(positions):
    halfway = HD // 2
    ladder = jnp.arange(halfway, dtype=F32) * (2.0 / HD)
    frequency = jnp.power(jnp.float32(10000.0), -ladder)
    angles = positions[:, None] * frequency[None, :]
    return jnp.cos(angles), jnp.sin(angles)


def layer_kernel(
    sent_ref, tok_ref, wo_ref, up_ref, down_ref, vec_ref, full_ref, lane_ref,
    merged_ref, out_ref, one_ref, ghead_ref, att_ref, vecs_ref, d_down_ref, d_up_ref, lanes_out,
    first, first_in, hid, act, slope, gdn, gup, hidden, unit_one, two,
    roots, near, near_in, far, far_in, low_out, low_in, send_sem, recv_sem, out_sem,
    lane_send, lane_recv, heads_in, push_send, push_recv,
    gm, heads_out, heads_back, back_send, back_recv, *, n_ctx, n_x
):
    core, slot = lax.axis_index("core"), lax.axis_index("slot")
    twin, across = at_device(core=1 - core), at_device(slot=1 - slot)
    ctx, x = lax.axis_index("ctx"), lax.axis_index("x")
    chip = ctx * n_x + x
    others = [
        (lax.rem(ctx + o // n_x, n_ctx), lax.rem(x + o % n_x, n_x)) for o in range(1, n_ctx * n_x)
    ]
    greet([twin, across] + [at_device(ctx=z, x=a) for z, a in others])
    pushes = [
        pltpu.make_async_remote_copy(
            sent_ref.at[z * n_x + a], heads_in.at[chip], push_send.at[o], push_recv.at[chip],
            device_id=at_device(ctx=z, x=a), device_id_type=MESH)
        for o, (z, a) in enumerate(others)
    ]
    for push in pushes:
        push.start()
    heads_in[chip] = sent_ref[chip]
    begin_lane, relay_lane, end_lane = lane_gather(
        lane_ref, lanes_out, lane_send, lane_recv, out_sem.at[0], n_ctx, n_x)
    begin_lane()
    rows, width = tok_ref.shape
    half = rows // 2
    tile = 256
    count = [0]
    started = []

    def launch(source, target_ref, target):
        i = count[0]
        count[0] += 1
        copy = pltpu.make_async_remote_copy(
            source, target_ref, send_sem.at[i], recv_sem.at[i],
            device_id=target, device_id_type=MESH)
        copy.start()
        started.append(copy)
        return copy

    def columns(body, n=width // tile):
        @pl.loop(0, n)
        def _(t):
            body(pl.ds(pl.multiple_of(t * tile, tile), tile))

    def chunks(body, size=64):
        @pl.loop(0, rows // size)
        def _(t):
            body(pl.ds(pl.multiple_of(t * size, size), size))

    def exchange(buf, turn, stage, product, between):
        halves = [
            launch(buf.at[pl.ds(h * half, half)], buf.at[pl.ds((2 + h) * rows, half)], across)
            for h in range(2)
        ]
        to_twin = launch(buf.at[pl.ds(0, rows)], buf.at[pl.ds(rows, rows)], twin)
        near_buf, far_buf = near.at[turn], far.at[turn]
        to_twin.wait_recv()
        stage(0, 2 * rows)
        product(0, 2 * rows, near_buf, 0)
        near_copy = launch(
            near_buf.at[pl.ds(rows, rows)], near_in.at[turn], twin)
        between()
        back = []
        for h in range(2):
            at = (2 + h) * rows
            halves[h].wait_recv()
            launch(
                buf.at[pl.ds(at, half)], buf.at[pl.ds(at + half, half)], twin).wait_recv()
            stage(at, rows)
            product(at, rows, far_buf, h * rows)
            i = 2 * turn + h
            launch(
                far_buf.at[pl.ds(h * rows + half, half)], far_in.at[i], twin).wait_recv()
            low_out[i] = (far_buf[pl.ds(h * rows, half), :] + far_in[i]).astype(BF16)
            back.append(launch(low_out.at[i], low_in.at[i], across))
        return near_copy, back

    for o, (z, a) in enumerate(others):
        source = z * n_x + a
        pltpu.make_async_remote_copy(
            sent_ref.at[source], heads_in.at[source], push_send.at[o], push_recv.at[source],
            device_id=twin, device_id_type=MESH).wait_recv()
    _, owners, slots, packed, pair_width = heads_in.shape
    for k in range(0, n_ctx * n_x, 2):
        for h in range(owners):
            for t in range(slots):
                left, right = heads_in[k, h, t], heads_in[k + 1, h, t]
                for piece in range(2):
                    at = ((h * slots + t) * 2 + piece) * packed
                    of = slice(piece * HD, (piece + 1) * HD)
                    merged_ref[at : at + packed, k * HD : (k + 2) * HD] = jnp.concatenate(
                        [left[:, of], right[:, of]], axis=1)

    def out_product(cols):
        first[:, cols] = mm(merged_ref[...], wo_ref[:, cols])

    columns(out_product)
    launch(first.at[pl.ds(rows, rows)], first_in, twin).wait_recv()

    def norm_one(at):
        values = tok_ref[at, :].astype(F32) + first[at, :] + first_in[at, :] + vec_ref[0:1, :]
        normed, unit, root = norm_forward(values, vec_ref[1:2, :], vec_ref[2:3, :])
        hidden[at, :] = normed
        unit_one[at, :] = unit
        roots[0, at, :] = jnp.broadcast_to(root, (root.shape[0], 128))
        hid[at, :] = normed.astype(BF16)

    chunks(norm_one)

    def up_stage(start, size):
        def body(cols):
            values = mm(hid[start : start + size, :], up_ref[:, cols]) + vec_ref[3:4, cols]
            active, bend = gelu_pair(values)
            act[start : start + size, cols] = active.astype(BF16)
            slope[start : start + size, cols] = bend

        columns(body)

    def down_product(start, size, target, at):
        def body(cols):
            target[at : at + size, cols] = mm(act[start : start + size, :], down_ref[:, cols])

        columns(body)

    near_copy, back = exchange(hid, 0, up_stage, down_product, lambda: relay_lane(1))
    relay_lane(2)
    vecs_ref[...] = jnp.zeros_like(vecs_ref)
    near_copy.wait_recv()

    def norm_two(at, h, local):
        downward = near[0, at, :] + near_in[0, at, :] + low_in[h, local, :].astype(F32)
        values = hidden[at, :] + downward + vec_ref[4:5, :]
        normed, unit, root = norm_forward(values, vec_ref[5:6, :], vec_ref[6:7, :])
        out_ref[at, :] = normed.astype(BF16)
        grad, gain, shift = norm_backward(full_ref[at, :], unit, root, vec_ref[5:6, :])
        two[at, :] = grad
        low = grad.astype(BF16)
        gdn[at, :] = low
        vecs_ref[5:6, :] += gain[None]
        vecs_ref[6:7, :] += shift[None]
        vecs_ref[4:5, :] += jnp.sum(low.astype(F32), axis=0, keepdims=True)

    def by_half(body, h, size=64):
        @pl.loop(0, half // size)
        def _(t):
            local = pl.multiple_of(t * size, size)
            body(pl.ds(h * half + local, size), h, pl.ds(local, size))

    for h in range(2):
        back[h].wait_recv()
        by_half(norm_two, h)

    def back_stage(start, size):
        def body(cols):
            grads = contract(gdn[start : start + size, :], down_ref[cols, :], 1, 1)
            low = (grads * slope[start : start + size, cols]).astype(BF16)
            gup[start : start + size, cols] = low
            vecs_ref[3:4, cols] += jnp.sum(low.astype(F32), axis=0, keepdims=True)

        columns(body)

    def back_product(start, size, target, at):
        def body(cols):
            target[at : at + size, cols] = contract(
                gup[start : start + size, :], up_ref[cols, :], 1, 1)

        columns(body)

    def last_relays():
        for r in range(3, n_ctx):
            relay_lane(r)

    near_copy, back = exchange(gdn, 1, back_stage, back_product, last_relays)
    near_copy.wait_recv()

    def norm_back(at, h, local):
        grad = near[1, at, :] + near_in[1, at, :] + low_in[2 + h, local, :].astype(F32)
        grad = grad + two[at, :]
        root = roots[0, at, 0:1]
        one, gain, shift = norm_backward(grad, unit_one[at, :], root, vec_ref[1:2, :])
        one_ref[at, :] = one
        low = one.astype(BF16)
        att_ref[at, :] = low
        vecs_ref[1:2, :] += gain[None]
        vecs_ref[2:3, :] += shift[None]
        vecs_ref[0:1, :] += jnp.sum(low.astype(F32), axis=0, keepdims=True)

    for h in range(2):
        back[h].wait_recv()
        by_half(norm_back, h)
    launch(att_ref.at[pl.ds(0, rows)], att_ref.at[pl.ds(rows, rows)], twin).wait_recv()

    def merged_product(cols):
        gm[:, cols] = contract(att_ref[...], wo_ref[cols, :], 1, 1).astype(BF16)

    columns(merged_product, wo_ref.shape[0] // tile)
    for k in range(n_ctx * n_x):
        of = slice(k * HD, (k + 1) * HD)
        for h in range(owners):
            for t in range(slots):
                at = (h * slots + t) * 2 * packed
                heads_out[k, h, t] = jnp.concatenate(
                    [gm[at : at + packed, of], gm[at + packed : at + 2 * packed, of]], axis=1)
    returns = [
        pltpu.make_async_remote_copy(
            heads_out.at[z * n_x + a], heads_back.at[chip], back_send.at[o], back_recv.at[chip],
            device_id=at_device(ctx=z, x=a), device_id_type=MESH)
        for o, (z, a) in enumerate(others)
    ]
    for copy in returns:
        copy.start()
    heads_back[chip] = heads_out[chip]

    half_tile = tile // 2

    @pl.loop(0, width // tile)
    def _(t):
        cols = pl.ds(pl.multiple_of(t * tile, tile), tile)
        down_grad = contract(act[:, cols], gdn[...], 0, 0).astype(BF16)
        up_grad = contract(hid[:, cols], gup[...], 0, 0).astype(BF16)
        for piece in range(2):
            of = slice(piece * half_tile, (piece + 1) * half_tile)
            d_down_ref[2 * t + piece] = down_grad[of]
            d_up_ref[2 * t + piece] = up_grad[of]

    for o, (z, a) in enumerate(others):
        source = z * n_x + a
        pltpu.make_async_remote_copy(
            heads_out.at[source], heads_back.at[source], back_send.at[o], back_recv.at[source],
            device_id=twin, device_id_type=MESH).wait_recv()
    for k in range(n_ctx * n_x):
        for h in range(owners):
            owner = core if h == 0 else 1 - core
            at = pl.multiple_of((2 * k + owner) * 2 * packed, 2 * packed)
            for t in range(slots):
                block = heads_back[k, h, t]
                ghead_ref[t, pl.ds(at, packed), :] = block[:, :HD]
                ghead_ref[t, pl.ds(at + packed, packed), :] = block[:, HD:]
    end_lane()
    for copy in started + pushes + returns:
        copy.wait_send()


def layer(sent, tokens, w_out, up, down, vectors, grad_full, lane_shard):
    n_ctx, n_x = lax.axis_size("ctx"), lax.axis_size("x")
    chips = n_ctx * n_x
    rows, width = tokens.shape
    hidden = up.shape[1]
    lane = w_out.shape[0]
    slots = sent.shape[2]
    vmem = pl.BlockSpec(memory_space=pltpu.VMEM)
    anywhere = pl.BlockSpec(memory_space=pl.ANY)
    dma = pltpu.SemaphoreType.DMA

    def shape(*dims, dtype=BF16):
        return jax.ShapeDtypeStruct(dims, dtype)

    def wide(*dims):
        return pltpu.VMEM(dims, F32)

    def low(*dims):
        return pltpu.VMEM(dims, BF16)

    return pl.pallas_call(
        partial(layer_kernel, n_ctx=n_ctx, n_x=n_x),
        in_specs=[vmem] * 8,
        out_specs=[vmem] * 8 + [anywhere],
        out_shape=[
            shape(2 * rows, lane),
            shape(rows, width),
            shape(rows, width, dtype=F32),
            shape(slots, 2 * chips * (rows // slots), HD),
            shape(2 * rows, width),
            shape(8, width, dtype=F32),
            shape(chips, hidden // chips, width),
            shape(chips, width // chips, hidden),
            shape(chips, *lane_shard.shape),
        ],
        scratch_shapes=[
            wide(2 * rows, width),
            wide(rows, width),
            low(4 * rows, width),
            low(4 * rows, hidden),
            wide(4 * rows, hidden),
            low(4 * rows, width),
            low(4 * rows, hidden),
            wide(rows, width),
            wide(rows, width),
            wide(rows, width),
            wide(1, rows, 128),
            wide(2, 2 * rows, width),
            wide(2, rows, width),
            wide(2, 2 * rows, width),
            wide(4, rows // 2, width),
            low(4, rows // 2, width),
            low(4, rows // 2, width),
            dma((24,)),
            dma((24,)),
            dma((5,)),
            dma((3, chips)),
            dma((chips,)),
            low(*sent.shape),
            dma((chips - 1,)),
            dma((chips,)),
            low(2 * rows, lane),
            low(*sent.shape),
            low(*sent.shape),
            dma((chips - 1,)),
            dma((chips,)),
        ],
        compiler_params=pltpu.CompilerParams(
            collective_id=3, has_side_effects=True, vmem_limit_bytes=VMEM_LIMIT
        ),
        cost_estimate=pl.CostEstimate(
            flops=16 * rows * width * hidden, bytes_accessed=16 * rows * width, transcendentals=0
        ),
        name="layer",
    )(sent, tokens, w_out, up, down, vectors, grad_full, lane_shard)


def head_device(
    tokens,
    lengths,
    w_qkv,
    b_qkv,
    w_out,
    b_out,
    ln1_gain,
    ln1_bias,
    w_up,
    b_up,
    w_down,
    b_down,
    ln2_gain,
    ln2_bias,
    w_proj,
    cot_out,
    cot_emb,
):
    n_lane = lax.axis_size("ctx") * lax.axis_size("x")
    n_group = 2 * n_lane
    core = lax.axis_index("core")
    slot = lax.axis_index("slot")
    chip = lax.axis_index("ctx") * lax.axis_size("x") + lax.axis_index("x")
    me = 2 * chip + core
    slots, part, width = tokens.shape
    seq = part * n_group
    rows = slots * part
    shard = width // n_group
    ff_shard = w_down.shape[0]
    ff_half = ff_shard // 2
    proj = w_proj.shape[1]
    head_cols = 3 * HD

    small = jnp.concatenate(
        [b_qkv, b_out, ln1_gain, ln1_bias, b_up, b_down, ln2_gain, ln2_bias]
    )
    small_at = [0]
    for piece in (b_qkv, b_out, ln1_gain, ln1_bias, b_up, b_down, ln2_gain, ln2_bias):
        small_at.append(small_at[-1] + piece.shape[0])
    small_rows = -(-small.shape[0] // proj)
    small_rows = -(-small_rows // 16) * 16
    small = jnp.pad(small, (0, small_rows * proj - small.shape[0])).reshape(small_rows, proj)
    def two_lanes(mine, theirs):
        low_first = jnp.stack([mine, theirs], axis=0)
        high_first = jnp.stack([theirs, mine], axis=0)
        return jnp.where(core == 0, low_first, high_first)

    up_split = w_up.reshape(shard, n_lane, 2, 2, ff_half)
    up_mine = pick(up_split, core, 2)
    up_theirs = swap_core(pick(up_split, 1 - core, 2))
    up_chip = two_lanes(pick(up_mine, slot, 2), pick(up_theirs, slot, 2))
    down_split = w_down.reshape(2, ff_half, width)

    by_head = w_qkv.reshape(shard, 3, n_group, HD).transpose(2, 0, 1, 3)
    all_tokens, my_head, packed = gather_start(
        tokens,
        by_head.reshape(n_group, shard, head_cols),
        jnp.concatenate([w_proj, small], axis=0),
    )
    proj_full = packed[:, :shard].reshape(width, proj)
    smalls = packed[:, shard:].reshape(n_group, small_rows * proj).astype(F32)
    qkv_bias, out_bias, gain_one, shift_one, up_bias, down_bias, gain_two, shift_two = (
        smalls[:, a:b].reshape(-1) for a, b in zip(small_at[:-1], small_at[1:])
    )

    head_weight = my_head.reshape(width, head_cols)
    all_tokens = all_tokens.reshape(slots * seq, width)
    head_bias = pick(qkv_bias.reshape(1, 3, n_group, HD), me, 2).reshape(1, head_cols)
    cosine, sine = rope_rows(jnp.arange(seq, dtype=jnp.int32).astype(F32))
    cos_wide = jnp.tile(cosine, (1, 4))
    sin_wide = jnp.tile(sine, (1, 4))
    queries, keys, values, mixture, send, norms, out_lane, up, down = heads(
        lengths,
        all_tokens,
        head_weight,
        head_bias,
        cos_wide,
        sin_wide,
        part,
        w_out,
        up_chip.reshape(2 * shard, n_lane * ff_half),
        pick(down_split, slot, 0),
    )
    out_lane, up, down = (t.reshape(-1, t.shape[2]) for t in (out_lane, up, down))
    bias_lane = pick(up_bias.reshape(n_lane, 2, 2, ff_half), core, 1)
    up_bias_own = pick(bias_lane, slot, 1).reshape(-1)

    place = me * part + jnp.arange(part, dtype=jnp.int32)
    live = (place[None, :] < lengths[:, None]).reshape(rows, 1)
    grad_out = jnp.where(live, cot_out.reshape(rows, width).astype(F32), 0.0)
    grad_emb = jnp.where(live, cot_emb.reshape(rows, proj), 0)
    grad_full = grad_out + contract(grad_emb, proj_full, 1, 1)
    vectors = jnp.stack(
        [out_bias, gain_one, shift_one, up_bias_own, down_bias, gain_two, shift_two, shift_two]
    )
    (
        merged,
        out_low,
        grad_one,
        grad_heads,
        grad_att,
        vector_grads,
        d_down,
        d_up,
        qkv_lane,
    ) = layer(
        send, tokens.reshape(rows, width), out_lane, up, down, vectors, grad_full, head_weight
    )
    embeds = mm(out_low, proj_full).astype(BF16)
    d_proj = contract(out_low, grad_emb, 0, 0)
    (
        d_out_bias,
        d_gain_one,
        d_shift_one,
        up_bias_own_grad,
        d_down_bias,
        d_gain_two,
        d_shift_two,
    ) = (vector_grads[i] for i in range(7))
    d_out = contract(merged, grad_att, 0, 0).astype(BF16)

    spread = (
        (jnp.arange(2) == core)[:, None, None] & (jnp.arange(2) == slot)[None, :, None]
    ).astype(F32)
    up_bias_grad = up_bias_own_grad.reshape(n_lane, 1, 1, ff_half) * spread[None]
    vectors = (
        d_out_bias,
        d_gain_one,
        d_shift_one,
        up_bias_grad.reshape(-1),
        d_down_bias,
        d_gain_two,
        d_shift_two,
    )
    small_grad = jnp.concatenate([v.reshape(n_group, -1) for v in vectors], axis=1)
    small_cols = small_grad.shape[1]
    vec_rows = -(-small_cols // proj)
    vec_rows = -(-(shard + vec_rows) // 16) * 16 - shard
    small_grad = jnp.pad(small_grad, ((0, 0), (0, vec_rows * proj - small_cols)))
    small_grad = jnp.concatenate(
        [d_proj.reshape(n_group, shard, proj), small_grad.reshape(n_group, vec_rows, proj)], axis=1
    )
    row_dots = jnp.sum(grad_heads.astype(F32) * mixture, axis=-1).reshape(slots, 1, seq)
    joined, d_qkv, reduced, out_sum, small_sum = grads(
        lengths,
        queries,
        keys,
        values,
        grad_heads,
        norms,
        row_dots,
        all_tokens,
        cos_wide,
        sin_wide,
        d_down,
        d_up,
        d_out.reshape(n_lane, shard, width),
        small_grad.astype(BF16),
        part,
    )
    grad_w_down, grad_w_up, grad_w_out, small_sum, grad_w_qkv, bias_rows, input_grad = finish_grads(
        out_sum,
        small_sum,
        d_qkv,
        reduced,
        joined,
        qkv_lane,
        grad_one,
    )
    grad_w_proj = small_sum[:shard]
    vec_sum = small_sum[shard:].reshape(-1)
    vec_outs = []
    at = 0
    for v in vectors:
        size = v.size // n_group
        vec_outs.append(vec_sum[at : at + size])
        at += size
    (
        grad_b_out,
        grad_gain_one,
        grad_shift_one,
        grad_b_up,
        grad_b_down,
        grad_gain_two,
        grad_shift_two,
    ) = vec_outs

    qkv_bias_grad = bias_rows.reshape(n_group, 3, HD).transpose(1, 0, 2).reshape(-1)
    grad_b_qkv = lax.dynamic_slice(qkv_bias_grad, (me * b_qkv.shape[0],), (b_qkv.shape[0],))

    return (
        out_low.reshape(slots, part, width),
        embeds.reshape(slots, part, proj),
        input_grad.reshape(slots, part, width),
        grad_w_qkv,
        grad_b_qkv,
        grad_w_out,
        grad_b_out,
        grad_gain_one,
        grad_shift_one,
        grad_w_up,
        grad_b_up,
        grad_w_down,
        grad_b_down,
        grad_gain_two,
        grad_shift_two,
        grad_w_proj,
    )


def layer_norm(hidden, gain, shift):
    center = hidden - jnp.mean(hidden, axis=-1, keepdims=True)
    spread = jnp.mean(center * center, axis=-1, keepdims=True)
    return center * lax.rsqrt(spread + LN_EPS) * gain + shift


def rope_tables(positions, head_width):
    halfway = head_width // 2
    ladder = jnp.arange(halfway, dtype=jnp.float32) * (2.0 / head_width)
    frequency = jnp.power(jnp.float32(10000.0), -ladder)
    angles = positions[:, None] * frequency[None, :]
    return (jnp.cos(angles)[:, None, :], jnp.sin(angles)[:, None, :])


def rotate(values, cosine, sine_part):
    halfway = values.shape[-1] // 2
    first_half = values[..., :halfway]
    second_half = values[..., halfway:]
    return jnp.concatenate(
        [
            first_half * cosine - second_half * sine_part,
            second_half * cosine + first_half * sine_part,
        ],
        axis=-1,
    )


def block_scores(query_block, key_block, key_start, length, scale):
    scores = (
        jnp.einsum("qhd,khd->hqk", query_block, key_block, preferred_element_type=jnp.float32)
        * scale
    )
    key_ids = key_start + jnp.arange(key_block.shape[0], dtype=jnp.int32)
    return jnp.where((key_ids < length)[None, None, :], scores, NEG_FILL)


def per_device(
    tokens,
    lengths,
    w_qkv,
    b_qkv,
    w_out,
    b_out,
    ln1_gain,
    ln1_bias,
    w_up,
    b_up,
    w_down,
    b_down,
    ln2_gain,
    ln2_bias,
    w_proj,
    cot_out,
    cot_emb,
):
    n_fsdp = lax.axis_size("fsdp")
    n_ctx = lax.axis_size("ctx")
    ctx_at = lax.axis_index("ctx")
    fsdp_at = lax.axis_index("fsdp")
    groups, tok_slot, width = tokens.shape
    heads_here = H // n_fsdp
    lane_width = heads_here * HD
    span_rows = tok_slot * n_fsdp
    key_count = span_rows * n_ctx
    row_count = groups * tok_slot
    scale = HD ** (-0.5)
    query_rows = min(512, span_rows)
    key_rows = min(2048, key_count // 4)
    query_blocks = span_rows // query_rows
    key_blocks = key_count // key_rows
    key_starts = jnp.arange(key_blocks, dtype=jnp.int32) * key_rows
    qkv_full, qkv_bias, out_full, out_bias, gain_one, shift_one = (
        lax.all_gather(w_qkv, ("ctx", "fsdp"), axis=0, tiled=True),
        lax.all_gather(b_qkv, ("ctx", "fsdp"), axis=0, tiled=True),
        lax.all_gather(w_out, ("ctx", "fsdp"), axis=0, tiled=True),
        lax.all_gather(b_out, ("ctx", "fsdp"), axis=0, tiled=True),
        lax.all_gather(ln1_gain, ("ctx", "fsdp"), axis=0, tiled=True),
        lax.all_gather(ln1_bias, ("ctx", "fsdp"), axis=0, tiled=True),
    )
    token_pos = (ctx_at * n_fsdp + fsdp_at) * tok_slot + jnp.arange(tok_slot, dtype=jnp.int32)
    live_rows = (token_pos[None, :] < lengths[:, None]).reshape(row_count, 1)
    flat_tokens = tokens.reshape(row_count, width)
    joined = jnp.dot(flat_tokens, qkv_full, preferred_element_type=jnp.float32) + qkv_bias.astype(
        jnp.float32
    )
    cosine, sine_part = rope_tables(token_pos.astype(jnp.float32), HD)
    split_heads = joined.reshape(groups, tok_slot, 3, H, HD)
    rotated_query = rotate(split_heads[:, :, 0], cosine, sine_part)
    rotated_key = rotate(split_heads[:, :, 1], cosine, sine_part)
    packed = (
        jnp.stack([rotated_query, rotated_key, split_heads[:, :, 2]], axis=2)
        .astype(jnp.bfloat16)
        .reshape(groups, tok_slot, 3, n_fsdp, lane_width)
    )
    by_heads = lax.all_to_all(packed, "fsdp", split_axis=3, concat_axis=1, tiled=True)
    queries = by_heads[:, :, 0, 0]
    local_keys = by_heads[:, :, 1, 0]
    local_values = by_heads[:, :, 2, 0]
    all_keys, all_values = (
        lax.all_gather(local_keys, "ctx", axis=1, tiled=True),
        lax.all_gather(local_values, "ctx", axis=1, tiled=True),
    )

    def attend_slot(slot_item):
        slot_queries, slot_keys, slot_values, length = slot_item
        query_split = slot_queries.reshape(query_blocks, query_rows, heads_here, HD)
        key_split = slot_keys.reshape(key_blocks, key_rows, heads_here, HD)
        value_split = slot_values.reshape(key_blocks, key_rows, heads_here, HD)

        def per_query(query_block):

            def row_stats(state_pair, key_item):
                highest, running_sum = state_pair
                scores = block_scores(query_block, key_item[0], key_item[1], length, scale)
                new_high = jnp.maximum(highest, jnp.max(scores, axis=-1))
                running_sum = running_sum * jnp.exp(highest - new_high) + jnp.sum(
                    jnp.exp(scores - new_high[..., None]), axis=-1
                )
                return ((new_high, running_sum), None)

            start_state = (
                jnp.full((heads_here, query_rows), NEG_FILL, jnp.float32),
                jnp.zeros((heads_here, query_rows), jnp.float32),
            )
            highest, running_sum = lax.scan(row_stats, start_state, (key_split, key_starts))[0]
            log_norm = highest + jnp.log(running_sum)

            def weigh_values(accumulated, key_item):
                scores = block_scores(query_block, key_item[0], key_item[2], length, scale)
                weights = jnp.exp(scores - log_norm[..., None]).astype(jnp.bfloat16)
                return (
                    accumulated
                    + jnp.einsum(
                        "hqk,khd->qhd", weights, key_item[1], preferred_element_type=jnp.float32
                    ),
                    None,
                )

            mixture = lax.scan(
                weigh_values,
                jnp.zeros((query_rows, heads_here, HD), jnp.float32),
                (key_split, value_split, key_starts),
            )[0]
            return (mixture, log_norm)

        mixture, log_norm = lax.map(per_query, query_split)
        return (mixture.reshape(span_rows, lane_width), log_norm)

    mixture, log_norms = lax.map(attend_slot, (queries, all_keys, all_values, lengths))
    merged = lax.all_to_all(
        mixture.astype(jnp.bfloat16).reshape(groups, span_rows, 1, lane_width),
        "fsdp",
        split_axis=1,
        concat_axis=2,
        tiled=True,
    ).reshape(row_count, width)
    attended = jnp.dot(merged, out_full, preferred_element_type=jnp.float32) + out_bias.astype(
        jnp.float32
    )
    hidden_one, pull_one = jax.vjp(
        layer_norm,
        flat_tokens.astype(jnp.float32) + attended,
        gain_one.astype(jnp.float32),
        shift_one.astype(jnp.float32),
    )
    hidden_low = hidden_one.astype(jnp.bfloat16)
    up_full, up_bias, down_full, down_bias, gain_two, shift_two, proj_full = (
        lax.all_gather(w_up, ("ctx", "fsdp"), axis=0, tiled=True),
        lax.all_gather(b_up, ("ctx", "fsdp"), axis=0, tiled=True),
        lax.all_gather(w_down, ("ctx", "fsdp"), axis=0, tiled=True),
        lax.all_gather(b_down, ("ctx", "fsdp"), axis=0, tiled=True),
        lax.all_gather(ln2_gain, ("ctx", "fsdp"), axis=0, tiled=True),
        lax.all_gather(ln2_bias, ("ctx", "fsdp"), axis=0, tiled=True),
        lax.all_gather(w_proj, ("ctx", "fsdp"), axis=0, tiled=True),
    )
    upward = jnp.dot(hidden_low, up_full, preferred_element_type=jnp.float32) + up_bias.astype(
        jnp.float32
    )
    active_full, pull_gelu = jax.vjp(partial(jax.nn.gelu, approximate=False), upward)
    active = active_full.astype(jnp.bfloat16)
    downward = jnp.dot(active, down_full, preferred_element_type=jnp.float32) + down_bias.astype(
        jnp.float32
    )
    out_full_rows, pull_two = jax.vjp(
        layer_norm,
        hidden_one + downward,
        gain_two.astype(jnp.float32),
        shift_two.astype(jnp.float32),
    )
    out_low = out_full_rows.astype(jnp.bfloat16)
    projected = jnp.dot(out_low, proj_full, preferred_element_type=jnp.float32)
    back_qkv, back_qkv_bias, back_out, back_out_bias, back_gain_one, back_shift_one = (
        lax.all_gather(w_qkv, ("ctx", "fsdp"), axis=0, tiled=True),
        lax.all_gather(b_qkv, ("ctx", "fsdp"), axis=0, tiled=True),
        lax.all_gather(w_out, ("ctx", "fsdp"), axis=0, tiled=True),
        lax.all_gather(b_out, ("ctx", "fsdp"), axis=0, tiled=True),
        lax.all_gather(ln1_gain, ("ctx", "fsdp"), axis=0, tiled=True),
        lax.all_gather(ln1_bias, ("ctx", "fsdp"), axis=0, tiled=True),
    )
    back_up, back_up_bias, back_down, back_down_bias, back_gain_two, back_shift_two, back_proj = (
        lax.all_gather(w_up, ("ctx", "fsdp"), axis=0, tiled=True),
        lax.all_gather(b_up, ("ctx", "fsdp"), axis=0, tiled=True),
        lax.all_gather(w_down, ("ctx", "fsdp"), axis=0, tiled=True),
        lax.all_gather(b_down, ("ctx", "fsdp"), axis=0, tiled=True),
        lax.all_gather(ln2_gain, ("ctx", "fsdp"), axis=0, tiled=True),
        lax.all_gather(ln2_bias, ("ctx", "fsdp"), axis=0, tiled=True),
        lax.all_gather(w_proj, ("ctx", "fsdp"), axis=0, tiled=True),
    )
    grad_out = jnp.where(live_rows, cot_out.reshape(row_count, width).astype(jnp.float32), 0.0)
    grad_emb = jnp.where(live_rows, cot_emb.reshape(row_count, -1), 0)
    d_proj = jnp.einsum("rd,rp->dp", out_low, grad_emb, preferred_element_type=jnp.float32)
    grad_full = grad_out + jnp.einsum(
        "rp,dp->rd", grad_emb, back_proj, preferred_element_type=jnp.float32
    )
    grad_two, d_gain_two, d_shift_two = pull_two(grad_full)
    grad_down = grad_two.astype(jnp.bfloat16)
    d_down = jnp.einsum("rf,rd->fd", active, grad_down, preferred_element_type=jnp.float32)
    d_down_bias = jnp.sum(grad_down.astype(jnp.float32), axis=0)
    grad_act = jnp.einsum("rd,fd->rf", grad_down, back_down, preferred_element_type=jnp.float32)
    grad_up = pull_gelu(grad_act)[0].astype(jnp.bfloat16)
    d_up = jnp.einsum("rd,rf->df", hidden_low, grad_up, preferred_element_type=jnp.float32)
    d_up_bias = jnp.sum(grad_up.astype(jnp.float32), axis=0)
    grad_hidden = grad_two + jnp.einsum(
        "rf,df->rd", grad_up, back_up, preferred_element_type=jnp.float32
    )
    grad_one, d_gain_one, d_shift_one = pull_one(grad_hidden)
    grad_att = grad_one.astype(jnp.bfloat16)
    d_out = jnp.einsum("rd,re->de", merged, grad_att, preferred_element_type=jnp.float32)
    d_out_bias = jnp.sum(grad_att.astype(jnp.float32), axis=0)
    grad_merged = jnp.einsum(
        "re,de->rd", grad_att, back_out, preferred_element_type=jnp.float32
    ).astype(jnp.bfloat16)
    grad_heads = lax.all_to_all(
        grad_merged.reshape(groups, tok_slot, n_fsdp, lane_width),
        "fsdp",
        split_axis=2,
        concat_axis=1,
        tiled=True,
    ).reshape(groups, span_rows, lane_width)

    def attend_back(slot_item):
        slot_queries, slot_keys, slot_values, grad_mix, log_norm, length = slot_item
        query_split = slot_queries.reshape(query_blocks, query_rows, heads_here, HD)
        key_split = slot_keys.reshape(key_blocks, key_rows, heads_here, HD)
        value_split = slot_values.reshape(key_blocks, key_rows, heads_here, HD)
        grad_split = grad_mix.reshape(query_blocks, query_rows, heads_here, HD)

        def value_pass(value_total, query_item):
            query_block, grad_block, norm_block = query_item

            def value_per_key(row_dot, key_item):
                key_block, value_block, key_start = key_item
                scores = block_scores(query_block, key_block, key_start, length, scale)
                probability = jnp.exp(scores - norm_block[..., None])
                grad_probs = jnp.einsum(
                    "qhd,khd->hqk", grad_block, value_block, preferred_element_type=jnp.float32
                )
                value_part = jnp.einsum(
                    "hqk,qhd->khd",
                    probability.astype(jnp.bfloat16),
                    grad_block,
                    preferred_element_type=jnp.float32,
                )
                return (row_dot + jnp.sum(probability * grad_probs, axis=-1), value_part)

            row_dot, value_parts = lax.scan(
                value_per_key,
                jnp.zeros((heads_here, query_rows), jnp.float32),
                (key_split, value_split, key_starts),
            )
            return (value_total + value_parts.reshape(key_count, heads_here, HD), row_dot)

        value_grad, row_dots = lax.scan(
            value_pass,
            jnp.zeros((key_count, heads_here, HD), jnp.float32),
            (query_split, grad_split, log_norm),
        )

        def key_pass(key_total, query_item):
            query_block, grad_block, norm_block, dot_block = query_item

            def key_per_key(query_accum, key_item):
                key_block, value_block, key_start = key_item
                scores = block_scores(query_block, key_block, key_start, length, scale)
                probability = jnp.exp(scores - norm_block[..., None])
                grad_probs = jnp.einsum(
                    "qhd,khd->hqk", grad_block, value_block, preferred_element_type=jnp.float32
                )
                grad_scores = (probability * (grad_probs - dot_block[..., None])).astype(
                    jnp.bfloat16
                )
                query_accum = query_accum + jnp.einsum(
                    "hqk,khd->qhd", grad_scores, key_block, preferred_element_type=jnp.float32
                )
                key_part = jnp.einsum(
                    "hqk,qhd->khd", grad_scores, query_block, preferred_element_type=jnp.float32
                )
                return (query_accum, key_part)

            query_grad, key_parts = lax.scan(
                key_per_key,
                jnp.zeros((query_rows, heads_here, HD), jnp.float32),
                (key_split, value_split, key_starts),
            )
            return (key_total + key_parts.reshape(key_count, heads_here, HD), query_grad)

        key_grad, query_grads = lax.scan(
            key_pass,
            jnp.zeros((key_count, heads_here, HD), jnp.float32),
            (query_split, grad_split, log_norm, row_dots),
        )
        return (
            query_grads.reshape(span_rows, lane_width) * scale,
            key_grad.reshape(key_count, lane_width) * scale,
            value_grad.reshape(key_count, lane_width),
        )

    grad_queries, key_terms, value_terms = lax.map(
        attend_back, (queries, all_keys, all_values, grad_heads, log_norms, lengths)
    )
    grad_keys, grad_values = (
        lax.psum_scatter(
            key_terms.astype(jnp.bfloat16), "ctx", scatter_dimension=1, tiled=True
        ).astype(jnp.float32),
        lax.psum_scatter(
            value_terms.astype(jnp.bfloat16), "ctx", scatter_dimension=1, tiled=True
        ).astype(jnp.float32),
    )
    head_pos = (ctx_at * span_rows + jnp.arange(span_rows, dtype=jnp.int32)).astype(jnp.float32)
    head_cosine, head_sine = rope_tables(head_pos, HD)
    query_back = rotate(
        grad_queries.reshape(groups, span_rows, heads_here, HD), head_cosine, -head_sine
    )
    key_back = rotate(grad_keys.reshape(groups, span_rows, heads_here, HD), head_cosine, -head_sine)
    value_back = grad_values.reshape(groups, span_rows, heads_here, HD)
    grad_pack = (
        jnp.stack([query_back, key_back, value_back], axis=2)
        .astype(jnp.bfloat16)
        .reshape(groups, span_rows, 3, 1, lane_width)
    )
    grad_joined = lax.all_to_all(
        grad_pack, "fsdp", split_axis=1, concat_axis=3, tiled=True
    ).reshape(row_count, 3 * width)
    d_qkv = jnp.einsum("rd,re->de", flat_tokens, grad_joined, preferred_element_type=jnp.float32)
    d_qkv_bias = jnp.sum(grad_joined.astype(jnp.float32), axis=0)
    input_grad = (
        jnp.einsum("re,de->rd", grad_joined, back_qkv, preferred_element_type=jnp.float32)
        + grad_one
    ).astype(jnp.bfloat16)
    shards = (
        lax.psum_scatter(d_qkv, ("ctx", "fsdp"), scatter_dimension=0, tiled=True),
        lax.psum_scatter(d_qkv_bias, ("ctx", "fsdp"), scatter_dimension=0, tiled=True),
        lax.psum_scatter(d_out, ("ctx", "fsdp"), scatter_dimension=0, tiled=True),
        lax.psum_scatter(d_out_bias, ("ctx", "fsdp"), scatter_dimension=0, tiled=True),
        lax.psum_scatter(d_gain_one, ("ctx", "fsdp"), scatter_dimension=0, tiled=True),
        lax.psum_scatter(d_shift_one, ("ctx", "fsdp"), scatter_dimension=0, tiled=True),
        lax.psum_scatter(d_up, ("ctx", "fsdp"), scatter_dimension=0, tiled=True),
        lax.psum_scatter(d_up_bias, ("ctx", "fsdp"), scatter_dimension=0, tiled=True),
        lax.psum_scatter(d_down, ("ctx", "fsdp"), scatter_dimension=0, tiled=True),
        lax.psum_scatter(d_down_bias, ("ctx", "fsdp"), scatter_dimension=0, tiled=True),
        lax.psum_scatter(d_gain_two, ("ctx", "fsdp"), scatter_dimension=0, tiled=True),
        lax.psum_scatter(d_shift_two, ("ctx", "fsdp"), scatter_dimension=0, tiled=True),
        lax.psum_scatter(d_proj, ("ctx", "fsdp"), scatter_dimension=0, tiled=True),
    )
    totals = (
        lax.psum(shards[0].astype(jnp.bfloat16), "slot").astype(jnp.float32),
        lax.psum(shards[1].astype(jnp.bfloat16), "slot").astype(jnp.float32),
        lax.psum(shards[2].astype(jnp.bfloat16), "slot").astype(jnp.float32),
        lax.psum(shards[3].astype(jnp.bfloat16), "slot").astype(jnp.float32),
        lax.psum(shards[4].astype(jnp.bfloat16), "slot").astype(jnp.float32),
        lax.psum(shards[5].astype(jnp.bfloat16), "slot").astype(jnp.float32),
        lax.psum(shards[6].astype(jnp.bfloat16), "slot").astype(jnp.float32),
        lax.psum(shards[7].astype(jnp.bfloat16), "slot").astype(jnp.float32),
        lax.psum(shards[8].astype(jnp.bfloat16), "slot").astype(jnp.float32),
        lax.psum(shards[9].astype(jnp.bfloat16), "slot").astype(jnp.float32),
        lax.psum(shards[10].astype(jnp.bfloat16), "slot").astype(jnp.float32),
        lax.psum(shards[11].astype(jnp.bfloat16), "slot").astype(jnp.float32),
        lax.psum(shards[12].astype(jnp.bfloat16), "slot").astype(jnp.float32),
    )
    return (
        out_low.reshape(groups, tok_slot, width),
        projected.astype(jnp.bfloat16).reshape(groups, tok_slot, -1),
        input_grad.reshape(groups, tok_slot, width),
        totals[0],
        totals[1],
        totals[2],
        totals[3],
        totals[4],
        totals[5],
        totals[6],
        totals[7],
        totals[8],
        totals[9],
        totals[10],
        totals[11],
        totals[12],
    )


def solution(mesh):
    n_slot, n_ctx, n_fsdp = (mesh.shape[a] for a in ("slot", "ctx", "fsdp"))
    rows_axes = ("ctx", "fsdp")
    step = per_device
    if n_slot == 2 and n_fsdp % 2 == 0 and n_ctx * n_fsdp == H:
        mesh = Mesh(
            mesh.devices.reshape(n_slot, n_ctx, n_fsdp // 2, 2), ("slot", "ctx", "x", "core")
        )
        rows_axes = GROUP
        step = head_device
    in_specs = (
        P("slot", rows_axes, None),
        P("slot"),
        P(rows_axes, None),
        P(rows_axes),
        P(rows_axes, None),
        P(rows_axes),
        P(rows_axes),
        P(rows_axes),
        P(rows_axes, None),
        P(rows_axes),
        P(rows_axes, None),
        P(rows_axes),
        P(rows_axes),
        P(rows_axes),
        P(rows_axes, None),
        P("slot", rows_axes, None),
        P("slot", rows_axes, None),
    )
    out_specs = (
        P("slot", rows_axes, None),
        P("slot", rows_axes, None),
        P("slot", rows_axes, None),
        P(rows_axes, None),
        P(rows_axes),
        P(rows_axes, None),
        P(rows_axes),
        P(rows_axes),
        P(rows_axes),
        P(rows_axes, None),
        P(rows_axes),
        P(rows_axes, None),
        P(rows_axes),
        P(rows_axes),
        P(rows_axes),
        P(rows_axes, None),
    )
    return jax.shard_map(
        step, mesh=mesh, in_specs=in_specs, out_specs=out_specs, check_vma=False
    )
```

```python
from functools import partial

import jax
import jax.numpy as jnp
from jax import lax
from jax.experimental import pallas as pl
from jax.experimental.pallas import tpu as pltpu
from jax.sharding import Mesh
from jax.sharding import PartitionSpec as P

H = 16
HD = 64
LN_EPS = 1e-05
NEG_FILL = -1e30
F32 = jnp.float32
BF16 = jnp.bfloat16
GROUP = ("ctx", "x", "core")
LANE = ("ctx", "x")
SWAP = [(0, 1), (1, 0)]
VMEM_LIMIT = 60 * 1024 * 1024


def mm(left, right):
    return jnp.dot(left, right, preferred_element_type=F32)


def contract(left, right, left_dim, right_dim):
    return lax.dot_general(
        left, right, (((left_dim,), (right_dim,)), ((), ())), preferred_element_type=F32
    )


def swap_core(value):
    return lax.ppermute(value, "core", SWAP)


def swap_slot(value):
    return lax.ppermute(value, "slot", SWAP)


def pick(stacked, index, axis):
    return lax.dynamic_index_in_dim(stacked, index, axis, keepdims=False)


MESH = pl.DeviceIdType.MESH


def at_device(**where):
    names = ("slot", "ctx", "x", "core")
    return tuple(where[n] if n in where else lax.axis_index(n) for n in names)


def greet(peers):
    barrier = pltpu.get_barrier_semaphore()
    for peer in peers:
        pl.semaphore_signal(barrier, inc=1, device_id=peer, device_id_type=MESH)
    pl.semaphore_wait(barrier, len(peers))


def group_peers(n_ctx, n_x):
    ctx, x, core = (lax.axis_index(n) for n in GROUP)
    peers = []
    for dz in range(n_ctx):
        for dx in range(n_x):
            for dc in range(2):
                if dz or dx or dc:
                    where = (lax.rem(ctx + dz, n_ctx), lax.rem(x + dx, n_x), lax.rem(core + dc, 2))
                    peers.append(where)
    return peers


def start_kernel(
    tok_ref, head_ref, small_ref, all_ref, heads_ref, smalls_ref,
    far_send, block_send, local_sem, head_recv, small_recv, block_recv, *, n_ctx, n_x
):
    part = tok_ref.shape[1]
    ctx, x, core = (lax.axis_index(n) for n in GROUP)
    me = (ctx * n_x + x) * 2 + core
    peers = group_peers(n_ctx, n_x)
    greet([at_device(ctx=z, x=a, core=c) for z, a, c in peers])

    def block_at(b):
        return all_ref.at[:, pl.ds(pl.multiple_of(b * part, part), part), :]

    pushes = []
    for k, (z, a, c) in enumerate(peers):
        them = (z * n_x + a) * 2 + c
        target = at_device(ctx=z, x=a, core=c)
        pushes.append(pltpu.make_async_remote_copy(
            head_ref.at[them], heads_ref.at[me], far_send.at[2 * k], head_recv.at[me],
            device_id=target, device_id_type=MESH))
        pushes.append(pltpu.make_async_remote_copy(
            small_ref, smalls_ref.at[me], far_send.at[2 * k + 1], small_recv.at[me],
            device_id=target, device_id_type=MESH))
    locals_ = [
        pltpu.make_async_copy(tok_ref, block_at(me), local_sem.at[0]),
        pltpu.make_async_copy(head_ref.at[me], heads_ref.at[me], local_sem.at[1]),
        pltpu.make_async_copy(small_ref, smalls_ref.at[me], local_sem.at[2]),
    ]

    def send(b, source, lane, target):
        return pltpu.make_async_remote_copy(
            source, block_at(b), block_send.at[lane, b], block_recv.at[b],
            device_id=target, device_id_type=MESH)

    up = at_device(ctx=lax.rem(ctx + 1, n_ctx))
    down = at_device(ctx=lax.rem(ctx + n_ctx - 1, n_ctx))
    side = at_device(x=1 - x)
    twin = at_device(core=1 - core)

    def here(b):
        return send(b, block_at(b), 0, twin)

    @pl.when(ctx + 1 < n_ctx)
    def _():
        send(me, tok_ref, 0, up).start()

    @pl.when(ctx > 0)
    def _():
        send(me, tok_ref, 1, down).start()

    send(me, tok_ref, 2, side).start()
    send(me, tok_ref, 3, twin).start()
    for copy in locals_:
        copy.start()

    for r in range(1, n_ctx):
        if r == n_ctx - 1:
            for push in pushes:
                push.start()
        low = ctx - r
        high = ctx + r

        @pl.when(low >= 0)
        def _():
            b = (low * n_x + x) * 2 + core
            here(b).wait_recv()

            @pl.when(ctx + 1 < n_ctx)
            def _():
                send(b, block_at(b), 0, up).start()

            send(b, block_at(b), 2, side).start()
            send(b, block_at(b), 3, twin).start()

        @pl.when(high < n_ctx)
        def _():
            b = (high * n_x + x) * 2 + core
            here(b).wait_recv()

            @pl.when(ctx > 0)
            def _():
                send(b, block_at(b), 1, down).start()

            send(b, block_at(b), 2, side).start()
            send(b, block_at(b), 3, twin).start()

    def from_side(z):
        b = (z * n_x + (1 - x)) * 2 + core
        here(b).wait_recv()
        send(b, block_at(b), 3, twin).start()

    from_side(ctx)
    for r in range(1, n_ctx):
        @pl.when(ctx - r >= 0)
        def _():
            from_side(ctx - r)

        @pl.when(ctx + r < n_ctx)
        def _():
            from_side(ctx + r)

    for z in range(n_ctx):
        for a in range(n_x):
            here((z * n_x + a) * 2 + 1 - core).wait_recv()
    for k, (z, a, c) in enumerate(peers):
        them = (z * n_x + a) * 2 + c
        pltpu.make_async_remote_copy(
            head_ref.at[them], heads_ref.at[them], far_send.at[2 * k], head_recv.at[them],
            device_id=twin, device_id_type=MESH).wait_recv()
        pltpu.make_async_remote_copy(
            small_ref, smalls_ref.at[them], far_send.at[2 * k + 1], small_recv.at[them],
            device_id=twin, device_id_type=MESH).wait_recv()
    for push in pushes:
        push.wait_send()
    for copy in locals_:
        copy.wait()

    for z in range(n_ctx):
        b = (z * n_x + x) * 2 + core

        @pl.when((z <= ctx) & (ctx + 1 < n_ctx))
        def _():
            send(b, block_at(b), 0, up).wait_send()

        @pl.when((z >= ctx) & (ctx > 0))
        def _():
            send(b, block_at(b), 1, down).wait_send()

        send(b, block_at(b), 2, side).wait_send()
        send(b, block_at(b), 3, twin).wait_send()
        other = (z * n_x + (1 - x)) * 2 + core
        send(other, block_at(other), 3, twin).wait_send()


def gather_start(tokens, heads, small):
    n_ctx, n_x = lax.axis_size("ctx"), lax.axis_size("x")
    n = 2 * n_ctx * n_x
    slots, part, width = tokens.shape
    vmem = pl.BlockSpec(memory_space=pltpu.VMEM)
    anywhere = pl.BlockSpec(memory_space=pl.ANY)
    dma = pltpu.SemaphoreType.DMA
    return pl.pallas_call(
        partial(start_kernel, n_ctx=n_ctx, n_x=n_x),
        in_specs=[vmem, vmem, vmem],
        out_specs=[anywhere, vmem, vmem],
        out_shape=[
            jax.ShapeDtypeStruct((slots, n * part, width), tokens.dtype),
            jax.ShapeDtypeStruct(heads.shape, heads.dtype),
            jax.ShapeDtypeStruct((n,) + small.shape, small.dtype),
        ],
        scratch_shapes=[
            dma((2 * (n - 1),)), dma((4, n)), dma((3,)), dma((n,)), dma((n,)), dma((n,))
        ],
        compiler_params=pltpu.CompilerParams(
            collective_id=1, has_side_effects=True, vmem_limit_bytes=VMEM_LIMIT
        ),
        cost_estimate=pl.CostEstimate(
            flops=0, bytes_accessed=2 * n * tokens.size, transcendentals=0
        ),
        name="gather_start",
    )(tokens, heads, small)


def finish_kernel(
    out_ref, small_ref, qkv_ref, red_ref, join_ref, weight_ref, one_ref,
    g_down, g_up, g_out, g_small, g_qkv, g_bias, g_in,
    pair_small, pair_qkv, sum_qkv, qkvs,
    pair_down, pair_out, last_up, joins, partial_in, pair_in,
    join_send, join_recv, far_send, qkv_recv, y_send, y_recv,
    *, n_ctx, n_x
):
    ctx, x, core = (lax.axis_index(n) for n in GROUP)
    slot = lax.axis_index("slot")
    chip = ctx * n_x + x
    me = 2 * chip + core
    shard, width = g_out.shape
    part = g_down.shape[0] // 2
    peers = group_peers(n_ctx, n_x)
    lane_peers = [(z, a) for z, a, c in peers[1::2]]
    across = at_device(slot=1 - slot)
    corner = at_device(slot=1 - slot, core=1 - core)
    twin = at_device(core=1 - core)
    greet([at_device(ctx=z, x=a, core=c) for z, a, c in peers] + [across, corner])

    def remote(source, target_ref, send_sem, recv_sem, target):
        return pltpu.make_async_remote_copy(
            source, target_ref, send_sem, recv_sem, device_id=target, device_id_type=MESH)

    started = []

    def launch(copy):
        copy.start()
        started.append(copy)
        return copy

    def pair_copy(i, source, target_ref, target):
        return launch(remote(source, target_ref, y_send.at[i], y_recv.at[i], target))

    qkv_copy = pair_copy(0, qkv_ref, pair_qkv, across)
    mine = pl.multiple_of(part + core * shard, shard)
    theirs = pl.multiple_of(part + (1 - core) * shard, shard)
    for k, (z, a) in enumerate(lane_peers):
        launch(remote(
            join_ref.at[z * n_x + a], joins.at[chip], join_send.at[k], join_recv.at[chip],
            at_device(ctx=z, x=a)))
    down_copy = pair_copy(4, red_ref.at[pl.ds(0, part)], pair_down, across)
    quarter_copies = [
        pair_copy(5, red_ref.at[pl.ds(theirs, shard)], last_up.at[0], twin),
        pair_copy(6, red_ref.at[pl.ds(mine, shard)], last_up.at[1], across),
        pair_copy(7, red_ref.at[pl.ds(theirs, shard)], last_up.at[2], corner),
    ]

    small_copy = pair_copy(1, small_ref, pair_small, across)
    out_copy = pair_copy(3, out_ref, pair_out, across)
    qkv_copy.wait_recv()
    sum_qkv[...] = (qkv_ref[...].astype(F32) + pair_qkv[...].astype(F32)).astype(BF16)
    for k, (z, a, c) in enumerate(peers):
        them = (z * n_x + a) * 2 + c
        launch(remote(
            sum_qkv.at[them], qkvs.at[me], far_send.at[k], qkv_recv.at[me],
            at_device(ctx=z, x=a, core=c)))
    qkvs[me] = sum_qkv[me]

    def add_head(source, rows_of, first):
        weight = weight_ref[source]
        for h in range(2):
            owner = core if h == 0 else 1 - core
            rows = rows_of(owner)
            cols = rows.shape[2] // 2
            rows = jnp.concatenate(
                [r for t in range(rows.shape[0]) for r in (rows[t, :, :cols], rows[t, :, cols:])],
                axis=0)
            term = contract(rows, weight, 1, 1)
            partial_in[h] = term if first else partial_in[h] + term

    add_head(chip, lambda owner: join_ref[chip, owner], True)

    half = pl.multiple_of(slot * part, part)
    other_half = pl.multiple_of((1 - slot) * part, part)
    g_down[pl.ds(half, part), :] = red_ref[pl.ds(0, part), :].astype(F32)
    down_copy.wait_recv()
    g_down[pl.ds(other_half, part), :] = pair_down[...].astype(F32)

    def place_quarter(rows, quarter_core, quarter_slot):
        for k in range(n_ctx * n_x):
            at = pl.multiple_of(((2 * k + quarter_core) * 2 + quarter_slot) * part, part)
            g_up[:, pl.ds(at, part)] = rows[:, k * part : (k + 1) * part].astype(F32)

    place_quarter(red_ref[pl.ds(mine, shard), :], core, slot)
    quarter_copies[0].wait_recv()
    place_quarter(last_up[0], 1 - core, slot)
    quarter_copies[1].wait_recv()
    place_quarter(last_up[1], core, 1 - slot)
    quarter_copies[2].wait_recv()
    place_quarter(last_up[2], 1 - core, 1 - slot)

    @pl.loop(1, n_ctx * n_x)
    def _(o):
        source = lax.rem(ctx + o // n_x, n_ctx) * n_x + lax.rem(x + o % n_x, n_x)
        remote(
            join_ref.at[source], joins.at[source], join_send.at[0], join_recv.at[source], twin
        ).wait_recv()
        add_head(source, lambda owner: joins[source, owner], False)

    in_copy = pair_copy(2, partial_in.at[1], pair_in, twin)

    small_copy.wait_recv()
    g_small[...] = small_ref[...].astype(F32) + pair_small[...].astype(F32)
    in_copy.wait_recv()
    g_in[...] = (partial_in[0] + pair_in[...] + one_ref[...]).astype(BF16)
    for z, a, c in peers:
        them = (z * n_x + a) * 2 + c
        remote(
            sum_qkv.at[them], qkvs.at[them], far_send.at[0], qkv_recv.at[them], twin
        ).wait_recv()
    for k in range(n_ctx * n_x):
        heads = [qkvs[2 * k + c, :shard, :].astype(F32) for c in range(2)]
        for t in range(3):
            at = t * width + 2 * HD * k
            g_qkv[:, at : at + 2 * HD] = jnp.concatenate(
                [h[:, t * HD : (t + 1) * HD] for h in heads], axis=1)
        for c in range(2):
            g_bias[2 * k + c : 2 * k + c + 1, :] = qkvs[2 * k + c, shard : shard + 1, :].astype(F32)
    out_copy.wait_recv()
    g_out[...] = out_ref[...].astype(F32) + pair_out[...].astype(F32)
    for copy in started:
        copy.wait_send()


def finish_grads(out, small, qkv, reduced, joined, weight, grad_one):
    n_ctx, n_x = lax.axis_size("ctx"), lax.axis_size("x")
    n = 2 * n_ctx * n_x
    shard, width = out.shape
    part = reduced.shape[0] // 2
    vmem = pl.BlockSpec(memory_space=pltpu.VMEM)
    dma = pltpu.SemaphoreType.DMA

    def low(*shape):
        return pltpu.VMEM(shape, BF16)

    def wide(*shape):
        return jax.ShapeDtypeStruct(shape, F32)

    return pl.pallas_call(
        partial(finish_kernel, n_ctx=n_ctx, n_x=n_x),
        in_specs=[vmem] * 7,
        out_specs=[vmem] * 7,
        out_shape=[
            wide(2 * part, width),
            wide(shard, 4 * width),
            wide(shard, width),
            wide(*small.shape),
            wide(shard, 3 * width),
            wide(n, qkv.shape[2]),
            jax.ShapeDtypeStruct(grad_one.shape, BF16),
        ],
        scratch_shapes=[
            low(*small.shape),
            low(*qkv.shape),
            low(*qkv.shape),
            low(*qkv.shape),
            low(part, width),
            low(*out.shape),
            low(3, shard, width),
            low(*joined.shape),
            pltpu.VMEM((2,) + grad_one.shape, F32),
            pltpu.VMEM(grad_one.shape, F32),
            dma((n_ctx * n_x - 1,)),
            dma((n_ctx * n_x,)),
            dma((n - 1,)),
            dma((n,)),
            dma((8,)),
            dma((8,)),
        ],
        compiler_params=pltpu.CompilerParams(
            collective_id=2, has_side_effects=True, vmem_limit_bytes=VMEM_LIMIT
        ),
        cost_estimate=pl.CostEstimate(flops=0, bytes_accessed=16 * joined.size, transcendentals=0),
        name="finish_grads",
    )(out, small, qkv, reduced, joined, weight, grad_one)


def lane_gather(mine_ref, all_ref, send_sem, recv_sem, local_sem, n_ctx, n_x):
    ctx, x = lax.axis_index("ctx"), lax.axis_index("x")
    chip = ctx * n_x + x
    routes = (
        at_device(ctx=lax.rem(ctx + 1, n_ctx)),
        at_device(ctx=lax.rem(ctx + n_ctx - 1, n_ctx)),
        at_device(x=1 - x),
    )

    def send(k, lane, own=False):
        return pltpu.make_async_remote_copy(
            mine_ref if own else all_ref.at[k], all_ref.at[k], send_sem.at[lane, k], recv_sem.at[k],
            device_id=routes[lane], device_id_type=MESH)

    local = pltpu.make_async_copy(mine_ref, all_ref.at[chip], local_sem)

    def begin():
        @pl.when(ctx + 1 < n_ctx)
        def _():
            send(chip, 0, own=True).start()

        @pl.when(ctx > 0)
        def _():
            send(chip, 1, own=True).start()

        send(chip, 2, own=True).start()
        local.start()

    def relay(r):
        for sign, lane, more in ((-1, 0, ctx + 1 < n_ctx), (1, 1, ctx > 0)):
            z = ctx + sign * r

            @pl.when((z >= 0) & (z < n_ctx))
            def _():
                k = z * n_x + x
                send(k, 0).wait_recv()

                @pl.when(more)
                def _():
                    send(k, lane).start()

                send(k, 2).start()

    def end():
        for z in range(n_ctx):
            k = z * n_x + x
            send(z * n_x + 1 - x, 0).wait_recv()

            @pl.when((z <= ctx) & (ctx + 1 < n_ctx))
            def _():
                send(k, 0).wait_send()

            @pl.when((z >= ctx) & (ctx > 0))
            def _():
                send(k, 1).wait_send()

            send(k, 2).wait_send()
        local.wait()

    return begin, relay, end


def lane_gather_x_first(mine_ref, all_ref, send_sem, recv_sem, local_sem, n_ctx, n_x):
    ctx, x = lax.axis_index("ctx"), lax.axis_index("x")
    chip = ctx * n_x + x
    pair = ctx * n_x + 1 - x
    routes = (
        at_device(ctx=lax.rem(ctx + 1, n_ctx)),
        at_device(ctx=lax.rem(ctx + n_ctx - 1, n_ctx)),
        at_device(x=1 - x),
    )
    ways = ((-1, 0, ctx + 1 < n_ctx), (1, 1, ctx > 0))

    def send(k, lane, own=False):
        return pltpu.make_async_remote_copy(
            mine_ref if own else all_ref.at[k], all_ref.at[k], send_sem.at[lane, k], recv_sem.at[k],
            device_id=routes[lane], device_id_type=MESH)

    local = pltpu.make_async_copy(mine_ref, all_ref.at[chip], local_sem)

    def along(k, own=False):
        for _, lane, more in ways:
            @pl.when(more)
            def _():
                send(k, lane, own).start()

    def begin():
        send(chip, 2, own=True).start()
        along(chip, own=True)
        local.start()

    def pass_on(r, line):
        for sign, lane, more in ways:
            z = ctx + sign * r

            @pl.when((z >= 0) & (z < n_ctx))
            def _():
                k = z * n_x + line
                send(k, lane).wait_recv()

                @pl.when(more)
                def _():
                    send(k, lane).start()

    def relay(r):
        if r == 1:
            send(pair, 2).wait_recv()
            along(pair)
        else:
            pass_on(r - 1, 1 - x)
        pass_on(r, x)

    def end():
        pass_on(n_ctx - 1, 1 - x)
        send(chip, 2).wait_send()
        for z in range(n_ctx):
            for line in range(n_x):
                @pl.when((z <= ctx) & (ctx + 1 < n_ctx))
                def _():
                    send(z * n_x + line, 0).wait_send()

                @pl.when((z >= ctx) & (ctx > 0))
                def _():
                    send(z * n_x + line, 1).wait_send()

        local.wait()

    return begin, relay, end


QB = 512
KB = 512


def turn(pair, cosine, sine):
    half = HD // 2
    lanes = lax.broadcasted_iota(jnp.int32, (1, 2 * HD), 1)
    low = lax.rem(lanes, HD) < half
    swapped = jnp.where(low, pltpu.roll(pair, 2 * HD - half, 1), pltpu.roll(pair, half, 1))
    return pair * cosine + swapped * jnp.where(low, -sine, sine)


def heads_kernel(
    len_ref, tok_ref, w_ref, b_ref, cos_ref, sin_ref, wa_ref, wu_ref, wd_ref,
    q_ref, k_ref, v_ref, mix_ref, send_ref, norm_ref, fa_ref, fu_ref, fd_ref,
    a_send, a_recv, u_send, u_recv, d_send, d_recv, local_sem, *, n_ctx, n_x, part
):
    core = lax.axis_index("core")
    ctx, x = lax.axis_index("ctx"), lax.axis_index("x")
    greet([
        at_device(x=1 - x),
        at_device(ctx=lax.rem(ctx + 1, n_ctx)),
        at_device(ctx=lax.rem(ctx + n_ctx - 1, n_ctx)),
    ])
    flows = [
        lane_gather_x_first(wa_ref, fa_ref, a_send, a_recv, local_sem.at[0], n_ctx, n_x),
        lane_gather(wu_ref, fu_ref, u_send, u_recv, local_sem.at[1], n_ctx, n_x),
        lane_gather(wd_ref, fd_ref, d_send, d_recv, local_sem.at[2], n_ctx, n_x),
    ]
    for begin, _, _ in flows:
        begin()
    slots, seq, _ = q_ref.shape

    def relay(r):
        if r < n_ctx:
            for _, hop, _ in flows:
                hop(r)

    blocks = seq // QB

    def project():
        @pl.loop(0, slots * blocks)
        def _(n):
            s, i = n // blocks, lax.rem(n, blocks)
            rows = pl.ds(pl.multiple_of(i * QB, QB), QB)
            tokens = tok_ref[pl.ds(pl.multiple_of(n * QB, QB), QB), :]
            joined = mm(tokens, w_ref[...]) + b_ref[...]
            turned = turn(joined[:, : 2 * HD], cos_ref[rows, :], sin_ref[rows, :])
            q_ref[s, rows, :] = (turned[:, :HD].astype(BF16) * HD ** (-0.5)).astype(BF16)
            k_ref[s, rows, :] = turned[:, HD:].astype(BF16)
            v_ref[s, rows, :] = joined[:, 2 * HD :].astype(BF16)

    def attend():
        @pl.loop(0, slots * blocks)
        def _(n):
            s, i = n // blocks, lax.rem(n, blocks)
            length = len_ref[s]
            rows = pl.ds(pl.multiple_of(i * QB, QB), QB)
            queries = q_ref[s, rows, :]

            @pl.when(n == blocks)
            def _():
                relay(2)

            def step(j, state):
                highest, total, mix = state
                start = pl.multiple_of(j * KB, KB)
                scores = contract(queries, k_ref[s, pl.ds(start, KB), :], 1, 1)
                ids = start + lax.broadcasted_iota(jnp.int32, (1, KB), 1)
                scores = jnp.where(ids < length, scores, NEG_FILL)
                higher = jnp.maximum(highest, jnp.max(scores, axis=1, keepdims=True))
                fade = jnp.exp(highest - higher)
                weights = jnp.exp(scores - higher)
                total = total * fade + jnp.sum(weights, axis=1, keepdims=True)
                mix = mix * fade + mm(weights.astype(BF16), v_ref[s, pl.ds(start, KB), :])
                return higher, total, mix

            highest, total, mix = lax.fori_loop(
                0,
                seq // KB,
                step,
                (
                    jnp.full((QB, 1), NEG_FILL, F32),
                    jnp.zeros((QB, 1), F32),
                    jnp.zeros((QB, HD), F32),
                ),
            )
            mix = mix / total
            mix_ref[s, rows, :] = mix
            log_norm = jnp.broadcast_to(highest + jnp.log(total), (QB, 128))
            norm_ref[s, :, rows] = jnp.transpose(log_norm)[0:1, :]
            low = mix.astype(BF16)
            chips = QB // (2 * part)
            for chip in range(chips):
                for half in range(2):
                    at = (2 * chip + half) * part
                    upper, lower = low[at : at + part // 2], low[at + part // 2 : at + part]
                    send_ref[i * chips + chip, half ^ core, s] = jnp.concatenate(
                        [upper, lower], axis=1)

    project()
    relay(1)
    attend()
    for r in range(3, n_ctx):
        relay(r)
    for _, _, end in flows:
        end()


def heads(lengths, tokens, weight, bias, cosine, sine, part, *shards):
    n_ctx, n_x = lax.axis_size("ctx"), lax.axis_size("x")
    chips = n_ctx * n_x
    slots, seq = lengths.shape[0], cosine.shape[0]
    vmem = pl.BlockSpec(memory_space=pltpu.VMEM)
    anywhere = pl.BlockSpec(memory_space=pl.ANY)
    dma = pltpu.SemaphoreType.DMA
    head = jax.ShapeDtypeStruct((slots, seq, HD), BF16)
    return pl.pallas_call(
        partial(heads_kernel, n_ctx=n_ctx, n_x=n_x, part=part),
        in_specs=[pl.BlockSpec(memory_space=pltpu.SMEM)] + [vmem] * 8,
        out_specs=[vmem] * 6 + [anywhere] * 3,
        out_shape=[
            head,
            head,
            head,
            jax.ShapeDtypeStruct((slots, seq, HD), F32),
            jax.ShapeDtypeStruct((chips, 2, slots, part // 2, 2 * HD), BF16),
            jax.ShapeDtypeStruct((slots, 1, seq), F32),
        ]
        + [jax.ShapeDtypeStruct((chips,) + w.shape, w.dtype) for w in shards],
        scratch_shapes=[dma((3, chips)), dma((chips,))] * 3 + [dma((3,))],
        compiler_params=pltpu.CompilerParams(
            collective_id=5, has_side_effects=True, vmem_limit_bytes=VMEM_LIMIT
        ),
        cost_estimate=pl.CostEstimate(
            flops=16 * slots * seq * seq * HD,
            bytes_accessed=2 * tokens.size,
            transcendentals=slots * seq * seq,
        ),
        name="heads",
    )(lengths, tokens, weight, bias, cosine, sine, *shards)


def grads_kernel(
    len_ref, q_ref, k_ref, v_ref, g_ref, norm_ref, dot_ref, tok_ref, cos_ref, sin_ref,
    down_ref, up_ref, out_ref, small_ref,
    join_ref, grad_ref, red_ref, sum_ref, small_sum,
    dqt, key_grads, value_grads, total, bias, x_down, x_up, x_out, s_down, s_up, s_out,
    z_down, z_up, z_out, top_down, top_up, top_out, own_down, own_up, own_out, smalls,
    x_send, x_recv, z_send, z_recv, top_recv, small_send, small_recv, *, n_ctx, n_x, part
):
    ctx, x, core = (lax.axis_index(n) for n in GROUP)
    me = (ctx * n_x + x) * 2 + core
    peers = group_peers(n_ctx, n_x)
    greet([at_device(ctx=z, x=a, core=c) for z, a, c in peers])
    side = at_device(x=1 - x)
    arrays = (
        (down_ref, x_down, s_down, z_down, top_down, own_down),
        (up_ref, x_up, s_up, z_up, top_up, own_up),
        (out_ref, x_out, s_out, z_out, top_out, own_out),
    )

    def remote(source, target_ref, send_sem, recv_sem, target):
        return pltpu.make_async_remote_copy(
            source, target_ref, send_sem, recv_sem, device_id=target, device_id_type=MESH)

    orders = [
        sorted(range(n_ctx), key=lambda p, z=z: (p == z, -abs(p - z), min(p, n_ctx - 1 - p))) for z in range(n_ctx)
    ]
    places = [
        sum(jnp.where(ctx == z, orders[z][j], 0) for z in range(n_ctx)) for j in range(n_ctx)
    ]
    above = at_device(ctx=lax.rem(ctx + 1, n_ctx))
    below = at_device(ctx=lax.rem(ctx + n_ctx - 1, n_ctx))
    first = [
        [
            remote(
                ref.at[places[j] * n_x + 1 - x], x_in.at[j], x_send.at[i, j], x_recv.at[i, j], side)
            for i, (ref, x_in, _, _, _, _) in enumerate(arrays)
        ]
        for j in range(n_ctx)
    ]

    def hop(j, i, target, last=False):
        _, _, s_low, z_in, top, _ = arrays[i]
        p = places[j]
        return remote(
            s_low.at[min(j, n_ctx - 2)], top if last else z_in.at[p], z_send.at[i, min(j, n_ctx - 2)],
            top_recv.at[i] if last else z_recv.at[i, p], target)

    pushes = []
    for k, (z, a, c) in enumerate(peers):
        them = (z * n_x + a) * 2 + c
        pushes.append(remote(
            small_ref.at[them], smalls.at[me], small_send.at[k], small_recv.at[me],
            at_device(ctx=z, x=a, core=c)))
    for copies in first:
        for copy in copies:
            copy.start()
    for copy in pushes:
        copy.start()
    smalls[me] = small_ref[me]

    def stage(j):
        p = places[j]
        going_up = p > ctx
        for i, (ref, x_in, s_low, z_in, _, own) in enumerate(arrays):
            first[j][i].wait_recv()
            own[...] = ref[p * n_x + x].astype(F32) + x_in[j].astype(F32)
            if j == n_ctx - 1:
                continue

            @pl.when((going_up & (ctx > 0)) | ((p < ctx) & (ctx < n_ctx - 1)))
            def _():
                hop(j, i, above).wait_recv()
                own[...] += z_in[p].astype(F32)

            s_low[j] = own[...].astype(BF16)

            @pl.when(going_up)
            def _():
                hop(j, i, above).start()

            @pl.when(p < ctx - 1)
            def _():
                hop(j, i, below).start()

            @pl.when(p == ctx - 1)
            def _():
                hop(j, i, below, last=True).start()

    slots, seq, _ = q_ref.shape
    total[...] = jnp.zeros_like(total)
    bias[...] = jnp.zeros_like(bias)

    def attention(s, between):
        length = len_ref[s]
        dqt[...] = jnp.zeros_like(dqt)

        @pl.loop(0, seq // KB)
        def _(j):
            start = pl.multiple_of(j * KB, KB)
            key_block = k_ref[s, pl.ds(start, KB), :]
            value_block = v_ref[s, pl.ds(start, KB), :]
            turned = jnp.transpose(key_block.astype(F32)).astype(BF16)
            ids = start + lax.broadcasted_iota(jnp.int32, (KB, 1), 0)
            shift = jnp.where(ids < length, 0.0, NEG_FILL)
            for at_step, number in between:
                @pl.when(j == at_step)
                def _():
                    stage(number)

            def step(i, state):
                key_grad, value_grad = state
                at = pl.multiple_of(i * QB, QB)
                queries = q_ref[s, pl.ds(at, QB), :]
                grads = g_ref[s, pl.ds(at, QB), :]
                scores = contract(key_block, queries, 1, 1) + shift
                probs = jnp.exp(scores - norm_ref[s, :, pl.ds(at, QB)])
                grad_probs = contract(value_block, grads, 1, 1)
                grad_scores = (probs * (grad_probs - dot_ref[s, :, pl.ds(at, QB)])).astype(BF16)
                value_grad = value_grad + mm(probs.astype(BF16), grads)
                key_grad = key_grad + mm(grad_scores, queries)
                dqt[:, pl.ds(at, QB)] += mm(turned, grad_scores)
                return key_grad, value_grad

            zero = jnp.zeros((KB, HD), F32)
            key_grad, value_grad = lax.fori_loop(0, seq // QB, step, (zero, zero))
            key_grads[pl.ds(start, KB), :] = key_grad
            value_grads[pl.ds(start, KB), :] = value_grad

    def join(s):
        @pl.loop(0, seq // QB)
        def _(i):
            at = pl.multiple_of(i * QB, QB)
            rows = pl.ds(at, QB)
            query_grad = jnp.transpose(dqt[:, rows]) * HD ** (-0.5)
            pair = jnp.concatenate([query_grad, key_grads[rows, :]], axis=1)
            turned = turn(pair, cos_ref[rows, :], -sin_ref[rows, :])
            joined = jnp.concatenate([turned, value_grads[rows, :]], axis=1).astype(BF16)
            chips = QB // (2 * part)
            for chip in range(chips):
                for owner in range(2):
                    near = (2 * chip + owner) * part
                    upper = joined[near : near + part // 2]
                    lower = joined[near + part // 2 : near + part]
                    join_ref[i * chips + chip, owner, s] = jnp.concatenate([upper, lower], axis=1)
            tokens = tok_ref[pl.ds(pl.multiple_of(s * seq + at, QB), QB), :]
            total[...] += contract(joined, tokens, 0, 0)
            bias[...] += jnp.sum(joined.astype(F32), axis=0, keepdims=True)

    for s in range(slots):
        attention(s, [(1, 1)] if s == 1 else [])
        stage(0 if s == 0 else 2)
        join(s)
    turned_total = jnp.transpose(total[...])
    shard = turned_total.shape[0] // grad_ref.shape[0]
    extra = jnp.broadcast_to(bias[...], (grad_ref.shape[1] - shard, bias.shape[1]))
    for d in range(grad_ref.shape[0]):
        grad_ref[d, :shard] = turned_total[d * shard : (d + 1) * shard].astype(BF16)
        grad_ref[d, shard:] = extra.astype(BF16)
    for j in range(slots + 1, n_ctx):
        stage(j)
    for z, a, c in peers:
        them = (z * n_x + a) * 2 + c
        remote(
            small_ref.at[them], smalls.at[them], small_send.at[0], small_recv.at[them], side
        ).wait_recv()
    small_sum[...] = jnp.sum(smalls[...].astype(F32), axis=0).astype(BF16)
    for i, (_, _, _, z_in, top, own) in enumerate(arrays):
        @pl.when(ctx > 0)
        def _():
            hop(n_ctx - 1, i, above).wait_recv()
            own[...] += z_in[ctx].astype(F32)

        @pl.when(ctx < n_ctx - 1)
        def _():
            hop(0, i, below, last=True).wait_recv()
            own[...] += top[...].astype(F32)

    rows = own_down.shape[0]
    red_ref[:rows] = own_down[...].astype(BF16)
    red_ref[rows:] = own_up[...].astype(BF16)
    sum_ref[...] = own_out[...].astype(BF16)
    for copies in first + [pushes]:
        for copy in copies:
            copy.wait_send()
    for j in range(n_ctx - 1):
        for i in range(len(arrays)):
            hop(j, i, above).wait_send()


def grads(lengths, queries, keys, values, grad_heads, norms, dots, tokens, cosine, sine,
          down, up, out, small, part):
    n_ctx, n_x = lax.axis_size("ctx"), lax.axis_size("x")
    n = 2 * n_ctx * n_x
    slots, seq, _ = queries.shape
    width = tokens.shape[1]
    shard = width // n
    cols = 3 * HD
    vmem = pl.BlockSpec(memory_space=pltpu.VMEM)
    dma = pltpu.SemaphoreType.DMA
    parts = (down, up, out)

    def low(*dims):
        return jax.ShapeDtypeStruct(dims, BF16)

    return pl.pallas_call(
        partial(grads_kernel, n_ctx=n_ctx, n_x=n_x, part=part),
        in_specs=[pl.BlockSpec(memory_space=pltpu.SMEM)] + [vmem] * 13,
        out_specs=[vmem] * 5,
        out_shape=[
            low(seq // (2 * part), 2, slots, part // 2, 2 * cols),
            low(n, shard + 16, cols),
            low(down.shape[1] + up.shape[1], width),
            low(*out.shape[1:]),
            low(*small.shape[1:]),
        ],
        scratch_shapes=[
            pltpu.VMEM((HD, seq), F32),
            pltpu.VMEM((seq, HD), F32),
            pltpu.VMEM((seq, HD), F32),
            pltpu.VMEM((cols, width), F32),
            pltpu.VMEM((1, cols), F32),
        ]
        + [pltpu.VMEM((n_ctx,) + t.shape[1:], BF16) for t in parts]
        + [pltpu.VMEM((n_ctx - 1,) + t.shape[1:], BF16) for t in parts]
        + [pltpu.VMEM((n_ctx,) + t.shape[1:], BF16) for t in parts]
        + [pltpu.VMEM(t.shape[1:], BF16) for t in parts]
        + [pltpu.VMEM(t.shape[1:], F32) for t in parts]
        + [
            pltpu.VMEM(small.shape, BF16),
            dma((3, n_ctx)),
            dma((3, n_ctx)),
            dma((3, n_ctx - 1)),
            dma((3, n_ctx)),
            dma((3,)),
            dma((n - 1,)),
            dma((n,)),
        ],
        compiler_params=pltpu.CompilerParams(
            collective_id=6, has_side_effects=True, vmem_limit_bytes=VMEM_LIMIT
        ),
        cost_estimate=pl.CostEstimate(
            flops=40 * slots * seq * seq * HD,
            bytes_accessed=4 * tokens.size,
            transcendentals=slots * seq * seq,
        ),
        name="grads",
    )(lengths, queries, keys, values, grad_heads, norms, dots, tokens, cosine, sine,
      down, up, out, small)


def norm_forward(values, gain, shift):
    center = values - jnp.mean(values, axis=-1, keepdims=True)
    spread = jnp.mean(center * center, axis=-1, keepdims=True)
    root = lax.rsqrt(spread + LN_EPS)
    unit = center * root
    return unit * gain + shift, unit, root


def norm_backward(grad, unit, root, gain):
    scaled = grad * gain
    inner = scaled - jnp.mean(scaled, axis=-1, keepdims=True)
    inner = inner - unit * jnp.mean(scaled * unit, axis=-1, keepdims=True)
    return root * inner, jnp.sum(grad * unit, axis=0), jnp.sum(grad, axis=0)


def gelu_pair(values):
    half = 0.5 + 0.5 * lax.erf(values * 0.7071067811865476)
    bell = jnp.exp(-0.5 * values * values) * 0.3989422804014327
    return values * half, half + values * bell


def rope_rows(positions):
    halfway = HD // 2
    ladder = jnp.arange(halfway, dtype=F32) * (2.0 / HD)
    frequency = jnp.power(jnp.float32(10000.0), -ladder)
    angles = positions[:, None] * frequency[None, :]
    return jnp.cos(angles), jnp.sin(angles)


def layer_kernel(
    sent_ref, tok_ref, wo_ref, up_ref, down_ref, vec_ref, full_ref, lane_ref,
    merged_ref, out_ref, one_ref, ghead_ref, att_ref, vecs_ref, d_down_ref, d_up_ref, lanes_out,
    first, first_in, hid, act, slope, gdn, gup, hidden, unit_one, two,
    roots, near, near_in, far, far_in, low_out, low_in, send_sem, recv_sem, out_sem,
    lane_send, lane_recv, heads_in, push_send, push_recv,
    gm, heads_out, heads_back, back_send, back_recv, *, n_ctx, n_x
):
    core, slot = lax.axis_index("core"), lax.axis_index("slot")
    twin, across = at_device(core=1 - core), at_device(slot=1 - slot)
    ctx, x = lax.axis_index("ctx"), lax.axis_index("x")
    chip = ctx * n_x + x
    others = [
        (lax.rem(ctx + o // n_x, n_ctx), lax.rem(x + o % n_x, n_x)) for o in range(1, n_ctx * n_x)
    ]
    greet([twin, across] + [at_device(ctx=z, x=a) for z, a in others])
    pushes = [
        pltpu.make_async_remote_copy(
            sent_ref.at[z * n_x + a], heads_in.at[chip], push_send.at[o], push_recv.at[chip],
            device_id=at_device(ctx=z, x=a), device_id_type=MESH)
        for o, (z, a) in enumerate(others)
    ]
    for push in pushes:
        push.start()
    heads_in[chip] = sent_ref[chip]
    begin_lane, relay_lane, end_lane = lane_gather(
        lane_ref, lanes_out, lane_send, lane_recv, out_sem.at[0], n_ctx, n_x)
    rows, width = tok_ref.shape
    half = rows // 2
    tile = 256
    count = [0]
    started = []

    def launch(source, target_ref, target):
        i = count[0]
        count[0] += 1
        copy = pltpu.make_async_remote_copy(
            source, target_ref, send_sem.at[i], recv_sem.at[i],
            device_id=target, device_id_type=MESH)
        copy.start()
        started.append(copy)
        return copy

    def columns(body, n=width // tile):
        @pl.loop(0, n)
        def _(t):
            body(pl.ds(pl.multiple_of(t * tile, tile), tile))

    def chunks(body, size=64):
        @pl.loop(0, rows // size)
        def _(t):
            body(pl.ds(pl.multiple_of(t * size, size), size))

    def exchange(buf, turn, stage, product, between):
        halves = [
            launch(buf.at[pl.ds(h * half, half)], buf.at[pl.ds((2 + h) * rows, half)], across)
            for h in range(2)
        ]
        to_twin = launch(buf.at[pl.ds(0, rows)], buf.at[pl.ds(rows, rows)], twin)
        near_buf, far_buf = near.at[turn], far.at[turn]
        to_twin.wait_recv()
        stage(0, 2 * rows)
        product(0, 2 * rows, near_buf, 0)
        near_copy = launch(
            near_buf.at[pl.ds(rows, rows)], near_in.at[turn], twin)
        between()
        back = []
        for h in range(2):
            at = (2 + h) * rows
            halves[h].wait_recv()
            launch(
                buf.at[pl.ds(at, half)], buf.at[pl.ds(at + half, half)], twin).wait_recv()
            stage(at, rows)
            product(at, rows, far_buf, h * rows)
            i = 2 * turn + h
            launch(
                far_buf.at[pl.ds(h * rows + half, half)], far_in.at[i], twin).wait_recv()
            low_out[i] = (far_buf[pl.ds(h * rows, half), :] + far_in[i]).astype(BF16)
            back.append(launch(low_out.at[i], low_in.at[i], across))
        return near_copy, back

    for o, (z, a) in enumerate(others):
        source = z * n_x + a
        pltpu.make_async_remote_copy(
            sent_ref.at[source], heads_in.at[source], push_send.at[o], push_recv.at[source],
            device_id=twin, device_id_type=MESH).wait_recv()
    begin_lane()
    _, owners, slots, packed, pair_width = heads_in.shape
    for k in range(0, n_ctx * n_x, 2):
        for h in range(owners):
            for t in range(slots):
                left, right = heads_in[k, h, t], heads_in[k + 1, h, t]
                for piece in range(2):
                    at = ((h * slots + t) * 2 + piece) * packed
                    of = slice(piece * HD, (piece + 1) * HD)
                    merged_ref[at : at + packed, k * HD : (k + 2) * HD] = jnp.concatenate(
                        [left[:, of], right[:, of]], axis=1)

    def out_product(cols):
        first[:, cols] = mm(merged_ref[...], wo_ref[:, cols])

    columns(out_product)
    launch(first.at[pl.ds(rows, rows)], first_in, twin).wait_recv()

    def norm_one(at):
        values = tok_ref[at, :].astype(F32) + first[at, :] + first_in[at, :] + vec_ref[0:1, :]
        normed, unit, root = norm_forward(values, vec_ref[1:2, :], vec_ref[2:3, :])
        hidden[at, :] = normed
        unit_one[at, :] = unit
        roots[0, at, :] = jnp.broadcast_to(root, (root.shape[0], 128))
        hid[at, :] = normed.astype(BF16)

    chunks(norm_one)

    def up_stage(start, size):
        def body(cols):
            values = mm(hid[start : start + size, :], up_ref[:, cols]) + vec_ref[3:4, cols]
            active, bend = gelu_pair(values)
            act[start : start + size, cols] = active.astype(BF16)
            slope[start : start + size, cols] = bend

        columns(body)

    def down_product(start, size, target, at):
        def body(cols):
            target[at : at + size, cols] = mm(act[start : start + size, :], down_ref[:, cols])

        columns(body)

    near_copy, back = exchange(hid, 0, up_stage, down_product, lambda: relay_lane(1))
    relay_lane(2)
    vecs_ref[...] = jnp.zeros_like(vecs_ref)
    near_copy.wait_recv()

    def norm_two(at, h, local):
        downward = near[0, at, :] + near_in[0, at, :] + low_in[h, local, :].astype(F32)
        values = hidden[at, :] + downward + vec_ref[4:5, :]
        normed, unit, root = norm_forward(values, vec_ref[5:6, :], vec_ref[6:7, :])
        out_ref[at, :] = normed.astype(BF16)
        grad, gain, shift = norm_backward(full_ref[at, :], unit, root, vec_ref[5:6, :])
        two[at, :] = grad
        low = grad.astype(BF16)
        gdn[at, :] = low
        vecs_ref[5:6, :] += gain[None]
        vecs_ref[6:7, :] += shift[None]
        vecs_ref[4:5, :] += jnp.sum(low.astype(F32), axis=0, keepdims=True)

    def by_half(body, h, size=64):
        @pl.loop(0, half // size)
        def _(t):
            local = pl.multiple_of(t * size, size)
            body(pl.ds(h * half + local, size), h, pl.ds(local, size))

    for h in range(2):
        back[h].wait_recv()
        by_half(norm_two, h)

    def back_stage(start, size):
        def body(cols):
            grads = contract(gdn[start : start + size, :], down_ref[cols, :], 1, 1)
            low = (grads * slope[start : start + size, cols]).astype(BF16)
            gup[start : start + size, cols] = low
            vecs_ref[3:4, cols] += jnp.sum(low.astype(F32), axis=0, keepdims=True)

        columns(body)

    def back_product(start, size, target, at):
        def body(cols):
            target[at : at + size, cols] = contract(
                gup[start : start + size, :], up_ref[cols, :], 1, 1)

        columns(body)

    def last_relays():
        for r in range(3, n_ctx):
            relay_lane(r)

    near_copy, back = exchange(gdn, 1, back_stage, back_product, last_relays)
    near_copy.wait_recv()

    def norm_back(at, h, local):
        grad = near[1, at, :] + near_in[1, at, :] + low_in[2 + h, local, :].astype(F32)
        grad = grad + two[at, :]
        root = roots[0, at, 0:1]
        one, gain, shift = norm_backward(grad, unit_one[at, :], root, vec_ref[1:2, :])
        one_ref[at, :] = one
        low = one.astype(BF16)
        att_ref[at, :] = low
        vecs_ref[1:2, :] += gain[None]
        vecs_ref[2:3, :] += shift[None]
        vecs_ref[0:1, :] += jnp.sum(low.astype(F32), axis=0, keepdims=True)

    for h in range(2):
        back[h].wait_recv()
        by_half(norm_back, h)
    launch(att_ref.at[pl.ds(0, rows)], att_ref.at[pl.ds(rows, rows)], twin).wait_recv()

    def merged_product(cols):
        gm[:, cols] = contract(att_ref[...], wo_ref[cols, :], 1, 1).astype(BF16)

    columns(merged_product, wo_ref.shape[0] // tile)
    for k in range(n_ctx * n_x):
        of = slice(k * HD, (k + 1) * HD)
        for h in range(owners):
            for t in range(slots):
                at = (h * slots + t) * 2 * packed
                heads_out[k, h, t] = jnp.concatenate(
                    [gm[at : at + packed, of], gm[at + packed : at + 2 * packed, of]], axis=1)
    returns = [
        pltpu.make_async_remote_copy(
            heads_out.at[z * n_x + a], heads_back.at[chip], back_send.at[o], back_recv.at[chip],
            device_id=at_device(ctx=z, x=a), device_id_type=MESH)
        for o, (z, a) in enumerate(others)
    ]
    for copy in returns:
        copy.start()
    heads_back[chip] = heads_out[chip]

    half_tile = tile // 2

    @pl.loop(0, width // tile)
    def _(t):
        cols = pl.ds(pl.multiple_of(t * tile, tile), tile)
        down_grad = contract(act[:, cols], gdn[...], 0, 0).astype(BF16)
        up_grad = contract(hid[:, cols], gup[...], 0, 0).astype(BF16)
        for piece in range(2):
            of = slice(piece * half_tile, (piece + 1) * half_tile)
            d_down_ref[2 * t + piece] = down_grad[of]
            d_up_ref[2 * t + piece] = up_grad[of]

    for o, (z, a) in enumerate(others):
        source = z * n_x + a
        pltpu.make_async_remote_copy(
            heads_out.at[source], heads_back.at[source], back_send.at[o], back_recv.at[source],
            device_id=twin, device_id_type=MESH).wait_recv()
    for k in range(n_ctx * n_x):
        for h in range(owners):
            owner = core if h == 0 else 1 - core
            at = pl.multiple_of((2 * k + owner) * 2 * packed, 2 * packed)
            for t in range(slots):
                block = heads_back[k, h, t]
                ghead_ref[t, pl.ds(at, packed), :] = block[:, :HD]
                ghead_ref[t, pl.ds(at + packed, packed), :] = block[:, HD:]
    end_lane()
    for copy in started + pushes + returns:
        copy.wait_send()


def layer(sent, tokens, w_out, up, down, vectors, grad_full, lane_shard):
    n_ctx, n_x = lax.axis_size("ctx"), lax.axis_size("x")
    chips = n_ctx * n_x
    rows, width = tokens.shape
    hidden = up.shape[1]
    lane = w_out.shape[0]
    slots = sent.shape[2]
    vmem = pl.BlockSpec(memory_space=pltpu.VMEM)
    anywhere = pl.BlockSpec(memory_space=pl.ANY)
    dma = pltpu.SemaphoreType.DMA

    def shape(*dims, dtype=BF16):
        return jax.ShapeDtypeStruct(dims, dtype)

    def wide(*dims):
        return pltpu.VMEM(dims, F32)

    def low(*dims):
        return pltpu.VMEM(dims, BF16)

    return pl.pallas_call(
        partial(layer_kernel, n_ctx=n_ctx, n_x=n_x),
        in_specs=[vmem] * 8,
        out_specs=[vmem] * 8 + [anywhere],
        out_shape=[
            shape(2 * rows, lane),
            shape(rows, width),
            shape(rows, width, dtype=F32),
            shape(slots, 2 * chips * (rows // slots), HD),
            shape(2 * rows, width),
            shape(8, width, dtype=F32),
            shape(chips, hidden // chips, width),
            shape(chips, width // chips, hidden),
            shape(chips, *lane_shard.shape),
        ],
        scratch_shapes=[
            wide(2 * rows, width),
            wide(rows, width),
            low(4 * rows, width),
            low(4 * rows, hidden),
            wide(4 * rows, hidden),
            low(4 * rows, width),
            low(4 * rows, hidden),
            wide(rows, width),
            wide(rows, width),
            wide(rows, width),
            wide(1, rows, 128),
            wide(2, 2 * rows, width),
            wide(2, rows, width),
            wide(2, 2 * rows, width),
            wide(4, rows // 2, width),
            low(4, rows // 2, width),
            low(4, rows // 2, width),
            dma((24,)),
            dma((24,)),
            dma((5,)),
            dma((3, chips)),
            dma((chips,)),
            low(*sent.shape),
            dma((chips - 1,)),
            dma((chips,)),
            low(2 * rows, lane),
            low(*sent.shape),
            low(*sent.shape),
            dma((chips - 1,)),
            dma((chips,)),
        ],
        compiler_params=pltpu.CompilerParams(
            collective_id=3, has_side_effects=True, vmem_limit_bytes=VMEM_LIMIT
        ),
        cost_estimate=pl.CostEstimate(
            flops=16 * rows * width * hidden, bytes_accessed=16 * rows * width, transcendentals=0
        ),
        name="layer",
    )(sent, tokens, w_out, up, down, vectors, grad_full, lane_shard)


def head_device(
    tokens,
    lengths,
    w_qkv,
    b_qkv,
    w_out,
    b_out,
    ln1_gain,
    ln1_bias,
    w_up,
    b_up,
    w_down,
    b_down,
    ln2_gain,
    ln2_bias,
    w_proj,
    cot_out,
    cot_emb,
):
    n_lane = lax.axis_size("ctx") * lax.axis_size("x")
    n_group = 2 * n_lane
    core = lax.axis_index("core")
    slot = lax.axis_index("slot")
    chip = lax.axis_index("ctx") * lax.axis_size("x") + lax.axis_index("x")
    me = 2 * chip + core
    slots, part, width = tokens.shape
    seq = part * n_group
    rows = slots * part
    shard = width // n_group
    ff_shard = w_down.shape[0]
    ff_half = ff_shard // 2
    proj = w_proj.shape[1]
    head_cols = 3 * HD

    small = jnp.concatenate(
        [b_qkv, b_out, ln1_gain, ln1_bias, b_up, b_down, ln2_gain, ln2_bias]
    )
    small_at = [0]
    for piece in (b_qkv, b_out, ln1_gain, ln1_bias, b_up, b_down, ln2_gain, ln2_bias):
        small_at.append(small_at[-1] + piece.shape[0])
    small_rows = -(-small.shape[0] // proj)
    small_rows = -(-small_rows // 16) * 16
    small = jnp.pad(small, (0, small_rows * proj - small.shape[0])).reshape(small_rows, proj)
    def two_lanes(mine, theirs):
        low_first = jnp.stack([mine, theirs], axis=0)
        high_first = jnp.stack([theirs, mine], axis=0)
        return jnp.where(core == 0, low_first, high_first)

    up_split = w_up.reshape(shard, n_lane, 2, 2, ff_half)
    up_mine = pick(up_split, core, 2)
    up_theirs = swap_core(pick(up_split, 1 - core, 2))
    up_chip = two_lanes(pick(up_mine, slot, 2), pick(up_theirs, slot, 2))
    down_split = w_down.reshape(2, ff_half, width)

    by_head = w_qkv.reshape(shard, 3, n_group, HD).transpose(2, 0, 1, 3)
    all_tokens, my_head, packed = gather_start(
        tokens,
        by_head.reshape(n_group, shard, head_cols),
        jnp.concatenate([w_proj, small], axis=0),
    )
    proj_full = packed[:, :shard].reshape(width, proj)
    smalls = packed[:, shard:].reshape(n_group, small_rows * proj).astype(F32)
    qkv_bias, out_bias, gain_one, shift_one, up_bias, down_bias, gain_two, shift_two = (
        smalls[:, a:b].reshape(-1) for a, b in zip(small_at[:-1], small_at[1:])
    )

    head_weight = my_head.reshape(width, head_cols)
    all_tokens = all_tokens.reshape(slots * seq, width)
    head_bias = pick(qkv_bias.reshape(1, 3, n_group, HD), me, 2).reshape(1, head_cols)
    cosine, sine = rope_rows(jnp.arange(seq, dtype=jnp.int32).astype(F32))
    cos_wide = jnp.tile(cosine, (1, 4))
    sin_wide = jnp.tile(sine, (1, 4))
    queries, keys, values, mixture, send, norms, out_lane, up, down = heads(
        lengths,
        all_tokens,
        head_weight,
        head_bias,
        cos_wide,
        sin_wide,
        part,
        w_out,
        up_chip.reshape(2 * shard, n_lane * ff_half),
        pick(down_split, slot, 0),
    )
    out_lane, up, down = (t.reshape(-1, t.shape[2]) for t in (out_lane, up, down))
    bias_lane = pick(up_bias.reshape(n_lane, 2, 2, ff_half), core, 1)
    up_bias_own = pick(bias_lane, slot, 1).reshape(-1)

    place = me * part + jnp.arange(part, dtype=jnp.int32)
    live = (place[None, :] < lengths[:, None]).reshape(rows, 1)
    grad_out = jnp.where(live, cot_out.reshape(rows, width).astype(F32), 0.0)
    grad_emb = jnp.where(live, cot_emb.reshape(rows, proj), 0)
    grad_full = grad_out + contract(grad_emb, proj_full, 1, 1)
    vectors = jnp.stack(
        [out_bias, gain_one, shift_one, up_bias_own, down_bias, gain_two, shift_two, shift_two]
    )
    (
        merged,
        out_low,
        grad_one,
        grad_heads,
        grad_att,
        vector_grads,
        d_down,
        d_up,
        qkv_lane,
    ) = layer(
        send, tokens.reshape(rows, width), out_lane, up, down, vectors, grad_full, head_weight
    )
    embeds = mm(out_low, proj_full).astype(BF16)
    d_proj = contract(out_low, grad_emb, 0, 0)
    (
        d_out_bias,
        d_gain_one,
        d_shift_one,
        up_bias_own_grad,
        d_down_bias,
        d_gain_two,
        d_shift_two,
    ) = (vector_grads[i] for i in range(7))
    d_out = contract(merged, grad_att, 0, 0).astype(BF16)

    spread = (
        (jnp.arange(2) == core)[:, None, None] & (jnp.arange(2) == slot)[None, :, None]
    ).astype(F32)
    up_bias_grad = up_bias_own_grad.reshape(n_lane, 1, 1, ff_half) * spread[None]
    vectors = (
        d_out_bias,
        d_gain_one,
        d_shift_one,
        up_bias_grad.reshape(-1),
        d_down_bias,
        d_gain_two,
        d_shift_two,
    )
    small_grad = jnp.concatenate([v.reshape(n_group, -1) for v in vectors], axis=1)
    small_cols = small_grad.shape[1]
    vec_rows = -(-small_cols // proj)
    vec_rows = -(-(shard + vec_rows) // 16) * 16 - shard
    small_grad = jnp.pad(small_grad, ((0, 0), (0, vec_rows * proj - small_cols)))
    small_grad = jnp.concatenate(
        [d_proj.reshape(n_group, shard, proj), small_grad.reshape(n_group, vec_rows, proj)], axis=1
    )
    row_dots = jnp.sum(grad_heads.astype(F32) * mixture, axis=-1).reshape(slots, 1, seq)
    joined, d_qkv, reduced, out_sum, small_sum = grads(
        lengths,
        queries,
        keys,
        values,
        grad_heads,
        norms,
        row_dots,
        all_tokens,
        cos_wide,
        sin_wide,
        d_down,
        d_up,
        d_out.reshape(n_lane, shard, width),
        small_grad.astype(BF16),
        part,
    )
    grad_w_down, grad_w_up, grad_w_out, small_sum, grad_w_qkv, bias_rows, input_grad = finish_grads(
        out_sum,
        small_sum,
        d_qkv,
        reduced,
        joined,
        qkv_lane,
        grad_one,
    )
    grad_w_proj = small_sum[:shard]
    vec_sum = small_sum[shard:].reshape(-1)
    vec_outs = []
    at = 0
    for v in vectors:
        size = v.size // n_group
        vec_outs.append(vec_sum[at : at + size])
        at += size
    (
        grad_b_out,
        grad_gain_one,
        grad_shift_one,
        grad_b_up,
        grad_b_down,
        grad_gain_two,
        grad_shift_two,
    ) = vec_outs

    qkv_bias_grad = bias_rows.reshape(n_group, 3, HD).transpose(1, 0, 2).reshape(-1)
    grad_b_qkv = lax.dynamic_slice(qkv_bias_grad, (me * b_qkv.shape[0],), (b_qkv.shape[0],))

    return (
        out_low.reshape(slots, part, width),
        embeds.reshape(slots, part, proj),
        input_grad.reshape(slots, part, width),
        grad_w_qkv,
        grad_b_qkv,
        grad_w_out,
        grad_b_out,
        grad_gain_one,
        grad_shift_one,
        grad_w_up,
        grad_b_up,
        grad_w_down,
        grad_b_down,
        grad_gain_two,
        grad_shift_two,
        grad_w_proj,
    )


def layer_norm(hidden, gain, shift):
    center = hidden - jnp.mean(hidden, axis=-1, keepdims=True)
    spread = jnp.mean(center * center, axis=-1, keepdims=True)
    return center * lax.rsqrt(spread + LN_EPS) * gain + shift


def rope_tables(positions, head_width):
    halfway = head_width // 2
    ladder = jnp.arange(halfway, dtype=jnp.float32) * (2.0 / head_width)
    frequency = jnp.power(jnp.float32(10000.0), -ladder)
    angles = positions[:, None] * frequency[None, :]
    return (jnp.cos(angles)[:, None, :], jnp.sin(angles)[:, None, :])


def rotate(values, cosine, sine_part):
    halfway = values.shape[-1] // 2
    first_half = values[..., :halfway]
    second_half = values[..., halfway:]
    return jnp.concatenate(
        [
            first_half * cosine - second_half * sine_part,
            second_half * cosine + first_half * sine_part,
        ],
        axis=-1,
    )


def block_scores(query_block, key_block, key_start, length, scale):
    scores = (
        jnp.einsum("qhd,khd->hqk", query_block, key_block, preferred_element_type=jnp.float32)
        * scale
    )
    key_ids = key_start + jnp.arange(key_block.shape[0], dtype=jnp.int32)
    return jnp.where((key_ids < length)[None, None, :], scores, NEG_FILL)


def per_device(
    tokens,
    lengths,
    w_qkv,
    b_qkv,
    w_out,
    b_out,
    ln1_gain,
    ln1_bias,
    w_up,
    b_up,
    w_down,
    b_down,
    ln2_gain,
    ln2_bias,
    w_proj,
    cot_out,
    cot_emb,
):
    n_fsdp = lax.axis_size("fsdp")
    n_ctx = lax.axis_size("ctx")
    ctx_at = lax.axis_index("ctx")
    fsdp_at = lax.axis_index("fsdp")
    groups, tok_slot, width = tokens.shape
    heads_here = H // n_fsdp
    lane_width = heads_here * HD
    span_rows = tok_slot * n_fsdp
    key_count = span_rows * n_ctx
    row_count = groups * tok_slot
    scale = HD ** (-0.5)
    query_rows = min(512, span_rows)
    key_rows = min(2048, key_count // 4)
    query_blocks = span_rows // query_rows
    key_blocks = key_count // key_rows
    key_starts = jnp.arange(key_blocks, dtype=jnp.int32) * key_rows
    qkv_full, qkv_bias, out_full, out_bias, gain_one, shift_one = (
        lax.all_gather(w_qkv, ("ctx", "fsdp"), axis=0, tiled=True),
        lax.all_gather(b_qkv, ("ctx", "fsdp"), axis=0, tiled=True),
        lax.all_gather(w_out, ("ctx", "fsdp"), axis=0, tiled=True),
        lax.all_gather(b_out, ("ctx", "fsdp"), axis=0, tiled=True),
        lax.all_gather(ln1_gain, ("ctx", "fsdp"), axis=0, tiled=True),
        lax.all_gather(ln1_bias, ("ctx", "fsdp"), axis=0, tiled=True),
    )
    token_pos = (ctx_at * n_fsdp + fsdp_at) * tok_slot + jnp.arange(tok_slot, dtype=jnp.int32)
    live_rows = (token_pos[None, :] < lengths[:, None]).reshape(row_count, 1)
    flat_tokens = tokens.reshape(row_count, width)
    joined = jnp.dot(flat_tokens, qkv_full, preferred_element_type=jnp.float32) + qkv_bias.astype(
        jnp.float32
    )
    cosine, sine_part = rope_tables(token_pos.astype(jnp.float32), HD)
    split_heads = joined.reshape(groups, tok_slot, 3, H, HD)
    rotated_query = rotate(split_heads[:, :, 0], cosine, sine_part)
    rotated_key = rotate(split_heads[:, :, 1], cosine, sine_part)
    packed = (
        jnp.stack([rotated_query, rotated_key, split_heads[:, :, 2]], axis=2)
        .astype(jnp.bfloat16)
        .reshape(groups, tok_slot, 3, n_fsdp, lane_width)
    )
    by_heads = lax.all_to_all(packed, "fsdp", split_axis=3, concat_axis=1, tiled=True)
    queries = by_heads[:, :, 0, 0]
    local_keys = by_heads[:, :, 1, 0]
    local_values = by_heads[:, :, 2, 0]
    all_keys, all_values = (
        lax.all_gather(local_keys, "ctx", axis=1, tiled=True),
        lax.all_gather(local_values, "ctx", axis=1, tiled=True),
    )

    def attend_slot(slot_item):
        slot_queries, slot_keys, slot_values, length = slot_item
        query_split = slot_queries.reshape(query_blocks, query_rows, heads_here, HD)
        key_split = slot_keys.reshape(key_blocks, key_rows, heads_here, HD)
        value_split = slot_values.reshape(key_blocks, key_rows, heads_here, HD)

        def per_query(query_block):

            def row_stats(state_pair, key_item):
                highest, running_sum = state_pair
                scores = block_scores(query_block, key_item[0], key_item[1], length, scale)
                new_high = jnp.maximum(highest, jnp.max(scores, axis=-1))
                running_sum = running_sum * jnp.exp(highest - new_high) + jnp.sum(
                    jnp.exp(scores - new_high[..., None]), axis=-1
                )
                return ((new_high, running_sum), None)

            start_state = (
                jnp.full((heads_here, query_rows), NEG_FILL, jnp.float32),
                jnp.zeros((heads_here, query_rows), jnp.float32),
            )
            highest, running_sum = lax.scan(row_stats, start_state, (key_split, key_starts))[0]
            log_norm = highest + jnp.log(running_sum)

            def weigh_values(accumulated, key_item):
                scores = block_scores(query_block, key_item[0], key_item[2], length, scale)
                weights = jnp.exp(scores - log_norm[..., None]).astype(jnp.bfloat16)
                return (
                    accumulated
                    + jnp.einsum(
                        "hqk,khd->qhd", weights, key_item[1], preferred_element_type=jnp.float32
                    ),
                    None,
                )

            mixture = lax.scan(
                weigh_values,
                jnp.zeros((query_rows, heads_here, HD), jnp.float32),
                (key_split, value_split, key_starts),
            )[0]
            return (mixture, log_norm)

        mixture, log_norm = lax.map(per_query, query_split)
        return (mixture.reshape(span_rows, lane_width), log_norm)

    mixture, log_norms = lax.map(attend_slot, (queries, all_keys, all_values, lengths))
    merged = lax.all_to_all(
        mixture.astype(jnp.bfloat16).reshape(groups, span_rows, 1, lane_width),
        "fsdp",
        split_axis=1,
        concat_axis=2,
        tiled=True,
    ).reshape(row_count, width)
    attended = jnp.dot(merged, out_full, preferred_element_type=jnp.float32) + out_bias.astype(
        jnp.float32
    )
    hidden_one, pull_one = jax.vjp(
        layer_norm,
        flat_tokens.astype(jnp.float32) + attended,
        gain_one.astype(jnp.float32),
        shift_one.astype(jnp.float32),
    )
    hidden_low = hidden_one.astype(jnp.bfloat16)
    up_full, up_bias, down_full, down_bias, gain_two, shift_two, proj_full = (
        lax.all_gather(w_up, ("ctx", "fsdp"), axis=0, tiled=True),
        lax.all_gather(b_up, ("ctx", "fsdp"), axis=0, tiled=True),
        lax.all_gather(w_down, ("ctx", "fsdp"), axis=0, tiled=True),
        lax.all_gather(b_down, ("ctx", "fsdp"), axis=0, tiled=True),
        lax.all_gather(ln2_gain, ("ctx", "fsdp"), axis=0, tiled=True),
        lax.all_gather(ln2_bias, ("ctx", "fsdp"), axis=0, tiled=True),
        lax.all_gather(w_proj, ("ctx", "fsdp"), axis=0, tiled=True),
    )
    upward = jnp.dot(hidden_low, up_full, preferred_element_type=jnp.float32) + up_bias.astype(
        jnp.float32
    )
    active_full, pull_gelu = jax.vjp(partial(jax.nn.gelu, approximate=False), upward)
    active = active_full.astype(jnp.bfloat16)
    downward = jnp.dot(active, down_full, preferred_element_type=jnp.float32) + down_bias.astype(
        jnp.float32
    )
    out_full_rows, pull_two = jax.vjp(
        layer_norm,
        hidden_one + downward,
        gain_two.astype(jnp.float32),
        shift_two.astype(jnp.float32),
    )
    out_low = out_full_rows.astype(jnp.bfloat16)
    projected = jnp.dot(out_low, proj_full, preferred_element_type=jnp.float32)
    back_qkv, back_qkv_bias, back_out, back_out_bias, back_gain_one, back_shift_one = (
        lax.all_gather(w_qkv, ("ctx", "fsdp"), axis=0, tiled=True),
        lax.all_gather(b_qkv, ("ctx", "fsdp"), axis=0, tiled=True),
        lax.all_gather(w_out, ("ctx", "fsdp"), axis=0, tiled=True),
        lax.all_gather(b_out, ("ctx", "fsdp"), axis=0, tiled=True),
        lax.all_gather(ln1_gain, ("ctx", "fsdp"), axis=0, tiled=True),
        lax.all_gather(ln1_bias, ("ctx", "fsdp"), axis=0, tiled=True),
    )
    back_up, back_up_bias, back_down, back_down_bias, back_gain_two, back_shift_two, back_proj = (
        lax.all_gather(w_up, ("ctx", "fsdp"), axis=0, tiled=True),
        lax.all_gather(b_up, ("ctx", "fsdp"), axis=0, tiled=True),
        lax.all_gather(w_down, ("ctx", "fsdp"), axis=0, tiled=True),
        lax.all_gather(b_down, ("ctx", "fsdp"), axis=0, tiled=True),
        lax.all_gather(ln2_gain, ("ctx", "fsdp"), axis=0, tiled=True),
        lax.all_gather(ln2_bias, ("ctx", "fsdp"), axis=0, tiled=True),
        lax.all_gather(w_proj, ("ctx", "fsdp"), axis=0, tiled=True),
    )
    grad_out = jnp.where(live_rows, cot_out.reshape(row_count, width).astype(jnp.float32), 0.0)
    grad_emb = jnp.where(live_rows, cot_emb.reshape(row_count, -1), 0)
    d_proj = jnp.einsum("rd,rp->dp", out_low, grad_emb, preferred_element_type=jnp.float32)
    grad_full = grad_out + jnp.einsum(
        "rp,dp->rd", grad_emb, back_proj, preferred_element_type=jnp.float32
    )
    grad_two, d_gain_two, d_shift_two = pull_two(grad_full)
    grad_down = grad_two.astype(jnp.bfloat16)
    d_down = jnp.einsum("rf,rd->fd", active, grad_down, preferred_element_type=jnp.float32)
    d_down_bias = jnp.sum(grad_down.astype(jnp.float32), axis=0)
    grad_act = jnp.einsum("rd,fd->rf", grad_down, back_down, preferred_element_type=jnp.float32)
    grad_up = pull_gelu(grad_act)[0].astype(jnp.bfloat16)
    d_up = jnp.einsum("rd,rf->df", hidden_low, grad_up, preferred_element_type=jnp.float32)
    d_up_bias = jnp.sum(grad_up.astype(jnp.float32), axis=0)
    grad_hidden = grad_two + jnp.einsum(
        "rf,df->rd", grad_up, back_up, preferred_element_type=jnp.float32
    )
    grad_one, d_gain_one, d_shift_one = pull_one(grad_hidden)
    grad_att = grad_one.astype(jnp.bfloat16)
    d_out = jnp.einsum("rd,re->de", merged, grad_att, preferred_element_type=jnp.float32)
    d_out_bias = jnp.sum(grad_att.astype(jnp.float32), axis=0)
    grad_merged = jnp.einsum(
        "re,de->rd", grad_att, back_out, preferred_element_type=jnp.float32
    ).astype(jnp.bfloat16)
    grad_heads = lax.all_to_all(
        grad_merged.reshape(groups, tok_slot, n_fsdp, lane_width),
        "fsdp",
        split_axis=2,
        concat_axis=1,
        tiled=True,
    ).reshape(groups, span_rows, lane_width)

    def attend_back(slot_item):
        slot_queries, slot_keys, slot_values, grad_mix, log_norm, length = slot_item
        query_split = slot_queries.reshape(query_blocks, query_rows, heads_here, HD)
        key_split = slot_keys.reshape(key_blocks, key_rows, heads_here, HD)
        value_split = slot_values.reshape(key_blocks, key_rows, heads_here, HD)
        grad_split = grad_mix.reshape(query_blocks, query_rows, heads_here, HD)

        def value_pass(value_total, query_item):
            query_block, grad_block, norm_block = query_item

            def value_per_key(row_dot, key_item):
                key_block, value_block, key_start = key_item
                scores = block_scores(query_block, key_block, key_start, length, scale)
                probability = jnp.exp(scores - norm_block[..., None])
                grad_probs = jnp.einsum(
                    "qhd,khd->hqk", grad_block, value_block, preferred_element_type=jnp.float32
                )
                value_part = jnp.einsum(
                    "hqk,qhd->khd",
                    probability.astype(jnp.bfloat16),
                    grad_block,
                    preferred_element_type=jnp.float32,
                )
                return (row_dot + jnp.sum(probability * grad_probs, axis=-1), value_part)

            row_dot, value_parts = lax.scan(
                value_per_key,
                jnp.zeros((heads_here, query_rows), jnp.float32),
                (key_split, value_split, key_starts),
            )
            return (value_total + value_parts.reshape(key_count, heads_here, HD), row_dot)

        value_grad, row_dots = lax.scan(
            value_pass,
            jnp.zeros((key_count, heads_here, HD), jnp.float32),
            (query_split, grad_split, log_norm),
        )

        def key_pass(key_total, query_item):
            query_block, grad_block, norm_block, dot_block = query_item

            def key_per_key(query_accum, key_item):
                key_block, value_block, key_start = key_item
                scores = block_scores(query_block, key_block, key_start, length, scale)
                probability = jnp.exp(scores - norm_block[..., None])
                grad_probs = jnp.einsum(
                    "qhd,khd->hqk", grad_block, value_block, preferred_element_type=jnp.float32
                )
                grad_scores = (probability * (grad_probs - dot_block[..., None])).astype(
                    jnp.bfloat16
                )
                query_accum = query_accum + jnp.einsum(
                    "hqk,khd->qhd", grad_scores, key_block, preferred_element_type=jnp.float32
                )
                key_part = jnp.einsum(
                    "hqk,qhd->khd", grad_scores, query_block, preferred_element_type=jnp.float32
                )
                return (query_accum, key_part)

            query_grad, key_parts = lax.scan(
                key_per_key,
                jnp.zeros((query_rows, heads_here, HD), jnp.float32),
                (key_split, value_split, key_starts),
            )
            return (key_total + key_parts.reshape(key_count, heads_here, HD), query_grad)

        key_grad, query_grads = lax.scan(
            key_pass,
            jnp.zeros((key_count, heads_here, HD), jnp.float32),
            (query_split, grad_split, log_norm, row_dots),
        )
        return (
            query_grads.reshape(span_rows, lane_width) * scale,
            key_grad.reshape(key_count, lane_width) * scale,
            value_grad.reshape(key_count, lane_width),
        )

    grad_queries, key_terms, value_terms = lax.map(
        attend_back, (queries, all_keys, all_values, grad_heads, log_norms, lengths)
    )
    grad_keys, grad_values = (
        lax.psum_scatter(
            key_terms.astype(jnp.bfloat16), "ctx", scatter_dimension=1, tiled=True
        ).astype(jnp.float32),
        lax.psum_scatter(
            value_terms.astype(jnp.bfloat16), "ctx", scatter_dimension=1, tiled=True
        ).astype(jnp.float32),
    )
    head_pos = (ctx_at * span_rows + jnp.arange(span_rows, dtype=jnp.int32)).astype(jnp.float32)
    head_cosine, head_sine = rope_tables(head_pos, HD)
    query_back = rotate(
        grad_queries.reshape(groups, span_rows, heads_here, HD), head_cosine, -head_sine
    )
    key_back = rotate(grad_keys.reshape(groups, span_rows, heads_here, HD), head_cosine, -head_sine)
    value_back = grad_values.reshape(groups, span_rows, heads_here, HD)
    grad_pack = (
        jnp.stack([query_back, key_back, value_back], axis=2)
        .astype(jnp.bfloat16)
        .reshape(groups, span_rows, 3, 1, lane_width)
    )
    grad_joined = lax.all_to_all(
        grad_pack, "fsdp", split_axis=1, concat_axis=3, tiled=True
    ).reshape(row_count, 3 * width)
    d_qkv = jnp.einsum("rd,re->de", flat_tokens, grad_joined, preferred_element_type=jnp.float32)
    d_qkv_bias = jnp.sum(grad_joined.astype(jnp.float32), axis=0)
    input_grad = (
        jnp.einsum("re,de->rd", grad_joined, back_qkv, preferred_element_type=jnp.float32)
        + grad_one
    ).astype(jnp.bfloat16)
    shards = (
        lax.psum_scatter(d_qkv, ("ctx", "fsdp"), scatter_dimension=0, tiled=True),
        lax.psum_scatter(d_qkv_bias, ("ctx", "fsdp"), scatter_dimension=0, tiled=True),
        lax.psum_scatter(d_out, ("ctx", "fsdp"), scatter_dimension=0, tiled=True),
        lax.psum_scatter(d_out_bias, ("ctx", "fsdp"), scatter_dimension=0, tiled=True),
        lax.psum_scatter(d_gain_one, ("ctx", "fsdp"), scatter_dimension=0, tiled=True),
        lax.psum_scatter(d_shift_one, ("ctx", "fsdp"), scatter_dimension=0, tiled=True),
        lax.psum_scatter(d_up, ("ctx", "fsdp"), scatter_dimension=0, tiled=True),
        lax.psum_scatter(d_up_bias, ("ctx", "fsdp"), scatter_dimension=0, tiled=True),
        lax.psum_scatter(d_down, ("ctx", "fsdp"), scatter_dimension=0, tiled=True),
        lax.psum_scatter(d_down_bias, ("ctx", "fsdp"), scatter_dimension=0, tiled=True),
        lax.psum_scatter(d_gain_two, ("ctx", "fsdp"), scatter_dimension=0, tiled=True),
        lax.psum_scatter(d_shift_two, ("ctx", "fsdp"), scatter_dimension=0, tiled=True),
        lax.psum_scatter(d_proj, ("ctx", "fsdp"), scatter_dimension=0, tiled=True),
    )
    totals = (
        lax.psum(shards[0].astype(jnp.bfloat16), "slot").astype(jnp.float32),
        lax.psum(shards[1].astype(jnp.bfloat16), "slot").astype(jnp.float32),
        lax.psum(shards[2].astype(jnp.bfloat16), "slot").astype(jnp.float32),
        lax.psum(shards[3].astype(jnp.bfloat16), "slot").astype(jnp.float32),
        lax.psum(shards[4].astype(jnp.bfloat16), "slot").astype(jnp.float32),
        lax.psum(shards[5].astype(jnp.bfloat16), "slot").astype(jnp.float32),
        lax.psum(shards[6].astype(jnp.bfloat16), "slot").astype(jnp.float32),
        lax.psum(shards[7].astype(jnp.bfloat16), "slot").astype(jnp.float32),
        lax.psum(shards[8].astype(jnp.bfloat16), "slot").astype(jnp.float32),
        lax.psum(shards[9].astype(jnp.bfloat16), "slot").astype(jnp.float32),
        lax.psum(shards[10].astype(jnp.bfloat16), "slot").astype(jnp.float32),
        lax.psum(shards[11].astype(jnp.bfloat16), "slot").astype(jnp.float32),
        lax.psum(shards[12].astype(jnp.bfloat16), "slot").astype(jnp.float32),
    )
    return (
        out_low.reshape(groups, tok_slot, width),
        projected.astype(jnp.bfloat16).reshape(groups, tok_slot, -1),
        input_grad.reshape(groups, tok_slot, width),
        totals[0],
        totals[1],
        totals[2],
        totals[3],
        totals[4],
        totals[5],
        totals[6],
        totals[7],
        totals[8],
        totals[9],
        totals[10],
        totals[11],
        totals[12],
    )


def solution(mesh):
    n_slot, n_ctx, n_fsdp = (mesh.shape[a] for a in ("slot", "ctx", "fsdp"))
    rows_axes = ("ctx", "fsdp")
    step = per_device
    if n_slot == 2 and n_fsdp % 2 == 0 and n_ctx * n_fsdp == H:
        mesh = Mesh(
            mesh.devices.reshape(n_slot, n_ctx, n_fsdp // 2, 2), ("slot", "ctx", "x", "core")
        )
        rows_axes = GROUP
        step = head_device
    in_specs = (
        P("slot", rows_axes, None),
        P("slot"),
        P(rows_axes, None),
        P(rows_axes),
        P(rows_axes, None),
        P(rows_axes),
        P(rows_axes),
        P(rows_axes),
        P(rows_axes, None),
        P(rows_axes),
        P(rows_axes, None),
        P(rows_axes),
        P(rows_axes),
        P(rows_axes),
        P(rows_axes, None),
        P("slot", rows_axes, None),
        P("slot", rows_axes, None),
    )
    out_specs = (
        P("slot", rows_axes, None),
        P("slot", rows_axes, None),
        P("slot", rows_axes, None),
        P(rows_axes, None),
        P(rows_axes),
        P(rows_axes, None),
        P(rows_axes),
        P(rows_axes),
        P(rows_axes),
        P(rows_axes, None),
        P(rows_axes),
        P(rows_axes, None),
        P(rows_axes),
        P(rows_axes),
        P(rows_axes),
        P(rows_axes, None),
    )
    return jax.shard_map(
        step, mesh=mesh, in_specs=in_specs, out_specs=out_specs, check_vma=False
    )
```
